32 devices in a mesh: ctx: 8 (over z, y), wa: 4 (over x, core).
Axes of the slice: x: 2, y: 2, z: 4, core: 2. Of those that a mesh axis runs over, the one named last changes fastest.
Arguments:
- tokens: bfloat16 [4, 1024, 896], P('wa', 'ctx'), may hold values from -6 to 6
- neighbours: bfloat16 [4, 16, 256, 896], P('wa', 'ctx'), may hold values from -6 to 6
- teacher: bfloat16 [4, 1024, 896], P('wa', 'ctx'), may hold values from -6 to 6
- valid_mask: int32 [4, 1024], P('wa', 'ctx'), may hold values from 0 to 1, as said below
- block_order: int32 [16], replicated, may hold values from 0 to 15, as said below
- query_weight: bfloat16 [896, 1024], P('wa'), may hold values from -0.1875 to 0.1875
- key_weight: bfloat16 [896, 1024], P('wa'), may hold values from -0.1875 to 0.1875
- value_weight: bfloat16 [896, 1024], P('wa'), may hold values from -0.1875 to 0.1875
- output_weight: bfloat16 [1024, 896], P('wa'), may hold values from -3 to 3
- relative_weight: bfloat16 [896, 1024], P('wa'), may hold values from -0.1875 to 0.1875
- content_bias: bfloat16 [1024], P('wa'), may hold values from -3 to 3
- position_bias: bfloat16 [1024], P('wa'), may hold values from -3 to 3
- cross_query_weight: bfloat16 [896, 1024], P('wa'), may hold values from -0.1875 to 0.1875
- cross_key_weight: bfloat16 [896, 1024], P('wa'), may hold values from -0.1875 to 0.1875
- cross_value_weight: bfloat16 [896, 1024], P('wa'), may hold values from -0.1875 to 0.1875
- cross_output_weight: bfloat16 [1024, 896], P('wa'), may hold values from -1.5 to 1.5
- up_weight: bfloat16 [896, 3584], P('wa'), may hold values from -0.1875 to 0.1875
- down_weight: bfloat16 [3584, 896], P('wa'), may hold values from -0.09375 to 0.09375
- attention_gain: bfloat16 [896], P('wa'), may hold values from 0.5 to 1.5
- cross_gain: bfloat16 [896], P('wa'), may hold values from 0.5 to 1.5
- feedforward_gain: bfloat16 [896], P('wa'), may hold values from 0.5 to 1.5
Outputs:
- layer_out: float32 [4, 1024, 896], P('wa', 'ctx')
- loss: float32 [], replicated
- tokens_grad: float32 [4, 1024, 896], P('wa', 'ctx')
- neighbours_grad: float32 [4, 16, 256, 896], P('wa', 'ctx')
- query_weight_grad: float32 [896, 1024], P('wa')
- key_weight_grad: float32 [896, 1024], P('wa')
- value_weight_grad: float32 [896, 1024], P('wa')
- output_weight_grad: float32 [1024, 896], P('wa')
- relative_weight_grad: float32 [896, 1024], P('wa')
- content_bias_grad: float32 [1024], P('wa')
- position_bias_grad: float32 [1024], P('wa')
- cross_query_weight_grad: float32 [896, 1024], P('wa')
- cross_key_weight_grad: float32 [896, 1024], P('wa')
- cross_value_weight_grad: float32 [896, 1024], P('wa')
- cross_output_weight_grad: float32 [1024, 896], P('wa')
- up_weight_grad: float32 [896, 3584], P('wa')
- down_weight_grad: float32 [3584, 896], P('wa')
- attention_gain_grad: float32 [896], P('wa')
- cross_gain_grad: float32 [896], P('wa')
- feedforward_gain_grad: float32 [896], P('wa')
The draws below stay inside these ranges and needn't reach their ends.
Inputs may be any that keep to these rules, and one draw needn't show every extreme that they name: `block_order`: a permutation of 0 to 15 in which entries 2 k and 2 k + 1 are p and 15 - p for some p. `valid_mask`: each entry 0 or 1; the entry of every stored position t with t % 16 == 15 is 1.
All inputs are finite; a program needn't handle non-finite values.
Results may differ from the reference program's by a relative error of at most 0.029.
Values may be sent and summed in bfloat16 or wider, within the bound.
A program may use at most 512 MiB of HBM per device.

```python
import jax
import jax.numpy as jnp
from jax import lax

D = 896
HEADS = 16
HEAD_DIM = 64
AW = 1024
FF = 3584
GROUP = 64
NK = 256
BLOCK = 64
NBLK = 16
SEQ_LEN = 1024
NCHUNK = 16
SEQS = 4


def draw_valid_mask(key, part):
    place = jnp.arange(SEQ_LEN, dtype=jnp.int32)
    level = 200 + 600 * place // SEQ_LEN
    roll = jax.random.randint(jax.random.fold_in(key, 11), (SEQS, SEQ_LEN), 0, 1000)
    keep = (roll < level[None, :]) | (place % 16 == 15)[None, :]
    return keep.astype(jnp.int32)


def draw_block_order(key, part):
    pairs = jax.random.permutation(jax.random.fold_in(key, 21), NBLK // 2).astype(jnp.int32)
    flip = jax.random.randint(jax.random.fold_in(key, 22), (NBLK // 2,), 0, 2)
    first = jnp.where(flip == 1, NBLK - 1 - pairs, pairs)
    second = NBLK - 1 - first
    return jnp.stack([first, second], axis=1).reshape(NBLK).astype(jnp.int32)


def levels(stream_key, shape, shards, low, top_value):
    def one(dim, shards_of):
        steps = jax.random.uniform(jax.random.fold_in(jax.random.fold_in(stream_key, 6), dim), (shards_of,), jnp.float32, low / len(shards), top_value / len(shards))
        return jnp.repeat(jnp.exp(steps), shape[dim] // shards_of).reshape((-1,) + (1,) * (len(shape) - dim - 1))

    level = one(*shards[0])
    for cut in shards[1:]:
        level = level * one(*cut)
    return level


def bell_draw(key, extent, spread, most, cuts=(), kind=jnp.bfloat16):
    values = spread * jax.random.normal(key, extent, jnp.float32)
    if cuts:
        values = values * levels(key, extent, cuts, -0.22, 0.18)
    return jnp.clip(values, -most, most).astype(kind)


def setup_inputs(seed: int = 0) -> dict:
    key_list = jax.random.split(jax.random.key(seed), 22)
    tokens = bell_draw(key_list[0], (SEQS, SEQ_LEN, D), 1.0, 6.0, ((0, 4), (1, 8)))
    neighbours = bell_draw(key_list[1], (SEQS, NCHUNK, NK, D), 1.0, 6.0, ((0, 4), (1, 8)))
    teacher = bell_draw(key_list[2], (SEQS, SEQ_LEN, D), 1.0, 6.0, ((0, 4), (1, 8)))
    valid_mask = draw_valid_mask(jax.random.fold_in(key_list[21], 71), 0)
    block_order = draw_block_order(jax.random.fold_in(key_list[21], 71), 0)
    query_weight = bell_draw(key_list[5], (D, AW), D ** -0.5, 0.1875, ((0, 4),))
    key_weight = bell_draw(key_list[6], (D, AW), D ** -0.5, 0.1875, ((0, 4),))
    value_weight = bell_draw(key_list[7], (D, AW), D ** -0.5, 0.1875, ((0, 4),))
    output_weight = bell_draw(key_list[8], (AW, D), (max(1, AW // 256)) ** -0.5, 3.0, ((0, 4),))
    relative_weight = bell_draw(key_list[9], (D, AW), D ** -0.5, 0.1875, ((0, 4),))
    content_bias = bell_draw(key_list[10], (AW,), 0.5, 3.0, ((0, 4),))
    position_bias = bell_draw(key_list[11], (AW,), 0.5, 3.0, ((0, 4),))
    cross_query_weight = bell_draw(key_list[12], (D, AW), D ** -0.5, 0.1875, ((0, 4),))
    cross_key_weight = bell_draw(key_list[13], (D, AW), D ** -0.5, 0.1875, ((0, 4),))
    cross_value_weight = bell_draw(key_list[14], (D, AW), D ** -0.5, 0.1875, ((0, 4),))
    cross_output_weight = bell_draw(key_list[15], (AW, D), (max(1, AW // 64)) ** -0.5, 1.5, ((0, 4),))
    up_weight = bell_draw(key_list[16], (D, FF), D ** -0.5, 0.1875, ((0, 4),))
    down_weight = bell_draw(key_list[17], (FF, D), FF ** -0.5, 0.09375, ((0, 4),))
    attention_gain = jnp.clip(1.0 + 0.1 * jax.random.normal(key_list[18], (D,), jnp.float32), 0.5, 1.5).astype(jnp.bfloat16)
    cross_gain = jnp.clip(1.0 + 0.1 * jax.random.normal(key_list[19], (D,), jnp.float32), 0.5, 1.5).astype(jnp.bfloat16)
    feedforward_gain = jnp.clip(1.0 + 0.1 * jax.random.normal(key_list[20], (D,), jnp.float32), 0.5, 1.5).astype(jnp.bfloat16)
    return dict(tokens=tokens, neighbours=neighbours, teacher=teacher, valid_mask=valid_mask, block_order=block_order, query_weight=query_weight, key_weight=key_weight, value_weight=value_weight, output_weight=output_weight, relative_weight=relative_weight, content_bias=content_bias, position_bias=position_bias, cross_query_weight=cross_query_weight, cross_key_weight=cross_key_weight, cross_value_weight=cross_value_weight, cross_output_weight=cross_output_weight, up_weight=up_weight, down_weight=down_weight, attention_gain=attention_gain, cross_gain=cross_gain, feedforward_gain=feedforward_gain)


@jax.custom_vjp
def low(v):
    return lax.optimization_barrier(v.astype(jnp.bfloat16)).astype(jnp.float32)

@jax.custom_vjp
def low_back(v):
    return v

def low_keep(v):
    return (low(v), None)

def low_pass(kept, grad):
    return (grad,)

def back_keep(v):
    return (v, None)

def back_low(kept, grad):
    return (low(grad),)
low.defvjp(low_keep, low_pass)
low_back.defvjp(back_keep, back_low)
highest = lax.Precision.HIGHEST
eps_norm = 1e-06
neg_big = -1e+30

def rms_scale(hidden, gain):
    return hidden * lax.rsqrt(lax.optimization_barrier(jnp.mean(hidden * hidden, axis=-1, keepdims=True)) + eps_norm) * gain

def sinusoid(distance, width):
    half = width // 2
    freq = jnp.exp(-jnp.log(10000.0) * jnp.arange(half, dtype=jnp.float32) * 2.0 / width)
    angle = distance[:, None] * freq[None, :]
    return jnp.concatenate([jnp.sin(angle), jnp.cos(angle)], axis=1)

def skew(wide, count):
    lead = wide.shape[:-2]
    rows, span = wide.shape[-2:]
    edge = [(0, 0)] * len(lead)
    padded = jnp.pad(wide, edge + [(0, 0), (0, 1)])
    flat = padded.reshape(lead + (rows * (span + 1),))
    flat = lax.slice_in_dim(flat, rows - 1, rows - 1 + rows * span, axis=len(lead))
    return flat.reshape(lead + (rows, span))[..., :count]

def project(left, right):
    return jnp.einsum('...i,ij->...j', left, right, precision=highest)

def attend(content_all, position_all, key_all, value_all, table):
    seq_len = key_all.shape[0]
    rows = min(512, seq_len)
    scale = HEAD_DIM ** (-0.5)
    key_place = jnp.arange(seq_len, dtype=jnp.int32)

    def block_fn(start):
        content = lax.dynamic_slice_in_dim(content_all, start, rows, 0)
        position = lax.dynamic_slice_in_dim(position_all, start, rows, 0)
        offset = (seq_len - rows - start).astype(jnp.int32)
        relative = lax.dynamic_slice_in_dim(table, offset, rows + seq_len, 0)
        scores = jnp.einsum('qhe,khe->hqk', content, key_all, precision=highest)
        wide = jnp.einsum('qhe,whe->hqw', position, relative, precision=highest)
        scores = low_back((scores + skew(wide, seq_len)) * scale)
        causal = (start + jnp.arange(rows, dtype=jnp.int32))[:, None] >= key_place[None, :]
        scores = jnp.where(causal[None], scores, neg_big)
        top = lax.optimization_barrier(jnp.max(scores, axis=-1, keepdims=True))
        raised = jnp.exp(scores - top)
        shares = low(raised / lax.optimization_barrier(jnp.sum(raised, axis=-1, keepdims=True)))
        return jnp.einsum('hqk,khe->qhe', shares, value_all, precision=highest)
    starts = (jnp.arange(seq_len // rows, dtype=jnp.int32) * rows).astype(jnp.int32)
    return lax.map(jax.checkpoint(block_fn), starts).reshape(seq_len, HEADS, HEAD_DIM)

def cross_one(parts):
    cross_q, cross_k, cross_v = parts
    scale = HEAD_DIM ** (-0.5)
    scores = low_back(jnp.einsum('czhe,ckhe->chzk', cross_q, cross_k, precision=highest) * scale)
    top = lax.optimization_barrier(jnp.max(scores, axis=-1, keepdims=True))
    raised = jnp.exp(scores - top)
    shares = low(raised / lax.optimization_barrier(jnp.sum(raised, axis=-1, keepdims=True)))
    return jnp.einsum('chzk,ckhe->czhe', shares, cross_v, precision=highest)

def layer(tokens, neighbours, order, weights):
    query_w, key_w, value_w, output_w, relative_w, content_b, position_b, cross_qw, cross_kw, cross_vw, cross_ow, up_w, down_w, gain_one, gain_two, gain_three = weights
    seqs, seq_len, width = tokens.shape
    attn_width = HEADS * HEAD_DIM
    slots = jnp.arange(NBLK, dtype=jnp.int32)
    inverse = lax.optimization_barrier(jnp.sum(jnp.where(order[None, :] == slots[:, None], slots[None, :], 0), axis=1)).astype(jnp.int32)
    place = jnp.arange(seq_len, dtype=jnp.int32)
    gather_glob = (inverse[place // BLOCK] * BLOCK + place % BLOCK).astype(jnp.int32)
    gather_back = (order[place // BLOCK] * BLOCK + place % BLOCK).astype(jnp.int32)
    distance = (seq_len - 1 - place).astype(jnp.float32)
    relative = low(project(low(sinusoid(distance, width)), relative_w))
    table = jnp.concatenate([relative, jnp.zeros_like(relative)], axis=0).reshape(2 * seq_len, HEADS, HEAD_DIM)
    normed_a = low(rms_scale(tokens, gain_one))
    query = low_back(project(normed_a, query_w))
    content = low(query + content_b).reshape(seqs, seq_len, HEADS, HEAD_DIM)
    position = low(query + position_b).reshape(seqs, seq_len, HEADS, HEAD_DIM)
    keys = low(low_back(project(normed_a, key_w))).reshape(seqs, seq_len, HEADS, HEAD_DIM)
    values = low(low_back(project(normed_a, value_w))).reshape(seqs, seq_len, HEADS, HEAD_DIM)

    def one_seq(parts):
        content_s, position_s, key_s, value_s = parts
        out = attend(content_s[gather_glob], position_s[gather_glob], key_s[gather_glob], value_s[gather_glob], table)
        return out[gather_back]
    attended = lax.map(one_seq, (content, position, keys, values)).reshape(seqs, seq_len, attn_width)
    mixed = low(low_back(attended))
    hidden_one = tokens + low_back(project(mixed, output_w))
    normed_b = low(rms_scale(hidden_one, gain_two))
    cross_q = low(low_back(project(normed_b, cross_qw))).reshape(seqs, NCHUNK, GROUP, HEADS, HEAD_DIM)
    cross_k = low(low_back(project(neighbours, cross_kw))).reshape(seqs, NCHUNK, NK, HEADS, HEAD_DIM)
    cross_v = low(low_back(project(neighbours, cross_vw))).reshape(seqs, NCHUNK, NK, HEADS, HEAD_DIM)
    crossed = lax.map(jax.checkpoint(cross_one), (cross_q, cross_k, cross_v)).reshape(seqs, seq_len, attn_width)
    hidden_two = hidden_one + low_back(project(low(low_back(crossed)), cross_ow))
    normed_c = low(rms_scale(hidden_two, gain_three))
    pre_act = low_back(project(normed_c, up_w))
    activated = low(jax.nn.gelu(pre_act, approximate=True))
    return hidden_two + low_back(project(activated, down_w))

def reference(tokens, neighbours, teacher, valid_mask, block_order, query_weight, key_weight, value_weight, output_weight, relative_weight, content_bias, position_bias, cross_query_weight, cross_key_weight, cross_value_weight, cross_output_weight, up_weight, down_weight, attention_gain, cross_gain, feedforward_gain):
    weights = tuple((w.astype(jnp.float32) for w in (query_weight, key_weight, value_weight, output_weight, relative_weight, content_bias, position_bias, cross_query_weight, cross_key_weight, cross_value_weight, cross_output_weight, up_weight, down_weight, attention_gain, cross_gain, feedforward_gain)))
    valid = valid_mask.astype(jnp.float32)
    count = jnp.sum(valid)
    target = teacher.astype(jnp.float32)
    seqs, seq_len, width = tokens.shape

    def objective(tokens_f, neighbours_f, *params):
        out = layer(tokens_f, neighbours_f, block_order, params)
        error = out - target
        loss = jnp.sum(valid[..., None] * error * error) / (2.0 * count * width)
        return (loss * (seqs * seq_len * width), (out, loss))
    scaled, pull, aux = jax.vjp(objective, tokens.astype(jnp.float32), neighbours.astype(jnp.float32), *weights, has_aux=True)
    out, loss = aux
    grads = pull(jnp.ones_like(scaled))
    return (out, loss, grads[0], grads[1], grads[2], grads[3], grads[4], grads[5], grads[6], grads[7], grads[8], grads[9], grads[10], grads[11], grads[12], grads[13], grads[14], grads[15], grads[16], grads[17])
```

```python
import functools

import jax
import jax.numpy as jnp
from jax import lax
from jax.experimental import pallas as pl
from jax.experimental.pallas import tpu as pltpu
from jax.sharding import PartitionSpec as P

HEADS = 16
HEAD_DIM = 64
GROUP = 64
NK = 256
TILE = 128

eps_norm = 1e-06
neg_big = -1e30
highest = lax.Precision.HIGHEST
f32 = jnp.float32
bf16 = jnp.bfloat16


def inverse_rms(hidden):
    return lax.rsqrt(jnp.mean(hidden * hidden, axis=-1, keepdims=True) + eps_norm)


def norm_pull(hidden, scale, gain, grad):
    scaled = grad * gain
    mean = jnp.mean(hidden * scaled, axis=-1, keepdims=True)
    return scale * scaled - hidden * (scale * scale * scale) * mean


def gelu_tanh(value):
    return jax.nn.gelu(value, approximate=True)


def sinusoid(distance, width):
    half = width // 2
    freq = jnp.exp(-jnp.log(10000.0) * jnp.arange(half, dtype=f32) * 2.0 / width)
    angle = distance[:, None] * freq[None, :]
    return jnp.concatenate([jnp.sin(angle), jnp.cos(angle)], axis=1)


def dot_nn(a, b):
    return lax.dot_general(a, b, (((1,), (0,)), ((), ())), preferred_element_type=f32)


def dot_nt(a, b):
    return lax.dot_general(a, b, (((1,), (1,)), ((), ())), preferred_element_type=f32)


def dot_tn(a, b):
    return lax.dot_general(a, b, (((0,), (0,)), ((), ())), preferred_element_type=f32)


def swap(value, axis, bit):
    pairs = [(i, i ^ bit) for i in range(lax.axis_size(axis))]
    return lax.ppermute(value, axis, pairs)


def bits_of(axis):
    bits, bit = [], 1
    while bit < lax.axis_size(axis):
        bits.append(bit)
        bit *= 2
    return bits


def my_bit(axis, bit):
    return (lax.axis_index(axis) // bit) % 2


def ordered(bit, own, other, dim):
    return jnp.where(
        bit == 0,
        jnp.concatenate([own, other], axis=dim),
        jnp.concatenate([other, own], axis=dim),
    )


def split(value, bit, dim):
    half = value.shape[dim] // 2
    keep = lax.dynamic_slice_in_dim(value, bit * half, half, dim)
    send = lax.dynamic_slice_in_dim(value, (1 - bit) * half, half, dim)
    return keep, send


def gather_parts(value):
    parts = {0: value}
    for bit in reversed(bits_of("wa")):
        parts.update({r | bit: swap(part, "wa", bit) for r, part in list(parts.items())})
    return [parts[r] for r in sorted(parts)]


def scatter_parts(parts):
    parts = dict(enumerate(parts))
    for bit in bits_of("wa"):
        kept = {}
        for r, part in parts.items():
            if not r & bit:
                got = swap(parts[r | bit].astype(bf16), "wa", bit)
                kept[r] = part + got.astype(f32)
        parts = kept
    return parts[0]


def take_columns(weight):
    value = weight[None]
    for bit in reversed(bits_of("wa")):
        mine = my_bit("wa", bit)
        keep, send = split(value, mine, 2)
        value = ordered(mine, keep[:, None], swap(send, "wa", bit)[:, None], 1)
        value = value.reshape((-1,) + value.shape[2:])
    return value.reshape(-1, value.shape[-1])


def spread_columns(value):
    for bit in bits_of("wa"):
        mine = my_bit("wa", bit)
        paired = value.reshape((value.shape[0], value.shape[1] // 2, 2) + value.shape[2:])
        keep, send = split(paired, mine, 2)
        value = ordered(mine, keep[:, :, 0], swap(send[:, :, 0], "wa", bit), 3)
    return value[:, 0]


def halving_dim(shape):
    if shape[-2] % 16 == 0:
        return len(shape) - 2
    if shape[0] % 2 == 0:
        return 0
    if shape[-2] % 2 == 0:
        return len(shape) - 2
    return len(shape) - 1


def sum_over_ctx(value, bits, finish):
    dims = []
    for bit in bits:
        dim = halving_dim(value.shape)
        keep, send = split(value, my_bit("ctx", bit), dim)
        value = (keep.astype(f32) + swap(send, "ctx", bit).astype(f32)).astype(bf16)
        dims.append(dim - value.ndim if dim else 0)
    value = finish(value)
    for bit, dim in reversed(list(zip(bits, dims))):
        dim = dim % value.ndim
        value = ordered(my_bit("ctx", bit), value, swap(value, "ctx", bit), dim)
    return value


def all_summed(value, axis):
    for bit in bits_of(axis):
        value = value + swap(value, axis, bit)
    return value


def sum_column_grads(grads):
    places = lax.axis_size("wa")
    grads = grads.reshape(grads.shape[0], places, grads.shape[1] // places, grads.shape[2])
    bits = bits_of("ctx")
    if grads.shape[2] % lax.axis_size("ctx") == 0:
        return sum_over_ctx(grads, bits, spread_columns).astype(f32)
    return sum_over_ctx(spread_columns(grads), bits, lambda value: value).astype(f32)


def sum_row_grads(grads):
    return sum_over_ctx(grads[None], bits_of("ctx"), lambda value: value)[0].astype(f32)


def first_half(shape):
    return lax.broadcasted_iota(jnp.int32, shape, 1) < HEAD_DIM


def stack_heads(rows):
    mask = first_half(rows.shape)
    zero = jnp.zeros_like(rows)
    return jnp.concatenate([jnp.where(mask, rows, zero), jnp.where(mask, zero, rows)], axis=0)


def join_heads(stacked):
    rows = stacked.shape[0] // 2
    return jnp.where(first_half((rows, stacked.shape[1])), stacked[:rows], stacked[rows:])


def copy_blocks(order_ref, source, target, block, inward):
    for place in range(source.shape[0] // block):
        start = pl.multiple_of(order_ref[place] * block, block)
        if inward:
            target[place * block : (place + 1) * block, :] = source[pl.ds(start, block), :]
        else:
            target[pl.ds(start, block), :] = source[place * block : (place + 1) * block, :]


def attention_shares(content, position, key_ref, rel_ref, row_start, seq_len):
    length = row_start + TILE
    wide_len = length + TILE
    offset = seq_len - TILE - row_start
    scale = HEAD_DIM ** (-0.5)
    scores = dot_nt(content, key_ref[0:length, :])
    wide = dot_nt(position, rel_ref[offset : offset + wide_len, :])
    halves = []
    for head in range(2):
        part = wide[head * TILE : (head + 1) * TILE]
        turned = pltpu.roll(part, wide_len - (TILE - 1), 1, stride=1, stride_axis=0)
        halves.append(turned[:, :length])
    scores = (scores + jnp.concatenate(halves, axis=0)) * scale
    row = lax.broadcasted_iota(jnp.int32, scores.shape, 0) % TILE + row_start
    col = lax.broadcasted_iota(jnp.int32, scores.shape, 1)
    scores = jnp.where(col <= row, scores, neg_big)
    top = jnp.max(scores, axis=1, keepdims=True)
    raised = jnp.exp(scores - top)
    total = jnp.sum(raised, axis=1, keepdims=True)
    return raised * (1.0 / total)


def attend_forward_kernel(seq_len, block, order_ref, qkv_ref, rel_ref, bias_ref, out_ref, qkv, out):
    copy_blocks(order_ref, qkv_ref, qkv, block, True)
    keys = qkv.at[:, 128:256]
    values = qkv.at[:, 256:384]
    content_bias = bias_ref[0:1, :]
    position_bias = bias_ref[1:2, :]
    for tile in range(seq_len // TILE):
        start = tile * TILE
        query = qkv[start : start + TILE, 0:128].astype(f32)
        content = stack_heads((query + content_bias).astype(bf16))
        position = stack_heads((query + position_bias).astype(bf16))
        shares = attention_shares(content, position, keys, rel_ref, start, seq_len)
        got = dot_nn(shares.astype(bf16), values[0 : start + TILE, :])
        out[start : start + TILE, :] = join_heads(got).astype(bf16)
    copy_blocks(order_ref, out, out_ref, block, False)


def attend_backward_kernel(
    seq_len,
    block,
    order_ref,
    qkv_ref,
    rel_ref,
    bias_ref,
    grad_ref,
    dqkv_ref,
    drel_ref,
    dbias_ref,
    qkv,
    grad,
    dqkv,
    dkey,
    dvalue,
    drel,
):
    scale = HEAD_DIM ** (-0.5)
    copy_blocks(order_ref, qkv_ref, qkv, block, True)
    copy_blocks(order_ref, grad_ref, grad, block, True)
    keys = qkv.at[:, 128:256]
    values = qkv.at[:, 256:384]
    content_bias = bias_ref[0:1, :]
    position_bias = bias_ref[1:2, :]
    dkey[...] = jnp.zeros_like(dkey)
    dvalue[...] = jnp.zeros_like(dvalue)
    drel[...] = jnp.zeros_like(drel)
    row = lax.broadcasted_iota(jnp.int32, (TILE, TILE), 0)
    col = lax.broadcasted_iota(jnp.int32, (TILE, TILE), 1)
    flip = jnp.where(row + col == TILE - 1, 1.0, 0.0).astype(bf16)
    content_sum = jnp.zeros((1, 128), f32)
    position_sum = jnp.zeros((1, 128), f32)
    for tile in range(seq_len // TILE):
        start = tile * TILE
        length = start + TILE
        wide_len = length + TILE
        offset = seq_len - TILE - start
        query = qkv[start : start + TILE, 0:128].astype(f32)
        content = stack_heads((query + content_bias).astype(bf16))
        plain = (query + position_bias).astype(bf16)
        position = stack_heads(plain)
        shares = attention_shares(content, position, keys, rel_ref, start, seq_len)
        out_grad = stack_heads(grad[start : start + TILE, :])
        share_grad = dot_nt(out_grad, values[0:length, :])
        delta = jnp.sum(shares * share_grad, axis=1, keepdims=True)
        score_grad = (shares * (share_grad - delta)).astype(bf16)
        content_grad = join_heads(dot_nn(score_grad, keys[0:length, :])) * scale
        parts = []
        for head in range(2):
            turned = dot_nn(flip, score_grad[head * TILE : (head + 1) * TILE])
            turned = jnp.concatenate([turned, jnp.zeros((TILE, TILE), f32)], axis=1)
            parts.append(pltpu.roll(turned, 0, 1, stride=1, stride_axis=0))
        wide_grad = jnp.concatenate(parts, axis=0).astype(bf16)
        relative = rel_ref[offset : offset + wide_len, :]
        turned_grad = join_heads(dot_nn(wide_grad, relative)) * scale
        turned_rows = stack_heads(dot_nn(flip, plain).astype(bf16))
        drel[offset : offset + wide_len, :] += dot_tn(wide_grad, turned_rows)
        high = turned_grad.astype(bf16)
        low = (turned_grad - high.astype(f32)).astype(bf16)
        position_grad = dot_nn(flip, high) + dot_nn(flip, low)
        content_sum += jnp.sum(content_grad, axis=0, keepdims=True)
        position_sum += jnp.sum(turned_grad, axis=0, keepdims=True)
        dqkv[start : start + TILE, 0:128] = (content_grad + position_grad).astype(bf16)
        dkey[0:length, :] += dot_tn(score_grad, content)
        dvalue[0:length, :] += dot_tn(shares.astype(bf16), out_grad)
    dqkv[:, 128:256] = (dkey[...] * scale).astype(bf16)
    dqkv[:, 256:384] = dvalue[...].astype(bf16)
    copy_blocks(order_ref, dqkv, dqkv_ref, block, False)
    drel_ref[...] = drel[0:seq_len, :] * scale
    dbias_ref[...] = jnp.concatenate(
        [content_sum, position_sum, jnp.zeros((6, 128), f32)], axis=0
    )


in_vmem = pl.BlockSpec(memory_space=pltpu.VMEM)
in_smem = pl.BlockSpec(memory_space=pltpu.SMEM)


def attend_forward(order, qkv, rel, bias, block):
    rows = qkv.shape[0]
    return pl.pallas_call(
        functools.partial(attend_forward_kernel, rows, block),
        out_shape=jax.ShapeDtypeStruct((rows, 128), bf16),
        in_specs=[in_smem, in_vmem, in_vmem, in_vmem],
        out_specs=in_vmem,
        scratch_shapes=[pltpu.VMEM((rows, 384), bf16), pltpu.VMEM((rows, 128), bf16)],
        compiler_params=pltpu.CompilerParams(vmem_limit_bytes=40 * 2**20),
        cost_estimate=pl.CostEstimate(
            flops=4 * 256 * rows * rows * 2, bytes_accessed=rows * 1300, transcendentals=rows * rows
        ),
        name="attend_forward",
    )(order, qkv, rel, bias)


def attend_backward(order, qkv, rel, bias, grad, block):
    rows = qkv.shape[0]
    return pl.pallas_call(
        functools.partial(attend_backward_kernel, rows, block),
        out_shape=[
            jax.ShapeDtypeStruct((rows, 384), bf16),
            jax.ShapeDtypeStruct((rows, 128), f32),
            jax.ShapeDtypeStruct((8, 128), f32),
        ],
        in_specs=[in_smem, in_vmem, in_vmem, in_vmem, in_vmem],
        out_specs=[in_vmem, in_vmem, in_vmem],
        scratch_shapes=[
            pltpu.VMEM((rows, 384), bf16),
            pltpu.VMEM((rows, 128), bf16),
            pltpu.VMEM((rows, 384), bf16),
            pltpu.VMEM((rows, 128), f32),
            pltpu.VMEM((rows, 128), f32),
            pltpu.VMEM((rows + TILE, 128), f32),
        ],
        compiler_params=pltpu.CompilerParams(vmem_limit_bytes=40 * 2**20),
        cost_estimate=pl.CostEstimate(
            flops=10 * 256 * rows * rows * 2, bytes_accessed=rows * 3000, transcendentals=rows * rows
        ),
        name="attend_backward",
    )(order, qkv, rel, bias, grad)


def head_mask(shape, head):
    lane = lax.broadcasted_iota(jnp.int32, shape, 1)
    return (lane >= head * HEAD_DIM) & (lane < (head + 1) * HEAD_DIM)


def stack_all(rows):
    zero = jnp.zeros_like(rows)
    heads = rows.shape[1] // HEAD_DIM
    return jnp.concatenate(
        [jnp.where(head_mask(rows.shape, head), rows, zero) for head in range(heads)], axis=0
    )


def join_all(stacked):
    heads = stacked.shape[1] // HEAD_DIM
    rows = stacked.shape[0] // heads
    out = jnp.zeros((rows, stacked.shape[1]), stacked.dtype)
    for head in range(heads):
        part = stacked[head * rows : (head + 1) * rows]
        out = jnp.where(head_mask(part.shape, head), part, out)
    return out


def cross_shares(query, keys):
    scores = dot_nt(query, keys) * (HEAD_DIM ** (-0.5))
    raised = jnp.exp(scores - jnp.max(scores, axis=1, keepdims=True))
    return raised / jnp.sum(raised, axis=1, keepdims=True)


def cross_forward_kernel(q_ref, kv_ref, out_ref):
    width = q_ref.shape[1]
    shares = cross_shares(stack_all(q_ref[...]), kv_ref[:, 0:width])
    out_ref[...] = join_all(dot_nn(shares.astype(bf16), kv_ref[:, width:])).astype(bf16)


def cross_backward_kernel(q_ref, kv_ref, grad_ref, dq_ref, dkv_ref):
    width = q_ref.shape[1]
    scale = HEAD_DIM ** (-0.5)
    keys = kv_ref[:, 0:width]
    query = stack_all(q_ref[...])
    grad = stack_all(grad_ref[...])
    shares = cross_shares(query, keys)
    share_grad = dot_nt(grad, kv_ref[:, width:])
    delta = jnp.sum(shares * share_grad, axis=1, keepdims=True)
    score_grad = (shares * (share_grad - delta)).astype(bf16)
    dq_ref[...] = (join_all(dot_nn(score_grad, keys)) * scale).astype(bf16)
    dkv_ref[:, 0:width] = (dot_tn(score_grad, query) * scale).astype(bf16)
    dkv_ref[:, width:] = dot_tn(shares.astype(bf16), grad).astype(bf16)


def cross_forward(query, pair):
    width = query.shape[1]
    groups = query.shape[0] // GROUP
    return pl.pallas_call(
        cross_forward_kernel,
        out_shape=jax.ShapeDtypeStruct(query.shape, bf16),
        grid=(groups,),
        in_specs=[
            pl.BlockSpec((GROUP, width), lambda g: (g, 0)),
            pl.BlockSpec((NK, 2 * width), lambda g: (g, 0)),
        ],
        out_specs=pl.BlockSpec((GROUP, width), lambda g: (g, 0)),
        cost_estimate=pl.CostEstimate(
            flops=groups * 4 * 256 * 256 * 256, bytes_accessed=groups * 330000, transcendentals=groups * 65536
        ),
        name="cross_forward",
    )(query, pair)


def cross_backward(query, pair, grad):
    width = query.shape[1]
    groups = query.shape[0] // GROUP
    return pl.pallas_call(
        cross_backward_kernel,
        out_shape=[
            jax.ShapeDtypeStruct(query.shape, bf16),
            jax.ShapeDtypeStruct(pair.shape, bf16),
        ],
        grid=(groups,),
        in_specs=[
            pl.BlockSpec((GROUP, width), lambda g: (g, 0)),
            pl.BlockSpec((NK, 2 * width), lambda g: (g, 0)),
            pl.BlockSpec((GROUP, width), lambda g: (g, 0)),
        ],
        out_specs=[
            pl.BlockSpec((GROUP, width), lambda g: (g, 0)),
            pl.BlockSpec((NK, 2 * width), lambda g: (g, 0)),
        ],
        cost_estimate=pl.CostEstimate(
            flops=groups * 10 * 256 * 256 * 256, bytes_accessed=groups * 660000, transcendentals=groups * 65536
        ),
        name="cross_backward",
    )(query, pair, grad)


def skew(wide, count):
    lead = wide.shape[:-2]
    rows, span = wide.shape[-2:]
    edge = [(0, 0)] * len(lead)
    padded = jnp.pad(wide, edge + [(0, 0), (0, 1)])
    flat = padded.reshape(lead + (rows * (span + 1),))
    flat = lax.slice_in_dim(flat, rows - 1, rows - 1 + rows * span, axis=len(lead))
    return flat.reshape(lead + (rows, span))[..., :count]


def unskew(grad, span):
    lead = grad.shape[:-2]
    rows, count = grad.shape[-2:]
    edge = [(0, 0)] * len(lead)
    wide = jnp.pad(grad, edge + [(0, 0), (0, span - count)])
    flat = jnp.pad(wide.reshape(lead + (rows * span,)), edge + [(rows - 1, 1)])
    return flat.reshape(lead + (rows, span + 1))[..., :span]


def tile_scores(content_rows, position_rows, key_rows, relative, row_start, key_start):
    rows = content_rows.shape[0]
    count = key_rows.shape[0]
    scale = content_rows.shape[-1] ** (-0.5)
    content = jnp.einsum("qhe,khe->hqk", content_rows, key_rows, preferred_element_type=f32)
    wide = jnp.einsum("qhe,whe->hqw", position_rows, relative, preferred_element_type=f32)
    scores = (content + skew(wide, count)) * scale
    causal = (row_start + jnp.arange(rows))[:, None] >= (key_start + jnp.arange(count))[None, :]
    return (scores, causal[None])


def tile_forward(
    content_rows, position_rows, row_start, relative, key_rows, value_rows, key_start, state
):
    top, total, accum = state
    scores, causal = tile_scores(
        content_rows, position_rows, key_rows, relative, row_start, key_start
    )
    scores = jnp.where(causal, scores, neg_big)
    new_top = jnp.maximum(top, jnp.max(scores, axis=-1))
    raised = jnp.where(causal, jnp.exp(scores - new_top[..., None]), 0.0)
    fade = jnp.exp(top - new_top)
    total = total * fade + jnp.sum(raised, axis=-1)
    accum = accum * fade[..., None] + jnp.einsum(
        "hqk,khe->hqe", raised.astype(bf16), value_rows, preferred_element_type=f32
    )
    return (new_top, total, accum)


def tile_backward(
    content_rows,
    position_rows,
    row_start,
    relative,
    key_rows,
    value_rows,
    grad_rows,
    log_rows,
    delta_rows,
    key_start,
):
    scores, causal = tile_scores(
        content_rows, position_rows, key_rows, relative, row_start, key_start
    )
    scale = content_rows.shape[-1] ** (-0.5)
    shares = jnp.where(causal, jnp.exp(scores - log_rows[..., None]), 0.0)
    share_grad = jnp.einsum("qhe,khe->hqk", grad_rows, value_rows, preferred_element_type=f32)
    score_grad = (shares * (share_grad - delta_rows[..., None])).astype(bf16)
    content_grad = jnp.einsum("hqk,khe->qhe", score_grad, key_rows, preferred_element_type=f32)
    wide_grad = unskew(score_grad, relative.shape[0])
    position_grad = jnp.einsum("hqw,whe->qhe", wide_grad, relative, preferred_element_type=f32)
    table_part = jnp.einsum("hqw,qhe->whe", wide_grad, position_rows, preferred_element_type=f32)
    key_grad = jnp.einsum("hqk,qhe->khe", score_grad, content_rows, preferred_element_type=f32)
    value_grad = jnp.einsum(
        "hqk,qhe->khe", shares.astype(bf16), grad_rows, preferred_element_type=f32
    )
    return (
        content_grad * scale,
        position_grad * scale,
        table_part * scale,
        key_grad * scale,
        value_grad,
    )


def nest_tiles(tile_fn):
    inner = jax.vmap(tile_fn, in_axes=(0, 0, 0, 0, None, None, 0))
    return jax.vmap(inner, in_axes=(0, 0, None, None, 0, 0, 0))


def to_global(stored, inverse, block):
    seqs, seq_len, width = stored.shape
    blocks = stored.reshape(seqs, seq_len // block, block * width)
    chosen = (inverse[:, None] == jnp.arange(seq_len // block)[None, :]).astype(bf16)
    moved = jnp.einsum("gs,nsx->ngx", chosen, blocks, preferred_element_type=f32)
    return moved.astype(bf16).reshape(stored.shape)


class SplitQueries:

    def __init__(self, query, keys, values, biases, relative, block_order, inverse, block):
        self.seqs, self.tok_dev, self.width = keys.shape
        self.heads = self.width // HEAD_DIM
        self.block = block
        self.block_order = block_order
        ctx_count = lax.axis_size("ctx")
        self.seq_len = self.tok_dev * ctx_count
        self.key_len = min(512, self.seq_len)
        pad = jnp.zeros((self.key_len + block, self.width), bf16)
        table = jnp.concatenate([relative, pad], axis=0)
        self.table = table.reshape(-1, self.heads, HEAD_DIM)
        lead = (self.seqs, 2, block, self.heads, HEAD_DIM)
        self.content = (query + biases[0]).astype(bf16).reshape(lead)
        self.position = (query + biases[1]).astype(bf16).reshape(lead)
        gathered = [lax.all_gather(part, "ctx", axis=1, tiled=True) for part in (keys, values)]
        shape = (self.seqs, self.seq_len, self.heads, HEAD_DIM)
        self.keys, self.values = [to_global(part, inverse, block).reshape(shape) for part in gathered]
        self.starts = lax.dynamic_slice_in_dim(block_order, 2 * lax.axis_index("ctx"), 2, 0) * block

    def rows(self, index):
        start = index * self.key_len
        keys = lax.dynamic_slice_in_dim(self.keys, start, self.key_len, 1)
        values = lax.dynamic_slice_in_dim(self.values, start, self.key_len, 1)
        span = self.block + self.key_len
        offsets = [self.seq_len - self.block - self.starts[slot] + start for slot in range(2)]
        relative = [lax.dynamic_slice_in_dim(self.table, offset, span, 0) for offset in offsets]
        return start, keys, values, jnp.stack(relative), offsets

    def to_stored(self, part):
        count = self.seq_len // self.block
        blocks = part.reshape(self.seqs, count, self.block * self.width)
        chosen = (self.block_order[:, None] == jnp.arange(count)[None, :]).astype(f32)
        moved = jnp.einsum("sg,ngx->nsx", chosen, blocks, precision=highest)
        return moved.reshape(self.seqs, self.seq_len, self.width)

    def forward(self):
        def step(state, index):
            start, keys, values, relative, _ = self.rows(index)

            def tile(content, position, row_start, table, keys_seq, values_seq, tile_state):
                return tile_forward(
                    content, position, row_start, table, keys_seq, values_seq, start, tile_state
                )

            return nest_tiles(tile)(
                self.content, self.position, self.starts, relative, keys, values, state
            ), None

        shape = (self.seqs, 2, self.heads, self.block)
        state = (
            jnp.full(shape, neg_big, f32),
            jnp.zeros(shape, f32),
            jnp.zeros(shape + (HEAD_DIM,), f32),
        )
        (top, total, accum), _ = lax.scan(step, state, jnp.arange(self.seq_len // self.key_len))
        self.log_total = top + jnp.log(total)
        self.out = accum / total[..., None]
        moved = jnp.transpose(self.out, (0, 1, 3, 2, 4))
        return moved.reshape(self.seqs * self.tok_dev, self.width).astype(bf16)

    def backward(self, grad):
        block, seq_len, key_len = self.block, self.seq_len, self.key_len
        lead = (self.seqs, 2, block, self.heads, HEAD_DIM)
        grad = grad.reshape(lead)
        delta = jnp.einsum("sbqhe,sbhqe->sbhq", grad.astype(f32), self.out)
        def step(carry, index):
            start, keys, values, relative, offsets = self.rows(index)

            def tile(content, position, row_start, table, keys_seq, values_seq, extra):
                return tile_backward(
                    content, position, row_start, table, keys_seq, values_seq, *extra, start
                )

            extra = (grad, self.log_total, delta)
            parts = nest_tiles(tile)(
                self.content, self.position, self.starts, relative, keys, values, extra
            )
            table = carry[2]
            table_sum = jnp.sum(parts[2], axis=0)
            for slot in range(2):
                offset = offsets[slot]
                current = lax.dynamic_slice_in_dim(table, offset, block + key_len, 0)
                table = lax.dynamic_update_slice_in_dim(table, current + table_sum[slot], offset, 0)
            sums = []
            for total, part in zip(carry[3:], parts[3:]):
                current = lax.dynamic_slice_in_dim(total, start, key_len, 1)
                part = current + jnp.sum(part, axis=1)
                sums.append(lax.dynamic_update_slice_in_dim(total, part, start, 1))
            key_acc, value_acc = sums
            return (carry[0] + parts[0], carry[1] + parts[1], table, key_acc, value_acc), None

        zero_tiles = jnp.zeros(lead, f32)
        zero_keys = jnp.zeros((self.seqs, seq_len, self.heads, HEAD_DIM), f32)
        carry = (zero_tiles, zero_tiles, jnp.zeros(self.table.shape, f32), zero_keys, zero_keys)
        carry, _ = lax.scan(step, carry, jnp.arange(seq_len // key_len))
        owned = [
            lax.psum_scatter(
                self.to_stored(part), "ctx", scatter_dimension=1, tiled=True
            )
            for part in carry[3:]
        ]
        flat = (self.seqs * self.tok_dev, self.width)
        query_grad = (carry[0] + carry[1]).reshape(flat).astype(bf16)
        key_grad, value_grad = [part.reshape(flat).astype(bf16) for part in owned]
        bias_grads = jnp.stack(
            [jnp.sum(part, axis=(0, 1, 2)).reshape(self.width) for part in carry[:2]]
        )
        table_grad = carry[2].reshape(-1, self.width)[:seq_len]
        return query_grad, key_grad, value_grad, bias_grads, table_grad


def local(
    tokens,
    neighbours,
    teacher,
    valid_mask,
    block_order,
    query_weight,
    key_weight,
    value_weight,
    output_weight,
    relative_weight,
    content_bias,
    position_bias,
    cross_query_weight,
    cross_key_weight,
    cross_value_weight,
    cross_output_weight,
    up_weight,
    down_weight,
    attention_gain,
    cross_gain,
    feedforward_gain,
):
    places = lax.axis_size("wa")
    ctx_count = lax.axis_size("ctx")
    place = lax.axis_index("wa")
    here = lax.axis_index("ctx")
    _, tok_dev, width = tokens.shape
    seq_len = tok_dev * ctx_count
    block = tok_dev // 2
    cols = HEADS * HEAD_DIM // places
    rows = places * tok_dev
    pairs = cols // 128
    by_heads = places * pairs == ctx_count and seq_len % TILE == 0

    token_parts = gather_parts(tokens[0])
    query_cols, key_cols, value_cols = [
        take_columns(weight) for weight in (query_weight, key_weight, value_weight)
    ]
    relative_cols = take_columns(relative_weight)
    gains = lax.all_gather(
        jnp.stack([attention_gain, cross_gain, feedforward_gain]), "wa", axis=1, tiled=True
    ).astype(f32)
    gain_one, gain_two, gain_three = gains[0:1], gains[1:2], gains[2:3]
    cross_query_cols, cross_key_cols, cross_value_cols = [
        take_columns(weight) for weight in (cross_query_weight, cross_key_weight, cross_value_weight)
    ]
    cross_pair_cols = jnp.concatenate([cross_key_cols, cross_value_cols], axis=1)
    near_rows = jnp.concatenate(gather_parts(neighbours.reshape(-1, width)), axis=0)
    up_cols = take_columns(up_weight)
    valid = valid_mask.astype(f32).reshape(tok_dev, 1)
    count = jnp.sum(valid).reshape(1, 1)
    count = all_summed(all_summed(count, "wa"), "ctx")

    slots = jnp.arange(2 * ctx_count)
    inverse = jnp.sum(jnp.where(block_order[None, :] == slots[:, None], slots[None, :], 0), axis=1)
    inverse = inverse.astype(jnp.int32)
    distance = (seq_len - 1 - jnp.arange(seq_len)).astype(f32)
    waves = sinusoid(distance, width).astype(bf16)

    hidden_all = jnp.concatenate(token_parts, axis=0).astype(f32)
    scale_all = inverse_rms(hidden_all)
    normed_a = (hidden_all * scale_all * gain_one).astype(bf16)
    biases = jnp.stack([content_bias, position_bias]).astype(f32)
    if by_heads:
        which = here % pairs
        mixed_cols = jnp.concatenate(
            [
                part[:, 128 * pair : 128 * (pair + 1)]
                for pair in range(pairs)
                for part in (query_cols, key_cols, value_cols)
            ],
            axis=1,
        )
        qkv = dot_nn(normed_a, mixed_cols).astype(bf16)
        qkv = qkv.reshape(places, tok_dev, pairs, 384).transpose(0, 2, 1, 3)
        qkv = qkv.reshape(ctx_count, tok_dev, 384)
        qkv = lax.all_to_all(qkv, "ctx", split_axis=0, concat_axis=0, tiled=True)
        qkv = qkv.reshape(seq_len, 384)
        my_relative = lax.dynamic_slice_in_dim(relative_cols, which * 128, 128, 1)
        table = dot_nn(waves, my_relative).astype(bf16)
        table = jnp.concatenate([table, jnp.zeros((TILE, 128), bf16)], axis=0)
        my_biases = lax.dynamic_slice_in_dim(biases, which * 128, 128, 1)
        my_biases = jnp.concatenate([my_biases, jnp.zeros((6, 128), f32)], axis=0)
        out = attend_forward(inverse, qkv, table, my_biases, block)
        out = lax.all_to_all(
            out.reshape(ctx_count, tok_dev, 128), "ctx", split_axis=0, concat_axis=0, tiled=True
        )
        out = out.reshape(places, pairs, tok_dev, 128).transpose(0, 2, 1, 3)
        attended = out.reshape(rows, cols)
    else:
        mixed_cols = jnp.concatenate([query_cols, key_cols, value_cols], axis=1)
        qkv = dot_nn(normed_a, mixed_cols).reshape(places, tok_dev, 3 * cols)
        relative = dot_nn(waves, relative_cols).astype(bf16)
        general = SplitQueries(
            qkv[..., :cols],
            qkv[..., cols : 2 * cols].astype(bf16),
            qkv[..., 2 * cols :].astype(bf16),
            biases,
            relative,
            block_order,
            inverse,
            block,
        )
        attended = general.forward()

    def to_owner(product):
        return scatter_parts([product[r * tok_dev : (r + 1) * tok_dev] for r in range(places)])

    def from_all(value):
        return jnp.concatenate(gather_parts(value), axis=0)

    hidden_in = tokens[0].astype(f32)
    hidden_one = hidden_in + to_owner(dot_nn(attended, output_weight))

    scale_two = inverse_rms(hidden_one)
    normed_b = from_all((hidden_one * scale_two * gain_two).astype(bf16))
    cross_q = dot_nn(normed_b, cross_query_cols).astype(bf16)
    cross_pair = dot_nn(near_rows, cross_pair_cols).astype(bf16)
    crossed = cross_forward(cross_q, cross_pair)
    hidden_two = hidden_one + to_owner(dot_nn(crossed, cross_output_weight))

    scale_three = inverse_rms(hidden_two)
    normed_c = from_all((hidden_two * scale_three * gain_three).astype(bf16))
    pre_act = dot_nn(normed_c, up_cols)
    activated = gelu_tanh(pre_act).astype(bf16)
    layer_out = hidden_two + to_owner(dot_nn(activated, down_weight))

    error = layer_out - teacher[0].astype(f32)
    error_sum = jnp.sum(valid * error * error).reshape(1, 1)
    error_sum = all_summed(all_summed(error_sum, "wa"), "ctx")
    loss = (error_sum / (2.0 * count * width)).reshape(())
    out_grad = (places * seq_len) / count * valid * error

    out_low = from_all(out_grad.astype(bf16))
    act_grad = dot_nt(out_low, down_weight)
    _, gelu_pull = jax.vjp(gelu_tanh, pre_act)
    pre_grad = gelu_pull(act_grad)[0].astype(bf16)
    down_grad = dot_tn(activated, out_low).astype(bf16)
    up_grad = dot_tn(normed_c, pre_grad).astype(bf16)
    normed_c_grad = to_owner(dot_nt(pre_grad, up_cols))
    two_grad = out_grad + norm_pull(hidden_two, scale_three, gain_three, normed_c_grad)
    gain_three_grad = jnp.sum(normed_c_grad * hidden_two * scale_three, axis=0, keepdims=True)
    down_out = sum_row_grads(down_grad)
    up_out = sum_column_grads(up_grad[None])[0]

    two_low = from_all(two_grad.astype(bf16))
    crossed_grad = dot_nt(two_low, cross_output_weight).astype(bf16)
    cross_q_grad, cross_pair_grad = cross_backward(cross_q, cross_pair, crossed_grad)
    normed_b_grad = to_owner(dot_nt(cross_q_grad, cross_query_cols))
    one_grad = two_grad + norm_pull(hidden_one, scale_two, gain_two, normed_b_grad)
    gain_two_grad = jnp.sum(normed_b_grad * hidden_one * scale_two, axis=0, keepdims=True)
    cross_output_grad = dot_tn(crossed, two_low).astype(bf16)
    cross_query_grad = dot_tn(normed_b, cross_q_grad).astype(bf16)
    cross_key_grad = dot_tn(near_rows, cross_pair_grad[:, :cols]).astype(bf16)
    cross_value_grad = dot_tn(near_rows, cross_pair_grad[:, cols:]).astype(bf16)
    cross_output_out = sum_row_grads(cross_output_grad)
    cross_out = sum_column_grads(jnp.stack([cross_key_grad, cross_value_grad]))
    cross_query_out = sum_column_grads(cross_query_grad[None])[0]
    near_grad = dot_nt(cross_pair_grad, cross_pair_cols)
    near_count = near_rows.shape[0] // places
    near_grad = scatter_parts(
        [near_grad[r * near_count : (r + 1) * near_count] for r in range(places)]
    )
    neighbours_grad = near_grad.reshape(neighbours.shape)

    one_low = from_all(one_grad.astype(bf16))
    attended_grad = dot_nt(one_low, output_weight).astype(bf16)
    output_grad = dot_tn(attended, one_low).astype(bf16)
    output_out = sum_row_grads(output_grad)
    if by_heads:
        grad = attended_grad.reshape(places, tok_dev, pairs, 128).transpose(0, 2, 1, 3)
        grad = grad.reshape(ctx_count, tok_dev, 128)
        grad = lax.all_to_all(grad, "ctx", split_axis=0, concat_axis=0, tiled=True)
        grad = grad.reshape(seq_len, 128)
        qkv_grad, table_grad, bias_part = attend_backward(
            inverse, qkv, table, my_biases, grad, block
        )
        qkv_grad = lax.all_to_all(
            qkv_grad.reshape(ctx_count, tok_dev, 384), "ctx", split_axis=0, concat_axis=0, tiled=True
        )
        qkv_grad = qkv_grad.reshape(places, pairs, tok_dev, 384).transpose(0, 2, 1, 3)
        qkv_grad = qkv_grad.reshape(rows, 3 * cols)
        bias_grads = jnp.concatenate(
            [jnp.where(which == pair, bias_part[0:2], 0.0) for pair in range(pairs)], axis=1
        )
    else:
        query_grad, key_grad, value_grad, bias_grads, table_grad = general.backward(attended_grad)
        qkv_grad = jnp.concatenate([query_grad, key_grad, value_grad], axis=1)
    table_high = table_grad.astype(bf16)
    table_low = (table_grad - table_high.astype(f32)).astype(bf16)
    relative_grad = (dot_tn(waves, table_high) + dot_tn(waves, table_low)).astype(bf16)
    mixed_grad = dot_tn(normed_a, qkv_grad).astype(bf16)
    if by_heads:
        relative_grad = jnp.concatenate(
            [jnp.where(which == pair, relative_grad, 0.0) for pair in range(pairs)], axis=1
        )
        whole = [
            jnp.concatenate(
                [
                    mixed_grad[:, 384 * pair + 128 * m : 384 * pair + 128 * (m + 1)]
                    for pair in range(pairs)
                ],
                axis=1,
            )
            for m in range(3)
        ]
    else:
        whole = [mixed_grad[:, m * cols : (m + 1) * cols] for m in range(3)]
    attention_out = sum_column_grads(jnp.stack(whole + [relative_grad]))
    normed_a_part = dot_nt(qkv_grad, mixed_cols)
    gain_one_part = jnp.sum(normed_a_part * hidden_all * scale_all, axis=0, keepdims=True)
    normed_a_grad = to_owner(normed_a_part)
    tokens_grad = one_grad + norm_pull(hidden_in, scale_all[:tok_dev], gain_one, normed_a_grad)

    gain_grads = jnp.concatenate([gain_one_part, gain_two_grad, gain_three_grad], axis=0)
    gain_grads = all_summed(gain_grads, "wa")
    share = width // places
    gain_grads = lax.dynamic_slice_in_dim(gain_grads, place * share, share, 1)
    small = jnp.concatenate([gain_grads.reshape(1, -1), bias_grads.reshape(1, -1)], axis=1)
    small = all_summed(small, "ctx")[0]
    gain_out = small[: 3 * share].reshape(3, share)
    bias_out = small[3 * share :].reshape(2, cols)

    return (
        layer_out[None],
        loss,
        tokens_grad[None],
        neighbours_grad,
        attention_out[0],
        attention_out[1],
        attention_out[2],
        output_out,
        attention_out[3],
        bias_out[0],
        bias_out[1],
        cross_query_out,
        cross_out[0],
        cross_out[1],
        cross_output_out,
        up_out,
        down_out,
        gain_out[0],
        gain_out[1],
        gain_out[2],
    )


def solution(mesh):
    row = P("wa", None)
    flat = P("wa")
    in_specs = (
        P("wa", "ctx", None),
        P("wa", "ctx", None, None),
        P("wa", "ctx", None),
        P("wa", "ctx"),
        P(),
        row,
        row,
        row,
        row,
        row,
        flat,
        flat,
        row,
        row,
        row,
        row,
        row,
        row,
        flat,
        flat,
        flat,
    )
    out_specs = (
        P("wa", "ctx", None),
        P(),
        P("wa", "ctx", None),
        P("wa", "ctx", None, None),
        row,
        row,
        row,
        row,
        row,
        flat,
        flat,
        row,
        row,
        row,
        row,
        row,
        row,
        flat,
        flat,
        flat,
    )
    return jax.shard_map(local, mesh=mesh, in_specs=in_specs, out_specs=out_specs, check_vma=False)
```

```python
import functools

import jax
import jax.numpy as jnp
from jax import lax
from jax.experimental import pallas as pl
from jax.experimental.pallas import tpu as pltpu
from jax.sharding import PartitionSpec as P

HEADS = 16
HEAD_DIM = 64
GROUP = 64
NK = 256
TILE = 128

eps_norm = 1e-06
neg_big = -1e30
highest = lax.Precision.HIGHEST
f32 = jnp.float32
bf16 = jnp.bfloat16


def inverse_rms(hidden):
    return lax.rsqrt(jnp.mean(hidden * hidden, axis=-1, keepdims=True) + eps_norm)


def norm_pull(hidden, scale, gain, grad):
    scaled = grad * gain
    mean = jnp.mean(hidden * scaled, axis=-1, keepdims=True)
    return scale * scaled - hidden * (scale * scale * scale) * mean


def gelu_tanh(value):
    return jax.nn.gelu(value, approximate=True)


def sinusoid(distance, width):
    half = width // 2
    freq = jnp.exp(-jnp.log(10000.0) * jnp.arange(half, dtype=f32) * 2.0 / width)
    angle = distance[:, None] * freq[None, :]
    return jnp.concatenate([jnp.sin(angle), jnp.cos(angle)], axis=1)


def dot_nn(a, b):
    return lax.dot_general(a, b, (((1,), (0,)), ((), ())), preferred_element_type=f32)


def dot_nt(a, b):
    return lax.dot_general(a, b, (((1,), (1,)), ((), ())), preferred_element_type=f32)


def dot_tn(a, b):
    return lax.dot_general(a, b, (((0,), (0,)), ((), ())), preferred_element_type=f32)


def swap(value, axis, bit):
    pairs = [(i, i ^ bit) for i in range(lax.axis_size(axis))]
    return lax.ppermute(value, axis, pairs)


def bits_of(axis):
    bits, bit = [], 1
    while bit < lax.axis_size(axis):
        bits.append(bit)
        bit *= 2
    return bits


def my_bit(axis, bit):
    return (lax.axis_index(axis) // bit) % 2


def ordered(bit, own, other, dim):
    return jnp.where(
        bit == 0,
        jnp.concatenate([own, other], axis=dim),
        jnp.concatenate([other, own], axis=dim),
    )


def split(value, bit, dim):
    half = value.shape[dim] // 2
    keep = lax.dynamic_slice_in_dim(value, bit * half, half, dim)
    send = lax.dynamic_slice_in_dim(value, (1 - bit) * half, half, dim)
    return keep, send


def gather_parts(value):
    parts = {0: value}
    for bit in reversed(bits_of("wa")):
        parts.update({r | bit: swap(part, "wa", bit) for r, part in list(parts.items())})
    return [parts[r] for r in sorted(parts)]


def scatter_parts(parts):
    parts = dict(enumerate(parts))
    for bit in bits_of("wa"):
        kept = {}
        for r, part in parts.items():
            if not r & bit:
                got = swap(parts[r | bit].astype(bf16), "wa", bit)
                kept[r] = part + got.astype(f32)
        parts = kept
    return parts[0]


def take_columns(weight):
    value = weight[None]
    for bit in reversed(bits_of("wa")):
        mine = my_bit("wa", bit)
        keep, send = split(value, mine, 2)
        value = ordered(mine, keep[:, None], swap(send, "wa", bit)[:, None], 1)
        value = value.reshape((-1,) + value.shape[2:])
    return value.reshape(-1, value.shape[-1])


def spread_columns(value):
    for bit in bits_of("wa"):
        mine = my_bit("wa", bit)
        paired = value.reshape((value.shape[0], value.shape[1] // 2, 2) + value.shape[2:])
        keep, send = split(paired, mine, 2)
        value = ordered(mine, keep[:, :, 0], swap(send[:, :, 0], "wa", bit), 3)
    return value[:, 0]


def halving_dim(shape):
    if shape[-2] % 16 == 0:
        return len(shape) - 2
    if shape[0] % 2 == 0:
        return 0
    if shape[-2] % 2 == 0:
        return len(shape) - 2
    return len(shape) - 1


def sum_over_ctx(value, bits, finish):
    dims = []
    for bit in bits:
        dim = halving_dim(value.shape)
        keep, send = split(value, my_bit("ctx", bit), dim)
        value = (keep.astype(f32) + swap(send, "ctx", bit).astype(f32)).astype(bf16)
        dims.append(dim - value.ndim if dim else 0)
    value = finish(value)
    for bit, dim in reversed(list(zip(bits, dims))):
        dim = dim % value.ndim
        value = ordered(my_bit("ctx", bit), value, swap(value, "ctx", bit), dim)
    return value


def all_summed(value, axis):
    for bit in bits_of(axis):
        value = value + swap(value, axis, bit)
    return value


def sum_column_grads(grads):
    places = lax.axis_size("wa")
    grads = grads.reshape(grads.shape[0], places, grads.shape[1] // places, grads.shape[2])
    bits = bits_of("ctx")
    if grads.shape[2] % lax.axis_size("ctx") == 0:
        return sum_over_ctx(grads, bits, spread_columns).astype(f32)
    return sum_over_ctx(spread_columns(grads), bits, lambda value: value).astype(f32)


def sum_row_grads(grads):
    return sum_over_ctx(grads[None], bits_of("ctx"), lambda value: value)[0].astype(f32)


def first_half(shape):
    return lax.broadcasted_iota(jnp.int32, shape, 1) < HEAD_DIM


def stack_heads(rows):
    mask = first_half(rows.shape)
    zero = jnp.zeros_like(rows)
    return jnp.concatenate([jnp.where(mask, rows, zero), jnp.where(mask, zero, rows)], axis=0)


def join_heads(stacked):
    rows = stacked.shape[0] // 2
    return jnp.where(first_half((rows, stacked.shape[1])), stacked[:rows], stacked[rows:])


def copy_blocks(order_ref, source, target, block, inward):
    for place in range(source.shape[0] // block):
        start = pl.multiple_of(order_ref[place] * block, block)
        if inward:
            target[place * block : (place + 1) * block, :] = source[pl.ds(start, block), :]
        else:
            target[pl.ds(start, block), :] = source[place * block : (place + 1) * block, :]


def attention_shares(content, position, key_ref, rel_ref, row_start, seq_len):
    length = row_start + TILE
    wide_len = length + TILE
    offset = seq_len - TILE - row_start
    scale = HEAD_DIM ** (-0.5)
    scores = dot_nt(content, key_ref[0:length, :])
    wide = dot_nt(position, rel_ref[offset : offset + wide_len, :])
    halves = []
    for head in range(2):
        part = wide[head * TILE : (head + 1) * TILE]
        turned = pltpu.roll(part, wide_len - (TILE - 1), 1, stride=1, stride_axis=0)
        halves.append(turned[:, :length])
    scores = (scores + jnp.concatenate(halves, axis=0)) * scale
    row = lax.broadcasted_iota(jnp.int32, scores.shape, 0) % TILE + row_start
    col = lax.broadcasted_iota(jnp.int32, scores.shape, 1)
    scores = jnp.where(col <= row, scores, neg_big)
    top = jnp.max(scores, axis=1, keepdims=True)
    raised = jnp.exp(scores - top)
    total = jnp.sum(raised, axis=1, keepdims=True)
    return raised * (1.0 / total)


def attend_forward_kernel(seq_len, block, order_ref, qkv_ref, rel_ref, bias_ref, out_ref, qkv, out):
    copy_blocks(order_ref, qkv_ref, qkv, block, True)
    keys = qkv.at[:, 128:256]
    values = qkv.at[:, 256:384]
    content_bias = bias_ref[0:1, :]
    position_bias = bias_ref[1:2, :]
    for tile in range(seq_len // TILE):
        start = tile * TILE
        query = qkv[start : start + TILE, 0:128].astype(f32)
        content = stack_heads((query + content_bias).astype(bf16))
        position = stack_heads((query + position_bias).astype(bf16))
        shares = attention_shares(content, position, keys, rel_ref, start, seq_len)
        got = dot_nn(shares.astype(bf16), values[0 : start + TILE, :])
        out[start : start + TILE, :] = join_heads(got).astype(bf16)
    copy_blocks(order_ref, out, out_ref, block, False)


def attend_backward_kernel(
    seq_len,
    block,
    order_ref,
    qkv_ref,
    rel_ref,
    bias_ref,
    grad_ref,
    dqkv_ref,
    drel_ref,
    dbias_ref,
    qkv,
    grad,
    dqkv,
    dkey,
    dvalue,
    drel,
):
    scale = HEAD_DIM ** (-0.5)
    copy_blocks(order_ref, qkv_ref, qkv, block, True)
    copy_blocks(order_ref, grad_ref, grad, block, True)
    keys = qkv.at[:, 128:256]
    values = qkv.at[:, 256:384]
    content_bias = bias_ref[0:1, :]
    position_bias = bias_ref[1:2, :]
    dkey[...] = jnp.zeros_like(dkey)
    dvalue[...] = jnp.zeros_like(dvalue)
    drel[...] = jnp.zeros_like(drel)
    row = lax.broadcasted_iota(jnp.int32, (TILE, TILE), 0)
    col = lax.broadcasted_iota(jnp.int32, (TILE, TILE), 1)
    flip = jnp.where(row + col == TILE - 1, 1.0, 0.0).astype(bf16)
    content_sum = jnp.zeros((1, 128), f32)
    position_sum = jnp.zeros((1, 128), f32)
    for tile in range(seq_len // TILE):
        start = tile * TILE
        length = start + TILE
        wide_len = length + TILE
        offset = seq_len - TILE - start
        query = qkv[start : start + TILE, 0:128].astype(f32)
        content = stack_heads((query + content_bias).astype(bf16))
        plain = (query + position_bias).astype(bf16)
        position = stack_heads(plain)
        shares = attention_shares(content, position, keys, rel_ref, start, seq_len)
        out_grad = stack_heads(grad[start : start + TILE, :])
        share_grad = dot_nt(out_grad, values[0:length, :])
        delta = jnp.sum(shares * share_grad, axis=1, keepdims=True)
        score_grad = (shares * (share_grad - delta)).astype(bf16)
        content_grad = join_heads(dot_nn(score_grad, keys[0:length, :])) * scale
        parts = []
        for head in range(2):
            turned = dot_nn(flip, score_grad[head * TILE : (head + 1) * TILE])
            turned = jnp.concatenate([turned, jnp.zeros((TILE, TILE), f32)], axis=1)
            parts.append(pltpu.roll(turned, 0, 1, stride=1, stride_axis=0))
        wide_grad = jnp.concatenate(parts, axis=0).astype(bf16)
        relative = rel_ref[offset : offset + wide_len, :]
        turned_grad = join_heads(dot_nn(wide_grad, relative)) * scale
        turned_rows = stack_heads(dot_nn(flip, plain).astype(bf16))
        drel[offset : offset + wide_len, :] += dot_tn(wide_grad, turned_rows)
        high = turned_grad.astype(bf16)
        low = (turned_grad - high.astype(f32)).astype(bf16)
        position_grad = dot_nn(flip, high) + dot_nn(flip, low)
        content_sum += jnp.sum(content_grad, axis=0, keepdims=True)
        position_sum += jnp.sum(turned_grad, axis=0, keepdims=True)
        dqkv[start : start + TILE, 0:128] = (content_grad + position_grad).astype(bf16)
        dkey[0:length, :] += dot_tn(score_grad, content)
        dvalue[0:length, :] += dot_tn(shares.astype(bf16), out_grad)
    dqkv[:, 128:256] = (dkey[...] * scale).astype(bf16)
    dqkv[:, 256:384] = dvalue[...].astype(bf16)
    copy_blocks(order_ref, dqkv, dqkv_ref, block, False)
    drel_ref[...] = drel[0:seq_len, :] * scale
    dbias_ref[...] = jnp.concatenate(
        [content_sum, position_sum, jnp.zeros((6, 128), f32)], axis=0
    )


in_vmem = pl.BlockSpec(memory_space=pltpu.VMEM)
in_smem = pl.BlockSpec(memory_space=pltpu.SMEM)


def attend_forward(order, qkv, rel, bias, block):
    rows = qkv.shape[0]
    return pl.pallas_call(
        functools.partial(attend_forward_kernel, rows, block),
        out_shape=jax.ShapeDtypeStruct((rows, 128), bf16),
        in_specs=[in_smem, in_vmem, in_vmem, in_vmem],
        out_specs=in_vmem,
        scratch_shapes=[pltpu.VMEM((rows, 384), bf16), pltpu.VMEM((rows, 128), bf16)],
        compiler_params=pltpu.CompilerParams(vmem_limit_bytes=40 * 2**20),
        cost_estimate=pl.CostEstimate(
            flops=4 * 256 * rows * rows * 2, bytes_accessed=rows * 1300, transcendentals=rows * rows
        ),
        name="attend_forward",
    )(order, qkv, rel, bias)


def attend_backward(order, qkv, rel, bias, grad, block):
    rows = qkv.shape[0]
    return pl.pallas_call(
        functools.partial(attend_backward_kernel, rows, block),
        out_shape=[
            jax.ShapeDtypeStruct((rows, 384), bf16),
            jax.ShapeDtypeStruct((rows, 128), f32),
            jax.ShapeDtypeStruct((8, 128), f32),
        ],
        in_specs=[in_smem, in_vmem, in_vmem, in_vmem, in_vmem],
        out_specs=[in_vmem, in_vmem, in_vmem],
        scratch_shapes=[
            pltpu.VMEM((rows, 384), bf16),
            pltpu.VMEM((rows, 128), bf16),
            pltpu.VMEM((rows, 384), bf16),
            pltpu.VMEM((rows, 128), f32),
            pltpu.VMEM((rows, 128), f32),
            pltpu.VMEM((rows + TILE, 128), f32),
        ],
        compiler_params=pltpu.CompilerParams(vmem_limit_bytes=40 * 2**20),
        cost_estimate=pl.CostEstimate(
            flops=10 * 256 * rows * rows * 2, bytes_accessed=rows * 3000, transcendentals=rows * rows
        ),
        name="attend_backward",
    )(order, qkv, rel, bias, grad)


def head_mask(shape, head):
    lane = lax.broadcasted_iota(jnp.int32, shape, 1)
    return (lane >= head * HEAD_DIM) & (lane < (head + 1) * HEAD_DIM)


def stack_all(rows):
    zero = jnp.zeros_like(rows)
    heads = rows.shape[1] // HEAD_DIM
    return jnp.concatenate(
        [jnp.where(head_mask(rows.shape, head), rows, zero) for head in range(heads)], axis=0
    )


def join_all(stacked):
    heads = stacked.shape[1] // HEAD_DIM
    rows = stacked.shape[0] // heads
    out = jnp.zeros((rows, stacked.shape[1]), stacked.dtype)
    for head in range(heads):
        part = stacked[head * rows : (head + 1) * rows]
        out = jnp.where(head_mask(part.shape, head), part, out)
    return out


def cross_shares(query, keys):
    scores = dot_nt(query, keys) * (HEAD_DIM ** (-0.5))
    raised = jnp.exp(scores - jnp.max(scores, axis=1, keepdims=True))
    return raised / jnp.sum(raised, axis=1, keepdims=True)


def cross_forward_kernel(q_ref, kv_ref, out_ref):
    width = q_ref.shape[1]
    shares = cross_shares(stack_all(q_ref[...]), kv_ref[:, 0:width])
    out_ref[...] = join_all(dot_nn(shares.astype(bf16), kv_ref[:, width:])).astype(bf16)


def cross_backward_kernel(q_ref, kv_ref, grad_ref, dq_ref, dkv_ref):
    width = q_ref.shape[1]
    scale = HEAD_DIM ** (-0.5)
    keys = kv_ref[:, 0:width]
    query = stack_all(q_ref[...])
    grad = stack_all(grad_ref[...])
    shares = cross_shares(query, keys)
    share_grad = dot_nt(grad, kv_ref[:, width:])
    delta = jnp.sum(shares * share_grad, axis=1, keepdims=True)
    score_grad = (shares * (share_grad - delta)).astype(bf16)
    dq_ref[...] = (join_all(dot_nn(score_grad, keys)) * scale).astype(bf16)
    dkv_ref[:, 0:width] = (dot_tn(score_grad, query) * scale).astype(bf16)
    dkv_ref[:, width:] = dot_tn(shares.astype(bf16), grad).astype(bf16)


def cross_forward(query, pair):
    width = query.shape[1]
    groups = query.shape[0] // GROUP
    return pl.pallas_call(
        cross_forward_kernel,
        out_shape=jax.ShapeDtypeStruct(query.shape, bf16),
        grid=(groups,),
        in_specs=[
            pl.BlockSpec((GROUP, width), lambda g: (g, 0)),
            pl.BlockSpec((NK, 2 * width), lambda g: (g, 0)),
        ],
        out_specs=pl.BlockSpec((GROUP, width), lambda g: (g, 0)),
        cost_estimate=pl.CostEstimate(
            flops=groups * 4 * 256 * 256 * 256, bytes_accessed=groups * 330000, transcendentals=groups * 65536
        ),
        name="cross_forward",
    )(query, pair)


def cross_backward(query, pair, grad):
    width = query.shape[1]
    groups = query.shape[0] // GROUP
    return pl.pallas_call(
        cross_backward_kernel,
        out_shape=[
            jax.ShapeDtypeStruct(query.shape, bf16),
            jax.ShapeDtypeStruct(pair.shape, bf16),
        ],
        grid=(groups,),
        in_specs=[
            pl.BlockSpec((GROUP, width), lambda g: (g, 0)),
            pl.BlockSpec((NK, 2 * width), lambda g: (g, 0)),
            pl.BlockSpec((GROUP, width), lambda g: (g, 0)),
        ],
        out_specs=[
            pl.BlockSpec((GROUP, width), lambda g: (g, 0)),
            pl.BlockSpec((NK, 2 * width), lambda g: (g, 0)),
        ],
        cost_estimate=pl.CostEstimate(
            flops=groups * 10 * 256 * 256 * 256, bytes_accessed=groups * 660000, transcendentals=groups * 65536
        ),
        name="cross_backward",
    )(query, pair, grad)


mesh_id = pl.DeviceIdType.MESH


def signal_to(barrier, ctx, wa):
    pl.semaphore_signal(barrier, inc=1, device_id=(ctx, wa), device_id_type=mesh_id)


def tree_sum(values):
    while len(values) > 1:
        values = [a + b for a, b in zip(values[::2], values[1::2])]
    return values[0]


def gather_kernel(
    parts,
    block_ref,
    small_ref,
    *refs,
):
    part_refs = refs[:parts]
    out_ref, total_ref = refs[parts : parts + 2]
    part_outs = refs[parts + 2 : 2 * parts + 2]
    near, far, y_send, y_recv, r_send, r_recv, l_send, l_recv, s_send, s_recv, p_send, p_recv, o_sem = refs[
        2 * parts + 2 :
    ]
    c = lax.axis_index("ctx")
    w = lax.axis_index("wa")
    z = c // 2
    right = z < 3
    left = z > 0
    barrier = pltpu.get_barrier_semaphore()
    for j in range(1, 8):
        signal_to(barrier, c ^ j, w)
    for j in range(1, 4):
        signal_to(barrier, c, w ^ j)
    pl.semaphore_wait(barrier, 10)

    def small_copy(source, j):
        wide = j < 4
        return pltpu.make_async_remote_copy(
            src_ref=source,
            dst_ref=near.at[j] if wide else far.at[j - 3],
            send_sem=s_send.at[j],
            recv_sem=s_recv.at[j],
            device_id=(c, w ^ j) if wide else (c ^ (j - 3), w),
            device_id_type=mesh_id,
        )

    for j in range(1, 4):
        small_copy(small_ref, j).start()

    def part_copy(m, j):
        return pltpu.make_async_remote_copy(
            src_ref=part_refs[m],
            dst_ref=part_outs[m].at[w],
            send_sem=p_send.at[m, j],
            recv_sem=p_recv.at[m, j],
            device_id=(c, w ^ j),
            device_id_type=mesh_id,
        )

    for m in reversed(range(parts)):
        for j in (1, 2, 3):
            part_copy(m, j).start()

    def y_copy(source, block, slot):
        return pltpu.make_async_remote_copy(
            src_ref=source,
            dst_ref=out_ref.at[block],
            send_sem=y_send.at[slot],
            recv_sem=y_recv.at[slot],
            device_id=(c ^ 1, w),
            device_id_type=mesh_id,
        )

    def z_copy(source, block, slot, step, send, recv):
        return pltpu.make_async_remote_copy(
            src_ref=source,
            dst_ref=out_ref.at[block],
            send_sem=send.at[slot],
            recv_sem=recv.at[slot],
            device_id=(c + step, w),
            device_id_type=mesh_id,
        )

    @pl.when(right)
    def _():
        z_copy(block_ref, c, 0, 2, r_send, r_recv).start()

    @pl.when(left)
    def _():
        z_copy(block_ref, c, 0, -2, l_send, l_recv).start()

    y_copy(block_ref, c, 0).start()
    own = [pltpu.make_async_copy(block_ref, out_ref.at[c], o_sem.at[0])]
    for m in range(parts):
        own.append(pltpu.make_async_copy(part_refs[m], part_outs[m].at[w], o_sem.at[1 + m]))
    for copy in own:
        copy.start()
    for j in range(1, 4):
        small_copy(small_ref, j).wait()
    total_ref[...] = tree_sum([small_ref[...]] + [near[j] for j in range(1, 4)])
    for j in range(4, 11):
        small_copy(total_ref, j).start()
    for t in range(3):

        @pl.when(z > t)
        def _(t=t):
            block = c - 2 * (t + 1)
            z_copy(out_ref.at[block], block, t, 2, r_send, r_recv).wait_recv()
            if t < 2:

                @pl.when(right)
                def _():
                    z_copy(out_ref.at[block], block, t + 1, 2, r_send, r_recv).start()

            y_copy(out_ref.at[block], block, t + 1).start()

        @pl.when(z < 3 - t)
        def _(t=t):
            block = c + 2 * (t + 1)
            z_copy(out_ref.at[block], block, t, -2, l_send, l_recv).wait_recv()
            if t < 2:

                @pl.when(left)
                def _():
                    z_copy(out_ref.at[block], block, t + 1, -2, l_send, l_recv).start()

            y_copy(out_ref.at[block], block, t + 4).start()

    for j in range(4, 11):
        small_copy(total_ref, j).wait()
    total_ref[...] = tree_sum([total_ref[...]] + [far[j] for j in range(1, 8)])
    y_copy(block_ref, c ^ 1, 0).wait()
    for t in range(3):

        @pl.when(z > t)
        def _(t=t):
            block = (c ^ 1) - 2 * (t + 1)
            y_copy(out_ref.at[block], block, t + 1).wait()

        @pl.when(z < 3 - t)
        def _(t=t):
            block = (c ^ 1) + 2 * (t + 1)
            y_copy(out_ref.at[block], block, t + 4).wait()

    @pl.when(right)
    def _():
        z_copy(block_ref, c, 0, 2, r_send, r_recv).wait_send()

    @pl.when(left)
    def _():
        z_copy(block_ref, c, 0, -2, l_send, l_recv).wait_send()

    for t in range(2):

        @pl.when(jnp.logical_and(z > t, right))
        def _(t=t):
            z_copy(block_ref, c, t + 1, 2, r_send, r_recv).wait_send()

        @pl.when(jnp.logical_and(z < 3 - t, left))
        def _(t=t):
            z_copy(block_ref, c, t + 1, -2, l_send, l_recv).wait_send()

    for m in range(parts):
        for j in range(1, 4):
            part_copy(m, j).wait_send()
            pltpu.make_async_remote_copy(
                src_ref=part_refs[m],
                dst_ref=part_outs[m].at[w ^ j],
                send_sem=p_send.at[m, j],
                recv_sem=p_recv.at[m, j],
                device_id=(c, w ^ j),
                device_id_type=mesh_id,
            ).wait_recv()
    for copy in own:
        copy.wait()


def gather_all(block, small, parts, collective_id):
    dma = pltpu.SemaphoreType.DMA
    count = len(parts)
    got = pl.pallas_call(
        functools.partial(gather_kernel, count),
        out_shape=[
            jax.ShapeDtypeStruct((8,) + block.shape, block.dtype),
            jax.ShapeDtypeStruct(small.shape, small.dtype),
        ]
        + [jax.ShapeDtypeStruct((4,) + part.shape, part.dtype) for part in parts],
        in_specs=[in_vmem] * (2 + count),
        out_specs=[in_vmem] * (2 + count),
        scratch_shapes=[
            pltpu.VMEM((4,) + small.shape, small.dtype),
            pltpu.VMEM((8,) + small.shape, small.dtype),
            dma((7,)),
            dma((7,)),
            dma((3,)),
            dma((3,)),
            dma((3,)),
            dma((3,)),
            dma((11,)),
            dma((11,)),
            dma((max(count, 1), 4)),
            dma((max(count, 1), 4)),
            dma((1 + count,)),
        ],
        compiler_params=pltpu.CompilerParams(
            collective_id=collective_id, has_side_effects=True, vmem_limit_bytes=40 * 2**20
        ),
        name="gather_all",
    )(block, small, *parts)
    return got[0], got[1], got[2:]


def swap_heads_kernel(outward, in_ref, out_ref, send_sem, recv_sem):
    c = lax.axis_index("ctx")
    w = lax.axis_index("wa")
    owner = c // 2
    half = c % 2
    own = owner == w
    other = jnp.logical_not(own)
    barrier = pltpu.get_barrier_semaphore()

    def lanes(start):
        return pl.ds(pl.multiple_of(start * 128, 128), 128)

    for j in range(1, 8):
        signal_to(barrier, c ^ j, owner)
    for r in range(4):
        for h in range(2):
            mine = jnp.logical_and(2 * w + h == c, r == 0)

            @pl.when(jnp.logical_not(mine))
            def _(r=r, h=h):
                signal_to(barrier, 2 * w + h, w ^ r)

    @pl.when(other)
    def _():
        signal_to(barrier, c, owner)

    pl.semaphore_wait(barrier, 16 - 2 * own.astype(jnp.int32))
    slot = w ^ owner
    if outward:

        def copy_to(j):
            return pltpu.make_async_remote_copy(
                src_ref=in_ref.at[c ^ j],
                dst_ref=out_ref.at[slot, :, lanes(half)],
                send_sem=send_sem.at[j],
                recv_sem=recv_sem.at[slot * 2 + half],
                device_id=(c ^ j, owner),
                device_id_type=mesh_id,
            )

        for j in range(7, 0, -1):
            copy_to(j).start()

        @pl.when(other)
        def _():
            copy_to(0).start()

        @pl.when(own)
        def _():
            pltpu.make_async_copy(
                in_ref.at[c], out_ref.at[slot, :, lanes(half)], recv_sem.at[slot * 2 + half]
            ).start()

        for r in range(4):
            for h in range(2):
                pltpu.make_async_remote_copy(
                    src_ref=in_ref.at[0],
                    dst_ref=out_ref.at[r, :, h * 128 : (h + 1) * 128],
                    send_sem=send_sem.at[0],
                    recv_sem=recv_sem.at[r * 2 + h],
                    device_id=(c ^ 1, w),
                    device_id_type=mesh_id,
                ).wait_recv()
        for j in range(1, 8):
            copy_to(j).wait_send()

        @pl.when(other)
        def _():
            copy_to(0).wait_send()

    else:

        def copy_to(r, h):
            return pltpu.make_async_remote_copy(
                src_ref=in_ref.at[r, :, h * 128 : (h + 1) * 128],
                dst_ref=out_ref.at[c],
                send_sem=send_sem.at[r * 2 + h],
                recv_sem=recv_sem.at[c],
                device_id=(2 * w + h, w ^ r),
                device_id_type=mesh_id,
            )

        for r in (3, 2, 1, 0):
            for h in range(2):
                mine = jnp.logical_and(2 * w + h == c, r == 0)

                @pl.when(jnp.logical_not(mine))
                def _(r=r, h=h):
                    copy_to(r, h).start()

                @pl.when(mine)
                def _(r=r, h=h):
                    pltpu.make_async_copy(
                        in_ref.at[r, :, h * 128 : (h + 1) * 128], out_ref.at[c], recv_sem.at[c]
                    ).start()

        for block in range(8):
            pltpu.make_async_remote_copy(
                src_ref=in_ref.at[0, :, 0:128],
                dst_ref=out_ref.at[block],
                send_sem=send_sem.at[0],
                recv_sem=recv_sem.at[block],
                device_id=(c ^ 1, w),
                device_id_type=mesh_id,
            ).wait_recv()
        for r in range(4):
            for h in range(2):
                mine = jnp.logical_and(2 * w + h == c, r == 0)

                @pl.when(jnp.logical_not(mine))
                def _(r=r, h=h):
                    copy_to(r, h).wait_send()


def swap_heads(value, outward, collective_id):
    rows = value.shape[1]
    shape = (4, rows, 256) if outward else (8, rows, 128)
    return pl.pallas_call(
        functools.partial(swap_heads_kernel, outward),
        out_shape=jax.ShapeDtypeStruct(shape, value.dtype),
        in_specs=[in_vmem],
        out_specs=in_vmem,
        scratch_shapes=[pltpu.SemaphoreType.DMA((8,)), pltpu.SemaphoreType.DMA((8,))],
        compiler_params=pltpu.CompilerParams(collective_id=collective_id, has_side_effects=True),
        name="swap_heads",
    )(value)


def blocks_to_columns_kernel(in_ref, out_ref, send_sem, recv_sem):
    c = lax.axis_index("ctx")
    w = lax.axis_index("wa")
    width = in_ref.shape[2]
    barrier = pltpu.get_barrier_semaphore()
    for j in range(1, 8):
        signal_to(barrier, c ^ j, w)
    pl.semaphore_wait(barrier, 7)

    def columns(block):
        return out_ref.at[:, pl.ds(pl.multiple_of(block * width, 128), width)]

    def copy_to(j, block):
        return pltpu.make_async_remote_copy(
            src_ref=in_ref.at[c ^ j],
            dst_ref=columns(block),
            send_sem=send_sem.at[j],
            recv_sem=recv_sem.at[j],
            device_id=(c ^ j, w),
            device_id_type=mesh_id,
        )

    for j in (4, 6, 5, 7, 2, 3, 1):
        copy_to(j, c).start()
    own = pltpu.make_async_copy(in_ref.at[c], columns(c), recv_sem.at[0])
    own.start()
    for j in range(1, 8):
        copy_to(j, c ^ j).wait_recv()
    for j in range(1, 8):
        copy_to(j, c).wait_send()
    own.wait()


def blocks_to_columns(value, collective_id):
    blocks, rows, width = value.shape
    return pl.pallas_call(
        blocks_to_columns_kernel,
        out_shape=jax.ShapeDtypeStruct((rows, blocks * width), value.dtype),
        in_specs=[in_vmem],
        out_specs=in_vmem,
        scratch_shapes=[pltpu.SemaphoreType.DMA((8,)), pltpu.SemaphoreType.DMA((8,))],
        compiler_params=pltpu.CompilerParams(collective_id=collective_id, has_side_effects=True),
        name="blocks_to_columns",
    )(value)


def skew(wide, count):
    lead = wide.shape[:-2]
    rows, span = wide.shape[-2:]
    edge = [(0, 0)] * len(lead)
    padded = jnp.pad(wide, edge + [(0, 0), (0, 1)])
    flat = padded.reshape(lead + (rows * (span + 1),))
    flat = lax.slice_in_dim(flat, rows - 1, rows - 1 + rows * span, axis=len(lead))
    return flat.reshape(lead + (rows, span))[..., :count]


def unskew(grad, span):
    lead = grad.shape[:-2]
    rows, count = grad.shape[-2:]
    edge = [(0, 0)] * len(lead)
    wide = jnp.pad(grad, edge + [(0, 0), (0, span - count)])
    flat = jnp.pad(wide.reshape(lead + (rows * span,)), edge + [(rows - 1, 1)])
    return flat.reshape(lead + (rows, span + 1))[..., :span]


def tile_scores(content_rows, position_rows, key_rows, relative, row_start, key_start):
    rows = content_rows.shape[0]
    count = key_rows.shape[0]
    scale = content_rows.shape[-1] ** (-0.5)
    content = jnp.einsum("qhe,khe->hqk", content_rows, key_rows, preferred_element_type=f32)
    wide = jnp.einsum("qhe,whe->hqw", position_rows, relative, preferred_element_type=f32)
    scores = (content + skew(wide, count)) * scale
    causal = (row_start + jnp.arange(rows))[:, None] >= (key_start + jnp.arange(count))[None, :]
    return (scores, causal[None])


def tile_forward(
    content_rows, position_rows, row_start, relative, key_rows, value_rows, key_start, state
):
    top, total, accum = state
    scores, causal = tile_scores(
        content_rows, position_rows, key_rows, relative, row_start, key_start
    )
    scores = jnp.where(causal, scores, neg_big)
    new_top = jnp.maximum(top, jnp.max(scores, axis=-1))
    raised = jnp.where(causal, jnp.exp(scores - new_top[..., None]), 0.0)
    fade = jnp.exp(top - new_top)
    total = total * fade + jnp.sum(raised, axis=-1)
    accum = accum * fade[..., None] + jnp.einsum(
        "hqk,khe->hqe", raised.astype(bf16), value_rows, preferred_element_type=f32
    )
    return (new_top, total, accum)


def tile_backward(
    content_rows,
    position_rows,
    row_start,
    relative,
    key_rows,
    value_rows,
    grad_rows,
    log_rows,
    delta_rows,
    key_start,
):
    scores, causal = tile_scores(
        content_rows, position_rows, key_rows, relative, row_start, key_start
    )
    scale = content_rows.shape[-1] ** (-0.5)
    shares = jnp.where(causal, jnp.exp(scores - log_rows[..., None]), 0.0)
    share_grad = jnp.einsum("qhe,khe->hqk", grad_rows, value_rows, preferred_element_type=f32)
    score_grad = (shares * (share_grad - delta_rows[..., None])).astype(bf16)
    content_grad = jnp.einsum("hqk,khe->qhe", score_grad, key_rows, preferred_element_type=f32)
    wide_grad = unskew(score_grad, relative.shape[0])
    position_grad = jnp.einsum("hqw,whe->qhe", wide_grad, relative, preferred_element_type=f32)
    table_part = jnp.einsum("hqw,qhe->whe", wide_grad, position_rows, preferred_element_type=f32)
    key_grad = jnp.einsum("hqk,qhe->khe", score_grad, content_rows, preferred_element_type=f32)
    value_grad = jnp.einsum(
        "hqk,qhe->khe", shares.astype(bf16), grad_rows, preferred_element_type=f32
    )
    return (
        content_grad * scale,
        position_grad * scale,
        table_part * scale,
        key_grad * scale,
        value_grad,
    )


def nest_tiles(tile_fn):
    inner = jax.vmap(tile_fn, in_axes=(0, 0, 0, 0, None, None, 0))
    return jax.vmap(inner, in_axes=(0, 0, None, None, 0, 0, 0))


def to_global(stored, inverse, block):
    seqs, seq_len, width = stored.shape
    blocks = stored.reshape(seqs, seq_len // block, block * width)
    chosen = (inverse[:, None] == jnp.arange(seq_len // block)[None, :]).astype(bf16)
    moved = jnp.einsum("gs,nsx->ngx", chosen, blocks, preferred_element_type=f32)
    return moved.astype(bf16).reshape(stored.shape)


class SplitQueries:

    def __init__(self, query, keys, values, biases, relative, block_order, inverse, block):
        self.seqs, self.tok_dev, self.width = keys.shape
        self.heads = self.width // HEAD_DIM
        self.block = block
        self.block_order = block_order
        ctx_count = lax.axis_size("ctx")
        self.seq_len = self.tok_dev * ctx_count
        self.key_len = min(512, self.seq_len)
        pad = jnp.zeros((self.key_len + block, self.width), bf16)
        table = jnp.concatenate([relative, pad], axis=0)
        self.table = table.reshape(-1, self.heads, HEAD_DIM)
        lead = (self.seqs, 2, block, self.heads, HEAD_DIM)
        self.content = (query + biases[0]).astype(bf16).reshape(lead)
        self.position = (query + biases[1]).astype(bf16).reshape(lead)
        gathered = [lax.all_gather(part, "ctx", axis=1, tiled=True) for part in (keys, values)]
        shape = (self.seqs, self.seq_len, self.heads, HEAD_DIM)
        self.keys, self.values = [to_global(part, inverse, block).reshape(shape) for part in gathered]
        self.starts = lax.dynamic_slice_in_dim(block_order, 2 * lax.axis_index("ctx"), 2, 0) * block

    def rows(self, index):
        start = index * self.key_len
        keys = lax.dynamic_slice_in_dim(self.keys, start, self.key_len, 1)
        values = lax.dynamic_slice_in_dim(self.values, start, self.key_len, 1)
        span = self.block + self.key_len
        offsets = [self.seq_len - self.block - self.starts[slot] + start for slot in range(2)]
        relative = [lax.dynamic_slice_in_dim(self.table, offset, span, 0) for offset in offsets]
        return start, keys, values, jnp.stack(relative), offsets

    def to_stored(self, part):
        count = self.seq_len // self.block
        blocks = part.reshape(self.seqs, count, self.block * self.width)
        chosen = (self.block_order[:, None] == jnp.arange(count)[None, :]).astype(f32)
        moved = jnp.einsum("sg,ngx->nsx", chosen, blocks, precision=highest)
        return moved.reshape(self.seqs, self.seq_len, self.width)

    def forward(self):
        def step(state, index):
            start, keys, values, relative, _ = self.rows(index)

            def tile(content, position, row_start, table, keys_seq, values_seq, tile_state):
                return tile_forward(
                    content, position, row_start, table, keys_seq, values_seq, start, tile_state
                )

            return nest_tiles(tile)(
                self.content, self.position, self.starts, relative, keys, values, state
            ), None

        shape = (self.seqs, 2, self.heads, self.block)
        state = (
            jnp.full(shape, neg_big, f32),
            jnp.zeros(shape, f32),
            jnp.zeros(shape + (HEAD_DIM,), f32),
        )
        (top, total, accum), _ = lax.scan(step, state, jnp.arange(self.seq_len // self.key_len))
        self.log_total = top + jnp.log(total)
        self.out = accum / total[..., None]
        moved = jnp.transpose(self.out, (0, 1, 3, 2, 4))
        return moved.reshape(self.seqs * self.tok_dev, self.width).astype(bf16)

    def backward(self, grad):
        block, seq_len, key_len = self.block, self.seq_len, self.key_len
        lead = (self.seqs, 2, block, self.heads, HEAD_DIM)
        grad = grad.reshape(lead)
        delta = jnp.einsum("sbqhe,sbhqe->sbhq", grad.astype(f32), self.out)
        def step(carry, index):
            start, keys, values, relative, offsets = self.rows(index)

            def tile(content, position, row_start, table, keys_seq, values_seq, extra):
                return tile_backward(
                    content, position, row_start, table, keys_seq, values_seq, *extra, start
                )

            extra = (grad, self.log_total, delta)
            parts = nest_tiles(tile)(
                self.content, self.position, self.starts, relative, keys, values, extra
            )
            table = carry[2]
            table_sum = jnp.sum(parts[2], axis=0)
            for slot in range(2):
                offset = offsets[slot]
                current = lax.dynamic_slice_in_dim(table, offset, block + key_len, 0)
                table = lax.dynamic_update_slice_in_dim(table, current + table_sum[slot], offset, 0)
            sums = []
            for total, part in zip(carry[3:], parts[3:]):
                current = lax.dynamic_slice_in_dim(total, start, key_len, 1)
                part = current + jnp.sum(part, axis=1)
                sums.append(lax.dynamic_update_slice_in_dim(total, part, start, 1))
            key_acc, value_acc = sums
            return (carry[0] + parts[0], carry[1] + parts[1], table, key_acc, value_acc), None

        zero_tiles = jnp.zeros(lead, f32)
        zero_keys = jnp.zeros((self.seqs, seq_len, self.heads, HEAD_DIM), f32)
        carry = (zero_tiles, zero_tiles, jnp.zeros(self.table.shape, f32), zero_keys, zero_keys)
        carry, _ = lax.scan(step, carry, jnp.arange(seq_len // key_len))
        owned = [
            lax.psum_scatter(
                self.to_stored(part), "ctx", scatter_dimension=1, tiled=True
            )
            for part in carry[3:]
        ]
        flat = (self.seqs * self.tok_dev, self.width)
        query_grad = (carry[0] + carry[1]).reshape(flat).astype(bf16)
        key_grad, value_grad = [part.reshape(flat).astype(bf16) for part in owned]
        bias_grads = jnp.stack(
            [jnp.sum(part, axis=(0, 1, 2)).reshape(self.width) for part in carry[:2]]
        )
        table_grad = carry[2].reshape(-1, self.width)[:seq_len]
        return query_grad, key_grad, value_grad, bias_grads, table_grad


def local_general(
    tokens,
    neighbours,
    teacher,
    valid_mask,
    block_order,
    query_weight,
    key_weight,
    value_weight,
    output_weight,
    relative_weight,
    content_bias,
    position_bias,
    cross_query_weight,
    cross_key_weight,
    cross_value_weight,
    cross_output_weight,
    up_weight,
    down_weight,
    attention_gain,
    cross_gain,
    feedforward_gain,
):
    places = lax.axis_size("wa")
    ctx_count = lax.axis_size("ctx")
    place = lax.axis_index("wa")
    here = lax.axis_index("ctx")
    _, tok_dev, width = tokens.shape
    seq_len = tok_dev * ctx_count
    block = tok_dev // 2
    cols = HEADS * HEAD_DIM // places
    rows = places * tok_dev

    token_parts = gather_parts(tokens[0])
    query_cols, key_cols, value_cols = [
        take_columns(weight) for weight in (query_weight, key_weight, value_weight)
    ]
    relative_cols = take_columns(relative_weight)
    gains = lax.all_gather(
        jnp.stack([attention_gain, cross_gain, feedforward_gain]), "wa", axis=1, tiled=True
    ).astype(f32)
    gain_one, gain_two, gain_three = gains[0:1], gains[1:2], gains[2:3]
    cross_query_cols, cross_key_cols, cross_value_cols = [
        take_columns(weight) for weight in (cross_query_weight, cross_key_weight, cross_value_weight)
    ]
    cross_pair_cols = jnp.concatenate([cross_key_cols, cross_value_cols], axis=1)
    near_rows = jnp.concatenate(gather_parts(neighbours.reshape(-1, width)), axis=0)
    up_cols = take_columns(up_weight)
    valid = valid_mask.astype(f32).reshape(tok_dev, 1)
    count = jnp.sum(valid).reshape(1, 1)
    count = all_summed(all_summed(count, "wa"), "ctx")

    slots = jnp.arange(2 * ctx_count)
    inverse = jnp.sum(jnp.where(block_order[None, :] == slots[:, None], slots[None, :], 0), axis=1)
    inverse = inverse.astype(jnp.int32)
    distance = (seq_len - 1 - jnp.arange(seq_len)).astype(f32)
    waves = sinusoid(distance, width).astype(bf16)

    hidden_all = jnp.concatenate(token_parts, axis=0).astype(f32)
    scale_all = inverse_rms(hidden_all)
    normed_a = (hidden_all * scale_all * gain_one).astype(bf16)
    biases = jnp.stack([content_bias, position_bias]).astype(f32)
    mixed_cols = jnp.concatenate([query_cols, key_cols, value_cols], axis=1)
    qkv = dot_nn(normed_a, mixed_cols).reshape(places, tok_dev, 3 * cols)
    relative = dot_nn(waves, relative_cols).astype(bf16)
    general = SplitQueries(
        qkv[..., :cols],
        qkv[..., cols : 2 * cols].astype(bf16),
        qkv[..., 2 * cols :].astype(bf16),
        biases,
        relative,
        block_order,
        inverse,
        block,
    )
    attended = general.forward()

    def to_owner(product):
        return scatter_parts([product[r * tok_dev : (r + 1) * tok_dev] for r in range(places)])

    def from_all(value):
        return jnp.concatenate(gather_parts(value), axis=0)

    hidden_in = tokens[0].astype(f32)
    hidden_one = hidden_in + to_owner(dot_nn(attended, output_weight))

    scale_two = inverse_rms(hidden_one)
    normed_b = from_all((hidden_one * scale_two * gain_two).astype(bf16))
    cross_q = dot_nn(normed_b, cross_query_cols).astype(bf16)
    cross_pair = dot_nn(near_rows, cross_pair_cols).astype(bf16)
    crossed = cross_forward(cross_q, cross_pair)
    hidden_two = hidden_one + to_owner(dot_nn(crossed, cross_output_weight))

    scale_three = inverse_rms(hidden_two)
    normed_c = from_all((hidden_two * scale_three * gain_three).astype(bf16))
    pre_act = dot_nn(normed_c, up_cols)
    activated = gelu_tanh(pre_act).astype(bf16)
    layer_out = hidden_two + to_owner(dot_nn(activated, down_weight))

    error = layer_out - teacher[0].astype(f32)
    error_sum = jnp.sum(valid * error * error).reshape(1, 1)
    error_sum = all_summed(all_summed(error_sum, "wa"), "ctx")
    loss = (error_sum / (2.0 * count * width)).reshape(())
    out_grad = (places * seq_len) / count * valid * error

    out_low = from_all(out_grad.astype(bf16))
    act_grad = dot_nt(out_low, down_weight)
    _, gelu_pull = jax.vjp(gelu_tanh, pre_act)
    pre_grad = gelu_pull(act_grad)[0].astype(bf16)
    down_grad = dot_tn(activated, out_low).astype(bf16)
    up_grad = dot_tn(normed_c, pre_grad).astype(bf16)
    normed_c_grad = to_owner(dot_nt(pre_grad, up_cols))
    two_grad = out_grad + norm_pull(hidden_two, scale_three, gain_three, normed_c_grad)
    gain_three_grad = jnp.sum(normed_c_grad * hidden_two * scale_three, axis=0, keepdims=True)
    down_out = sum_row_grads(down_grad)
    up_out = sum_column_grads(up_grad[None])[0]

    two_low = from_all(two_grad.astype(bf16))
    crossed_grad = dot_nt(two_low, cross_output_weight).astype(bf16)
    cross_q_grad, cross_pair_grad = cross_backward(cross_q, cross_pair, crossed_grad)
    normed_b_grad = to_owner(dot_nt(cross_q_grad, cross_query_cols))
    one_grad = two_grad + norm_pull(hidden_one, scale_two, gain_two, normed_b_grad)
    gain_two_grad = jnp.sum(normed_b_grad * hidden_one * scale_two, axis=0, keepdims=True)
    cross_output_grad = dot_tn(crossed, two_low).astype(bf16)
    cross_query_grad = dot_tn(normed_b, cross_q_grad).astype(bf16)
    cross_key_grad = dot_tn(near_rows, cross_pair_grad[:, :cols]).astype(bf16)
    cross_value_grad = dot_tn(near_rows, cross_pair_grad[:, cols:]).astype(bf16)
    cross_output_out = sum_row_grads(cross_output_grad)
    cross_out = sum_column_grads(jnp.stack([cross_key_grad, cross_value_grad]))
    cross_query_out = sum_column_grads(cross_query_grad[None])[0]
    near_grad = dot_nt(cross_pair_grad, cross_pair_cols)
    near_count = near_rows.shape[0] // places
    near_grad = scatter_parts(
        [near_grad[r * near_count : (r + 1) * near_count] for r in range(places)]
    )
    neighbours_grad = near_grad.reshape(neighbours.shape)

    one_low = from_all(one_grad.astype(bf16))
    attended_grad = dot_nt(one_low, output_weight).astype(bf16)
    output_grad = dot_tn(attended, one_low).astype(bf16)
    output_out = sum_row_grads(output_grad)
    query_grad, key_grad, value_grad, bias_grads, table_grad = general.backward(attended_grad)
    qkv_grad = jnp.concatenate([query_grad, key_grad, value_grad], axis=1)
    table_high = table_grad.astype(bf16)
    table_low = (table_grad - table_high.astype(f32)).astype(bf16)
    relative_grad = (dot_tn(waves, table_high) + dot_tn(waves, table_low)).astype(bf16)
    mixed_grad = dot_tn(normed_a, qkv_grad).astype(bf16)
    whole = [mixed_grad[:, m * cols : (m + 1) * cols] for m in range(3)]
    attention_out = sum_column_grads(jnp.stack(whole + [relative_grad]))
    normed_a_part = dot_nt(qkv_grad, mixed_cols)
    gain_one_part = jnp.sum(normed_a_part * hidden_all * scale_all, axis=0, keepdims=True)
    normed_a_grad = to_owner(normed_a_part)
    tokens_grad = one_grad + norm_pull(hidden_in, scale_all[:tok_dev], gain_one, normed_a_grad)

    gain_grads = jnp.concatenate([gain_one_part, gain_two_grad, gain_three_grad], axis=0)
    gain_grads = all_summed(gain_grads, "wa")
    share = width // places
    gain_grads = lax.dynamic_slice_in_dim(gain_grads, place * share, share, 1)
    small = jnp.concatenate([gain_grads.reshape(1, -1), bias_grads.reshape(1, -1)], axis=1)
    small = all_summed(small, "ctx")[0]
    gain_out = small[: 3 * share].reshape(3, share)
    bias_out = small[3 * share :].reshape(2, cols)

    return (
        layer_out[None],
        loss,
        tokens_grad[None],
        neighbours_grad,
        attention_out[0],
        attention_out[1],
        attention_out[2],
        output_out,
        attention_out[3],
        bias_out[0],
        bias_out[1],
        cross_query_out,
        cross_out[0],
        cross_out[1],
        cross_output_out,
        up_out,
        down_out,
        gain_out[0],
        gain_out[1],
        gain_out[2],
    )


def local_by_heads(
    tokens,
    neighbours,
    teacher,
    valid_mask,
    block_order,
    query_weight,
    key_weight,
    value_weight,
    output_weight,
    relative_weight,
    content_bias,
    position_bias,
    cross_query_weight,
    cross_key_weight,
    cross_value_weight,
    cross_output_weight,
    up_weight,
    down_weight,
    attention_gain,
    cross_gain,
    feedforward_gain,
):
    places = 4
    ctx_count = 8
    place = lax.axis_index("wa")
    here = lax.axis_index("ctx")
    _, tok_dev, width = tokens.shape
    seq_len = tok_dev * ctx_count
    block = tok_dev // 2
    attn = HEADS * HEAD_DIM
    cols = attn // places
    rows = places * tok_dev
    share = width // places

    slots = jnp.arange(2 * ctx_count)
    inverse = jnp.sum(jnp.where(block_order[None, :] == slots[:, None], slots[None, :], 0), axis=1)
    inverse = inverse.astype(jnp.int32)
    valid = valid_mask.astype(f32).reshape(tok_dev, 1)

    pair_rows = jnp.concatenate(
        [
            lax.dynamic_slice_in_dim(weight, here * 128, 128, 1)
            for weight in (query_weight, key_weight, value_weight, relative_weight)
        ],
        axis=1,
    )
    gain_rows = jnp.stack([attention_gain, cross_gain, feedforward_gain]).astype(f32)
    bias_rows = jnp.stack([content_bias, position_bias]).astype(f32)
    gain_rows = jnp.concatenate(
        [jnp.pad(gain_rows, ((0, 0), (0, cols - share))), bias_rows, jnp.zeros((3, cols), f32)], axis=0
    )
    count_row = jnp.broadcast_to(jnp.sum(valid), (8, 128))
    tokens_all, count_all, (pair_cols, gains) = gather_all(
        tokens[0], count_row, (pair_rows, gain_rows), 1
    )
    count = count_all[0:1, 0:1]
    pair_cols = pair_cols.reshape(width, 512)
    bias_all = gains[:, 3:5].transpose(1, 0, 2).reshape(2, attn)
    gains = gains[:, :3, :share].transpose(1, 0, 2).reshape(3, width)
    gain_one, gain_two, gain_three = gains[0:1], gains[1:2], gains[2:3]

    cross_query_cols, cross_key_cols, cross_value_cols = [
        take_columns(weight) for weight in (cross_query_weight, cross_key_weight, cross_value_weight)
    ]
    cross_pair_cols = jnp.concatenate([cross_key_cols, cross_value_cols], axis=1)
    near_rows = jnp.concatenate(gather_parts(neighbours.reshape(-1, width)), axis=0)
    up_cols = take_columns(up_weight)
    qkv_rows = jnp.stack(
        [weight.reshape(share, ctx_count, 128) for weight in (query_weight, key_weight, value_weight)],
        axis=2,
    ).reshape(share, 3 * attn)
    qkv_full = lax.all_gather(qkv_rows, "wa", axis=0, tiled=True)

    distance = (seq_len - 1 - jnp.arange(seq_len)).astype(f32)
    waves = sinusoid(distance, width).astype(bf16)

    hidden_all = tokens_all.reshape(seq_len, width).astype(f32)
    normed_a = (hidden_all * inverse_rms(hidden_all) * gain_one).astype(bf16)
    qkv = dot_nn(normed_a, pair_cols[:, :384]).astype(bf16)
    table = dot_nn(waves, pair_cols[:, 384:]).astype(bf16)
    table = jnp.concatenate([table, jnp.zeros((TILE, 128), bf16)], axis=0)
    my_biases = lax.dynamic_slice_in_dim(bias_all, here * 128, 128, 1)
    my_biases = jnp.concatenate([my_biases, jnp.zeros((6, 128), f32)], axis=0)
    out = attend_forward(inverse, qkv, table, my_biases, block)
    attended = swap_heads(out.reshape(ctx_count, tok_dev, 128), True, 2).reshape(rows, cols)

    def to_owner(product):
        return scatter_parts([product[r * tok_dev : (r + 1) * tok_dev] for r in range(places)])

    def from_all(value):
        return jnp.concatenate(gather_parts(value), axis=0)

    hidden_in = tokens[0].astype(f32)
    hidden_one = hidden_in + to_owner(dot_nn(attended, output_weight))

    scale_two = inverse_rms(hidden_one)
    normed_b = from_all((hidden_one * scale_two * gain_two).astype(bf16))
    cross_q = dot_nn(normed_b, cross_query_cols).astype(bf16)
    cross_pair = dot_nn(near_rows, cross_pair_cols).astype(bf16)
    crossed = cross_forward(cross_q, cross_pair)
    hidden_two = hidden_one + to_owner(dot_nn(crossed, cross_output_weight))

    scale_three = inverse_rms(hidden_two)
    normed_c = from_all((hidden_two * scale_three * gain_three).astype(bf16))
    pre_act = dot_nn(normed_c, up_cols)
    activated = gelu_tanh(pre_act).astype(bf16)
    layer_out = hidden_two + to_owner(dot_nn(activated, down_weight))

    error = layer_out - teacher[0].astype(f32)
    error_sum = jnp.sum(valid * error * error)
    out_grad = (places * seq_len) / count * valid * error

    out_low = from_all(out_grad.astype(bf16))
    act_grad = dot_nt(out_low, down_weight)
    _, gelu_pull = jax.vjp(gelu_tanh, pre_act)
    pre_grad = gelu_pull(act_grad)[0].astype(bf16)
    down_grad = dot_tn(activated, out_low).astype(bf16)
    up_grad = dot_tn(normed_c, pre_grad).astype(bf16)
    normed_c_grad = to_owner(dot_nt(pre_grad, up_cols))
    two_grad = out_grad + norm_pull(hidden_two, scale_three, gain_three, normed_c_grad)
    gain_three_grad = jnp.sum(normed_c_grad * hidden_two * scale_three, axis=0)
    down_out = sum_row_grads(down_grad)
    up_out = sum_column_grads(up_grad[None])[0]

    two_low = from_all(two_grad.astype(bf16))
    crossed_grad = dot_nt(two_low, cross_output_weight).astype(bf16)
    cross_q_grad, cross_pair_grad = cross_backward(cross_q, cross_pair, crossed_grad)
    normed_b_grad = to_owner(dot_nt(cross_q_grad, cross_query_cols))
    one_grad = two_grad + norm_pull(hidden_one, scale_two, gain_two, normed_b_grad)
    gain_two_grad = jnp.sum(normed_b_grad * hidden_one * scale_two, axis=0)
    cross_output_grad = dot_tn(crossed, two_low).astype(bf16)
    cross_query_grad = dot_tn(normed_b, cross_q_grad).astype(bf16)
    cross_key_grad = dot_tn(near_rows, cross_pair_grad[:, :cols]).astype(bf16)
    cross_value_grad = dot_tn(near_rows, cross_pair_grad[:, cols:]).astype(bf16)
    cross_output_out = sum_row_grads(cross_output_grad)
    cross_out = sum_column_grads(jnp.stack([cross_key_grad, cross_value_grad]))
    cross_query_out = sum_column_grads(cross_query_grad[None])[0]
    near_grad = dot_nt(cross_pair_grad, cross_pair_cols)
    near_count = near_rows.shape[0] // places
    near_grad = scatter_parts(
        [near_grad[r * near_count : (r + 1) * near_count] for r in range(places)]
    )
    neighbours_grad = near_grad.reshape(neighbours.shape)

    one_low = from_all(one_grad.astype(bf16))
    attended_grad = dot_nt(one_low, output_weight).astype(bf16)
    output_grad = dot_tn(attended, one_low).astype(bf16)
    output_out = sum_row_grads(output_grad)
    grad = swap_heads(attended_grad.reshape(places, tok_dev, cols), False, 3)
    qkv_grad, table_grad, bias_part = attend_backward(
        inverse, qkv, table, my_biases, grad.reshape(seq_len, 128), block
    )
    table_high = table_grad.astype(bf16)
    table_low = (table_grad - table_high.astype(f32)).astype(bf16)
    relative_grad = dot_tn(waves, table_high) + dot_tn(waves, table_low)
    pair_grad = jnp.concatenate([dot_tn(normed_a, qkv_grad), relative_grad], axis=1).astype(bf16)
    pair_grad = pair_grad.reshape(places, share, 512)
    for bit in reversed(bits_of("wa")):
        keep, send = split(pair_grad, my_bit("wa", bit), 0)
        pair_grad = (keep.astype(f32) + swap(send, "wa", bit).astype(f32)).astype(bf16)

    mine = blocks_to_columns(qkv_grad.reshape(ctx_count, tok_dev, 384), 4)
    normed_a_grad = dot_nt(mine, qkv_full)
    scale_one = inverse_rms(hidden_in)
    tokens_grad = one_grad + norm_pull(hidden_in, scale_one, gain_one, normed_a_grad)
    gain_one_grad = jnp.sum(normed_a_grad * hidden_in * scale_one, axis=0)

    pair_slots = jnp.arange(ctx_count)[:, None, None]
    bias_slots = jnp.where(pair_slots == here, bias_part[None, 0:2], 0.0)
    gain_grads = jnp.concatenate([gain_one_grad, gain_two_grad, gain_three_grad])
    small = jnp.concatenate(
        [
            gain_grads.reshape(-1, 128),
            bias_slots.reshape(-1, 128),
            jnp.broadcast_to(error_sum, (3, 128)),
        ],
        axis=0,
    )
    pair_all, small, _ = gather_all(pair_grad[0], small, (), 5)
    gain_count = gain_grads.shape[0] // 128
    gain_out = small[:gain_count].reshape(3, width)
    gain_out = lax.dynamic_slice_in_dim(gain_out, place * share, share, 1)
    bias_out = small[gain_count : gain_count + 2 * ctx_count].reshape(ctx_count, 2, 128)
    bias_out = lax.dynamic_slice_in_dim(bias_out, place * 2, 2, 0)
    bias_out = bias_out.transpose(1, 0, 2).reshape(2, cols)
    loss = small[gain_count + 2 * ctx_count, 0] / (2.0 * count[0, 0] * width)
    whole = [
        pair_all[:, :, 128 * m : 128 * (m + 1)].transpose(1, 0, 2).reshape(share, attn).astype(f32)
        for m in range(4)
    ]

    return (
        layer_out[None],
        loss,
        tokens_grad[None],
        neighbours_grad,
        whole[0],
        whole[1],
        whole[2],
        output_out,
        whole[3],
        bias_out[0],
        bias_out[1],
        cross_query_out,
        cross_out[0],
        cross_out[1],
        cross_output_out,
        up_out,
        down_out,
        gain_out[0],
        gain_out[1],
        gain_out[2],
    )


def solution(mesh):
    row = P("wa", None)
    flat = P("wa")
    in_specs = (
        P("wa", "ctx", None),
        P("wa", "ctx", None, None),
        P("wa", "ctx", None),
        P("wa", "ctx"),
        P(),
        row,
        row,
        row,
        row,
        row,
        flat,
        flat,
        row,
        row,
        row,
        row,
        row,
        row,
        flat,
        flat,
        flat,
    )
    out_specs = (
        P("wa", "ctx", None),
        P(),
        P("wa", "ctx", None),
        P("wa", "ctx", None, None),
        row,
        row,
        row,
        row,
        row,
        flat,
        flat,
        row,
        row,
        row,
        row,
        row,
        row,
        flat,
        flat,
        flat,
    )
    by_heads = mesh.shape["ctx"] == 8 and mesh.shape["wa"] == 4
    local = local_by_heads if by_heads else local_general
    return jax.shard_map(local, mesh=mesh, in_specs=in_specs, out_specs=out_specs, check_vma=False)
```

```python
import functools

import jax
import jax.numpy as jnp
from jax import lax
from jax.experimental import pallas as pl
from jax.experimental.pallas import tpu as pltpu
from jax.sharding import PartitionSpec as P

HEADS = 16
HEAD_DIM = 64
GROUP = 64
NK = 256
TILE = 128

eps_norm = 1e-06
neg_big = -1e30
highest = lax.Precision.HIGHEST
f32 = jnp.float32
bf16 = jnp.bfloat16


def inverse_rms(hidden):
    return lax.rsqrt(jnp.mean(hidden * hidden, axis=-1, keepdims=True) + eps_norm)


def norm_pull(hidden, scale, gain, grad):
    scaled = grad * gain
    mean = jnp.mean(hidden * scaled, axis=-1, keepdims=True)
    return scale * scaled - hidden * (scale * scale * scale) * mean


def gelu_tanh(value):
    return jax.nn.gelu(value, approximate=True)


def sinusoid(distance, width):
    half = width // 2
    freq = jnp.exp(-jnp.log(10000.0) * jnp.arange(half, dtype=f32) * 2.0 / width)
    angle = distance[:, None] * freq[None, :]
    return jnp.concatenate([jnp.sin(angle), jnp.cos(angle)], axis=1)


def dot_nn(a, b):
    return lax.dot_general(a, b, (((1,), (0,)), ((), ())), preferred_element_type=f32)


def dot_nt(a, b):
    return lax.dot_general(a, b, (((1,), (1,)), ((), ())), preferred_element_type=f32)


def dot_tn(a, b):
    return lax.dot_general(a, b, (((0,), (0,)), ((), ())), preferred_element_type=f32)


def swap(value, axis, bit):
    pairs = [(i, i ^ bit) for i in range(lax.axis_size(axis))]
    return lax.ppermute(value, axis, pairs)


def bits_of(axis):
    bits, bit = [], 1
    while bit < lax.axis_size(axis):
        bits.append(bit)
        bit *= 2
    return bits


def my_bit(axis, bit):
    return (lax.axis_index(axis) // bit) % 2


def ordered(bit, own, other, dim):
    return jnp.where(
        bit == 0,
        jnp.concatenate([own, other], axis=dim),
        jnp.concatenate([other, own], axis=dim),
    )


def split(value, bit, dim):
    half = value.shape[dim] // 2
    keep = lax.dynamic_slice_in_dim(value, bit * half, half, dim)
    send = lax.dynamic_slice_in_dim(value, (1 - bit) * half, half, dim)
    return keep, send


def gather_parts(value):
    parts = {0: value}
    for bit in reversed(bits_of("wa")):
        parts.update({r | bit: swap(part, "wa", bit) for r, part in list(parts.items())})
    return [parts[r] for r in sorted(parts)]


def scatter_parts(parts):
    parts = dict(enumerate(parts))
    for bit in bits_of("wa"):
        kept = {}
        for r, part in parts.items():
            if not r & bit:
                got = swap(parts[r | bit].astype(bf16), "wa", bit)
                kept[r] = part + got.astype(f32)
        parts = kept
    return parts[0]


def take_columns(weight):
    value = weight[None]
    for bit in reversed(bits_of("wa")):
        mine = my_bit("wa", bit)
        keep, send = split(value, mine, 2)
        value = ordered(mine, keep[:, None], swap(send, "wa", bit)[:, None], 1)
        value = value.reshape((-1,) + value.shape[2:])
    return value.reshape(-1, value.shape[-1])


def spread_columns(value):
    for bit in bits_of("wa"):
        mine = my_bit("wa", bit)
        paired = value.reshape((value.shape[0], value.shape[1] // 2, 2) + value.shape[2:])
        keep, send = split(paired, mine, 2)
        value = ordered(mine, keep[:, :, 0], swap(send[:, :, 0], "wa", bit), 3)
    return value[:, 0]


def halving_dim(shape):
    if shape[-2] % 16 == 0:
        return len(shape) - 2
    if shape[0] % 2 == 0:
        return 0
    if shape[-2] % 2 == 0:
        return len(shape) - 2
    return len(shape) - 1


def sum_over_ctx(value, bits, finish):
    dims = []
    for bit in bits:
        dim = halving_dim(value.shape)
        keep, send = split(value, my_bit("ctx", bit), dim)
        value = (keep.astype(f32) + swap(send, "ctx", bit).astype(f32)).astype(bf16)
        dims.append(dim - value.ndim if dim else 0)
    value = finish(value)
    for bit, dim in reversed(list(zip(bits, dims))):
        dim = dim % value.ndim
        value = ordered(my_bit("ctx", bit), value, swap(value, "ctx", bit), dim)
    return value


def all_summed(value, axis):
    for bit in bits_of(axis):
        value = value + swap(value, axis, bit)
    return value


def sum_column_grads(grads):
    places = lax.axis_size("wa")
    grads = grads.reshape(grads.shape[0], places, grads.shape[1] // places, grads.shape[2])
    bits = bits_of("ctx")
    if grads.shape[2] % lax.axis_size("ctx") == 0:
        return sum_over_ctx(grads, bits, spread_columns).astype(f32)
    return sum_over_ctx(spread_columns(grads), bits, lambda value: value).astype(f32)


def sum_row_grads(grads):
    return sum_over_ctx(grads[None], bits_of("ctx"), lambda value: value)[0].astype(f32)


def first_half(shape):
    return lax.broadcasted_iota(jnp.int32, shape, 1) < HEAD_DIM


def stack_heads(rows):
    mask = first_half(rows.shape)
    zero = jnp.zeros_like(rows)
    return jnp.concatenate([jnp.where(mask, rows, zero), jnp.where(mask, zero, rows)], axis=0)


def join_heads(stacked):
    rows = stacked.shape[0] // 2
    return jnp.where(first_half((rows, stacked.shape[1])), stacked[:rows], stacked[rows:])


def copy_blocks(order_ref, source, target, block, inward):
    for place in range(source.shape[0] // block):
        start = pl.multiple_of(order_ref[place] * block, block)
        if inward:
            target[place * block : (place + 1) * block, :] = source[pl.ds(start, block), :]
        else:
            target[pl.ds(start, block), :] = source[place * block : (place + 1) * block, :]


def attention_shares(content, position, key_ref, rel_ref, row_start, seq_len):
    length = row_start + TILE
    wide_len = length + TILE
    offset = seq_len - TILE - row_start
    scale = HEAD_DIM ** (-0.5)
    scores = dot_nt(content, key_ref[0:length, :])
    wide = dot_nt(position, rel_ref[offset : offset + wide_len, :])
    halves = []
    for head in range(2):
        part = wide[head * TILE : (head + 1) * TILE]
        turned = pltpu.roll(part, wide_len - (TILE - 1), 1, stride=1, stride_axis=0)
        halves.append(turned[:, :length])
    scores = (scores + jnp.concatenate(halves, axis=0)) * scale
    row = lax.broadcasted_iota(jnp.int32, scores.shape, 0) % TILE + row_start
    col = lax.broadcasted_iota(jnp.int32, scores.shape, 1)
    scores = jnp.where(col <= row, scores, neg_big)
    top = jnp.max(scores, axis=1, keepdims=True)
    raised = jnp.exp(scores - top)
    total = jnp.sum(raised, axis=1, keepdims=True)
    return raised * (1.0 / total)


def attend_forward_kernel(seq_len, block, order_ref, qkv_ref, rel_ref, bias_ref, out_ref, qkv, out):
    copy_blocks(order_ref, qkv_ref, qkv, block, True)
    keys = qkv.at[:, 128:256]
    values = qkv.at[:, 256:384]
    content_bias = bias_ref[0:1, :]
    position_bias = bias_ref[1:2, :]
    for tile in range(seq_len // TILE):
        start = tile * TILE
        query = qkv[start : start + TILE, 0:128].astype(f32)
        content = stack_heads((query + content_bias).astype(bf16))
        position = stack_heads((query + position_bias).astype(bf16))
        shares = attention_shares(content, position, keys, rel_ref, start, seq_len)
        got = dot_nn(shares.astype(bf16), values[0 : start + TILE, :])
        out[start : start + TILE, :] = join_heads(got).astype(bf16)
    copy_blocks(order_ref, out, out_ref, block, False)


def attend_backward_kernel(
    seq_len,
    block,
    order_ref,
    qkv_ref,
    rel_ref,
    bias_ref,
    grad_ref,
    dqkv_ref,
    drel_ref,
    dbias_ref,
    qkv,
    grad,
    dqkv,
    dkey,
    dvalue,
    drel,
):
    scale = HEAD_DIM ** (-0.5)
    copy_blocks(order_ref, qkv_ref, qkv, block, True)
    copy_blocks(order_ref, grad_ref, grad, block, True)
    keys = qkv.at[:, 128:256]
    values = qkv.at[:, 256:384]
    content_bias = bias_ref[0:1, :]
    position_bias = bias_ref[1:2, :]
    dkey[...] = jnp.zeros_like(dkey)
    dvalue[...] = jnp.zeros_like(dvalue)
    drel[...] = jnp.zeros_like(drel)
    row = lax.broadcasted_iota(jnp.int32, (TILE, TILE), 0)
    col = lax.broadcasted_iota(jnp.int32, (TILE, TILE), 1)
    flip = jnp.where(row + col == TILE - 1, 1.0, 0.0).astype(bf16)
    content_sum = jnp.zeros((1, 128), f32)
    position_sum = jnp.zeros((1, 128), f32)
    for tile in range(seq_len // TILE):
        start = tile * TILE
        length = start + TILE
        wide_len = length + TILE
        offset = seq_len - TILE - start
        query = qkv[start : start + TILE, 0:128].astype(f32)
        content = stack_heads((query + content_bias).astype(bf16))
        plain = (query + position_bias).astype(bf16)
        position = stack_heads(plain)
        shares = attention_shares(content, position, keys, rel_ref, start, seq_len)
        out_grad = stack_heads(grad[start : start + TILE, :])
        share_grad = dot_nt(out_grad, values[0:length, :])
        delta = jnp.sum(shares * share_grad, axis=1, keepdims=True)
        score_grad = (shares * (share_grad - delta)).astype(bf16)
        content_grad = join_heads(dot_nn(score_grad, keys[0:length, :])) * scale
        parts = []
        for head in range(2):
            turned = dot_nn(flip, score_grad[head * TILE : (head + 1) * TILE])
            turned = jnp.concatenate([turned, jnp.zeros((TILE, TILE), f32)], axis=1)
            parts.append(pltpu.roll(turned, 0, 1, stride=1, stride_axis=0))
        wide_grad = jnp.concatenate(parts, axis=0).astype(bf16)
        relative = rel_ref[offset : offset + wide_len, :]
        turned_grad = join_heads(dot_nn(wide_grad, relative)) * scale
        turned_rows = stack_heads(dot_nn(flip, plain).astype(bf16))
        drel[offset : offset + wide_len, :] += dot_tn(wide_grad, turned_rows)
        high = turned_grad.astype(bf16)
        low = (turned_grad - high.astype(f32)).astype(bf16)
        position_grad = dot_nn(flip, high) + dot_nn(flip, low)
        content_sum += jnp.sum(content_grad, axis=0, keepdims=True)
        position_sum += jnp.sum(turned_grad, axis=0, keepdims=True)
        dqkv[start : start + TILE, 0:128] = (content_grad + position_grad).astype(bf16)
        dkey[0:length, :] += dot_tn(score_grad, content)
        dvalue[0:length, :] += dot_tn(shares.astype(bf16), out_grad)
    dqkv[:, 128:256] = (dkey[...] * scale).astype(bf16)
    dqkv[:, 256:384] = dvalue[...].astype(bf16)
    copy_blocks(order_ref, dqkv, dqkv_ref, block, False)
    drel_ref[...] = drel[0:seq_len, :] * scale
    dbias_ref[...] = jnp.concatenate(
        [content_sum, position_sum, jnp.zeros((6, 128), f32)], axis=0
    )


in_vmem = pl.BlockSpec(memory_space=pltpu.VMEM)
in_smem = pl.BlockSpec(memory_space=pltpu.SMEM)


def attend_forward(order, qkv, rel, bias, block):
    rows = qkv.shape[0]
    return pl.pallas_call(
        functools.partial(attend_forward_kernel, rows, block),
        out_shape=jax.ShapeDtypeStruct((rows, 128), bf16),
        in_specs=[in_smem, in_vmem, in_vmem, in_vmem],
        out_specs=in_vmem,
        scratch_shapes=[pltpu.VMEM((rows, 384), bf16), pltpu.VMEM((rows, 128), bf16)],
        compiler_params=pltpu.CompilerParams(vmem_limit_bytes=40 * 2**20),
        cost_estimate=pl.CostEstimate(
            flops=4 * 256 * rows * rows * 2, bytes_accessed=rows * 1300, transcendentals=rows * rows
        ),
        name="attend_forward",
    )(order, qkv, rel, bias)


def attend_backward(order, qkv, rel, bias, grad, block):
    rows = qkv.shape[0]
    return pl.pallas_call(
        functools.partial(attend_backward_kernel, rows, block),
        out_shape=[
            jax.ShapeDtypeStruct((rows, 384), bf16),
            jax.ShapeDtypeStruct((rows, 128), f32),
            jax.ShapeDtypeStruct((8, 128), f32),
        ],
        in_specs=[in_smem, in_vmem, in_vmem, in_vmem, in_vmem],
        out_specs=[in_vmem, in_vmem, in_vmem],
        scratch_shapes=[
            pltpu.VMEM((rows, 384), bf16),
            pltpu.VMEM((rows, 128), bf16),
            pltpu.VMEM((rows, 384), bf16),
            pltpu.VMEM((rows, 128), f32),
            pltpu.VMEM((rows, 128), f32),
            pltpu.VMEM((rows + TILE, 128), f32),
        ],
        compiler_params=pltpu.CompilerParams(vmem_limit_bytes=40 * 2**20),
        cost_estimate=pl.CostEstimate(
            flops=10 * 256 * rows * rows * 2, bytes_accessed=rows * 3000, transcendentals=rows * rows
        ),
        name="attend_backward",
    )(order, qkv, rel, bias, grad)


def head_mask(shape, head):
    lane = lax.broadcasted_iota(jnp.int32, shape, 1)
    return (lane >= head * HEAD_DIM) & (lane < (head + 1) * HEAD_DIM)


def stack_all(rows):
    zero = jnp.zeros_like(rows)
    heads = rows.shape[1] // HEAD_DIM
    return jnp.concatenate(
        [jnp.where(head_mask(rows.shape, head), rows, zero) for head in range(heads)], axis=0
    )


def join_all(stacked):
    heads = stacked.shape[1] // HEAD_DIM
    rows = stacked.shape[0] // heads
    out = jnp.zeros((rows, stacked.shape[1]), stacked.dtype)
    for head in range(heads):
        part = stacked[head * rows : (head + 1) * rows]
        out = jnp.where(head_mask(part.shape, head), part, out)
    return out


def cross_shares(query, keys):
    scores = dot_nt(query, keys) * (HEAD_DIM ** (-0.5))
    raised = jnp.exp(scores - jnp.max(scores, axis=1, keepdims=True))
    return raised / jnp.sum(raised, axis=1, keepdims=True)


def cross_forward_kernel(q_ref, kv_ref, out_ref):
    width = q_ref.shape[1]
    shares = cross_shares(stack_all(q_ref[...]), kv_ref[:, 0:width])
    out_ref[...] = join_all(dot_nn(shares.astype(bf16), kv_ref[:, width:])).astype(bf16)


def cross_backward_kernel(q_ref, kv_ref, grad_ref, dq_ref, dkv_ref):
    width = q_ref.shape[1]
    scale = HEAD_DIM ** (-0.5)
    keys = kv_ref[:, 0:width]
    query = stack_all(q_ref[...])
    grad = stack_all(grad_ref[...])
    shares = cross_shares(query, keys)
    share_grad = dot_nt(grad, kv_ref[:, width:])
    delta = jnp.sum(shares * share_grad, axis=1, keepdims=True)
    score_grad = (shares * (share_grad - delta)).astype(bf16)
    dq_ref[...] = (join_all(dot_nn(score_grad, keys)) * scale).astype(bf16)
    dkv_ref[:, 0:width] = (dot_tn(score_grad, query) * scale).astype(bf16)
    dkv_ref[:, width:] = dot_tn(shares.astype(bf16), grad).astype(bf16)


def cross_forward(query, pair):
    width = query.shape[1]
    groups = query.shape[0] // GROUP
    return pl.pallas_call(
        cross_forward_kernel,
        out_shape=jax.ShapeDtypeStruct(query.shape, bf16),
        grid=(groups,),
        in_specs=[
            pl.BlockSpec((GROUP, width), lambda g: (g, 0)),
            pl.BlockSpec((NK, 2 * width), lambda g: (g, 0)),
        ],
        out_specs=pl.BlockSpec((GROUP, width), lambda g: (g, 0)),
        cost_estimate=pl.CostEstimate(
            flops=groups * 4 * 256 * 256 * 256, bytes_accessed=groups * 330000, transcendentals=groups * 65536
        ),
        name="cross_forward",
    )(query, pair)


def cross_backward(query, pair, grad):
    width = query.shape[1]
    groups = query.shape[0] // GROUP
    return pl.pallas_call(
        cross_backward_kernel,
        out_shape=[
            jax.ShapeDtypeStruct(query.shape, bf16),
            jax.ShapeDtypeStruct(pair.shape, bf16),
        ],
        grid=(groups,),
        in_specs=[
            pl.BlockSpec((GROUP, width), lambda g: (g, 0)),
            pl.BlockSpec((NK, 2 * width), lambda g: (g, 0)),
            pl.BlockSpec((GROUP, width), lambda g: (g, 0)),
        ],
        out_specs=[
            pl.BlockSpec((GROUP, width), lambda g: (g, 0)),
            pl.BlockSpec((NK, 2 * width), lambda g: (g, 0)),
        ],
        cost_estimate=pl.CostEstimate(
            flops=groups * 10 * 256 * 256 * 256, bytes_accessed=groups * 660000, transcendentals=groups * 65536
        ),
        name="cross_backward",
    )(query, pair, grad)


mesh_id = pl.DeviceIdType.MESH


def signal_to(barrier, ctx, wa):
    pl.semaphore_signal(barrier, inc=1, device_id=(ctx, wa), device_id_type=mesh_id)


def tree_sum(values):
    while len(values) > 1:
        values = [a + b for a, b in zip(values[::2], values[1::2])]
    return values[0]


def gather_kernel(
    parts,
    block_ref,
    small_ref,
    *refs,
):
    part_refs = refs[:parts]
    out_ref, total_ref = refs[parts : parts + 2]
    part_outs = refs[parts + 2 : 2 * parts + 2]
    near, far, y_send, y_recv, r_send, r_recv, l_send, l_recv, s_send, s_recv, p_send, p_recv, o_sem = refs[
        2 * parts + 2 :
    ]
    c = lax.axis_index("ctx")
    w = lax.axis_index("wa")
    z = c // 2
    right = z < 3
    left = z > 0
    barrier = pltpu.get_barrier_semaphore()
    for j in range(1, 8):
        signal_to(barrier, c ^ j, w)
    for j in range(1, 4):
        signal_to(barrier, c, w ^ j)
    pl.semaphore_wait(barrier, 10)

    def small_copy(source, j):
        wide = j < 4
        return pltpu.make_async_remote_copy(
            src_ref=source,
            dst_ref=near.at[j] if wide else far.at[j - 3],
            send_sem=s_send.at[j],
            recv_sem=s_recv.at[j],
            device_id=(c, w ^ j) if wide else (c ^ (j - 3), w),
            device_id_type=mesh_id,
        )

    for j in range(1, 4):
        small_copy(small_ref, j).start()

    def part_copy(m, j):
        return pltpu.make_async_remote_copy(
            src_ref=part_refs[m],
            dst_ref=part_outs[m].at[w],
            send_sem=p_send.at[m, j],
            recv_sem=p_recv.at[m, j],
            device_id=(c, w ^ j),
            device_id_type=mesh_id,
        )

    for m in reversed(range(parts)):
        for j in (1, 2, 3):
            part_copy(m, j).start()

    def y_copy(source, block, slot):
        return pltpu.make_async_remote_copy(
            src_ref=source,
            dst_ref=out_ref.at[block],
            send_sem=y_send.at[slot],
            recv_sem=y_recv.at[slot],
            device_id=(c ^ 1, w),
            device_id_type=mesh_id,
        )

    def z_copy(source, block, slot, step, send, recv):
        return pltpu.make_async_remote_copy(
            src_ref=source,
            dst_ref=out_ref.at[block],
            send_sem=send.at[slot],
            recv_sem=recv.at[slot],
            device_id=(c + step, w),
            device_id_type=mesh_id,
        )

    @pl.when(right)
    def _():
        z_copy(block_ref, c, 0, 2, r_send, r_recv).start()

    @pl.when(left)
    def _():
        z_copy(block_ref, c, 0, -2, l_send, l_recv).start()

    y_copy(block_ref, c, 0).start()
    own = [pltpu.make_async_copy(block_ref, out_ref.at[c], o_sem.at[0])]
    for m in range(parts):
        own.append(pltpu.make_async_copy(part_refs[m], part_outs[m].at[w], o_sem.at[1 + m]))
    for copy in own:
        copy.start()
    for j in range(1, 4):
        small_copy(small_ref, j).wait()
    total_ref[...] = tree_sum([small_ref[...]] + [near[j] for j in range(1, 4)])
    for j in range(4, 11):
        small_copy(total_ref, j).start()
    for t in range(3):

        @pl.when(z > t)
        def _(t=t):
            block = c - 2 * (t + 1)
            z_copy(out_ref.at[block], block, t, 2, r_send, r_recv).wait_recv()
            if t < 2:

                @pl.when(right)
                def _():
                    z_copy(out_ref.at[block], block, t + 1, 2, r_send, r_recv).start()

            y_copy(out_ref.at[block], block, t + 1).start()

        @pl.when(z < 3 - t)
        def _(t=t):
            block = c + 2 * (t + 1)
            z_copy(out_ref.at[block], block, t, -2, l_send, l_recv).wait_recv()
            if t < 2:

                @pl.when(left)
                def _():
                    z_copy(out_ref.at[block], block, t + 1, -2, l_send, l_recv).start()

            y_copy(out_ref.at[block], block, t + 4).start()

    for j in range(4, 11):
        small_copy(total_ref, j).wait()
    total_ref[...] = tree_sum([total_ref[...]] + [far[j] for j in range(1, 8)])
    y_copy(block_ref, c ^ 1, 0).wait()
    for t in range(3):

        @pl.when(z > t)
        def _(t=t):
            block = (c ^ 1) - 2 * (t + 1)
            y_copy(out_ref.at[block], block, t + 1).wait()

        @pl.when(z < 3 - t)
        def _(t=t):
            block = (c ^ 1) + 2 * (t + 1)
            y_copy(out_ref.at[block], block, t + 4).wait()

    @pl.when(right)
    def _():
        z_copy(block_ref, c, 0, 2, r_send, r_recv).wait_send()

    @pl.when(left)
    def _():
        z_copy(block_ref, c, 0, -2, l_send, l_recv).wait_send()

    for t in range(2):

        @pl.when(jnp.logical_and(z > t, right))
        def _(t=t):
            z_copy(block_ref, c, t + 1, 2, r_send, r_recv).wait_send()

        @pl.when(jnp.logical_and(z < 3 - t, left))
        def _(t=t):
            z_copy(block_ref, c, t + 1, -2, l_send, l_recv).wait_send()

    for m in range(parts):
        for j in range(1, 4):
            part_copy(m, j).wait_send()
            pltpu.make_async_remote_copy(
                src_ref=part_refs[m],
                dst_ref=part_outs[m].at[w ^ j],
                send_sem=p_send.at[m, j],
                recv_sem=p_recv.at[m, j],
                device_id=(c, w ^ j),
                device_id_type=mesh_id,
            ).wait_recv()
    for copy in own:
        copy.wait()


def gather_all(block, small, parts, collective_id):
    dma = pltpu.SemaphoreType.DMA
    count = len(parts)
    got = pl.pallas_call(
        functools.partial(gather_kernel, count),
        out_shape=[
            jax.ShapeDtypeStruct((8,) + block.shape, block.dtype),
            jax.ShapeDtypeStruct(small.shape, small.dtype),
        ]
        + [jax.ShapeDtypeStruct((4,) + part.shape, part.dtype) for part in parts],
        in_specs=[in_vmem] * (2 + count),
        out_specs=[in_vmem] * (2 + count),
        scratch_shapes=[
            pltpu.VMEM((4,) + small.shape, small.dtype),
            pltpu.VMEM((8,) + small.shape, small.dtype),
            dma((7,)),
            dma((7,)),
            dma((3,)),
            dma((3,)),
            dma((3,)),
            dma((3,)),
            dma((11,)),
            dma((11,)),
            dma((max(count, 1), 4)),
            dma((max(count, 1), 4)),
            dma((1 + count,)),
        ],
        compiler_params=pltpu.CompilerParams(
            collective_id=collective_id, has_side_effects=True, vmem_limit_bytes=40 * 2**20
        ),
        name="gather_all",
    )(block, small, *parts)
    return got[0], got[1], got[2:]


def swap_heads_kernel(outward, in_ref, out_ref, send_sem, recv_sem):
    c = lax.axis_index("ctx")
    w = lax.axis_index("wa")
    owner = c // 2
    half = c % 2
    own = owner == w
    other = jnp.logical_not(own)
    barrier = pltpu.get_barrier_semaphore()

    def lanes(start):
        return pl.ds(pl.multiple_of(start * 128, 128), 128)

    for j in range(1, 8):
        signal_to(barrier, c ^ j, owner)
    for r in range(4):
        for h in range(2):
            mine = jnp.logical_and(2 * w + h == c, r == 0)

            @pl.when(jnp.logical_not(mine))
            def _(r=r, h=h):
                signal_to(barrier, 2 * w + h, w ^ r)

    @pl.when(other)
    def _():
        signal_to(barrier, c, owner)

    pl.semaphore_wait(barrier, 16 - 2 * own.astype(jnp.int32))
    slot = w ^ owner
    if outward:

        def copy_to(j):
            return pltpu.make_async_remote_copy(
                src_ref=in_ref.at[c ^ j],
                dst_ref=out_ref.at[slot, :, lanes(half)],
                send_sem=send_sem.at[j],
                recv_sem=recv_sem.at[slot * 2 + half],
                device_id=(c ^ j, owner),
                device_id_type=mesh_id,
            )

        for j in range(7, 0, -1):
            copy_to(j).start()

        @pl.when(other)
        def _():
            copy_to(0).start()

        @pl.when(own)
        def _():
            pltpu.make_async_copy(
                in_ref.at[c], out_ref.at[slot, :, lanes(half)], recv_sem.at[slot * 2 + half]
            ).start()

        for r in range(4):
            for h in range(2):
                pltpu.make_async_remote_copy(
                    src_ref=in_ref.at[0],
                    dst_ref=out_ref.at[r, :, h * 128 : (h + 1) * 128],
                    send_sem=send_sem.at[0],
                    recv_sem=recv_sem.at[r * 2 + h],
                    device_id=(c ^ 1, w),
                    device_id_type=mesh_id,
                ).wait_recv()
        for j in range(1, 8):
            copy_to(j).wait_send()

        @pl.when(other)
        def _():
            copy_to(0).wait_send()

    else:

        def copy_to(r, h):
            return pltpu.make_async_remote_copy(
                src_ref=in_ref.at[r, :, h * 128 : (h + 1) * 128],
                dst_ref=out_ref.at[c],
                send_sem=send_sem.at[r * 2 + h],
                recv_sem=recv_sem.at[c],
                device_id=(2 * w + h, w ^ r),
                device_id_type=mesh_id,
            )

        for r in (3, 2, 1, 0):
            for h in range(2):
                mine = jnp.logical_and(2 * w + h == c, r == 0)

                @pl.when(jnp.logical_not(mine))
                def _(r=r, h=h):
                    copy_to(r, h).start()

                @pl.when(mine)
                def _(r=r, h=h):
                    pltpu.make_async_copy(
                        in_ref.at[r, :, h * 128 : (h + 1) * 128], out_ref.at[c], recv_sem.at[c]
                    ).start()

        for block in range(8):
            pltpu.make_async_remote_copy(
                src_ref=in_ref.at[0, :, 0:128],
                dst_ref=out_ref.at[block],
                send_sem=send_sem.at[0],
                recv_sem=recv_sem.at[block],
                device_id=(c ^ 1, w),
                device_id_type=mesh_id,
            ).wait_recv()
        for r in range(4):
            for h in range(2):
                mine = jnp.logical_and(2 * w + h == c, r == 0)

                @pl.when(jnp.logical_not(mine))
                def _(r=r, h=h):
                    copy_to(r, h).wait_send()


def swap_heads(value, outward, collective_id):
    rows = value.shape[1]
    shape = (4, rows, 256) if outward else (8, rows, 128)
    return pl.pallas_call(
        functools.partial(swap_heads_kernel, outward),
        out_shape=jax.ShapeDtypeStruct(shape, value.dtype),
        in_specs=[in_vmem],
        out_specs=in_vmem,
        scratch_shapes=[pltpu.SemaphoreType.DMA((8,)), pltpu.SemaphoreType.DMA((8,))],
        compiler_params=pltpu.CompilerParams(collective_id=collective_id, has_side_effects=True),
        name="swap_heads",
    )(value)


def gelu_slope(value):
    inner = 0.7978845608028654 * (value + 0.044715 * value * value * value)
    turned = jnp.tanh(inner)
    slope = 0.7978845608028654 * (1.0 + 3.0 * 0.044715 * value * value)
    return 0.5 * (1.0 + turned) + 0.5 * value * (1.0 - turned * turned) * slope


def places_here():
    return lax.axis_index("ctx"), lax.axis_index("wa")


def meet_all():
    c, w = places_here()
    owner = c // 2
    own = owner == w
    barrier = pltpu.get_barrier_semaphore()
    for j in range(1, 8):
        signal_to(barrier, c ^ j, w)
    for j in range(1, 4):
        signal_to(barrier, c, w ^ j)
    for j in range(1, 8):
        signal_to(barrier, c ^ j, owner)
    for r in range(4):
        for h in range(2):

            @pl.when(jnp.logical_not(jnp.logical_and(2 * w + h == c, r == 0)))
            def _(r=r, h=h):
                signal_to(barrier, 2 * w + h, w ^ r)

    @pl.when(jnp.logical_not(own))
    def _():
        signal_to(barrier, c, owner)

    pl.semaphore_wait(barrier, 26 - 2 * own.astype(jnp.int32))


def meet_lines():
    c, w = places_here()
    barrier = pltpu.get_barrier_semaphore()
    for j in range(1, 8):
        signal_to(barrier, c ^ j, w)
    for j in range(1, 4):
        signal_to(barrier, c, w ^ j)
    pl.semaphore_wait(barrier, 10)


def remote(source, target, send, recv, ctx, wa):
    return pltpu.make_async_remote_copy(
        src_ref=source,
        dst_ref=target,
        send_sem=send,
        recv_sem=recv,
        device_id=(ctx, wa),
        device_id_type=mesh_id,
    )


class GatherRows:

    def __init__(self, buf, send, recv):
        self.buf, self.send, self.recv = buf, send, recv
        self.c, self.w = places_here()

    def copy(self, k):
        source, entry, j = ((0, 1, 1), (0, 2, 2), (2, 3, 1))[k]
        return remote(
            self.buf.at[source],
            self.buf.at[entry],
            self.send.at[k],
            self.recv.at[k],
            self.c,
            self.w ^ j,
        )

    def start(self):
        self.copy(1).start()
        self.copy(0).start()

    def near(self):
        self.copy(0).wait()

    def relay(self):
        self.copy(1).wait()
        self.copy(2).start()

    def far(self):
        self.copy(2).wait()


class SumRows:

    def __init__(self, out_buf, in_buf, send, recv):
        self.out, self.inn, self.send, self.recv = out_buf, in_buf, send, recv
        self.c, self.w = places_here()

    def copy(self, k):
        j = (1, 1, 2)[k]
        return remote(
            self.out.at[k], self.inn.at[k], self.send.at[k], self.recv.at[k], self.c, self.w ^ j
        )

    def give_near(self, value):
        self.out[0] = value.astype(bf16)
        self.copy(0).start()

    def give_far(self, value):
        self.out[1] = value.astype(bf16)
        self.copy(1).start()

    def pass_on(self, value):
        self.copy(1).wait()
        self.out[2] = (value + self.inn[1].astype(f32)).astype(bf16)
        self.copy(2).start()

    def total(self, value):
        self.copy(0).wait()
        value = value + self.inn[0].astype(f32)
        self.copy(2).wait()
        return value + self.inn[2].astype(f32)


class CtxSum:

    def __init__(self, send, recv, x=None, half=None, part=None, share=None, out=None, spread=0):
        self.send, self.recv = send, recv
        self.x, self.half, self.part, self.share, self.out = x, half, part, share, out
        self.spread = spread
        self.c, self.w = places_here()
        self.z, self.y = self.c // 2, self.c % 2

    def y_copy(self):
        return remote(
            self.x.at[:, 1 - self.y], self.half, self.send.at[0], self.recv.at[0], self.c ^ 1, self.w
        )

    def start_y(self):
        self.y_copy().start()

    def finish_y(self):
        self.y_copy().wait()
        for z in range(4):
            mine = self.x[z, self.y].astype(f32)
            self.half[z] = (self.half[z].astype(f32) + mine).astype(bf16)

    def z_copy(self, j):
        return remote(
            self.half.at[self.z ^ j],
            self.part.at[j - 1],
            self.send.at[j],
            self.recv.at[j],
            self.c ^ (2 * j),
            self.w,
        )

    def start_z(self):
        for j in (2, 3, 1):
            self.z_copy(j).start()

    def finish_z(self):
        total = self.half[self.z].astype(f32)
        for j in (1, 2, 3):
            self.z_copy(j).wait()
            total = total + self.part[j - 1].astype(f32)
        self.share[...] = total.astype(bf16)

    def columns(self, place):
        width = self.spread
        return self.out.at[self.z, self.y, :, pl.ds(pl.multiple_of(place * width, 128), width)]

    def wa_copy(self, j, place):
        return remote(
            self.share.at[self.w ^ j],
            self.columns(place),
            self.send.at[3 + j],
            self.recv.at[3 + j],
            self.c,
            self.w ^ j,
        )

    def own_copy(self):
        source = self.share.at[self.w] if self.spread else self.share
        target = self.columns(self.w) if self.spread else self.out.at[self.z, self.y]
        return pltpu.make_async_copy(source, target, self.send.at[11])

    def start_wa(self):
        if self.spread:
            for j in (2, 3, 1):
                self.wa_copy(j, self.w).start()
        self.own_copy().start()

    def finish_wa(self):
        self.own_copy().wait()
        if self.spread:
            for j in (1, 2, 3):
                self.wa_copy(j, self.w).wait_send()
                self.wa_copy(j, self.w ^ j).wait_recv()

    def back_z_copy(self, j, z):
        mine = self.out.at[z, self.y]
        return remote(mine, mine, self.send.at[6 + j], self.recv.at[6 + j], self.c ^ (2 * j), self.w)

    def start_back_z(self):
        for j in (2, 3, 1):
            self.back_z_copy(j, self.z).start()

    def finish_back_z(self):
        for j in (1, 2, 3):
            self.back_z_copy(j, self.z).wait_send()
            self.back_z_copy(j, self.z ^ j).wait_recv()

    def back_y_copy(self, y):
        part = self.out.at[:, y]
        return remote(part, part, self.send.at[10], self.recv.at[10], self.c ^ 1, self.w)

    def start_back_y(self):
        self.back_y_copy(self.y).start()

    def finish_back_y(self):
        self.back_y_copy(self.y).wait_send()
        self.back_y_copy(1 - self.y).wait_recv()


def put_shares(target, grads, first=0):
    count = grads.shape[0] // 32
    padded = target.shape[3]
    for place in range(4):
        for share in range(8):
            start = (place * 8 + share) * count
            part = grads[start : start + count]
            part = jnp.concatenate([part, jnp.zeros((padded - count, part.shape[1]), f32)], axis=0)
            target[share // 2, share % 2, place, :, first : first + part.shape[1]] = part.astype(bf16)


def put_rows(target, grads):
    count = grads.shape[0] // 8
    for share in range(8):
        target[share // 2, share % 2] = grads[share * count : (share + 1) * count].astype(bf16)


def middle_back_kernel(
    out_grad_ref,
    down_ref,
    pre_act_ref,
    activated_ref,
    normed_c_ref,
    hidden_two_ref,
    hidden_one_ref,
    gains_ref,
    up_any,
    cross_out_any,
    crossed_any,
    cross_q_any,
    cross_pair_any,
    cross_query_any,
    near_any,
    normed_b_any,
    output_any,
    attended_any,
    one_grad_ref,
    gain_grad_ref,
    heads_ref,
    pair_grad_ref,
    down_share,
    up_share,
    cross_half,
    cross_out_x,
    output_x,
    up_ref,
    cross_out_ref,
    crossed_ref,
    cross_q_ref,
    cross_pair_ref,
    cross_query_ref,
    near_ref,
    normed_b_ref,
    output_ref,
    attended_ref,
    rows_ref,
    rows_two_ref,
    rows_one_ref,
    pre_grad_ref,
    query_grad_ref,
    heads_out,
    give_ref,
    take_ref,
    give_two_ref,
    take_two_ref,
    keep_ref,
    down_x,
    down_half,
    down_part,
    up_x,
    up_half,
    up_part,
    cross_x,
    load_sem,
    g_send,
    g_recv,
    s_send,
    s_recv,
    h_send,
    h_recv,
    down_send,
    down_recv,
    up_send,
    up_recv,
    cross_send,
    cross_recv,
):
    c, w = places_here()
    tok = out_grad_ref.shape[0]
    scale = HEAD_DIM ** (-0.5)
    sources = (
        up_any,
        cross_out_any,
        crossed_any,
        cross_q_any,
        cross_pair_any,
        cross_query_any,
        near_any,
        normed_b_any,
        output_any,
        attended_any,
    )
    targets = (
        up_ref,
        cross_out_ref,
        crossed_ref,
        cross_q_ref,
        cross_pair_ref,
        cross_query_ref,
        near_ref,
        normed_b_ref,
        output_ref,
        attended_ref,
    )
    loads = [
        pltpu.make_async_copy(source, target, load_sem.at[k])
        for k, (source, target) in enumerate(zip(sources, targets))
    ]
    for load in loads:
        load.start()
    rows_ref[0] = out_grad_ref[...].astype(bf16)
    meet_all()
    first = GatherRows(rows_ref, g_send.at[0], g_recv.at[0])
    second = GatherRows(rows_two_ref, g_send.at[1], g_recv.at[1])
    third = GatherRows(rows_one_ref, g_send.at[2], g_recv.at[2])
    sum_c = SumRows(give_ref, take_ref, s_send.at[0], s_recv.at[0])
    sum_b = SumRows(give_two_ref, take_two_ref, s_send.at[1], s_recv.at[1])
    down = CtxSum(down_send, down_recv, down_x, down_half, down_part, down_share)
    up = CtxSum(up_send, up_recv, up_x, up_half, up_part, up_share)
    cross = CtxSum(cross_send, cross_recv, cross_x, cross_half)

    first.start()

    def feed_back(r):
        part = pl.ds(r * tok, tok)
        act_grad = dot_nt(rows_ref[r], down_ref[...])
        pre_grad_ref[part, :] = (act_grad * gelu_slope(pre_act_ref[part, :])).astype(bf16)
        return dot_nt(pre_grad_ref[part, :], up_ref[...])

    loads[0].wait()
    keep_ref[0] = feed_back(0)
    first.near()
    sum_c.give_near(feed_back(1))
    first.relay()
    keep_ref[1] = feed_back(2)
    first.far()
    sum_c.give_far(feed_back(3))
    sum_c.pass_on(keep_ref[1])
    put_rows(down_x, dot_tn(activated_ref[...], rows_ref[...].reshape(4 * tok, -1)))
    down.start_y()
    put_shares(up_x, dot_tn(normed_c_ref[...], pre_grad_ref[...]))
    for load in loads[1:]:
        load.wait()
    normed_grad = sum_c.total(keep_ref[0])
    hidden = hidden_two_ref[...]
    inverse = inverse_rms(hidden)
    two_grad = out_grad_ref[...] + norm_pull(hidden, inverse, gains_ref[2:3, :], normed_grad)
    gain_three = jnp.sum(normed_grad * hidden * inverse, axis=0, keepdims=True)
    keep_ref[1] = two_grad
    rows_two_ref[0] = two_grad.astype(bf16)

    second.start()
    width = cross_q_ref.shape[1]

    def cross_back(r):
        part = pl.ds(r * tok, tok)
        crossed_grad = dot_nt(rows_two_ref[r], cross_out_ref[...]).astype(bf16)
        for g in range(tok // GROUP):
            at = r * tok + g * GROUP
            near = (r * (tok // GROUP) + g) * NK
            query = stack_all(cross_q_ref[at : at + GROUP, :])
            grad = stack_all(crossed_grad[g * GROUP : (g + 1) * GROUP])
            keys = cross_pair_ref[near : near + NK, 0:width]
            shares = cross_shares(query, keys)
            share_grad = dot_nt(grad, cross_pair_ref[near : near + NK, width:])
            delta = jnp.sum(shares * share_grad, axis=1, keepdims=True)
            score_grad = (shares * (share_grad - delta)).astype(bf16)
            query_grad = join_all(dot_nn(score_grad, keys)) * scale
            query_grad_ref[at : at + GROUP, :] = query_grad.astype(bf16)
            pair_grad_ref[near : near + NK, 0:width] = (dot_tn(score_grad, query) * scale).astype(bf16)
            pair_grad_ref[near : near + NK, width:] = dot_tn(shares.astype(bf16), grad).astype(bf16)
        return dot_nt(query_grad_ref[part, :], cross_query_ref[...])

    keep_ref[0] = cross_back(0)
    second.near()
    sum_b.give_near(cross_back(1))
    second.relay()
    keep_ref[2] = cross_back(2)
    second.far()
    sum_b.give_far(cross_back(3))
    sum_b.pass_on(keep_ref[2])
    down.finish_y()
    down.start_z()
    up.start_y()
    normed_b = normed_b_ref[...]
    put_rows(cross_out_x, dot_tn(crossed_ref[...], rows_two_ref[...].reshape(4 * tok, -1)))
    put_shares(cross_x, dot_tn(normed_b, query_grad_ref[...]), 0)
    normed_grad = sum_b.total(keep_ref[0])
    hidden = hidden_one_ref[...]
    inverse = inverse_rms(hidden)
    one_grad = keep_ref[1] + norm_pull(hidden, inverse, gains_ref[1:2, :], normed_grad)
    gain_two = jnp.sum(normed_grad * hidden * inverse, axis=0, keepdims=True)
    gain_grad_ref[...] = jnp.concatenate(
        [gain_two, gain_three, jnp.zeros((6, gain_two.shape[1]), f32)], axis=0
    )
    one_grad_ref[...] = one_grad
    rows_one_ref[0] = one_grad.astype(bf16)

    third.start()
    put_shares(cross_x, dot_tn(near_ref[...], pair_grad_ref[...]), width)

    def head_copy(r, h):
        return remote(
            heads_out.at[r, :, h * 128 : (h + 1) * 128],
            heads_ref.at[c],
            h_send.at[r * 2 + h],
            h_recv.at[c],
            2 * w + h,
            w ^ r,
        )

    def head_back(r):
        heads_out[r] = dot_nt(rows_one_ref[r], output_ref[...]).astype(bf16)
        for h in range(2):
            mine = jnp.logical_and(2 * w + h == c, r == 0)

            @pl.when(jnp.logical_not(mine))
            def _():
                head_copy(r, h).start()

            @pl.when(mine)
            def _():
                pltpu.make_async_copy(
                    heads_out.at[r, :, h * 128 : (h + 1) * 128], heads_ref.at[c], h_recv.at[c]
                ).start()

    head_back(0)
    third.near()
    head_back(1)
    third.relay()
    head_back(2)
    third.far()
    head_back(3)
    up.finish_y()
    up.start_z()
    cross.start_y()
    put_rows(output_x, dot_tn(attended_ref[...], rows_one_ref[...].reshape(4 * tok, -1)))
    for block in range(8):
        remote(
            heads_out.at[0, :, 0:128], heads_ref.at[block], h_send.at[0], h_recv.at[block], c ^ 1, w
        ).wait_recv()
    for r in range(4):
        for h in range(2):

            @pl.when(jnp.logical_not(jnp.logical_and(2 * w + h == c, r == 0)))
            def _(r=r, h=h):
                head_copy(r, h).wait_send()

    down.finish_z()
    up.finish_z()
    cross.finish_y()


def middle_back(
    out_grad,
    down_weight,
    pre_act,
    activated,
    normed_c,
    hidden_two,
    hidden_one,
    gains,
    later,
    collective_id,
):
    tok, width = out_grad.shape
    hidden = down_weight.shape[0]
    cols = later[3].shape[1]
    near = later[6].shape[0]
    any_space = pl.BlockSpec(memory_space=pl.ANY)
    dma = pltpu.SemaphoreType.DMA
    shape = jax.ShapeDtypeStruct
    vmem = pltpu.VMEM
    rows = -(-(width // 32) // 8) * 8
    return pl.pallas_call(
        middle_back_kernel,
        out_shape=[
            shape((tok, width), f32),
            shape((8, width), f32),
            shape((8, tok, 128), bf16),
            shape((near, 2 * cols), bf16),
            shape((hidden // 8, width), bf16),
            shape((4, rows, hidden), bf16),
            shape((4, 4, rows, 3 * cols), bf16),
            shape((4, 2, cols // 8, width), bf16),
            shape((4, 2, cols // 8, width), bf16),
        ],
        in_specs=[in_vmem] * 8 + [any_space] * 10,
        out_specs=[in_vmem] * 9,
        scratch_shapes=[vmem(value.shape, value.dtype) for value in later]
        + [
            vmem((4, tok, width), bf16),
            vmem((4, tok, width), bf16),
            vmem((4, tok, width), bf16),
            vmem((4 * tok, hidden), bf16),
            vmem((4 * tok, cols), bf16),
            vmem((4, tok, cols), bf16),
            vmem((3, tok, width), bf16),
            vmem((3, tok, width), bf16),
            vmem((3, tok, width), bf16),
            vmem((3, tok, width), bf16),
            vmem((3, tok, width), f32),
            vmem((4, 2, hidden // 8, width), bf16),
            vmem((4, hidden // 8, width), bf16),
            vmem((3, hidden // 8, width), bf16),
            vmem((4, 2, 4, rows, hidden), bf16),
            vmem((4, 4, rows, hidden), bf16),
            vmem((3, 4, rows, hidden), bf16),
            vmem((4, 2, 4, rows, 3 * cols), bf16),
            dma((10,)),
            dma((3, 3)),
            dma((3, 3)),
            dma((2, 3)),
            dma((2, 3)),
            dma((8,)),
            dma((8,)),
            dma((12,)),
            dma((12,)),
            dma((12,)),
            dma((12,)),
            dma((12,)),
            dma((12,)),
        ],
        compiler_params=pltpu.CompilerParams(
            collective_id=collective_id, has_side_effects=True, vmem_limit_bytes=58 * 2**20
        ),
        name="middle_back",
    )(out_grad, down_weight, pre_act, activated, normed_c, hidden_two, hidden_one, gains, *later)


def finish_kernel(
    query_grad_ref,
    normed_a_ref,
    waves_ref,
    table_grad_ref,
    small_ref,
    pair_grad_ref,
    pair_cols_ref,
    down_share,
    up_share,
    cross_half,
    cross_out_x,
    output_x,
    one_grad_ref,
    tokens_ref,
    gains_ref,
    full_any,
    tokens_grad_ref,
    near_grad_ref,
    total_ref,
    down_out,
    up_out,
    cross_out,
    cross_out_out,
    output_out,
    pair_out,
    full_ref,
    mine_ref,
    sums_ref,
    cross_part,
    cross_share,
    cross_out_half,
    cross_out_part,
    cross_out_share,
    output_half,
    output_part,
    output_share,
    pair_give,
    pair_take,
    pair_share,
    near_give,
    near_take,
    near_keep,
    near_sum,
    far_sum,
    load_sem,
    b_send,
    b_recv,
    e_send,
    e_recv,
    n_send,
    n_recv,
    s_send,
    s_recv,
    chain_send,
    chain_recv,
):
    c, w = places_here()
    load = pltpu.make_async_copy(full_any, full_ref, load_sem)
    load.start()
    down = CtxSum(chain_send.at[0], chain_recv.at[0], share=down_share, out=down_out)
    up = CtxSum(
        chain_send.at[1], chain_recv.at[1], share=up_share, out=up_out, spread=up_share.shape[2]
    )
    cross = CtxSum(
        chain_send.at[2],
        chain_recv.at[2],
        half=cross_half,
        part=cross_part,
        share=cross_share,
        out=cross_out,
        spread=cross_share.shape[2],
    )
    ctx_o = CtxSum(
        chain_send.at[3],
        chain_recv.at[3],
        cross_out_x,
        cross_out_half,
        cross_out_part,
        cross_out_share,
        cross_out_out,
    )
    out_o = CtxSum(
        chain_send.at[4],
        chain_recv.at[4],
        output_x,
        output_half,
        output_part,
        output_share,
        output_out,
    )
    pair = CtxSum(chain_send.at[5], chain_recv.at[5], share=pair_share, out=pair_out)
    sum_pair = SumRows(pair_give, pair_take, e_send, e_recv)
    sum_near = SumRows(near_give, near_take, n_send, n_recv)
    width = query_grad_ref.shape[2]

    def columns(block):
        return mine_ref.at[:, pl.ds(pl.multiple_of(block * width, 128), width)]

    def block_copy(j, block):
        return remote(
            query_grad_ref.at[c ^ j], columns(block), b_send.at[j], b_recv.at[j], c ^ j, w
        )

    meet_lines()
    ctx_o.start_y()
    out_o.start_y()
    cross.start_z()
    up.start_wa()
    down.start_wa()
    for j in (4, 6, 5, 7, 2, 3, 1):
        block_copy(j, c).start()
    own = pltpu.make_async_copy(query_grad_ref.at[c], columns(c), b_recv.at[0])
    own.start()

    query_grad = query_grad_ref[...].reshape(-1, width)
    high = table_grad_ref[...].astype(bf16)
    low = (table_grad_ref[...] - high.astype(f32)).astype(bf16)
    share = sums_ref.shape[1]
    mixed = dot_tn(normed_a_ref[...], query_grad)
    turned = dot_tn(waves_ref[...], high) + dot_tn(waves_ref[...], low)
    for place in range(4):
        at = place * share
        sums_ref[place] = jnp.concatenate([mixed[at : at + share], turned[at : at + share]], axis=1)
    sum_pair.give_far(sums_ref[w ^ 3])
    sum_pair.give_near(sums_ref[w ^ 1])
    down.finish_wa()
    down.start_back_z()
    up.finish_wa()
    up.start_back_z()
    ctx_o.finish_y()
    ctx_o.start_z()
    out_o.finish_y()
    out_o.start_z()
    sum_pair.pass_on(sums_ref[w ^ 2])

    count = near_grad_ref.shape[0]

    def near_part(r):
        return dot_nt(pair_grad_ref[r * count : (r + 1) * count, :], pair_cols_ref[...])

    sum_near.give_far(near_part(3))
    sum_near.give_near(near_part(1))
    cross.finish_z()
    cross.start_wa()
    pair_share[...] = sum_pair.total(sums_ref[w]).astype(bf16)
    pair.start_wa()
    pair.finish_wa()
    pair.start_back_z()
    sum_near.pass_on(near_part(2))
    near_keep[...] = near_part(0)
    ctx_o.finish_z()
    ctx_o.start_wa()
    out_o.finish_z()
    out_o.start_wa()
    cross.finish_wa()
    cross.start_back_z()
    ctx_o.finish_wa()
    ctx_o.start_back_z()
    out_o.finish_wa()
    out_o.start_back_z()
    down.finish_back_z()
    down.start_back_y()

    for j in range(1, 8):
        block_copy(j, c ^ j).wait_recv()
    own.wait()
    load.wait()
    normed_grad = dot_nt(mine_ref[...], full_ref[...])
    hidden = tokens_ref[...].astype(f32)
    inverse = inverse_rms(hidden)
    tokens_grad_ref[...] = one_grad_ref[...] + norm_pull(
        hidden, inverse, gains_ref[0:1, :], normed_grad
    )
    gain_one = jnp.sum(normed_grad * hidden * inverse, axis=0, keepdims=True)
    small_rows = small_ref.shape[0]
    total_ref[...] = small_ref[...]
    total_ref[small_rows - 8 : small_rows - 7, 0 : gain_one.shape[1]] = gain_one

    def small_copy(source, k):
        near = k < 3
        j = k + 1 if near else k - 2
        return remote(
            source,
            near_sum.at[k] if near else far_sum.at[k - 3],
            s_send.at[k],
            s_recv.at[k],
            c if near else c ^ j,
            w ^ j if near else w,
        )

    for k in range(3):
        small_copy(total_ref, k).start()
    up.finish_back_z()
    up.start_back_y()
    pair.finish_back_z()
    pair.start_back_y()
    near_grad_ref[...] = sum_near.total(near_keep[...])
    for k in range(3):
        small_copy(total_ref, k).wait()
    total_ref[...] = tree_sum([total_ref[...]] + [near_sum[k] for k in range(3)])
    for k in range(3, 10):
        small_copy(total_ref, k).start()
    cross.finish_back_z()
    cross.start_back_y()
    ctx_o.finish_back_z()
    ctx_o.start_back_y()
    out_o.finish_back_z()
    out_o.start_back_y()
    for k in range(3, 10):
        small_copy(total_ref, k).wait()
    total_ref[...] = tree_sum([total_ref[...]] + [far_sum[k] for k in range(7)])
    for j in range(1, 8):
        block_copy(j, c).wait_send()
    for chain in (down, up, pair, cross, ctx_o, out_o):
        chain.finish_back_y()


def finish(
    query_grad,
    normed_a,
    waves,
    table_grad,
    small,
    pair_grad,
    pair_cols,
    down_share,
    up_share,
    cross_half,
    cross_out_x,
    output_x,
    one_grad,
    tokens,
    gains,
    full,
    collective_id,
):
    tok, width = tokens.shape
    near = pair_grad.shape[0]
    rows = up_share.shape[1]
    cols = output_x.shape[2] * 8
    share = width // 4
    any_space = pl.BlockSpec(memory_space=pl.ANY)
    dma = pltpu.SemaphoreType.DMA
    shape = jax.ShapeDtypeStruct
    vmem = pltpu.VMEM
    return pl.pallas_call(
        finish_kernel,
        out_shape=[
            shape((tok, width), f32),
            shape((near // 4, width), f32),
            shape(small.shape, f32),
            shape((4, 2) + down_share.shape, bf16),
            shape((4, 2, rows, 4 * up_share.shape[2]), bf16),
            shape((4, 2, rows, 12 * cols), bf16),
            shape((4, 2, cols // 8, width), bf16),
            shape((4, 2, cols // 8, width), bf16),
            shape((4, 2, share, 512), bf16),
        ],
        in_specs=[in_vmem] * 15 + [any_space],
        out_specs=[in_vmem] * 9,
        scratch_shapes=[
            vmem(full.shape, bf16),
            vmem((tok, full.shape[1]), bf16),
            vmem((4, share, 512), f32),
            vmem((3, 4, rows, 3 * cols), bf16),
            vmem((4, rows, 3 * cols), bf16),
            vmem((4, cols // 8, width), bf16),
            vmem((3, cols // 8, width), bf16),
            vmem((cols // 8, width), bf16),
            vmem((4, cols // 8, width), bf16),
            vmem((3, cols // 8, width), bf16),
            vmem((cols // 8, width), bf16),
            vmem((3, share, 512), bf16),
            vmem((3, share, 512), bf16),
            vmem((share, 512), bf16),
            vmem((3, near // 4, width), bf16),
            vmem((3, near // 4, width), bf16),
            vmem((near // 4, width), f32),
            vmem((3,) + small.shape, f32),
            vmem((7,) + small.shape, f32),
            dma(()),
            dma((8,)),
            dma((8,)),
            dma((3,)),
            dma((3,)),
            dma((3,)),
            dma((3,)),
            dma((10,)),
            dma((10,)),
            dma((6, 12)),
            dma((6, 12)),
        ],
        compiler_params=pltpu.CompilerParams(
            collective_id=collective_id, has_side_effects=True, vmem_limit_bytes=60 * 2**20
        ),
        name="finish",
    )(
        query_grad,
        normed_a,
        waves,
        table_grad,
        small,
        pair_grad,
        pair_cols,
        down_share,
        up_share,
        cross_half,
        cross_out_x,
        output_x,
        one_grad,
        tokens,
        gains,
        full,
    )


def skew(wide, count):
    lead = wide.shape[:-2]
    rows, span = wide.shape[-2:]
    edge = [(0, 0)] * len(lead)
    padded = jnp.pad(wide, edge + [(0, 0), (0, 1)])
    flat = padded.reshape(lead + (rows * (span + 1),))
    flat = lax.slice_in_dim(flat, rows - 1, rows - 1 + rows * span, axis=len(lead))
    return flat.reshape(lead + (rows, span))[..., :count]


def unskew(grad, span):
    lead = grad.shape[:-2]
    rows, count = grad.shape[-2:]
    edge = [(0, 0)] * len(lead)
    wide = jnp.pad(grad, edge + [(0, 0), (0, span - count)])
    flat = jnp.pad(wide.reshape(lead + (rows * span,)), edge + [(rows - 1, 1)])
    return flat.reshape(lead + (rows, span + 1))[..., :span]


def tile_scores(content_rows, position_rows, key_rows, relative, row_start, key_start):
    rows = content_rows.shape[0]
    count = key_rows.shape[0]
    scale = content_rows.shape[-1] ** (-0.5)
    content = jnp.einsum("qhe,khe->hqk", content_rows, key_rows, preferred_element_type=f32)
    wide = jnp.einsum("qhe,whe->hqw", position_rows, relative, preferred_element_type=f32)
    scores = (content + skew(wide, count)) * scale
    causal = (row_start + jnp.arange(rows))[:, None] >= (key_start + jnp.arange(count))[None, :]
    return (scores, causal[None])


def tile_forward(
    content_rows, position_rows, row_start, relative, key_rows, value_rows, key_start, state
):
    top, total, accum = state
    scores, causal = tile_scores(
        content_rows, position_rows, key_rows, relative, row_start, key_start
    )
    scores = jnp.where(causal, scores, neg_big)
    new_top = jnp.maximum(top, jnp.max(scores, axis=-1))
    raised = jnp.where(causal, jnp.exp(scores - new_top[..., None]), 0.0)
    fade = jnp.exp(top - new_top)
    total = total * fade + jnp.sum(raised, axis=-1)
    accum = accum * fade[..., None] + jnp.einsum(
        "hqk,khe->hqe", raised.astype(bf16), value_rows, preferred_element_type=f32
    )
    return (new_top, total, accum)


def tile_backward(
    content_rows,
    position_rows,
    row_start,
    relative,
    key_rows,
    value_rows,
    grad_rows,
    log_rows,
    delta_rows,
    key_start,
):
    scores, causal = tile_scores(
        content_rows, position_rows, key_rows, relative, row_start, key_start
    )
    scale = content_rows.shape[-1] ** (-0.5)
    shares = jnp.where(causal, jnp.exp(scores - log_rows[..., None]), 0.0)
    share_grad = jnp.einsum("qhe,khe->hqk", grad_rows, value_rows, preferred_element_type=f32)
    score_grad = (shares * (share_grad - delta_rows[..., None])).astype(bf16)
    content_grad = jnp.einsum("hqk,khe->qhe", score_grad, key_rows, preferred_element_type=f32)
    wide_grad = unskew(score_grad, relative.shape[0])
    position_grad = jnp.einsum("hqw,whe->qhe", wide_grad, relative, preferred_element_type=f32)
    table_part = jnp.einsum("hqw,qhe->whe", wide_grad, position_rows, preferred_element_type=f32)
    key_grad = jnp.einsum("hqk,qhe->khe", score_grad, content_rows, preferred_element_type=f32)
    value_grad = jnp.einsum(
        "hqk,qhe->khe", shares.astype(bf16), grad_rows, preferred_element_type=f32
    )
    return (
        content_grad * scale,
        position_grad * scale,
        table_part * scale,
        key_grad * scale,
        value_grad,
    )


def nest_tiles(tile_fn):
    inner = jax.vmap(tile_fn, in_axes=(0, 0, 0, 0, None, None, 0))
    return jax.vmap(inner, in_axes=(0, 0, None, None, 0, 0, 0))


def to_global(stored, inverse, block):
    seqs, seq_len, width = stored.shape
    blocks = stored.reshape(seqs, seq_len // block, block * width)
    chosen = (inverse[:, None] == jnp.arange(seq_len // block)[None, :]).astype(bf16)
    moved = jnp.einsum("gs,nsx->ngx", chosen, blocks, preferred_element_type=f32)
    return moved.astype(bf16).reshape(stored.shape)


class SplitQueries:

    def __init__(self, query, keys, values, biases, relative, block_order, inverse, block):
        self.seqs, self.tok_dev, self.width = keys.shape
        self.heads = self.width // HEAD_DIM
        self.block = block
        self.block_order = block_order
        ctx_count = lax.axis_size("ctx")
        self.seq_len = self.tok_dev * ctx_count
        self.key_len = min(512, self.seq_len)
        pad = jnp.zeros((self.key_len + block, self.width), bf16)
        table = jnp.concatenate([relative, pad], axis=0)
        self.table = table.reshape(-1, self.heads, HEAD_DIM)
        lead = (self.seqs, 2, block, self.heads, HEAD_DIM)
        self.content = (query + biases[0]).astype(bf16).reshape(lead)
        self.position = (query + biases[1]).astype(bf16).reshape(lead)
        gathered = [lax.all_gather(part, "ctx", axis=1, tiled=True) for part in (keys, values)]
        shape = (self.seqs, self.seq_len, self.heads, HEAD_DIM)
        self.keys, self.values = [to_global(part, inverse, block).reshape(shape) for part in gathered]
        self.starts = lax.dynamic_slice_in_dim(block_order, 2 * lax.axis_index("ctx"), 2, 0) * block

    def rows(self, index):
        start = index * self.key_len
        keys = lax.dynamic_slice_in_dim(self.keys, start, self.key_len, 1)
        values = lax.dynamic_slice_in_dim(self.values, start, self.key_len, 1)
        span = self.block + self.key_len
        offsets = [self.seq_len - self.block - self.starts[slot] + start for slot in range(2)]
        relative = [lax.dynamic_slice_in_dim(self.table, offset, span, 0) for offset in offsets]
        return start, keys, values, jnp.stack(relative), offsets

    def to_stored(self, part):
        count = self.seq_len // self.block
        blocks = part.reshape(self.seqs, count, self.block * self.width)
        chosen = (self.block_order[:, None] == jnp.arange(count)[None, :]).astype(f32)
        moved = jnp.einsum("sg,ngx->nsx", chosen, blocks, precision=highest)
        return moved.reshape(self.seqs, self.seq_len, self.width)

    def forward(self):
        def step(state, index):
            start, keys, values, relative, _ = self.rows(index)

            def tile(content, position, row_start, table, keys_seq, values_seq, tile_state):
                return tile_forward(
                    content, position, row_start, table, keys_seq, values_seq, start, tile_state
                )

            return nest_tiles(tile)(
                self.content, self.position, self.starts, relative, keys, values, state
            ), None

        shape = (self.seqs, 2, self.heads, self.block)
        state = (
            jnp.full(shape, neg_big, f32),
            jnp.zeros(shape, f32),
            jnp.zeros(shape + (HEAD_DIM,), f32),
        )
        (top, total, accum), _ = lax.scan(step, state, jnp.arange(self.seq_len // self.key_len))
        self.log_total = top + jnp.log(total)
        self.out = accum / total[..., None]
        moved = jnp.transpose(self.out, (0, 1, 3, 2, 4))
        return moved.reshape(self.seqs * self.tok_dev, self.width).astype(bf16)

    def backward(self, grad):
        block, seq_len, key_len = self.block, self.seq_len, self.key_len
        lead = (self.seqs, 2, block, self.heads, HEAD_DIM)
        grad = grad.reshape(lead)
        delta = jnp.einsum("sbqhe,sbhqe->sbhq", grad.astype(f32), self.out)
        def step(carry, index):
            start, keys, values, relative, offsets = self.rows(index)

            def tile(content, position, row_start, table, keys_seq, values_seq, extra):
                return tile_backward(
                    content, position, row_start, table, keys_seq, values_seq, *extra, start
                )

            extra = (grad, self.log_total, delta)
            parts = nest_tiles(tile)(
                self.content, self.position, self.starts, relative, keys, values, extra
            )
            table = carry[2]
            table_sum = jnp.sum(parts[2], axis=0)
            for slot in range(2):
                offset = offsets[slot]
                current = lax.dynamic_slice_in_dim(table, offset, block + key_len, 0)
                table = lax.dynamic_update_slice_in_dim(table, current + table_sum[slot], offset, 0)
            sums = []
            for total, part in zip(carry[3:], parts[3:]):
                current = lax.dynamic_slice_in_dim(total, start, key_len, 1)
                part = current + jnp.sum(part, axis=1)
                sums.append(lax.dynamic_update_slice_in_dim(total, part, start, 1))
            key_acc, value_acc = sums
            return (carry[0] + parts[0], carry[1] + parts[1], table, key_acc, value_acc), None

        zero_tiles = jnp.zeros(lead, f32)
        zero_keys = jnp.zeros((self.seqs, seq_len, self.heads, HEAD_DIM), f32)
        carry = (zero_tiles, zero_tiles, jnp.zeros(self.table.shape, f32), zero_keys, zero_keys)
        carry, _ = lax.scan(step, carry, jnp.arange(seq_len // key_len))
        owned = [
            lax.psum_scatter(
                self.to_stored(part), "ctx", scatter_dimension=1, tiled=True
            )
            for part in carry[3:]
        ]
        flat = (self.seqs * self.tok_dev, self.width)
        query_grad = (carry[0] + carry[1]).reshape(flat).astype(bf16)
        key_grad, value_grad = [part.reshape(flat).astype(bf16) for part in owned]
        bias_grads = jnp.stack(
            [jnp.sum(part, axis=(0, 1, 2)).reshape(self.width) for part in carry[:2]]
        )
        table_grad = carry[2].reshape(-1, self.width)[:seq_len]
        return query_grad, key_grad, value_grad, bias_grads, table_grad


def local_general(
    tokens,
    neighbours,
    teacher,
    valid_mask,
    block_order,
    query_weight,
    key_weight,
    value_weight,
    output_weight,
    relative_weight,
    content_bias,
    position_bias,
    cross_query_weight,
    cross_key_weight,
    cross_value_weight,
    cross_output_weight,
    up_weight,
    down_weight,
    attention_gain,
    cross_gain,
    feedforward_gain,
):
    places = lax.axis_size("wa")
    ctx_count = lax.axis_size("ctx")
    place = lax.axis_index("wa")
    here = lax.axis_index("ctx")
    _, tok_dev, width = tokens.shape
    seq_len = tok_dev * ctx_count
    block = tok_dev // 2
    cols = HEADS * HEAD_DIM // places
    rows = places * tok_dev

    token_parts = gather_parts(tokens[0])
    query_cols, key_cols, value_cols = [
        take_columns(weight) for weight in (query_weight, key_weight, value_weight)
    ]
    relative_cols = take_columns(relative_weight)
    gains = lax.all_gather(
        jnp.stack([attention_gain, cross_gain, feedforward_gain]), "wa", axis=1, tiled=True
    ).astype(f32)
    gain_one, gain_two, gain_three = gains[0:1], gains[1:2], gains[2:3]
    cross_query_cols, cross_key_cols, cross_value_cols = [
        take_columns(weight) for weight in (cross_query_weight, cross_key_weight, cross_value_weight)
    ]
    cross_pair_cols = jnp.concatenate([cross_key_cols, cross_value_cols], axis=1)
    near_rows = jnp.concatenate(gather_parts(neighbours.reshape(-1, width)), axis=0)
    up_cols = take_columns(up_weight)
    valid = valid_mask.astype(f32).reshape(tok_dev, 1)
    count = jnp.sum(valid).reshape(1, 1)
    count = all_summed(all_summed(count, "wa"), "ctx")

    slots = jnp.arange(2 * ctx_count)
    inverse = jnp.sum(jnp.where(block_order[None, :] == slots[:, None], slots[None, :], 0), axis=1)
    inverse = inverse.astype(jnp.int32)
    distance = (seq_len - 1 - jnp.arange(seq_len)).astype(f32)
    waves = sinusoid(distance, width).astype(bf16)

    hidden_all = jnp.concatenate(token_parts, axis=0).astype(f32)
    scale_all = inverse_rms(hidden_all)
    normed_a = (hidden_all * scale_all * gain_one).astype(bf16)
    biases = jnp.stack([content_bias, position_bias]).astype(f32)
    mixed_cols = jnp.concatenate([query_cols, key_cols, value_cols], axis=1)
    qkv = dot_nn(normed_a, mixed_cols).reshape(places, tok_dev, 3 * cols)
    relative = dot_nn(waves, relative_cols).astype(bf16)
    general = SplitQueries(
        qkv[..., :cols],
        qkv[..., cols : 2 * cols].astype(bf16),
        qkv[..., 2 * cols :].astype(bf16),
        biases,
        relative,
        block_order,
        inverse,
        block,
    )
    attended = general.forward()

    def to_owner(product):
        return scatter_parts([product[r * tok_dev : (r + 1) * tok_dev] for r in range(places)])

    def from_all(value):
        return jnp.concatenate(gather_parts(value), axis=0)

    hidden_in = tokens[0].astype(f32)
    hidden_one = hidden_in + to_owner(dot_nn(attended, output_weight))

    scale_two = inverse_rms(hidden_one)
    normed_b = from_all((hidden_one * scale_two * gain_two).astype(bf16))
    cross_q = dot_nn(normed_b, cross_query_cols).astype(bf16)
    cross_pair = dot_nn(near_rows, cross_pair_cols).astype(bf16)
    crossed = cross_forward(cross_q, cross_pair)
    hidden_two = hidden_one + to_owner(dot_nn(crossed, cross_output_weight))

    scale_three = inverse_rms(hidden_two)
    normed_c = from_all((hidden_two * scale_three * gain_three).astype(bf16))
    pre_act = dot_nn(normed_c, up_cols)
    activated = gelu_tanh(pre_act).astype(bf16)
    layer_out = hidden_two + to_owner(dot_nn(activated, down_weight))

    error = layer_out - teacher[0].astype(f32)
    error_sum = jnp.sum(valid * error * error).reshape(1, 1)
    error_sum = all_summed(all_summed(error_sum, "wa"), "ctx")
    loss = (error_sum / (2.0 * count * width)).reshape(())
    out_grad = (places * seq_len) / count * valid * error

    out_low = from_all(out_grad.astype(bf16))
    act_grad = dot_nt(out_low, down_weight)
    _, gelu_pull = jax.vjp(gelu_tanh, pre_act)
    pre_grad = gelu_pull(act_grad)[0].astype(bf16)
    down_grad = dot_tn(activated, out_low).astype(bf16)
    up_grad = dot_tn(normed_c, pre_grad).astype(bf16)
    normed_c_grad = to_owner(dot_nt(pre_grad, up_cols))
    two_grad = out_grad + norm_pull(hidden_two, scale_three, gain_three, normed_c_grad)
    gain_three_grad = jnp.sum(normed_c_grad * hidden_two * scale_three, axis=0, keepdims=True)
    down_out = sum_row_grads(down_grad)
    up_out = sum_column_grads(up_grad[None])[0]

    two_low = from_all(two_grad.astype(bf16))
    crossed_grad = dot_nt(two_low, cross_output_weight).astype(bf16)
    cross_q_grad, cross_pair_grad = cross_backward(cross_q, cross_pair, crossed_grad)
    normed_b_grad = to_owner(dot_nt(cross_q_grad, cross_query_cols))
    one_grad = two_grad + norm_pull(hidden_one, scale_two, gain_two, normed_b_grad)
    gain_two_grad = jnp.sum(normed_b_grad * hidden_one * scale_two, axis=0, keepdims=True)
    cross_output_grad = dot_tn(crossed, two_low).astype(bf16)
    cross_query_grad = dot_tn(normed_b, cross_q_grad).astype(bf16)
    cross_key_grad = dot_tn(near_rows, cross_pair_grad[:, :cols]).astype(bf16)
    cross_value_grad = dot_tn(near_rows, cross_pair_grad[:, cols:]).astype(bf16)
    cross_output_out = sum_row_grads(cross_output_grad)
    cross_out = sum_column_grads(jnp.stack([cross_key_grad, cross_value_grad]))
    cross_query_out = sum_column_grads(cross_query_grad[None])[0]
    near_grad = dot_nt(cross_pair_grad, cross_pair_cols)
    near_count = near_rows.shape[0] // places
    near_grad = scatter_parts(
        [near_grad[r * near_count : (r + 1) * near_count] for r in range(places)]
    )
    neighbours_grad = near_grad.reshape(neighbours.shape)

    one_low = from_all(one_grad.astype(bf16))
    attended_grad = dot_nt(one_low, output_weight).astype(bf16)
    output_grad = dot_tn(attended, one_low).astype(bf16)
    output_out = sum_row_grads(output_grad)
    query_grad, key_grad, value_grad, bias_grads, table_grad = general.backward(attended_grad)
    qkv_grad = jnp.concatenate([query_grad, key_grad, value_grad], axis=1)
    table_high = table_grad.astype(bf16)
    table_low = (table_grad - table_high.astype(f32)).astype(bf16)
    relative_grad = (dot_tn(waves, table_high) + dot_tn(waves, table_low)).astype(bf16)
    mixed_grad = dot_tn(normed_a, qkv_grad).astype(bf16)
    whole = [mixed_grad[:, m * cols : (m + 1) * cols] for m in range(3)]
    attention_out = sum_column_grads(jnp.stack(whole + [relative_grad]))
    normed_a_part = dot_nt(qkv_grad, mixed_cols)
    gain_one_part = jnp.sum(normed_a_part * hidden_all * scale_all, axis=0, keepdims=True)
    normed_a_grad = to_owner(normed_a_part)
    tokens_grad = one_grad + norm_pull(hidden_in, scale_all[:tok_dev], gain_one, normed_a_grad)

    gain_grads = jnp.concatenate([gain_one_part, gain_two_grad, gain_three_grad], axis=0)
    gain_grads = all_summed(gain_grads, "wa")
    share = width // places
    gain_grads = lax.dynamic_slice_in_dim(gain_grads, place * share, share, 1)
    small = jnp.concatenate([gain_grads.reshape(1, -1), bias_grads.reshape(1, -1)], axis=1)
    small = all_summed(small, "ctx")[0]
    gain_out = small[: 3 * share].reshape(3, share)
    bias_out = small[3 * share :].reshape(2, cols)

    return (
        layer_out[None],
        loss,
        tokens_grad[None],
        neighbours_grad,
        attention_out[0],
        attention_out[1],
        attention_out[2],
        output_out,
        attention_out[3],
        bias_out[0],
        bias_out[1],
        cross_query_out,
        cross_out[0],
        cross_out[1],
        cross_output_out,
        up_out,
        down_out,
        gain_out[0],
        gain_out[1],
        gain_out[2],
    )


def local_by_heads(
    tokens,
    neighbours,
    teacher,
    valid_mask,
    block_order,
    query_weight,
    key_weight,
    value_weight,
    output_weight,
    relative_weight,
    content_bias,
    position_bias,
    cross_query_weight,
    cross_key_weight,
    cross_value_weight,
    cross_output_weight,
    up_weight,
    down_weight,
    attention_gain,
    cross_gain,
    feedforward_gain,
):
    places = 4
    ctx_count = 8
    place = lax.axis_index("wa")
    here = lax.axis_index("ctx")
    _, tok_dev, width = tokens.shape
    seq_len = tok_dev * ctx_count
    block = tok_dev // 2
    attn = HEADS * HEAD_DIM
    cols = attn // places
    rows = places * tok_dev
    share = width // places

    slots = jnp.arange(2 * ctx_count)
    inverse = jnp.sum(jnp.where(block_order[None, :] == slots[:, None], slots[None, :], 0), axis=1)
    inverse = inverse.astype(jnp.int32)
    valid = valid_mask.astype(f32).reshape(tok_dev, 1)

    pair_rows = jnp.concatenate(
        [
            lax.dynamic_slice_in_dim(weight, here * 128, 128, 1)
            for weight in (query_weight, key_weight, value_weight, relative_weight)
        ],
        axis=1,
    )
    gain_rows = jnp.stack([attention_gain, cross_gain, feedforward_gain]).astype(f32)
    bias_rows = jnp.stack([content_bias, position_bias]).astype(f32)
    gain_rows = jnp.concatenate(
        [jnp.pad(gain_rows, ((0, 0), (0, cols - share))), bias_rows, jnp.zeros((3, cols), f32)], axis=0
    )
    count_row = jnp.broadcast_to(jnp.sum(valid), (8, 128))
    tokens_all, count_all, (pair_cols, gains) = gather_all(
        tokens[0], count_row, (pair_rows, gain_rows), 1
    )
    count = count_all[0:1, 0:1]
    pair_cols = pair_cols.reshape(width, 512)
    bias_all = gains[:, 3:5].transpose(1, 0, 2).reshape(2, attn)
    gains = gains[:, :3, :share].transpose(1, 0, 2).reshape(3, width)
    gain_one, gain_two, gain_three = gains[0:1], gains[1:2], gains[2:3]
    gains_eight = jnp.pad(gains, ((0, 5), (0, 0)))

    cross_query_cols, cross_key_cols, cross_value_cols = [
        take_columns(weight) for weight in (cross_query_weight, cross_key_weight, cross_value_weight)
    ]
    cross_pair_cols = jnp.concatenate([cross_key_cols, cross_value_cols], axis=1)
    near_rows = jnp.concatenate(gather_parts(neighbours.reshape(-1, width)), axis=0)
    up_cols = take_columns(up_weight)
    qkv_rows = jnp.stack(
        [weight.reshape(share, ctx_count, 128) for weight in (query_weight, key_weight, value_weight)],
        axis=2,
    ).reshape(share, 3 * attn)
    qkv_full = lax.all_gather(qkv_rows, "wa", axis=0, tiled=True)

    distance = (seq_len - 1 - jnp.arange(seq_len)).astype(f32)
    waves = sinusoid(distance, width).astype(bf16)

    hidden_all = tokens_all.reshape(seq_len, width).astype(f32)
    normed_a = (hidden_all * inverse_rms(hidden_all) * gain_one).astype(bf16)
    qkv = dot_nn(normed_a, pair_cols[:, :384]).astype(bf16)
    table = dot_nn(waves, pair_cols[:, 384:]).astype(bf16)
    table = jnp.concatenate([table, jnp.zeros((TILE, 128), bf16)], axis=0)
    my_biases = lax.dynamic_slice_in_dim(bias_all, here * 128, 128, 1)
    my_biases = jnp.concatenate([my_biases, jnp.zeros((6, 128), f32)], axis=0)
    out = attend_forward(inverse, qkv, table, my_biases, block)
    attended = swap_heads(out.reshape(ctx_count, tok_dev, 128), True, 2).reshape(rows, cols)

    def to_owner(product):
        return scatter_parts([product[r * tok_dev : (r + 1) * tok_dev] for r in range(places)])

    def from_all(value):
        return jnp.concatenate(gather_parts(value), axis=0)

    hidden_in = tokens[0].astype(f32)
    hidden_one = hidden_in + to_owner(dot_nn(attended, output_weight))

    scale_two = inverse_rms(hidden_one)
    normed_b = from_all((hidden_one * scale_two * gain_two).astype(bf16))
    cross_q = dot_nn(normed_b, cross_query_cols).astype(bf16)
    cross_pair = dot_nn(near_rows, cross_pair_cols).astype(bf16)
    crossed = cross_forward(cross_q, cross_pair)
    hidden_two = hidden_one + to_owner(dot_nn(crossed, cross_output_weight))

    scale_three = inverse_rms(hidden_two)
    normed_c = from_all((hidden_two * scale_three * gain_three).astype(bf16))
    pre_act = dot_nn(normed_c, up_cols)
    activated = gelu_tanh(pre_act).astype(bf16)
    layer_out = hidden_two + to_owner(dot_nn(activated, down_weight))

    error = layer_out - teacher[0].astype(f32)
    error_sum = jnp.sum(valid * error * error)
    out_grad = (places * seq_len) / count * valid * error

    one_grad, gain_part, heads_grad, cross_pair_grad, down_share, up_share, cross_x, cross_o_x, output_x = (
        middle_back(
            out_grad,
            down_weight,
            pre_act,
            activated,
            normed_c,
            hidden_two,
            hidden_one,
            gains_eight,
            (
                up_cols,
                cross_output_weight,
                crossed,
                cross_q,
                cross_pair,
                cross_query_cols,
                near_rows,
                normed_b,
                output_weight,
                attended,
            ),
            3,
        )
    )
    qkv_grad, table_grad, bias_part = attend_backward(
        inverse, qkv, table, my_biases, heads_grad.reshape(seq_len, 128), block
    )

    pair_slots = jnp.arange(ctx_count)[:, None, None]
    bias_slots = jnp.where(pair_slots == here, bias_part[None, 0:2], 0.0)
    small = jnp.concatenate(
        [
            jnp.pad(gain_part[2:3], ((0, 0), (0, attn - width))),
            jnp.pad(gain_part[0:2], ((0, 0), (0, attn - width))),
            bias_slots.reshape(2, attn),
            jnp.broadcast_to(error_sum, (3, attn)),
        ],
        axis=0,
    )
    (
        tokens_grad,
        near_grad,
        small,
        down_out,
        up_out,
        cross_out,
        cross_output_out,
        output_out,
        pair_all,
    ) = finish(
        qkv_grad.reshape(ctx_count, tok_dev, 384),
        normed_a,
        waves,
        table_grad,
        small,
        cross_pair_grad,
        cross_pair_cols,
        down_share,
        up_share,
        cross_x,
        cross_o_x,
        output_x,
        one_grad,
        tokens[0],
        gains_eight,
        qkv_full,
        4,
    )
    neighbours_grad = near_grad.reshape(neighbours.shape)
    gain_out = lax.dynamic_slice_in_dim(small[0:3], place * share, share, 1)
    bias_out = lax.dynamic_slice_in_dim(
        small[3:5].reshape(ctx_count, 2, 128), place * 2, 2, 0
    )
    bias_out = bias_out.transpose(1, 0, 2).reshape(2, cols)
    loss = small[5, 0] / (2.0 * count[0, 0] * width)
    pair_all = pair_all.reshape(ctx_count, share, 512)
    whole = [
        pair_all[:, :, 128 * m : 128 * (m + 1)].transpose(1, 0, 2).reshape(share, attn).astype(f32)
        for m in range(4)
    ]
    down_out = down_out.reshape(down_weight.shape).astype(f32)
    cross_output_out = cross_output_out.reshape(cols, width).astype(f32)
    output_out = output_out.reshape(cols, width).astype(f32)
    used = share // ctx_count
    up_out = up_out.reshape(ctx_count, -1, up_out.shape[-1])[:, :used].reshape(share, -1).astype(f32)
    cross_out = cross_out.reshape(ctx_count, -1, places, 3 * cols)[:, :used]
    cross_query_out, *cross_out = [
        cross_out[..., m * cols : (m + 1) * cols].reshape(share, attn).astype(f32) for m in range(3)
    ]

    return (
        layer_out[None],
        loss,
        tokens_grad[None],
        neighbours_grad,
        whole[0],
        whole[1],
        whole[2],
        output_out,
        whole[3],
        bias_out[0],
        bias_out[1],
        cross_query_out,
        cross_out[0],
        cross_out[1],
        cross_output_out,
        up_out,
        down_out,
        gain_out[0],
        gain_out[1],
        gain_out[2],
    )


def solution(mesh):
    row = P("wa", None)
    flat = P("wa")
    in_specs = (
        P("wa", "ctx", None),
        P("wa", "ctx", None, None),
        P("wa", "ctx", None),
        P("wa", "ctx"),
        P(),
        row,
        row,
        row,
        row,
        row,
        flat,
        flat,
        row,
        row,
        row,
        row,
        row,
        row,
        flat,
        flat,
        flat,
    )
    out_specs = (
        P("wa", "ctx", None),
        P(),
        P("wa", "ctx", None),
        P("wa", "ctx", None, None),
        row,
        row,
        row,
        row,
        row,
        flat,
        flat,
        row,
        row,
        row,
        row,
        row,
        row,
        flat,
        flat,
        flat,
    )
    by_heads = mesh.shape["ctx"] == 8 and mesh.shape["wa"] == 4
    local = local_by_heads if by_heads else local_general
    return jax.shard_map(local, mesh=mesh, in_specs=in_specs, out_specs=out_specs, check_vma=False)
```

```python
import functools
import types

import jax
import jax.numpy as jnp
from jax import lax
from jax.experimental import pallas as pl
from jax.experimental.pallas import tpu as pltpu
from jax.sharding import PartitionSpec as P

HEADS = 16
HEAD_DIM = 64
GROUP = 64
NK = 256
TILE = 128

eps_norm = 1e-06
neg_big = -1e30
highest = lax.Precision.HIGHEST
f32 = jnp.float32
bf16 = jnp.bfloat16


def inverse_rms(hidden):
    return lax.rsqrt(jnp.mean(hidden * hidden, axis=-1, keepdims=True) + eps_norm)


def norm_pull(hidden, scale, gain, grad):
    scaled = grad * gain
    mean = jnp.mean(hidden * scaled, axis=-1, keepdims=True)
    return scale * scaled - hidden * (scale * scale * scale) * mean


def gelu_tanh(value):
    return jax.nn.gelu(value, approximate=True)


def sinusoid(distance, width):
    half = width // 2
    freq = jnp.exp(-jnp.log(10000.0) * jnp.arange(half, dtype=f32) * 2.0 / width)
    angle = distance[:, None] * freq[None, :]
    return jnp.concatenate([jnp.sin(angle), jnp.cos(angle)], axis=1)


def dot_nn(a, b):
    return lax.dot_general(a, b, (((1,), (0,)), ((), ())), preferred_element_type=f32)


def dot_nt(a, b):
    return lax.dot_general(a, b, (((1,), (1,)), ((), ())), preferred_element_type=f32)


def dot_tn(a, b):
    return lax.dot_general(a, b, (((0,), (0,)), ((), ())), preferred_element_type=f32)


def swap(value, axis, bit):
    pairs = [(i, i ^ bit) for i in range(lax.axis_size(axis))]
    return lax.ppermute(value, axis, pairs)


def bits_of(axis):
    bits, bit = [], 1
    while bit < lax.axis_size(axis):
        bits.append(bit)
        bit *= 2
    return bits


def my_bit(axis, bit):
    return (lax.axis_index(axis) // bit) % 2


def ordered(bit, own, other, dim):
    return jnp.where(
        bit == 0,
        jnp.concatenate([own, other], axis=dim),
        jnp.concatenate([other, own], axis=dim),
    )


def split(value, bit, dim):
    half = value.shape[dim] // 2
    keep = lax.dynamic_slice_in_dim(value, bit * half, half, dim)
    send = lax.dynamic_slice_in_dim(value, (1 - bit) * half, half, dim)
    return keep, send


def gather_parts(value):
    parts = {0: value}
    for bit in reversed(bits_of("wa")):
        parts.update({r | bit: swap(part, "wa", bit) for r, part in list(parts.items())})
    return [parts[r] for r in sorted(parts)]


def scatter_parts(parts):
    parts = dict(enumerate(parts))
    for bit in bits_of("wa"):
        kept = {}
        for r, part in parts.items():
            if not r & bit:
                got = swap(parts[r | bit].astype(bf16), "wa", bit)
                kept[r] = part + got.astype(f32)
        parts = kept
    return parts[0]


def take_columns(weight):
    value = weight[None]
    for bit in reversed(bits_of("wa")):
        mine = my_bit("wa", bit)
        keep, send = split(value, mine, 2)
        value = ordered(mine, keep[:, None], swap(send, "wa", bit)[:, None], 1)
        value = value.reshape((-1,) + value.shape[2:])
    return value.reshape(-1, value.shape[-1])


def spread_columns(value):
    for bit in bits_of("wa"):
        mine = my_bit("wa", bit)
        paired = value.reshape((value.shape[0], value.shape[1] // 2, 2) + value.shape[2:])
        keep, send = split(paired, mine, 2)
        value = ordered(mine, keep[:, :, 0], swap(send[:, :, 0], "wa", bit), 3)
    return value[:, 0]


def halving_dim(shape):
    if shape[-2] % 16 == 0:
        return len(shape) - 2
    if shape[0] % 2 == 0:
        return 0
    if shape[-2] % 2 == 0:
        return len(shape) - 2
    return len(shape) - 1


def sum_over_ctx(value, bits, finish):
    dims = []
    for bit in bits:
        dim = halving_dim(value.shape)
        keep, send = split(value, my_bit("ctx", bit), dim)
        value = (keep.astype(f32) + swap(send, "ctx", bit).astype(f32)).astype(bf16)
        dims.append(dim - value.ndim if dim else 0)
    value = finish(value)
    for bit, dim in reversed(list(zip(bits, dims))):
        dim = dim % value.ndim
        value = ordered(my_bit("ctx", bit), value, swap(value, "ctx", bit), dim)
    return value


def all_summed(value, axis):
    for bit in bits_of(axis):
        value = value + swap(value, axis, bit)
    return value


def sum_column_grads(grads):
    places = lax.axis_size("wa")
    grads = grads.reshape(grads.shape[0], places, grads.shape[1] // places, grads.shape[2])
    bits = bits_of("ctx")
    if grads.shape[2] % lax.axis_size("ctx") == 0:
        return sum_over_ctx(grads, bits, spread_columns).astype(f32)
    return sum_over_ctx(spread_columns(grads), bits, lambda value: value).astype(f32)


def sum_row_grads(grads):
    return sum_over_ctx(grads[None], bits_of("ctx"), lambda value: value)[0].astype(f32)


def first_half(shape):
    return lax.broadcasted_iota(jnp.int32, shape, 1) < HEAD_DIM


def stack_heads(rows):
    mask = first_half(rows.shape)
    zero = jnp.zeros_like(rows)
    return jnp.concatenate([jnp.where(mask, rows, zero), jnp.where(mask, zero, rows)], axis=0)


def join_heads(stacked):
    rows = stacked.shape[0] // 2
    return jnp.where(first_half((rows, stacked.shape[1])), stacked[:rows], stacked[rows:])


def copy_blocks(order_ref, source, target, block, inward):
    for place in range(source.shape[0] // block):
        start = pl.multiple_of(order_ref[place] * block, block)
        if inward:
            target[place * block : (place + 1) * block, :] = source[pl.ds(start, block), :]
        else:
            target[pl.ds(start, block), :] = source[place * block : (place + 1) * block, :]


def attention_shares(content, position, key_ref, rel_ref, row_start, seq_len):
    length = row_start + TILE
    wide_len = length + TILE
    offset = seq_len - TILE - row_start
    scale = HEAD_DIM ** (-0.5)
    scores = dot_nt(content, key_ref[0:length, :])
    wide = dot_nt(position, rel_ref[offset : offset + wide_len, :])
    halves = []
    for head in range(2):
        part = wide[head * TILE : (head + 1) * TILE]
        turned = pltpu.roll(part, wide_len - (TILE - 1), 1, stride=1, stride_axis=0)
        halves.append(turned[:, :length])
    scores = (scores + jnp.concatenate(halves, axis=0)) * scale
    row = lax.broadcasted_iota(jnp.int32, scores.shape, 0) % TILE + row_start
    col = lax.broadcasted_iota(jnp.int32, scores.shape, 1)
    scores = jnp.where(col <= row, scores, neg_big)
    top = jnp.max(scores, axis=1, keepdims=True)
    raised = jnp.exp(scores - top)
    total = jnp.sum(raised, axis=1, keepdims=True)
    return raised * (1.0 / total)


def attend_tiles(qkv, rel_ref, content_bias, position_bias, out):
    seq_len = qkv.shape[0]
    keys = qkv.at[:, 128:256]
    values = qkv.at[:, 256:384]
    for tile in range(seq_len // TILE):
        start = tile * TILE
        query = qkv[start : start + TILE, 0:128].astype(f32)
        content = stack_heads((query + content_bias).astype(bf16))
        position = stack_heads((query + position_bias).astype(bf16))
        shares = attention_shares(content, position, keys, rel_ref, start, seq_len)
        got = dot_nn(shares.astype(bf16), values[0 : start + TILE, :])
        out[start : start + TILE, :] = join_heads(got).astype(bf16)


def attend_backward_kernel(
    seq_len,
    block,
    order_ref,
    qkv_ref,
    rel_ref,
    bias_ref,
    grad_ref,
    dqkv_ref,
    drel_ref,
    dbias_ref,
    qkv,
    grad,
    dqkv,
    dkey,
    dvalue,
    drel,
):
    scale = HEAD_DIM ** (-0.5)
    copy_blocks(order_ref, qkv_ref, qkv, block, True)
    copy_blocks(order_ref, grad_ref, grad, block, True)
    keys = qkv.at[:, 128:256]
    values = qkv.at[:, 256:384]
    content_bias = bias_ref[3:4, :]
    position_bias = bias_ref[4:5, :]
    dkey[...] = jnp.zeros_like(dkey)
    dvalue[...] = jnp.zeros_like(dvalue)
    drel[...] = jnp.zeros_like(drel)
    row = lax.broadcasted_iota(jnp.int32, (TILE, TILE), 0)
    col = lax.broadcasted_iota(jnp.int32, (TILE, TILE), 1)
    flip = jnp.where(row + col == TILE - 1, 1.0, 0.0).astype(bf16)
    content_sum = jnp.zeros((1, 128), f32)
    position_sum = jnp.zeros((1, 128), f32)
    for tile in range(seq_len // TILE):
        start = tile * TILE
        length = start + TILE
        wide_len = length + TILE
        offset = seq_len - TILE - start
        query = qkv[start : start + TILE, 0:128].astype(f32)
        content = stack_heads((query + content_bias).astype(bf16))
        plain = (query + position_bias).astype(bf16)
        position = stack_heads(plain)
        shares = attention_shares(content, position, keys, rel_ref, start, seq_len)
        out_grad = stack_heads(grad[start : start + TILE, :])
        share_grad = dot_nt(out_grad, values[0:length, :])
        delta = jnp.sum(shares * share_grad, axis=1, keepdims=True)
        score_grad = (shares * (share_grad - delta)).astype(bf16)
        content_grad = join_heads(dot_nn(score_grad, keys[0:length, :])) * scale
        parts = []
        for head in range(2):
            turned = dot_nn(flip, score_grad[head * TILE : (head + 1) * TILE])
            turned = jnp.concatenate([turned, jnp.zeros((TILE, TILE), f32)], axis=1)
            parts.append(pltpu.roll(turned, 0, 1, stride=1, stride_axis=0))
        wide_grad = jnp.concatenate(parts, axis=0).astype(bf16)
        relative = rel_ref[offset : offset + wide_len, :]
        turned_grad = join_heads(dot_nn(wide_grad, relative)) * scale
        turned_rows = stack_heads(dot_nn(flip, plain).astype(bf16))
        drel[offset : offset + wide_len, :] += dot_tn(wide_grad, turned_rows)
        high = turned_grad.astype(bf16)
        low = (turned_grad - high.astype(f32)).astype(bf16)
        position_grad = dot_nn(flip, high) + dot_nn(flip, low)
        content_sum += jnp.sum(content_grad, axis=0, keepdims=True)
        position_sum += jnp.sum(turned_grad, axis=0, keepdims=True)
        dqkv[start : start + TILE, 0:128] = (content_grad + position_grad).astype(bf16)
        dkey[0:length, :] += dot_tn(score_grad, content)
        dvalue[0:length, :] += dot_tn(shares.astype(bf16), out_grad)
    dqkv[:, 128:256] = (dkey[...] * scale).astype(bf16)
    dqkv[:, 256:384] = dvalue[...].astype(bf16)
    copy_blocks(order_ref, dqkv, dqkv_ref, block, False)
    drel_ref[...] = drel[0:seq_len, :] * scale
    dbias_ref[...] = jnp.concatenate(
        [content_sum, position_sum, jnp.zeros((6, 128), f32)], axis=0
    )


in_vmem = pl.BlockSpec(memory_space=pltpu.VMEM)
in_smem = pl.BlockSpec(memory_space=pltpu.SMEM)


def attend_backward(order, qkv, rel, bias, grad, block):
    rows = qkv.shape[0]
    return pl.pallas_call(
        functools.partial(attend_backward_kernel, rows, block),
        out_shape=[
            jax.ShapeDtypeStruct((rows, 384), bf16),
            jax.ShapeDtypeStruct((rows, 128), f32),
            jax.ShapeDtypeStruct((8, 128), f32),
        ],
        in_specs=[in_smem, in_vmem, in_vmem, in_vmem, in_vmem],
        out_specs=[in_vmem, in_vmem, in_vmem],
        scratch_shapes=[
            pltpu.VMEM((rows, 384), bf16),
            pltpu.VMEM((rows, 128), bf16),
            pltpu.VMEM((rows, 384), bf16),
            pltpu.VMEM((rows, 128), f32),
            pltpu.VMEM((rows, 128), f32),
            pltpu.VMEM((rows + TILE, 128), f32),
        ],
        compiler_params=pltpu.CompilerParams(vmem_limit_bytes=40 * 2**20),
        cost_estimate=pl.CostEstimate(
            flops=10 * 256 * rows * rows * 2, bytes_accessed=rows * 3000, transcendentals=rows * rows
        ),
        name="attend_backward",
    )(order, qkv, rel, bias, grad)


def head_mask(shape, head):
    lane = lax.broadcasted_iota(jnp.int32, shape, 1)
    return (lane >= head * HEAD_DIM) & (lane < (head + 1) * HEAD_DIM)


def stack_all(rows):
    zero = jnp.zeros_like(rows)
    heads = rows.shape[1] // HEAD_DIM
    return jnp.concatenate(
        [jnp.where(head_mask(rows.shape, head), rows, zero) for head in range(heads)], axis=0
    )


def join_all(stacked):
    heads = stacked.shape[1] // HEAD_DIM
    rows = stacked.shape[0] // heads
    out = jnp.zeros((rows, stacked.shape[1]), stacked.dtype)
    for head in range(heads):
        part = stacked[head * rows : (head + 1) * rows]
        out = jnp.where(head_mask(part.shape, head), part, out)
    return out


def cross_shares(query, keys):
    scores = dot_nt(query, keys) * (HEAD_DIM ** (-0.5))
    raised = jnp.exp(scores - jnp.max(scores, axis=1, keepdims=True))
    return raised / jnp.sum(raised, axis=1, keepdims=True)


def cross_forward_kernel(q_ref, kv_ref, out_ref):
    width = q_ref.shape[1]
    shares = cross_shares(stack_all(q_ref[...]), kv_ref[:, 0:width])
    out_ref[...] = join_all(dot_nn(shares.astype(bf16), kv_ref[:, width:])).astype(bf16)


def cross_backward_kernel(q_ref, kv_ref, grad_ref, dq_ref, dkv_ref):
    width = q_ref.shape[1]
    scale = HEAD_DIM ** (-0.5)
    keys = kv_ref[:, 0:width]
    query = stack_all(q_ref[...])
    grad = stack_all(grad_ref[...])
    shares = cross_shares(query, keys)
    share_grad = dot_nt(grad, kv_ref[:, width:])
    delta = jnp.sum(shares * share_grad, axis=1, keepdims=True)
    score_grad = (shares * (share_grad - delta)).astype(bf16)
    dq_ref[...] = (join_all(dot_nn(score_grad, keys)) * scale).astype(bf16)
    dkv_ref[:, 0:width] = (dot_tn(score_grad, query) * scale).astype(bf16)
    dkv_ref[:, width:] = dot_tn(shares.astype(bf16), grad).astype(bf16)


def cross_forward(query, pair):
    width = query.shape[1]
    groups = query.shape[0] // GROUP
    return pl.pallas_call(
        cross_forward_kernel,
        out_shape=jax.ShapeDtypeStruct(query.shape, bf16),
        grid=(groups,),
        in_specs=[
            pl.BlockSpec((GROUP, width), lambda g: (g, 0)),
            pl.BlockSpec((NK, 2 * width), lambda g: (g, 0)),
        ],
        out_specs=pl.BlockSpec((GROUP, width), lambda g: (g, 0)),
        cost_estimate=pl.CostEstimate(
            flops=groups * 4 * 256 * 256 * 256, bytes_accessed=groups * 330000, transcendentals=groups * 65536
        ),
        name="cross_forward",
    )(query, pair)


def cross_backward(query, pair, grad):
    width = query.shape[1]
    groups = query.shape[0] // GROUP
    return pl.pallas_call(
        cross_backward_kernel,
        out_shape=[
            jax.ShapeDtypeStruct(query.shape, bf16),
            jax.ShapeDtypeStruct(pair.shape, bf16),
        ],
        grid=(groups,),
        in_specs=[
            pl.BlockSpec((GROUP, width), lambda g: (g, 0)),
            pl.BlockSpec((NK, 2 * width), lambda g: (g, 0)),
            pl.BlockSpec((GROUP, width), lambda g: (g, 0)),
        ],
        out_specs=[
            pl.BlockSpec((GROUP, width), lambda g: (g, 0)),
            pl.BlockSpec((NK, 2 * width), lambda g: (g, 0)),
        ],
        cost_estimate=pl.CostEstimate(
            flops=groups * 10 * 256 * 256 * 256, bytes_accessed=groups * 660000, transcendentals=groups * 65536
        ),
        name="cross_backward",
    )(query, pair, grad)


mesh_id = pl.DeviceIdType.MESH


def signal_to(barrier, ctx, wa):
    pl.semaphore_signal(barrier, inc=1, device_id=(ctx, wa), device_id_type=mesh_id)


def tree_sum(values):
    while len(values) > 1:
        values = [a + b for a, b in zip(values[::2], values[1::2])]
    return values[0]


def gelu_slope(value):
    inner = 0.7978845608028654 * (value + 0.044715 * value * value * value)
    turned = jnp.tanh(inner)
    slope = 0.7978845608028654 * (1.0 + 3.0 * 0.044715 * value * value)
    return 0.5 * (1.0 + turned) + 0.5 * value * (1.0 - turned * turned) * slope


def places_here():
    return lax.axis_index("ctx"), lax.axis_index("wa")


def meet_all():
    c, w = places_here()
    owner = c // 2
    own = owner == w
    barrier = pltpu.get_barrier_semaphore()
    for j in range(1, 8):
        signal_to(barrier, c ^ j, w)
    for j in range(1, 4):
        signal_to(barrier, c, w ^ j)
    for j in range(1, 8):
        signal_to(barrier, c ^ j, owner)
    for r in range(4):
        for h in range(2):

            @pl.when(jnp.logical_not(jnp.logical_and(2 * w + h == c, r == 0)))
            def _(r=r, h=h):
                signal_to(barrier, 2 * w + h, w ^ r)

    @pl.when(jnp.logical_not(own))
    def _():
        signal_to(barrier, c, owner)

    pl.semaphore_wait(barrier, 26 - 2 * own.astype(jnp.int32))


def meet_lines():
    c, w = places_here()
    barrier = pltpu.get_barrier_semaphore()
    for j in range(1, 8):
        signal_to(barrier, c ^ j, w)
    for j in range(1, 4):
        signal_to(barrier, c, w ^ j)
    pl.semaphore_wait(barrier, 10)


def remote(source, target, send, recv, ctx, wa):
    return pltpu.make_async_remote_copy(
        src_ref=source,
        dst_ref=target,
        send_sem=send,
        recv_sem=recv,
        device_id=(ctx, wa),
        device_id_type=mesh_id,
    )


class GatherRows:

    def __init__(self, buf, send, recv):
        self.buf, self.send, self.recv = buf, send, recv
        self.c, self.w = places_here()

    def copy(self, k):
        source, entry, j = ((0, 1, 1), (0, 2, 2), (2, 3, 1))[k]
        return remote(
            self.buf.at[source],
            self.buf.at[entry],
            self.send.at[k],
            self.recv.at[k],
            self.c,
            self.w ^ j,
        )

    def start(self):
        self.copy(1).start()
        self.copy(0).start()

    def near(self):
        self.copy(0).wait()

    def relay(self):
        self.copy(1).wait()
        self.copy(2).start()

    def far(self):
        self.copy(2).wait()


class SumRows:

    def __init__(self, out_buf, in_buf, send, recv):
        self.out, self.inn, self.send, self.recv = out_buf, in_buf, send, recv
        self.c, self.w = places_here()

    def copy(self, k):
        j = (1, 1, 2)[k]
        return remote(
            self.out.at[k], self.inn.at[k], self.send.at[k], self.recv.at[k], self.c, self.w ^ j
        )

    def give_near(self, value):
        self.out[0] = value.astype(bf16)
        self.copy(0).start()

    def give_far(self, value):
        self.out[1] = value.astype(bf16)
        self.copy(1).start()

    def pass_on(self, value):
        self.copy(1).wait()
        self.out[2] = (value + self.inn[1].astype(f32)).astype(bf16)
        self.copy(2).start()

    def total(self, value):
        self.copy(0).wait()
        value = value + self.inn[0].astype(f32)
        self.copy(2).wait()
        return value + self.inn[2].astype(f32)


class CtxSum:

    def __init__(self, send, recv, x=None, half=None, part=None, share=None, out=None, spread=0):
        self.send, self.recv = send, recv
        self.x, self.half, self.part, self.share, self.out = x, half, part, share, out
        self.spread = spread
        self.c, self.w = places_here()
        self.z, self.y = self.c // 2, self.c % 2

    def y_copy(self):
        return remote(
            self.x.at[:, 1 - self.y], self.half, self.send.at[0], self.recv.at[0], self.c ^ 1, self.w
        )

    def start_y(self):
        self.y_copy().start()

    def finish_y(self):
        self.y_copy().wait()
        for z in range(4):
            mine = self.x[z, self.y].astype(f32)
            self.half[z] = (self.half[z].astype(f32) + mine).astype(bf16)

    def z_copy(self, j):
        return remote(
            self.half.at[self.z ^ j],
            self.part.at[j - 1],
            self.send.at[j],
            self.recv.at[j],
            self.c ^ (2 * j),
            self.w,
        )

    def start_z(self):
        for j in (2, 3, 1):
            self.z_copy(j).start()

    def finish_z(self):
        total = self.half[self.z].astype(f32)
        for j in (1, 2, 3):
            self.z_copy(j).wait()
            total = total + self.part[j - 1].astype(f32)
        self.share[...] = total.astype(bf16)

    def columns(self, place):
        width = self.spread
        return self.out.at[self.z, self.y, :, pl.ds(pl.multiple_of(place * width, 128), width)]

    def wa_copy(self, j, place):
        return remote(
            self.share.at[self.w ^ j],
            self.columns(place),
            self.send.at[3 + j],
            self.recv.at[3 + j],
            self.c,
            self.w ^ j,
        )

    def own_copy(self):
        source = self.share.at[self.w] if self.spread else self.share
        target = self.columns(self.w) if self.spread else self.out.at[self.z, self.y]
        return pltpu.make_async_copy(source, target, self.send.at[11])

    def start_wa(self):
        if self.spread:
            for j in (2, 3, 1):
                self.wa_copy(j, self.w).start()
        self.own_copy().start()

    def finish_wa(self):
        self.own_copy().wait()
        if self.spread:
            for j in (1, 2, 3):
                self.wa_copy(j, self.w).wait_send()
                self.wa_copy(j, self.w ^ j).wait_recv()

    def back_z_copy(self, j, z):
        mine = self.out.at[z, self.y]
        return remote(mine, mine, self.send.at[6 + j], self.recv.at[6 + j], self.c ^ (2 * j), self.w)

    def start_back_z(self):
        for j in (2, 3, 1):
            self.back_z_copy(j, self.z).start()

    def finish_back_z(self):
        for j in (1, 2, 3):
            self.back_z_copy(j, self.z).wait_send()
            self.back_z_copy(j, self.z ^ j).wait_recv()

    def back_y_copy(self, y):
        part = self.out.at[:, y]
        return remote(part, part, self.send.at[10], self.recv.at[10], self.c ^ 1, self.w)

    def start_back_y(self):
        self.back_y_copy(self.y).start()

    def finish_back_y(self):
        self.back_y_copy(self.y).wait_send()
        self.back_y_copy(1 - self.y).wait_recv()


def put_shares(target, grads, first=0):
    count = grads.shape[0] // 32
    padded = target.shape[3]
    for place in range(4):
        for share in range(8):
            start = (place * 8 + share) * count
            part = grads[start : start + count]
            part = jnp.concatenate([part, jnp.zeros((padded - count, part.shape[1]), f32)], axis=0)
            target[share // 2, share % 2, place, :, first : first + part.shape[1]] = part.astype(bf16)


def put_rows(target, grads):
    count = grads.shape[0] // 8
    for share in range(8):
        target[share // 2, share % 2] = grads[share * count : (share + 1) * count].astype(bf16)


class Cut:

    def __init__(self, ref, start):
        self.ref, self.start = ref, start

    @property
    def at(self):
        return self

    def __getitem__(self, k):
        return self.ref.at[self.start + k]


class Pool:
    def __init__(self, ref):
        self.ref, self.used = ref, 0

    def take(self, count):
        cut = Cut(self.ref, self.used)
        self.used += count
        return cut


class LineGather:

    def __init__(self, out, send, recv):
        self.out, self.send, self.recv = out, send, recv
        self.c, self.w = places_here()
        self.z = self.c // 2
        self.right, self.left = self.z < 3, self.z > 0

    def y_copy(self, block, slot):
        ref = self.out.at[block]
        return remote(ref, ref, self.send.at[slot], self.recv.at[slot], self.c ^ 1, self.w)

    def z_copy(self, block, slot, step):
        k = slot + (7 if step > 0 else 10)
        ref = self.out.at[block]
        return remote(ref, ref, self.send.at[k], self.recv.at[k], self.c + step, self.w)

    def start(self):
        @pl.when(self.right)
        def _():
            self.z_copy(self.c, 0, 2).start()

        @pl.when(self.left)
        def _():
            self.z_copy(self.c, 0, -2).start()

        self.y_copy(self.c, 0).start()

    def step(self, t):
        @pl.when(self.z > t)
        def _():
            block = self.c - 2 * (t + 1)
            self.z_copy(block, t, 2).wait_recv()
            if t < 2:

                @pl.when(self.right)
                def _():
                    self.z_copy(block, t + 1, 2).start()

            self.y_copy(block, t + 1).start()

        @pl.when(self.z < 3 - t)
        def _():
            block = self.c + 2 * (t + 1)
            self.z_copy(block, t, -2).wait_recv()
            if t < 2:

                @pl.when(self.left)
                def _():
                    self.z_copy(block, t + 1, -2).start()

            self.y_copy(block, t + 4).start()

    def finish(self):
        self.y_copy(self.c, 0).wait_send()
        self.y_copy(self.c ^ 1, 0).wait_recv()
        for t in range(3):
            for step, at, near in ((-2, t + 1, self.z > t), (2, t + 4, self.z < 3 - t)):

                @pl.when(near)
                def _(step=step, at=at):
                    self.y_copy(self.c + step * (t + 1), at).wait_send()
                    self.y_copy((self.c ^ 1) + step * (t + 1), at).wait_recv()

        @pl.when(self.right)
        def _():
            self.z_copy(self.c, 0, 2).wait_send()

        @pl.when(self.left)
        def _():
            self.z_copy(self.c, 0, -2).wait_send()

        for t in range(2):

            @pl.when(jnp.logical_and(self.z > t, self.right))
            def _():
                self.z_copy(self.c, t + 1, 2).wait_send()

            @pl.when(jnp.logical_and(self.z < 3 - t, self.left))
            def _():
                self.z_copy(self.c, t + 1, -2).wait_send()


class Columns:

    def __init__(self, source, target, width, first, send, recv, at=None):
        self.source, self.target, self.width, self.first = source, target, width, first
        self.send, self.recv, self.column = send, recv, at
        self.c, self.w = places_here()

    def taken(self, place):
        start = place * self.width if self.column is None else self.column
        return self.source.at[:, pl.ds(pl.multiple_of(start, 128), self.width)]

    def put(self, place):
        rows = self.source.shape[0]
        return self.target.at[
            pl.ds(pl.multiple_of(place * rows, 32), rows), self.first : self.first + self.width
        ]

    def copy(self, j, place):
        return remote(
            self.taken(self.w ^ j),
            self.put(place),
            self.send.at[j],
            self.recv.at[j],
            self.c,
            self.w ^ j,
        )

    def own(self):
        return pltpu.make_async_copy(self.taken(self.w), self.put(self.w), self.send.at[0])

    def start(self):
        for j in (2, 3, 1):
            self.copy(j, self.w).start()
        self.own().start()

    def finish(self):
        self.own().wait()
        for j in (1, 2, 3):
            self.copy(j, self.w).wait_send()
            self.copy(j, self.w ^ j).wait_recv()


class SmallSum:

    def __init__(self, ref, got, axis, send, recv):
        self.ref, self.got, self.axis, self.send, self.recv = ref, got, axis, send, recv
        self.c, self.w = places_here()

    def copy(self, k):
        j = k + 1
        ctx, wa = (self.c ^ j, self.w) if self.axis == "ctx" else (self.c, self.w ^ j)
        return remote(self.ref, self.got.at[k], self.send.at[k], self.recv.at[k], ctx, wa)

    def start(self):
        for k in range(self.got.shape[0]):
            self.copy(k).start()

    def finish(self):
        count = self.got.shape[0]
        for k in range(count):
            self.copy(k).wait()
        self.ref[...] = tree_sum([self.ref[...]] + [self.got[k] for k in range(count)])


class SwapHeads:

    def __init__(self, by_heads, by_rows, outward, send, recv):
        self.heads, self.rows, self.outward = by_heads, by_rows, outward
        self.send, self.recv = send, recv
        self.c, self.w = places_here()
        self.owner, self.half = self.c // 2, self.c % 2
        self.own = self.owner == self.w
        self.other = jnp.logical_not(self.own)

    def lanes(self):
        return pl.ds(pl.multiple_of(self.half * 128, 128), 128)

    def out_copy(self, j):
        slot = self.w ^ self.owner
        return remote(
            self.heads.at[self.c ^ j],
            self.rows.at[slot, :, self.lanes()],
            self.send.at[j],
            self.recv.at[slot * 2 + self.half],
            self.c ^ j,
            self.owner,
        )

    def start_out(self):
        for j in range(7, 0, -1):
            self.out_copy(j).start()

        @pl.when(self.other)
        def _():
            self.out_copy(0).start()

        @pl.when(self.own)
        def _():
            slot = self.w ^ self.owner
            pltpu.make_async_copy(
                self.heads.at[self.c],
                self.rows.at[slot, :, self.lanes()],
                self.recv.at[slot * 2 + self.half],
            ).start()

    def wait_rows(self, r):
        for h in range(2):
            remote(
                self.heads.at[0],
                self.rows.at[r, :, h * 128 : (h + 1) * 128],
                self.send.at[0],
                self.recv.at[r * 2 + h],
                self.c ^ 1,
                self.w,
            ).wait_recv()

    def finish_out(self):
        for j in range(1, 8):
            self.out_copy(j).wait_send()

        @pl.when(self.other)
        def _():
            self.out_copy(0).wait_send()

    def in_copy(self, r, h):
        return remote(
            self.rows.at[r, :, h * 128 : (h + 1) * 128],
            self.heads.at[self.c],
            self.send.at[r * 2 + h],
            self.recv.at[self.c],
            2 * self.w + h,
            self.w ^ r,
        )

    def mine(self, r, h):
        return jnp.logical_and(2 * self.w + h == self.c, r == 0)

    def start_in(self, r):
        for h in range(2):

            @pl.when(jnp.logical_not(self.mine(r, h)))
            def _():
                self.in_copy(r, h).start()

            @pl.when(self.mine(r, h))
            def _():
                pltpu.make_async_copy(
                    self.rows.at[r, :, h * 128 : (h + 1) * 128],
                    self.heads.at[self.c],
                    self.recv.at[self.c],
                ).start()

    def finish_in(self):
        for block in range(8):
            remote(
                self.rows.at[0, :, 0:128],
                self.heads.at[block],
                self.send.at[0],
                self.recv.at[block],
                self.c ^ 1,
                self.w,
            ).wait_recv()
        for r in range(4):
            for h in range(2):

                @pl.when(jnp.logical_not(self.mine(r, h)))
                def _(r=r, h=h):
                    self.in_copy(r, h).wait_send()


def layer_kernel(names, total_tokens, *refs):
    v = types.SimpleNamespace(**dict(zip(names, refs, strict=True)))
    c, w = places_here()
    send, recv, local = Pool(v.send), Pool(v.recv), Pool(v.local)
    tok, width = v.tokens.shape
    seq_len = 8 * tok
    rows = 4 * tok
    cols = v.output_w.shape[0]
    hidden = v.down_w.shape[0]
    scale = HEAD_DIM ** (-0.5)

    def load(source, target):
        copy = pltpu.make_async_copy(source, target, local.take(1).at[0])
        copy.start()
        return copy

    near_load = load(v.neighbours, v.near.at[0])
    early = [load(v.waves_any, v.waves)]
    late = [
        load(v.output_any, v.output_w),
        load(v.cross_out_any, v.cross_out_w),
        load(v.down_any, v.down_w),
    ]
    v.small_all[...] = v.small[...]
    v.tokens_all[c] = v.tokens[...]
    meet_all()

    near_sum = SmallSum(v.small_all, v.small_near, "wa", send.take(3), recv.take(3))
    count_sum = SmallSum(v.count, v.count_far, "ctx", send.take(7), recv.take(7))
    gather = LineGather(v.tokens_all, send.take(13), recv.take(13))
    pair = [
        Columns(weight, v.pair, 128, 128 * m, send.take(4), recv.take(4), c * 128)
        for m, weight in enumerate((v.query_any, v.key_any, v.value_any, v.relative_any))
    ]
    cross = [
        Columns(weight, target, cols, first, send.take(4), recv.take(4))
        for weight, target, first in (
            (v.cross_key_any, v.pair_cols, 0),
            (v.cross_value_any, v.pair_cols, cols),
            (v.cross_query_any, v.query_cols, 0),
        )
    ]
    up_columns = Columns(v.up_any, v.up_cols, hidden, 0, send.take(4), recv.take(4))
    near_send, near_recv = send.take(3), recv.take(3)
    near_gather = GatherRows(v.near, near_send, near_recv)
    gather.start()
    near_sum.start()
    for part in pair:
        part.start()
    gather.step(0)
    near_sum.finish()
    v.count[...] = jnp.broadcast_to(v.small_all[5:6, 0:128], v.count.shape)
    count_sum.start()
    gather.step(1)
    for part in pair:
        part.finish()
    near_load.wait()
    near_gather.start()
    for part in cross:
        part.start()
    for copy in early:
        copy.wait()
    v.table[0:seq_len, :] = dot_nn(v.waves[...], v.pair[:, 384:512]).astype(bf16)
    v.table[seq_len:, :] = jnp.zeros((TILE, 128), bf16)
    v.biases[...] = v.small_all[:, pl.ds(pl.multiple_of(c * 128, 128), 128)]
    v.gains[...] = v.small_all[:, 0:width]
    gather.step(2)
    gather.finish()
    gain_one, gain_two, gain_three = (v.gains[k : k + 1, :] for k in range(3))

    def project(part, carry):
        start = pl.multiple_of(part * tok, tok)
        value = v.tokens_all[part].astype(f32)
        normed = (value * inverse_rms(value) * gain_one).astype(bf16)
        v.normed_a[pl.ds(start, tok), :] = normed
        v.qkv[pl.ds(start, tok), :] = dot_nn(normed, v.pair[:, 0:384]).astype(bf16)
        return carry

    lax.fori_loop(0, 8, project, 0)
    column = lax.broadcasted_iota(jnp.int32, (TILE, seq_len), 1)

    def move_rows(source, chosen, target):
        def some(part, carry):
            start = pl.multiple_of(part * TILE, TILE)
            pick = jnp.where(chosen[pl.ds(start, TILE), :] == column, 1.0, 0.0).astype(bf16)
            target[pl.ds(start, TILE), :] = dot_nn(pick, source[...]).astype(bf16)
            return carry

        lax.fori_loop(0, seq_len // TILE, some, 0)

    move_rows(v.qkv, v.inverse, v.qkv_order)
    near_gather.near()
    near_gather.relay()
    attend_tiles(v.qkv_order, v.table, v.biases[3:4, :], v.biases[4:5, :], v.heads_order)
    move_rows(v.heads_order, v.order, v.heads_stored)
    for part in range(8):
        v.heads[part] = v.heads_stored[part * tok : (part + 1) * tok, :]
    out_swap = SwapHeads(v.heads, v.attended, True, send.take(8), recv.take(8))
    out_swap.start_out()
    for copy in late:
        copy.wait()

    gathers = [GatherRows(ref, send.take(3), recv.take(3)) for ref in (v.rows_b, v.rows_c)]
    sums = [SumRows(v.give.at[k], v.take.at[k], send.take(3), recv.take(3)) for k in range(3)]

    def output_part(r):
        return dot_nn(v.attended[r], v.output_w[...])

    out_swap.wait_rows(3)
    sums[0].give_far(output_part(3))
    out_swap.wait_rows(1)
    sums[0].give_near(output_part(1))
    out_swap.wait_rows(2)
    sums[0].pass_on(output_part(2))
    out_swap.wait_rows(0)
    v.hidden_one[...] = v.tokens[...].astype(f32) + sums[0].total(output_part(0))
    value = v.hidden_one[...]
    v.rows_b[0] = (value * inverse_rms(value) * gain_two).astype(bf16)

    gathers[0].start()
    out_swap.finish_out()
    near_gather.far()
    for part in cross:
        part.finish()
    up_columns.start()
    near_count = v.near.shape[1]

    def near_project(r, carry):
        start = pl.multiple_of(r * near_count, near_count)
        v.cross_pair[pl.ds(start, near_count), :] = dot_nn(v.near[r], v.pair_cols[...]).astype(bf16)
        return carry

    lax.fori_loop(0, 4, near_project, 0)

    def cross_part(r):
        v.cross_q[r * tok : (r + 1) * tok, :] = dot_nn(v.rows_b[r], v.query_cols[...]).astype(bf16)

        def group(g, carry):
            at = pl.multiple_of(r * tok + g * GROUP, GROUP)
            near = pl.multiple_of((r * (tok // GROUP) + g) * NK, NK)
            query = stack_all(v.cross_q[pl.ds(at, GROUP), :])
            shares = cross_shares(query, v.cross_pair[pl.ds(near, NK), 0:cols])
            out = dot_nn(shares.astype(bf16), v.cross_pair[pl.ds(near, NK), cols:])
            v.crossed[pl.ds(at, GROUP), :] = join_all(out).astype(bf16)
            return carry

        lax.fori_loop(0, tok // GROUP, group, 0)
        return dot_nn(v.crossed[r * tok : (r + 1) * tok, :], v.cross_out_w[...])

    def in_turn(gathered, summed, part, between=None):
        v.keep[0] = part(0)
        gathered.near()
        summed.give_near(part(1))
        gathered.relay()
        v.keep[2] = part(2)
        gathered.far()
        summed.give_far(part(3))
        summed.pass_on(v.keep[2])
        if between is not None:
            between()
        return summed.total(v.keep[0])

    v.hidden_two[...] = v.hidden_one[...] + in_turn(gathers[0], sums[1], cross_part)
    value = v.hidden_two[...]
    v.rows_c[0] = (value * inverse_rms(value) * gain_three).astype(bf16)

    gathers[1].start()
    up_columns.finish()

    def feed_part(r):
        part = pl.ds(r * tok, tok)
        v.pre_act[part, :] = dot_nn(v.rows_c[r], v.up_cols[...])
        v.activated[part, :] = gelu_tanh(v.pre_act[part, :]).astype(bf16)
        return dot_nn(v.activated[part, :], v.down_w[...])

    layer_out = v.hidden_two[...] + in_turn(gathers[1], sums[2], feed_part)
    v.layer_out[...] = layer_out

    count_sum.finish()
    error = layer_out - v.teacher[...].astype(f32)
    valid = v.valid[...]
    weighted = valid * error
    v.error[...] = jnp.broadcast_to(jnp.sum(weighted * error, keepdims=True), v.error.shape)
    v.out_grad[...] = (total_tokens / v.count[0:1, 0:1]) * weighted

    middle_back(v, send, recv)


def middle_back(v, send, recv):
    c, w = places_here()
    tok, width = v.tokens.shape
    rows = 4 * tok
    cols = v.output_w.shape[0]
    scale = HEAD_DIM ** (-0.5)
    first, second, third = (
        GatherRows(ref, send.take(3), recv.take(3)) for ref in (v.rows_o, v.rows_two, v.rows_one)
    )
    sum_c, sum_b = (
        SumRows(v.give.at[k], v.take.at[k], send.take(3), recv.take(3)) for k in (3, 4)
    )
    down = CtxSum(send.take(12), recv.take(12), v.down_x, v.down_half, v.down_part, v.down_share)
    up = CtxSum(send.take(12), recv.take(12), v.up_x, v.up_half, v.up_part, v.up_share)
    cross = CtxSum(send.take(12), recv.take(12), v.cross_x, v.cross_half)
    heads = SwapHeads(v.heads_grad, v.heads_out, False, send.take(8), recv.take(8))
    v.rows_o[0] = v.out_grad[...].astype(bf16)

    first.start()

    def feed_back(r):
        part = pl.ds(r * tok, tok)
        act_grad = dot_nt(v.rows_o[r], v.down_w[...])
        v.pre_grad[part, :] = (act_grad * gelu_slope(v.pre_act[part, :])).astype(bf16)
        return dot_nt(v.pre_grad[part, :], v.up_cols[...])

    v.keep[0] = feed_back(0)
    first.near()
    sum_c.give_near(feed_back(1))
    first.relay()
    v.keep[1] = feed_back(2)
    first.far()
    sum_c.give_far(feed_back(3))
    sum_c.pass_on(v.keep[1])
    put_rows(v.down_x, dot_tn(v.activated[...], v.rows_o[...].reshape(rows, width)))
    down.start_y()
    put_shares(v.up_x, dot_tn(v.rows_c[...].reshape(rows, width), v.pre_grad[...]))
    normed_grad = sum_c.total(v.keep[0])
    value = v.hidden_two[...]
    inverse = inverse_rms(value)
    two_grad = v.out_grad[...] + norm_pull(value, inverse, v.gains[2:3, :], normed_grad)
    gain_three = jnp.sum(normed_grad * value * inverse, axis=0, keepdims=True)
    v.keep[1] = two_grad
    v.rows_two[0] = two_grad.astype(bf16)

    second.start()

    def cross_back(r):
        part = slice(r * tok, (r + 1) * tok)
        v.crossed_grad[...] = dot_nt(v.rows_two[r], v.cross_out_w[...]).astype(bf16)

        def group(g, carry):
            within = pl.multiple_of(g * GROUP, GROUP)
            at = pl.multiple_of(r * tok + g * GROUP, GROUP)
            near = pl.ds(pl.multiple_of((r * (tok // GROUP) + g) * NK, NK), NK)
            query = stack_all(v.cross_q[pl.ds(at, GROUP), :])
            grad = stack_all(v.crossed_grad[pl.ds(within, GROUP), :])
            keys = v.cross_pair[near, 0:cols]
            shares = cross_shares(query, keys)
            share_grad = dot_nt(grad, v.cross_pair[near, cols:])
            delta = jnp.sum(shares * share_grad, axis=1, keepdims=True)
            score_grad = (shares * (share_grad - delta)).astype(bf16)
            query_grad = join_all(dot_nn(score_grad, keys)) * scale
            v.query_grad[pl.ds(at, GROUP), :] = query_grad.astype(bf16)
            v.pair_grad[near, 0:cols] = (dot_tn(score_grad, query) * scale).astype(bf16)
            v.pair_grad[near, cols:] = dot_tn(shares.astype(bf16), grad).astype(bf16)
            return carry

        lax.fori_loop(0, tok // GROUP, group, 0)
        return dot_nt(v.query_grad[part, :], v.query_cols[...])

    v.keep[0] = cross_back(0)
    second.near()
    sum_b.give_near(cross_back(1))
    second.relay()
    v.keep[2] = cross_back(2)
    second.far()
    sum_b.give_far(cross_back(3))
    sum_b.pass_on(v.keep[2])
    down.finish_y()
    down.start_z()
    up.start_y()
    normed_b = v.rows_b[...].reshape(rows, width)
    put_rows(v.cross_out_x, dot_tn(v.crossed[...], v.rows_two[...].reshape(rows, width)))
    put_shares(v.cross_x, dot_tn(normed_b, v.query_grad[...]), 0)
    normed_grad = sum_b.total(v.keep[0])
    value = v.hidden_one[...]
    inverse = inverse_rms(value)
    one_grad = v.keep[1] + norm_pull(value, inverse, v.gains[1:2, :], normed_grad)
    gain_two = jnp.sum(normed_grad * value * inverse, axis=0, keepdims=True)
    v.gain_grad[...] = jnp.concatenate(
        [gain_two, gain_three, jnp.zeros((6, gain_two.shape[1]), f32)], axis=0
    )
    v.one_grad[...] = one_grad
    v.rows_one[0] = one_grad.astype(bf16)

    third.start()
    near = v.near[...].reshape(-1, width)
    put_shares(v.cross_x, dot_tn(near, v.pair_grad[...]), cols)

    def head_back(r):
        v.heads_out[r] = dot_nt(v.rows_one[r], v.output_w[...]).astype(bf16)
        heads.start_in(r)

    head_back(0)
    third.near()
    head_back(1)
    third.relay()
    head_back(2)
    third.far()
    head_back(3)
    up.finish_y()
    up.start_z()
    cross.start_y()
    attended = jnp.concatenate([v.attended[r] for r in range(4)], axis=0)
    put_rows(v.output_x, dot_tn(attended, v.rows_one[...].reshape(rows, width)))
    heads.finish_in()
    down.finish_z()
    up.finish_z()
    cross.finish_y()


def layer(total_tokens, given, collective_id):
    tok, width = given["tokens"].shape
    hidden = given["down_any"].shape[0]
    cols = given["output_any"].shape[0]
    near = given["neighbours"].shape[0]
    seq_len = 8 * tok
    rows = 4 * tok
    padded = -(-(width // 32) // 8) * 8
    any_space = pl.BlockSpec(memory_space=pl.ANY)
    shape = jax.ShapeDtypeStruct
    vmem = pltpu.VMEM
    dma = pltpu.SemaphoreType.DMA
    results = dict(
        layer_out=shape((tok, width), f32),
        error=shape((8, 128), f32),
        count=shape((8, 128), f32),
        qkv=shape((seq_len, 384), bf16),
        table=shape((seq_len + TILE, 128), bf16),
        biases=shape((8, 128), f32),
        gains=shape((8, width), f32),
        normed_a=shape((seq_len, width), bf16),
        pair_cols=shape((width, 2 * cols), bf16),
        one_grad=shape((tok, width), f32),
        gain_grad=shape((8, width), f32),
        heads_grad=shape((8, tok, 128), bf16),
        pair_grad=shape((4 * near, 2 * cols), bf16),
        down_share=shape((hidden // 8, width), bf16),
        up_share=shape((4, padded, hidden), bf16),
        cross_half=shape((4, 4, padded, 3 * cols), bf16),
        cross_out_x=shape((4, 2, cols // 8, width), bf16),
        output_x=shape((4, 2, cols // 8, width), bf16),
    )
    scratch = dict(
        small_all=vmem(given["small"].shape, f32),
        small_near=vmem((3,) + given["small"].shape, f32),
        count_far=vmem((7, 8, 128), f32),
        tokens_all=vmem((8, tok, width), bf16),
        pair=vmem((width, 512), bf16),
        waves=vmem((seq_len, width), bf16),
        qkv_order=vmem((seq_len, 384), bf16),
        heads_order=vmem((seq_len, 128), bf16),
        heads_stored=vmem((seq_len, 128), bf16),
        heads=vmem((8, tok, 128), bf16),
        attended=vmem((4, tok, cols), bf16),
        near=vmem((4, near, width), bf16),
        query_cols=vmem((width, cols), bf16),
        up_cols=vmem((width, hidden), bf16),
        output_w=vmem((cols, width), bf16),
        cross_out_w=vmem((cols, width), bf16),
        down_w=vmem((hidden, width), bf16),
        cross_pair=vmem((4 * near, 2 * cols), bf16),
        cross_q=vmem((rows, cols), bf16),
        crossed=vmem((rows, cols), bf16),
        crossed_grad=vmem((tok, cols), bf16),
        hidden_one=vmem((tok, width), f32),
        hidden_two=vmem((tok, width), f32),
        out_grad=vmem((tok, width), f32),
        pre_act=vmem((rows, hidden), f32),
        activated=vmem((rows, hidden), bf16),
        rows_b=vmem((4, tok, width), bf16),
        rows_c=vmem((4, tok, width), bf16),
        rows_o=vmem((4, tok, width), bf16),
        rows_two=vmem((4, tok, width), bf16),
        rows_one=vmem((4, tok, width), bf16),
        give=vmem((5, 3, tok, width), bf16),
        take=vmem((5, 3, tok, width), bf16),
        keep=vmem((3, tok, width), f32),
        pre_grad=vmem((rows, hidden), bf16),
        query_grad=vmem((rows, cols), bf16),
        heads_out=vmem((4, tok, cols), bf16),
        down_x=vmem((4, 2, hidden // 8, width), bf16),
        down_half=vmem((4, hidden // 8, width), bf16),
        down_part=vmem((3, hidden // 8, width), bf16),
        up_x=vmem((4, 2, 4, padded, hidden), bf16),
        up_half=vmem((4, 4, padded, hidden), bf16),
        up_part=vmem((3, 4, padded, hidden), bf16),
        cross_x=vmem((4, 2, 4, padded, 3 * cols), bf16),
        send=dma((200,)),
        recv=dma((200,)),
        local=dma((8,)),
    )
    names = [*given, *results, *scratch]
    specs = [
        any_space if name.endswith("_any") or name == "neighbours" else in_vmem for name in given
    ]
    got = pl.pallas_call(
        functools.partial(layer_kernel, names, total_tokens),
        out_shape=list(results.values()),
        in_specs=specs,
        out_specs=[in_vmem] * len(results),
        scratch_shapes=list(scratch.values()),
        compiler_params=pltpu.CompilerParams(
            collective_id=collective_id, has_side_effects=True, vmem_limit_bytes=62 * 2**20
        ),
        name="layer",
    )(*given.values())
    return types.SimpleNamespace(**dict(zip(results, got, strict=True)))


def finish_kernel(
    query_grad_ref,
    normed_a_ref,
    waves_ref,
    table_grad_ref,
    small_ref,
    pair_grad_ref,
    pair_cols_ref,
    down_share,
    up_share,
    cross_half,
    cross_out_x,
    output_x,
    one_grad_ref,
    tokens_ref,
    gains_ref,
    full_any,
    tokens_grad_ref,
    near_grad_ref,
    total_ref,
    down_out,
    up_out,
    cross_out,
    cross_out_out,
    output_out,
    pair_out,
    full_ref,
    mine_ref,
    sums_ref,
    cross_part,
    cross_share,
    cross_out_half,
    cross_out_part,
    cross_out_share,
    output_half,
    output_part,
    output_share,
    pair_give,
    pair_take,
    pair_share,
    near_give,
    near_take,
    near_keep,
    near_sum,
    far_sum,
    load_sem,
    b_send,
    b_recv,
    e_send,
    e_recv,
    n_send,
    n_recv,
    s_send,
    s_recv,
    chain_send,
    chain_recv,
):
    c, w = places_here()
    load = pltpu.make_async_copy(full_any, full_ref, load_sem)
    load.start()
    down = CtxSum(chain_send.at[0], chain_recv.at[0], share=down_share, out=down_out)
    up = CtxSum(
        chain_send.at[1], chain_recv.at[1], share=up_share, out=up_out, spread=up_share.shape[2]
    )
    cross = CtxSum(
        chain_send.at[2],
        chain_recv.at[2],
        half=cross_half,
        part=cross_part,
        share=cross_share,
        out=cross_out,
        spread=cross_share.shape[2],
    )
    ctx_o = CtxSum(
        chain_send.at[3],
        chain_recv.at[3],
        cross_out_x,
        cross_out_half,
        cross_out_part,
        cross_out_share,
        cross_out_out,
    )
    out_o = CtxSum(
        chain_send.at[4],
        chain_recv.at[4],
        output_x,
        output_half,
        output_part,
        output_share,
        output_out,
    )
    pair = CtxSum(chain_send.at[5], chain_recv.at[5], share=pair_share, out=pair_out)
    sum_pair = SumRows(pair_give, pair_take, e_send, e_recv)
    sum_near = SumRows(near_give, near_take, n_send, n_recv)
    width = query_grad_ref.shape[2]

    def columns(block):
        return mine_ref.at[:, pl.ds(pl.multiple_of(block * width, 128), width)]

    def block_copy(j, block):
        return remote(
            query_grad_ref.at[c ^ j], columns(block), b_send.at[j], b_recv.at[j], c ^ j, w
        )

    meet_lines()
    ctx_o.start_y()
    out_o.start_y()
    cross.start_z()
    up.start_wa()
    down.start_wa()
    for j in (4, 6, 5, 7, 2, 3, 1):
        block_copy(j, c).start()
    own = pltpu.make_async_copy(query_grad_ref.at[c], columns(c), b_recv.at[0])
    own.start()

    query_grad = query_grad_ref[...].reshape(-1, width)
    high = table_grad_ref[...].astype(bf16)
    low = (table_grad_ref[...] - high.astype(f32)).astype(bf16)
    share = sums_ref.shape[1]
    mixed = dot_tn(normed_a_ref[...], query_grad)
    turned = dot_tn(waves_ref[...], high) + dot_tn(waves_ref[...], low)
    for place in range(4):
        at = place * share
        sums_ref[place] = jnp.concatenate([mixed[at : at + share], turned[at : at + share]], axis=1)
    sum_pair.give_far(sums_ref[w ^ 3])
    sum_pair.give_near(sums_ref[w ^ 1])
    down.finish_wa()
    down.start_back_z()
    up.finish_wa()
    up.start_back_z()
    ctx_o.finish_y()
    ctx_o.start_z()
    out_o.finish_y()
    out_o.start_z()
    sum_pair.pass_on(sums_ref[w ^ 2])

    count = near_grad_ref.shape[0]

    def near_part(r):
        return dot_nt(pair_grad_ref[r * count : (r + 1) * count, :], pair_cols_ref[...])

    sum_near.give_far(near_part(3))
    sum_near.give_near(near_part(1))
    cross.finish_z()
    cross.start_wa()
    pair_share[...] = sum_pair.total(sums_ref[w]).astype(bf16)
    pair.start_wa()
    pair.finish_wa()
    pair.start_back_z()
    sum_near.pass_on(near_part(2))
    near_keep[...] = near_part(0)
    ctx_o.finish_z()
    ctx_o.start_wa()
    out_o.finish_z()
    out_o.start_wa()
    cross.finish_wa()
    cross.start_back_z()
    ctx_o.finish_wa()
    ctx_o.start_back_z()
    out_o.finish_wa()
    out_o.start_back_z()
    down.finish_back_z()
    down.start_back_y()

    for j in range(1, 8):
        block_copy(j, c ^ j).wait_recv()
    own.wait()
    load.wait()
    normed_grad = dot_nt(mine_ref[...], full_ref[...])
    hidden = tokens_ref[...].astype(f32)
    inverse = inverse_rms(hidden)
    tokens_grad_ref[...] = one_grad_ref[...] + norm_pull(
        hidden, inverse, gains_ref[0:1, :], normed_grad
    )
    gain_one = jnp.sum(normed_grad * hidden * inverse, axis=0, keepdims=True)
    small_rows = small_ref.shape[0]
    total_ref[...] = small_ref[...]
    total_ref[small_rows - 8 : small_rows - 7, 0 : gain_one.shape[1]] = gain_one

    def small_copy(source, k):
        near = k < 3
        j = k + 1 if near else k - 2
        return remote(
            source,
            near_sum.at[k] if near else far_sum.at[k - 3],
            s_send.at[k],
            s_recv.at[k],
            c if near else c ^ j,
            w ^ j if near else w,
        )

    for k in range(3):
        small_copy(total_ref, k).start()
    up.finish_back_z()
    up.start_back_y()
    pair.finish_back_z()
    pair.start_back_y()
    near_grad_ref[...] = sum_near.total(near_keep[...])
    for k in range(3):
        small_copy(total_ref, k).wait()
    total_ref[...] = tree_sum([total_ref[...]] + [near_sum[k] for k in range(3)])
    for k in range(3, 10):
        small_copy(total_ref, k).start()
    cross.finish_back_z()
    cross.start_back_y()
    ctx_o.finish_back_z()
    ctx_o.start_back_y()
    out_o.finish_back_z()
    out_o.start_back_y()
    for k in range(3, 10):
        small_copy(total_ref, k).wait()
    total_ref[...] = tree_sum([total_ref[...]] + [far_sum[k] for k in range(7)])
    for j in range(1, 8):
        block_copy(j, c).wait_send()
    for chain in (down, up, pair, cross, ctx_o, out_o):
        chain.finish_back_y()


def finish(
    query_grad,
    normed_a,
    waves,
    table_grad,
    small,
    pair_grad,
    pair_cols,
    down_share,
    up_share,
    cross_half,
    cross_out_x,
    output_x,
    one_grad,
    tokens,
    gains,
    full,
    collective_id,
):
    tok, width = tokens.shape
    near = pair_grad.shape[0]
    rows = up_share.shape[1]
    cols = output_x.shape[2] * 8
    share = width // 4
    any_space = pl.BlockSpec(memory_space=pl.ANY)
    dma = pltpu.SemaphoreType.DMA
    shape = jax.ShapeDtypeStruct
    vmem = pltpu.VMEM
    return pl.pallas_call(
        finish_kernel,
        out_shape=[
            shape((tok, width), f32),
            shape((near // 4, width), f32),
            shape(small.shape, f32),
            shape((4, 2) + down_share.shape, bf16),
            shape((4, 2, rows, 4 * up_share.shape[2]), bf16),
            shape((4, 2, rows, 12 * cols), bf16),
            shape((4, 2, cols // 8, width), bf16),
            shape((4, 2, cols // 8, width), bf16),
            shape((4, 2, share, 512), bf16),
        ],
        in_specs=[in_vmem] * 15 + [any_space],
        out_specs=[in_vmem] * 9,
        scratch_shapes=[
            vmem(full.shape, bf16),
            vmem((tok, full.shape[1]), bf16),
            vmem((4, share, 512), f32),
            vmem((3, 4, rows, 3 * cols), bf16),
            vmem((4, rows, 3 * cols), bf16),
            vmem((4, cols // 8, width), bf16),
            vmem((3, cols // 8, width), bf16),
            vmem((cols // 8, width), bf16),
            vmem((4, cols // 8, width), bf16),
            vmem((3, cols // 8, width), bf16),
            vmem((cols // 8, width), bf16),
            vmem((3, share, 512), bf16),
            vmem((3, share, 512), bf16),
            vmem((share, 512), bf16),
            vmem((3, near // 4, width), bf16),
            vmem((3, near // 4, width), bf16),
            vmem((near // 4, width), f32),
            vmem((3,) + small.shape, f32),
            vmem((7,) + small.shape, f32),
            dma(()),
            dma((8,)),
            dma((8,)),
            dma((3,)),
            dma((3,)),
            dma((3,)),
            dma((3,)),
            dma((10,)),
            dma((10,)),
            dma((6, 12)),
            dma((6, 12)),
        ],
        compiler_params=pltpu.CompilerParams(
            collective_id=collective_id, has_side_effects=True, vmem_limit_bytes=60 * 2**20
        ),
        name="finish",
    )(
        query_grad,
        normed_a,
        waves,
        table_grad,
        small,
        pair_grad,
        pair_cols,
        down_share,
        up_share,
        cross_half,
        cross_out_x,
        output_x,
        one_grad,
        tokens,
        gains,
        full,
    )


def skew(wide, count):
    lead = wide.shape[:-2]
    rows, span = wide.shape[-2:]
    edge = [(0, 0)] * len(lead)
    padded = jnp.pad(wide, edge + [(0, 0), (0, 1)])
    flat = padded.reshape(lead + (rows * (span + 1),))
    flat = lax.slice_in_dim(flat, rows - 1, rows - 1 + rows * span, axis=len(lead))
    return flat.reshape(lead + (rows, span))[..., :count]


def unskew(grad, span):
    lead = grad.shape[:-2]
    rows, count = grad.shape[-2:]
    edge = [(0, 0)] * len(lead)
    wide = jnp.pad(grad, edge + [(0, 0), (0, span - count)])
    flat = jnp.pad(wide.reshape(lead + (rows * span,)), edge + [(rows - 1, 1)])
    return flat.reshape(lead + (rows, span + 1))[..., :span]


def tile_scores(content_rows, position_rows, key_rows, relative, row_start, key_start):
    rows = content_rows.shape[0]
    count = key_rows.shape[0]
    scale = content_rows.shape[-1] ** (-0.5)
    content = jnp.einsum("qhe,khe->hqk", content_rows, key_rows, preferred_element_type=f32)
    wide = jnp.einsum("qhe,whe->hqw", position_rows, relative, preferred_element_type=f32)
    scores = (content + skew(wide, count)) * scale
    causal = (row_start + jnp.arange(rows))[:, None] >= (key_start + jnp.arange(count))[None, :]
    return (scores, causal[None])


def tile_forward(
    content_rows, position_rows, row_start, relative, key_rows, value_rows, key_start, state
):
    top, total, accum = state
    scores, causal = tile_scores(
        content_rows, position_rows, key_rows, relative, row_start, key_start
    )
    scores = jnp.where(causal, scores, neg_big)
    new_top = jnp.maximum(top, jnp.max(scores, axis=-1))
    raised = jnp.where(causal, jnp.exp(scores - new_top[..., None]), 0.0)
    fade = jnp.exp(top - new_top)
    total = total * fade + jnp.sum(raised, axis=-1)
    accum = accum * fade[..., None] + jnp.einsum(
        "hqk,khe->hqe", raised.astype(bf16), value_rows, preferred_element_type=f32
    )
    return (new_top, total, accum)


def tile_backward(
    content_rows,
    position_rows,
    row_start,
    relative,
    key_rows,
    value_rows,
    grad_rows,
    log_rows,
    delta_rows,
    key_start,
):
    scores, causal = tile_scores(
        content_rows, position_rows, key_rows, relative, row_start, key_start
    )
    scale = content_rows.shape[-1] ** (-0.5)
    shares = jnp.where(causal, jnp.exp(scores - log_rows[..., None]), 0.0)
    share_grad = jnp.einsum("qhe,khe->hqk", grad_rows, value_rows, preferred_element_type=f32)
    score_grad = (shares * (share_grad - delta_rows[..., None])).astype(bf16)
    content_grad = jnp.einsum("hqk,khe->qhe", score_grad, key_rows, preferred_element_type=f32)
    wide_grad = unskew(score_grad, relative.shape[0])
    position_grad = jnp.einsum("hqw,whe->qhe", wide_grad, relative, preferred_element_type=f32)
    table_part = jnp.einsum("hqw,qhe->whe", wide_grad, position_rows, preferred_element_type=f32)
    key_grad = jnp.einsum("hqk,qhe->khe", score_grad, content_rows, preferred_element_type=f32)
    value_grad = jnp.einsum(
        "hqk,qhe->khe", shares.astype(bf16), grad_rows, preferred_element_type=f32
    )
    return (
        content_grad * scale,
        position_grad * scale,
        table_part * scale,
        key_grad * scale,
        value_grad,
    )


def nest_tiles(tile_fn):
    inner = jax.vmap(tile_fn, in_axes=(0, 0, 0, 0, None, None, 0))
    return jax.vmap(inner, in_axes=(0, 0, None, None, 0, 0, 0))


def to_global(stored, inverse, block):
    seqs, seq_len, width = stored.shape
    blocks = stored.reshape(seqs, seq_len // block, block * width)
    chosen = (inverse[:, None] == jnp.arange(seq_len // block)[None, :]).astype(bf16)
    moved = jnp.einsum("gs,nsx->ngx", chosen, blocks, preferred_element_type=f32)
    return moved.astype(bf16).reshape(stored.shape)


class SplitQueries:

    def __init__(self, query, keys, values, biases, relative, block_order, inverse, block):
        self.seqs, self.tok_dev, self.width = keys.shape
        self.heads = self.width // HEAD_DIM
        self.block = block
        self.block_order = block_order
        ctx_count = lax.axis_size("ctx")
        self.seq_len = self.tok_dev * ctx_count
        self.key_len = min(512, self.seq_len)
        pad = jnp.zeros((self.key_len + block, self.width), bf16)
        table = jnp.concatenate([relative, pad], axis=0)
        self.table = table.reshape(-1, self.heads, HEAD_DIM)
        lead = (self.seqs, 2, block, self.heads, HEAD_DIM)
        self.content = (query + biases[0]).astype(bf16).reshape(lead)
        self.position = (query + biases[1]).astype(bf16).reshape(lead)
        gathered = [lax.all_gather(part, "ctx", axis=1, tiled=True) for part in (keys, values)]
        shape = (self.seqs, self.seq_len, self.heads, HEAD_DIM)
        self.keys, self.values = [to_global(part, inverse, block).reshape(shape) for part in gathered]
        self.starts = lax.dynamic_slice_in_dim(block_order, 2 * lax.axis_index("ctx"), 2, 0) * block

    def rows(self, index):
        start = index * self.key_len
        keys = lax.dynamic_slice_in_dim(self.keys, start, self.key_len, 1)
        values = lax.dynamic_slice_in_dim(self.values, start, self.key_len, 1)
        span = self.block + self.key_len
        offsets = [self.seq_len - self.block - self.starts[slot] + start for slot in range(2)]
        relative = [lax.dynamic_slice_in_dim(self.table, offset, span, 0) for offset in offsets]
        return start, keys, values, jnp.stack(relative), offsets

    def to_stored(self, part):
        count = self.seq_len // self.block
        blocks = part.reshape(self.seqs, count, self.block * self.width)
        chosen = (self.block_order[:, None] == jnp.arange(count)[None, :]).astype(f32)
        moved = jnp.einsum("sg,ngx->nsx", chosen, blocks, precision=highest)
        return moved.reshape(self.seqs, self.seq_len, self.width)

    def forward(self):
        def step(state, index):
            start, keys, values, relative, _ = self.rows(index)

            def tile(content, position, row_start, table, keys_seq, values_seq, tile_state):
                return tile_forward(
                    content, position, row_start, table, keys_seq, values_seq, start, tile_state
                )

            return nest_tiles(tile)(
                self.content, self.position, self.starts, relative, keys, values, state
            ), None

        shape = (self.seqs, 2, self.heads, self.block)
        state = (
            jnp.full(shape, neg_big, f32),
            jnp.zeros(shape, f32),
            jnp.zeros(shape + (HEAD_DIM,), f32),
        )
        (top, total, accum), _ = lax.scan(step, state, jnp.arange(self.seq_len // self.key_len))
        self.log_total = top + jnp.log(total)
        self.out = accum / total[..., None]
        moved = jnp.transpose(self.out, (0, 1, 3, 2, 4))
        return moved.reshape(self.seqs * self.tok_dev, self.width).astype(bf16)

    def backward(self, grad):
        block, seq_len, key_len = self.block, self.seq_len, self.key_len
        lead = (self.seqs, 2, block, self.heads, HEAD_DIM)
        grad = grad.reshape(lead)
        delta = jnp.einsum("sbqhe,sbhqe->sbhq", grad.astype(f32), self.out)
        def step(carry, index):
            start, keys, values, relative, offsets = self.rows(index)

            def tile(content, position, row_start, table, keys_seq, values_seq, extra):
                return tile_backward(
                    content, position, row_start, table, keys_seq, values_seq, *extra, start
                )

            extra = (grad, self.log_total, delta)
            parts = nest_tiles(tile)(
                self.content, self.position, self.starts, relative, keys, values, extra
            )
            table = carry[2]
            table_sum = jnp.sum(parts[2], axis=0)
            for slot in range(2):
                offset = offsets[slot]
                current = lax.dynamic_slice_in_dim(table, offset, block + key_len, 0)
                table = lax.dynamic_update_slice_in_dim(table, current + table_sum[slot], offset, 0)
            sums = []
            for total, part in zip(carry[3:], parts[3:]):
                current = lax.dynamic_slice_in_dim(total, start, key_len, 1)
                part = current + jnp.sum(part, axis=1)
                sums.append(lax.dynamic_update_slice_in_dim(total, part, start, 1))
            key_acc, value_acc = sums
            return (carry[0] + parts[0], carry[1] + parts[1], table, key_acc, value_acc), None

        zero_tiles = jnp.zeros(lead, f32)
        zero_keys = jnp.zeros((self.seqs, seq_len, self.heads, HEAD_DIM), f32)
        carry = (zero_tiles, zero_tiles, jnp.zeros(self.table.shape, f32), zero_keys, zero_keys)
        carry, _ = lax.scan(step, carry, jnp.arange(seq_len // key_len))
        owned = [
            lax.psum_scatter(
                self.to_stored(part), "ctx", scatter_dimension=1, tiled=True
            )
            for part in carry[3:]
        ]
        flat = (self.seqs * self.tok_dev, self.width)
        query_grad = (carry[0] + carry[1]).reshape(flat).astype(bf16)
        key_grad, value_grad = [part.reshape(flat).astype(bf16) for part in owned]
        bias_grads = jnp.stack(
            [jnp.sum(part, axis=(0, 1, 2)).reshape(self.width) for part in carry[:2]]
        )
        table_grad = carry[2].reshape(-1, self.width)[:seq_len]
        return query_grad, key_grad, value_grad, bias_grads, table_grad


def local_general(
    tokens,
    neighbours,
    teacher,
    valid_mask,
    block_order,
    query_weight,
    key_weight,
    value_weight,
    output_weight,
    relative_weight,
    content_bias,
    position_bias,
    cross_query_weight,
    cross_key_weight,
    cross_value_weight,
    cross_output_weight,
    up_weight,
    down_weight,
    attention_gain,
    cross_gain,
    feedforward_gain,
):
    places = lax.axis_size("wa")
    ctx_count = lax.axis_size("ctx")
    place = lax.axis_index("wa")
    here = lax.axis_index("ctx")
    _, tok_dev, width = tokens.shape
    seq_len = tok_dev * ctx_count
    block = tok_dev // 2
    cols = HEADS * HEAD_DIM // places
    rows = places * tok_dev

    token_parts = gather_parts(tokens[0])
    query_cols, key_cols, value_cols = [
        take_columns(weight) for weight in (query_weight, key_weight, value_weight)
    ]
    relative_cols = take_columns(relative_weight)
    gains = lax.all_gather(
        jnp.stack([attention_gain, cross_gain, feedforward_gain]), "wa", axis=1, tiled=True
    ).astype(f32)
    gain_one, gain_two, gain_three = gains[0:1], gains[1:2], gains[2:3]
    cross_query_cols, cross_key_cols, cross_value_cols = [
        take_columns(weight) for weight in (cross_query_weight, cross_key_weight, cross_value_weight)
    ]
    cross_pair_cols = jnp.concatenate([cross_key_cols, cross_value_cols], axis=1)
    near_rows = jnp.concatenate(gather_parts(neighbours.reshape(-1, width)), axis=0)
    up_cols = take_columns(up_weight)
    valid = valid_mask.astype(f32).reshape(tok_dev, 1)
    count = jnp.sum(valid).reshape(1, 1)
    count = all_summed(all_summed(count, "wa"), "ctx")

    slots = jnp.arange(2 * ctx_count)
    inverse = jnp.sum(jnp.where(block_order[None, :] == slots[:, None], slots[None, :], 0), axis=1)
    inverse = inverse.astype(jnp.int32)
    distance = (seq_len - 1 - jnp.arange(seq_len)).astype(f32)
    waves = sinusoid(distance, width).astype(bf16)

    hidden_all = jnp.concatenate(token_parts, axis=0).astype(f32)
    scale_all = inverse_rms(hidden_all)
    normed_a = (hidden_all * scale_all * gain_one).astype(bf16)
    biases = jnp.stack([content_bias, position_bias]).astype(f32)
    mixed_cols = jnp.concatenate([query_cols, key_cols, value_cols], axis=1)
    qkv = dot_nn(normed_a, mixed_cols).reshape(places, tok_dev, 3 * cols)
    relative = dot_nn(waves, relative_cols).astype(bf16)
    general = SplitQueries(
        qkv[..., :cols],
        qkv[..., cols : 2 * cols].astype(bf16),
        qkv[..., 2 * cols :].astype(bf16),
        biases,
        relative,
        block_order,
        inverse,
        block,
    )
    attended = general.forward()

    def to_owner(product):
        return scatter_parts([product[r * tok_dev : (r + 1) * tok_dev] for r in range(places)])

    def from_all(value):
        return jnp.concatenate(gather_parts(value), axis=0)

    hidden_in = tokens[0].astype(f32)
    hidden_one = hidden_in + to_owner(dot_nn(attended, output_weight))

    scale_two = inverse_rms(hidden_one)
    normed_b = from_all((hidden_one * scale_two * gain_two).astype(bf16))
    cross_q = dot_nn(normed_b, cross_query_cols).astype(bf16)
    cross_pair = dot_nn(near_rows, cross_pair_cols).astype(bf16)
    crossed = cross_forward(cross_q, cross_pair)
    hidden_two = hidden_one + to_owner(dot_nn(crossed, cross_output_weight))

    scale_three = inverse_rms(hidden_two)
    normed_c = from_all((hidden_two * scale_three * gain_three).astype(bf16))
    pre_act = dot_nn(normed_c, up_cols)
    activated = gelu_tanh(pre_act).astype(bf16)
    layer_out = hidden_two + to_owner(dot_nn(activated, down_weight))

    error = layer_out - teacher[0].astype(f32)
    error_sum = jnp.sum(valid * error * error).reshape(1, 1)
    error_sum = all_summed(all_summed(error_sum, "wa"), "ctx")
    loss = (error_sum / (2.0 * count * width)).reshape(())
    out_grad = (places * seq_len) / count * valid * error

    out_low = from_all(out_grad.astype(bf16))
    act_grad = dot_nt(out_low, down_weight)
    _, gelu_pull = jax.vjp(gelu_tanh, pre_act)
    pre_grad = gelu_pull(act_grad)[0].astype(bf16)
    down_grad = dot_tn(activated, out_low).astype(bf16)
    up_grad = dot_tn(normed_c, pre_grad).astype(bf16)
    normed_c_grad = to_owner(dot_nt(pre_grad, up_cols))
    two_grad = out_grad + norm_pull(hidden_two, scale_three, gain_three, normed_c_grad)
    gain_three_grad = jnp.sum(normed_c_grad * hidden_two * scale_three, axis=0, keepdims=True)
    down_out = sum_row_grads(down_grad)
    up_out = sum_column_grads(up_grad[None])[0]

    two_low = from_all(two_grad.astype(bf16))
    crossed_grad = dot_nt(two_low, cross_output_weight).astype(bf16)
    cross_q_grad, cross_pair_grad = cross_backward(cross_q, cross_pair, crossed_grad)
    normed_b_grad = to_owner(dot_nt(cross_q_grad, cross_query_cols))
    one_grad = two_grad + norm_pull(hidden_one, scale_two, gain_two, normed_b_grad)
    gain_two_grad = jnp.sum(normed_b_grad * hidden_one * scale_two, axis=0, keepdims=True)
    cross_output_grad = dot_tn(crossed, two_low).astype(bf16)
    cross_query_grad = dot_tn(normed_b, cross_q_grad).astype(bf16)
    cross_key_grad = dot_tn(near_rows, cross_pair_grad[:, :cols]).astype(bf16)
    cross_value_grad = dot_tn(near_rows, cross_pair_grad[:, cols:]).astype(bf16)
    cross_output_out = sum_row_grads(cross_output_grad)
    cross_out = sum_column_grads(jnp.stack([cross_key_grad, cross_value_grad]))
    cross_query_out = sum_column_grads(cross_query_grad[None])[0]
    near_grad = dot_nt(cross_pair_grad, cross_pair_cols)
    near_count = near_rows.shape[0] // places
    near_grad = scatter_parts(
        [near_grad[r * near_count : (r + 1) * near_count] for r in range(places)]
    )
    neighbours_grad = near_grad.reshape(neighbours.shape)

    one_low = from_all(one_grad.astype(bf16))
    attended_grad = dot_nt(one_low, output_weight).astype(bf16)
    output_grad = dot_tn(attended, one_low).astype(bf16)
    output_out = sum_row_grads(output_grad)
    query_grad, key_grad, value_grad, bias_grads, table_grad = general.backward(attended_grad)
    qkv_grad = jnp.concatenate([query_grad, key_grad, value_grad], axis=1)
    table_high = table_grad.astype(bf16)
    table_low = (table_grad - table_high.astype(f32)).astype(bf16)
    relative_grad = (dot_tn(waves, table_high) + dot_tn(waves, table_low)).astype(bf16)
    mixed_grad = dot_tn(normed_a, qkv_grad).astype(bf16)
    whole = [mixed_grad[:, m * cols : (m + 1) * cols] for m in range(3)]
    attention_out = sum_column_grads(jnp.stack(whole + [relative_grad]))
    normed_a_part = dot_nt(qkv_grad, mixed_cols)
    gain_one_part = jnp.sum(normed_a_part * hidden_all * scale_all, axis=0, keepdims=True)
    normed_a_grad = to_owner(normed_a_part)
    tokens_grad = one_grad + norm_pull(hidden_in, scale_all[:tok_dev], gain_one, normed_a_grad)

    gain_grads = jnp.concatenate([gain_one_part, gain_two_grad, gain_three_grad], axis=0)
    gain_grads = all_summed(gain_grads, "wa")
    share = width // places
    gain_grads = lax.dynamic_slice_in_dim(gain_grads, place * share, share, 1)
    small = jnp.concatenate([gain_grads.reshape(1, -1), bias_grads.reshape(1, -1)], axis=1)
    small = all_summed(small, "ctx")[0]
    gain_out = small[: 3 * share].reshape(3, share)
    bias_out = small[3 * share :].reshape(2, cols)

    return (
        layer_out[None],
        loss,
        tokens_grad[None],
        neighbours_grad,
        attention_out[0],
        attention_out[1],
        attention_out[2],
        output_out,
        attention_out[3],
        bias_out[0],
        bias_out[1],
        cross_query_out,
        cross_out[0],
        cross_out[1],
        cross_output_out,
        up_out,
        down_out,
        gain_out[0],
        gain_out[1],
        gain_out[2],
    )


def local_by_heads(
    tokens,
    neighbours,
    teacher,
    valid_mask,
    block_order,
    query_weight,
    key_weight,
    value_weight,
    output_weight,
    relative_weight,
    content_bias,
    position_bias,
    cross_query_weight,
    cross_key_weight,
    cross_value_weight,
    cross_output_weight,
    up_weight,
    down_weight,
    attention_gain,
    cross_gain,
    feedforward_gain,
):
    places = 4
    ctx_count = 8
    place = lax.axis_index("wa")
    here = lax.axis_index("ctx")
    _, tok_dev, width = tokens.shape
    seq_len = tok_dev * ctx_count
    block = tok_dev // 2
    attn = HEADS * HEAD_DIM
    cols = attn // places
    share = width // places

    slots = jnp.arange(2 * ctx_count)
    inverse = jnp.sum(jnp.where(block_order[None, :] == slots[:, None], slots[None, :], 0), axis=1)
    inverse = inverse.astype(jnp.int32)
    valid = valid_mask.astype(f32)

    def rows_of(blocks):
        return (blocks[:, None] * block + jnp.arange(block, dtype=jnp.int32)).reshape(seq_len, 1)


    small = jnp.concatenate([jnp.zeros((5, attn), f32), jnp.broadcast_to(jnp.sum(valid), (3, attn))])
    gain_rows = jnp.stack([attention_gain, cross_gain, feedforward_gain]).astype(f32)
    bias_rows = jnp.stack([content_bias, position_bias]).astype(f32)
    small = lax.dynamic_update_slice(small, gain_rows, (0, place * share))
    small = lax.dynamic_update_slice(small, bias_rows, (3, place * cols))

    half = width // 2
    freq = jnp.exp(-jnp.log(10000.0) * jnp.arange(half, dtype=f32) * 2.0 / width)
    coarse = (64.0 * jnp.arange(seq_len // 64, dtype=f32)[::-1])[:, None] * freq
    fine = jnp.arange(64, dtype=f32)[::-1][:, None] * freq
    sin_a, cos_a = jnp.sin(coarse)[:, None], jnp.cos(coarse)[:, None]
    sin_b, cos_b = jnp.sin(fine)[None], jnp.cos(fine)[None]
    waves = jnp.concatenate(
        [sin_a * cos_b + cos_a * sin_b, cos_a * cos_b - sin_a * sin_b], axis=-1
    )
    waves = waves.reshape(seq_len, width).astype(bf16)

    done = layer(
        float(places * seq_len),
        dict(
            inverse=rows_of(inverse),
            order=rows_of(block_order),
            tokens=tokens[0],
            teacher=teacher[0],
            valid=valid.reshape(tok_dev, 1),
            small=small,
            neighbours=neighbours.reshape(-1, width),
            waves_any=waves,
            query_any=query_weight,
            key_any=key_weight,
            value_any=value_weight,
            relative_any=relative_weight,
            cross_query_any=cross_query_weight,
            cross_key_any=cross_key_weight,
            cross_value_any=cross_value_weight,
            up_any=up_weight,
            output_any=output_weight,
            cross_out_any=cross_output_weight,
            down_any=down_weight,
        ),
        1,
    )
    qkv_rows = jnp.stack(
        [weight.reshape(share, ctx_count, 128) for weight in (query_weight, key_weight, value_weight)],
        axis=2,
    ).reshape(share, 3 * attn)
    qkv_full = lax.all_gather(qkv_rows, "wa", axis=0, tiled=True)
    qkv_grad, table_grad, bias_part = attend_backward(
        inverse, done.qkv, done.table, done.biases, done.heads_grad.reshape(seq_len, 128), block
    )

    pair_slots = jnp.arange(ctx_count)[:, None, None]
    bias_slots = jnp.where(pair_slots == here, bias_part[None, 0:2], 0.0)
    gain_part = done.gain_grad
    small = jnp.concatenate(
        [
            jnp.pad(gain_part[2:3], ((0, 0), (0, attn - width))),
            jnp.pad(gain_part[0:2], ((0, 0), (0, attn - width))),
            bias_slots.reshape(2, attn),
            jnp.broadcast_to(done.error[0:1, 0:1], (3, attn)),
        ],
        axis=0,
    )
    (
        tokens_grad,
        near_grad,
        small,
        down_out,
        up_out,
        cross_out,
        cross_output_out,
        output_out,
        pair_all,
    ) = finish(
        qkv_grad.reshape(ctx_count, tok_dev, 384),
        done.normed_a,
        waves,
        table_grad,
        small,
        done.pair_grad,
        done.pair_cols,
        done.down_share,
        done.up_share,
        done.cross_half,
        done.cross_out_x,
        done.output_x,
        done.one_grad,
        tokens[0],
        done.gains,
        qkv_full,
        4,
    )
    neighbours_grad = near_grad.reshape(neighbours.shape)
    gain_out = lax.dynamic_slice_in_dim(small[0:3], place * share, share, 1)
    bias_out = lax.dynamic_slice_in_dim(small[3:5].reshape(ctx_count, 2, 128), place * 2, 2, 0)
    bias_out = bias_out.transpose(1, 0, 2).reshape(2, cols)
    loss = small[5, 0] / (2.0 * done.count[0, 0] * width)
    pair_all = pair_all.reshape(ctx_count, share, 512)
    whole = [
        pair_all[:, :, 128 * m : 128 * (m + 1)].transpose(1, 0, 2).reshape(share, attn).astype(f32)
        for m in range(4)
    ]
    down_out = down_out.reshape(down_weight.shape).astype(f32)
    cross_output_out = cross_output_out.reshape(cols, width).astype(f32)
    output_out = output_out.reshape(cols, width).astype(f32)
    used = share // ctx_count
    up_out = up_out.reshape(ctx_count, -1, up_out.shape[-1])[:, :used].reshape(share, -1).astype(f32)
    cross_out = cross_out.reshape(ctx_count, -1, places, 3 * cols)[:, :used]
    cross_query_out, *cross_out = [
        cross_out[..., m * cols : (m + 1) * cols].reshape(share, attn).astype(f32) for m in range(3)
    ]

    return (
        done.layer_out[None],
        loss,
        tokens_grad[None],
        neighbours_grad,
        whole[0],
        whole[1],
        whole[2],
        output_out,
        whole[3],
        bias_out[0],
        bias_out[1],
        cross_query_out,
        cross_out[0],
        cross_out[1],
        cross_output_out,
        up_out,
        down_out,
        gain_out[0],
        gain_out[1],
        gain_out[2],
    )


def solution(mesh):
    row = P("wa", None)
    flat = P("wa")
    in_specs = (
        P("wa", "ctx", None),
        P("wa", "ctx", None, None),
        P("wa", "ctx", None),
        P("wa", "ctx"),
        P(),
        row,
        row,
        row,
        row,
        row,
        flat,
        flat,
        row,
        row,
        row,
        row,
        row,
        row,
        flat,
        flat,
        flat,
    )
    out_specs = (
        P("wa", "ctx", None),
        P(),
        P("wa", "ctx", None),
        P("wa", "ctx", None, None),
        row,
        row,
        row,
        row,
        row,
        flat,
        flat,
        row,
        row,
        row,
        row,
        row,
        row,
        flat,
        flat,
        flat,
    )
    by_heads = mesh.shape["ctx"] == 8 and mesh.shape["wa"] == 4
    local = local_by_heads if by_heads else local_general
    return jax.shard_map(local, mesh=mesh, in_specs=in_specs, out_specs=out_specs, check_vma=False)
```

```python
import functools
import types

import jax
import jax.numpy as jnp
from jax import lax
from jax.experimental import pallas as pl
from jax.experimental.pallas import tpu as pltpu
from jax.sharding import PartitionSpec as P

HEADS = 16
HEAD_DIM = 64
GROUP = 64
NK = 256
TILE = 128

eps_norm = 1e-06
neg_big = -1e30
highest = lax.Precision.HIGHEST
f32 = jnp.float32
bf16 = jnp.bfloat16


def inverse_rms(hidden):
    return lax.rsqrt(jnp.mean(hidden * hidden, axis=-1, keepdims=True) + eps_norm)


def norm_pull(hidden, scale, gain, grad):
    scaled = grad * gain
    mean = jnp.mean(hidden * scaled, axis=-1, keepdims=True)
    return scale * scaled - hidden * (scale * scale * scale) * mean


def gelu_tanh(value):
    return jax.nn.gelu(value, approximate=True)


def sinusoid(distance, width):
    half = width // 2
    freq = jnp.exp(-jnp.log(10000.0) * jnp.arange(half, dtype=f32) * 2.0 / width)
    angle = distance[:, None] * freq[None, :]
    return jnp.concatenate([jnp.sin(angle), jnp.cos(angle)], axis=1)


def dot_nn(a, b):
    return lax.dot_general(a, b, (((1,), (0,)), ((), ())), preferred_element_type=f32)


def dot_nt(a, b):
    return lax.dot_general(a, b, (((1,), (1,)), ((), ())), preferred_element_type=f32)


def dot_tn(a, b):
    return lax.dot_general(a, b, (((0,), (0,)), ((), ())), preferred_element_type=f32)


def swap(value, axis, bit):
    pairs = [(i, i ^ bit) for i in range(lax.axis_size(axis))]
    return lax.ppermute(value, axis, pairs)


def bits_of(axis):
    bits, bit = [], 1
    while bit < lax.axis_size(axis):
        bits.append(bit)
        bit *= 2
    return bits


def my_bit(axis, bit):
    return (lax.axis_index(axis) // bit) % 2


def ordered(bit, own, other, dim):
    return jnp.where(
        bit == 0,
        jnp.concatenate([own, other], axis=dim),
        jnp.concatenate([other, own], axis=dim),
    )


def split(value, bit, dim):
    half = value.shape[dim] // 2
    keep = lax.dynamic_slice_in_dim(value, bit * half, half, dim)
    send = lax.dynamic_slice_in_dim(value, (1 - bit) * half, half, dim)
    return keep, send


def gather_parts(value):
    parts = {0: value}
    for bit in reversed(bits_of("wa")):
        parts.update({r | bit: swap(part, "wa", bit) for r, part in list(parts.items())})
    return [parts[r] for r in sorted(parts)]


def scatter_parts(parts):
    parts = dict(enumerate(parts))
    for bit in bits_of("wa"):
        kept = {}
        for r, part in parts.items():
            if not r & bit:
                got = swap(parts[r | bit].astype(bf16), "wa", bit)
                kept[r] = part + got.astype(f32)
        parts = kept
    return parts[0]


def take_columns(weight):
    value = weight[None]
    for bit in reversed(bits_of("wa")):
        mine = my_bit("wa", bit)
        keep, send = split(value, mine, 2)
        value = ordered(mine, keep[:, None], swap(send, "wa", bit)[:, None], 1)
        value = value.reshape((-1,) + value.shape[2:])
    return value.reshape(-1, value.shape[-1])


def spread_columns(value):
    for bit in bits_of("wa"):
        mine = my_bit("wa", bit)
        paired = value.reshape((value.shape[0], value.shape[1] // 2, 2) + value.shape[2:])
        keep, send = split(paired, mine, 2)
        value = ordered(mine, keep[:, :, 0], swap(send[:, :, 0], "wa", bit), 3)
    return value[:, 0]


def halving_dim(shape):
    if shape[-2] % 16 == 0:
        return len(shape) - 2
    if shape[0] % 2 == 0:
        return 0
    if shape[-2] % 2 == 0:
        return len(shape) - 2
    return len(shape) - 1


def sum_over_ctx(value, bits, finish):
    dims = []
    for bit in bits:
        dim = halving_dim(value.shape)
        keep, send = split(value, my_bit("ctx", bit), dim)
        value = (keep.astype(f32) + swap(send, "ctx", bit).astype(f32)).astype(bf16)
        dims.append(dim - value.ndim if dim else 0)
    value = finish(value)
    for bit, dim in reversed(list(zip(bits, dims))):
        dim = dim % value.ndim
        value = ordered(my_bit("ctx", bit), value, swap(value, "ctx", bit), dim)
    return value


def all_summed(value, axis):
    for bit in bits_of(axis):
        value = value + swap(value, axis, bit)
    return value


def sum_column_grads(grads):
    places = lax.axis_size("wa")
    grads = grads.reshape(grads.shape[0], places, grads.shape[1] // places, grads.shape[2])
    bits = bits_of("ctx")
    if grads.shape[2] % lax.axis_size("ctx") == 0:
        return sum_over_ctx(grads, bits, spread_columns).astype(f32)
    return sum_over_ctx(spread_columns(grads), bits, lambda value: value).astype(f32)


def sum_row_grads(grads):
    return sum_over_ctx(grads[None], bits_of("ctx"), lambda value: value)[0].astype(f32)


def first_half(shape):
    return lax.broadcasted_iota(jnp.int32, shape, 1) < HEAD_DIM


def stack_heads(rows):
    mask = first_half(rows.shape)
    zero = jnp.zeros_like(rows)
    return jnp.concatenate([jnp.where(mask, rows, zero), jnp.where(mask, zero, rows)], axis=0)


def join_heads(stacked):
    rows = stacked.shape[0] // 2
    return jnp.where(first_half((rows, stacked.shape[1])), stacked[:rows], stacked[rows:])


def copy_blocks(order_ref, source, target, block, inward):
    for place in range(source.shape[0] // block):
        start = pl.multiple_of(order_ref[place] * block, block)
        if inward:
            target[place * block : (place + 1) * block, :] = source[pl.ds(start, block), :]
        else:
            target[pl.ds(start, block), :] = source[place * block : (place + 1) * block, :]


def attention_shares(content, position, key_ref, rel_ref, row_start, seq_len):
    length = row_start + TILE
    wide_len = length + TILE
    offset = seq_len - TILE - row_start
    scale = HEAD_DIM ** (-0.5)
    scores = dot_nt(content, key_ref[0:length, :])
    wide = dot_nt(position, rel_ref[offset : offset + wide_len, :])
    halves = []
    for head in range(2):
        part = wide[head * TILE : (head + 1) * TILE]
        turned = pltpu.roll(part, wide_len - (TILE - 1), 1, stride=1, stride_axis=0)
        halves.append(turned[:, :length])
    scores = (scores + jnp.concatenate(halves, axis=0)) * scale
    row = lax.broadcasted_iota(jnp.int32, scores.shape, 0) % TILE + row_start
    col = lax.broadcasted_iota(jnp.int32, scores.shape, 1)
    scores = jnp.where(col <= row, scores, neg_big)
    top = jnp.max(scores, axis=1, keepdims=True)
    raised = jnp.exp(scores - top)
    total = jnp.sum(raised, axis=1, keepdims=True)
    return raised * (1.0 / total)


def attend_tiles(qkv, rel_ref, content_bias, position_bias, out):
    seq_len = qkv.shape[0]
    keys = qkv.at[:, 128:256]
    values = qkv.at[:, 256:384]
    for tile in range(seq_len // TILE):
        start = tile * TILE
        query = qkv[start : start + TILE, 0:128].astype(f32)
        content = stack_heads((query + content_bias).astype(bf16))
        position = stack_heads((query + position_bias).astype(bf16))
        shares = attention_shares(content, position, keys, rel_ref, start, seq_len)
        got = dot_nn(shares.astype(bf16), values[0 : start + TILE, :])
        out[start : start + TILE, :] = join_heads(got).astype(bf16)


def attend_backward_kernel(
    seq_len,
    block,
    order_ref,
    qkv_ref,
    rel_ref,
    bias_ref,
    grad_ref,
    dqkv_ref,
    drel_ref,
    dbias_ref,
    qkv,
    grad,
    dqkv,
    dkey,
    dvalue,
    drel,
):
    scale = HEAD_DIM ** (-0.5)
    copy_blocks(order_ref, qkv_ref, qkv, block, True)
    copy_blocks(order_ref, grad_ref, grad, block, True)
    keys = qkv.at[:, 128:256]
    values = qkv.at[:, 256:384]
    content_bias = bias_ref[3:4, :]
    position_bias = bias_ref[4:5, :]
    dkey[...] = jnp.zeros_like(dkey)
    dvalue[...] = jnp.zeros_like(dvalue)
    drel[...] = jnp.zeros_like(drel)
    row = lax.broadcasted_iota(jnp.int32, (TILE, TILE), 0)
    col = lax.broadcasted_iota(jnp.int32, (TILE, TILE), 1)
    flip = jnp.where(row + col == TILE - 1, 1.0, 0.0).astype(bf16)
    content_sum = jnp.zeros((1, 128), f32)
    position_sum = jnp.zeros((1, 128), f32)
    for tile in range(seq_len // TILE):
        start = tile * TILE
        length = start + TILE
        wide_len = length + TILE
        offset = seq_len - TILE - start
        query = qkv[start : start + TILE, 0:128].astype(f32)
        content = stack_heads((query + content_bias).astype(bf16))
        plain = (query + position_bias).astype(bf16)
        position = stack_heads(plain)
        shares = attention_shares(content, position, keys, rel_ref, start, seq_len)
        out_grad = stack_heads(grad[start : start + TILE, :])
        share_grad = dot_nt(out_grad, values[0:length, :])
        delta = jnp.sum(shares * share_grad, axis=1, keepdims=True)
        score_grad = (shares * (share_grad - delta)).astype(bf16)
        content_grad = join_heads(dot_nn(score_grad, keys[0:length, :])) * scale
        parts = []
        for head in range(2):
            turned = dot_nn(flip, score_grad[head * TILE : (head + 1) * TILE])
            turned = jnp.concatenate([turned, jnp.zeros((TILE, TILE), f32)], axis=1)
            parts.append(pltpu.roll(turned, 0, 1, stride=1, stride_axis=0))
        wide_grad = jnp.concatenate(parts, axis=0).astype(bf16)
        relative = rel_ref[offset : offset + wide_len, :]
        turned_grad = join_heads(dot_nn(wide_grad, relative)) * scale
        turned_rows = stack_heads(dot_nn(flip, plain).astype(bf16))
        drel[offset : offset + wide_len, :] += dot_tn(wide_grad, turned_rows)
        high = turned_grad.astype(bf16)
        low = (turned_grad - high.astype(f32)).astype(bf16)
        position_grad = dot_nn(flip, high) + dot_nn(flip, low)
        content_sum += jnp.sum(content_grad, axis=0, keepdims=True)
        position_sum += jnp.sum(turned_grad, axis=0, keepdims=True)
        dqkv[start : start + TILE, 0:128] = (content_grad + position_grad).astype(bf16)
        dkey[0:length, :] += dot_tn(score_grad, content)
        dvalue[0:length, :] += dot_tn(shares.astype(bf16), out_grad)
    dqkv[:, 128:256] = (dkey[...] * scale).astype(bf16)
    dqkv[:, 256:384] = dvalue[...].astype(bf16)
    copy_blocks(order_ref, dqkv, dqkv_ref, block, False)
    drel_ref[...] = drel[0:seq_len, :] * scale
    dbias_ref[...] = jnp.concatenate(
        [content_sum, position_sum, jnp.zeros((6, 128), f32)], axis=0
    )


in_vmem = pl.BlockSpec(memory_space=pltpu.VMEM)
in_smem = pl.BlockSpec(memory_space=pltpu.SMEM)


def attend_backward(order, qkv, rel, bias, grad, block):
    rows = qkv.shape[0]
    return pl.pallas_call(
        functools.partial(attend_backward_kernel, rows, block),
        out_shape=[
            jax.ShapeDtypeStruct((rows, 384), bf16),
            jax.ShapeDtypeStruct((rows, 128), f32),
            jax.ShapeDtypeStruct((8, 128), f32),
        ],
        in_specs=[in_smem, in_vmem, in_vmem, in_vmem, in_vmem],
        out_specs=[in_vmem, in_vmem, in_vmem],
        scratch_shapes=[
            pltpu.VMEM((rows, 384), bf16),
            pltpu.VMEM((rows, 128), bf16),
            pltpu.VMEM((rows, 384), bf16),
            pltpu.VMEM((rows, 128), f32),
            pltpu.VMEM((rows, 128), f32),
            pltpu.VMEM((rows + TILE, 128), f32),
        ],
        compiler_params=pltpu.CompilerParams(vmem_limit_bytes=40 * 2**20),
        cost_estimate=pl.CostEstimate(
            flops=10 * 256 * rows * rows * 2, bytes_accessed=rows * 3000, transcendentals=rows * rows
        ),
        name="attend_backward",
    )(order, qkv, rel, bias, grad)


def head_mask(shape, head):
    lane = lax.broadcasted_iota(jnp.int32, shape, 1)
    return (lane >= head * HEAD_DIM) & (lane < (head + 1) * HEAD_DIM)


def stack_all(rows):
    zero = jnp.zeros_like(rows)
    heads = rows.shape[1] // HEAD_DIM
    return jnp.concatenate(
        [jnp.where(head_mask(rows.shape, head), rows, zero) for head in range(heads)], axis=0
    )


def join_all(stacked):
    heads = stacked.shape[1] // HEAD_DIM
    rows = stacked.shape[0] // heads
    out = jnp.zeros((rows, stacked.shape[1]), stacked.dtype)
    for head in range(heads):
        part = stacked[head * rows : (head + 1) * rows]
        out = jnp.where(head_mask(part.shape, head), part, out)
    return out


def cross_shares(query, keys):
    scores = dot_nt(query, keys) * (HEAD_DIM ** (-0.5))
    raised = jnp.exp(scores - jnp.max(scores, axis=1, keepdims=True))
    return raised / jnp.sum(raised, axis=1, keepdims=True)


def cross_forward_kernel(q_ref, kv_ref, out_ref):
    width = q_ref.shape[1]
    shares = cross_shares(stack_all(q_ref[...]), kv_ref[:, 0:width])
    out_ref[...] = join_all(dot_nn(shares.astype(bf16), kv_ref[:, width:])).astype(bf16)


def cross_backward_kernel(q_ref, kv_ref, grad_ref, dq_ref, dkv_ref):
    width = q_ref.shape[1]
    scale = HEAD_DIM ** (-0.5)
    keys = kv_ref[:, 0:width]
    query = stack_all(q_ref[...])
    grad = stack_all(grad_ref[...])
    shares = cross_shares(query, keys)
    share_grad = dot_nt(grad, kv_ref[:, width:])
    delta = jnp.sum(shares * share_grad, axis=1, keepdims=True)
    score_grad = (shares * (share_grad - delta)).astype(bf16)
    dq_ref[...] = (join_all(dot_nn(score_grad, keys)) * scale).astype(bf16)
    dkv_ref[:, 0:width] = (dot_tn(score_grad, query) * scale).astype(bf16)
    dkv_ref[:, width:] = dot_tn(shares.astype(bf16), grad).astype(bf16)


def cross_forward(query, pair):
    width = query.shape[1]
    groups = query.shape[0] // GROUP
    return pl.pallas_call(
        cross_forward_kernel,
        out_shape=jax.ShapeDtypeStruct(query.shape, bf16),
        grid=(groups,),
        in_specs=[
            pl.BlockSpec((GROUP, width), lambda g: (g, 0)),
            pl.BlockSpec((NK, 2 * width), lambda g: (g, 0)),
        ],
        out_specs=pl.BlockSpec((GROUP, width), lambda g: (g, 0)),
        cost_estimate=pl.CostEstimate(
            flops=groups * 4 * 256 * 256 * 256, bytes_accessed=groups * 330000, transcendentals=groups * 65536
        ),
        name="cross_forward",
    )(query, pair)


def cross_backward(query, pair, grad):
    width = query.shape[1]
    groups = query.shape[0] // GROUP
    return pl.pallas_call(
        cross_backward_kernel,
        out_shape=[
            jax.ShapeDtypeStruct(query.shape, bf16),
            jax.ShapeDtypeStruct(pair.shape, bf16),
        ],
        grid=(groups,),
        in_specs=[
            pl.BlockSpec((GROUP, width), lambda g: (g, 0)),
            pl.BlockSpec((NK, 2 * width), lambda g: (g, 0)),
            pl.BlockSpec((GROUP, width), lambda g: (g, 0)),
        ],
        out_specs=[
            pl.BlockSpec((GROUP, width), lambda g: (g, 0)),
            pl.BlockSpec((NK, 2 * width), lambda g: (g, 0)),
        ],
        cost_estimate=pl.CostEstimate(
            flops=groups * 10 * 256 * 256 * 256, bytes_accessed=groups * 660000, transcendentals=groups * 65536
        ),
        name="cross_backward",
    )(query, pair, grad)


mesh_id = pl.DeviceIdType.MESH


def signal_to(barrier, ctx, wa):
    pl.semaphore_signal(barrier, inc=1, device_id=(ctx, wa), device_id_type=mesh_id)


def tree_sum(values):
    while len(values) > 1:
        values = [a + b for a, b in zip(values[::2], values[1::2])]
    return values[0]


def gelu_slope(value):
    inner = 0.7978845608028654 * (value + 0.044715 * value * value * value)
    turned = jnp.tanh(inner)
    slope = 0.7978845608028654 * (1.0 + 3.0 * 0.044715 * value * value)
    return 0.5 * (1.0 + turned) + 0.5 * value * (1.0 - turned * turned) * slope


def places_here():
    return lax.axis_index("ctx"), lax.axis_index("wa")


def meet_all():
    c, w = places_here()
    owner = c // 2
    own = owner == w
    barrier = pltpu.get_barrier_semaphore()
    for j in range(1, 8):
        signal_to(barrier, c ^ j, w)
    for j in range(1, 4):
        signal_to(barrier, c, w ^ j)
    for j in range(1, 8):
        signal_to(barrier, c ^ j, owner)
    for r in range(4):
        for h in range(2):

            @pl.when(jnp.logical_not(jnp.logical_and(2 * w + h == c, r == 0)))
            def _(r=r, h=h):
                signal_to(barrier, 2 * w + h, w ^ r)

    @pl.when(jnp.logical_not(own))
    def _():
        signal_to(barrier, c, owner)

    pl.semaphore_wait(barrier, 26 - 2 * own.astype(jnp.int32))


def meet_lines():
    c, w = places_here()
    barrier = pltpu.get_barrier_semaphore()
    for j in range(1, 8):
        signal_to(barrier, c ^ j, w)
    for j in range(1, 4):
        signal_to(barrier, c, w ^ j)
    pl.semaphore_wait(barrier, 10)


def remote(source, target, send, recv, ctx, wa):
    return pltpu.make_async_remote_copy(
        src_ref=source,
        dst_ref=target,
        send_sem=send,
        recv_sem=recv,
        device_id=(ctx, wa),
        device_id_type=mesh_id,
    )


class GatherRows:

    def __init__(self, buf, send, recv):
        self.buf, self.send, self.recv = buf, send, recv
        self.c, self.w = places_here()

    def copy(self, k):
        source, entry, j = ((0, 1, 1), (0, 2, 2), (2, 3, 1))[k]
        return remote(
            self.buf.at[source],
            self.buf.at[entry],
            self.send.at[k],
            self.recv.at[k],
            self.c,
            self.w ^ j,
        )

    def start(self):
        self.copy(1).start()
        self.copy(0).start()

    def near(self):
        self.copy(0).wait()

    def relay(self):
        self.copy(1).wait()
        self.copy(2).start()

    def far(self):
        self.copy(2).wait()


class SumRows:

    def __init__(self, out_buf, in_buf, send, recv):
        self.out, self.inn, self.send, self.recv = out_buf, in_buf, send, recv
        self.c, self.w = places_here()

    def copy(self, k):
        j = (1, 1, 2)[k]
        return remote(
            self.out.at[k], self.inn.at[k], self.send.at[k], self.recv.at[k], self.c, self.w ^ j
        )

    def give_near(self, value):
        self.out[0] = value.astype(bf16)
        self.copy(0).start()

    def give_far(self, value):
        self.out[1] = value.astype(bf16)
        self.copy(1).start()

    def pass_on(self, value):
        self.copy(1).wait()
        self.out[2] = (value + self.inn[1].astype(f32)).astype(bf16)
        self.copy(2).start()

    def total(self, value):
        self.copy(0).wait()
        value = value + self.inn[0].astype(f32)
        self.copy(2).wait()
        return value + self.inn[2].astype(f32)


class CtxSum:

    def __init__(self, send, recv, x=None, half=None, part=None, share=None, out=None, spread=0):
        self.send, self.recv = send, recv
        self.x, self.half, self.part, self.share, self.out = x, half, part, share, out
        self.spread = spread
        self.c, self.w = places_here()
        self.z, self.y = self.c // 2, self.c % 2

    def y_copy(self):
        return remote(
            self.x.at[:, 1 - self.y], self.half, self.send.at[0], self.recv.at[0], self.c ^ 1, self.w
        )

    def start_y(self):
        self.y_copy().start()

    def finish_y(self):
        self.y_copy().wait()
        for z in range(4):
            mine = self.x[z, self.y].astype(f32)
            self.half[z] = (self.half[z].astype(f32) + mine).astype(bf16)

    def z_copy(self, j):
        return remote(
            self.half.at[self.z ^ j],
            self.part.at[j - 1],
            self.send.at[j],
            self.recv.at[j],
            self.c ^ (2 * j),
            self.w,
        )

    def start_z(self):
        for j in (2, 3, 1):
            self.z_copy(j).start()

    def finish_z(self):
        total = self.half[self.z].astype(f32)
        for j in (1, 2, 3):
            self.z_copy(j).wait()
            total = total + self.part[j - 1].astype(f32)
        self.share[...] = total.astype(bf16)

    def columns(self, place):
        width = self.spread
        return self.out.at[self.z, self.y, :, pl.ds(pl.multiple_of(place * width, 128), width)]

    def wa_copy(self, j, place):
        return remote(
            self.share.at[self.w ^ j],
            self.columns(place),
            self.send.at[3 + j],
            self.recv.at[3 + j],
            self.c,
            self.w ^ j,
        )

    def own_copy(self):
        source = self.share.at[self.w] if self.spread else self.share
        target = self.columns(self.w) if self.spread else self.out.at[self.z, self.y]
        return pltpu.make_async_copy(source, target, self.send.at[11])

    def start_wa(self):
        if self.spread:
            for j in (2, 3, 1):
                self.wa_copy(j, self.w).start()
        self.own_copy().start()

    def finish_wa(self):
        self.own_copy().wait()
        if self.spread:
            for j in (1, 2, 3):
                self.wa_copy(j, self.w).wait_send()
                self.wa_copy(j, self.w ^ j).wait_recv()

    def back_z_copy(self, j, z):
        mine = self.out.at[z, self.y]
        return remote(mine, mine, self.send.at[6 + j], self.recv.at[6 + j], self.c ^ (2 * j), self.w)

    def start_back_z(self):
        for j in (2, 3, 1):
            self.back_z_copy(j, self.z).start()

    def finish_back_z(self):
        for j in (1, 2, 3):
            self.back_z_copy(j, self.z).wait_send()
            self.back_z_copy(j, self.z ^ j).wait_recv()

    def back_y_copy(self, y):
        part = self.out.at[:, y]
        return remote(part, part, self.send.at[10], self.recv.at[10], self.c ^ 1, self.w)

    def start_back_y(self):
        self.back_y_copy(self.y).start()

    def finish_back_y(self):
        self.back_y_copy(self.y).wait_send()
        self.back_y_copy(1 - self.y).wait_recv()


def put_shares(target, grads, first=0):
    count = grads.shape[0] // 32
    padded = target.shape[3]
    for place in range(4):
        for share in range(8):
            start = (place * 8 + share) * count
            part = grads[start : start + count]
            part = jnp.concatenate([part, jnp.zeros((padded - count, part.shape[1]), f32)], axis=0)
            target[share // 2, share % 2, place, :, first : first + part.shape[1]] = part.astype(bf16)


def put_rows(target, grads):
    count = grads.shape[0] // 8
    for share in range(8):
        target[share // 2, share % 2] = grads[share * count : (share + 1) * count].astype(bf16)


class Cut:

    def __init__(self, ref, start):
        self.ref, self.start = ref, start

    @property
    def at(self):
        return self

    def __getitem__(self, k):
        return self.ref.at[self.start + k]


class Pool:
    def __init__(self, ref):
        self.ref, self.used = ref, 0

    def take(self, count):
        cut = Cut(self.ref, self.used)
        self.used += count
        return cut


class LineGather:

    def __init__(self, out, send, recv):
        self.out, self.send, self.recv = out, send, recv
        self.c, self.w = places_here()
        self.z = self.c // 2
        self.right, self.left = self.z < 3, self.z > 0

    def y_copy(self, block, slot):
        ref = self.out.at[block]
        return remote(ref, ref, self.send.at[slot], self.recv.at[slot], self.c ^ 1, self.w)

    def z_copy(self, block, slot, step):
        k = slot + (7 if step > 0 else 10)
        ref = self.out.at[block]
        return remote(ref, ref, self.send.at[k], self.recv.at[k], self.c + step, self.w)

    def start(self):
        @pl.when(self.right)
        def _():
            self.z_copy(self.c, 0, 2).start()

        @pl.when(self.left)
        def _():
            self.z_copy(self.c, 0, -2).start()

        self.y_copy(self.c, 0).start()

    def step(self, t):
        @pl.when(self.z > t)
        def _():
            block = self.c - 2 * (t + 1)
            self.z_copy(block, t, 2).wait_recv()
            if t < 2:

                @pl.when(self.right)
                def _():
                    self.z_copy(block, t + 1, 2).start()

            self.y_copy(block, t + 1).start()

        @pl.when(self.z < 3 - t)
        def _():
            block = self.c + 2 * (t + 1)
            self.z_copy(block, t, -2).wait_recv()
            if t < 2:

                @pl.when(self.left)
                def _():
                    self.z_copy(block, t + 1, -2).start()

            self.y_copy(block, t + 4).start()

    def finish(self):
        self.y_copy(self.c, 0).wait_send()
        self.y_copy(self.c ^ 1, 0).wait_recv()
        for t in range(3):
            for step, at, near in ((-2, t + 1, self.z > t), (2, t + 4, self.z < 3 - t)):

                @pl.when(near)
                def _(step=step, at=at):
                    self.y_copy(self.c + step * (t + 1), at).wait_send()
                    self.y_copy((self.c ^ 1) + step * (t + 1), at).wait_recv()

        @pl.when(self.right)
        def _():
            self.z_copy(self.c, 0, 2).wait_send()

        @pl.when(self.left)
        def _():
            self.z_copy(self.c, 0, -2).wait_send()

        for t in range(2):

            @pl.when(jnp.logical_and(self.z > t, self.right))
            def _():
                self.z_copy(self.c, t + 1, 2).wait_send()

            @pl.when(jnp.logical_and(self.z < 3 - t, self.left))
            def _():
                self.z_copy(self.c, t + 1, -2).wait_send()


class Columns:

    def __init__(self, source, target, width, first, send, recv, at=None):
        self.source, self.target, self.width, self.first = source, target, width, first
        self.send, self.recv, self.column = send, recv, at
        self.c, self.w = places_here()

    def taken(self, place):
        start = place * self.width if self.column is None else self.column
        return self.source.at[:, pl.ds(pl.multiple_of(start, 128), self.width)]

    def put(self, place):
        rows = self.source.shape[0]
        return self.target.at[
            pl.ds(pl.multiple_of(place * rows, 32), rows), self.first : self.first + self.width
        ]

    def copy(self, j, place):
        return remote(
            self.taken(self.w ^ j),
            self.put(place),
            self.send.at[j],
            self.recv.at[j],
            self.c,
            self.w ^ j,
        )

    def own(self):
        return pltpu.make_async_copy(self.taken(self.w), self.put(self.w), self.send.at[0])

    def start(self):
        for j in (2, 3, 1):
            self.copy(j, self.w).start()
        self.own().start()

    def finish(self):
        self.own().wait()
        for j in (1, 2, 3):
            self.copy(j, self.w).wait_send()
            self.copy(j, self.w ^ j).wait_recv()


class SmallSum:

    def __init__(self, ref, got, axis, send, recv):
        self.ref, self.got, self.axis, self.send, self.recv = ref, got, axis, send, recv
        self.c, self.w = places_here()

    def copy(self, k):
        j = k + 1
        ctx, wa = (self.c ^ j, self.w) if self.axis == "ctx" else (self.c, self.w ^ j)
        return remote(self.ref, self.got.at[k], self.send.at[k], self.recv.at[k], ctx, wa)

    def start(self):
        for k in range(self.got.shape[0]):
            self.copy(k).start()

    def finish(self):
        count = self.got.shape[0]
        for k in range(count):
            self.copy(k).wait()
        self.ref[...] = tree_sum([self.ref[...]] + [self.got[k] for k in range(count)])


class SwapHeads:

    def __init__(self, by_heads, by_rows, outward, send, recv):
        self.heads, self.rows, self.outward = by_heads, by_rows, outward
        self.send, self.recv = send, recv
        self.c, self.w = places_here()
        self.owner, self.half = self.c // 2, self.c % 2
        self.own = self.owner == self.w
        self.other = jnp.logical_not(self.own)

    def lanes(self):
        return pl.ds(pl.multiple_of(self.half * 128, 128), 128)

    def out_copy(self, j):
        slot = self.w ^ self.owner
        return remote(
            self.heads.at[self.c ^ j],
            self.rows.at[slot, :, self.lanes()],
            self.send.at[j],
            self.recv.at[slot * 2 + self.half],
            self.c ^ j,
            self.owner,
        )

    def start_out(self):
        for j in range(7, 0, -1):
            self.out_copy(j).start()

        @pl.when(self.other)
        def _():
            self.out_copy(0).start()

        @pl.when(self.own)
        def _():
            slot = self.w ^ self.owner
            pltpu.make_async_copy(
                self.heads.at[self.c],
                self.rows.at[slot, :, self.lanes()],
                self.recv.at[slot * 2 + self.half],
            ).start()

    def wait_rows(self, r):
        for h in range(2):
            remote(
                self.heads.at[0],
                self.rows.at[r, :, h * 128 : (h + 1) * 128],
                self.send.at[0],
                self.recv.at[r * 2 + h],
                self.c ^ 1,
                self.w,
            ).wait_recv()

    def finish_out(self):
        for j in range(1, 8):
            self.out_copy(j).wait_send()

        @pl.when(self.other)
        def _():
            self.out_copy(0).wait_send()

    def in_copy(self, r, h):
        return remote(
            self.rows.at[r, :, h * 128 : (h + 1) * 128],
            self.heads.at[self.c],
            self.send.at[r * 2 + h],
            self.recv.at[self.c],
            2 * self.w + h,
            self.w ^ r,
        )

    def mine(self, r, h):
        return jnp.logical_and(2 * self.w + h == self.c, r == 0)

    def start_in(self, r):
        for h in range(2):

            @pl.when(jnp.logical_not(self.mine(r, h)))
            def _():
                self.in_copy(r, h).start()

            @pl.when(self.mine(r, h))
            def _():
                pltpu.make_async_copy(
                    self.rows.at[r, :, h * 128 : (h + 1) * 128],
                    self.heads.at[self.c],
                    self.recv.at[self.c],
                ).start()

    def finish_in(self):
        for block in range(8):
            remote(
                self.rows.at[0, :, 0:128],
                self.heads.at[block],
                self.send.at[0],
                self.recv.at[block],
                self.c ^ 1,
                self.w,
            ).wait_recv()
        for r in range(4):
            for h in range(2):

                @pl.when(jnp.logical_not(self.mine(r, h)))
                def _(r=r, h=h):
                    self.in_copy(r, h).wait_send()


def layer_kernel(names, total_tokens, *refs):
    v = types.SimpleNamespace(**dict(zip(names, refs, strict=True)))
    c, w = places_here()
    send, recv, local = Pool(v.send), Pool(v.recv), Pool(v.local)
    tok, width = v.tokens.shape
    seq_len = 8 * tok
    rows = 4 * tok
    cols = v.output_w.shape[0]
    hidden = v.down_w.shape[0]
    scale = HEAD_DIM ** (-0.5)

    def load(source, target):
        copy = pltpu.make_async_copy(source, target, local.take(1).at[0])
        copy.start()
        return copy

    near_load = load(v.neighbours, v.near.at[0])
    early = [load(v.waves_any, v.waves)]
    late = [
        load(v.output_any, v.output_w),
        load(v.cross_out_any, v.cross_out_w),
        load(v.down_any, v.down_w),
    ]
    v.small_all[...] = v.small[...]
    v.tokens_all[c] = v.tokens[...]
    meet_all()

    near_sum = SmallSum(v.small_all, v.small_near, "wa", send.take(3), recv.take(3))
    count_sum = SmallSum(v.count, v.count_far, "ctx", send.take(7), recv.take(7))
    gather = LineGather(v.tokens_all, send.take(13), recv.take(13))
    pair = [
        Columns(weight, v.pair, 128, 128 * m, send.take(4), recv.take(4), c * 128)
        for m, weight in enumerate((v.query_any, v.key_any, v.value_any, v.relative_any))
    ]
    cross = [
        Columns(weight, target, cols, first, send.take(4), recv.take(4))
        for weight, target, first in (
            (v.cross_key_any, v.pair_cols, 0),
            (v.cross_value_any, v.pair_cols, cols),
            (v.cross_query_any, v.query_cols, 0),
        )
    ]
    up_columns = Columns(v.up_any, v.up_cols, hidden, 0, send.take(4), recv.take(4))
    near_send, near_recv = send.take(3), recv.take(3)
    near_gather = GatherRows(v.near, near_send, near_recv)
    gather.start()
    near_sum.start()
    for part in pair:
        part.start()
    gather.step(0)
    near_sum.finish()
    v.count[...] = jnp.broadcast_to(v.small_all[5:6, 0:128], v.count.shape)
    count_sum.start()
    gather.step(1)
    for part in pair:
        part.finish()
    near_load.wait()
    near_gather.start()
    for part in cross:
        part.start()
    for copy in early:
        copy.wait()
    v.table[0:seq_len, :] = dot_nn(v.waves[...], v.pair[:, 384:512]).astype(bf16)
    v.table[seq_len:, :] = jnp.zeros((TILE, 128), bf16)
    v.biases[...] = v.small_all[:, pl.ds(pl.multiple_of(c * 128, 128), 128)]
    v.gains[...] = v.small_all[:, 0:width]
    gather.step(2)
    gather.finish()
    gain_one, gain_two, gain_three = (v.gains[k : k + 1, :] for k in range(3))

    def project(part, carry):
        start = pl.multiple_of(part * tok, tok)
        value = v.tokens_all[part].astype(f32)
        normed = (value * inverse_rms(value) * gain_one).astype(bf16)
        v.normed_a[pl.ds(start, tok), :] = normed
        v.qkv[pl.ds(start, tok), :] = dot_nn(normed, v.pair[:, 0:384]).astype(bf16)
        return carry

    lax.fori_loop(0, 8, project, 0)
    column = lax.broadcasted_iota(jnp.int32, (TILE, seq_len), 1)

    def move_rows(source, chosen, target):
        def some(part, carry):
            start = pl.multiple_of(part * TILE, TILE)
            pick = jnp.where(chosen[pl.ds(start, TILE), :] == column, 1.0, 0.0).astype(bf16)
            target[pl.ds(start, TILE), :] = dot_nn(pick, source[...]).astype(bf16)
            return carry

        lax.fori_loop(0, seq_len // TILE, some, 0)

    move_rows(v.qkv, v.inverse, v.qkv_order)
    near_gather.near()
    near_gather.relay()
    attend_tiles(v.qkv_order, v.table, v.biases[3:4, :], v.biases[4:5, :], v.heads_order)
    move_rows(v.heads_order, v.order, v.heads_stored)
    for part in range(8):
        v.heads[part] = v.heads_stored[part * tok : (part + 1) * tok, :]
    out_swap = SwapHeads(v.heads, v.attended, True, send.take(8), recv.take(8))
    out_swap.start_out()
    for copy in late:
        copy.wait()

    gathers = [GatherRows(ref, send.take(3), recv.take(3)) for ref in (v.rows_b, v.rows_c)]
    sums = [SumRows(v.give.at[k], v.take.at[k], send.take(3), recv.take(3)) for k in range(3)]

    def output_part(r):
        return dot_nn(v.attended[r], v.output_w[...])

    out_swap.wait_rows(3)
    sums[0].give_far(output_part(3))
    out_swap.wait_rows(1)
    sums[0].give_near(output_part(1))
    out_swap.wait_rows(2)
    sums[0].pass_on(output_part(2))
    out_swap.wait_rows(0)
    v.hidden_one[...] = v.tokens[...].astype(f32) + sums[0].total(output_part(0))
    value = v.hidden_one[...]
    v.rows_b[0] = (value * inverse_rms(value) * gain_two).astype(bf16)

    gathers[0].start()
    out_swap.finish_out()
    near_gather.far()
    for part in cross:
        part.finish()
    up_columns.start()
    near_count = v.near.shape[1]

    def near_project(r, carry):
        start = pl.multiple_of(r * near_count, near_count)
        v.cross_pair[pl.ds(start, near_count), :] = dot_nn(v.near[r], v.pair_cols[...]).astype(bf16)
        return carry

    lax.fori_loop(0, 4, near_project, 0)

    def cross_part(r):
        v.cross_q[r * tok : (r + 1) * tok, :] = dot_nn(v.rows_b[r], v.query_cols[...]).astype(bf16)

        def group(g, carry):
            at = pl.multiple_of(r * tok + g * GROUP, GROUP)
            near = pl.multiple_of((r * (tok // GROUP) + g) * NK, NK)
            query = stack_all(v.cross_q[pl.ds(at, GROUP), :])
            shares = cross_shares(query, v.cross_pair[pl.ds(near, NK), 0:cols])
            out = dot_nn(shares.astype(bf16), v.cross_pair[pl.ds(near, NK), cols:])
            v.crossed[pl.ds(at, GROUP), :] = join_all(out).astype(bf16)
            return carry

        lax.fori_loop(0, tok // GROUP, group, 0)
        return dot_nn(v.crossed[r * tok : (r + 1) * tok, :], v.cross_out_w[...])

    def in_turn(gathered, summed, part, between=None):
        v.keep[0] = part(0)
        gathered.near()
        summed.give_near(part(1))
        gathered.relay()
        v.keep[2] = part(2)
        gathered.far()
        summed.give_far(part(3))
        summed.pass_on(v.keep[2])
        if between is not None:
            between()
        return summed.total(v.keep[0])

    v.hidden_two[...] = v.hidden_one[...] + in_turn(gathers[0], sums[1], cross_part)
    value = v.hidden_two[...]
    v.rows_c[0] = (value * inverse_rms(value) * gain_three).astype(bf16)

    gathers[1].start()
    up_columns.finish()

    def feed_part(r):
        part = pl.ds(r * tok, tok)
        v.pre_act[part, :] = dot_nn(v.rows_c[r], v.up_cols[...])
        v.activated[part, :] = gelu_tanh(v.pre_act[part, :]).astype(bf16)
        return dot_nn(v.activated[part, :], v.down_w[...])

    layer_out = v.hidden_two[...] + in_turn(gathers[1], sums[2], feed_part)
    v.layer_out[...] = layer_out

    count_sum.finish()
    error = layer_out - v.teacher[...].astype(f32)
    valid = v.valid[...]
    weighted = valid * error
    v.error[...] = jnp.broadcast_to(jnp.sum(weighted * error, keepdims=True), v.error.shape)
    v.out_grad[...] = (total_tokens / v.count[0:1, 0:1]) * weighted

    middle_back(v, send, recv)


def middle_back(v, send, recv):
    c, w = places_here()
    tok, width = v.tokens.shape
    rows = 4 * tok
    cols = v.output_w.shape[0]
    scale = HEAD_DIM ** (-0.5)
    first, second, third = (
        GatherRows(ref, send.take(3), recv.take(3)) for ref in (v.rows_o, v.rows_two, v.rows_one)
    )
    sum_c, sum_b = (
        SumRows(v.give.at[k], v.take.at[k], send.take(3), recv.take(3)) for k in (3, 4)
    )
    down = CtxSum(send.take(12), recv.take(12), v.down_x, v.down_half, v.down_part, v.down_share)
    up = CtxSum(send.take(12), recv.take(12), v.up_x, v.up_half, v.up_part, v.up_share)
    cross = CtxSum(send.take(12), recv.take(12), v.cross_x, v.cross_half)
    heads = SwapHeads(v.heads_grad, v.heads_out, False, send.take(8), recv.take(8))
    v.rows_o[0] = v.out_grad[...].astype(bf16)

    first.start()

    def feed_back(r):
        part = pl.ds(r * tok, tok)
        act_grad = dot_nt(v.rows_o[r], v.down_w[...])
        v.pre_grad[part, :] = (act_grad * gelu_slope(v.pre_act[part, :])).astype(bf16)
        return dot_nt(v.pre_grad[part, :], v.up_cols[...])

    v.keep[0] = feed_back(0)
    first.near()
    sum_c.give_near(feed_back(1))
    first.relay()
    v.keep[1] = feed_back(2)
    first.far()
    sum_c.give_far(feed_back(3))
    sum_c.pass_on(v.keep[1])
    put_rows(v.down_x, dot_tn(v.activated[...], v.rows_o[...].reshape(rows, width)))
    down.start_y()
    put_shares(v.up_x, dot_tn(v.rows_c[...].reshape(rows, width), v.pre_grad[...]))
    normed_grad = sum_c.total(v.keep[0])
    value = v.hidden_two[...]
    inverse = inverse_rms(value)
    two_grad = v.out_grad[...] + norm_pull(value, inverse, v.gains[2:3, :], normed_grad)
    gain_three = jnp.sum(normed_grad * value * inverse, axis=0, keepdims=True)
    v.keep[1] = two_grad
    v.rows_two[0] = two_grad.astype(bf16)

    second.start()

    def cross_back(r):
        part = slice(r * tok, (r + 1) * tok)
        v.crossed_grad[...] = dot_nt(v.rows_two[r], v.cross_out_w[...]).astype(bf16)

        def group(g, carry):
            within = pl.multiple_of(g * GROUP, GROUP)
            at = pl.multiple_of(r * tok + g * GROUP, GROUP)
            near = pl.ds(pl.multiple_of((r * (tok // GROUP) + g) * NK, NK), NK)
            query = stack_all(v.cross_q[pl.ds(at, GROUP), :])
            grad = stack_all(v.crossed_grad[pl.ds(within, GROUP), :])
            keys = v.cross_pair[near, 0:cols]
            shares = cross_shares(query, keys)
            share_grad = dot_nt(grad, v.cross_pair[near, cols:])
            delta = jnp.sum(shares * share_grad, axis=1, keepdims=True)
            score_grad = (shares * (share_grad - delta)).astype(bf16)
            query_grad = join_all(dot_nn(score_grad, keys)) * scale
            v.query_grad[pl.ds(at, GROUP), :] = query_grad.astype(bf16)
            v.pair_grad[near, 0:cols] = (dot_tn(score_grad, query) * scale).astype(bf16)
            v.pair_grad[near, cols:] = dot_tn(shares.astype(bf16), grad).astype(bf16)
            return carry

        lax.fori_loop(0, tok // GROUP, group, 0)
        return dot_nt(v.query_grad[part, :], v.query_cols[...])

    v.keep[0] = cross_back(0)
    second.near()
    sum_b.give_near(cross_back(1))
    second.relay()
    v.keep[2] = cross_back(2)
    second.far()
    sum_b.give_far(cross_back(3))
    sum_b.pass_on(v.keep[2])
    down.finish_y()
    down.start_z()
    up.start_y()
    normed_b = v.rows_b[...].reshape(rows, width)
    put_rows(v.cross_out_x, dot_tn(v.crossed[...], v.rows_two[...].reshape(rows, width)))
    put_shares(v.cross_x, dot_tn(normed_b, v.query_grad[...]), 0)
    normed_grad = sum_b.total(v.keep[0])
    value = v.hidden_one[...]
    inverse = inverse_rms(value)
    one_grad = v.keep[1] + norm_pull(value, inverse, v.gains[1:2, :], normed_grad)
    gain_two = jnp.sum(normed_grad * value * inverse, axis=0, keepdims=True)
    v.gain_grad[...] = jnp.concatenate(
        [gain_two, gain_three, jnp.zeros((6, gain_two.shape[1]), f32)], axis=0
    )
    v.one_grad[...] = one_grad
    v.rows_one[0] = one_grad.astype(bf16)

    third.start()
    near = v.near[...].reshape(-1, width)
    put_shares(v.cross_x, dot_tn(near, v.pair_grad[...]), cols)

    def head_back(r):
        v.heads_out[r] = dot_nt(v.rows_one[r], v.output_w[...]).astype(bf16)
        heads.start_in(r)

    head_back(0)
    third.near()
    head_back(1)
    third.relay()
    head_back(2)
    third.far()
    head_back(3)
    up.finish_y()
    up.start_z()
    cross.start_y()
    attended = jnp.concatenate([v.attended[r] for r in range(4)], axis=0)
    put_rows(v.output_x, dot_tn(attended, v.rows_one[...].reshape(rows, width)))
    heads.finish_in()
    down.finish_z()
    up.finish_z()
    cross.finish_y()


def layer(total_tokens, given, collective_id):
    tok, width = given["tokens"].shape
    hidden = given["down_any"].shape[0]
    cols = given["output_any"].shape[0]
    near = given["neighbours"].shape[0]
    seq_len = 8 * tok
    rows = 4 * tok
    padded = -(-(width // 32) // 8) * 8
    any_space = pl.BlockSpec(memory_space=pl.ANY)
    shape = jax.ShapeDtypeStruct
    vmem = pltpu.VMEM
    dma = pltpu.SemaphoreType.DMA
    results = dict(
        layer_out=shape((tok, width), f32),
        error=shape((8, 128), f32),
        count=shape((8, 128), f32),
        qkv=shape((seq_len, 384), bf16),
        table=shape((seq_len + TILE, 128), bf16),
        biases=shape((8, 128), f32),
        gains=shape((8, width), f32),
        normed_a=shape((seq_len, width), bf16),
        pair_cols=shape((width, 2 * cols), bf16),
        one_grad=shape((tok, width), f32),
        gain_grad=shape((8, width), f32),
        heads_grad=shape((8, tok, 128), bf16),
        pair_grad=shape((4 * near, 2 * cols), bf16),
        down_share=shape((hidden // 8, width), bf16),
        up_share=shape((4, padded, hidden), bf16),
        cross_half=shape((4, 4, padded, 3 * cols), bf16),
        cross_out_x=shape((4, 2, cols // 8, width), bf16),
        output_x=shape((4, 2, cols // 8, width), bf16),
    )
    scratch = dict(
        small_all=vmem(given["small"].shape, f32),
        small_near=vmem((3,) + given["small"].shape, f32),
        count_far=vmem((7, 8, 128), f32),
        tokens_all=vmem((8, tok, width), bf16),
        pair=vmem((width, 512), bf16),
        waves=vmem((seq_len, width), bf16),
        qkv_order=vmem((seq_len, 384), bf16),
        heads_order=vmem((seq_len, 128), bf16),
        heads_stored=vmem((seq_len, 128), bf16),
        heads=vmem((8, tok, 128), bf16),
        attended=vmem((4, tok, cols), bf16),
        near=vmem((4, near, width), bf16),
        query_cols=vmem((width, cols), bf16),
        up_cols=vmem((width, hidden), bf16),
        output_w=vmem((cols, width), bf16),
        cross_out_w=vmem((cols, width), bf16),
        down_w=vmem((hidden, width), bf16),
        cross_pair=vmem((4 * near, 2 * cols), bf16),
        cross_q=vmem((rows, cols), bf16),
        crossed=vmem((rows, cols), bf16),
        crossed_grad=vmem((tok, cols), bf16),
        hidden_one=vmem((tok, width), f32),
        hidden_two=vmem((tok, width), f32),
        out_grad=vmem((tok, width), f32),
        pre_act=vmem((rows, hidden), f32),
        activated=vmem((rows, hidden), bf16),
        rows_b=vmem((4, tok, width), bf16),
        rows_c=vmem((4, tok, width), bf16),
        rows_o=vmem((4, tok, width), bf16),
        rows_two=vmem((4, tok, width), bf16),
        rows_one=vmem((4, tok, width), bf16),
        give=vmem((5, 3, tok, width), bf16),
        take=vmem((5, 3, tok, width), bf16),
        keep=vmem((3, tok, width), f32),
        pre_grad=vmem((rows, hidden), bf16),
        query_grad=vmem((rows, cols), bf16),
        heads_out=vmem((4, tok, cols), bf16),
        down_x=vmem((4, 2, hidden // 8, width), bf16),
        down_half=vmem((4, hidden // 8, width), bf16),
        down_part=vmem((3, hidden // 8, width), bf16),
        up_x=vmem((4, 2, 4, padded, hidden), bf16),
        up_half=vmem((4, 4, padded, hidden), bf16),
        up_part=vmem((3, 4, padded, hidden), bf16),
        cross_x=vmem((4, 2, 4, padded, 3 * cols), bf16),
        send=dma((200,)),
        recv=dma((200,)),
        local=dma((8,)),
    )
    names = [*given, *results, *scratch]
    specs = [
        any_space if name.endswith("_any") or name == "neighbours" else in_vmem for name in given
    ]
    got = pl.pallas_call(
        functools.partial(layer_kernel, names, total_tokens),
        out_shape=list(results.values()),
        in_specs=specs,
        out_specs=[in_vmem] * len(results),
        scratch_shapes=list(scratch.values()),
        compiler_params=pltpu.CompilerParams(
            collective_id=collective_id, has_side_effects=True, vmem_limit_bytes=62 * 2**20
        ),
        name="layer",
    )(*given.values())
    return types.SimpleNamespace(**dict(zip(results, got, strict=True)))


class Spread:

    def __init__(self, share, out, send, recv):
        self.share, self.out, self.send, self.recv = share, out, send, recv
        self.c, self.w = places_here()

    def columns(self, place):
        width = self.share.shape[2]
        return self.out.at[self.c, :, pl.ds(pl.multiple_of(place * width, 128), width)]

    def copy(self, j, place):
        return remote(
            self.share.at[self.w ^ j],
            self.columns(place),
            self.send.at[j],
            self.recv.at[j],
            self.c,
            self.w ^ j,
        )

    def own(self):
        return pltpu.make_async_copy(
            self.share.at[self.w], self.columns(self.w), self.send.at[0]
        )

    def start(self):
        for j in (2, 3, 1):
            self.copy(j, self.w).start()
        self.own().start()

    def finish(self):
        self.own().wait()
        for j in (1, 2, 3):
            self.copy(j, self.w).wait_send()
            self.copy(j, self.w ^ j).wait_recv()


class Whole:

    def __init__(self, source, target, send, recv):
        self.source, self.target, self.send, self.recv = source, target, send, recv
        self.c, self.w = places_here()

    def put(self, place):
        rows = self.source.shape[0]
        return self.target.at[pl.ds(pl.multiple_of(place * rows, 32), rows), :]

    def copy(self, j, place):
        return remote(
            self.source, self.put(place), self.send.at[j], self.recv.at[j], self.c, self.w ^ j
        )

    def passed(self, place):
        ref = self.put(place)
        return remote(ref, ref, self.send.at[3], self.recv.at[3], self.c, self.w ^ 1)

    def own(self):
        return pltpu.make_async_copy(self.source, self.put(self.w), self.send.at[0])

    def start(self):
        self.copy(2, self.w).start()
        self.copy(1, self.w).start()
        self.own().start()

    def relay(self):
        self.copy(2, self.w).wait_send()
        self.copy(2, self.w ^ 2).wait_recv()
        self.passed(self.w ^ 2).start()

    def finish(self):
        self.own().wait()
        self.copy(1, self.w).wait_send()
        self.copy(1, self.w ^ 1).wait_recv()
        self.passed(self.w ^ 2).wait_send()
        self.passed(self.w ^ 3).wait_recv()


class MaskSum:

    def __init__(self, ref, got, masks, send, recv):
        self.ref, self.got, self.masks, self.send, self.recv = ref, got, masks, send, recv
        self.c, self.w = places_here()

    def copy(self, k):
        ctx, wa = self.masks[k]
        return remote(
            self.ref, self.got.at[k], self.send.at[k], self.recv.at[k], self.c ^ ctx, self.w ^ wa
        )

    def start(self):
        for k in range(len(self.masks)):
            self.copy(k).start()

    def finish(self):
        for k in range(len(self.masks)):
            self.copy(k).wait()
        self.ref[...] = tree_sum([self.ref[...]] + [self.got[k] for k in range(len(self.masks))])


def finish_kernel(names, *refs):
    v = types.SimpleNamespace(**dict(zip(names, refs, strict=True)))
    c, w = places_here()
    send, recv, local = Pool(v.send), Pool(v.recv), Pool(v.local)
    tok, width = v.tokens.shape
    cols = v.output_x.shape[2] * 8
    share = width // 4

    def load(source, target):
        copy = pltpu.make_async_copy(source, target, local.take(1).at[0])
        copy.start()
        return copy

    loads = [load(v.normed_a_any, v.normed_a), load(v.waves_any, v.waves)]
    late = [load(v.pair_cols_any, v.pair_cols), load(v.near_any, v.near_rows)]

    def line(out):
        return LineGather(out, send.take(13), recv.take(13))

    def summed(x, half, part, got):
        return CtxSum(send.take(12), recv.take(12), x, half, part, got)

    down, up, cross, ctx_o, out_o, pair = (
        line(out)
        for out in (v.down_out, v.up_all, v.cross_all, v.cross_o_out, v.output_out, v.pair_all)
    )
    cross_sum = summed(None, v.cross_half, v.cross_part, v.cross_share)
    ctx_o_sum = summed(v.cross_out_x, v.ctx_o_half, v.ctx_o_part, v.ctx_o_share)
    out_o_sum = summed(v.output_x, v.out_o_half, v.out_o_part, v.out_o_share)
    up_spread = Spread(v.up_share, v.up_all, send.take(4), recv.take(4))
    cross_spread = Spread(v.cross_share, v.cross_all, send.take(4), recv.take(4))
    sum_pair = SumRows(v.pair_give, v.pair_take, send.take(3), recv.take(3))
    sum_near = SumRows(v.near_give, v.near_take, send.take(3), recv.take(3))
    weights = [
        Whole(weight, v.full.at[m], send.take(4), recv.take(4))
        for m, weight in enumerate((v.query_any, v.key_any, v.value_any))
    ]
    stages = [
        MaskSum(v.total, got, masks, send.take(3), recv.take(3))
        for got, masks in (
            (v.got_wa, ((0, 1), (0, 2), (0, 3))),
            (v.got_y, ((1, 0),)),
            (v.got_z, ((2, 0), (4, 0), (6, 0))),
        )
    ]
    b_send, b_recv = send.take(24), recv.take(24)

    def block_copy(j, m, place):
        return remote(
            v.query_grad.at[c ^ j, :, 128 * m : 128 * (m + 1)],
            v.mine.at[m, :, pl.ds(pl.multiple_of(place * 128, 128), 128)],
            b_send.at[3 * j + m],
            b_recv.at[3 * j + m],
            c ^ j,
            w,
        )

    own_blocks = [
        pltpu.make_async_copy(
            v.query_grad.at[c, :, 128 * m : 128 * (m + 1)],
            v.mine.at[m, :, pl.ds(pl.multiple_of(c * 128, 128), 128)],
            b_recv.at[m],
        )
        for m in range(3)
    ]
    v.down_out[c] = v.down_share[...]
    meet_lines()
    ctx_o_sum.start_y()
    out_o_sum.start_y()
    down.start()
    up_spread.start()
    cross_sum.start_z()
    for copy in own_blocks:
        copy.start()

    query_grad = v.query_grad[...].reshape(-1, v.query_grad.shape[2])
    high = v.table_grad[...].astype(bf16)
    low = (v.table_grad[...] - high.astype(f32)).astype(bf16)
    for copy in loads:
        copy.wait()
    mixed = dot_tn(v.normed_a[...], query_grad)
    turned = dot_tn(v.waves[...], high) + dot_tn(v.waves[...], low)
    for place in range(4):
        at = place * share
        v.sums[place] = jnp.concatenate([mixed[at : at + share], turned[at : at + share]], axis=1)
    sum_pair.give_far(v.sums[w ^ 3])
    sum_pair.give_near(v.sums[w ^ 1])
    up_spread.finish()
    up.start()
    sum_pair.pass_on(v.sums[w ^ 2])
    ctx_o_sum.finish_y()
    ctx_o_sum.start_z()
    out_o_sum.finish_y()
    out_o_sum.start_z()
    down.step(0)
    for j in (4, 6, 5, 7, 2, 3, 1):
        for m in range(3):
            block_copy(j, m, c).start()
    v.pair_all[c] = sum_pair.total(v.sums[w]).astype(bf16)
    pair.start()
    for copy in late:
        copy.wait()
    near_count = v.near_grad.shape[0]

    def near_part(r):
        return dot_nt(v.near_rows[r * near_count : (r + 1) * near_count, :], v.pair_cols[...])

    sum_near.give_far(near_part(3))
    sum_near.give_near(near_part(1))
    sum_near.pass_on(near_part(2))
    for weight in weights:
        weight.start()
    v.near_grad[...] = near_part(0)
    up.step(0)
    cross_sum.finish_z()
    cross_spread.start()
    down.step(1)
    ctx_o_sum.finish_z()
    v.cross_o_out[c] = v.ctx_o_share[...]
    ctx_o.start()
    out_o_sum.finish_z()
    v.output_out[c] = v.out_o_share[...]
    out_o.start()
    cross_spread.finish()
    cross.start()
    up.step(1)
    pair.step(0)
    down.step(2)
    ctx_o.step(0)
    out_o.step(0)
    cross.step(0)
    up.step(2)
    pair.step(1)
    ctx_o.step(1)
    out_o.step(1)

    for j in range(1, 8):
        for m in range(3):
            block_copy(j, m, c ^ j).wait_recv()
    for copy in own_blocks:
        copy.wait()
    cross.step(1)
    pair.step(2)
    for weight in weights:
        weight.relay()
    for weight in weights:
        weight.finish()
    normed_grad = dot_nt(v.mine[0], v.full[0])
    normed_grad = normed_grad + dot_nt(v.mine[1], v.full[1])
    normed_grad = normed_grad + dot_nt(v.mine[2], v.full[2])
    hidden = v.tokens[...].astype(f32)
    inverse = inverse_rms(hidden)
    v.tokens_grad[...] = v.one_grad[...] + norm_pull(hidden, inverse, v.gains[0:1, :], normed_grad)
    v.total[...] = v.small[...]
    v.total[0:1, 0:width] = jnp.sum(normed_grad * hidden * inverse, axis=0, keepdims=True)
    stages[0].start()
    ctx_o.step(2)
    out_o.step(2)
    cross.step(2)
    stages[0].finish()
    stages[1].start()
    v.near_grad[...] = sum_near.total(v.near_grad[...])
    stages[1].finish()
    stages[2].start()
    down.finish()
    up.finish()
    used = share // 8

    def lay_up(part, at):
        v.up_out[at : at + used, :] = v.up_all[part, 0:used, :].astype(f32)

    for part in range(8):
        lay_up(part, part * used)
    pair.finish()
    for part in range(8):
        for m in range(4):
            v.pair_out[m, :, 128 * part : 128 * (part + 1)] = v.pair_all[
                part, :, 128 * m : 128 * (m + 1)
            ]
    ctx_o.finish()
    out_o.finish()
    cross.finish()
    for part in range(8):
        for m in range(3):
            for place in range(4):
                at = (place * 3 + m) * cols
                v.cross_out[m, part * used : (part + 1) * used, place * cols : (place + 1) * cols] = (
                    v.cross_all[part, 0:used, at : at + cols].astype(f32)
                )
    stages[2].finish()
    for j in range(1, 8):
        for m in range(3):
            block_copy(j, m, c).wait_send()


def finish(given, collective_id):
    tok, width = given["tokens"].shape
    near = given["near_any"].shape[0]
    padded = given["up_share"].shape[1]
    hidden = given["up_share"].shape[2]
    cols = given["output_x"].shape[2] * 8
    share = width // 4
    any_space = pl.BlockSpec(memory_space=pl.ANY)
    shape = jax.ShapeDtypeStruct
    vmem = pltpu.VMEM
    dma = pltpu.SemaphoreType.DMA
    part = (cols // 8, width)
    results = dict(
        tokens_grad=shape((tok, width), f32),
        near_grad=shape((near // 4, width), f32),
        total=shape(given["small"].shape, f32),
        down_out=shape((8,) + given["down_share"].shape, bf16),
        up_out=shape((share, 4 * hidden), f32),
        cross_out=shape((3, share, 4 * cols), f32),
        cross_o_out=shape((8,) + part, bf16),
        output_out=shape((8,) + part, bf16),
        pair_out=shape((4, share, 1024), bf16),
    )
    scratch = dict(
        normed_a=vmem(given["normed_a_any"].shape, bf16),
        waves=vmem(given["waves_any"].shape, bf16),
        pair_cols=vmem(given["pair_cols_any"].shape, bf16),
        near_rows=vmem(given["near_any"].shape, bf16),
        full=vmem((3, width, 1024), bf16),
        mine=vmem((3, tok, 1024), bf16),
        sums=vmem((4, share, 512), f32),
        up_all=vmem((8, padded, 4 * hidden), bf16),
        cross_all=vmem((8, padded, 12 * cols), bf16),
        pair_all=vmem((8, share, 512), bf16),
        cross_part=vmem((3, 4, padded, 3 * cols), bf16),
        cross_share=vmem((4, padded, 3 * cols), bf16),
        ctx_o_half=vmem((4,) + part, bf16),
        ctx_o_part=vmem((3,) + part, bf16),
        ctx_o_share=vmem(part, bf16),
        out_o_half=vmem((4,) + part, bf16),
        out_o_part=vmem((3,) + part, bf16),
        out_o_share=vmem(part, bf16),
        pair_give=vmem((3, share, 512), bf16),
        pair_take=vmem((3, share, 512), bf16),
        near_give=vmem((3, near // 4, width), bf16),
        near_take=vmem((3, near // 4, width), bf16),
        got_wa=vmem((3,) + given["small"].shape, f32),
        got_y=vmem((1,) + given["small"].shape, f32),
        got_z=vmem((3,) + given["small"].shape, f32),
        send=dma((184,)),
        recv=dma((184,)),
        local=dma((4,)),
    )
    names = [*given, *results, *scratch]
    got = pl.pallas_call(
        functools.partial(finish_kernel, names),
        out_shape=list(results.values()),
        in_specs=[any_space if name.endswith("_any") else in_vmem for name in given],
        out_specs=[in_vmem] * len(results),
        scratch_shapes=list(scratch.values()),
        compiler_params=pltpu.CompilerParams(
            collective_id=collective_id, has_side_effects=True, vmem_limit_bytes=62 * 2**20
        ),
        name="finish",
    )(*given.values())
    return types.SimpleNamespace(**dict(zip(results, got, strict=True)))


def skew(wide, count):
    lead = wide.shape[:-2]
    rows, span = wide.shape[-2:]
    edge = [(0, 0)] * len(lead)
    padded = jnp.pad(wide, edge + [(0, 0), (0, 1)])
    flat = padded.reshape(lead + (rows * (span + 1),))
    flat = lax.slice_in_dim(flat, rows - 1, rows - 1 + rows * span, axis=len(lead))
    return flat.reshape(lead + (rows, span))[..., :count]


def unskew(grad, span):
    lead = grad.shape[:-2]
    rows, count = grad.shape[-2:]
    edge = [(0, 0)] * len(lead)
    wide = jnp.pad(grad, edge + [(0, 0), (0, span - count)])
    flat = jnp.pad(wide.reshape(lead + (rows * span,)), edge + [(rows - 1, 1)])
    return flat.reshape(lead + (rows, span + 1))[..., :span]


def tile_scores(content_rows, position_rows, key_rows, relative, row_start, key_start):
    rows = content_rows.shape[0]
    count = key_rows.shape[0]
    scale = content_rows.shape[-1] ** (-0.5)
    content = jnp.einsum("qhe,khe->hqk", content_rows, key_rows, preferred_element_type=f32)
    wide = jnp.einsum("qhe,whe->hqw", position_rows, relative, preferred_element_type=f32)
    scores = (content + skew(wide, count)) * scale
    causal = (row_start + jnp.arange(rows))[:, None] >= (key_start + jnp.arange(count))[None, :]
    return (scores, causal[None])


def tile_forward(
    content_rows, position_rows, row_start, relative, key_rows, value_rows, key_start, state
):
    top, total, accum = state
    scores, causal = tile_scores(
        content_rows, position_rows, key_rows, relative, row_start, key_start
    )
    scores = jnp.where(causal, scores, neg_big)
    new_top = jnp.maximum(top, jnp.max(scores, axis=-1))
    raised = jnp.where(causal, jnp.exp(scores - new_top[..., None]), 0.0)
    fade = jnp.exp(top - new_top)
    total = total * fade + jnp.sum(raised, axis=-1)
    accum = accum * fade[..., None] + jnp.einsum(
        "hqk,khe->hqe", raised.astype(bf16), value_rows, preferred_element_type=f32
    )
    return (new_top, total, accum)


def tile_backward(
    content_rows,
    position_rows,
    row_start,
    relative,
    key_rows,
    value_rows,
    grad_rows,
    log_rows,
    delta_rows,
    key_start,
):
    scores, causal = tile_scores(
        content_rows, position_rows, key_rows, relative, row_start, key_start
    )
    scale = content_rows.shape[-1] ** (-0.5)
    shares = jnp.where(causal, jnp.exp(scores - log_rows[..., None]), 0.0)
    share_grad = jnp.einsum("qhe,khe->hqk", grad_rows, value_rows, preferred_element_type=f32)
    score_grad = (shares * (share_grad - delta_rows[..., None])).astype(bf16)
    content_grad = jnp.einsum("hqk,khe->qhe", score_grad, key_rows, preferred_element_type=f32)
    wide_grad = unskew(score_grad, relative.shape[0])
    position_grad = jnp.einsum("hqw,whe->qhe", wide_grad, relative, preferred_element_type=f32)
    table_part = jnp.einsum("hqw,qhe->whe", wide_grad, position_rows, preferred_element_type=f32)
    key_grad = jnp.einsum("hqk,qhe->khe", score_grad, content_rows, preferred_element_type=f32)
    value_grad = jnp.einsum(
        "hqk,qhe->khe", shares.astype(bf16), grad_rows, preferred_element_type=f32
    )
    return (
        content_grad * scale,
        position_grad * scale,
        table_part * scale,
        key_grad * scale,
        value_grad,
    )


def nest_tiles(tile_fn):
    inner = jax.vmap(tile_fn, in_axes=(0, 0, 0, 0, None, None, 0))
    return jax.vmap(inner, in_axes=(0, 0, None, None, 0, 0, 0))


def to_global(stored, inverse, block):
    seqs, seq_len, width = stored.shape
    blocks = stored.reshape(seqs, seq_len // block, block * width)
    chosen = (inverse[:, None] == jnp.arange(seq_len // block)[None, :]).astype(bf16)
    moved = jnp.einsum("gs,nsx->ngx", chosen, blocks, preferred_element_type=f32)
    return moved.astype(bf16).reshape(stored.shape)


class SplitQueries:

    def __init__(self, query, keys, values, biases, relative, block_order, inverse, block):
        self.seqs, self.tok_dev, self.width = keys.shape
        self.heads = self.width // HEAD_DIM
        self.block = block
        self.block_order = block_order
        ctx_count = lax.axis_size("ctx")
        self.seq_len = self.tok_dev * ctx_count
        self.key_len = min(512, self.seq_len)
        pad = jnp.zeros((self.key_len + block, self.width), bf16)
        table = jnp.concatenate([relative, pad], axis=0)
        self.table = table.reshape(-1, self.heads, HEAD_DIM)
        lead = (self.seqs, 2, block, self.heads, HEAD_DIM)
        self.content = (query + biases[0]).astype(bf16).reshape(lead)
        self.position = (query + biases[1]).astype(bf16).reshape(lead)
        gathered = [lax.all_gather(part, "ctx", axis=1, tiled=True) for part in (keys, values)]
        shape = (self.seqs, self.seq_len, self.heads, HEAD_DIM)
        self.keys, self.values = [to_global(part, inverse, block).reshape(shape) for part in gathered]
        self.starts = lax.dynamic_slice_in_dim(block_order, 2 * lax.axis_index("ctx"), 2, 0) * block

    def rows(self, index):
        start = index * self.key_len
        keys = lax.dynamic_slice_in_dim(self.keys, start, self.key_len, 1)
        values = lax.dynamic_slice_in_dim(self.values, start, self.key_len, 1)
        span = self.block + self.key_len
        offsets = [self.seq_len - self.block - self.starts[slot] + start for slot in range(2)]
        relative = [lax.dynamic_slice_in_dim(self.table, offset, span, 0) for offset in offsets]
        return start, keys, values, jnp.stack(relative), offsets

    def to_stored(self, part):
        count = self.seq_len // self.block
        blocks = part.reshape(self.seqs, count, self.block * self.width)
        chosen = (self.block_order[:, None] == jnp.arange(count)[None, :]).astype(f32)
        moved = jnp.einsum("sg,ngx->nsx", chosen, blocks, precision=highest)
        return moved.reshape(self.seqs, self.seq_len, self.width)

    def forward(self):
        def step(state, index):
            start, keys, values, relative, _ = self.rows(index)

            def tile(content, position, row_start, table, keys_seq, values_seq, tile_state):
                return tile_forward(
                    content, position, row_start, table, keys_seq, values_seq, start, tile_state
                )

            return nest_tiles(tile)(
                self.content, self.position, self.starts, relative, keys, values, state
            ), None

        shape = (self.seqs, 2, self.heads, self.block)
        state = (
            jnp.full(shape, neg_big, f32),
            jnp.zeros(shape, f32),
            jnp.zeros(shape + (HEAD_DIM,), f32),
        )
        (top, total, accum), _ = lax.scan(step, state, jnp.arange(self.seq_len // self.key_len))
        self.log_total = top + jnp.log(total)
        self.out = accum / total[..., None]
        moved = jnp.transpose(self.out, (0, 1, 3, 2, 4))
        return moved.reshape(self.seqs * self.tok_dev, self.width).astype(bf16)

    def backward(self, grad):
        block, seq_len, key_len = self.block, self.seq_len, self.key_len
        lead = (self.seqs, 2, block, self.heads, HEAD_DIM)
        grad = grad.reshape(lead)
        delta = jnp.einsum("sbqhe,sbhqe->sbhq", grad.astype(f32), self.out)
        def step(carry, index):
            start, keys, values, relative, offsets = self.rows(index)

            def tile(content, position, row_start, table, keys_seq, values_seq, extra):
                return tile_backward(
                    content, position, row_start, table, keys_seq, values_seq, *extra, start
                )

            extra = (grad, self.log_total, delta)
            parts = nest_tiles(tile)(
                self.content, self.position, self.starts, relative, keys, values, extra
            )
            table = carry[2]
            table_sum = jnp.sum(parts[2], axis=0)
            for slot in range(2):
                offset = offsets[slot]
                current = lax.dynamic_slice_in_dim(table, offset, block + key_len, 0)
                table = lax.dynamic_update_slice_in_dim(table, current + table_sum[slot], offset, 0)
            sums = []
            for total, part in zip(carry[3:], parts[3:]):
                current = lax.dynamic_slice_in_dim(total, start, key_len, 1)
                part = current + jnp.sum(part, axis=1)
                sums.append(lax.dynamic_update_slice_in_dim(total, part, start, 1))
            key_acc, value_acc = sums
            return (carry[0] + parts[0], carry[1] + parts[1], table, key_acc, value_acc), None

        zero_tiles = jnp.zeros(lead, f32)
        zero_keys = jnp.zeros((self.seqs, seq_len, self.heads, HEAD_DIM), f32)
        carry = (zero_tiles, zero_tiles, jnp.zeros(self.table.shape, f32), zero_keys, zero_keys)
        carry, _ = lax.scan(step, carry, jnp.arange(seq_len // key_len))
        owned = [
            lax.psum_scatter(
                self.to_stored(part), "ctx", scatter_dimension=1, tiled=True
            )
            for part in carry[3:]
        ]
        flat = (self.seqs * self.tok_dev, self.width)
        query_grad = (carry[0] + carry[1]).reshape(flat).astype(bf16)
        key_grad, value_grad = [part.reshape(flat).astype(bf16) for part in owned]
        bias_grads = jnp.stack(
            [jnp.sum(part, axis=(0, 1, 2)).reshape(self.width) for part in carry[:2]]
        )
        table_grad = carry[2].reshape(-1, self.width)[:seq_len]
        return query_grad, key_grad, value_grad, bias_grads, table_grad


def local_general(
    tokens,
    neighbours,
    teacher,
    valid_mask,
    block_order,
    query_weight,
    key_weight,
    value_weight,
    output_weight,
    relative_weight,
    content_bias,
    position_bias,
    cross_query_weight,
    cross_key_weight,
    cross_value_weight,
    cross_output_weight,
    up_weight,
    down_weight,
    attention_gain,
    cross_gain,
    feedforward_gain,
):
    places = lax.axis_size("wa")
    ctx_count = lax.axis_size("ctx")
    place = lax.axis_index("wa")
    here = lax.axis_index("ctx")
    _, tok_dev, width = tokens.shape
    seq_len = tok_dev * ctx_count
    block = tok_dev // 2
    cols = HEADS * HEAD_DIM // places
    rows = places * tok_dev

    token_parts = gather_parts(tokens[0])
    query_cols, key_cols, value_cols = [
        take_columns(weight) for weight in (query_weight, key_weight, value_weight)
    ]
    relative_cols = take_columns(relative_weight)
    gains = lax.all_gather(
        jnp.stack([attention_gain, cross_gain, feedforward_gain]), "wa", axis=1, tiled=True
    ).astype(f32)
    gain_one, gain_two, gain_three = gains[0:1], gains[1:2], gains[2:3]
    cross_query_cols, cross_key_cols, cross_value_cols = [
        take_columns(weight) for weight in (cross_query_weight, cross_key_weight, cross_value_weight)
    ]
    cross_pair_cols = jnp.concatenate([cross_key_cols, cross_value_cols], axis=1)
    near_rows = jnp.concatenate(gather_parts(neighbours.reshape(-1, width)), axis=0)
    up_cols = take_columns(up_weight)
    valid = valid_mask.astype(f32).reshape(tok_dev, 1)
    count = jnp.sum(valid).reshape(1, 1)
    count = all_summed(all_summed(count, "wa"), "ctx")

    slots = jnp.arange(2 * ctx_count)
    inverse = jnp.sum(jnp.where(block_order[None, :] == slots[:, None], slots[None, :], 0), axis=1)
    inverse = inverse.astype(jnp.int32)
    distance = (seq_len - 1 - jnp.arange(seq_len)).astype(f32)
    waves = sinusoid(distance, width).astype(bf16)

    hidden_all = jnp.concatenate(token_parts, axis=0).astype(f32)
    scale_all = inverse_rms(hidden_all)
    normed_a = (hidden_all * scale_all * gain_one).astype(bf16)
    biases = jnp.stack([content_bias, position_bias]).astype(f32)
    mixed_cols = jnp.concatenate([query_cols, key_cols, value_cols], axis=1)
    qkv = dot_nn(normed_a, mixed_cols).reshape(places, tok_dev, 3 * cols)
    relative = dot_nn(waves, relative_cols).astype(bf16)
    general = SplitQueries(
        qkv[..., :cols],
        qkv[..., cols : 2 * cols].astype(bf16),
        qkv[..., 2 * cols :].astype(bf16),
        biases,
        relative,
        block_order,
        inverse,
        block,
    )
    attended = general.forward()

    def to_owner(product):
        return scatter_parts([product[r * tok_dev : (r + 1) * tok_dev] for r in range(places)])

    def from_all(value):
        return jnp.concatenate(gather_parts(value), axis=0)

    hidden_in = tokens[0].astype(f32)
    hidden_one = hidden_in + to_owner(dot_nn(attended, output_weight))

    scale_two = inverse_rms(hidden_one)
    normed_b = from_all((hidden_one * scale_two * gain_two).astype(bf16))
    cross_q = dot_nn(normed_b, cross_query_cols).astype(bf16)
    cross_pair = dot_nn(near_rows, cross_pair_cols).astype(bf16)
    crossed = cross_forward(cross_q, cross_pair)
    hidden_two = hidden_one + to_owner(dot_nn(crossed, cross_output_weight))

    scale_three = inverse_rms(hidden_two)
    normed_c = from_all((hidden_two * scale_three * gain_three).astype(bf16))
    pre_act = dot_nn(normed_c, up_cols)
    activated = gelu_tanh(pre_act).astype(bf16)
    layer_out = hidden_two + to_owner(dot_nn(activated, down_weight))

    error = layer_out - teacher[0].astype(f32)
    error_sum = jnp.sum(valid * error * error).reshape(1, 1)
    error_sum = all_summed(all_summed(error_sum, "wa"), "ctx")
    loss = (error_sum / (2.0 * count * width)).reshape(())
    out_grad = (places * seq_len) / count * valid * error

    out_low = from_all(out_grad.astype(bf16))
    act_grad = dot_nt(out_low, down_weight)
    _, gelu_pull = jax.vjp(gelu_tanh, pre_act)
    pre_grad = gelu_pull(act_grad)[0].astype(bf16)
    down_grad = dot_tn(activated, out_low).astype(bf16)
    up_grad = dot_tn(normed_c, pre_grad).astype(bf16)
    normed_c_grad = to_owner(dot_nt(pre_grad, up_cols))
    two_grad = out_grad + norm_pull(hidden_two, scale_three, gain_three, normed_c_grad)
    gain_three_grad = jnp.sum(normed_c_grad * hidden_two * scale_three, axis=0, keepdims=True)
    down_out = sum_row_grads(down_grad)
    up_out = sum_column_grads(up_grad[None])[0]

    two_low = from_all(two_grad.astype(bf16))
    crossed_grad = dot_nt(two_low, cross_output_weight).astype(bf16)
    cross_q_grad, cross_pair_grad = cross_backward(cross_q, cross_pair, crossed_grad)
    normed_b_grad = to_owner(dot_nt(cross_q_grad, cross_query_cols))
    one_grad = two_grad + norm_pull(hidden_one, scale_two, gain_two, normed_b_grad)
    gain_two_grad = jnp.sum(normed_b_grad * hidden_one * scale_two, axis=0, keepdims=True)
    cross_output_grad = dot_tn(crossed, two_low).astype(bf16)
    cross_query_grad = dot_tn(normed_b, cross_q_grad).astype(bf16)
    cross_key_grad = dot_tn(near_rows, cross_pair_grad[:, :cols]).astype(bf16)
    cross_value_grad = dot_tn(near_rows, cross_pair_grad[:, cols:]).astype(bf16)
    cross_output_out = sum_row_grads(cross_output_grad)
    cross_out = sum_column_grads(jnp.stack([cross_key_grad, cross_value_grad]))
    cross_query_out = sum_column_grads(cross_query_grad[None])[0]
    near_grad = dot_nt(cross_pair_grad, cross_pair_cols)
    near_count = near_rows.shape[0] // places
    near_grad = scatter_parts(
        [near_grad[r * near_count : (r + 1) * near_count] for r in range(places)]
    )
    neighbours_grad = near_grad.reshape(neighbours.shape)

    one_low = from_all(one_grad.astype(bf16))
    attended_grad = dot_nt(one_low, output_weight).astype(bf16)
    output_grad = dot_tn(attended, one_low).astype(bf16)
    output_out = sum_row_grads(output_grad)
    query_grad, key_grad, value_grad, bias_grads, table_grad = general.backward(attended_grad)
    qkv_grad = jnp.concatenate([query_grad, key_grad, value_grad], axis=1)
    table_high = table_grad.astype(bf16)
    table_low = (table_grad - table_high.astype(f32)).astype(bf16)
    relative_grad = (dot_tn(waves, table_high) + dot_tn(waves, table_low)).astype(bf16)
    mixed_grad = dot_tn(normed_a, qkv_grad).astype(bf16)
    whole = [mixed_grad[:, m * cols : (m + 1) * cols] for m in range(3)]
    attention_out = sum_column_grads(jnp.stack(whole + [relative_grad]))
    normed_a_part = dot_nt(qkv_grad, mixed_cols)
    gain_one_part = jnp.sum(normed_a_part * hidden_all * scale_all, axis=0, keepdims=True)
    normed_a_grad = to_owner(normed_a_part)
    tokens_grad = one_grad + norm_pull(hidden_in, scale_all[:tok_dev], gain_one, normed_a_grad)

    gain_grads = jnp.concatenate([gain_one_part, gain_two_grad, gain_three_grad], axis=0)
    gain_grads = all_summed(gain_grads, "wa")
    share = width // places
    gain_grads = lax.dynamic_slice_in_dim(gain_grads, place * share, share, 1)
    small = jnp.concatenate([gain_grads.reshape(1, -1), bias_grads.reshape(1, -1)], axis=1)
    small = all_summed(small, "ctx")[0]
    gain_out = small[: 3 * share].reshape(3, share)
    bias_out = small[3 * share :].reshape(2, cols)

    return (
        layer_out[None],
        loss,
        tokens_grad[None],
        neighbours_grad,
        attention_out[0],
        attention_out[1],
        attention_out[2],
        output_out,
        attention_out[3],
        bias_out[0],
        bias_out[1],
        cross_query_out,
        cross_out[0],
        cross_out[1],
        cross_output_out,
        up_out,
        down_out,
        gain_out[0],
        gain_out[1],
        gain_out[2],
    )


def local_by_heads(
    tokens,
    neighbours,
    teacher,
    valid_mask,
    block_order,
    query_weight,
    key_weight,
    value_weight,
    output_weight,
    relative_weight,
    content_bias,
    position_bias,
    cross_query_weight,
    cross_key_weight,
    cross_value_weight,
    cross_output_weight,
    up_weight,
    down_weight,
    attention_gain,
    cross_gain,
    feedforward_gain,
):
    places = 4
    ctx_count = 8
    place = lax.axis_index("wa")
    here = lax.axis_index("ctx")
    _, tok_dev, width = tokens.shape
    seq_len = tok_dev * ctx_count
    block = tok_dev // 2
    attn = HEADS * HEAD_DIM
    cols = attn // places
    share = width // places

    slots = jnp.arange(2 * ctx_count)
    inverse = jnp.sum(jnp.where(block_order[None, :] == slots[:, None], slots[None, :], 0), axis=1)
    inverse = inverse.astype(jnp.int32)
    valid = valid_mask.astype(f32)

    def rows_of(blocks):
        return (blocks[:, None] * block + jnp.arange(block, dtype=jnp.int32)).reshape(seq_len, 1)


    small = jnp.concatenate([jnp.zeros((5, attn), f32), jnp.broadcast_to(jnp.sum(valid), (3, attn))])
    gain_rows = jnp.stack([attention_gain, cross_gain, feedforward_gain]).astype(f32)
    bias_rows = jnp.stack([content_bias, position_bias]).astype(f32)
    small = lax.dynamic_update_slice(small, gain_rows, (0, place * share))
    small = lax.dynamic_update_slice(small, bias_rows, (3, place * cols))

    half = width // 2
    freq = jnp.exp(-jnp.log(10000.0) * jnp.arange(half, dtype=f32) * 2.0 / width)
    coarse = (64.0 * jnp.arange(seq_len // 64, dtype=f32)[::-1])[:, None] * freq
    fine = jnp.arange(64, dtype=f32)[::-1][:, None] * freq
    sin_a, cos_a = jnp.sin(coarse)[:, None], jnp.cos(coarse)[:, None]
    sin_b, cos_b = jnp.sin(fine)[None], jnp.cos(fine)[None]
    waves = jnp.concatenate(
        [sin_a * cos_b + cos_a * sin_b, cos_a * cos_b - sin_a * sin_b], axis=-1
    )
    waves = waves.reshape(seq_len, width).astype(bf16)

    done = layer(
        float(places * seq_len),
        dict(
            inverse=rows_of(inverse),
            order=rows_of(block_order),
            tokens=tokens[0],
            teacher=teacher[0],
            valid=valid.reshape(tok_dev, 1),
            small=small,
            neighbours=neighbours.reshape(-1, width),
            waves_any=waves,
            query_any=query_weight,
            key_any=key_weight,
            value_any=value_weight,
            relative_any=relative_weight,
            cross_query_any=cross_query_weight,
            cross_key_any=cross_key_weight,
            cross_value_any=cross_value_weight,
            up_any=up_weight,
            output_any=output_weight,
            cross_out_any=cross_output_weight,
            down_any=down_weight,
        ),
        1,
    )
    qkv_grad, table_grad, bias_part = attend_backward(
        inverse, done.qkv, done.table, done.biases, done.heads_grad.reshape(seq_len, 128), block
    )

    pair_slots = jnp.arange(ctx_count)[:, None, None]
    bias_slots = jnp.where(pair_slots == here, bias_part[None, 0:2], 0.0)
    gain_part = done.gain_grad
    small = jnp.concatenate(
        [
            jnp.pad(gain_part[2:3], ((0, 0), (0, attn - width))),
            jnp.pad(gain_part[0:2], ((0, 0), (0, attn - width))),
            bias_slots.reshape(2, attn),
            jnp.broadcast_to(done.error[0:1, 0:1], (3, attn)),
        ],
        axis=0,
    )
    last = finish(
        dict(
            query_grad=qkv_grad.reshape(ctx_count, tok_dev, 384),
            table_grad=table_grad,
            small=small,
            down_share=done.down_share,
            up_share=done.up_share,
            cross_half=done.cross_half,
            cross_out_x=done.cross_out_x,
            output_x=done.output_x,
            one_grad=done.one_grad,
            tokens=tokens[0],
            gains=done.gains,
            normed_a_any=done.normed_a,
            waves_any=waves,
            near_any=done.pair_grad,
            pair_cols_any=done.pair_cols,
            query_any=query_weight,
            key_any=key_weight,
            value_any=value_weight,
        ),
        2,
    )
    total = last.total
    gain_out = lax.dynamic_slice_in_dim(total[0:3], place * share, share, 1)
    bias_out = lax.dynamic_slice_in_dim(total[3:5].reshape(ctx_count, 2, 128), place * 2, 2, 0)
    bias_out = bias_out.transpose(1, 0, 2).reshape(2, cols)
    loss = total[5, 0] / (2.0 * done.count[0, 0] * width)
    pair_out = last.pair_out.astype(f32)
    down_out = last.down_out.reshape(down_weight.shape).astype(f32)
    cross_output_out = last.cross_o_out.reshape(cols, width).astype(f32)
    output_out = last.output_out.reshape(cols, width).astype(f32)

    return (
        done.layer_out[None],
        loss,
        last.tokens_grad[None],
        last.near_grad.reshape(neighbours.shape),
        pair_out[0],
        pair_out[1],
        pair_out[2],
        output_out,
        pair_out[3],
        bias_out[0],
        bias_out[1],
        last.cross_out[0],
        last.cross_out[1],
        last.cross_out[2],
        cross_output_out,
        last.up_out,
        down_out,
        gain_out[0],
        gain_out[1],
        gain_out[2],
    )


def solution(mesh):
    row = P("wa", None)
    flat = P("wa")
    in_specs = (
        P("wa", "ctx", None),
        P("wa", "ctx", None, None),
        P("wa", "ctx", None),
        P("wa", "ctx"),
        P(),
        row,
        row,
        row,
        row,
        row,
        flat,
        flat,
        row,
        row,
        row,
        row,
        row,
        row,
        flat,
        flat,
        flat,
    )
    out_specs = (
        P("wa", "ctx", None),
        P(),
        P("wa", "ctx", None),
        P("wa", "ctx", None, None),
        row,
        row,
        row,
        row,
        row,
        flat,
        flat,
        row,
        row,
        row,
        row,
        row,
        row,
        flat,
        flat,
        flat,
    )
    by_heads = mesh.shape["ctx"] == 8 and mesh.shape["wa"] == 4
    local = local_by_heads if by_heads else local_general
    return jax.shard_map(local, mesh=mesh, in_specs=in_specs, out_specs=out_specs, check_vma=False)
```

```python
import functools
import types

import jax
import jax.numpy as jnp
from jax import lax
from jax.experimental import pallas as pl
from jax.experimental.pallas import tpu as pltpu
from jax.sharding import PartitionSpec as P

HEADS = 16
HEAD_DIM = 64
GROUP = 64
NK = 256
TILE = 128

eps_norm = 1e-06
neg_big = -1e30
highest = lax.Precision.HIGHEST
f32 = jnp.float32
bf16 = jnp.bfloat16


def inverse_rms(hidden):
    return lax.rsqrt(jnp.mean(hidden * hidden, axis=-1, keepdims=True) + eps_norm)


def norm_pull(hidden, scale, gain, grad):
    scaled = grad * gain
    mean = jnp.mean(hidden * scaled, axis=-1, keepdims=True)
    return scale * scaled - hidden * (scale * scale * scale) * mean


def gelu_tanh(value):
    return jax.nn.gelu(value, approximate=True)


def sinusoid(distance, width):
    half = width // 2
    freq = jnp.exp(-jnp.log(10000.0) * jnp.arange(half, dtype=f32) * 2.0 / width)
    angle = distance[:, None] * freq[None, :]
    return jnp.concatenate([jnp.sin(angle), jnp.cos(angle)], axis=1)


def dot_nn(a, b):
    return lax.dot_general(a, b, (((1,), (0,)), ((), ())), preferred_element_type=f32)


def dot_nt(a, b):
    return lax.dot_general(a, b, (((1,), (1,)), ((), ())), preferred_element_type=f32)


def dot_tn(a, b):
    return lax.dot_general(a, b, (((0,), (0,)), ((), ())), preferred_element_type=f32)


def swap(value, axis, bit):
    pairs = [(i, i ^ bit) for i in range(lax.axis_size(axis))]
    return lax.ppermute(value, axis, pairs)


def bits_of(axis):
    bits, bit = [], 1
    while bit < lax.axis_size(axis):
        bits.append(bit)
        bit *= 2
    return bits


def my_bit(axis, bit):
    return (lax.axis_index(axis) // bit) % 2


def ordered(bit, own, other, dim):
    return jnp.where(
        bit == 0,
        jnp.concatenate([own, other], axis=dim),
        jnp.concatenate([other, own], axis=dim),
    )


def split(value, bit, dim):
    half = value.shape[dim] // 2
    keep = lax.dynamic_slice_in_dim(value, bit * half, half, dim)
    send = lax.dynamic_slice_in_dim(value, (1 - bit) * half, half, dim)
    return keep, send


def gather_parts(value):
    parts = {0: value}
    for bit in reversed(bits_of("wa")):
        parts.update({r | bit: swap(part, "wa", bit) for r, part in list(parts.items())})
    return [parts[r] for r in sorted(parts)]


def scatter_parts(parts):
    parts = dict(enumerate(parts))
    for bit in bits_of("wa"):
        kept = {}
        for r, part in parts.items():
            if not r & bit:
                got = swap(parts[r | bit].astype(bf16), "wa", bit)
                kept[r] = part + got.astype(f32)
        parts = kept
    return parts[0]


def take_columns(weight):
    value = weight[None]
    for bit in reversed(bits_of("wa")):
        mine = my_bit("wa", bit)
        keep, send = split(value, mine, 2)
        value = ordered(mine, keep[:, None], swap(send, "wa", bit)[:, None], 1)
        value = value.reshape((-1,) + value.shape[2:])
    return value.reshape(-1, value.shape[-1])


def spread_columns(value):
    for bit in bits_of("wa"):
        mine = my_bit("wa", bit)
        paired = value.reshape((value.shape[0], value.shape[1] // 2, 2) + value.shape[2:])
        keep, send = split(paired, mine, 2)
        value = ordered(mine, keep[:, :, 0], swap(send[:, :, 0], "wa", bit), 3)
    return value[:, 0]


def halving_dim(shape):
    if shape[-2] % 16 == 0:
        return len(shape) - 2
    if shape[0] % 2 == 0:
        return 0
    if shape[-2] % 2 == 0:
        return len(shape) - 2
    return len(shape) - 1


def sum_over_ctx(value, bits, finish):
    dims = []
    for bit in bits:
        dim = halving_dim(value.shape)
        keep, send = split(value, my_bit("ctx", bit), dim)
        value = (keep.astype(f32) + swap(send, "ctx", bit).astype(f32)).astype(bf16)
        dims.append(dim - value.ndim if dim else 0)
    value = finish(value)
    for bit, dim in reversed(list(zip(bits, dims))):
        dim = dim % value.ndim
        value = ordered(my_bit("ctx", bit), value, swap(value, "ctx", bit), dim)
    return value


def all_summed(value, axis):
    for bit in bits_of(axis):
        value = value + swap(value, axis, bit)
    return value


def sum_column_grads(grads):
    places = lax.axis_size("wa")
    grads = grads.reshape(grads.shape[0], places, grads.shape[1] // places, grads.shape[2])
    bits = bits_of("ctx")
    if grads.shape[2] % lax.axis_size("ctx") == 0:
        return sum_over_ctx(grads, bits, spread_columns).astype(f32)
    return sum_over_ctx(spread_columns(grads), bits, lambda value: value).astype(f32)


def sum_row_grads(grads):
    return sum_over_ctx(grads[None], bits_of("ctx"), lambda value: value)[0].astype(f32)


def first_half(shape):
    return lax.broadcasted_iota(jnp.int32, shape, 1) < HEAD_DIM


def stack_heads(rows):
    mask = first_half(rows.shape)
    zero = jnp.zeros_like(rows)
    return jnp.concatenate([jnp.where(mask, rows, zero), jnp.where(mask, zero, rows)], axis=0)


def join_heads(stacked):
    rows = stacked.shape[0] // 2
    return jnp.where(first_half((rows, stacked.shape[1])), stacked[:rows], stacked[rows:])


def copy_blocks(order_ref, source, target, block, inward):
    for place in range(source.shape[0] // block):
        start = pl.multiple_of(order_ref[place] * block, block)
        if inward:
            target[place * block : (place + 1) * block, :] = source[pl.ds(start, block), :]
        else:
            target[pl.ds(start, block), :] = source[place * block : (place + 1) * block, :]


def attention_shares(content, position, key_ref, rel_ref, row_start, seq_len):
    length = row_start + TILE
    wide_len = length + TILE
    offset = seq_len - TILE - row_start
    scale = HEAD_DIM ** (-0.5)
    scores = dot_nt(content, key_ref[0:length, :])
    wide = dot_nt(position, rel_ref[offset : offset + wide_len, :])
    halves = []
    for head in range(2):
        part = wide[head * TILE : (head + 1) * TILE]
        turned = pltpu.roll(part, wide_len - (TILE - 1), 1, stride=1, stride_axis=0)
        halves.append(turned[:, :length])
    scores = (scores + jnp.concatenate(halves, axis=0)) * scale
    row = lax.broadcasted_iota(jnp.int32, scores.shape, 0) % TILE + row_start
    col = lax.broadcasted_iota(jnp.int32, scores.shape, 1)
    scores = jnp.where(col <= row, scores, neg_big)
    top = jnp.max(scores, axis=1, keepdims=True)
    raised = jnp.exp(scores - top)
    total = jnp.sum(raised, axis=1, keepdims=True)
    return raised * (1.0 / total)


def attend_tiles(qkv, rel_ref, content_bias, position_bias, out):
    seq_len = qkv.shape[0]
    keys = qkv.at[:, 128:256]
    values = qkv.at[:, 256:384]
    for tile in range(seq_len // TILE):
        start = tile * TILE
        query = qkv[start : start + TILE, 0:128].astype(f32)
        content = stack_heads((query + content_bias).astype(bf16))
        position = stack_heads((query + position_bias).astype(bf16))
        shares = attention_shares(content, position, keys, rel_ref, start, seq_len)
        got = dot_nn(shares.astype(bf16), values[0 : start + TILE, :])
        got = join_heads(got).astype(bf16)
        block = out.shape[1]
        for part in range(TILE // block):
            out[start // block + part] = got[part * block : (part + 1) * block]


def attend_back_tiles(
    qkv, grad, rel_ref, content_bias, position_bias, dqkv, dkey, dvalue, drel, poll
):
    scale = HEAD_DIM ** (-0.5)
    seq_len = qkv.shape[0]
    block = dqkv.shape[1]
    keys = qkv.at[:, 128:256]
    values = qkv.at[:, 256:384]
    dkey[...] = jnp.zeros_like(dkey)
    dvalue[...] = jnp.zeros_like(dvalue)
    drel[...] = jnp.zeros_like(drel)
    row = lax.broadcasted_iota(jnp.int32, (TILE, TILE), 0)
    col = lax.broadcasted_iota(jnp.int32, (TILE, TILE), 1)
    flip = jnp.where(row + col == TILE - 1, 1.0, 0.0).astype(bf16)
    content_sum = jnp.zeros((1, 128), f32)
    position_sum = jnp.zeros((1, 128), f32)
    for tile in range(seq_len // TILE):
        poll(tile)
        start = tile * TILE
        length = start + TILE
        wide_len = length + TILE
        offset = seq_len - TILE - start
        query = qkv[start : start + TILE, 0:128].astype(f32)
        content = stack_heads((query + content_bias).astype(bf16))
        plain = (query + position_bias).astype(bf16)
        position = stack_heads(plain)
        shares = attention_shares(content, position, keys, rel_ref, start, seq_len)
        out_grad = stack_heads(grad[start : start + TILE, :])
        share_grad = dot_nt(out_grad, values[0:length, :])
        delta = jnp.sum(shares * share_grad, axis=1, keepdims=True)
        score_grad = (shares * (share_grad - delta)).astype(bf16)
        content_grad = join_heads(dot_nn(score_grad, keys[0:length, :])) * scale
        parts = []
        for head in range(2):
            turned = dot_nn(flip, score_grad[head * TILE : (head + 1) * TILE])
            turned = jnp.concatenate([turned, jnp.zeros((TILE, TILE), f32)], axis=1)
            parts.append(pltpu.roll(turned, 0, 1, stride=1, stride_axis=0))
        wide_grad = jnp.concatenate(parts, axis=0).astype(bf16)
        relative = rel_ref[offset : offset + wide_len, :]
        turned_grad = join_heads(dot_nn(wide_grad, relative)) * scale
        turned_rows = stack_heads(dot_nn(flip, plain).astype(bf16))
        drel[offset : offset + wide_len, :] += dot_tn(wide_grad, turned_rows)
        high = turned_grad.astype(bf16)
        low = (turned_grad - high.astype(f32)).astype(bf16)
        position_grad = dot_nn(flip, high) + dot_nn(flip, low)
        content_sum += jnp.sum(content_grad, axis=0, keepdims=True)
        position_sum += jnp.sum(turned_grad, axis=0, keepdims=True)
        query_grad = (content_grad + position_grad).astype(bf16)
        for part in range(TILE // block):
            dqkv[start // block + part, :, 0:128] = query_grad[part * block : (part + 1) * block]
        dkey[0:length, :] += dot_tn(score_grad, content)
        dvalue[0:length, :] += dot_tn(shares.astype(bf16), out_grad)
    for part in range(seq_len // block):
        rows = slice(part * block, (part + 1) * block)
        dqkv[part, :, 128:256] = (dkey[rows, :] * scale).astype(bf16)
        dqkv[part, :, 256:384] = dvalue[rows, :].astype(bf16)
    return content_sum, position_sum


in_vmem = pl.BlockSpec(memory_space=pltpu.VMEM)
in_smem = pl.BlockSpec(memory_space=pltpu.SMEM)


def head_mask(shape, head):
    lane = lax.broadcasted_iota(jnp.int32, shape, 1)
    return (lane >= head * HEAD_DIM) & (lane < (head + 1) * HEAD_DIM)


def stack_all(rows):
    zero = jnp.zeros_like(rows)
    heads = rows.shape[1] // HEAD_DIM
    return jnp.concatenate(
        [jnp.where(head_mask(rows.shape, head), rows, zero) for head in range(heads)], axis=0
    )


def join_all(stacked):
    heads = stacked.shape[1] // HEAD_DIM
    rows = stacked.shape[0] // heads
    out = jnp.zeros((rows, stacked.shape[1]), stacked.dtype)
    for head in range(heads):
        part = stacked[head * rows : (head + 1) * rows]
        out = jnp.where(head_mask(part.shape, head), part, out)
    return out


def cross_shares(query, keys):
    scores = dot_nt(query, keys) * (HEAD_DIM ** (-0.5))
    raised = jnp.exp(scores - jnp.max(scores, axis=1, keepdims=True))
    return raised / jnp.sum(raised, axis=1, keepdims=True)


def cross_forward_kernel(q_ref, kv_ref, out_ref):
    width = q_ref.shape[1]
    shares = cross_shares(stack_all(q_ref[...]), kv_ref[:, 0:width])
    out_ref[...] = join_all(dot_nn(shares.astype(bf16), kv_ref[:, width:])).astype(bf16)


def cross_backward_kernel(q_ref, kv_ref, grad_ref, dq_ref, dkv_ref):
    width = q_ref.shape[1]
    scale = HEAD_DIM ** (-0.5)
    keys = kv_ref[:, 0:width]
    query = stack_all(q_ref[...])
    grad = stack_all(grad_ref[...])
    shares = cross_shares(query, keys)
    share_grad = dot_nt(grad, kv_ref[:, width:])
    delta = jnp.sum(shares * share_grad, axis=1, keepdims=True)
    score_grad = (shares * (share_grad - delta)).astype(bf16)
    dq_ref[...] = (join_all(dot_nn(score_grad, keys)) * scale).astype(bf16)
    dkv_ref[:, 0:width] = (dot_tn(score_grad, query) * scale).astype(bf16)
    dkv_ref[:, width:] = dot_tn(shares.astype(bf16), grad).astype(bf16)


def cross_forward(query, pair):
    width = query.shape[1]
    groups = query.shape[0] // GROUP
    return pl.pallas_call(
        cross_forward_kernel,
        out_shape=jax.ShapeDtypeStruct(query.shape, bf16),
        grid=(groups,),
        in_specs=[
            pl.BlockSpec((GROUP, width), lambda g: (g, 0)),
            pl.BlockSpec((NK, 2 * width), lambda g: (g, 0)),
        ],
        out_specs=pl.BlockSpec((GROUP, width), lambda g: (g, 0)),
        cost_estimate=pl.CostEstimate(
            flops=groups * 4 * 256 * 256 * 256, bytes_accessed=groups * 330000, transcendentals=groups * 65536
        ),
        name="cross_forward",
    )(query, pair)


def cross_backward(query, pair, grad):
    width = query.shape[1]
    groups = query.shape[0] // GROUP
    return pl.pallas_call(
        cross_backward_kernel,
        out_shape=[
            jax.ShapeDtypeStruct(query.shape, bf16),
            jax.ShapeDtypeStruct(pair.shape, bf16),
        ],
        grid=(groups,),
        in_specs=[
            pl.BlockSpec((GROUP, width), lambda g: (g, 0)),
            pl.BlockSpec((NK, 2 * width), lambda g: (g, 0)),
            pl.BlockSpec((GROUP, width), lambda g: (g, 0)),
        ],
        out_specs=[
            pl.BlockSpec((GROUP, width), lambda g: (g, 0)),
            pl.BlockSpec((NK, 2 * width), lambda g: (g, 0)),
        ],
        cost_estimate=pl.CostEstimate(
            flops=groups * 10 * 256 * 256 * 256, bytes_accessed=groups * 660000, transcendentals=groups * 65536
        ),
        name="cross_backward",
    )(query, pair, grad)


mesh_id = pl.DeviceIdType.MESH


def signal_to(barrier, ctx, wa):
    pl.semaphore_signal(barrier, inc=1, device_id=(ctx, wa), device_id_type=mesh_id)


def tree_sum(values):
    while len(values) > 1:
        values = [a + b for a, b in zip(values[::2], values[1::2])]
    return values[0]


def gelu_slope(value):
    inner = 0.7978845608028654 * (value + 0.044715 * value * value * value)
    turned = jnp.tanh(inner)
    slope = 0.7978845608028654 * (1.0 + 3.0 * 0.044715 * value * value)
    return 0.5 * (1.0 + turned) + 0.5 * value * (1.0 - turned * turned) * slope


def places_here():
    return lax.axis_index("ctx"), lax.axis_index("wa")


def meet_all():
    c, w = places_here()
    owner = c // 2
    own = owner == w
    barrier = pltpu.get_barrier_semaphore()
    for j in range(1, 8):
        signal_to(barrier, c ^ j, w)
    for j in range(1, 4):
        signal_to(barrier, c, w ^ j)
    for j in range(1, 8):
        signal_to(barrier, c ^ j, owner)
    for r in range(4):
        for h in range(2):

            @pl.when(jnp.logical_not(jnp.logical_and(2 * w + h == c, r == 0)))
            def _(r=r, h=h):
                signal_to(barrier, 2 * w + h, w ^ r)

    @pl.when(jnp.logical_not(own))
    def _():
        signal_to(barrier, c, owner)

    pl.semaphore_wait(barrier, 26 - 2 * own.astype(jnp.int32))


def meet_lines():
    c, w = places_here()
    barrier = pltpu.get_barrier_semaphore()
    for j in range(1, 8):
        signal_to(barrier, c ^ j, w)
    for j in range(1, 4):
        signal_to(barrier, c, w ^ j)
    pl.semaphore_wait(barrier, 10)


def remote(source, target, send, recv, ctx, wa):
    return pltpu.make_async_remote_copy(
        src_ref=source,
        dst_ref=target,
        send_sem=send,
        recv_sem=recv,
        device_id=(ctx, wa),
        device_id_type=mesh_id,
    )


class GatherRows:

    def __init__(self, buf, send, recv):
        self.buf, self.send, self.recv = buf, send, recv
        self.c, self.w = places_here()

    def copy(self, k):
        source, entry, j = ((0, 1, 1), (0, 2, 2), (2, 3, 1))[k]
        return remote(
            self.buf.at[source],
            self.buf.at[entry],
            self.send.at[k],
            self.recv.at[k],
            self.c,
            self.w ^ j,
        )

    def start(self):
        self.copy(1).start()
        self.copy(0).start()

    def near(self):
        self.copy(0).wait()

    def relay(self):
        self.copy(1).wait()
        self.copy(2).start()

    def far(self):
        self.copy(2).wait()


class SumRows:

    def __init__(self, out_buf, in_buf, send, recv):
        self.out, self.inn, self.send, self.recv = out_buf, in_buf, send, recv
        self.c, self.w = places_here()

    def copy(self, k):
        j = (1, 1, 2)[k]
        return remote(
            self.out.at[k], self.inn.at[k], self.send.at[k], self.recv.at[k], self.c, self.w ^ j
        )

    def give_near(self, value):
        self.out[0] = value.astype(bf16)
        self.copy(0).start()

    def give_far(self, value):
        self.out[1] = value.astype(bf16)
        self.copy(1).start()

    def pass_on(self, value):
        self.copy(1).wait()
        self.out[2] = (value + self.inn[1].astype(f32)).astype(bf16)
        self.copy(2).start()

    def total(self, value):
        self.copy(0).wait()
        value = value + self.inn[0].astype(f32)
        self.copy(2).wait()
        return value + self.inn[2].astype(f32)


class CtxSum:

    def __init__(self, send, recv, x=None, half=None, part=None, share=None, out=None, spread=0):
        self.send, self.recv = send, recv
        self.x, self.half, self.part, self.share, self.out = x, half, part, share, out
        self.spread = spread
        self.c, self.w = places_here()
        self.z, self.y = self.c // 2, self.c % 2

    def y_copy(self):
        return remote(
            self.x.at[:, 1 - self.y], self.half, self.send.at[0], self.recv.at[0], self.c ^ 1, self.w
        )

    def start_y(self):
        self.y_copy().start()

    def finish_y(self):
        self.y_copy().wait()
        for z in range(4):
            mine = self.x[z, self.y].astype(f32)
            self.half[z] = (self.half[z].astype(f32) + mine).astype(bf16)

    def z_copy(self, j):
        return remote(
            self.half.at[self.z ^ j],
            self.part.at[j - 1],
            self.send.at[j],
            self.recv.at[j],
            self.c ^ (2 * j),
            self.w,
        )

    def start_z(self):
        for j in (2, 3, 1):
            self.z_copy(j).start()

    def finish_z(self):
        total = self.half[self.z].astype(f32)
        for j in (1, 2, 3):
            self.z_copy(j).wait()
            total = total + self.part[j - 1].astype(f32)
        self.share[...] = total.astype(bf16)

    def columns(self, place):
        width = self.spread
        return self.out.at[self.z, self.y, :, pl.ds(pl.multiple_of(place * width, 128), width)]

    def wa_copy(self, j, place):
        return remote(
            self.share.at[self.w ^ j],
            self.columns(place),
            self.send.at[3 + j],
            self.recv.at[3 + j],
            self.c,
            self.w ^ j,
        )

    def own_copy(self):
        source = self.share.at[self.w] if self.spread else self.share
        target = self.columns(self.w) if self.spread else self.out.at[self.z, self.y]
        return pltpu.make_async_copy(source, target, self.send.at[11])

    def start_wa(self):
        if self.spread:
            for j in (2, 3, 1):
                self.wa_copy(j, self.w).start()
        self.own_copy().start()

    def finish_wa(self):
        self.own_copy().wait()
        if self.spread:
            for j in (1, 2, 3):
                self.wa_copy(j, self.w).wait_send()
                self.wa_copy(j, self.w ^ j).wait_recv()

    def back_z_copy(self, j, z):
        mine = self.out.at[z, self.y]
        return remote(mine, mine, self.send.at[6 + j], self.recv.at[6 + j], self.c ^ (2 * j), self.w)

    def start_back_z(self):
        for j in (2, 3, 1):
            self.back_z_copy(j, self.z).start()

    def finish_back_z(self):
        for j in (1, 2, 3):
            self.back_z_copy(j, self.z).wait_send()
            self.back_z_copy(j, self.z ^ j).wait_recv()

    def back_y_copy(self, y):
        part = self.out.at[:, y]
        return remote(part, part, self.send.at[10], self.recv.at[10], self.c ^ 1, self.w)

    def start_back_y(self):
        self.back_y_copy(self.y).start()

    def finish_back_y(self):
        self.back_y_copy(self.y).wait_send()
        self.back_y_copy(1 - self.y).wait_recv()


def put_shares(target, grads, first=0):
    count = grads.shape[0] // 32
    padded = target.shape[3]
    for place in range(4):
        for share in range(8):
            start = (place * 8 + share) * count
            part = grads[start : start + count]
            part = jnp.concatenate([part, jnp.zeros((padded - count, part.shape[1]), f32)], axis=0)
            target[share // 2, share % 2, place, :, first : first + part.shape[1]] = part.astype(bf16)


def put_rows(target, grads):
    count = grads.shape[0] // 8
    for share in range(8):
        target[share // 2, share % 2] = grads[share * count : (share + 1) * count].astype(bf16)


class Cut:

    def __init__(self, ref, start):
        self.ref, self.start = ref, start

    @property
    def at(self):
        return self

    def __getitem__(self, k):
        return self.ref.at[self.start + k]


class Pool:
    def __init__(self, ref):
        self.ref, self.used = ref, 0

    def take(self, count):
        cut = Cut(self.ref, self.used)
        self.used += count
        return cut


class LineGather:

    def __init__(self, out, send, recv):
        self.out, self.send, self.recv = out, send, recv
        self.c, self.w = places_here()
        self.z = self.c // 2
        self.right, self.left = self.z < 3, self.z > 0

    def y_copy(self, block, slot):
        ref = self.out.at[block]
        return remote(ref, ref, self.send.at[slot], self.recv.at[slot], self.c ^ 1, self.w)

    def z_copy(self, block, slot, step):
        k = slot + (7 if step > 0 else 10)
        ref = self.out.at[block]
        return remote(ref, ref, self.send.at[k], self.recv.at[k], self.c + step, self.w)

    def start(self):
        @pl.when(self.right)
        def _():
            self.z_copy(self.c, 0, 2).start()

        @pl.when(self.left)
        def _():
            self.z_copy(self.c, 0, -2).start()

        self.y_copy(self.c, 0).start()

    def step(self, t):
        @pl.when(self.z > t)
        def _():
            block = self.c - 2 * (t + 1)
            self.z_copy(block, t, 2).wait_recv()
            if t < 2:

                @pl.when(self.right)
                def _():
                    self.z_copy(block, t + 1, 2).start()

            self.y_copy(block, t + 1).start()

        @pl.when(self.z < 3 - t)
        def _():
            block = self.c + 2 * (t + 1)
            self.z_copy(block, t, -2).wait_recv()
            if t < 2:

                @pl.when(self.left)
                def _():
                    self.z_copy(block, t + 1, -2).start()

            self.y_copy(block, t + 4).start()

    def finish(self):
        self.y_copy(self.c, 0).wait_send()
        self.y_copy(self.c ^ 1, 0).wait_recv()
        for t in range(3):
            for step, at, near in ((-2, t + 1, self.z > t), (2, t + 4, self.z < 3 - t)):

                @pl.when(near)
                def _(step=step, at=at):
                    self.y_copy(self.c + step * (t + 1), at).wait_send()
                    self.y_copy((self.c ^ 1) + step * (t + 1), at).wait_recv()

        @pl.when(self.right)
        def _():
            self.z_copy(self.c, 0, 2).wait_send()

        @pl.when(self.left)
        def _():
            self.z_copy(self.c, 0, -2).wait_send()

        for t in range(2):

            @pl.when(jnp.logical_and(self.z > t, self.right))
            def _():
                self.z_copy(self.c, t + 1, 2).wait_send()

            @pl.when(jnp.logical_and(self.z < 3 - t, self.left))
            def _():
                self.z_copy(self.c, t + 1, -2).wait_send()


class Columns:

    def __init__(self, source, target, width, first, send, recv, at=None):
        self.source, self.target, self.width, self.first = source, target, width, first
        self.send, self.recv, self.column = send, recv, at
        self.shared = at is None
        self.c, self.w = places_here()
        self.y = self.c % 2

    def taken(self, place, half=None):
        start = place * self.width if self.column is None else self.column
        rows = self.source.shape[0]
        which = slice(None) if half is None else pl.ds(pl.multiple_of(half * (rows // 2), 16), rows // 2)
        return self.source.at[which, pl.ds(pl.multiple_of(start, 128), self.width)]

    def put(self, place, half=None):
        rows = self.source.shape[0]
        start, count = place * rows, rows
        if half is not None:
            start, count = start + half * (rows // 2), rows // 2
        return self.target.at[
            pl.ds(pl.multiple_of(start, 16), count), self.first : self.first + self.width
        ]

    def copy(self, j, place):
        half = self.y if self.shared and j > 1 else None
        return remote(
            self.taken(self.w ^ j, half),
            self.put(place, half),
            self.send.at[j],
            self.recv.at[j],
            self.c,
            self.w ^ j,
        )

    def passed(self, j, half):
        ref = self.put(self.w ^ j, half)
        return remote(ref, ref, self.send.at[2 + j], self.recv.at[2 + j], self.c ^ 1, self.w)

    def own(self):
        return pltpu.make_async_copy(self.taken(self.w), self.put(self.w), self.send.at[0])

    def start(self):
        for j in (2, 3, 1):
            self.copy(j, self.w).start()
        self.own().start()

    def relay(self):
        for j in (2, 3):
            self.copy(j, self.w).wait_send()
            self.copy(j, self.w ^ j).wait_recv()
            self.passed(j, self.y).start()

    def finish(self):
        self.own().wait()
        for j in (1,) if self.shared else (1, 2, 3):
            self.copy(j, self.w).wait_send()
            self.copy(j, self.w ^ j).wait_recv()
        if self.shared:
            for j in (2, 3):
                self.passed(j, self.y).wait_send()
                self.passed(j, 1 - self.y).wait_recv()


class SmallSum:

    def __init__(self, ref, got, axis, send, recv):
        self.ref, self.got, self.axis, self.send, self.recv = ref, got, axis, send, recv
        self.c, self.w = places_here()

    def copy(self, k):
        j = k + 1
        ctx, wa = (self.c ^ j, self.w) if self.axis == "ctx" else (self.c, self.w ^ j)
        return remote(self.ref, self.got.at[k], self.send.at[k], self.recv.at[k], ctx, wa)

    def start(self):
        for k in range(self.got.shape[0]):
            self.copy(k).start()

    def finish(self):
        count = self.got.shape[0]
        for k in range(count):
            self.copy(k).wait()
        self.ref[...] = tree_sum([self.ref[...]] + [self.got[k] for k in range(count)])


class SwapHeads:

    def __init__(self, by_heads, by_rows, outward, send, recv):
        self.heads, self.rows, self.outward = by_heads, by_rows, outward
        self.send, self.recv = send, recv
        self.c, self.w = places_here()
        self.owner, self.half = self.c // 2, self.c % 2
        self.own = self.owner == self.w
        self.other = jnp.logical_not(self.own)

    def lanes(self):
        return pl.ds(pl.multiple_of(self.half * 128, 128), 128)

    def out_copy(self, j):
        slot = self.w ^ self.owner
        return remote(
            self.heads.at[self.c ^ j],
            self.rows.at[slot, :, self.lanes()],
            self.send.at[j],
            self.recv.at[slot * 2 + self.half],
            self.c ^ j,
            self.owner,
        )

    def start_out(self):
        for j in range(7, 0, -1):
            self.out_copy(j).start()

        @pl.when(self.other)
        def _():
            self.out_copy(0).start()

        @pl.when(self.own)
        def _():
            slot = self.w ^ self.owner
            pltpu.make_async_copy(
                self.heads.at[self.c],
                self.rows.at[slot, :, self.lanes()],
                self.recv.at[slot * 2 + self.half],
            ).start()

    def wait_rows(self, r):
        for h in range(2):
            remote(
                self.heads.at[0],
                self.rows.at[r, :, h * 128 : (h + 1) * 128],
                self.send.at[0],
                self.recv.at[r * 2 + h],
                self.c ^ 1,
                self.w,
            ).wait_recv()

    def finish_out(self):
        for j in range(1, 8):
            self.out_copy(j).wait_send()

        @pl.when(self.other)
        def _():
            self.out_copy(0).wait_send()

    def in_copy(self, r, h):
        return remote(
            self.rows.at[r, :, h * 128 : (h + 1) * 128],
            self.heads.at[self.c],
            self.send.at[r * 2 + h],
            self.recv.at[self.c],
            2 * self.w + h,
            self.w ^ r,
        )

    def mine(self, r, h):
        return jnp.logical_and(2 * self.w + h == self.c, r == 0)

    def start_in(self, r):
        for h in range(2):

            @pl.when(jnp.logical_not(self.mine(r, h)))
            def _():
                self.in_copy(r, h).start()

            @pl.when(self.mine(r, h))
            def _():
                pltpu.make_async_copy(
                    self.rows.at[r, :, h * 128 : (h + 1) * 128],
                    self.heads.at[self.c],
                    self.recv.at[self.c],
                ).start()

    def finish_in(self):
        for block in range(8):
            remote(
                self.rows.at[0, :, 0:128],
                self.heads.at[block],
                self.send.at[0],
                self.recv.at[block],
                self.c ^ 1,
                self.w,
            ).wait_recv()
        for r in range(4):
            for h in range(2):

                @pl.when(jnp.logical_not(self.mine(r, h)))
                def _(r=r, h=h):
                    self.in_copy(r, h).wait_send()


def layer_kernel(names, total_tokens, block, *refs):
    v = types.SimpleNamespace(**dict(zip(names, refs, strict=True)))
    c, w = places_here()
    send, recv, local = Pool(v.send), Pool(v.recv), Pool(v.local)
    tok, width = v.tokens.shape
    seq_len = 8 * tok
    rows = 4 * tok
    cols = v.output_w.shape[0]
    hidden = v.down_w.shape[0]
    scale = HEAD_DIM ** (-0.5)

    def load(source, target):
        copy = pltpu.make_async_copy(source, target, local.take(1).at[0])
        copy.start()
        return copy

    near_load = load(v.neighbours, v.near.at[0])
    early = [load(v.waves_any, v.waves)]
    late = [
        load(v.output_any, v.output_w),
        load(v.cross_out_any, v.cross_out_w),
        load(v.down_any, v.down_w),
    ]
    column = lax.broadcasted_iota(jnp.int32, (256, 1024), 1)
    line = lax.broadcasted_iota(jnp.int32, (256, 1024), 0)

    def placed(value, start):
        chosen = jnp.where(column == line + start, 1.0, 0.0).astype(bf16)
        return dot_nn(value, chosen[: value.shape[1]])

    v.small_all[...] = placed(v.gain_rows[...], w * (width // 4)) + placed(v.bias_rows[...], w * cols)
    mask = v.mask[...].astype(f32)
    v.small_all[5:6, :] = jnp.broadcast_to(jnp.sum(mask, keepdims=True), (1, 1024))
    v.tokens_all[c] = v.tokens[...]
    meet_all()

    near_sum = SmallSum(v.small_all, v.small_near, "wa", send.take(3), recv.take(3))
    count_sum = SmallSum(v.count, v.count_far, "ctx", send.take(7), recv.take(7))
    gather = LineGather(v.tokens_all, send.take(13), recv.take(13))
    pair = [
        Columns(weight, v.pair, 128, 128 * m, send.take(4), recv.take(4), c * 128)
        for m, weight in enumerate((v.query_any, v.key_any, v.value_any, v.relative_any))
    ]
    cross = [
        Columns(weight, target, cols, first, send.take(6), recv.take(6))
        for weight, target, first in (
            (v.cross_key_any, v.pair_cols, 0),
            (v.cross_value_any, v.pair_cols, cols),
            (v.cross_query_any, v.query_cols, 0),
        )
    ]
    up_columns = Columns(v.up_any, v.up_cols, hidden, 0, send.take(6), recv.take(6))
    near_send, near_recv = send.take(3), recv.take(3)
    near_gather = GatherRows(v.near, near_send, near_recv)
    gather.start()
    near_sum.start()
    for part in pair:
        part.start()
    gather.step(0)
    near_sum.finish()
    v.count[...] = jnp.broadcast_to(v.small_all[5:6, 0:128], v.count.shape)
    count_sum.start()
    gather.step(1)
    for part in pair:
        part.finish()
    near_load.wait()
    near_gather.start()
    for part in cross:
        part.start()
    up_columns.start()
    for copy in early:
        copy.wait()
    v.table[0:seq_len, :] = dot_nn(v.waves[...], v.pair[:, 384:512]).astype(bf16)
    v.table[seq_len:, :] = jnp.zeros((TILE, 128), bf16)
    v.biases[...] = v.small_all[:, pl.ds(pl.multiple_of(c * 128, 128), 128)]
    v.gains[...] = v.small_all[:, 0:width]
    gather.step(2)
    gather.finish()
    gain_one, gain_two, gain_three = (v.gains[k : k + 1, :] for k in range(3))

    def project(part, carry):
        start = pl.multiple_of(part * tok, tok)
        value = v.tokens_all[part].astype(f32)
        normed = (value * inverse_rms(value) * gain_one).astype(bf16)
        v.normed_a[pl.ds(start, tok), :] = normed
        mixed = dot_nn(normed, v.pair[:, 0:384]).astype(bf16)
        for h in range(tok // block):
            v.qkv[part * (tok // block) + h] = mixed[h * block : (h + 1) * block]
        return carry

    lax.fori_loop(0, 8, project, 0)
    normed_out = pltpu.make_async_copy(v.normed_a, v.normed_a_any, local.take(1).at[0])
    normed_out.start()
    pair_out = pltpu.make_async_copy(v.pair_cols, v.pair_cols_any, local.take(1).at[0])
    for place in range(seq_len // block):
        take_block(v.qkv, v.inverse, place, v.qkv_order.at[place * block : (place + 1) * block, :])
    attend_tiles(v.qkv_order, v.table, v.biases[3:4, :], v.biases[4:5, :], v.heads_order)
    per = tok // block
    for place in range(seq_len // block):
        at = (place % per) * block
        take_block(v.heads_order, v.order, place, v.heads.at[place // per, at : at + block, :])
    out_swap = SwapHeads(v.heads, v.attended, True, send.take(8), recv.take(8))
    out_swap.start_out()
    near_gather.near()
    near_gather.relay()
    for part in cross:
        part.relay()
    up_columns.relay()
    for copy in late:
        copy.wait()

    gathers = [GatherRows(ref, send.take(3), recv.take(3)) for ref in (v.rows_b, v.rows_c)]
    sums = [SumRows(v.give.at[k], v.take.at[k], send.take(3), recv.take(3)) for k in range(3)]

    def output_part(r):
        return dot_nn(v.attended[r], v.output_w[...])

    out_swap.wait_rows(3)
    sums[0].give_far(output_part(3))
    out_swap.wait_rows(1)
    sums[0].give_near(output_part(1))
    out_swap.wait_rows(2)
    sums[0].pass_on(output_part(2))
    out_swap.wait_rows(0)
    v.hidden_one[...] = v.tokens[...].astype(f32) + sums[0].total(output_part(0))
    value = v.hidden_one[...]
    v.rows_b[0] = (value * inverse_rms(value) * gain_two).astype(bf16)

    gathers[0].start()
    out_swap.finish_out()
    near_gather.far()
    for part in cross:
        part.finish()
    pair_out.start()
    near_count = v.near.shape[1]

    def near_project(r, carry):
        start = pl.multiple_of(r * near_count, near_count)
        v.cross_pair[pl.ds(start, near_count), :] = dot_nn(v.near[r], v.pair_cols[...]).astype(bf16)
        return carry

    lax.fori_loop(0, 4, near_project, 0)

    def cross_part(r):
        v.cross_q[r * tok : (r + 1) * tok, :] = dot_nn(v.rows_b[r], v.query_cols[...]).astype(bf16)

        def group(g, carry):
            at = pl.multiple_of(r * tok + g * GROUP, GROUP)
            near = pl.multiple_of((r * (tok // GROUP) + g) * NK, NK)
            query = stack_all(v.cross_q[pl.ds(at, GROUP), :])
            shares = cross_shares(query, v.cross_pair[pl.ds(near, NK), 0:cols])
            out = dot_nn(shares.astype(bf16), v.cross_pair[pl.ds(near, NK), cols:])
            v.crossed[pl.ds(at, GROUP), :] = join_all(out).astype(bf16)
            return carry

        lax.fori_loop(0, tok // GROUP, group, 0)
        return dot_nn(v.crossed[r * tok : (r + 1) * tok, :], v.cross_out_w[...])

    def in_turn(gathered, summed, part, between=None):
        v.keep[0] = part(0)
        gathered.near()
        summed.give_near(part(1))
        gathered.relay()
        v.keep[2] = part(2)
        gathered.far()
        summed.give_far(part(3))
        summed.pass_on(v.keep[2])
        if between is not None:
            between()
        return summed.total(v.keep[0])

    v.hidden_two[...] = v.hidden_one[...] + in_turn(gathers[0], sums[1], cross_part)
    value = v.hidden_two[...]
    v.rows_c[0] = (value * inverse_rms(value) * gain_three).astype(bf16)

    gathers[1].start()
    up_columns.finish()

    def feed_part(r):
        part = pl.ds(r * tok, tok)
        v.pre_act[part, :] = dot_nn(v.rows_c[r], v.up_cols[...])
        v.activated[part, :] = gelu_tanh(v.pre_act[part, :]).astype(bf16)
        return dot_nn(v.activated[part, :], v.down_w[...])

    layer_out = v.hidden_two[...] + in_turn(gathers[1], sums[2], feed_part)
    v.layer_out[...] = layer_out

    count_sum.finish()
    error = layer_out - v.teacher[...].astype(f32)
    square = (tok, tok)
    same = lax.broadcasted_iota(jnp.int32, square, 0) == lax.broadcasted_iota(jnp.int32, square, 1)
    valid = jnp.sum(jnp.where(same, mask, 0.0), axis=1, keepdims=True)
    weighted = valid * error
    v.error[...] = jnp.broadcast_to(jnp.sum(weighted * error, keepdims=True), v.error.shape)
    v.out_grad[...] = (total_tokens / v.count[0:1, 0:1]) * weighted

    middle_back(v, send, recv, local, block)
    normed_out.wait()
    pair_out.wait()


def take_block(source, chosen, place, target):
    target[...] = source[chosen[place]]


def middle_back(v, send, recv, local, block):
    c, w = places_here()
    tok, width = v.tokens.shape
    rows = 4 * tok
    cols = v.output_w.shape[0]
    scale = HEAD_DIM ** (-0.5)
    first, second, third = (
        GatherRows(ref, send.take(3), recv.take(3)) for ref in (v.rows_o, v.rows_two, v.rows_one)
    )
    sum_c, sum_b = (
        SumRows(v.give.at[k], v.take.at[k], send.take(3), recv.take(3)) for k in (3, 4)
    )
    down = CtxSum(send.take(12), recv.take(12), v.down_x, v.down_half, v.down_part, v.down_share)
    up = CtxSum(send.take(12), recv.take(12), v.up_x, v.up_half, v.up_part, v.up_share)
    cross = CtxSum(
        send.take(12), recv.take(12), v.cross_x, v.cross_half, v.cross_part, v.cross_share
    )
    ctx_o = CtxSum(send.take(12), recv.take(12), v.cross_out_x, v.ctx_o_half)
    out_o = CtxSum(send.take(12), recv.take(12), v.output_x, v.out_o_half)
    heads = SwapHeads(v.heads_grad, v.heads_out, False, send.take(8), recv.take(8))
    v.rows_o[0] = v.out_grad[...].astype(bf16)

    first.start()

    def feed_back(r):
        part = pl.ds(r * tok, tok)
        act_grad = dot_nt(v.rows_o[r], v.down_w[...])
        v.pre_grad[part, :] = (act_grad * gelu_slope(v.pre_act[part, :])).astype(bf16)
        return dot_nt(v.pre_grad[part, :], v.up_cols[...])

    v.keep[0] = feed_back(0)
    first.near()
    sum_c.give_near(feed_back(1))
    first.relay()
    v.keep[1] = feed_back(2)
    first.far()
    sum_c.give_far(feed_back(3))
    sum_c.pass_on(v.keep[1])
    put_rows(v.down_x, dot_tn(v.activated[...], v.rows_o[...].reshape(rows, width)))
    down.start_y()
    put_shares(v.up_x, dot_tn(v.rows_c[...].reshape(rows, width), v.pre_grad[...]))
    up.start_y()
    normed_grad = sum_c.total(v.keep[0])
    value = v.hidden_two[...]
    inverse = inverse_rms(value)
    two_grad = v.out_grad[...] + norm_pull(value, inverse, v.gains[2:3, :], normed_grad)
    gain_three = jnp.sum(normed_grad * value * inverse, axis=0, keepdims=True)
    v.keep[1] = two_grad
    v.rows_two[0] = two_grad.astype(bf16)

    second.start()

    def cross_back(r):
        part = slice(r * tok, (r + 1) * tok)
        v.crossed_grad[...] = dot_nt(v.rows_two[r], v.cross_out_w[...]).astype(bf16)

        def group(g, carry):
            within = pl.multiple_of(g * GROUP, GROUP)
            at = pl.multiple_of(r * tok + g * GROUP, GROUP)
            near = pl.ds(pl.multiple_of((r * (tok // GROUP) + g) * NK, NK), NK)
            query = stack_all(v.cross_q[pl.ds(at, GROUP), :])
            grad = stack_all(v.crossed_grad[pl.ds(within, GROUP), :])
            keys = v.cross_pair[near, 0:cols]
            shares = cross_shares(query, keys)
            share_grad = dot_nt(grad, v.cross_pair[near, cols:])
            delta = jnp.sum(shares * share_grad, axis=1, keepdims=True)
            score_grad = (shares * (share_grad - delta)).astype(bf16)
            query_grad = join_all(dot_nn(score_grad, keys)) * scale
            v.query_grad[pl.ds(at, GROUP), :] = query_grad.astype(bf16)
            v.pair_grad[near, 0:cols] = (dot_tn(score_grad, query) * scale).astype(bf16)
            v.pair_grad[near, cols:] = dot_tn(shares.astype(bf16), grad).astype(bf16)
            return carry

        lax.fori_loop(0, tok // GROUP, group, 0)
        return dot_nt(v.query_grad[part, :], v.query_cols[...])

    v.keep[0] = cross_back(0)
    second.near()
    sum_b.give_near(cross_back(1))
    second.relay()
    v.keep[2] = cross_back(2)
    second.far()
    down.finish_y()
    down.start_z()
    sum_b.give_far(cross_back(3))
    sum_b.pass_on(v.keep[2])
    pair_grad_out = pltpu.make_async_copy(v.pair_grad, v.pair_grad_any, local.take(1).at[0])
    pair_grad_out.start()
    normed_b = v.rows_b[...].reshape(rows, width)
    put_rows(v.cross_out_x, dot_tn(v.crossed[...], v.rows_two[...].reshape(rows, width)))
    ctx_o.start_y()
    put_shares(v.cross_x, dot_tn(normed_b, v.query_grad[...]), 0)
    normed_grad = sum_b.total(v.keep[0])
    value = v.hidden_one[...]
    inverse = inverse_rms(value)
    one_grad = v.keep[1] + norm_pull(value, inverse, v.gains[1:2, :], normed_grad)
    gain_two = jnp.sum(normed_grad * value * inverse, axis=0, keepdims=True)
    v.gain_grad[...] = jnp.concatenate(
        [gain_two, gain_three, jnp.zeros((6, gain_two.shape[1]), f32)], axis=0
    )
    v.one_grad[...] = one_grad
    v.rows_one[0] = one_grad.astype(bf16)

    third.start()
    near = v.near[...].reshape(-1, width)
    put_shares(v.cross_x, dot_tn(near, v.pair_grad[...]), cols)
    cross.start_y()

    def head_back(r):
        v.heads_out[r] = dot_nt(v.rows_one[r], v.output_w[...]).astype(bf16)
        heads.start_in(r)

    head_back(0)
    third.near()
    head_back(1)
    third.relay()
    head_back(2)
    third.far()
    head_back(3)
    up.finish_y()
    up.start_z()
    attended = jnp.concatenate([v.attended[r] for r in range(4)], axis=0)
    put_rows(v.output_x, dot_tn(attended, v.rows_one[...].reshape(rows, width)))
    out_o.start_y()
    heads.finish_in()

    per = tok // block
    for place in range(8 * per):
        at = (place % per) * block
        v.heads_stored[place] = v.heads_grad[place // per, at : at + block, :]
    for place in range(8 * per):
        take_block(
            v.heads_stored, v.inverse, place, v.grad_order.at[place * block : (place + 1) * block, :]
        )

    def poll(tile):
        if tile == 1:
            down.finish_z()
        if tile == 3:
            ctx_o.finish_y()
            cross.finish_y()
            cross.start_z()
        if tile == 5:
            out_o.finish_y()
        if tile == 6:
            up.finish_z()

    content_sum, position_sum = attend_back_tiles(
        v.qkv_order,
        v.grad_order,
        v.table,
        v.biases[3:4, :],
        v.biases[4:5, :],
        v.qkv_grad_order,
        v.dkey,
        v.dvalue,
        v.drel,
        poll,
    )
    v.table_grad[...] = v.drel[0 : v.table_grad.shape[0], :] * scale
    v.bias_grad[...] = jnp.concatenate([content_sum, position_sum, jnp.zeros((6, 128), f32)], axis=0)
    for place in range(8 * per):
        at = (place % per) * block
        take_block(
            v.qkv_grad_order, v.order, place, v.query_grad_out.at[place // per, at : at + block, :]
        )
    cross.finish_z()
    pair_grad_out.wait()


def layer(total_tokens, block, orders, given, collective_id):
    tok, width = given["tokens"].shape
    hidden = given["down_any"].shape[0]
    cols = given["output_any"].shape[0]
    near = given["neighbours"].shape[0]
    seq_len = 8 * tok
    rows = 4 * tok
    padded = -(-(width // 32) // 8) * 8
    any_space = pl.BlockSpec(memory_space=pl.ANY)
    shape = jax.ShapeDtypeStruct
    vmem = pltpu.VMEM
    dma = pltpu.SemaphoreType.DMA
    results = dict(
        layer_out=shape((tok, width), f32),
        error=shape((8, 128), f32),
        count=shape((8, 128), f32),
        gains=shape((8, width), f32),
        normed_a_any=shape((seq_len, width), bf16),
        pair_cols_any=shape((width, 2 * cols), bf16),
        one_grad=shape((tok, width), f32),
        gain_grad=shape((8, width), f32),
        pair_grad_any=shape((4 * near, 2 * cols), bf16),
        query_grad_out=shape((8, tok, 384), bf16),
        table_grad=shape((seq_len, 128), f32),
        bias_grad=shape((8, 128), f32),
        down_share=shape((hidden // 8, width), bf16),
        up_share=shape((4, padded, hidden), bf16),
        cross_share=shape((4, padded, 3 * cols), bf16),
        ctx_o_half=shape((4, cols // 8, width), bf16),
        out_o_half=shape((4, cols // 8, width), bf16),
    )
    scratch = dict(
        small_all=vmem((8, 1024), f32),
        small_near=vmem((3, 8, 1024), f32),
        qkv=vmem((seq_len // block, block, 384), bf16),
        table=vmem((seq_len + TILE, 128), bf16),
        biases=vmem((8, 128), f32),
        normed_a=vmem((seq_len, width), bf16),
        pair_cols=vmem((width, 2 * cols), bf16),
        heads_grad=vmem((8, tok, 128), bf16),
        grad_order=vmem((seq_len, 128), bf16),
        pair_grad=vmem((4 * near, 2 * cols), bf16),
        qkv_grad_order=vmem((seq_len // block, block, 384), bf16),
        dkey=vmem((seq_len, 128), f32),
        dvalue=vmem((seq_len, 128), f32),
        drel=vmem((seq_len + TILE, 128), f32),
        cross_half=vmem((4, 4, padded, 3 * cols), bf16),
        cross_part=vmem((3, 4, padded, 3 * cols), bf16),
        cross_out_x=vmem((4, 2, cols // 8, width), bf16),
        output_x=vmem((4, 2, cols // 8, width), bf16),
        count_far=vmem((7, 8, 128), f32),
        tokens_all=vmem((8, tok, width), bf16),
        pair=vmem((width, 512), bf16),
        waves=vmem((seq_len, width), bf16),
        qkv_order=vmem((seq_len, 384), bf16),
        heads_order=vmem((seq_len // block, block, 128), bf16),
        heads_stored=vmem((seq_len // block, block, 128), bf16),
        heads=vmem((8, tok, 128), bf16),
        attended=vmem((4, tok, cols), bf16),
        near=vmem((4, near, width), bf16),
        query_cols=vmem((width, cols), bf16),
        up_cols=vmem((width, hidden), bf16),
        output_w=vmem((cols, width), bf16),
        cross_out_w=vmem((cols, width), bf16),
        down_w=vmem((hidden, width), bf16),
        cross_pair=vmem((4 * near, 2 * cols), bf16),
        cross_q=vmem((rows, cols), bf16),
        crossed=vmem((rows, cols), bf16),
        crossed_grad=vmem((tok, cols), bf16),
        hidden_one=vmem((tok, width), f32),
        hidden_two=vmem((tok, width), f32),
        out_grad=vmem((tok, width), f32),
        pre_act=vmem((rows, hidden), f32),
        activated=vmem((rows, hidden), bf16),
        rows_b=vmem((4, tok, width), bf16),
        rows_c=vmem((4, tok, width), bf16),
        rows_o=vmem((4, tok, width), bf16),
        rows_two=vmem((4, tok, width), bf16),
        rows_one=vmem((4, tok, width), bf16),
        give=vmem((5, 3, tok, width), bf16),
        take=vmem((5, 3, tok, width), bf16),
        keep=vmem((3, tok, width), f32),
        pre_grad=vmem((rows, hidden), bf16),
        query_grad=vmem((rows, cols), bf16),
        heads_out=vmem((4, tok, cols), bf16),
        down_x=vmem((4, 2, hidden // 8, width), bf16),
        down_half=vmem((4, hidden // 8, width), bf16),
        down_part=vmem((3, hidden // 8, width), bf16),
        up_x=vmem((4, 2, 4, padded, hidden), bf16),
        up_half=vmem((4, 4, padded, hidden), bf16),
        up_part=vmem((3, 4, padded, hidden), bf16),
        cross_x=vmem((4, 2, 4, padded, 3 * cols), bf16),
        send=dma((232,)),
        recv=dma((232,)),
        local=dma((8,)),
    )
    names = [*orders, *given, *results, *scratch]
    specs = [in_smem] * len(orders) + [
        any_space if name.endswith("_any") or name == "neighbours" else in_vmem for name in given
    ]
    got = pl.pallas_call(
        functools.partial(layer_kernel, names, total_tokens, block),
        out_shape=list(results.values()),
        in_specs=specs,
        out_specs=[any_space if name.endswith("_any") else in_vmem for name in results],
        scratch_shapes=list(scratch.values()),
        compiler_params=pltpu.CompilerParams(
            collective_id=collective_id, has_side_effects=True, vmem_limit_bytes=62 * 2**20
        ),
        name="layer",
    )(*orders.values(), *given.values())
    return types.SimpleNamespace(**dict(zip(results, got, strict=True)))


class Spread:

    def __init__(self, share, out, send, recv):
        self.share, self.out, self.send, self.recv = share, out, send, recv
        self.c, self.w = places_here()

    def columns(self, place):
        width = self.share.shape[2]
        return self.out.at[self.c, :, pl.ds(pl.multiple_of(place * width, 128), width)]

    def copy(self, j, place):
        return remote(
            self.share.at[self.w ^ j],
            self.columns(place),
            self.send.at[j],
            self.recv.at[j],
            self.c,
            self.w ^ j,
        )

    def own(self):
        return pltpu.make_async_copy(
            self.share.at[self.w], self.columns(self.w), self.send.at[0]
        )

    def start(self):
        for j in (2, 3, 1):
            self.copy(j, self.w).start()
        self.own().start()

    def finish(self):
        self.own().wait()
        for j in (1, 2, 3):
            self.copy(j, self.w).wait_send()
            self.copy(j, self.w ^ j).wait_recv()


class Whole:

    def __init__(self, source, target, send, recv):
        self.source, self.target, self.send, self.recv = source, target, send, recv
        self.c, self.w = places_here()

    def put(self, place):
        rows = self.source.shape[0]
        return self.target.at[pl.ds(pl.multiple_of(place * rows, 32), rows), :]

    def copy(self, j, place):
        return remote(
            self.source, self.put(place), self.send.at[j], self.recv.at[j], self.c, self.w ^ j
        )

    def passed(self, place):
        ref = self.put(place)
        return remote(ref, ref, self.send.at[3], self.recv.at[3], self.c, self.w ^ 1)

    def own(self):
        return pltpu.make_async_copy(self.source, self.put(self.w), self.send.at[0])

    def start(self):
        self.copy(2, self.w).start()
        self.copy(1, self.w).start()
        self.own().start()

    def relay(self):
        self.copy(2, self.w).wait_send()
        self.copy(2, self.w ^ 2).wait_recv()
        self.passed(self.w ^ 2).start()

    def finish(self):
        self.own().wait()
        self.copy(1, self.w).wait_send()
        self.copy(1, self.w ^ 1).wait_recv()
        self.passed(self.w ^ 2).wait_send()
        self.passed(self.w ^ 3).wait_recv()


class MaskSum:

    def __init__(self, ref, got, masks, send, recv):
        self.ref, self.got, self.masks, self.send, self.recv = ref, got, masks, send, recv
        self.c, self.w = places_here()

    def copy(self, k):
        ctx, wa = self.masks[k]
        return remote(
            self.ref, self.got.at[k], self.send.at[k], self.recv.at[k], self.c ^ ctx, self.w ^ wa
        )

    def start(self):
        for k in range(len(self.masks)):
            self.copy(k).start()

    def finish(self):
        for k in range(len(self.masks)):
            self.copy(k).wait()
        self.ref[...] = tree_sum([self.ref[...]] + [self.got[k] for k in range(len(self.masks))])


def finish_kernel(names, *refs):
    v = types.SimpleNamespace(**dict(zip(names, refs, strict=True)))
    c, w = places_here()
    send, recv, local = Pool(v.send), Pool(v.recv), Pool(v.local)
    tok, width = v.tokens.shape
    cols = v.out_o_half.shape[1] * 8
    share = width // 4

    def load(source, target):
        copy = pltpu.make_async_copy(source, target, local.take(1).at[0])
        copy.start()
        return copy

    loads = [load(v.normed_a_any, v.normed_a), load(v.waves_any, v.waves)]
    late = [load(v.pair_cols_any, v.pair_cols), load(v.near_any, v.near_rows)]

    def line(out):
        return LineGather(out, send.take(13), recv.take(13))

    def summed(x, half, part, got):
        return CtxSum(send.take(12), recv.take(12), x, half, part, got)

    down, up, cross, ctx_o, out_o, pair = (
        line(out)
        for out in (v.down_out, v.up_all, v.cross_all, v.cross_o_out, v.output_out, v.pair_all)
    )
    ctx_o_sum = summed(None, v.ctx_o_half, v.ctx_o_part, v.ctx_o_share)
    out_o_sum = summed(None, v.out_o_half, v.out_o_part, v.out_o_share)
    up_spread = Spread(v.up_share, v.up_all, send.take(4), recv.take(4))
    cross_spread = Spread(v.cross_share, v.cross_all, send.take(4), recv.take(4))
    sum_pair = SumRows(v.pair_give, v.pair_take, send.take(3), recv.take(3))
    sum_near = SumRows(v.near_give, v.near_take, send.take(3), recv.take(3))
    weights = [
        Whole(weight, v.full.at[m], send.take(4), recv.take(4))
        for m, weight in enumerate((v.query_any, v.key_any, v.value_any))
    ]
    stages = [
        MaskSum(v.total, got, masks, send.take(3), recv.take(3))
        for got, masks in (
            (v.got_wa, ((0, 1), (0, 2), (0, 3))),
            (v.got_y, ((1, 0),)),
            (v.got_z, ((2, 0), (4, 0), (6, 0))),
        )
    ]
    b_send, b_recv = send.take(24), recv.take(24)

    def block_copy(j, m, place):
        return remote(
            v.query_grad.at[c ^ j, :, 128 * m : 128 * (m + 1)],
            v.mine.at[m, :, pl.ds(pl.multiple_of(place * 128, 128), 128)],
            b_send.at[3 * j + m],
            b_recv.at[3 * j + m],
            c ^ j,
            w,
        )

    own_blocks = [
        pltpu.make_async_copy(
            v.query_grad.at[c, :, 128 * m : 128 * (m + 1)],
            v.mine.at[m, :, pl.ds(pl.multiple_of(c * 128, 128), 128)],
            b_recv.at[m],
        )
        for m in range(3)
    ]
    v.down_out[c] = v.down_share[...]
    meet_lines()
    up_spread.start()
    cross_spread.start()
    down.start()
    ctx_o_sum.start_z()
    out_o_sum.start_z()
    for copy in own_blocks:
        copy.start()

    query_grad = v.query_grad[...].reshape(-1, v.query_grad.shape[2])
    high = v.table_grad[...].astype(bf16)
    low = (v.table_grad[...] - high.astype(f32)).astype(bf16)
    for copy in loads:
        copy.wait()
    mixed = dot_tn(v.normed_a[...], query_grad)
    turned = dot_tn(v.waves[...], high) + dot_tn(v.waves[...], low)
    for place in range(4):
        at = place * share
        v.sums[place] = jnp.concatenate([mixed[at : at + share], turned[at : at + share]], axis=1)
    sum_pair.give_far(v.sums[w ^ 3])
    sum_pair.give_near(v.sums[w ^ 1])
    up_spread.finish()
    up.start()
    cross_spread.finish()
    cross.start()
    sum_pair.pass_on(v.sums[w ^ 2])
    down.step(0)
    for j in (4, 6, 5, 7, 2, 3, 1):
        for m in range(3):
            block_copy(j, m, c).start()
    v.pair_all[c] = sum_pair.total(v.sums[w]).astype(bf16)
    pair.start()
    for copy in late:
        copy.wait()
    near_count = v.near_grad.shape[0]

    def near_part(r):
        return dot_nt(v.near_rows[r * near_count : (r + 1) * near_count, :], v.pair_cols[...])

    sum_near.give_far(near_part(3))
    sum_near.give_near(near_part(1))
    sum_near.pass_on(near_part(2))
    for weight in weights:
        weight.start()
    v.near_grad[...] = near_part(0)
    up.step(0)
    down.step(1)
    cross.step(0)
    ctx_o_sum.finish_z()
    v.cross_o_out[c] = v.ctx_o_share[...]
    ctx_o.start()
    out_o_sum.finish_z()
    v.output_out[c] = v.out_o_share[...]
    out_o.start()
    up.step(1)
    cross.step(1)
    pair.step(0)
    down.step(2)
    ctx_o.step(0)
    out_o.step(0)
    up.step(2)
    cross.step(2)
    pair.step(1)
    ctx_o.step(1)
    out_o.step(1)

    for j in range(1, 8):
        for m in range(3):
            block_copy(j, m, c ^ j).wait_recv()
    for copy in own_blocks:
        copy.wait()
    pair.step(2)
    for weight in weights:
        weight.relay()
    for weight in weights:
        weight.finish()
    normed_grad = dot_nt(v.mine[0], v.full[0])
    normed_grad = normed_grad + dot_nt(v.mine[1], v.full[1])
    normed_grad = normed_grad + dot_nt(v.mine[2], v.full[2])
    hidden = v.tokens[...].astype(f32)
    inverse = inverse_rms(hidden)
    v.tokens_grad[...] = v.one_grad[...] + norm_pull(hidden, inverse, v.gains[0:1, :], normed_grad)
    v.total[...] = v.small[...]
    v.total[0:1, 0:width] = jnp.sum(normed_grad * hidden * inverse, axis=0, keepdims=True)
    stages[0].start()
    ctx_o.step(2)
    out_o.step(2)
    stages[0].finish()
    stages[1].start()
    v.near_grad[...] = sum_near.total(v.near_grad[...])
    stages[1].finish()
    stages[2].start()
    down.finish()
    up.finish()
    used = share // 8

    def lay_up(part, at):
        v.up_out[at : at + used, :] = v.up_all[part, 0:used, :].astype(f32)

    for part in range(8):
        lay_up(part, part * used)
    pair.finish()
    for part in range(8):
        for m in range(4):
            v.pair_out[m, :, 128 * part : 128 * (part + 1)] = v.pair_all[
                part, :, 128 * m : 128 * (m + 1)
            ]
    ctx_o.finish()
    out_o.finish()
    cross.finish()
    for part in range(8):
        for m in range(3):
            for place in range(4):
                at = (place * 3 + m) * cols
                v.cross_out[m, part * used : (part + 1) * used, place * cols : (place + 1) * cols] = (
                    v.cross_all[part, 0:used, at : at + cols].astype(f32)
                )
    stages[2].finish()
    for j in range(1, 8):
        for m in range(3):
            block_copy(j, m, c).wait_send()


def finish(given, collective_id):
    tok, width = given["tokens"].shape
    near = given["near_any"].shape[0]
    padded = given["up_share"].shape[1]
    hidden = given["up_share"].shape[2]
    cols = given["out_o_half"].shape[1] * 8
    share = width // 4
    any_space = pl.BlockSpec(memory_space=pl.ANY)
    shape = jax.ShapeDtypeStruct
    vmem = pltpu.VMEM
    dma = pltpu.SemaphoreType.DMA
    part = (cols // 8, width)
    results = dict(
        tokens_grad=shape((tok, width), f32),
        near_grad=shape((near // 4, width), f32),
        total=shape(given["small"].shape, f32),
        down_out=shape((8,) + given["down_share"].shape, bf16),
        up_out=shape((share, 4 * hidden), f32),
        cross_out=shape((3, share, 4 * cols), f32),
        cross_o_out=shape((8,) + part, bf16),
        output_out=shape((8,) + part, bf16),
        pair_out=shape((4, share, 1024), bf16),
    )
    scratch = dict(
        normed_a=vmem(given["normed_a_any"].shape, bf16),
        waves=vmem(given["waves_any"].shape, bf16),
        pair_cols=vmem(given["pair_cols_any"].shape, bf16),
        near_rows=vmem(given["near_any"].shape, bf16),
        full=vmem((3, width, 1024), bf16),
        mine=vmem((3, tok, 1024), bf16),
        sums=vmem((4, share, 512), f32),
        up_all=vmem((8, padded, 4 * hidden), bf16),
        cross_all=vmem((8, padded, 12 * cols), bf16),
        pair_all=vmem((8, share, 512), bf16),
        ctx_o_part=vmem((3,) + part, bf16),
        ctx_o_share=vmem(part, bf16),
        out_o_part=vmem((3,) + part, bf16),
        out_o_share=vmem(part, bf16),
        pair_give=vmem((3, share, 512), bf16),
        pair_take=vmem((3, share, 512), bf16),
        near_give=vmem((3, near // 4, width), bf16),
        near_take=vmem((3, near // 4, width), bf16),
        got_wa=vmem((3,) + given["small"].shape, f32),
        got_y=vmem((1,) + given["small"].shape, f32),
        got_z=vmem((3,) + given["small"].shape, f32),
        send=dma((184,)),
        recv=dma((184,)),
        local=dma((4,)),
    )
    names = [*given, *results, *scratch]
    got = pl.pallas_call(
        functools.partial(finish_kernel, names),
        out_shape=list(results.values()),
        in_specs=[any_space if name.endswith("_any") else in_vmem for name in given],
        out_specs=[in_vmem] * len(results),
        scratch_shapes=list(scratch.values()),
        compiler_params=pltpu.CompilerParams(
            collective_id=collective_id, has_side_effects=True, vmem_limit_bytes=62 * 2**20
        ),
        name="finish",
    )(*given.values())
    return types.SimpleNamespace(**dict(zip(results, got, strict=True)))


def skew(wide, count):
    lead = wide.shape[:-2]
    rows, span = wide.shape[-2:]
    edge = [(0, 0)] * len(lead)
    padded = jnp.pad(wide, edge + [(0, 0), (0, 1)])
    flat = padded.reshape(lead + (rows * (span + 1),))
    flat = lax.slice_in_dim(flat, rows - 1, rows - 1 + rows * span, axis=len(lead))
    return flat.reshape(lead + (rows, span))[..., :count]


def unskew(grad, span):
    lead = grad.shape[:-2]
    rows, count = grad.shape[-2:]
    edge = [(0, 0)] * len(lead)
    wide = jnp.pad(grad, edge + [(0, 0), (0, span - count)])
    flat = jnp.pad(wide.reshape(lead + (rows * span,)), edge + [(rows - 1, 1)])
    return flat.reshape(lead + (rows, span + 1))[..., :span]


def tile_scores(content_rows, position_rows, key_rows, relative, row_start, key_start):
    rows = content_rows.shape[0]
    count = key_rows.shape[0]
    scale = content_rows.shape[-1] ** (-0.5)
    content = jnp.einsum("qhe,khe->hqk", content_rows, key_rows, preferred_element_type=f32)
    wide = jnp.einsum("qhe,whe->hqw", position_rows, relative, preferred_element_type=f32)
    scores = (content + skew(wide, count)) * scale
    causal = (row_start + jnp.arange(rows))[:, None] >= (key_start + jnp.arange(count))[None, :]
    return (scores, causal[None])


def tile_forward(
    content_rows, position_rows, row_start, relative, key_rows, value_rows, key_start, state
):
    top, total, accum = state
    scores, causal = tile_scores(
        content_rows, position_rows, key_rows, relative, row_start, key_start
    )
    scores = jnp.where(causal, scores, neg_big)
    new_top = jnp.maximum(top, jnp.max(scores, axis=-1))
    raised = jnp.where(causal, jnp.exp(scores - new_top[..., None]), 0.0)
    fade = jnp.exp(top - new_top)
    total = total * fade + jnp.sum(raised, axis=-1)
    accum = accum * fade[..., None] + jnp.einsum(
        "hqk,khe->hqe", raised.astype(bf16), value_rows, preferred_element_type=f32
    )
    return (new_top, total, accum)


def tile_backward(
    content_rows,
    position_rows,
    row_start,
    relative,
    key_rows,
    value_rows,
    grad_rows,
    log_rows,
    delta_rows,
    key_start,
):
    scores, causal = tile_scores(
        content_rows, position_rows, key_rows, relative, row_start, key_start
    )
    scale = content_rows.shape[-1] ** (-0.5)
    shares = jnp.where(causal, jnp.exp(scores - log_rows[..., None]), 0.0)
    share_grad = jnp.einsum("qhe,khe->hqk", grad_rows, value_rows, preferred_element_type=f32)
    score_grad = (shares * (share_grad - delta_rows[..., None])).astype(bf16)
    content_grad = jnp.einsum("hqk,khe->qhe", score_grad, key_rows, preferred_element_type=f32)
    wide_grad = unskew(score_grad, relative.shape[0])
    position_grad = jnp.einsum("hqw,whe->qhe", wide_grad, relative, preferred_element_type=f32)
    table_part = jnp.einsum("hqw,qhe->whe", wide_grad, position_rows, preferred_element_type=f32)
    key_grad = jnp.einsum("hqk,qhe->khe", score_grad, content_rows, preferred_element_type=f32)
    value_grad = jnp.einsum(
        "hqk,qhe->khe", shares.astype(bf16), grad_rows, preferred_element_type=f32
    )
    return (
        content_grad * scale,
        position_grad * scale,
        table_part * scale,
        key_grad * scale,
        value_grad,
    )


def nest_tiles(tile_fn):
    inner = jax.vmap(tile_fn, in_axes=(0, 0, 0, 0, None, None, 0))
    return jax.vmap(inner, in_axes=(0, 0, None, None, 0, 0, 0))


def to_global(stored, inverse, block):
    seqs, seq_len, width = stored.shape
    blocks = stored.reshape(seqs, seq_len // block, block * width)
    chosen = (inverse[:, None] == jnp.arange(seq_len // block)[None, :]).astype(bf16)
    moved = jnp.einsum("gs,nsx->ngx", chosen, blocks, preferred_element_type=f32)
    return moved.astype(bf16).reshape(stored.shape)


class SplitQueries:

    def __init__(self, query, keys, values, biases, relative, block_order, inverse, block):
        self.seqs, self.tok_dev, self.width = keys.shape
        self.heads = self.width // HEAD_DIM
        self.block = block
        self.block_order = block_order
        ctx_count = lax.axis_size("ctx")
        self.seq_len = self.tok_dev * ctx_count
        self.key_len = min(512, self.seq_len)
        pad = jnp.zeros((self.key_len + block, self.width), bf16)
        table = jnp.concatenate([relative, pad], axis=0)
        self.table = table.reshape(-1, self.heads, HEAD_DIM)
        lead = (self.seqs, 2, block, self.heads, HEAD_DIM)
        self.content = (query + biases[0]).astype(bf16).reshape(lead)
        self.position = (query + biases[1]).astype(bf16).reshape(lead)
        gathered = [lax.all_gather(part, "ctx", axis=1, tiled=True) for part in (keys, values)]
        shape = (self.seqs, self.seq_len, self.heads, HEAD_DIM)
        self.keys, self.values = [to_global(part, inverse, block).reshape(shape) for part in gathered]
        self.starts = lax.dynamic_slice_in_dim(block_order, 2 * lax.axis_index("ctx"), 2, 0) * block

    def rows(self, index):
        start = index * self.key_len
        keys = lax.dynamic_slice_in_dim(self.keys, start, self.key_len, 1)
        values = lax.dynamic_slice_in_dim(self.values, start, self.key_len, 1)
        span = self.block + self.key_len
        offsets = [self.seq_len - self.block - self.starts[slot] + start for slot in range(2)]
        relative = [lax.dynamic_slice_in_dim(self.table, offset, span, 0) for offset in offsets]
        return start, keys, values, jnp.stack(relative), offsets

    def to_stored(self, part):
        count = self.seq_len // self.block
        blocks = part.reshape(self.seqs, count, self.block * self.width)
        chosen = (self.block_order[:, None] == jnp.arange(count)[None, :]).astype(f32)
        moved = jnp.einsum("sg,ngx->nsx", chosen, blocks, precision=highest)
        return moved.reshape(self.seqs, self.seq_len, self.width)

    def forward(self):
        def step(state, index):
            start, keys, values, relative, _ = self.rows(index)

            def tile(content, position, row_start, table, keys_seq, values_seq, tile_state):
                return tile_forward(
                    content, position, row_start, table, keys_seq, values_seq, start, tile_state
                )

            return nest_tiles(tile)(
                self.content, self.position, self.starts, relative, keys, values, state
            ), None

        shape = (self.seqs, 2, self.heads, self.block)
        state = (
            jnp.full(shape, neg_big, f32),
            jnp.zeros(shape, f32),
            jnp.zeros(shape + (HEAD_DIM,), f32),
        )
        (top, total, accum), _ = lax.scan(step, state, jnp.arange(self.seq_len // self.key_len))
        self.log_total = top + jnp.log(total)
        self.out = accum / total[..., None]
        moved = jnp.transpose(self.out, (0, 1, 3, 2, 4))
        return moved.reshape(self.seqs * self.tok_dev, self.width).astype(bf16)

    def backward(self, grad):
        block, seq_len, key_len = self.block, self.seq_len, self.key_len
        lead = (self.seqs, 2, block, self.heads, HEAD_DIM)
        grad = grad.reshape(lead)
        delta = jnp.einsum("sbqhe,sbhqe->sbhq", grad.astype(f32), self.out)
        def step(carry, index):
            start, keys, values, relative, offsets = self.rows(index)

            def tile(content, position, row_start, table, keys_seq, values_seq, extra):
                return tile_backward(
                    content, position, row_start, table, keys_seq, values_seq, *extra, start
                )

            extra = (grad, self.log_total, delta)
            parts = nest_tiles(tile)(
                self.content, self.position, self.starts, relative, keys, values, extra
            )
            table = carry[2]
            table_sum = jnp.sum(parts[2], axis=0)
            for slot in range(2):
                offset = offsets[slot]
                current = lax.dynamic_slice_in_dim(table, offset, block + key_len, 0)
                table = lax.dynamic_update_slice_in_dim(table, current + table_sum[slot], offset, 0)
            sums = []
            for total, part in zip(carry[3:], parts[3:]):
                current = lax.dynamic_slice_in_dim(total, start, key_len, 1)
                part = current + jnp.sum(part, axis=1)
                sums.append(lax.dynamic_update_slice_in_dim(total, part, start, 1))
            key_acc, value_acc = sums
            return (carry[0] + parts[0], carry[1] + parts[1], table, key_acc, value_acc), None

        zero_tiles = jnp.zeros(lead, f32)
        zero_keys = jnp.zeros((self.seqs, seq_len, self.heads, HEAD_DIM), f32)
        carry = (zero_tiles, zero_tiles, jnp.zeros(self.table.shape, f32), zero_keys, zero_keys)
        carry, _ = lax.scan(step, carry, jnp.arange(seq_len // key_len))
        owned = [
            lax.psum_scatter(
                self.to_stored(part), "ctx", scatter_dimension=1, tiled=True
            )
            for part in carry[3:]
        ]
        flat = (self.seqs * self.tok_dev, self.width)
        query_grad = (carry[0] + carry[1]).reshape(flat).astype(bf16)
        key_grad, value_grad = [part.reshape(flat).astype(bf16) for part in owned]
        bias_grads = jnp.stack(
            [jnp.sum(part, axis=(0, 1, 2)).reshape(self.width) for part in carry[:2]]
        )
        table_grad = carry[2].reshape(-1, self.width)[:seq_len]
        return query_grad, key_grad, value_grad, bias_grads, table_grad


def local_general(
    tokens,
    neighbours,
    teacher,
    valid_mask,
    block_order,
    query_weight,
    key_weight,
    value_weight,
    output_weight,
    relative_weight,
    content_bias,
    position_bias,
    cross_query_weight,
    cross_key_weight,
    cross_value_weight,
    cross_output_weight,
    up_weight,
    down_weight,
    attention_gain,
    cross_gain,
    feedforward_gain,
):
    places = lax.axis_size("wa")
    ctx_count = lax.axis_size("ctx")
    place = lax.axis_index("wa")
    here = lax.axis_index("ctx")
    _, tok_dev, width = tokens.shape
    seq_len = tok_dev * ctx_count
    block = tok_dev // 2
    cols = HEADS * HEAD_DIM // places
    rows = places * tok_dev

    token_parts = gather_parts(tokens[0])
    query_cols, key_cols, value_cols = [
        take_columns(weight) for weight in (query_weight, key_weight, value_weight)
    ]
    relative_cols = take_columns(relative_weight)
    gains = lax.all_gather(
        jnp.stack([attention_gain, cross_gain, feedforward_gain]), "wa", axis=1, tiled=True
    ).astype(f32)
    gain_one, gain_two, gain_three = gains[0:1], gains[1:2], gains[2:3]
    cross_query_cols, cross_key_cols, cross_value_cols = [
        take_columns(weight) for weight in (cross_query_weight, cross_key_weight, cross_value_weight)
    ]
    cross_pair_cols = jnp.concatenate([cross_key_cols, cross_value_cols], axis=1)
    near_rows = jnp.concatenate(gather_parts(neighbours.reshape(-1, width)), axis=0)
    up_cols = take_columns(up_weight)
    valid = valid_mask.astype(f32).reshape(tok_dev, 1)
    count = jnp.sum(valid).reshape(1, 1)
    count = all_summed(all_summed(count, "wa"), "ctx")

    slots = jnp.arange(2 * ctx_count)
    inverse = jnp.sum(jnp.where(block_order[None, :] == slots[:, None], slots[None, :], 0), axis=1)
    inverse = inverse.astype(jnp.int32)
    distance = (seq_len - 1 - jnp.arange(seq_len)).astype(f32)
    waves = sinusoid(distance, width).astype(bf16)

    hidden_all = jnp.concatenate(token_parts, axis=0).astype(f32)
    scale_all = inverse_rms(hidden_all)
    normed_a = (hidden_all * scale_all * gain_one).astype(bf16)
    biases = jnp.stack([content_bias, position_bias]).astype(f32)
    mixed_cols = jnp.concatenate([query_cols, key_cols, value_cols], axis=1)
    qkv = dot_nn(normed_a, mixed_cols).reshape(places, tok_dev, 3 * cols)
    relative = dot_nn(waves, relative_cols).astype(bf16)
    general = SplitQueries(
        qkv[..., :cols],
        qkv[..., cols : 2 * cols].astype(bf16),
        qkv[..., 2 * cols :].astype(bf16),
        biases,
        relative,
        block_order,
        inverse,
        block,
    )
    attended = general.forward()

    def to_owner(product):
        return scatter_parts([product[r * tok_dev : (r + 1) * tok_dev] for r in range(places)])

    def from_all(value):
        return jnp.concatenate(gather_parts(value), axis=0)

    hidden_in = tokens[0].astype(f32)
    hidden_one = hidden_in + to_owner(dot_nn(attended, output_weight))

    scale_two = inverse_rms(hidden_one)
    normed_b = from_all((hidden_one * scale_two * gain_two).astype(bf16))
    cross_q = dot_nn(normed_b, cross_query_cols).astype(bf16)
    cross_pair = dot_nn(near_rows, cross_pair_cols).astype(bf16)
    crossed = cross_forward(cross_q, cross_pair)
    hidden_two = hidden_one + to_owner(dot_nn(crossed, cross_output_weight))

    scale_three = inverse_rms(hidden_two)
    normed_c = from_all((hidden_two * scale_three * gain_three).astype(bf16))
    pre_act = dot_nn(normed_c, up_cols)
    activated = gelu_tanh(pre_act).astype(bf16)
    layer_out = hidden_two + to_owner(dot_nn(activated, down_weight))

    error = layer_out - teacher[0].astype(f32)
    error_sum = jnp.sum(valid * error * error).reshape(1, 1)
    error_sum = all_summed(all_summed(error_sum, "wa"), "ctx")
    loss = (error_sum / (2.0 * count * width)).reshape(())
    out_grad = (places * seq_len) / count * valid * error

    out_low = from_all(out_grad.astype(bf16))
    act_grad = dot_nt(out_low, down_weight)
    _, gelu_pull = jax.vjp(gelu_tanh, pre_act)
    pre_grad = gelu_pull(act_grad)[0].astype(bf16)
    down_grad = dot_tn(activated, out_low).astype(bf16)
    up_grad = dot_tn(normed_c, pre_grad).astype(bf16)
    normed_c_grad = to_owner(dot_nt(pre_grad, up_cols))
    two_grad = out_grad + norm_pull(hidden_two, scale_three, gain_three, normed_c_grad)
    gain_three_grad = jnp.sum(normed_c_grad * hidden_two * scale_three, axis=0, keepdims=True)
    down_out = sum_row_grads(down_grad)
    up_out = sum_column_grads(up_grad[None])[0]

    two_low = from_all(two_grad.astype(bf16))
    crossed_grad = dot_nt(two_low, cross_output_weight).astype(bf16)
    cross_q_grad, cross_pair_grad = cross_backward(cross_q, cross_pair, crossed_grad)
    normed_b_grad = to_owner(dot_nt(cross_q_grad, cross_query_cols))
    one_grad = two_grad + norm_pull(hidden_one, scale_two, gain_two, normed_b_grad)
    gain_two_grad = jnp.sum(normed_b_grad * hidden_one * scale_two, axis=0, keepdims=True)
    cross_output_grad = dot_tn(crossed, two_low).astype(bf16)
    cross_query_grad = dot_tn(normed_b, cross_q_grad).astype(bf16)
    cross_key_grad = dot_tn(near_rows, cross_pair_grad[:, :cols]).astype(bf16)
    cross_value_grad = dot_tn(near_rows, cross_pair_grad[:, cols:]).astype(bf16)
    cross_output_out = sum_row_grads(cross_output_grad)
    cross_out = sum_column_grads(jnp.stack([cross_key_grad, cross_value_grad]))
    cross_query_out = sum_column_grads(cross_query_grad[None])[0]
    near_grad = dot_nt(cross_pair_grad, cross_pair_cols)
    near_count = near_rows.shape[0] // places
    near_grad = scatter_parts(
        [near_grad[r * near_count : (r + 1) * near_count] for r in range(places)]
    )
    neighbours_grad = near_grad.reshape(neighbours.shape)

    one_low = from_all(one_grad.astype(bf16))
    attended_grad = dot_nt(one_low, output_weight).astype(bf16)
    output_grad = dot_tn(attended, one_low).astype(bf16)
    output_out = sum_row_grads(output_grad)
    query_grad, key_grad, value_grad, bias_grads, table_grad = general.backward(attended_grad)
    qkv_grad = jnp.concatenate([query_grad, key_grad, value_grad], axis=1)
    table_high = table_grad.astype(bf16)
    table_low = (table_grad - table_high.astype(f32)).astype(bf16)
    relative_grad = (dot_tn(waves, table_high) + dot_tn(waves, table_low)).astype(bf16)
    mixed_grad = dot_tn(normed_a, qkv_grad).astype(bf16)
    whole = [mixed_grad[:, m * cols : (m + 1) * cols] for m in range(3)]
    attention_out = sum_column_grads(jnp.stack(whole + [relative_grad]))
    normed_a_part = dot_nt(qkv_grad, mixed_cols)
    gain_one_part = jnp.sum(normed_a_part * hidden_all * scale_all, axis=0, keepdims=True)
    normed_a_grad = to_owner(normed_a_part)
    tokens_grad = one_grad + norm_pull(hidden_in, scale_all[:tok_dev], gain_one, normed_a_grad)

    gain_grads = jnp.concatenate([gain_one_part, gain_two_grad, gain_three_grad], axis=0)
    gain_grads = all_summed(gain_grads, "wa")
    share = width // places
    gain_grads = lax.dynamic_slice_in_dim(gain_grads, place * share, share, 1)
    small = jnp.concatenate([gain_grads.reshape(1, -1), bias_grads.reshape(1, -1)], axis=1)
    small = all_summed(small, "ctx")[0]
    gain_out = small[: 3 * share].reshape(3, share)
    bias_out = small[3 * share :].reshape(2, cols)

    return (
        layer_out[None],
        loss,
        tokens_grad[None],
        neighbours_grad,
        attention_out[0],
        attention_out[1],
        attention_out[2],
        output_out,
        attention_out[3],
        bias_out[0],
        bias_out[1],
        cross_query_out,
        cross_out[0],
        cross_out[1],
        cross_output_out,
        up_out,
        down_out,
        gain_out[0],
        gain_out[1],
        gain_out[2],
    )


def local_by_heads(
    tokens,
    neighbours,
    teacher,
    valid_mask,
    block_order,
    query_weight,
    key_weight,
    value_weight,
    output_weight,
    relative_weight,
    content_bias,
    position_bias,
    cross_query_weight,
    cross_key_weight,
    cross_value_weight,
    cross_output_weight,
    up_weight,
    down_weight,
    attention_gain,
    cross_gain,
    feedforward_gain,
):
    places = 4
    ctx_count = 8
    place = lax.axis_index("wa")
    here = lax.axis_index("ctx")
    _, tok_dev, width = tokens.shape
    seq_len = tok_dev * ctx_count
    block = tok_dev // 2
    attn = HEADS * HEAD_DIM
    cols = attn // places
    share = width // places

    slots = jnp.arange(2 * ctx_count)
    inverse = jnp.sum(jnp.where(block_order[None, :] == slots[:, None], slots[None, :], 0), axis=1)
    inverse = inverse.astype(jnp.int32)
    gain_rows = jnp.concatenate(
        [jnp.stack([attention_gain, cross_gain, feedforward_gain]), jnp.zeros((5, share), bf16)]
    )
    blank = jnp.zeros((3, cols), bf16)
    bias_rows = jnp.concatenate([blank, content_bias[None], position_bias[None], blank])

    half = width // 2
    freq = jnp.exp(-jnp.log(10000.0) * jnp.arange(half, dtype=f32) * 2.0 / width)
    coarse = (64.0 * jnp.arange(seq_len // 64, dtype=f32)[::-1])[:, None] * freq
    fine = jnp.arange(64, dtype=f32)[::-1][:, None] * freq
    sin_a, cos_a = jnp.sin(coarse)[:, None], jnp.cos(coarse)[:, None]
    sin_b, cos_b = jnp.sin(fine)[None], jnp.cos(fine)[None]
    waves = jnp.concatenate(
        [sin_a * cos_b + cos_a * sin_b, cos_a * cos_b - sin_a * sin_b], axis=-1
    )
    waves = waves.reshape(seq_len, width).astype(bf16)

    done = layer(
        float(places * seq_len),
        block,
        dict(inverse=inverse, order=block_order),
        dict(
            tokens=tokens[0],
            teacher=teacher[0],
            mask=valid_mask,
            gain_rows=gain_rows,
            bias_rows=bias_rows,
            neighbours=neighbours.reshape(-1, width),
            waves_any=waves,
            query_any=query_weight,
            key_any=key_weight,
            value_any=value_weight,
            relative_any=relative_weight,
            cross_query_any=cross_query_weight,
            cross_key_any=cross_key_weight,
            cross_value_any=cross_value_weight,
            up_any=up_weight,
            output_any=output_weight,
            cross_out_any=cross_output_weight,
            down_any=down_weight,
        ),
        1,
    )
    pair_slots = jnp.arange(ctx_count)[:, None, None]
    bias_slots = jnp.where(pair_slots == here, done.bias_grad[None, 0:2], 0.0)
    gain_part = done.gain_grad
    small = jnp.concatenate(
        [
            jnp.pad(gain_part[2:3], ((0, 0), (0, attn - width))),
            jnp.pad(gain_part[0:2], ((0, 0), (0, attn - width))),
            bias_slots.reshape(2, attn),
            jnp.broadcast_to(done.error[0:1, 0:1], (3, attn)),
        ],
        axis=0,
    )
    last = finish(
        dict(
            query_grad=done.query_grad_out,
            table_grad=done.table_grad,
            small=small,
            down_share=done.down_share,
            up_share=done.up_share,
            cross_share=done.cross_share,
            ctx_o_half=done.ctx_o_half,
            out_o_half=done.out_o_half,
            one_grad=done.one_grad,
            tokens=tokens[0],
            gains=done.gains,
            normed_a_any=done.normed_a_any,
            waves_any=waves,
            near_any=done.pair_grad_any,
            pair_cols_any=done.pair_cols_any,
            query_any=query_weight,
            key_any=key_weight,
            value_any=value_weight,
        ),
        2,
    )
    total = last.total
    gain_out = lax.dynamic_slice_in_dim(total[0:3], place * share, share, 1)
    bias_out = lax.dynamic_slice_in_dim(total[3:5].reshape(ctx_count, 2, 128), place * 2, 2, 0)
    bias_out = bias_out.transpose(1, 0, 2).reshape(2, cols)
    loss = total[5, 0] / (2.0 * done.count[0, 0] * width)
    pair_out = last.pair_out.astype(f32)
    down_out = last.down_out.reshape(down_weight.shape).astype(f32)
    cross_output_out = last.cross_o_out.reshape(cols, width).astype(f32)
    output_out = last.output_out.reshape(cols, width).astype(f32)

    return (
        done.layer_out[None],
        loss,
        last.tokens_grad[None],
        last.near_grad.reshape(neighbours.shape),
        pair_out[0],
        pair_out[1],
        pair_out[2],
        output_out,
        pair_out[3],
        bias_out[0],
        bias_out[1],
        last.cross_out[0],
        last.cross_out[1],
        last.cross_out[2],
        cross_output_out,
        last.up_out,
        down_out,
        gain_out[0],
        gain_out[1],
        gain_out[2],
    )


def solution(mesh):
    row = P("wa", None)
    flat = P("wa")
    in_specs = (
        P("wa", "ctx", None),
        P("wa", "ctx", None, None),
        P("wa", "ctx", None),
        P("wa", "ctx"),
        P(),
        row,
        row,
        row,
        row,
        row,
        flat,
        flat,
        row,
        row,
        row,
        row,
        row,
        row,
        flat,
        flat,
        flat,
    )
    out_specs = (
        P("wa", "ctx", None),
        P(),
        P("wa", "ctx", None),
        P("wa", "ctx", None, None),
        row,
        row,
        row,
        row,
        row,
        flat,
        flat,
        row,
        row,
        row,
        row,
        row,
        row,
        flat,
        flat,
        flat,
    )
    by_heads = mesh.shape["ctx"] == 8 and mesh.shape["wa"] == 4
    local = local_by_heads if by_heads else local_general
    return jax.shard_map(local, mesh=mesh, in_specs=in_specs, out_specs=out_specs, check_vma=False)
```

```python
import functools
import types

import jax
import jax.numpy as jnp
from jax import lax
from jax.experimental import pallas as pl
from jax.experimental.pallas import tpu as pltpu
from jax.sharding import PartitionSpec as P

HEADS = 16
HEAD_DIM = 64
GROUP = 64
NK = 256
TILE = 128

eps_norm = 1e-06
neg_big = -1e30
highest = lax.Precision.HIGHEST
f32 = jnp.float32
bf16 = jnp.bfloat16


def inverse_rms(hidden):
    return lax.rsqrt(jnp.mean(hidden * hidden, axis=-1, keepdims=True) + eps_norm)


def norm_pull(hidden, scale, gain, grad):
    scaled = grad * gain
    mean = jnp.mean(hidden * scaled, axis=-1, keepdims=True)
    return scale * scaled - hidden * (scale * scale * scale) * mean


def gelu_tanh(value):
    return jax.nn.gelu(value, approximate=True)


def sinusoid(distance, width):
    half = width // 2
    freq = jnp.exp(-jnp.log(10000.0) * jnp.arange(half, dtype=f32) * 2.0 / width)
    angle = distance[:, None] * freq[None, :]
    return jnp.concatenate([jnp.sin(angle), jnp.cos(angle)], axis=1)


def dot_nn(a, b):
    return lax.dot_general(a, b, (((1,), (0,)), ((), ())), preferred_element_type=f32)


def dot_nt(a, b):
    return lax.dot_general(a, b, (((1,), (1,)), ((), ())), preferred_element_type=f32)


def dot_tn(a, b):
    return lax.dot_general(a, b, (((0,), (0,)), ((), ())), preferred_element_type=f32)


def swap(value, axis, bit):
    pairs = [(i, i ^ bit) for i in range(lax.axis_size(axis))]
    return lax.ppermute(value, axis, pairs)


def bits_of(axis):
    bits, bit = [], 1
    while bit < lax.axis_size(axis):
        bits.append(bit)
        bit *= 2
    return bits


def my_bit(axis, bit):
    return (lax.axis_index(axis) // bit) % 2


def ordered(bit, own, other, dim):
    return jnp.where(
        bit == 0,
        jnp.concatenate([own, other], axis=dim),
        jnp.concatenate([other, own], axis=dim),
    )


def split(value, bit, dim):
    half = value.shape[dim] // 2
    keep = lax.dynamic_slice_in_dim(value, bit * half, half, dim)
    send = lax.dynamic_slice_in_dim(value, (1 - bit) * half, half, dim)
    return keep, send


def gather_parts(value):
    parts = {0: value}
    for bit in reversed(bits_of("wa")):
        parts.update({r | bit: swap(part, "wa", bit) for r, part in list(parts.items())})
    return [parts[r] for r in sorted(parts)]


def scatter_parts(parts):
    parts = dict(enumerate(parts))
    for bit in bits_of("wa"):
        kept = {}
        for r, part in parts.items():
            if not r & bit:
                got = swap(parts[r | bit].astype(bf16), "wa", bit)
                kept[r] = part + got.astype(f32)
        parts = kept
    return parts[0]


def take_columns(weight):
    value = weight[None]
    for bit in reversed(bits_of("wa")):
        mine = my_bit("wa", bit)
        keep, send = split(value, mine, 2)
        value = ordered(mine, keep[:, None], swap(send, "wa", bit)[:, None], 1)
        value = value.reshape((-1,) + value.shape[2:])
    return value.reshape(-1, value.shape[-1])


def spread_columns(value):
    for bit in bits_of("wa"):
        mine = my_bit("wa", bit)
        paired = value.reshape((value.shape[0], value.shape[1] // 2, 2) + value.shape[2:])
        keep, send = split(paired, mine, 2)
        value = ordered(mine, keep[:, :, 0], swap(send[:, :, 0], "wa", bit), 3)
    return value[:, 0]


def halving_dim(shape):
    if shape[-2] % 16 == 0:
        return len(shape) - 2
    if shape[0] % 2 == 0:
        return 0
    if shape[-2] % 2 == 0:
        return len(shape) - 2
    return len(shape) - 1


def sum_over_ctx(value, bits, finish):
    dims = []
    for bit in bits:
        dim = halving_dim(value.shape)
        keep, send = split(value, my_bit("ctx", bit), dim)
        value = (keep.astype(f32) + swap(send, "ctx", bit).astype(f32)).astype(bf16)
        dims.append(dim - value.ndim if dim else 0)
    value = finish(value)
    for bit, dim in reversed(list(zip(bits, dims))):
        dim = dim % value.ndim
        value = ordered(my_bit("ctx", bit), value, swap(value, "ctx", bit), dim)
    return value


def all_summed(value, axis):
    for bit in bits_of(axis):
        value = value + swap(value, axis, bit)
    return value


def sum_column_grads(grads):
    places = lax.axis_size("wa")
    grads = grads.reshape(grads.shape[0], places, grads.shape[1] // places, grads.shape[2])
    bits = bits_of("ctx")
    if grads.shape[2] % lax.axis_size("ctx") == 0:
        return sum_over_ctx(grads, bits, spread_columns).astype(f32)
    return sum_over_ctx(spread_columns(grads), bits, lambda value: value).astype(f32)


def sum_row_grads(grads):
    return sum_over_ctx(grads[None], bits_of("ctx"), lambda value: value)[0].astype(f32)


def first_half(shape):
    return lax.broadcasted_iota(jnp.int32, shape, 1) < HEAD_DIM


def stack_heads(rows):
    mask = first_half(rows.shape)
    zero = jnp.zeros_like(rows)
    return jnp.concatenate([jnp.where(mask, rows, zero), jnp.where(mask, zero, rows)], axis=0)


def join_heads(stacked):
    rows = stacked.shape[0] // 2
    return jnp.where(first_half((rows, stacked.shape[1])), stacked[:rows], stacked[rows:])


def copy_blocks(order_ref, source, target, block, inward):
    for place in range(source.shape[0] // block):
        start = pl.multiple_of(order_ref[place] * block, block)
        if inward:
            target[place * block : (place + 1) * block, :] = source[pl.ds(start, block), :]
        else:
            target[pl.ds(start, block), :] = source[place * block : (place + 1) * block, :]


def attention_shares(content, position, key_ref, rel_ref, row_start, seq_len):
    length = row_start + TILE
    wide_len = length + TILE
    offset = seq_len - TILE - row_start
    scale = HEAD_DIM ** (-0.5)
    scores = dot_nt(content, key_ref[0:length, :])
    wide = dot_nt(position, rel_ref[offset : offset + wide_len, :])
    halves = []
    for head in range(2):
        part = wide[head * TILE : (head + 1) * TILE]
        turned = pltpu.roll(part, wide_len - (TILE - 1), 1, stride=1, stride_axis=0)
        halves.append(turned[:, :length])
    scores = (scores + jnp.concatenate(halves, axis=0)) * scale
    row = lax.broadcasted_iota(jnp.int32, scores.shape, 0) % TILE + row_start
    col = lax.broadcasted_iota(jnp.int32, scores.shape, 1)
    scores = jnp.where(col <= row, scores, neg_big)
    top = jnp.max(scores, axis=1, keepdims=True)
    raised = jnp.exp(scores - top)
    total = jnp.sum(raised, axis=1, keepdims=True)
    return raised * (1.0 / total)


def attend_tiles(qkv, rel_ref, content_bias, position_bias, out):
    seq_len = qkv.shape[0]
    keys = qkv.at[:, 128:256]
    values = qkv.at[:, 256:384]
    for tile in range(seq_len // TILE):
        start = tile * TILE
        query = qkv[start : start + TILE, 0:128].astype(f32)
        content = stack_heads((query + content_bias).astype(bf16))
        position = stack_heads((query + position_bias).astype(bf16))
        shares = attention_shares(content, position, keys, rel_ref, start, seq_len)
        got = dot_nn(shares.astype(bf16), values[0 : start + TILE, :])
        got = join_heads(got).astype(bf16)
        block = out.shape[1]
        for part in range(TILE // block):
            out[start // block + part] = got[part * block : (part + 1) * block]


def attend_back_tiles(
    qkv, grad, rel_ref, content_bias, position_bias, dqkv, dkey, dvalue, drel, poll
):
    scale = HEAD_DIM ** (-0.5)
    seq_len = qkv.shape[0]
    block = dqkv.shape[1]
    keys = qkv.at[:, 128:256]
    values = qkv.at[:, 256:384]
    dkey[...] = jnp.zeros_like(dkey)
    dvalue[...] = jnp.zeros_like(dvalue)
    drel[...] = jnp.zeros_like(drel)
    row = lax.broadcasted_iota(jnp.int32, (TILE, TILE), 0)
    col = lax.broadcasted_iota(jnp.int32, (TILE, TILE), 1)
    flip = jnp.where(row + col == TILE - 1, 1.0, 0.0).astype(bf16)
    content_sum = jnp.zeros((1, 128), f32)
    position_sum = jnp.zeros((1, 128), f32)
    for tile in range(seq_len // TILE):
        poll(tile)
        start = tile * TILE
        length = start + TILE
        wide_len = length + TILE
        offset = seq_len - TILE - start
        query = qkv[start : start + TILE, 0:128].astype(f32)
        content = stack_heads((query + content_bias).astype(bf16))
        plain = (query + position_bias).astype(bf16)
        position = stack_heads(plain)
        shares = attention_shares(content, position, keys, rel_ref, start, seq_len)
        out_grad = stack_heads(grad[start : start + TILE, :])
        share_grad = dot_nt(out_grad, values[0:length, :])
        delta = jnp.sum(shares * share_grad, axis=1, keepdims=True)
        score_grad = (shares * (share_grad - delta)).astype(bf16)
        content_grad = join_heads(dot_nn(score_grad, keys[0:length, :])) * scale
        parts = []
        for head in range(2):
            turned = dot_nn(flip, score_grad[head * TILE : (head + 1) * TILE])
            turned = jnp.concatenate([turned, jnp.zeros((TILE, TILE), f32)], axis=1)
            parts.append(pltpu.roll(turned, 0, 1, stride=1, stride_axis=0))
        wide_grad = jnp.concatenate(parts, axis=0).astype(bf16)
        relative = rel_ref[offset : offset + wide_len, :]
        turned_grad = join_heads(dot_nn(wide_grad, relative)) * scale
        turned_rows = stack_heads(dot_nn(flip, plain).astype(bf16))
        drel[offset : offset + wide_len, :] += dot_tn(wide_grad, turned_rows)
        high = turned_grad.astype(bf16)
        low = (turned_grad - high.astype(f32)).astype(bf16)
        position_grad = dot_nn(flip, high) + dot_nn(flip, low)
        content_sum += jnp.sum(content_grad, axis=0, keepdims=True)
        position_sum += jnp.sum(turned_grad, axis=0, keepdims=True)
        query_grad = (content_grad + position_grad).astype(bf16)
        for part in range(TILE // block):
            dqkv[start // block + part, :, 0:128] = query_grad[part * block : (part + 1) * block]
        dkey[0:length, :] += dot_tn(score_grad, content)
        dvalue[0:length, :] += dot_tn(shares.astype(bf16), out_grad)
    for part in range(seq_len // block):
        rows = slice(part * block, (part + 1) * block)
        dqkv[part, :, 128:256] = (dkey[rows, :] * scale).astype(bf16)
        dqkv[part, :, 256:384] = dvalue[rows, :].astype(bf16)
    return content_sum, position_sum


in_vmem = pl.BlockSpec(memory_space=pltpu.VMEM)
in_smem = pl.BlockSpec(memory_space=pltpu.SMEM)


def head_mask(shape, head):
    lane = lax.broadcasted_iota(jnp.int32, shape, 1)
    return (lane >= head * HEAD_DIM) & (lane < (head + 1) * HEAD_DIM)


def stack_all(rows):
    zero = jnp.zeros_like(rows)
    heads = rows.shape[1] // HEAD_DIM
    return jnp.concatenate(
        [jnp.where(head_mask(rows.shape, head), rows, zero) for head in range(heads)], axis=0
    )


def join_all(stacked):
    heads = stacked.shape[1] // HEAD_DIM
    rows = stacked.shape[0] // heads
    out = jnp.zeros((rows, stacked.shape[1]), stacked.dtype)
    for head in range(heads):
        part = stacked[head * rows : (head + 1) * rows]
        out = jnp.where(head_mask(part.shape, head), part, out)
    return out


def cross_shares(query, keys):
    scores = dot_nt(query, keys) * (HEAD_DIM ** (-0.5))
    raised = jnp.exp(scores - jnp.max(scores, axis=1, keepdims=True))
    return raised / jnp.sum(raised, axis=1, keepdims=True)


def cross_forward_kernel(q_ref, kv_ref, out_ref):
    width = q_ref.shape[1]
    shares = cross_shares(stack_all(q_ref[...]), kv_ref[:, 0:width])
    out_ref[...] = join_all(dot_nn(shares.astype(bf16), kv_ref[:, width:])).astype(bf16)


def cross_backward_kernel(q_ref, kv_ref, grad_ref, dq_ref, dkv_ref):
    width = q_ref.shape[1]
    scale = HEAD_DIM ** (-0.5)
    keys = kv_ref[:, 0:width]
    query = stack_all(q_ref[...])
    grad = stack_all(grad_ref[...])
    shares = cross_shares(query, keys)
    share_grad = dot_nt(grad, kv_ref[:, width:])
    delta = jnp.sum(shares * share_grad, axis=1, keepdims=True)
    score_grad = (shares * (share_grad - delta)).astype(bf16)
    dq_ref[...] = (join_all(dot_nn(score_grad, keys)) * scale).astype(bf16)
    dkv_ref[:, 0:width] = (dot_tn(score_grad, query) * scale).astype(bf16)
    dkv_ref[:, width:] = dot_tn(shares.astype(bf16), grad).astype(bf16)


def cross_forward(query, pair):
    width = query.shape[1]
    groups = query.shape[0] // GROUP
    return pl.pallas_call(
        cross_forward_kernel,
        out_shape=jax.ShapeDtypeStruct(query.shape, bf16),
        grid=(groups,),
        in_specs=[
            pl.BlockSpec((GROUP, width), lambda g: (g, 0)),
            pl.BlockSpec((NK, 2 * width), lambda g: (g, 0)),
        ],
        out_specs=pl.BlockSpec((GROUP, width), lambda g: (g, 0)),
        cost_estimate=pl.CostEstimate(
            flops=groups * 4 * 256 * 256 * 256, bytes_accessed=groups * 330000, transcendentals=groups * 65536
        ),
        name="cross_forward",
    )(query, pair)


def cross_backward(query, pair, grad):
    width = query.shape[1]
    groups = query.shape[0] // GROUP
    return pl.pallas_call(
        cross_backward_kernel,
        out_shape=[
            jax.ShapeDtypeStruct(query.shape, bf16),
            jax.ShapeDtypeStruct(pair.shape, bf16),
        ],
        grid=(groups,),
        in_specs=[
            pl.BlockSpec((GROUP, width), lambda g: (g, 0)),
            pl.BlockSpec((NK, 2 * width), lambda g: (g, 0)),
            pl.BlockSpec((GROUP, width), lambda g: (g, 0)),
        ],
        out_specs=[
            pl.BlockSpec((GROUP, width), lambda g: (g, 0)),
            pl.BlockSpec((NK, 2 * width), lambda g: (g, 0)),
        ],
        cost_estimate=pl.CostEstimate(
            flops=groups * 10 * 256 * 256 * 256, bytes_accessed=groups * 660000, transcendentals=groups * 65536
        ),
        name="cross_backward",
    )(query, pair, grad)


mesh_id = pl.DeviceIdType.MESH


def signal_to(barrier, ctx, wa):
    pl.semaphore_signal(barrier, inc=1, device_id=(ctx, wa), device_id_type=mesh_id)


def tree_sum(values):
    while len(values) > 1:
        values = [a + b for a, b in zip(values[::2], values[1::2])]
    return values[0]


def gelu_slope(value):
    inner = 0.7978845608028654 * (value + 0.044715 * value * value * value)
    turned = jnp.tanh(inner)
    slope = 0.7978845608028654 * (1.0 + 3.0 * 0.044715 * value * value)
    return 0.5 * (1.0 + turned) + 0.5 * value * (1.0 - turned * turned) * slope


def places_here():
    return lax.axis_index("ctx"), lax.axis_index("wa")


def meet_all():
    c, w = places_here()
    owner = c // 2
    own = owner == w
    barrier = pltpu.get_barrier_semaphore()
    for j in range(1, 8):
        signal_to(barrier, c ^ j, w)
    for j in range(1, 4):
        signal_to(barrier, c, w ^ j)
    for j in range(1, 8):
        signal_to(barrier, c ^ j, owner)
    for r in range(4):
        for h in range(2):

            @pl.when(jnp.logical_not(jnp.logical_and(2 * w + h == c, r == 0)))
            def _(r=r, h=h):
                signal_to(barrier, 2 * w + h, w ^ r)

    @pl.when(jnp.logical_not(own))
    def _():
        signal_to(barrier, c, owner)

    pl.semaphore_wait(barrier, 26 - 2 * own.astype(jnp.int32))


def meet_lines():
    c, w = places_here()
    barrier = pltpu.get_barrier_semaphore()
    for j in range(1, 8):
        signal_to(barrier, c ^ j, w)
    for j in range(1, 4):
        signal_to(barrier, c, w ^ j)
    pl.semaphore_wait(barrier, 10)


def remote(source, target, send, recv, ctx, wa):
    return pltpu.make_async_remote_copy(
        src_ref=source,
        dst_ref=target,
        send_sem=send,
        recv_sem=recv,
        device_id=(ctx, wa),
        device_id_type=mesh_id,
    )


class GatherRows:

    def __init__(self, buf, send, recv):
        self.buf, self.send, self.recv = buf, send, recv
        self.c, self.w = places_here()

    def copy(self, k):
        source, entry, j = ((0, 1, 1), (0, 2, 2), (2, 3, 1))[k]
        return remote(
            self.buf.at[source],
            self.buf.at[entry],
            self.send.at[k],
            self.recv.at[k],
            self.c,
            self.w ^ j,
        )

    def start(self):
        self.copy(1).start()
        self.copy(0).start()

    def near(self):
        self.copy(0).wait()

    def relay(self):
        self.copy(1).wait()
        self.copy(2).start()

    def far(self):
        self.copy(2).wait()


class SumRows:

    def __init__(self, out_buf, in_buf, send, recv):
        self.out, self.inn, self.send, self.recv = out_buf, in_buf, send, recv
        self.c, self.w = places_here()

    def copy(self, k):
        j = (1, 1, 2)[k]
        return remote(
            self.out.at[k], self.inn.at[k], self.send.at[k], self.recv.at[k], self.c, self.w ^ j
        )

    def give_near(self, value):
        self.out[0] = value.astype(bf16)
        self.copy(0).start()

    def give_far(self, value):
        self.out[1] = value.astype(bf16)
        self.copy(1).start()

    def pass_on(self, value):
        self.copy(1).wait()
        self.out[2] = (value + self.inn[1].astype(f32)).astype(bf16)
        self.copy(2).start()

    def total(self, value):
        self.copy(0).wait()
        value = value + self.inn[0].astype(f32)
        self.copy(2).wait()
        return value + self.inn[2].astype(f32)


class CtxSum:

    def __init__(self, send, recv, x=None, half=None, part=None, share=None, out=None, spread=0):
        self.send, self.recv = send, recv
        self.x, self.half, self.part, self.share, self.out = x, half, part, share, out
        self.spread = spread
        self.c, self.w = places_here()
        self.z, self.y = self.c // 2, self.c % 2

    def y_copy(self):
        return remote(
            self.x.at[:, 1 - self.y], self.half, self.send.at[0], self.recv.at[0], self.c ^ 1, self.w
        )

    def start_y(self):
        self.y_copy().start()

    def finish_y(self):
        self.y_copy().wait()
        for z in range(4):
            mine = self.x[z, self.y].astype(f32)
            self.half[z] = (self.half[z].astype(f32) + mine).astype(bf16)

    def z_copy(self, j):
        return remote(
            self.half.at[self.z ^ j],
            self.part.at[j - 1],
            self.send.at[j],
            self.recv.at[j],
            self.c ^ (2 * j),
            self.w,
        )

    def start_z(self):
        for j in (2, 3, 1):
            self.z_copy(j).start()

    def finish_z(self):
        total = self.half[self.z].astype(f32)
        for j in (1, 2, 3):
            self.z_copy(j).wait()
            total = total + self.part[j - 1].astype(f32)
        self.share[...] = total.astype(bf16)

    def columns(self, place):
        width = self.spread
        return self.out.at[self.z, self.y, :, pl.ds(pl.multiple_of(place * width, 128), width)]

    def wa_copy(self, j, place):
        return remote(
            self.share.at[self.w ^ j],
            self.columns(place),
            self.send.at[3 + j],
            self.recv.at[3 + j],
            self.c,
            self.w ^ j,
        )

    def own_copy(self):
        source = self.share.at[self.w] if self.spread else self.share
        target = self.columns(self.w) if self.spread else self.out.at[self.z, self.y]
        return pltpu.make_async_copy(source, target, self.send.at[11])

    def start_wa(self):
        if self.spread:
            for j in (2, 3, 1):
                self.wa_copy(j, self.w).start()
        self.own_copy().start()

    def finish_wa(self):
        self.own_copy().wait()
        if self.spread:
            for j in (1, 2, 3):
                self.wa_copy(j, self.w).wait_send()
                self.wa_copy(j, self.w ^ j).wait_recv()

    def back_z_copy(self, j, z):
        mine = self.out.at[z, self.y]
        return remote(mine, mine, self.send.at[6 + j], self.recv.at[6 + j], self.c ^ (2 * j), self.w)

    def start_back_z(self):
        for j in (2, 3, 1):
            self.back_z_copy(j, self.z).start()

    def finish_back_z(self):
        for j in (1, 2, 3):
            self.back_z_copy(j, self.z).wait_send()
            self.back_z_copy(j, self.z ^ j).wait_recv()

    def back_y_copy(self, y):
        part = self.out.at[:, y]
        return remote(part, part, self.send.at[10], self.recv.at[10], self.c ^ 1, self.w)

    def start_back_y(self):
        self.back_y_copy(self.y).start()

    def finish_back_y(self):
        self.back_y_copy(self.y).wait_send()
        self.back_y_copy(1 - self.y).wait_recv()


def put_shares(target, grads, first=0):
    count = grads.shape[0] // 32
    padded = target.shape[3]
    for place in range(4):
        for share in range(8):
            start = (place * 8 + share) * count
            part = grads[start : start + count]
            part = jnp.concatenate([part, jnp.zeros((padded - count, part.shape[1]), f32)], axis=0)
            target[share // 2, share % 2, place, :, first : first + part.shape[1]] = part.astype(bf16)


def put_rows(target, grads):
    count = grads.shape[0] // 8
    for share in range(8):
        target[share // 2, share % 2] = grads[share * count : (share + 1) * count].astype(bf16)


class Cut:

    def __init__(self, ref, start):
        self.ref, self.start = ref, start

    @property
    def at(self):
        return self

    def __getitem__(self, k):
        return self.ref.at[self.start + k]


class Pool:
    def __init__(self, ref):
        self.ref, self.used = ref, 0

    def take(self, count):
        cut = Cut(self.ref, self.used)
        self.used += count
        return cut


class LineGather:

    def __init__(self, out, send, recv):
        self.out, self.send, self.recv = out, send, recv
        self.c, self.w = places_here()
        self.z = self.c // 2
        self.right, self.left = self.z < 3, self.z > 0

    def y_copy(self, block, slot):
        ref = self.out.at[block]
        return remote(ref, ref, self.send.at[slot], self.recv.at[slot], self.c ^ 1, self.w)

    def z_copy(self, block, slot, step):
        k = slot + (7 if step > 0 else 10)
        ref = self.out.at[block]
        return remote(ref, ref, self.send.at[k], self.recv.at[k], self.c + step, self.w)

    def start(self):
        @pl.when(self.right)
        def _():
            self.z_copy(self.c, 0, 2).start()

        @pl.when(self.left)
        def _():
            self.z_copy(self.c, 0, -2).start()

        self.y_copy(self.c, 0).start()

    def step(self, t):
        @pl.when(self.z > t)
        def _():
            block = self.c - 2 * (t + 1)
            self.z_copy(block, t, 2).wait_recv()
            if t < 2:

                @pl.when(self.right)
                def _():
                    self.z_copy(block, t + 1, 2).start()

            self.y_copy(block, t + 1).start()

        @pl.when(self.z < 3 - t)
        def _():
            block = self.c + 2 * (t + 1)
            self.z_copy(block, t, -2).wait_recv()
            if t < 2:

                @pl.when(self.left)
                def _():
                    self.z_copy(block, t + 1, -2).start()

            self.y_copy(block, t + 4).start()

    def finish(self):
        self.y_copy(self.c, 0).wait_send()
        self.y_copy(self.c ^ 1, 0).wait_recv()
        for t in range(3):
            for step, at, near in ((-2, t + 1, self.z > t), (2, t + 4, self.z < 3 - t)):

                @pl.when(near)
                def _(step=step, at=at):
                    self.y_copy(self.c + step * (t + 1), at).wait_send()
                    self.y_copy((self.c ^ 1) + step * (t + 1), at).wait_recv()

        @pl.when(self.right)
        def _():
            self.z_copy(self.c, 0, 2).wait_send()

        @pl.when(self.left)
        def _():
            self.z_copy(self.c, 0, -2).wait_send()

        for t in range(2):

            @pl.when(jnp.logical_and(self.z > t, self.right))
            def _():
                self.z_copy(self.c, t + 1, 2).wait_send()

            @pl.when(jnp.logical_and(self.z < 3 - t, self.left))
            def _():
                self.z_copy(self.c, t + 1, -2).wait_send()


class Columns:

    def __init__(self, source, target, width, first, send, recv, at=None):
        self.source, self.target, self.width, self.first = source, target, width, first
        self.send, self.recv, self.column = send, recv, at
        self.shared = at is None
        self.c, self.w = places_here()
        self.y = self.c % 2

    def taken(self, place, half=None):
        start = place * self.width if self.column is None else self.column
        rows = self.source.shape[0]
        which = slice(None) if half is None else pl.ds(pl.multiple_of(half * (rows // 2), 16), rows // 2)
        return self.source.at[which, pl.ds(pl.multiple_of(start, 128), self.width)]

    def put(self, place, half=None):
        rows = self.source.shape[0]
        start, count = place * rows, rows
        if half is not None:
            start, count = start + half * (rows // 2), rows // 2
        return self.target.at[
            pl.ds(pl.multiple_of(start, 16), count), self.first : self.first + self.width
        ]

    def copy(self, j, place):
        half = self.y if self.shared and j > 1 else None
        return remote(
            self.taken(self.w ^ j, half),
            self.put(place, half),
            self.send.at[j],
            self.recv.at[j],
            self.c,
            self.w ^ j,
        )

    def passed(self, j, half):
        ref = self.put(self.w ^ j, half)
        return remote(ref, ref, self.send.at[2 + j], self.recv.at[2 + j], self.c ^ 1, self.w)

    def own(self):
        return pltpu.make_async_copy(self.taken(self.w), self.put(self.w), self.send.at[0])

    def start(self):
        for j in (2, 3, 1):
            self.copy(j, self.w).start()
        self.own().start()

    def relay(self):
        for j in (2, 3):
            self.copy(j, self.w).wait_send()
            self.copy(j, self.w ^ j).wait_recv()
            self.passed(j, self.y).start()

    def finish(self):
        self.own().wait()
        for j in (1,) if self.shared else (1, 2, 3):
            self.copy(j, self.w).wait_send()
            self.copy(j, self.w ^ j).wait_recv()
        if self.shared:
            for j in (2, 3):
                self.passed(j, self.y).wait_send()
                self.passed(j, 1 - self.y).wait_recv()


class SmallSum:

    def __init__(self, ref, got, axis, send, recv):
        self.ref, self.got, self.axis, self.send, self.recv = ref, got, axis, send, recv
        self.c, self.w = places_here()

    def copy(self, k):
        j = k + 1
        ctx, wa = (self.c ^ j, self.w) if self.axis == "ctx" else (self.c, self.w ^ j)
        return remote(self.ref, self.got.at[k], self.send.at[k], self.recv.at[k], ctx, wa)

    def start(self):
        for k in range(self.got.shape[0]):
            self.copy(k).start()

    def finish(self):
        count = self.got.shape[0]
        for k in range(count):
            self.copy(k).wait()
        self.ref[...] = tree_sum([self.ref[...]] + [self.got[k] for k in range(count)])


class SwapHeads:

    def __init__(self, by_heads, by_rows, outward, send, recv):
        self.heads, self.rows, self.outward = by_heads, by_rows, outward
        self.send, self.recv = send, recv
        self.c, self.w = places_here()
        self.owner, self.half = self.c // 2, self.c % 2
        self.own = self.owner == self.w
        self.other = jnp.logical_not(self.own)

    def lanes(self):
        return pl.ds(pl.multiple_of(self.half * 128, 128), 128)

    def out_copy(self, j):
        slot = self.w ^ self.owner
        return remote(
            self.heads.at[self.c ^ j],
            self.rows.at[slot, :, self.lanes()],
            self.send.at[j],
            self.recv.at[slot * 2 + self.half],
            self.c ^ j,
            self.owner,
        )

    def start_out(self):
        for j in range(7, 0, -1):
            self.out_copy(j).start()

        @pl.when(self.other)
        def _():
            self.out_copy(0).start()

        @pl.when(self.own)
        def _():
            slot = self.w ^ self.owner
            pltpu.make_async_copy(
                self.heads.at[self.c],
                self.rows.at[slot, :, self.lanes()],
                self.recv.at[slot * 2 + self.half],
            ).start()

    def wait_rows(self, r):
        for h in range(2):
            remote(
                self.heads.at[0],
                self.rows.at[r, :, h * 128 : (h + 1) * 128],
                self.send.at[0],
                self.recv.at[r * 2 + h],
                self.c ^ 1,
                self.w,
            ).wait_recv()

    def finish_out(self):
        for j in range(1, 8):
            self.out_copy(j).wait_send()

        @pl.when(self.other)
        def _():
            self.out_copy(0).wait_send()

    def in_copy(self, r, h):
        return remote(
            self.rows.at[r, :, h * 128 : (h + 1) * 128],
            self.heads.at[self.c],
            self.send.at[r * 2 + h],
            self.recv.at[self.c],
            2 * self.w + h,
            self.w ^ r,
        )

    def mine(self, r, h):
        return jnp.logical_and(2 * self.w + h == self.c, r == 0)

    def start_in(self, r):
        for h in range(2):

            @pl.when(jnp.logical_not(self.mine(r, h)))
            def _():
                self.in_copy(r, h).start()

            @pl.when(self.mine(r, h))
            def _():
                pltpu.make_async_copy(
                    self.rows.at[r, :, h * 128 : (h + 1) * 128],
                    self.heads.at[self.c],
                    self.recv.at[self.c],
                ).start()

    def finish_in(self):
        for block in range(8):
            remote(
                self.rows.at[0, :, 0:128],
                self.heads.at[block],
                self.send.at[0],
                self.recv.at[block],
                self.c ^ 1,
                self.w,
            ).wait_recv()
        for r in range(4):
            for h in range(2):

                @pl.when(jnp.logical_not(self.mine(r, h)))
                def _(r=r, h=h):
                    self.in_copy(r, h).wait_send()


def layer_kernel(names, total_tokens, block, *refs):
    v = types.SimpleNamespace(**dict(zip(names, refs, strict=True)))
    c, w = places_here()
    send, recv, local = Pool(v.send), Pool(v.recv), Pool(v.local)
    tok, width = v.tokens.shape
    seq_len = 8 * tok
    rows = 4 * tok
    cols = v.output_w.shape[0]
    hidden = v.down_w.shape[0]
    scale = HEAD_DIM ** (-0.5)

    def load(source, target):
        copy = pltpu.make_async_copy(source, target, local.take(1).at[0])
        copy.start()
        return copy

    near_load = load(v.neighbours, v.near.at[0])
    early = [load(v.waves_any, v.waves)]
    late = [
        load(v.output_any, v.output_w),
        load(v.cross_out_any, v.cross_out_w),
        load(v.down_any, v.down_w),
    ]
    column = lax.broadcasted_iota(jnp.int32, (256, 1024), 1)
    line = lax.broadcasted_iota(jnp.int32, (256, 1024), 0)

    def placed(value, start):
        chosen = jnp.where(column == line + start, 1.0, 0.0).astype(bf16)
        return dot_nn(value, chosen[: value.shape[1]])

    v.small_all[...] = placed(v.gain_rows[...], w * (width // 4)) + placed(v.bias_rows[...], w * cols)
    mask = v.mask[...].astype(f32)
    v.small_all[5:6, :] = jnp.broadcast_to(jnp.sum(mask, keepdims=True), (1, 1024))
    v.tokens_all[c] = v.tokens[...]
    meet_all()

    near_sum = SmallSum(v.small_all, v.small_near, "wa", send.take(3), recv.take(3))
    count_sum = SmallSum(v.count, v.count_far, "ctx", send.take(7), recv.take(7))
    gather = LineGather(v.tokens_all, send.take(13), recv.take(13))
    pair = [
        Columns(weight, v.pair, 128, 128 * m, send.take(4), recv.take(4), c * 128)
        for m, weight in enumerate((v.query_any, v.key_any, v.value_any, v.relative_any))
    ]
    cross = [
        Columns(weight, target, cols, first, send.take(6), recv.take(6))
        for weight, target, first in (
            (v.cross_key_any, v.pair_cols, 0),
            (v.cross_value_any, v.pair_cols, cols),
            (v.cross_query_any, v.query_cols, 0),
        )
    ]
    up_columns = Columns(v.up_any, v.up_cols, hidden, 0, send.take(6), recv.take(6))
    near_send, near_recv = send.take(3), recv.take(3)
    near_gather = GatherRows(v.near, near_send, near_recv)
    gather.start()
    near_sum.start()
    for part in pair:
        part.start()
    near_load.wait()
    near_gather.start()
    for part in cross:
        part.start()
    up_columns.start()
    gather.step(0)
    near_sum.finish()
    v.count[...] = jnp.broadcast_to(v.small_all[5:6, 0:128], v.count.shape)
    count_sum.start()
    gather.step(1)
    for part in pair:
        part.finish()
    for copy in early:
        copy.wait()
    v.table[0:seq_len, :] = dot_nn(v.waves[...], v.pair[:, 384:512]).astype(bf16)
    v.table[seq_len:, :] = jnp.zeros((TILE, 128), bf16)
    v.biases[...] = v.small_all[:, pl.ds(pl.multiple_of(c * 128, 128), 128)]
    v.gains[...] = v.small_all[:, 0:width]
    gather.step(2)
    gather.finish()
    gain_one, gain_two, gain_three = (v.gains[k : k + 1, :] for k in range(3))

    def project(part, carry):
        start = pl.multiple_of(part * tok, tok)
        value = v.tokens_all[part].astype(f32)
        normed = (value * inverse_rms(value) * gain_one).astype(bf16)
        v.normed_a[pl.ds(start, tok), :] = normed
        mixed = dot_nn(normed, v.pair[:, 0:384]).astype(bf16)
        for h in range(tok // block):
            v.qkv[part * (tok // block) + h] = mixed[h * block : (h + 1) * block]
        return carry

    lax.fori_loop(0, 8, project, 0)
    leaving = Leaving(v, local)
    leaving.leave("normed_a")
    for place in range(seq_len // block):
        take_block(v.qkv, v.inverse, place, v.qkv_order.at[place * block : (place + 1) * block, :])
    attend_tiles(v.qkv_order, v.table, v.biases[3:4, :], v.biases[4:5, :], v.heads_order)
    per = tok // block
    for place in range(seq_len // block):
        at = (place % per) * block
        take_block(v.heads_order, v.order, place, v.heads.at[place // per, at : at + block, :])
    out_swap = SwapHeads(v.heads, v.attended, True, send.take(8), recv.take(8))
    out_swap.start_out()
    for copy in late:
        copy.wait()

    gathers = [GatherRows(ref, send.take(3), recv.take(3)) for ref in (v.rows_b, v.rows_c)]
    sums = [SumRows(v.give.at[k], v.take.at[k], send.take(3), recv.take(3)) for k in range(3)]

    def output_part(r):
        return dot_nn(v.attended[r], v.output_w[...])

    out_swap.wait_rows(3)
    sums[0].give_far(output_part(3))
    out_swap.wait_rows(1)
    sums[0].give_near(output_part(1))
    out_swap.wait_rows(2)
    sums[0].pass_on(output_part(2))
    near_gather.near()
    near_gather.relay()
    for part in cross:
        part.relay()
    up_columns.relay()
    out_swap.wait_rows(0)
    v.hidden_one[...] = v.tokens[...].astype(f32) + sums[0].total(output_part(0))
    value = v.hidden_one[...]
    v.rows_b[0] = (value * inverse_rms(value) * gain_two).astype(bf16)

    gathers[0].start()
    out_swap.finish_out()
    near_gather.far()
    for part in cross:
        part.finish()
    leaving.leave("pair_cols")
    near_count = v.near.shape[1]

    def near_project(r, carry):
        start = pl.multiple_of(r * near_count, near_count)
        v.cross_pair[pl.ds(start, near_count), :] = dot_nn(v.near[r], v.pair_cols[...]).astype(bf16)
        return carry

    lax.fori_loop(0, 4, near_project, 0)

    def cross_part(r):
        v.cross_q[r * tok : (r + 1) * tok, :] = dot_nn(v.rows_b[r], v.query_cols[...]).astype(bf16)

        def group(g, carry):
            at = pl.multiple_of(r * tok + g * GROUP, GROUP)
            near = pl.multiple_of((r * (tok // GROUP) + g) * NK, NK)
            query = stack_all(v.cross_q[pl.ds(at, GROUP), :])
            shares = cross_shares(query, v.cross_pair[pl.ds(near, NK), 0:cols])
            out = dot_nn(shares.astype(bf16), v.cross_pair[pl.ds(near, NK), cols:])
            v.crossed[pl.ds(at, GROUP), :] = join_all(out).astype(bf16)
            return carry

        lax.fori_loop(0, tok // GROUP, group, 0, unroll=True)
        return dot_nn(v.crossed[r * tok : (r + 1) * tok, :], v.cross_out_w[...])

    def in_turn(gathered, summed, part, between=None):
        v.keep[0] = part(0)
        gathered.near()
        summed.give_near(part(1))
        gathered.relay()
        v.keep[2] = part(2)
        gathered.far()
        summed.give_far(part(3))
        summed.pass_on(v.keep[2])
        if between is not None:
            between()
        return summed.total(v.keep[0])

    v.hidden_two[...] = v.hidden_one[...] + in_turn(gathers[0], sums[1], cross_part)
    value = v.hidden_two[...]
    v.rows_c[0] = (value * inverse_rms(value) * gain_three).astype(bf16)

    gathers[1].start()
    up_columns.finish()

    def feed_part(r):
        part = pl.ds(r * tok, tok)
        v.pre_act[part, :] = dot_nn(v.rows_c[r], v.up_cols[...])
        v.activated[part, :] = gelu_tanh(v.pre_act[part, :]).astype(bf16)
        return dot_nn(v.activated[part, :], v.down_w[...])

    layer_out = v.hidden_two[...] + in_turn(gathers[1], sums[2], feed_part)
    v.layer_out[...] = layer_out

    count_sum.finish()
    error = layer_out - v.teacher[...].astype(f32)
    square = (tok, tok)
    same = lax.broadcasted_iota(jnp.int32, square, 0) == lax.broadcasted_iota(jnp.int32, square, 1)
    valid = jnp.sum(jnp.where(same, mask, 0.0), axis=1, keepdims=True)
    weighted = valid * error
    v.small[0:5, :] = jnp.zeros((5, 1024), f32)
    v.small[5:6, :] = jnp.broadcast_to(jnp.sum(weighted * error, keepdims=True), (1, 1024))
    v.small[6:8, :] = jnp.broadcast_to(v.count[0:1, 0:1], (2, 1024))
    v.out_grad[...] = (total_tokens / v.count[0:1, 0:1]) * weighted

    leaving.leave("layer_out")
    middle_back(v, send, recv, leaving, block)
    leaving.finish()


class Leaving:

    def __init__(self, v, local):
        self.v, self.local, self.copies = v, local, []

    def leave(self, name):
        copy = pltpu.make_async_copy(
            getattr(self.v, name), getattr(self.v, name + "_any"), self.local.take(1).at[0]
        )
        copy.start()
        self.copies.append(copy)

    def finish(self):
        for copy in self.copies:
            copy.wait()


def take_block(source, chosen, place, target):
    target[...] = source[chosen[place]]


def middle_back(v, send, recv, leaving, block):
    c, w = places_here()
    tok, width = v.tokens.shape
    rows = 4 * tok
    cols = v.output_w.shape[0]
    scale = HEAD_DIM ** (-0.5)
    first, second, third = (
        GatherRows(ref, send.take(3), recv.take(3)) for ref in (v.rows_o, v.rows_two, v.rows_one)
    )
    sum_c, sum_b = (
        SumRows(v.give.at[k], v.take.at[k], send.take(3), recv.take(3)) for k in (3, 4)
    )
    down = CtxSum(send.take(12), recv.take(12), v.down_x, v.down_half, v.down_part, v.down_share)
    up = CtxSum(send.take(12), recv.take(12), v.up_x, v.up_half, v.up_part, v.up_share)
    cross = CtxSum(
        send.take(12), recv.take(12), v.cross_x, v.cross_half, v.cross_part, v.cross_share
    )
    ctx_o = CtxSum(send.take(12), recv.take(12), v.cross_out_x, v.ctx_o_half)
    out_o = CtxSum(send.take(12), recv.take(12), v.output_x, v.out_o_half)
    heads = SwapHeads(v.heads_grad, v.heads_out, False, send.take(8), recv.take(8))
    v.rows_o[0] = v.out_grad[...].astype(bf16)

    first.start()

    def feed_back(r):
        part = pl.ds(r * tok, tok)
        act_grad = dot_nt(v.rows_o[r], v.down_w[...])
        v.pre_grad[part, :] = (act_grad * gelu_slope(v.pre_act[part, :])).astype(bf16)
        return dot_nt(v.pre_grad[part, :], v.up_cols[...])

    v.keep[0] = feed_back(0)
    first.near()
    sum_c.give_near(feed_back(1))
    first.relay()
    v.keep[1] = feed_back(2)
    first.far()
    sum_c.give_far(feed_back(3))
    sum_c.pass_on(v.keep[1])
    put_rows(v.down_x, dot_tn(v.activated[...], v.rows_o[...].reshape(rows, width)))
    down.start_y()
    put_shares(v.up_x, dot_tn(v.rows_c[...].reshape(rows, width), v.pre_grad[...]))
    up.start_y()
    normed_grad = sum_c.total(v.keep[0])
    value = v.hidden_two[...]
    inverse = inverse_rms(value)
    two_grad = v.out_grad[...] + norm_pull(value, inverse, v.gains[2:3, :], normed_grad)
    gain_three = jnp.sum(normed_grad * value * inverse, axis=0, keepdims=True)
    v.keep[1] = two_grad
    v.rows_two[0] = two_grad.astype(bf16)

    second.start()

    def cross_back(r):
        part = slice(r * tok, (r + 1) * tok)
        v.crossed_grad[...] = dot_nt(v.rows_two[r], v.cross_out_w[...]).astype(bf16)

        def group(g, carry):
            within = pl.multiple_of(g * GROUP, GROUP)
            at = pl.multiple_of(r * tok + g * GROUP, GROUP)
            near = pl.ds(pl.multiple_of((r * (tok // GROUP) + g) * NK, NK), NK)
            query = stack_all(v.cross_q[pl.ds(at, GROUP), :])
            grad = stack_all(v.crossed_grad[pl.ds(within, GROUP), :])
            keys = v.cross_pair[near, 0:cols]
            shares = cross_shares(query, keys)
            share_grad = dot_nt(grad, v.cross_pair[near, cols:])
            delta = jnp.sum(shares * share_grad, axis=1, keepdims=True)
            score_grad = (shares * (share_grad - delta)).astype(bf16)
            query_grad = join_all(dot_nn(score_grad, keys)) * scale
            v.cross_grad[pl.ds(at, GROUP), :] = query_grad.astype(bf16)
            v.pair_grad[near, 0:cols] = (dot_tn(score_grad, query) * scale).astype(bf16)
            v.pair_grad[near, cols:] = dot_tn(shares.astype(bf16), grad).astype(bf16)
            return carry

        lax.fori_loop(0, tok // GROUP, group, 0, unroll=True)
        return dot_nt(v.cross_grad[part, :], v.query_cols[...])

    v.keep[0] = cross_back(0)
    second.near()
    sum_b.give_near(cross_back(1))
    second.relay()
    v.keep[2] = cross_back(2)
    second.far()
    down.finish_y()
    down.start_z()
    sum_b.give_far(cross_back(3))
    sum_b.pass_on(v.keep[2])
    leaving.leave("pair_grad")
    normed_b = v.rows_b[...].reshape(rows, width)
    put_rows(v.cross_out_x, dot_tn(v.crossed[...], v.rows_two[...].reshape(rows, width)))
    ctx_o.start_y()
    put_shares(v.cross_x, dot_tn(normed_b, v.cross_grad[...]), 0)
    normed_grad = sum_b.total(v.keep[0])
    value = v.hidden_one[...]
    inverse = inverse_rms(value)
    one_grad = v.keep[1] + norm_pull(value, inverse, v.gains[1:2, :], normed_grad)
    gain_two = jnp.sum(normed_grad * value * inverse, axis=0, keepdims=True)
    v.small[1:2, 0:width] = gain_two
    v.small[2:3, 0:width] = gain_three
    v.one_grad[...] = one_grad
    leaving.leave("one_grad")
    v.rows_one[0] = one_grad.astype(bf16)

    third.start()
    near = v.near[...].reshape(-1, width)
    put_shares(v.cross_x, dot_tn(near, v.pair_grad[...]), cols)
    cross.start_y()

    def head_back(r):
        v.heads_out[r] = dot_nt(v.rows_one[r], v.output_w[...]).astype(bf16)
        heads.start_in(r)

    head_back(0)
    third.near()
    head_back(1)
    third.relay()
    head_back(2)
    third.far()
    head_back(3)
    up.finish_y()
    up.start_z()
    attended = jnp.concatenate([v.attended[r] for r in range(4)], axis=0)
    put_rows(v.output_x, dot_tn(attended, v.rows_one[...].reshape(rows, width)))
    out_o.start_y()
    heads.finish_in()
    leaving.leave("gains")
    cross.finish_y()
    cross.start_z()

    per = tok // block
    for place in range(8 * per):
        at = (place % per) * block
        v.heads_stored[place] = v.heads_grad[place // per, at : at + block, :]
    for place in range(8 * per):
        take_block(
            v.heads_stored, v.inverse, place, v.grad_order.at[place * block : (place + 1) * block, :]
        )

    def poll(tile):
        if tile == 1:
            down.finish_z()
            leaving.leave("down_share")
        if tile == 3:
            ctx_o.finish_y()
            leaving.leave("ctx_o_half")
        if tile == 4:
            up.finish_z()
            leaving.leave("up_share")
        if tile == 6:
            out_o.finish_y()
            leaving.leave("out_o_half")

    content_sum, position_sum = attend_back_tiles(
        v.qkv_order,
        v.grad_order,
        v.table,
        v.biases[3:4, :],
        v.biases[4:5, :],
        v.qkv_grad_order,
        v.dkey,
        v.dvalue,
        v.drel,
        poll,
    )
    v.table_grad[...] = v.drel[0 : v.table_grad.shape[0], :] * scale
    leaving.leave("table_grad")
    both = jnp.concatenate([content_sum, position_sum] * 4, axis=1)
    pairs = lax.broadcasted_iota(jnp.int32, both.shape, 1) // 256
    v.small[3:4, :] = jnp.where(pairs == c, both, 0.0)
    v.small[4:5, :] = jnp.where(pairs + 4 == c, both, 0.0)
    leaving.leave("small")
    for place in range(8 * per):
        at = (place % per) * block
        take_block(
            v.qkv_grad_order, v.order, place, v.query_grad.at[place // per, at : at + block, :]
        )
    leaving.leave("query_grad")
    cross.finish_z()
    leaving.leave("cross_share")


def layer(total_tokens, block, orders, given, collective_id):
    tok, width = given["tokens"].shape
    hidden = given["down_any"].shape[0]
    cols = given["output_any"].shape[0]
    near = given["neighbours"].shape[0]
    seq_len = 8 * tok
    rows = 4 * tok
    padded = -(-(width // 32) // 8) * 8
    any_space = pl.BlockSpec(memory_space=pl.ANY)
    shape = jax.ShapeDtypeStruct
    vmem = pltpu.VMEM
    dma = pltpu.SemaphoreType.DMA
    kept = dict(
        layer_out=shape((tok, width), f32),
        small=shape((8, 1024), f32),
        gains=shape((8, width), f32),
        normed_a=shape((seq_len, width), bf16),
        pair_cols=shape((width, 2 * cols), bf16),
        one_grad=shape((tok, width), f32),
        pair_grad=shape((4 * near, 2 * cols), bf16),
        query_grad=shape((8, tok, 384), bf16),
        table_grad=shape((seq_len, 128), f32),
        down_share=shape((hidden // 8, width), bf16),
        up_share=shape((4, padded, hidden), bf16),
        cross_share=shape((4, padded, 3 * cols), bf16),
        ctx_o_half=shape((4, cols // 8, width), bf16),
        out_o_half=shape((4, cols // 8, width), bf16),
    )
    results = {name + "_any": value for name, value in kept.items()}
    scratch = dict(
        small_all=vmem((8, 1024), f32),
        small_near=vmem((3, 8, 1024), f32),
        qkv=vmem((seq_len // block, block, 384), bf16),
        table=vmem((seq_len + TILE, 128), bf16),
        biases=vmem((8, 128), f32),
        count=vmem((8, 128), f32),
        heads_grad=vmem((8, tok, 128), bf16),
        grad_order=vmem((seq_len, 128), bf16),
        qkv_grad_order=vmem((seq_len // block, block, 384), bf16),
        dkey=vmem((seq_len, 128), f32),
        dvalue=vmem((seq_len, 128), f32),
        drel=vmem((seq_len + TILE, 128), f32),
        cross_half=vmem((4, 4, padded, 3 * cols), bf16),
        cross_part=vmem((3, 4, padded, 3 * cols), bf16),
        cross_out_x=vmem((4, 2, cols // 8, width), bf16),
        output_x=vmem((4, 2, cols // 8, width), bf16),
        count_far=vmem((7, 8, 128), f32),
        tokens_all=vmem((8, tok, width), bf16),
        pair=vmem((width, 512), bf16),
        waves=vmem((seq_len, width), bf16),
        qkv_order=vmem((seq_len, 384), bf16),
        heads_order=vmem((seq_len // block, block, 128), bf16),
        heads_stored=vmem((seq_len // block, block, 128), bf16),
        heads=vmem((8, tok, 128), bf16),
        attended=vmem((4, tok, cols), bf16),
        near=vmem((4, near, width), bf16),
        query_cols=vmem((width, cols), bf16),
        up_cols=vmem((width, hidden), bf16),
        output_w=vmem((cols, width), bf16),
        cross_out_w=vmem((cols, width), bf16),
        down_w=vmem((hidden, width), bf16),
        cross_pair=vmem((4 * near, 2 * cols), bf16),
        cross_q=vmem((rows, cols), bf16),
        crossed=vmem((rows, cols), bf16),
        crossed_grad=vmem((tok, cols), bf16),
        hidden_one=vmem((tok, width), f32),
        hidden_two=vmem((tok, width), f32),
        out_grad=vmem((tok, width), f32),
        pre_act=vmem((rows, hidden), f32),
        activated=vmem((rows, hidden), bf16),
        rows_b=vmem((4, tok, width), bf16),
        rows_c=vmem((4, tok, width), bf16),
        rows_o=vmem((4, tok, width), bf16),
        rows_two=vmem((4, tok, width), bf16),
        rows_one=vmem((4, tok, width), bf16),
        give=vmem((5, 3, tok, width), bf16),
        take=vmem((5, 3, tok, width), bf16),
        keep=vmem((3, tok, width), f32),
        pre_grad=vmem((rows, hidden), bf16),
        cross_grad=vmem((rows, cols), bf16),
        heads_out=vmem((4, tok, cols), bf16),
        down_x=vmem((4, 2, hidden // 8, width), bf16),
        down_half=vmem((4, hidden // 8, width), bf16),
        down_part=vmem((3, hidden // 8, width), bf16),
        up_x=vmem((4, 2, 4, padded, hidden), bf16),
        up_half=vmem((4, 4, padded, hidden), bf16),
        up_part=vmem((3, 4, padded, hidden), bf16),
        cross_x=vmem((4, 2, 4, padded, 3 * cols), bf16),
        send=dma((232,)),
        recv=dma((232,)),
        local=dma((24,)),
    )
    scratch.update({name: vmem(value.shape, value.dtype) for name, value in kept.items()})
    names = [*orders, *given, *results, *scratch]
    specs = [in_smem] * len(orders) + [
        any_space if name.endswith("_any") or name == "neighbours" else in_vmem for name in given
    ]
    got = pl.pallas_call(
        functools.partial(layer_kernel, names, total_tokens, block),
        out_shape=list(results.values()),
        in_specs=specs,
        out_specs=[any_space] * len(results),
        scratch_shapes=list(scratch.values()),
        compiler_params=pltpu.CompilerParams(
            collective_id=collective_id, has_side_effects=True, vmem_limit_bytes=62 * 2**20
        ),
        name="layer",
    )(*orders.values(), *given.values())
    return types.SimpleNamespace(**dict(zip(kept, got, strict=True)))


class Spread:

    def __init__(self, share, out, send, recv):
        self.share, self.out, self.send, self.recv = share, out, send, recv
        self.c, self.w = places_here()

    def columns(self, place):
        width = self.share.shape[2]
        return self.out.at[self.c, :, pl.ds(pl.multiple_of(place * width, 128), width)]

    def copy(self, j, place):
        return remote(
            self.share.at[self.w ^ j],
            self.columns(place),
            self.send.at[j],
            self.recv.at[j],
            self.c,
            self.w ^ j,
        )

    def own(self):
        return pltpu.make_async_copy(
            self.share.at[self.w], self.columns(self.w), self.send.at[0]
        )

    def start(self):
        for j in (2, 3, 1):
            self.copy(j, self.w).start()
        self.own().start()

    def finish(self):
        self.own().wait()
        for j in (1, 2, 3):
            self.copy(j, self.w).wait_send()
            self.copy(j, self.w ^ j).wait_recv()


class Whole:

    def __init__(self, source, target, send, recv):
        self.source, self.target, self.send, self.recv = source, target, send, recv
        self.c, self.w = places_here()

    def put(self, place):
        rows = self.source.shape[0]
        return self.target.at[pl.ds(pl.multiple_of(place * rows, 32), rows), :]

    def copy(self, j, place):
        return remote(
            self.source, self.put(place), self.send.at[j], self.recv.at[j], self.c, self.w ^ j
        )

    def passed(self, place):
        ref = self.put(place)
        return remote(ref, ref, self.send.at[3], self.recv.at[3], self.c, self.w ^ 1)

    def own(self):
        return pltpu.make_async_copy(self.source, self.put(self.w), self.send.at[0])

    def start(self):
        self.copy(2, self.w).start()
        self.copy(1, self.w).start()
        self.own().start()

    def relay(self):
        self.copy(2, self.w).wait_send()
        self.copy(2, self.w ^ 2).wait_recv()
        self.passed(self.w ^ 2).start()

    def finish(self):
        self.own().wait()
        self.copy(1, self.w).wait_send()
        self.copy(1, self.w ^ 1).wait_recv()
        self.passed(self.w ^ 2).wait_send()
        self.passed(self.w ^ 3).wait_recv()


class MaskSum:

    def __init__(self, ref, got, masks, send, recv):
        self.ref, self.got, self.masks, self.send, self.recv = ref, got, masks, send, recv
        self.c, self.w = places_here()

    def copy(self, k):
        ctx, wa = self.masks[k]
        return remote(
            self.ref, self.got.at[k], self.send.at[k], self.recv.at[k], self.c ^ ctx, self.w ^ wa
        )

    def start(self):
        for k in range(len(self.masks)):
            self.copy(k).start()

    def finish(self):
        for k in range(len(self.masks)):
            self.copy(k).wait()
        self.ref[...] = tree_sum([self.ref[...]] + [self.got[k] for k in range(len(self.masks))])


def finish_kernel(names, *refs):
    v = types.SimpleNamespace(**dict(zip(names, refs, strict=True)))
    c, w = places_here()
    send, recv, local = Pool(v.send), Pool(v.recv), Pool(v.local)
    tok, width = v.tokens.shape
    cols = v.out_o_half.shape[1] * 8
    share = width // 4

    def load(source, target):
        copy = pltpu.make_async_copy(source, target, local.take(1).at[0])
        copy.start()
        return copy

    loads = [load(v.normed_a_any, v.normed_a), load(v.waves_any, v.waves)]
    late = [load(v.pair_cols_any, v.pair_cols), load(v.near_any, v.near_rows)]
    leaving = Leaving(v, local)

    def line(out):
        return LineGather(out, send.take(13), recv.take(13))

    def summed(x, half, part, got):
        return CtxSum(send.take(12), recv.take(12), x, half, part, got)

    down, up, cross, ctx_o, out_o, pair = (
        line(out)
        for out in (v.down_out, v.up_all, v.cross_all, v.cross_o_out, v.output_out, v.pair_all)
    )
    ctx_o_sum = summed(None, v.ctx_o_half, v.ctx_o_part, v.ctx_o_share)
    out_o_sum = summed(None, v.out_o_half, v.out_o_part, v.out_o_share)
    up_spread = Spread(v.up_share, v.up_all, send.take(4), recv.take(4))
    cross_spread = Spread(v.cross_share, v.cross_all, send.take(4), recv.take(4))
    sum_pair = SumRows(v.pair_give, v.pair_take, send.take(3), recv.take(3))
    sum_near = SumRows(v.near_give, v.near_take, send.take(3), recv.take(3))
    weights = [
        Whole(weight, v.full.at[m], send.take(4), recv.take(4))
        for m, weight in enumerate((v.query_any, v.key_any, v.value_any))
    ]
    stages = [
        MaskSum(v.total, got, masks, send.take(3), recv.take(3))
        for got, masks in (
            (v.got_wa, ((0, 1), (0, 2), (0, 3))),
            (v.got_y, ((1, 0),)),
            (v.got_z, ((2, 0), (4, 0), (6, 0))),
        )
    ]
    b_send, b_recv = send.take(24), recv.take(24)

    def block_copy(j, m, place):
        return remote(
            v.query_grad.at[c ^ j, :, 128 * m : 128 * (m + 1)],
            v.mine.at[m, :, pl.ds(pl.multiple_of(place * 128, 128), 128)],
            b_send.at[3 * j + m],
            b_recv.at[3 * j + m],
            c ^ j,
            w,
        )

    own_blocks = [
        pltpu.make_async_copy(
            v.query_grad.at[c, :, 128 * m : 128 * (m + 1)],
            v.mine.at[m, :, pl.ds(pl.multiple_of(c * 128, 128), 128)],
            b_recv.at[m],
        )
        for m in range(3)
    ]
    v.down_out[c] = v.down_share[...]
    meet_lines()
    up_spread.start()
    cross_spread.start()
    down.start()
    ctx_o_sum.start_z()
    out_o_sum.start_z()
    for copy in own_blocks:
        copy.start()

    query_grad = v.query_grad[...].reshape(-1, v.query_grad.shape[2])
    high = v.table_grad[...].astype(bf16)
    low = (v.table_grad[...] - high.astype(f32)).astype(bf16)
    for copy in loads:
        copy.wait()
    mixed = dot_tn(v.normed_a[...], query_grad)
    turned = dot_tn(v.waves[...], high) + dot_tn(v.waves[...], low)
    for place in range(4):
        at = place * share
        v.sums[place] = jnp.concatenate([mixed[at : at + share], turned[at : at + share]], axis=1)
    sum_pair.give_far(v.sums[w ^ 3])
    sum_pair.give_near(v.sums[w ^ 1])
    up_spread.finish()
    up.start()
    cross_spread.finish()
    cross.start()
    sum_pair.pass_on(v.sums[w ^ 2])
    down.step(0)
    for j in (4, 6, 5, 7, 2, 3, 1):
        for m in range(3):
            block_copy(j, m, c).start()
    v.pair_all[c] = sum_pair.total(v.sums[w]).astype(bf16)
    pair.start()
    for copy in late:
        copy.wait()
    near_count = v.near_grad.shape[0]

    def near_part(r):
        return dot_nt(v.near_rows[r * near_count : (r + 1) * near_count, :], v.pair_cols[...])

    sum_near.give_far(near_part(3))
    sum_near.give_near(near_part(1))
    sum_near.pass_on(near_part(2))
    for weight in weights:
        weight.start()
    v.near_grad[...] = near_part(0)
    up.step(0)
    down.step(1)
    cross.step(0)
    ctx_o_sum.finish_z()
    v.cross_o_out[c] = v.ctx_o_share[...]
    ctx_o.start()
    out_o_sum.finish_z()
    v.output_out[c] = v.out_o_share[...]
    out_o.start()
    up.step(1)
    cross.step(1)
    pair.step(0)
    down.step(2)
    ctx_o.step(0)
    out_o.step(0)
    up.step(2)
    cross.step(2)
    pair.step(1)
    ctx_o.step(1)
    out_o.step(1)

    for j in range(1, 8):
        for m in range(3):
            block_copy(j, m, c ^ j).wait_recv()
    for copy in own_blocks:
        copy.wait()
    pair.step(2)
    for weight in weights:
        weight.relay()
    for weight in weights:
        weight.finish()
    normed_grad = dot_nt(v.mine[0], v.full[0])
    normed_grad = normed_grad + dot_nt(v.mine[1], v.full[1])
    normed_grad = normed_grad + dot_nt(v.mine[2], v.full[2])
    hidden = v.tokens[...].astype(f32)
    inverse = inverse_rms(hidden)
    v.tokens_grad[...] = v.one_grad[...] + norm_pull(hidden, inverse, v.gains[0:1, :], normed_grad)
    leaving.leave("tokens_grad")
    v.total[...] = v.small[...]
    v.total[0:1, 0:width] = jnp.sum(normed_grad * hidden * inverse, axis=0, keepdims=True)
    stages[0].start()
    ctx_o.step(2)
    out_o.step(2)
    stages[0].finish()
    stages[1].start()
    v.near_grad[...] = sum_near.total(v.near_grad[...])
    leaving.leave("near_grad")
    stages[1].finish()
    stages[2].start()
    down.finish()
    leaving.leave("down_out")
    up.finish()
    used = share // 8
    for part in range(8):
        v.up_out[part * used : (part + 1) * used, :] = v.up_all[part, 0:used, :].astype(f32)
    leaving.leave("up_out")
    pair.finish()
    pair_outs = (v.query_out, v.key_out, v.value_out, v.relative_out)
    for part in range(8):
        for m, out in enumerate(pair_outs):
            out[:, 128 * part : 128 * (part + 1)] = v.pair_all[part, :, 128 * m : 128 * (m + 1)]
    for name in ("query_out", "key_out", "value_out", "relative_out"):
        leaving.leave(name)
    ctx_o.finish()
    leaving.leave("cross_o_out")
    out_o.finish()
    leaving.leave("output_out")
    cross.finish()
    for m, out in enumerate((v.cross_query_out, v.cross_key_out, v.cross_value_out)):
        for part in range(8):
            for place in range(4):
                at = (place * 3 + m) * cols
                out[part * used : (part + 1) * used, place * cols : (place + 1) * cols] = v.cross_all[
                    part, 0:used, at : at + cols
                ].astype(f32)
    for name in ("cross_query_out", "cross_key_out", "cross_value_out"):
        leaving.leave(name)
    stages[2].finish()
    devices = 32.0
    loss = v.total[5:6, :] * devices / (2.0 * width * v.total[6:7, :])
    v.total[7:8, :] = loss
    leaving.leave("total")
    for j in range(1, 8):
        for m in range(3):
            block_copy(j, m, c).wait_send()
    leaving.finish()


def finish(given, collective_id):
    tok, width = given["tokens"].shape
    near = given["near_any"].shape[0]
    padded = given["up_share"].shape[1]
    hidden = given["up_share"].shape[2]
    cols = given["out_o_half"].shape[1] * 8
    share = width // 4
    any_space = pl.BlockSpec(memory_space=pl.ANY)
    shape = jax.ShapeDtypeStruct
    vmem = pltpu.VMEM
    dma = pltpu.SemaphoreType.DMA
    part = (cols // 8, width)
    kept = dict(
        tokens_grad=shape((tok, width), f32),
        near_grad=shape((near // 4, width), f32),
        total=shape(given["small"].shape, f32),
        down_out=shape((8,) + given["down_share"].shape, bf16),
        up_out=shape((share, 4 * hidden), f32),
        cross_query_out=shape((share, 4 * cols), f32),
        cross_key_out=shape((share, 4 * cols), f32),
        cross_value_out=shape((share, 4 * cols), f32),
        cross_o_out=shape((8,) + part, bf16),
        output_out=shape((8,) + part, bf16),
        query_out=shape((share, 1024), bf16),
        key_out=shape((share, 1024), bf16),
        value_out=shape((share, 1024), bf16),
        relative_out=shape((share, 1024), bf16),
    )
    results = {name + "_any": value for name, value in kept.items()}
    scratch = dict(
        normed_a=vmem(given["normed_a_any"].shape, bf16),
        waves=vmem(given["waves_any"].shape, bf16),
        pair_cols=vmem(given["pair_cols_any"].shape, bf16),
        near_rows=vmem(given["near_any"].shape, bf16),
        full=vmem((3, width, 1024), bf16),
        mine=vmem((3, tok, 1024), bf16),
        sums=vmem((4, share, 512), f32),
        up_all=vmem((8, padded, 4 * hidden), bf16),
        cross_all=vmem((8, padded, 12 * cols), bf16),
        pair_all=vmem((8, share, 512), bf16),
        ctx_o_part=vmem((3,) + part, bf16),
        ctx_o_share=vmem(part, bf16),
        out_o_part=vmem((3,) + part, bf16),
        out_o_share=vmem(part, bf16),
        pair_give=vmem((3, share, 512), bf16),
        pair_take=vmem((3, share, 512), bf16),
        near_give=vmem((3, near // 4, width), bf16),
        near_take=vmem((3, near // 4, width), bf16),
        got_wa=vmem((3,) + given["small"].shape, f32),
        got_y=vmem((1,) + given["small"].shape, f32),
        got_z=vmem((3,) + given["small"].shape, f32),
        send=dma((184,)),
        recv=dma((184,)),
        local=dma((24,)),
    )
    scratch.update({name: vmem(value.shape, value.dtype) for name, value in kept.items()})
    names = [*given, *results, *scratch]
    got = pl.pallas_call(
        functools.partial(finish_kernel, names),
        out_shape=list(results.values()),
        in_specs=[any_space if name.endswith("_any") else in_vmem for name in given],
        out_specs=[any_space] * len(results),
        scratch_shapes=list(scratch.values()),
        compiler_params=pltpu.CompilerParams(
            collective_id=collective_id, has_side_effects=True, vmem_limit_bytes=62 * 2**20
        ),
        name="finish",
    )(*given.values())
    return types.SimpleNamespace(**dict(zip(kept, got, strict=True)))


def skew(wide, count):
    lead = wide.shape[:-2]
    rows, span = wide.shape[-2:]
    edge = [(0, 0)] * len(lead)
    padded = jnp.pad(wide, edge + [(0, 0), (0, 1)])
    flat = padded.reshape(lead + (rows * (span + 1),))
    flat = lax.slice_in_dim(flat, rows - 1, rows - 1 + rows * span, axis=len(lead))
    return flat.reshape(lead + (rows, span))[..., :count]


def unskew(grad, span):
    lead = grad.shape[:-2]
    rows, count = grad.shape[-2:]
    edge = [(0, 0)] * len(lead)
    wide = jnp.pad(grad, edge + [(0, 0), (0, span - count)])
    flat = jnp.pad(wide.reshape(lead + (rows * span,)), edge + [(rows - 1, 1)])
    return flat.reshape(lead + (rows, span + 1))[..., :span]


def tile_scores(content_rows, position_rows, key_rows, relative, row_start, key_start):
    rows = content_rows.shape[0]
    count = key_rows.shape[0]
    scale = content_rows.shape[-1] ** (-0.5)
    content = jnp.einsum("qhe,khe->hqk", content_rows, key_rows, preferred_element_type=f32)
    wide = jnp.einsum("qhe,whe->hqw", position_rows, relative, preferred_element_type=f32)
    scores = (content + skew(wide, count)) * scale
    causal = (row_start + jnp.arange(rows))[:, None] >= (key_start + jnp.arange(count))[None, :]
    return (scores, causal[None])


def tile_forward(
    content_rows, position_rows, row_start, relative, key_rows, value_rows, key_start, state
):
    top, total, accum = state
    scores, causal = tile_scores(
        content_rows, position_rows, key_rows, relative, row_start, key_start
    )
    scores = jnp.where(causal, scores, neg_big)
    new_top = jnp.maximum(top, jnp.max(scores, axis=-1))
    raised = jnp.where(causal, jnp.exp(scores - new_top[..., None]), 0.0)
    fade = jnp.exp(top - new_top)
    total = total * fade + jnp.sum(raised, axis=-1)
    accum = accum * fade[..., None] + jnp.einsum(
        "hqk,khe->hqe", raised.astype(bf16), value_rows, preferred_element_type=f32
    )
    return (new_top, total, accum)


def tile_backward(
    content_rows,
    position_rows,
    row_start,
    relative,
    key_rows,
    value_rows,
    grad_rows,
    log_rows,
    delta_rows,
    key_start,
):
    scores, causal = tile_scores(
        content_rows, position_rows, key_rows, relative, row_start, key_start
    )
    scale = content_rows.shape[-1] ** (-0.5)
    shares = jnp.where(causal, jnp.exp(scores - log_rows[..., None]), 0.0)
    share_grad = jnp.einsum("qhe,khe->hqk", grad_rows, value_rows, preferred_element_type=f32)
    score_grad = (shares * (share_grad - delta_rows[..., None])).astype(bf16)
    content_grad = jnp.einsum("hqk,khe->qhe", score_grad, key_rows, preferred_element_type=f32)
    wide_grad = unskew(score_grad, relative.shape[0])
    position_grad = jnp.einsum("hqw,whe->qhe", wide_grad, relative, preferred_element_type=f32)
    table_part = jnp.einsum("hqw,qhe->whe", wide_grad, position_rows, preferred_element_type=f32)
    key_grad = jnp.einsum("hqk,qhe->khe", score_grad, content_rows, preferred_element_type=f32)
    value_grad = jnp.einsum(
        "hqk,qhe->khe", shares.astype(bf16), grad_rows, preferred_element_type=f32
    )
    return (
        content_grad * scale,
        position_grad * scale,
        table_part * scale,
        key_grad * scale,
        value_grad,
    )


def nest_tiles(tile_fn):
    inner = jax.vmap(tile_fn, in_axes=(0, 0, 0, 0, None, None, 0))
    return jax.vmap(inner, in_axes=(0, 0, None, None, 0, 0, 0))


def to_global(stored, inverse, block):
    seqs, seq_len, width = stored.shape
    blocks = stored.reshape(seqs, seq_len // block, block * width)
    chosen = (inverse[:, None] == jnp.arange(seq_len // block)[None, :]).astype(bf16)
    moved = jnp.einsum("gs,nsx->ngx", chosen, blocks, preferred_element_type=f32)
    return moved.astype(bf16).reshape(stored.shape)


class SplitQueries:

    def __init__(self, query, keys, values, biases, relative, block_order, inverse, block):
        self.seqs, self.tok_dev, self.width = keys.shape
        self.heads = self.width // HEAD_DIM
        self.block = block
        self.block_order = block_order
        ctx_count = lax.axis_size("ctx")
        self.seq_len = self.tok_dev * ctx_count
        self.key_len = min(512, self.seq_len)
        pad = jnp.zeros((self.key_len + block, self.width), bf16)
        table = jnp.concatenate([relative, pad], axis=0)
        self.table = table.reshape(-1, self.heads, HEAD_DIM)
        lead = (self.seqs, 2, block, self.heads, HEAD_DIM)
        self.content = (query + biases[0]).astype(bf16).reshape(lead)
        self.position = (query + biases[1]).astype(bf16).reshape(lead)
        gathered = [lax.all_gather(part, "ctx", axis=1, tiled=True) for part in (keys, values)]
        shape = (self.seqs, self.seq_len, self.heads, HEAD_DIM)
        self.keys, self.values = [to_global(part, inverse, block).reshape(shape) for part in gathered]
        self.starts = lax.dynamic_slice_in_dim(block_order, 2 * lax.axis_index("ctx"), 2, 0) * block

    def rows(self, index):
        start = index * self.key_len
        keys = lax.dynamic_slice_in_dim(self.keys, start, self.key_len, 1)
        values = lax.dynamic_slice_in_dim(self.values, start, self.key_len, 1)
        span = self.block + self.key_len
        offsets = [self.seq_len - self.block - self.starts[slot] + start for slot in range(2)]
        relative = [lax.dynamic_slice_in_dim(self.table, offset, span, 0) for offset in offsets]
        return start, keys, values, jnp.stack(relative), offsets

    def to_stored(self, part):
        count = self.seq_len // self.block
        blocks = part.reshape(self.seqs, count, self.block * self.width)
        chosen = (self.block_order[:, None] == jnp.arange(count)[None, :]).astype(f32)
        moved = jnp.einsum("sg,ngx->nsx", chosen, blocks, precision=highest)
        return moved.reshape(self.seqs, self.seq_len, self.width)

    def forward(self):
        def step(state, index):
            start, keys, values, relative, _ = self.rows(index)

            def tile(content, position, row_start, table, keys_seq, values_seq, tile_state):
                return tile_forward(
                    content, position, row_start, table, keys_seq, values_seq, start, tile_state
                )

            return nest_tiles(tile)(
                self.content, self.position, self.starts, relative, keys, values, state
            ), None

        shape = (self.seqs, 2, self.heads, self.block)
        state = (
            jnp.full(shape, neg_big, f32),
            jnp.zeros(shape, f32),
            jnp.zeros(shape + (HEAD_DIM,), f32),
        )
        (top, total, accum), _ = lax.scan(step, state, jnp.arange(self.seq_len // self.key_len))
        self.log_total = top + jnp.log(total)
        self.out = accum / total[..., None]
        moved = jnp.transpose(self.out, (0, 1, 3, 2, 4))
        return moved.reshape(self.seqs * self.tok_dev, self.width).astype(bf16)

    def backward(self, grad):
        block, seq_len, key_len = self.block, self.seq_len, self.key_len
        lead = (self.seqs, 2, block, self.heads, HEAD_DIM)
        grad = grad.reshape(lead)
        delta = jnp.einsum("sbqhe,sbhqe->sbhq", grad.astype(f32), self.out)
        def step(carry, index):
            start, keys, values, relative, offsets = self.rows(index)

            def tile(content, position, row_start, table, keys_seq, values_seq, extra):
                return tile_backward(
                    content, position, row_start, table, keys_seq, values_seq, *extra, start
                )

            extra = (grad, self.log_total, delta)
            parts = nest_tiles(tile)(
                self.content, self.position, self.starts, relative, keys, values, extra
            )
            table = carry[2]
            table_sum = jnp.sum(parts[2], axis=0)
            for slot in range(2):
                offset = offsets[slot]
                current = lax.dynamic_slice_in_dim(table, offset, block + key_len, 0)
                table = lax.dynamic_update_slice_in_dim(table, current + table_sum[slot], offset, 0)
            sums = []
            for total, part in zip(carry[3:], parts[3:]):
                current = lax.dynamic_slice_in_dim(total, start, key_len, 1)
                part = current + jnp.sum(part, axis=1)
                sums.append(lax.dynamic_update_slice_in_dim(total, part, start, 1))
            key_acc, value_acc = sums
            return (carry[0] + parts[0], carry[1] + parts[1], table, key_acc, value_acc), None

        zero_tiles = jnp.zeros(lead, f32)
        zero_keys = jnp.zeros((self.seqs, seq_len, self.heads, HEAD_DIM), f32)
        carry = (zero_tiles, zero_tiles, jnp.zeros(self.table.shape, f32), zero_keys, zero_keys)
        carry, _ = lax.scan(step, carry, jnp.arange(seq_len // key_len))
        owned = [
            lax.psum_scatter(
                self.to_stored(part), "ctx", scatter_dimension=1, tiled=True
            )
            for part in carry[3:]
        ]
        flat = (self.seqs * self.tok_dev, self.width)
        query_grad = (carry[0] + carry[1]).reshape(flat).astype(bf16)
        key_grad, value_grad = [part.reshape(flat).astype(bf16) for part in owned]
        bias_grads = jnp.stack(
            [jnp.sum(part, axis=(0, 1, 2)).reshape(self.width) for part in carry[:2]]
        )
        table_grad = carry[2].reshape(-1, self.width)[:seq_len]
        return query_grad, key_grad, value_grad, bias_grads, table_grad


def local_general(
    tokens,
    neighbours,
    teacher,
    valid_mask,
    block_order,
    query_weight,
    key_weight,
    value_weight,
    output_weight,
    relative_weight,
    content_bias,
    position_bias,
    cross_query_weight,
    cross_key_weight,
    cross_value_weight,
    cross_output_weight,
    up_weight,
    down_weight,
    attention_gain,
    cross_gain,
    feedforward_gain,
):
    places = lax.axis_size("wa")
    ctx_count = lax.axis_size("ctx")
    place = lax.axis_index("wa")
    here = lax.axis_index("ctx")
    _, tok_dev, width = tokens.shape
    seq_len = tok_dev * ctx_count
    block = tok_dev // 2
    cols = HEADS * HEAD_DIM // places
    rows = places * tok_dev

    token_parts = gather_parts(tokens[0])
    query_cols, key_cols, value_cols = [
        take_columns(weight) for weight in (query_weight, key_weight, value_weight)
    ]
    relative_cols = take_columns(relative_weight)
    gains = lax.all_gather(
        jnp.stack([attention_gain, cross_gain, feedforward_gain]), "wa", axis=1, tiled=True
    ).astype(f32)
    gain_one, gain_two, gain_three = gains[0:1], gains[1:2], gains[2:3]
    cross_query_cols, cross_key_cols, cross_value_cols = [
        take_columns(weight) for weight in (cross_query_weight, cross_key_weight, cross_value_weight)
    ]
    cross_pair_cols = jnp.concatenate([cross_key_cols, cross_value_cols], axis=1)
    near_rows = jnp.concatenate(gather_parts(neighbours.reshape(-1, width)), axis=0)
    up_cols = take_columns(up_weight)
    valid = valid_mask.astype(f32).reshape(tok_dev, 1)
    count = jnp.sum(valid).reshape(1, 1)
    count = all_summed(all_summed(count, "wa"), "ctx")

    slots = jnp.arange(2 * ctx_count)
    inverse = jnp.sum(jnp.where(block_order[None, :] == slots[:, None], slots[None, :], 0), axis=1)
    inverse = inverse.astype(jnp.int32)
    distance = (seq_len - 1 - jnp.arange(seq_len)).astype(f32)
    waves = sinusoid(distance, width).astype(bf16)

    hidden_all = jnp.concatenate(token_parts, axis=0).astype(f32)
    scale_all = inverse_rms(hidden_all)
    normed_a = (hidden_all * scale_all * gain_one).astype(bf16)
    biases = jnp.stack([content_bias, position_bias]).astype(f32)
    mixed_cols = jnp.concatenate([query_cols, key_cols, value_cols], axis=1)
    qkv = dot_nn(normed_a, mixed_cols).reshape(places, tok_dev, 3 * cols)
    relative = dot_nn(waves, relative_cols).astype(bf16)
    general = SplitQueries(
        qkv[..., :cols],
        qkv[..., cols : 2 * cols].astype(bf16),
        qkv[..., 2 * cols :].astype(bf16),
        biases,
        relative,
        block_order,
        inverse,
        block,
    )
    attended = general.forward()

    def to_owner(product):
        return scatter_parts([product[r * tok_dev : (r + 1) * tok_dev] for r in range(places)])

    def from_all(value):
        return jnp.concatenate(gather_parts(value), axis=0)

    hidden_in = tokens[0].astype(f32)
    hidden_one = hidden_in + to_owner(dot_nn(attended, output_weight))

    scale_two = inverse_rms(hidden_one)
    normed_b = from_all((hidden_one * scale_two * gain_two).astype(bf16))
    cross_q = dot_nn(normed_b, cross_query_cols).astype(bf16)
    cross_pair = dot_nn(near_rows, cross_pair_cols).astype(bf16)
    crossed = cross_forward(cross_q, cross_pair)
    hidden_two = hidden_one + to_owner(dot_nn(crossed, cross_output_weight))

    scale_three = inverse_rms(hidden_two)
    normed_c = from_all((hidden_two * scale_three * gain_three).astype(bf16))
    pre_act = dot_nn(normed_c, up_cols)
    activated = gelu_tanh(pre_act).astype(bf16)
    layer_out = hidden_two + to_owner(dot_nn(activated, down_weight))

    error = layer_out - teacher[0].astype(f32)
    error_sum = jnp.sum(valid * error * error).reshape(1, 1)
    error_sum = all_summed(all_summed(error_sum, "wa"), "ctx")
    loss = (error_sum / (2.0 * count * width)).reshape(())
    out_grad = (places * seq_len) / count * valid * error

    out_low = from_all(out_grad.astype(bf16))
    act_grad = dot_nt(out_low, down_weight)
    _, gelu_pull = jax.vjp(gelu_tanh, pre_act)
    pre_grad = gelu_pull(act_grad)[0].astype(bf16)
    down_grad = dot_tn(activated, out_low).astype(bf16)
    up_grad = dot_tn(normed_c, pre_grad).astype(bf16)
    normed_c_grad = to_owner(dot_nt(pre_grad, up_cols))
    two_grad = out_grad + norm_pull(hidden_two, scale_three, gain_three, normed_c_grad)
    gain_three_grad = jnp.sum(normed_c_grad * hidden_two * scale_three, axis=0, keepdims=True)
    down_out = sum_row_grads(down_grad)
    up_out = sum_column_grads(up_grad[None])[0]

    two_low = from_all(two_grad.astype(bf16))
    crossed_grad = dot_nt(two_low, cross_output_weight).astype(bf16)
    cross_q_grad, cross_pair_grad = cross_backward(cross_q, cross_pair, crossed_grad)
    normed_b_grad = to_owner(dot_nt(cross_q_grad, cross_query_cols))
    one_grad = two_grad + norm_pull(hidden_one, scale_two, gain_two, normed_b_grad)
    gain_two_grad = jnp.sum(normed_b_grad * hidden_one * scale_two, axis=0, keepdims=True)
    cross_output_grad = dot_tn(crossed, two_low).astype(bf16)
    cross_query_grad = dot_tn(normed_b, cross_q_grad).astype(bf16)
    cross_key_grad = dot_tn(near_rows, cross_pair_grad[:, :cols]).astype(bf16)
    cross_value_grad = dot_tn(near_rows, cross_pair_grad[:, cols:]).astype(bf16)
    cross_output_out = sum_row_grads(cross_output_grad)
    cross_out = sum_column_grads(jnp.stack([cross_key_grad, cross_value_grad]))
    cross_query_out = sum_column_grads(cross_query_grad[None])[0]
    near_grad = dot_nt(cross_pair_grad, cross_pair_cols)
    near_count = near_rows.shape[0] // places
    near_grad = scatter_parts(
        [near_grad[r * near_count : (r + 1) * near_count] for r in range(places)]
    )
    neighbours_grad = near_grad.reshape(neighbours.shape)

    one_low = from_all(one_grad.astype(bf16))
    attended_grad = dot_nt(one_low, output_weight).astype(bf16)
    output_grad = dot_tn(attended, one_low).astype(bf16)
    output_out = sum_row_grads(output_grad)
    query_grad, key_grad, value_grad, bias_grads, table_grad = general.backward(attended_grad)
    qkv_grad = jnp.concatenate([query_grad, key_grad, value_grad], axis=1)
    table_high = table_grad.astype(bf16)
    table_low = (table_grad - table_high.astype(f32)).astype(bf16)
    relative_grad = (dot_tn(waves, table_high) + dot_tn(waves, table_low)).astype(bf16)
    mixed_grad = dot_tn(normed_a, qkv_grad).astype(bf16)
    whole = [mixed_grad[:, m * cols : (m + 1) * cols] for m in range(3)]
    attention_out = sum_column_grads(jnp.stack(whole + [relative_grad]))
    normed_a_part = dot_nt(qkv_grad, mixed_cols)
    gain_one_part = jnp.sum(normed_a_part * hidden_all * scale_all, axis=0, keepdims=True)
    normed_a_grad = to_owner(normed_a_part)
    tokens_grad = one_grad + norm_pull(hidden_in, scale_all[:tok_dev], gain_one, normed_a_grad)

    gain_grads = jnp.concatenate([gain_one_part, gain_two_grad, gain_three_grad], axis=0)
    gain_grads = all_summed(gain_grads, "wa")
    share = width // places
    gain_grads = lax.dynamic_slice_in_dim(gain_grads, place * share, share, 1)
    small = jnp.concatenate([gain_grads.reshape(1, -1), bias_grads.reshape(1, -1)], axis=1)
    small = all_summed(small, "ctx")[0]
    gain_out = small[: 3 * share].reshape(3, share)
    bias_out = small[3 * share :].reshape(2, cols)

    return (
        layer_out[None],
        loss,
        tokens_grad[None],
        neighbours_grad,
        attention_out[0],
        attention_out[1],
        attention_out[2],
        output_out,
        attention_out[3],
        bias_out[0],
        bias_out[1],
        cross_query_out,
        cross_out[0],
        cross_out[1],
        cross_output_out,
        up_out,
        down_out,
        gain_out[0],
        gain_out[1],
        gain_out[2],
    )


def local_by_heads(
    tokens,
    neighbours,
    teacher,
    valid_mask,
    block_order,
    query_weight,
    key_weight,
    value_weight,
    output_weight,
    relative_weight,
    content_bias,
    position_bias,
    cross_query_weight,
    cross_key_weight,
    cross_value_weight,
    cross_output_weight,
    up_weight,
    down_weight,
    attention_gain,
    cross_gain,
    feedforward_gain,
):
    places = 4
    ctx_count = 8
    place = lax.axis_index("wa")
    here = lax.axis_index("ctx")
    _, tok_dev, width = tokens.shape
    seq_len = tok_dev * ctx_count
    block = tok_dev // 2
    attn = HEADS * HEAD_DIM
    cols = attn // places
    share = width // places

    slots = jnp.arange(2 * ctx_count)
    inverse = jnp.sum(jnp.where(block_order[None, :] == slots[:, None], slots[None, :], 0), axis=1)
    inverse = inverse.astype(jnp.int32)
    gain_rows = jnp.concatenate(
        [jnp.stack([attention_gain, cross_gain, feedforward_gain]), jnp.zeros((5, share), bf16)]
    )
    blank = jnp.zeros((3, cols), bf16)
    bias_rows = jnp.concatenate([blank, content_bias[None], position_bias[None], blank])

    half = width // 2
    freq = jnp.exp(-jnp.log(10000.0) * jnp.arange(half, dtype=f32) * 2.0 / width)
    coarse = (64.0 * jnp.arange(seq_len // 64, dtype=f32)[::-1])[:, None] * freq
    fine = jnp.arange(64, dtype=f32)[::-1][:, None] * freq
    sin_a, cos_a = jnp.sin(coarse)[:, None], jnp.cos(coarse)[:, None]
    sin_b, cos_b = jnp.sin(fine)[None], jnp.cos(fine)[None]
    waves = jnp.concatenate(
        [sin_a * cos_b + cos_a * sin_b, cos_a * cos_b - sin_a * sin_b], axis=-1
    )
    waves = waves.reshape(seq_len, width).astype(bf16)

    done = layer(
        float(places * seq_len),
        block,
        dict(inverse=inverse, order=block_order),
        dict(
            tokens=tokens[0],
            teacher=teacher[0],
            mask=valid_mask,
            gain_rows=gain_rows,
            bias_rows=bias_rows,
            neighbours=neighbours.reshape(-1, width),
            waves_any=waves,
            query_any=query_weight,
            key_any=key_weight,
            value_any=value_weight,
            relative_any=relative_weight,
            cross_query_any=cross_query_weight,
            cross_key_any=cross_key_weight,
            cross_value_any=cross_value_weight,
            up_any=up_weight,
            output_any=output_weight,
            cross_out_any=cross_output_weight,
            down_any=down_weight,
        ),
        1,
    )
    last = finish(
        dict(
            query_grad=done.query_grad,
            table_grad=done.table_grad,
            small=done.small,
            down_share=done.down_share,
            up_share=done.up_share,
            cross_share=done.cross_share,
            ctx_o_half=done.ctx_o_half,
            out_o_half=done.out_o_half,
            one_grad=done.one_grad,
            tokens=tokens[0],
            gains=done.gains,
            normed_a_any=done.normed_a,
            waves_any=waves,
            near_any=done.pair_grad,
            pair_cols_any=done.pair_cols,
            query_any=query_weight,
            key_any=key_weight,
            value_any=value_weight,
        ),
        2,
    )
    total = last.total
    gain_out = lax.dynamic_slice_in_dim(total[0:3], place * share, share, 1)
    bias_out = lax.dynamic_slice_in_dim(total[3:5].reshape(ctx_count, 2, 128), place * 2, 2, 0)
    bias_out = bias_out.transpose(1, 0, 2).reshape(2, cols)
    loss = total[7, 0]
    down_out = last.down_out.reshape(down_weight.shape).astype(f32)
    cross_output_out = last.cross_o_out.reshape(cols, width).astype(f32)
    output_out = last.output_out.reshape(cols, width).astype(f32)

    return (
        done.layer_out[None],
        loss,
        last.tokens_grad[None],
        last.near_grad.reshape(neighbours.shape),
        last.query_out.astype(f32),
        last.key_out.astype(f32),
        last.value_out.astype(f32),
        output_out,
        last.relative_out.astype(f32),
        bias_out[0],
        bias_out[1],
        last.cross_query_out,
        last.cross_key_out,
        last.cross_value_out,
        cross_output_out,
        last.up_out,
        down_out,
        gain_out[0],
        gain_out[1],
        gain_out[2],
    )


def solution(mesh):
    row = P("wa", None)
    flat = P("wa")
    in_specs = (
        P("wa", "ctx", None),
        P("wa", "ctx", None, None),
        P("wa", "ctx", None),
        P("wa", "ctx"),
        P(),
        row,
        row,
        row,
        row,
        row,
        flat,
        flat,
        row,
        row,
        row,
        row,
        row,
        row,
        flat,
        flat,
        flat,
    )
    out_specs = (
        P("wa", "ctx", None),
        P(),
        P("wa", "ctx", None),
        P("wa", "ctx", None, None),
        row,
        row,
        row,
        row,
        row,
        flat,
        flat,
        row,
        row,
        row,
        row,
        row,
        row,
        flat,
        flat,
        flat,
    )
    by_heads = mesh.shape["ctx"] == 8 and mesh.shape["wa"] == 4
    local = local_by_heads if by_heads else local_general
    return jax.shard_map(local, mesh=mesh, in_specs=in_specs, out_specs=out_specs, check_vma=False)
```

```python
import functools
import types

import jax
import jax.numpy as jnp
from jax import lax
from jax.experimental import pallas as pl
from jax.experimental.pallas import tpu as pltpu
from jax.sharding import PartitionSpec as P

HEADS = 16
HEAD_DIM = 64
GROUP = 64
NK = 256
TILE = 128

eps_norm = 1e-06
neg_big = -1e30
highest = lax.Precision.HIGHEST
f32 = jnp.float32
bf16 = jnp.bfloat16


def inverse_rms(hidden):
    return lax.rsqrt(jnp.mean(hidden * hidden, axis=-1, keepdims=True) + eps_norm)


def norm_pull(hidden, scale, gain, grad):
    scaled = grad * gain
    mean = jnp.mean(hidden * scaled, axis=-1, keepdims=True)
    return scale * scaled - hidden * (scale * scale * scale) * mean


def gelu_tanh(value):
    return jax.nn.gelu(value, approximate=True)


def sinusoid(distance, width):
    half = width // 2
    freq = jnp.exp(-jnp.log(10000.0) * jnp.arange(half, dtype=f32) * 2.0 / width)
    angle = distance[:, None] * freq[None, :]
    return jnp.concatenate([jnp.sin(angle), jnp.cos(angle)], axis=1)


def dot_nn(a, b):
    return lax.dot_general(a, b, (((1,), (0,)), ((), ())), preferred_element_type=f32)


def dot_nt(a, b):
    return lax.dot_general(a, b, (((1,), (1,)), ((), ())), preferred_element_type=f32)


def dot_tn(a, b):
    return lax.dot_general(a, b, (((0,), (0,)), ((), ())), preferred_element_type=f32)


def swap(value, axis, bit):
    pairs = [(i, i ^ bit) for i in range(lax.axis_size(axis))]
    return lax.ppermute(value, axis, pairs)


def bits_of(axis):
    bits, bit = [], 1
    while bit < lax.axis_size(axis):
        bits.append(bit)
        bit *= 2
    return bits


def my_bit(axis, bit):
    return (lax.axis_index(axis) // bit) % 2


def ordered(bit, own, other, dim):
    return jnp.where(
        bit == 0,
        jnp.concatenate([own, other], axis=dim),
        jnp.concatenate([other, own], axis=dim),
    )


def split(value, bit, dim):
    half = value.shape[dim] // 2
    keep = lax.dynamic_slice_in_dim(value, bit * half, half, dim)
    send = lax.dynamic_slice_in_dim(value, (1 - bit) * half, half, dim)
    return keep, send


def gather_parts(value):
    parts = {0: value}
    for bit in reversed(bits_of("wa")):
        parts.update({r | bit: swap(part, "wa", bit) for r, part in list(parts.items())})
    return [parts[r] for r in sorted(parts)]


def scatter_parts(parts):
    parts = dict(enumerate(parts))
    for bit in bits_of("wa"):
        kept = {}
        for r, part in parts.items():
            if not r & bit:
                got = swap(parts[r | bit].astype(bf16), "wa", bit)
                kept[r] = part + got.astype(f32)
        parts = kept
    return parts[0]


def take_columns(weight):
    value = weight[None]
    for bit in reversed(bits_of("wa")):
        mine = my_bit("wa", bit)
        keep, send = split(value, mine, 2)
        value = ordered(mine, keep[:, None], swap(send, "wa", bit)[:, None], 1)
        value = value.reshape((-1,) + value.shape[2:])
    return value.reshape(-1, value.shape[-1])


def spread_columns(value):
    for bit in bits_of("wa"):
        mine = my_bit("wa", bit)
        paired = value.reshape((value.shape[0], value.shape[1] // 2, 2) + value.shape[2:])
        keep, send = split(paired, mine, 2)
        value = ordered(mine, keep[:, :, 0], swap(send[:, :, 0], "wa", bit), 3)
    return value[:, 0]


def halving_dim(shape):
    if shape[-2] % 16 == 0:
        return len(shape) - 2
    if shape[0] % 2 == 0:
        return 0
    if shape[-2] % 2 == 0:
        return len(shape) - 2
    return len(shape) - 1


def sum_over_ctx(value, bits, finish):
    dims = []
    for bit in bits:
        dim = halving_dim(value.shape)
        keep, send = split(value, my_bit("ctx", bit), dim)
        value = (keep.astype(f32) + swap(send, "ctx", bit).astype(f32)).astype(bf16)
        dims.append(dim - value.ndim if dim else 0)
    value = finish(value)
    for bit, dim in reversed(list(zip(bits, dims))):
        dim = dim % value.ndim
        value = ordered(my_bit("ctx", bit), value, swap(value, "ctx", bit), dim)
    return value


def all_summed(value, axis):
    for bit in bits_of(axis):
        value = value + swap(value, axis, bit)
    return value


def sum_column_grads(grads):
    places = lax.axis_size("wa")
    grads = grads.reshape(grads.shape[0], places, grads.shape[1] // places, grads.shape[2])
    bits = bits_of("ctx")
    if grads.shape[2] % lax.axis_size("ctx") == 0:
        return sum_over_ctx(grads, bits, spread_columns).astype(f32)
    return sum_over_ctx(spread_columns(grads), bits, lambda value: value).astype(f32)


def sum_row_grads(grads):
    return sum_over_ctx(grads[None], bits_of("ctx"), lambda value: value)[0].astype(f32)


def first_half(shape):
    return lax.broadcasted_iota(jnp.int32, shape, 1) < HEAD_DIM


def stack_heads(rows):
    mask = first_half(rows.shape)
    zero = jnp.zeros_like(rows)
    return jnp.concatenate([jnp.where(mask, rows, zero), jnp.where(mask, zero, rows)], axis=0)


def join_heads(stacked):
    rows = stacked.shape[0] // 2
    return jnp.where(first_half((rows, stacked.shape[1])), stacked[:rows], stacked[rows:])


def copy_blocks(order_ref, source, target, block, inward):
    for place in range(source.shape[0] // block):
        start = pl.multiple_of(order_ref[place] * block, block)
        if inward:
            target[place * block : (place + 1) * block, :] = source[pl.ds(start, block), :]
        else:
            target[pl.ds(start, block), :] = source[place * block : (place + 1) * block, :]


def attention_shares(content, position, key_ref, rel_ref, row_start, seq_len):
    length = row_start + TILE
    wide_len = length + TILE
    offset = seq_len - TILE - row_start
    scale = HEAD_DIM ** (-0.5)
    scores = dot_nt(content, key_ref[0:length, :])
    wide = dot_nt(position, rel_ref[offset : offset + wide_len, :])
    halves = []
    for head in range(2):
        part = wide[head * TILE : (head + 1) * TILE]
        turned = pltpu.roll(part, wide_len - (TILE - 1), 1, stride=1, stride_axis=0)
        halves.append(turned[:, :length])
    scores = (scores + jnp.concatenate(halves, axis=0)) * scale
    row = lax.broadcasted_iota(jnp.int32, scores.shape, 0) % TILE + row_start
    col = lax.broadcasted_iota(jnp.int32, scores.shape, 1)
    scores = jnp.where(col <= row, scores, neg_big)
    top = jnp.max(scores, axis=1, keepdims=True)
    raised = jnp.exp(scores - top)
    total = jnp.sum(raised, axis=1, keepdims=True)
    return raised * (1.0 / total)


def attend_tiles(qkv, rel_ref, content_bias, position_bias, out):
    seq_len = qkv.shape[0]
    keys = qkv.at[:, 128:256]
    values = qkv.at[:, 256:384]
    for tile in range(seq_len // TILE):
        start = tile * TILE
        query = qkv[start : start + TILE, 0:128].astype(f32)
        content = stack_heads((query + content_bias).astype(bf16))
        position = stack_heads((query + position_bias).astype(bf16))
        shares = attention_shares(content, position, keys, rel_ref, start, seq_len)
        got = dot_nn(shares.astype(bf16), values[0 : start + TILE, :])
        got = join_heads(got).astype(bf16)
        block = out.shape[1]
        for part in range(TILE // block):
            out[start // block + part] = got[part * block : (part + 1) * block]


def attend_back_tiles(
    qkv, grad, rel_ref, content_bias, position_bias, dqkv, dkey, dvalue, drel, poll
):
    scale = HEAD_DIM ** (-0.5)
    seq_len = qkv.shape[0]
    block = dqkv.shape[1]
    keys = qkv.at[:, 128:256]
    values = qkv.at[:, 256:384]
    dkey[...] = jnp.zeros_like(dkey)
    dvalue[...] = jnp.zeros_like(dvalue)
    drel[...] = jnp.zeros_like(drel)
    row = lax.broadcasted_iota(jnp.int32, (TILE, TILE), 0)
    col = lax.broadcasted_iota(jnp.int32, (TILE, TILE), 1)
    flip = jnp.where(row + col == TILE - 1, 1.0, 0.0).astype(bf16)
    content_sum = jnp.zeros((1, 128), f32)
    position_sum = jnp.zeros((1, 128), f32)
    for tile in range(seq_len // TILE):
        poll(tile)
        start = tile * TILE
        length = start + TILE
        wide_len = length + TILE
        offset = seq_len - TILE - start
        query = qkv[start : start + TILE, 0:128].astype(f32)
        content = stack_heads((query + content_bias).astype(bf16))
        plain = (query + position_bias).astype(bf16)
        position = stack_heads(plain)
        shares = attention_shares(content, position, keys, rel_ref, start, seq_len)
        out_grad = stack_heads(grad[start : start + TILE, :])
        share_grad = dot_nt(out_grad, values[0:length, :])
        delta = jnp.sum(shares * share_grad, axis=1, keepdims=True)
        score_grad = (shares * (share_grad - delta)).astype(bf16)
        content_grad = join_heads(dot_nn(score_grad, keys[0:length, :])) * scale
        parts = []
        for head in range(2):
            turned = dot_nn(flip, score_grad[head * TILE : (head + 1) * TILE])
            turned = jnp.concatenate([turned, jnp.zeros((TILE, TILE), f32)], axis=1)
            parts.append(pltpu.roll(turned, 0, 1, stride=1, stride_axis=0))
        wide_grad = jnp.concatenate(parts, axis=0).astype(bf16)
        relative = rel_ref[offset : offset + wide_len, :]
        turned_grad = join_heads(dot_nn(wide_grad, relative)) * scale
        turned_rows = stack_heads(dot_nn(flip, plain).astype(bf16))
        drel[offset : offset + wide_len, :] += dot_tn(wide_grad, turned_rows)
        high = turned_grad.astype(bf16)
        low = (turned_grad - high.astype(f32)).astype(bf16)
        position_grad = dot_nn(flip, high) + dot_nn(flip, low)
        content_sum += jnp.sum(content_grad, axis=0, keepdims=True)
        position_sum += jnp.sum(turned_grad, axis=0, keepdims=True)
        query_grad = (content_grad + position_grad).astype(bf16)
        for part in range(TILE // block):
            dqkv[start // block + part, :, 0:128] = query_grad[part * block : (part + 1) * block]
        dkey[0:length, :] += dot_tn(score_grad, content)
        dvalue[0:length, :] += dot_tn(shares.astype(bf16), out_grad)
    for part in range(seq_len // block):
        rows = slice(part * block, (part + 1) * block)
        dqkv[part, :, 128:256] = (dkey[rows, :] * scale).astype(bf16)
        dqkv[part, :, 256:384] = dvalue[rows, :].astype(bf16)
    return content_sum, position_sum


in_vmem = pl.BlockSpec(memory_space=pltpu.VMEM)
in_smem = pl.BlockSpec(memory_space=pltpu.SMEM)


def head_mask(shape, head):
    lane = lax.broadcasted_iota(jnp.int32, shape, 1)
    return (lane >= head * HEAD_DIM) & (lane < (head + 1) * HEAD_DIM)


def stack_all(rows):
    zero = jnp.zeros_like(rows)
    heads = rows.shape[1] // HEAD_DIM
    return jnp.concatenate(
        [jnp.where(head_mask(rows.shape, head), rows, zero) for head in range(heads)], axis=0
    )


def join_all(stacked):
    heads = stacked.shape[1] // HEAD_DIM
    rows = stacked.shape[0] // heads
    out = jnp.zeros((rows, stacked.shape[1]), stacked.dtype)
    for head in range(heads):
        part = stacked[head * rows : (head + 1) * rows]
        out = jnp.where(head_mask(part.shape, head), part, out)
    return out


def cross_shares(query, keys):
    scores = dot_nt(query, keys) * (HEAD_DIM ** (-0.5))
    raised = jnp.exp(scores - jnp.max(scores, axis=1, keepdims=True))
    return raised / jnp.sum(raised, axis=1, keepdims=True)


def cross_forward_kernel(q_ref, kv_ref, out_ref):
    width = q_ref.shape[1]
    shares = cross_shares(stack_all(q_ref[...]), kv_ref[:, 0:width])
    out_ref[...] = join_all(dot_nn(shares.astype(bf16), kv_ref[:, width:])).astype(bf16)


def cross_backward_kernel(q_ref, kv_ref, grad_ref, dq_ref, dkv_ref):
    width = q_ref.shape[1]
    scale = HEAD_DIM ** (-0.5)
    keys = kv_ref[:, 0:width]
    query = stack_all(q_ref[...])
    grad = stack_all(grad_ref[...])
    shares = cross_shares(query, keys)
    share_grad = dot_nt(grad, kv_ref[:, width:])
    delta = jnp.sum(shares * share_grad, axis=1, keepdims=True)
    score_grad = (shares * (share_grad - delta)).astype(bf16)
    dq_ref[...] = (join_all(dot_nn(score_grad, keys)) * scale).astype(bf16)
    dkv_ref[:, 0:width] = (dot_tn(score_grad, query) * scale).astype(bf16)
    dkv_ref[:, width:] = dot_tn(shares.astype(bf16), grad).astype(bf16)


def cross_forward(query, pair):
    width = query.shape[1]
    groups = query.shape[0] // GROUP
    return pl.pallas_call(
        cross_forward_kernel,
        out_shape=jax.ShapeDtypeStruct(query.shape, bf16),
        grid=(groups,),
        in_specs=[
            pl.BlockSpec((GROUP, width), lambda g: (g, 0)),
            pl.BlockSpec((NK, 2 * width), lambda g: (g, 0)),
        ],
        out_specs=pl.BlockSpec((GROUP, width), lambda g: (g, 0)),
        cost_estimate=pl.CostEstimate(
            flops=groups * 4 * 256 * 256 * 256, bytes_accessed=groups * 330000, transcendentals=groups * 65536
        ),
        name="cross_forward",
    )(query, pair)


def cross_backward(query, pair, grad):
    width = query.shape[1]
    groups = query.shape[0] // GROUP
    return pl.pallas_call(
        cross_backward_kernel,
        out_shape=[
            jax.ShapeDtypeStruct(query.shape, bf16),
            jax.ShapeDtypeStruct(pair.shape, bf16),
        ],
        grid=(groups,),
        in_specs=[
            pl.BlockSpec((GROUP, width), lambda g: (g, 0)),
            pl.BlockSpec((NK, 2 * width), lambda g: (g, 0)),
            pl.BlockSpec((GROUP, width), lambda g: (g, 0)),
        ],
        out_specs=[
            pl.BlockSpec((GROUP, width), lambda g: (g, 0)),
            pl.BlockSpec((NK, 2 * width), lambda g: (g, 0)),
        ],
        cost_estimate=pl.CostEstimate(
            flops=groups * 10 * 256 * 256 * 256, bytes_accessed=groups * 660000, transcendentals=groups * 65536
        ),
        name="cross_backward",
    )(query, pair, grad)


mesh_id = pl.DeviceIdType.MESH


def signal_to(barrier, ctx, wa):
    pl.semaphore_signal(barrier, inc=1, device_id=(ctx, wa), device_id_type=mesh_id)


def tree_sum(values):
    while len(values) > 1:
        values = [a + b for a, b in zip(values[::2], values[1::2])]
    return values[0]


def gelu_slope(value):
    inner = 0.7978845608028654 * (value + 0.044715 * value * value * value)
    turned = jnp.tanh(inner)
    slope = 0.7978845608028654 * (1.0 + 3.0 * 0.044715 * value * value)
    return 0.5 * (1.0 + turned) + 0.5 * value * (1.0 - turned * turned) * slope


def places_here():
    return lax.axis_index("ctx"), lax.axis_index("wa")


def meet_all():
    c, w = places_here()
    owner = c // 2
    own = owner == w
    barrier = pltpu.get_barrier_semaphore()
    for j in range(1, 8):
        signal_to(barrier, c ^ j, w)
    for j in range(1, 4):
        signal_to(barrier, c, w ^ j)
    for j in range(1, 8):
        signal_to(barrier, c ^ j, owner)
    for r in range(4):
        for h in range(2):

            @pl.when(jnp.logical_not(jnp.logical_and(2 * w + h == c, r == 0)))
            def _(r=r, h=h):
                signal_to(barrier, 2 * w + h, w ^ r)

    @pl.when(jnp.logical_not(own))
    def _():
        signal_to(barrier, c, owner)

    pl.semaphore_wait(barrier, 26 - 2 * own.astype(jnp.int32))


def meet_lines():
    c, w = places_here()
    barrier = pltpu.get_barrier_semaphore()
    for j in range(1, 8):
        signal_to(barrier, c ^ j, w)
    for j in range(1, 4):
        signal_to(barrier, c, w ^ j)
    pl.semaphore_wait(barrier, 10)


def remote(source, target, send, recv, ctx, wa):
    return pltpu.make_async_remote_copy(
        src_ref=source,
        dst_ref=target,
        send_sem=send,
        recv_sem=recv,
        device_id=(ctx, wa),
        device_id_type=mesh_id,
    )


class GatherRows:

    def __init__(self, buf, send, recv):
        self.buf, self.send, self.recv = buf, send, recv
        self.c, self.w = places_here()

    def copy(self, k):
        source, entry, j = ((0, 1, 1), (0, 2, 2), (2, 3, 1))[k]
        return remote(
            self.buf.at[source],
            self.buf.at[entry],
            self.send.at[k],
            self.recv.at[k],
            self.c,
            self.w ^ j,
        )

    def start(self):
        self.copy(1).start()
        self.copy(0).start()

    def near(self):
        self.copy(0).wait()

    def relay(self):
        self.copy(1).wait()
        self.copy(2).start()

    def far(self):
        self.copy(2).wait()


class SumRows:

    def __init__(self, out_buf, in_buf, send, recv):
        self.out, self.inn, self.send, self.recv = out_buf, in_buf, send, recv
        self.c, self.w = places_here()

    def copy(self, k):
        j = (1, 1, 2)[k]
        return remote(
            self.out.at[k], self.inn.at[k], self.send.at[k], self.recv.at[k], self.c, self.w ^ j
        )

    def give_near(self, value):
        self.out[0] = value.astype(bf16)
        self.copy(0).start()

    def give_far(self, value):
        self.out[1] = value.astype(bf16)
        self.copy(1).start()

    def pass_on(self, value):
        self.copy(1).wait()
        self.out[2] = (value + self.inn[1].astype(f32)).astype(bf16)
        self.copy(2).start()

    def total(self, value):
        self.copy(0).wait()
        value = value + self.inn[0].astype(f32)
        self.copy(2).wait()
        return value + self.inn[2].astype(f32)


class CtxSum:

    def __init__(self, send, recv, x=None, half=None, part=None, share=None, out=None, spread=0):
        self.send, self.recv = send, recv
        self.x, self.half, self.part, self.share, self.out = x, half, part, share, out
        self.spread = spread
        self.c, self.w = places_here()
        self.z, self.y = self.c // 2, self.c % 2

    def y_copy(self):
        return remote(
            self.x.at[:, 1 - self.y], self.half, self.send.at[0], self.recv.at[0], self.c ^ 1, self.w
        )

    def start_y(self):
        self.y_copy().start()

    def finish_y(self):
        self.y_copy().wait()
        for z in range(4):
            mine = self.x[z, self.y].astype(f32)
            self.half[z] = (self.half[z].astype(f32) + mine).astype(bf16)

    def z_copy(self, j):
        return remote(
            self.half.at[self.z ^ j],
            self.part.at[j - 1],
            self.send.at[j],
            self.recv.at[j],
            self.c ^ (2 * j),
            self.w,
        )

    def start_z(self):
        for j in (2, 3, 1):
            self.z_copy(j).start()

    def finish_z(self):
        total = self.half[self.z].astype(f32)
        for j in (1, 2, 3):
            self.z_copy(j).wait()
            total = total + self.part[j - 1].astype(f32)
        self.share[...] = total.astype(bf16)

    def columns(self, place):
        width = self.spread
        return self.out.at[self.z, self.y, :, pl.ds(pl.multiple_of(place * width, 128), width)]

    def wa_copy(self, j, place):
        return remote(
            self.share.at[self.w ^ j],
            self.columns(place),
            self.send.at[3 + j],
            self.recv.at[3 + j],
            self.c,
            self.w ^ j,
        )

    def own_copy(self):
        source = self.share.at[self.w] if self.spread else self.share
        target = self.columns(self.w) if self.spread else self.out.at[self.z, self.y]
        return pltpu.make_async_copy(source, target, self.send.at[11])

    def start_wa(self):
        if self.spread:
            for j in (2, 3, 1):
                self.wa_copy(j, self.w).start()
        self.own_copy().start()

    def finish_wa(self):
        self.own_copy().wait()
        if self.spread:
            for j in (1, 2, 3):
                self.wa_copy(j, self.w).wait_send()
                self.wa_copy(j, self.w ^ j).wait_recv()

    def back_z_copy(self, j, z):
        mine = self.out.at[z, self.y]
        return remote(mine, mine, self.send.at[6 + j], self.recv.at[6 + j], self.c ^ (2 * j), self.w)

    def start_back_z(self):
        for j in (2, 3, 1):
            self.back_z_copy(j, self.z).start()

    def finish_back_z(self):
        for j in (1, 2, 3):
            self.back_z_copy(j, self.z).wait_send()
            self.back_z_copy(j, self.z ^ j).wait_recv()

    def back_y_copy(self, y):
        part = self.out.at[:, y]
        return remote(part, part, self.send.at[10], self.recv.at[10], self.c ^ 1, self.w)

    def start_back_y(self):
        self.back_y_copy(self.y).start()

    def finish_back_y(self):
        self.back_y_copy(self.y).wait_send()
        self.back_y_copy(1 - self.y).wait_recv()


def put_shares(target, grads, first=0):
    count = grads.shape[0] // 32
    padded = target.shape[3]
    for place in range(4):
        for share in range(8):
            start = (place * 8 + share) * count
            part = grads[start : start + count]
            part = jnp.concatenate([part, jnp.zeros((padded - count, part.shape[1]), f32)], axis=0)
            target[share // 2, share % 2, place, :, first : first + part.shape[1]] = part.astype(bf16)


def put_rows(target, grads):
    count = grads.shape[0] // 8
    for share in range(8):
        target[share // 2, share % 2] = grads[share * count : (share + 1) * count].astype(bf16)


class Cut:

    def __init__(self, ref, start):
        self.ref, self.start = ref, start

    @property
    def at(self):
        return self

    def __getitem__(self, k):
        return self.ref.at[self.start + k]


class Pool:
    def __init__(self, ref):
        self.ref, self.used = ref, 0

    def take(self, count):
        cut = Cut(self.ref, self.used)
        self.used += count
        return cut


class LineGather:

    def __init__(self, out, send, recv):
        self.out, self.send, self.recv = out, send, recv
        self.c, self.w = places_here()
        self.z = self.c // 2
        self.right, self.left = self.z < 3, self.z > 0

    def y_copy(self, block, slot):
        ref = self.out.at[block]
        return remote(ref, ref, self.send.at[slot], self.recv.at[slot], self.c ^ 1, self.w)

    def z_copy(self, block, slot, step):
        k = slot + (7 if step > 0 else 10)
        ref = self.out.at[block]
        return remote(ref, ref, self.send.at[k], self.recv.at[k], self.c + step, self.w)

    def start(self):
        @pl.when(self.right)
        def _():
            self.z_copy(self.c, 0, 2).start()

        @pl.when(self.left)
        def _():
            self.z_copy(self.c, 0, -2).start()

        self.y_copy(self.c, 0).start()

    def step(self, t):
        @pl.when(self.z > t)
        def _():
            block = self.c - 2 * (t + 1)
            self.z_copy(block, t, 2).wait_recv()
            if t < 2:

                @pl.when(self.right)
                def _():
                    self.z_copy(block, t + 1, 2).start()

            self.y_copy(block, t + 1).start()

        @pl.when(self.z < 3 - t)
        def _():
            block = self.c + 2 * (t + 1)
            self.z_copy(block, t, -2).wait_recv()
            if t < 2:

                @pl.when(self.left)
                def _():
                    self.z_copy(block, t + 1, -2).start()

            self.y_copy(block, t + 4).start()

    def finish(self):
        self.y_copy(self.c, 0).wait_send()
        self.y_copy(self.c ^ 1, 0).wait_recv()
        for t in range(3):
            for step, at, near in ((-2, t + 1, self.z > t), (2, t + 4, self.z < 3 - t)):

                @pl.when(near)
                def _(step=step, at=at):
                    self.y_copy(self.c + step * (t + 1), at).wait_send()
                    self.y_copy((self.c ^ 1) + step * (t + 1), at).wait_recv()

        @pl.when(self.right)
        def _():
            self.z_copy(self.c, 0, 2).wait_send()

        @pl.when(self.left)
        def _():
            self.z_copy(self.c, 0, -2).wait_send()

        for t in range(2):

            @pl.when(jnp.logical_and(self.z > t, self.right))
            def _():
                self.z_copy(self.c, t + 1, 2).wait_send()

            @pl.when(jnp.logical_and(self.z < 3 - t, self.left))
            def _():
                self.z_copy(self.c, t + 1, -2).wait_send()


class Columns:

    def __init__(self, source, target, width, first, send, recv, at=None):
        self.source, self.target, self.width, self.first = source, target, width, first
        self.send, self.recv, self.column = send, recv, at
        self.shared = at is None
        self.c, self.w = places_here()
        self.y = self.c % 2

    def taken(self, place, half=None):
        start = place * self.width if self.column is None else self.column
        rows = self.source.shape[0]
        which = slice(None) if half is None else pl.ds(pl.multiple_of(half * (rows // 2), 16), rows // 2)
        return self.source.at[which, pl.ds(pl.multiple_of(start, 128), self.width)]

    def put(self, place, half=None):
        rows = self.source.shape[0]
        start, count = place * rows, rows
        if half is not None:
            start, count = start + half * (rows // 2), rows // 2
        return self.target.at[
            pl.ds(pl.multiple_of(start, 16), count), self.first : self.first + self.width
        ]

    def copy(self, j, place):
        half = self.y if self.shared and j > 1 else None
        return remote(
            self.taken(self.w ^ j, half),
            self.put(place, half),
            self.send.at[j],
            self.recv.at[j],
            self.c,
            self.w ^ j,
        )

    def handed(self, place):
        ref = self.put(place)
        return remote(ref, ref, self.send.at[3], self.recv.at[3], self.c, self.w ^ 1)

    def passed(self, j, half):
        ref = self.put(self.w ^ j, half)
        return remote(ref, ref, self.send.at[2 + j], self.recv.at[2 + j], self.c ^ 1, self.w)

    def own(self):
        return pltpu.make_async_copy(self.taken(self.w), self.put(self.w), self.send.at[0])

    def start(self):
        for j in (2, 3, 1) if self.shared else (2, 1):
            self.copy(j, self.w).start()
        self.own().start()

    def relay(self):
        if not self.shared:
            self.copy(2, self.w).wait_send()
            self.copy(2, self.w ^ 2).wait_recv()
            self.handed(self.w ^ 2).start()
            return
        for j in (2, 3):
            self.copy(j, self.w).wait_send()
            self.copy(j, self.w ^ j).wait_recv()
            self.passed(j, self.y).start()

    def finish(self):
        self.own().wait()
        self.copy(1, self.w).wait_send()
        self.copy(1, self.w ^ 1).wait_recv()
        if not self.shared:
            self.handed(self.w ^ 2).wait_send()
            self.handed(self.w ^ 3).wait_recv()
        else:
            for j in (2, 3):
                self.passed(j, self.y).wait_send()
                self.passed(j, 1 - self.y).wait_recv()


class SmallSum:

    def __init__(self, ref, got, axis, send, recv):
        self.ref, self.got, self.axis, self.send, self.recv = ref, got, axis, send, recv
        self.c, self.w = places_here()

    def copy(self, k):
        j = k + 1
        ctx, wa = (self.c ^ j, self.w) if self.axis == "ctx" else (self.c, self.w ^ j)
        return remote(self.ref, self.got.at[k], self.send.at[k], self.recv.at[k], ctx, wa)

    def start(self):
        for k in range(self.got.shape[0]):
            self.copy(k).start()

    def finish(self):
        count = self.got.shape[0]
        for k in range(count):
            self.copy(k).wait()
        self.ref[...] = tree_sum([self.ref[...]] + [self.got[k] for k in range(count)])


class SwapHeads:

    def __init__(self, by_heads, by_rows, outward, send, recv):
        self.heads, self.rows, self.outward = by_heads, by_rows, outward
        self.send, self.recv = send, recv
        self.c, self.w = places_here()
        self.owner, self.half = self.c // 2, self.c % 2
        self.own = self.owner == self.w
        self.other = jnp.logical_not(self.own)

    def lanes(self):
        return pl.ds(pl.multiple_of(self.half * 128, 128), 128)

    def out_copy(self, j):
        slot = self.w ^ self.owner
        return remote(
            self.heads.at[self.c ^ j],
            self.rows.at[slot, :, self.lanes()],
            self.send.at[j],
            self.recv.at[slot * 2 + self.half],
            self.c ^ j,
            self.owner,
        )

    def start_out(self):
        for j in range(7, 0, -1):
            self.out_copy(j).start()

        @pl.when(self.other)
        def _():
            self.out_copy(0).start()

        @pl.when(self.own)
        def _():
            slot = self.w ^ self.owner
            pltpu.make_async_copy(
                self.heads.at[self.c],
                self.rows.at[slot, :, self.lanes()],
                self.recv.at[slot * 2 + self.half],
            ).start()

    def wait_rows(self, r):
        for h in range(2):
            remote(
                self.heads.at[0],
                self.rows.at[r, :, h * 128 : (h + 1) * 128],
                self.send.at[0],
                self.recv.at[r * 2 + h],
                self.c ^ 1,
                self.w,
            ).wait_recv()

    def finish_out(self):
        for j in range(1, 8):
            self.out_copy(j).wait_send()

        @pl.when(self.other)
        def _():
            self.out_copy(0).wait_send()

    def in_copy(self, r, h):
        return remote(
            self.rows.at[r, :, h * 128 : (h + 1) * 128],
            self.heads.at[self.c],
            self.send.at[r * 2 + h],
            self.recv.at[self.c],
            2 * self.w + h,
            self.w ^ r,
        )

    def mine(self, r, h):
        return jnp.logical_and(2 * self.w + h == self.c, r == 0)

    def start_in(self, r):
        for h in range(2):

            @pl.when(jnp.logical_not(self.mine(r, h)))
            def _():
                self.in_copy(r, h).start()

            @pl.when(self.mine(r, h))
            def _():
                pltpu.make_async_copy(
                    self.rows.at[r, :, h * 128 : (h + 1) * 128],
                    self.heads.at[self.c],
                    self.recv.at[self.c],
                ).start()

    def finish_in(self):
        for block in range(8):
            remote(
                self.rows.at[0, :, 0:128],
                self.heads.at[block],
                self.send.at[0],
                self.recv.at[block],
                self.c ^ 1,
                self.w,
            ).wait_recv()
        for r in range(4):
            for h in range(2):

                @pl.when(jnp.logical_not(self.mine(r, h)))
                def _(r=r, h=h):
                    self.in_copy(r, h).wait_send()


def layer_kernel(names, total_tokens, block, *refs):
    v = types.SimpleNamespace(**dict(zip(names, refs, strict=True)))
    c, w = places_here()
    send, recv, local = Pool(v.send), Pool(v.recv), Pool(v.local)
    tok, width = v.tokens.shape
    seq_len = 8 * tok
    rows = 4 * tok
    cols = v.output_w.shape[0]
    hidden = v.down_w.shape[0]
    scale = HEAD_DIM ** (-0.5)

    def load(source, target):
        copy = pltpu.make_async_copy(source, target, local.take(1).at[0])
        copy.start()
        return copy

    near_load = load(v.neighbours, v.near.at[0])
    late = [
        load(v.output_any, v.output_w),
        load(v.cross_out_any, v.cross_out_w),
        load(v.down_any, v.down_w),
    ]
    mask = v.mask[...].astype(f32)
    v.tokens_all[c] = v.tokens[...]
    meet_all()

    near_sum = SmallSum(v.small_all, v.small_near, "wa", send.take(3), recv.take(3))
    count_sum = SmallSum(v.count, v.count_far, "ctx", send.take(7), recv.take(7))
    gather = LineGather(v.tokens_all, send.take(13), recv.take(13))
    pair = [
        Columns(weight, v.pair, 128, 128 * m, send.take(4), recv.take(4), c * 128)
        for m, weight in enumerate((v.query_any, v.key_any, v.value_any, v.relative_any))
    ]
    cross = [
        Columns(weight, target, cols, first, send.take(6), recv.take(6))
        for weight, target, first in (
            (v.cross_key_any, v.pair_cols, 0),
            (v.cross_value_any, v.pair_cols, cols),
            (v.cross_query_any, v.query_cols, 0),
        )
    ]
    up_columns = Columns(v.up_any, v.up_cols, hidden, 0, send.take(6), recv.take(6))
    near_send, near_recv = send.take(3), recv.take(3)
    near_gather = GatherRows(v.near, near_send, near_recv)
    gather.start()
    for part in pair:
        part.start()

    part_width = width // 4
    count = 3 * part_width + 2 * cols
    entry = lax.broadcasted_iota(jnp.int32, (count, 1024), 0)
    for k in range(1, 3):
        entry = jnp.where(
            lax.broadcasted_iota(jnp.int32, (count, 1024), 0) >= k * part_width, entry - part_width, entry
        )
    bias = lax.broadcasted_iota(jnp.int32, (count, 1024), 0) - 3 * part_width
    entry = jnp.where(bias >= 0, bias, entry)
    entry = jnp.where(bias >= cols, bias - cols, entry)
    start = jnp.where(bias >= 0, w * cols, w * part_width)
    chosen = lax.broadcasted_iota(jnp.int32, (count, 1024), 1) == entry + start
    lane = lax.broadcasted_iota(jnp.int32, (8, count), 1)
    row = lax.broadcasted_iota(jnp.int32, (8, count), 0)
    bounds = (0, part_width, 2 * part_width, 3 * part_width, 3 * part_width + cols, count)
    picked = jnp.zeros((8, count), f32)
    for k in range(5):
        inside = (row == k) & (lane >= bounds[k]) & (lane < bounds[k + 1])
        picked = jnp.where(inside, v.gain_row[...].astype(f32), picked)
    v.small_all[...] = dot_nn(picked.astype(bf16), jnp.where(chosen, 1.0, 0.0).astype(bf16))
    v.small_all[5:6, :] = jnp.broadcast_to(jnp.sum(mask, keepdims=True), (1, 1024))
    near_sum.start()
    near_load.wait()
    near_gather.start()
    for part in cross:
        part.start()

    def wave_rows(part, carry):
        start = pl.multiple_of(part * 64, 64)
        first = v.tables[pl.ds(part, 1), :] * v.tables[32:96, :]
        second = v.tables[pl.ds(part + 16, 1), :] * v.tables[96:160, :]
        v.waves[pl.ds(start, 64), :] = (first + second).astype(bf16)
        return carry

    lax.fori_loop(0, seq_len // 64, wave_rows, 0)
    leaving = Leaving(v, local)
    leaving.leave("waves")
    gather.step(0)
    near_sum.finish()
    v.count[...] = jnp.broadcast_to(v.small_all[5:6, 0:128], v.count.shape)
    count_sum.start()
    for part in pair:
        part.relay()
    gather.step(1)
    for part in pair:
        part.finish()
    v.table[0:seq_len, :] = dot_nn(v.waves[...], v.pair[:, 384:512]).astype(bf16)
    v.table[seq_len:, :] = jnp.zeros((TILE, 128), bf16)
    v.biases[...] = v.small_all[:, pl.ds(pl.multiple_of(c * 128, 128), 128)]
    v.gains[...] = v.small_all[:, 0:width]
    gather.step(2)
    gather.finish()
    gain_one, gain_two, gain_three = (v.gains[k : k + 1, :] for k in range(3))

    def project(part, carry):
        start = pl.multiple_of(part * tok, tok)
        value = v.tokens_all[part].astype(f32)
        normed = (value * inverse_rms(value) * gain_one).astype(bf16)
        v.normed_a[pl.ds(start, tok), :] = normed
        mixed = dot_nn(normed, v.pair[:, 0:384]).astype(bf16)
        for h in range(tok // block):
            v.qkv[part * (tok // block) + h] = mixed[h * block : (h + 1) * block]
        return carry

    lax.fori_loop(0, 8, project, 0)
    leaving.leave("normed_a")
    for place in range(seq_len // block):
        take_block(v.qkv, v.inverse, place, v.qkv_order.at[place * block : (place + 1) * block, :])
    attend_tiles(v.qkv_order, v.table, v.biases[3:4, :], v.biases[4:5, :], v.heads_order)
    per = tok // block
    for place in range(seq_len // block):
        at = (place % per) * block
        take_block(v.heads_order, v.order, place, v.heads.at[place // per, at : at + block, :])
    out_swap = SwapHeads(v.heads, v.attended, True, send.take(8), recv.take(8))
    out_swap.start_out()
    for copy in late:
        copy.wait()

    gathers = [GatherRows(ref, send.take(3), recv.take(3)) for ref in (v.rows_b, v.rows_c)]
    sums = [SumRows(v.give.at[k], v.take.at[k], send.take(3), recv.take(3)) for k in range(3)]

    def output_part(r):
        return dot_nn(v.attended[r], v.output_w[...])

    out_swap.wait_rows(3)
    sums[0].give_far(output_part(3))
    out_swap.wait_rows(1)
    sums[0].give_near(output_part(1))
    out_swap.wait_rows(2)
    sums[0].pass_on(output_part(2))
    near_gather.near()
    near_gather.relay()
    for part in cross:
        part.relay()
    out_swap.wait_rows(0)
    v.hidden_one[...] = v.tokens[...].astype(f32) + sums[0].total(output_part(0))
    value = v.hidden_one[...]
    v.rows_b[0] = (value * inverse_rms(value) * gain_two).astype(bf16)

    gathers[0].start()
    out_swap.finish_out()
    near_gather.far()
    for part in cross:
        part.finish()
    leaving.leave("pair_cols")
    near_count = v.near.shape[1]

    def near_project(r, carry):
        start = pl.multiple_of(r * near_count, near_count)
        v.cross_pair[pl.ds(start, near_count), :] = dot_nn(v.near[r], v.pair_cols[...]).astype(bf16)
        return carry

    lax.fori_loop(0, 4, near_project, 0)

    def cross_part(r):
        v.cross_q[r * tok : (r + 1) * tok, :] = dot_nn(v.rows_b[r], v.query_cols[...]).astype(bf16)

        def group(g, carry):
            at = pl.multiple_of(r * tok + g * GROUP, GROUP)
            near = pl.multiple_of((r * (tok // GROUP) + g) * NK, NK)
            query = stack_all(v.cross_q[pl.ds(at, GROUP), :])
            shares = cross_shares(query, v.cross_pair[pl.ds(near, NK), 0:cols])
            out = dot_nn(shares.astype(bf16), v.cross_pair[pl.ds(near, NK), cols:])
            v.crossed[pl.ds(at, GROUP), :] = join_all(out).astype(bf16)
            return carry

        lax.fori_loop(0, tok // GROUP, group, 0, unroll=True)
        return dot_nn(v.crossed[r * tok : (r + 1) * tok, :], v.cross_out_w[...])

    def in_turn(gathered, summed, part, arrived=None, between=None):
        v.keep[0] = part(0)
        gathered.near()
        summed.give_near(part(1))
        gathered.relay()
        if arrived is not None:
            arrived()
        v.keep[2] = part(2)
        gathered.far()
        summed.give_far(part(3))
        summed.pass_on(v.keep[2])
        if between is not None:
            between()
        return summed.total(v.keep[0])

    v.hidden_two[...] = v.hidden_one[...] + in_turn(
        gathers[0], sums[1], cross_part, up_columns.start, up_columns.relay
    )
    value = v.hidden_two[...]
    v.rows_c[0] = (value * inverse_rms(value) * gain_three).astype(bf16)

    gathers[1].start()
    up_columns.finish()

    def feed_part(r):
        part = pl.ds(r * tok, tok)
        v.pre_act[part, :] = dot_nn(v.rows_c[r], v.up_cols[...])
        v.activated[part, :] = gelu_tanh(v.pre_act[part, :]).astype(bf16)
        return dot_nn(v.activated[part, :], v.down_w[...])

    layer_out = v.hidden_two[...] + in_turn(gathers[1], sums[2], feed_part)
    v.layer_out[...] = layer_out

    count_sum.finish()
    error = layer_out - v.teacher[...].astype(f32)
    square = (tok, tok)
    same = lax.broadcasted_iota(jnp.int32, square, 0) == lax.broadcasted_iota(jnp.int32, square, 1)
    valid = jnp.sum(jnp.where(same, mask, 0.0), axis=1, keepdims=True)
    weighted = valid * error
    v.small[0:5, :] = jnp.zeros((5, 1024), f32)
    v.small[5:6, :] = jnp.broadcast_to(jnp.sum(weighted * error, keepdims=True), (1, 1024))
    v.small[6:8, :] = jnp.broadcast_to(v.count[0:1, 0:1], (2, 1024))
    v.out_grad[...] = (total_tokens / v.count[0:1, 0:1]) * weighted

    leaving.leave("layer_out")
    middle_back(v, send, recv, leaving, block)
    leaving.finish()


class Leaving:

    def __init__(self, v, local):
        self.v, self.local, self.copies = v, local, []

    def leave(self, name):
        copy = pltpu.make_async_copy(
            getattr(self.v, name), getattr(self.v, name + "_any"), self.local.take(1).at[0]
        )
        copy.start()
        self.copies.append(copy)

    def finish(self):
        for copy in self.copies:
            copy.wait()


def take_block(source, chosen, place, target):
    target[...] = source[chosen[place]]


def middle_back(v, send, recv, leaving, block):
    c, w = places_here()
    tok, width = v.tokens.shape
    rows = 4 * tok
    cols = v.output_w.shape[0]
    scale = HEAD_DIM ** (-0.5)
    first, second, third = (
        GatherRows(ref, send.take(3), recv.take(3)) for ref in (v.rows_o, v.rows_two, v.rows_one)
    )
    sum_c, sum_b = (
        SumRows(v.give.at[k], v.take.at[k], send.take(3), recv.take(3)) for k in (3, 4)
    )
    down = CtxSum(send.take(12), recv.take(12), v.down_x, v.down_half, v.down_part, v.down_share)
    up = CtxSum(send.take(12), recv.take(12), v.up_x, v.up_half, v.up_part, v.up_share)
    cross = CtxSum(send.take(12), recv.take(12), v.cross_x, v.cross_half)
    ctx_o = CtxSum(send.take(12), recv.take(12), v.cross_out_x, v.ctx_o_half)
    out_o = CtxSum(send.take(12), recv.take(12), v.output_x, v.out_o_half)
    heads = SwapHeads(v.heads_grad, v.heads_out, False, send.take(8), recv.take(8))
    v.rows_o[0] = v.out_grad[...].astype(bf16)

    first.start()

    def feed_back(r):
        part = pl.ds(r * tok, tok)
        act_grad = dot_nt(v.rows_o[r], v.down_w[...])
        v.pre_grad[part, :] = (act_grad * gelu_slope(v.pre_act[part, :])).astype(bf16)
        return dot_nt(v.pre_grad[part, :], v.up_cols[...])

    v.keep[0] = feed_back(0)
    first.near()
    sum_c.give_near(feed_back(1))
    first.relay()
    v.keep[1] = feed_back(2)
    first.far()
    sum_c.give_far(feed_back(3))
    sum_c.pass_on(v.keep[1])
    put_rows(v.down_x, dot_tn(v.activated[...], v.rows_o[...].reshape(rows, width)))
    down.start_y()
    put_shares(v.up_x, dot_tn(v.rows_c[...].reshape(rows, width), v.pre_grad[...]))
    up.start_y()
    normed_grad = sum_c.total(v.keep[0])
    value = v.hidden_two[...]
    inverse = inverse_rms(value)
    two_grad = v.out_grad[...] + norm_pull(value, inverse, v.gains[2:3, :], normed_grad)
    gain_three = jnp.sum(normed_grad * value * inverse, axis=0, keepdims=True)
    v.keep[1] = two_grad
    v.rows_two[0] = two_grad.astype(bf16)

    second.start()

    def cross_back(r):
        part = slice(r * tok, (r + 1) * tok)
        v.crossed_grad[...] = dot_nt(v.rows_two[r], v.cross_out_w[...]).astype(bf16)

        def group(g, carry):
            within = pl.multiple_of(g * GROUP, GROUP)
            at = pl.multiple_of(r * tok + g * GROUP, GROUP)
            near = pl.ds(pl.multiple_of((r * (tok // GROUP) + g) * NK, NK), NK)
            query = stack_all(v.cross_q[pl.ds(at, GROUP), :])
            grad = stack_all(v.crossed_grad[pl.ds(within, GROUP), :])
            keys = v.cross_pair[near, 0:cols]
            shares = cross_shares(query, keys)
            share_grad = dot_nt(grad, v.cross_pair[near, cols:])
            delta = jnp.sum(shares * share_grad, axis=1, keepdims=True)
            score_grad = (shares * (share_grad - delta)).astype(bf16)
            query_grad = join_all(dot_nn(score_grad, keys)) * scale
            v.cross_grad[pl.ds(at, GROUP), :] = query_grad.astype(bf16)
            v.pair_grad[near, 0:cols] = (dot_tn(score_grad, query) * scale).astype(bf16)
            v.pair_grad[near, cols:] = dot_tn(shares.astype(bf16), grad).astype(bf16)
            return carry

        lax.fori_loop(0, tok // GROUP, group, 0, unroll=True)
        return dot_nt(v.cross_grad[part, :], v.query_cols[...])

    v.keep[0] = cross_back(0)
    second.near()
    sum_b.give_near(cross_back(1))
    second.relay()
    v.keep[2] = cross_back(2)
    second.far()
    down.finish_y()
    down.start_z()
    sum_b.give_far(cross_back(3))
    sum_b.pass_on(v.keep[2])
    leaving.leave("pair_grad")
    normed_b = v.rows_b[...].reshape(rows, width)
    put_rows(v.cross_out_x, dot_tn(v.crossed[...], v.rows_two[...].reshape(rows, width)))
    ctx_o.start_y()
    put_shares(v.cross_x, dot_tn(normed_b, v.cross_grad[...]), 0)
    normed_grad = sum_b.total(v.keep[0])
    value = v.hidden_one[...]
    inverse = inverse_rms(value)
    one_grad = v.keep[1] + norm_pull(value, inverse, v.gains[1:2, :], normed_grad)
    gain_two = jnp.sum(normed_grad * value * inverse, axis=0, keepdims=True)
    v.small[1:2, 0:width] = gain_two
    v.small[2:3, 0:width] = gain_three
    v.one_grad[...] = one_grad
    leaving.leave("one_grad")
    v.rows_one[0] = one_grad.astype(bf16)

    third.start()
    near = v.near[...].reshape(-1, width)
    put_shares(v.cross_x, dot_tn(near, v.pair_grad[...]), cols)

    def head_back(r):
        v.heads_out[r] = dot_nt(v.rows_one[r], v.output_w[...]).astype(bf16)
        heads.start_in(r)

    head_back(0)
    third.near()
    head_back(1)
    third.relay()
    head_back(2)
    third.far()
    head_back(3)
    attended = jnp.concatenate([v.attended[r] for r in range(4)], axis=0)
    put_rows(v.output_x, dot_tn(attended, v.rows_one[...].reshape(rows, width)))
    heads.finish_in()
    up.finish_y()
    up.start_z()
    cross.start_y()
    out_o.start_y()
    leaving.leave("gains")

    per = tok // block
    for place in range(8 * per):
        at = (place % per) * block
        v.heads_stored[place] = v.heads_grad[place // per, at : at + block, :]
    for place in range(8 * per):
        take_block(
            v.heads_stored, v.inverse, place, v.grad_order.at[place * block : (place + 1) * block, :]
        )

    def poll(tile):
        if tile == 1:
            down.finish_z()
            leaving.leave("down_share")
        if tile == 3:
            ctx_o.finish_y()
            leaving.leave("ctx_o_half")

    content_sum, position_sum = attend_back_tiles(
        v.qkv_order,
        v.grad_order,
        v.table,
        v.biases[3:4, :],
        v.biases[4:5, :],
        v.qkv_grad_order,
        v.dkey,
        v.dvalue,
        v.drel,
        poll,
    )
    v.table_grad[...] = v.drel[0 : v.table_grad.shape[0], :] * scale
    leaving.leave("table_grad")
    both = jnp.concatenate([content_sum, position_sum] * 4, axis=1)
    pairs = lax.broadcasted_iota(jnp.int32, both.shape, 1) // 256
    v.small[3:4, :] = jnp.where(pairs == c, both, 0.0)
    v.small[4:5, :] = jnp.where(pairs + 4 == c, both, 0.0)
    leaving.leave("small")
    for place in range(8 * per):
        at = (place % per) * block
        take_block(
            v.qkv_grad_order, v.order, place, v.query_grad.at[place // per, at : at + block, :]
        )
    leaving.leave("query_grad")
    cross.finish_y()
    leaving.leave("cross_half")
    out_o.finish_y()
    leaving.leave("out_o_half")
    up.finish_z()
    leaving.leave("up_share")


def layer(total_tokens, block, orders, given, collective_id):
    tok, width = given["tokens"].shape
    hidden = given["down_any"].shape[0]
    cols = given["output_any"].shape[0]
    near = given["neighbours"].shape[0]
    seq_len = 8 * tok
    rows = 4 * tok
    padded = -(-(width // 32) // 8) * 8
    any_space = pl.BlockSpec(memory_space=pl.ANY)
    shape = jax.ShapeDtypeStruct
    vmem = pltpu.VMEM
    dma = pltpu.SemaphoreType.DMA
    kept = dict(
        layer_out=shape((tok, width), f32),
        small=shape((8, 1024), f32),
        gains=shape((8, width), f32),
        waves=shape((seq_len, width), bf16),
        normed_a=shape((seq_len, width), bf16),
        pair_cols=shape((width, 2 * cols), bf16),
        one_grad=shape((tok, width), f32),
        pair_grad=shape((4 * near, 2 * cols), bf16),
        query_grad=shape((8, tok, 384), bf16),
        table_grad=shape((seq_len, 128), f32),
        down_share=shape((hidden // 8, width), bf16),
        up_share=shape((4, padded, hidden), bf16),
        cross_half=shape((4, 4, padded, 3 * cols), bf16),
        ctx_o_half=shape((4, cols // 8, width), bf16),
        out_o_half=shape((4, cols // 8, width), bf16),
    )
    results = {name + "_any": value for name, value in kept.items()}
    scratch = dict(
        small_all=vmem((8, 1024), f32),
        small_near=vmem((3, 8, 1024), f32),
        qkv=vmem((seq_len // block, block, 384), bf16),
        table=vmem((seq_len + TILE, 128), bf16),
        biases=vmem((8, 128), f32),
        count=vmem((8, 128), f32),
        heads_grad=vmem((8, tok, 128), bf16),
        grad_order=vmem((seq_len, 128), bf16),
        qkv_grad_order=vmem((seq_len // block, block, 384), bf16),
        dkey=vmem((seq_len, 128), f32),
        dvalue=vmem((seq_len, 128), f32),
        drel=vmem((seq_len + TILE, 128), f32),
        cross_out_x=vmem((4, 2, cols // 8, width), bf16),
        output_x=vmem((4, 2, cols // 8, width), bf16),
        count_far=vmem((7, 8, 128), f32),
        tokens_all=vmem((8, tok, width), bf16),
        pair=vmem((width, 512), bf16),
        qkv_order=vmem((seq_len, 384), bf16),
        heads_order=vmem((seq_len // block, block, 128), bf16),
        heads_stored=vmem((seq_len // block, block, 128), bf16),
        heads=vmem((8, tok, 128), bf16),
        attended=vmem((4, tok, cols), bf16),
        near=vmem((4, near, width), bf16),
        query_cols=vmem((width, cols), bf16),
        up_cols=vmem((width, hidden), bf16),
        output_w=vmem((cols, width), bf16),
        cross_out_w=vmem((cols, width), bf16),
        down_w=vmem((hidden, width), bf16),
        cross_pair=vmem((4 * near, 2 * cols), bf16),
        cross_q=vmem((rows, cols), bf16),
        crossed=vmem((rows, cols), bf16),
        crossed_grad=vmem((tok, cols), bf16),
        hidden_one=vmem((tok, width), f32),
        hidden_two=vmem((tok, width), f32),
        out_grad=vmem((tok, width), f32),
        pre_act=vmem((rows, hidden), f32),
        activated=vmem((rows, hidden), bf16),
        rows_b=vmem((4, tok, width), bf16),
        rows_c=vmem((4, tok, width), bf16),
        rows_o=vmem((4, tok, width), bf16),
        rows_two=vmem((4, tok, width), bf16),
        rows_one=vmem((4, tok, width), bf16),
        give=vmem((5, 3, tok, width), bf16),
        take=vmem((5, 3, tok, width), bf16),
        keep=vmem((3, tok, width), f32),
        pre_grad=vmem((rows, hidden), bf16),
        cross_grad=vmem((rows, cols), bf16),
        heads_out=vmem((4, tok, cols), bf16),
        down_x=vmem((4, 2, hidden // 8, width), bf16),
        down_half=vmem((4, hidden // 8, width), bf16),
        down_part=vmem((3, hidden // 8, width), bf16),
        up_x=vmem((4, 2, 4, padded, hidden), bf16),
        up_half=vmem((4, 4, padded, hidden), bf16),
        up_part=vmem((3, 4, padded, hidden), bf16),
        cross_x=vmem((4, 2, 4, padded, 3 * cols), bf16),
        send=dma((232,)),
        recv=dma((232,)),
        local=dma((24,)),
    )
    scratch.update({name: vmem(value.shape, value.dtype) for name, value in kept.items()})
    names = [*orders, *given, *results, *scratch]
    specs = [in_smem] * len(orders) + [
        any_space if name.endswith("_any") or name == "neighbours" else in_vmem for name in given
    ]
    got = pl.pallas_call(
        functools.partial(layer_kernel, names, total_tokens, block),
        out_shape=list(results.values()),
        in_specs=specs,
        out_specs=[any_space] * len(results),
        scratch_shapes=list(scratch.values()),
        compiler_params=pltpu.CompilerParams(
            collective_id=collective_id, has_side_effects=True, vmem_limit_bytes=62 * 2**20
        ),
        name="layer",
    )(*orders.values(), *given.values())
    return types.SimpleNamespace(**dict(zip(kept, got, strict=True)))


class Spread:

    def __init__(self, share, out, send, recv):
        self.share, self.out, self.send, self.recv = share, out, send, recv
        self.c, self.w = places_here()

    def columns(self, place):
        width = self.share.shape[2]
        return self.out.at[self.c, :, pl.ds(pl.multiple_of(place * width, 128), width)]

    def copy(self, j, place):
        return remote(
            self.share.at[self.w ^ j],
            self.columns(place),
            self.send.at[j],
            self.recv.at[j],
            self.c,
            self.w ^ j,
        )

    def own(self):
        return pltpu.make_async_copy(
            self.share.at[self.w], self.columns(self.w), self.send.at[0]
        )

    def start(self):
        for j in (2, 3, 1):
            self.copy(j, self.w).start()
        self.own().start()

    def finish(self):
        self.own().wait()
        for j in (1, 2, 3):
            self.copy(j, self.w).wait_send()
            self.copy(j, self.w ^ j).wait_recv()


class Whole:

    def __init__(self, source, target, send, recv):
        self.source, self.target, self.send, self.recv = source, target, send, recv
        self.c, self.w = places_here()

    def put(self, place):
        rows = self.source.shape[0]
        return self.target.at[pl.ds(pl.multiple_of(place * rows, 32), rows), :]

    def copy(self, j, place):
        return remote(
            self.source, self.put(place), self.send.at[j], self.recv.at[j], self.c, self.w ^ j
        )

    def passed(self, place):
        ref = self.put(place)
        return remote(ref, ref, self.send.at[3], self.recv.at[3], self.c, self.w ^ 1)

    def own(self):
        return pltpu.make_async_copy(self.source, self.put(self.w), self.send.at[0])

    def start(self):
        self.copy(2, self.w).start()
        self.copy(1, self.w).start()
        self.own().start()

    def relay(self):
        self.copy(2, self.w).wait_send()
        self.copy(2, self.w ^ 2).wait_recv()
        self.passed(self.w ^ 2).start()

    def finish(self):
        self.own().wait()
        self.copy(1, self.w).wait_send()
        self.copy(1, self.w ^ 1).wait_recv()
        self.passed(self.w ^ 2).wait_send()
        self.passed(self.w ^ 3).wait_recv()


class MaskSum:

    def __init__(self, ref, got, masks, send, recv):
        self.ref, self.got, self.masks, self.send, self.recv = ref, got, masks, send, recv
        self.c, self.w = places_here()

    def copy(self, k):
        ctx, wa = self.masks[k]
        return remote(
            self.ref, self.got.at[k], self.send.at[k], self.recv.at[k], self.c ^ ctx, self.w ^ wa
        )

    def start(self):
        for k in range(len(self.masks)):
            self.copy(k).start()

    def finish(self):
        for k in range(len(self.masks)):
            self.copy(k).wait()
        self.ref[...] = tree_sum([self.ref[...]] + [self.got[k] for k in range(len(self.masks))])


def finish_kernel(names, *refs):
    v = types.SimpleNamespace(**dict(zip(names, refs, strict=True)))
    c, w = places_here()
    send, recv, local = Pool(v.send), Pool(v.recv), Pool(v.local)
    tok, width = v.tokens.shape
    cols = v.out_o_half.shape[1] * 8
    share = width // 4

    def load(source, target):
        copy = pltpu.make_async_copy(source, target, local.take(1).at[0])
        copy.start()
        return copy

    loads = [load(v.normed_a_any, v.normed_a), load(v.waves_any, v.waves)]
    late = [load(v.pair_cols_any, v.pair_cols), load(v.near_any, v.near_rows)]
    leaving = Leaving(v, local)

    def line(out):
        return LineGather(out, send.take(13), recv.take(13))

    def summed(x, half, part, got):
        return CtxSum(send.take(12), recv.take(12), x, half, part, got)

    down, up, cross, ctx_o, out_o, pair = (
        line(out)
        for out in (v.down_out, v.up_all, v.cross_all, v.cross_o_out, v.output_out, v.pair_all)
    )
    cross_sum = summed(None, v.cross_half, v.cross_part, v.cross_share)
    ctx_o_sum = summed(None, v.ctx_o_half, v.ctx_o_part, v.ctx_o_share)
    out_o_sum = summed(None, v.out_o_half, v.out_o_part, v.out_o_share)
    up_spread = Spread(v.up_share, v.up_all, send.take(4), recv.take(4))
    cross_spread = Spread(v.cross_share, v.cross_all, send.take(4), recv.take(4))
    sum_pair = SumRows(v.pair_give, v.pair_take, send.take(3), recv.take(3))
    sum_near = SumRows(v.near_give, v.near_take, send.take(3), recv.take(3))
    weights = [
        Whole(weight, v.full.at[m], send.take(4), recv.take(4))
        for m, weight in enumerate((v.query_any, v.key_any, v.value_any))
    ]
    stages = [
        MaskSum(v.total, got, masks, send.take(3), recv.take(3))
        for got, masks in (
            (v.got_wa, ((0, 1), (0, 2), (0, 3))),
            (v.got_y, ((1, 0),)),
            (v.got_z, ((2, 0), (4, 0), (6, 0))),
        )
    ]
    b_send, b_recv = send.take(24), recv.take(24)

    def block_copy(j, m, place):
        return remote(
            v.query_grad.at[c ^ j, :, 128 * m : 128 * (m + 1)],
            v.mine.at[m, :, pl.ds(pl.multiple_of(place * 128, 128), 128)],
            b_send.at[3 * j + m],
            b_recv.at[3 * j + m],
            c ^ j,
            w,
        )

    own_blocks = [
        pltpu.make_async_copy(
            v.query_grad.at[c, :, 128 * m : 128 * (m + 1)],
            v.mine.at[m, :, pl.ds(pl.multiple_of(c * 128, 128), 128)],
            b_recv.at[m],
        )
        for m in range(3)
    ]
    v.down_out[c] = v.down_share[...]
    meet_lines()
    up_spread.start()
    cross_sum.start_z()
    down.start()
    ctx_o_sum.start_z()
    out_o_sum.start_z()
    for copy in own_blocks:
        copy.start()

    query_grad = v.query_grad[...].reshape(-1, v.query_grad.shape[2])
    high = v.table_grad[...].astype(bf16)
    low = (v.table_grad[...] - high.astype(f32)).astype(bf16)
    for copy in loads:
        copy.wait()
    mixed = dot_tn(v.normed_a[...], query_grad)
    turned = dot_tn(v.waves[...], high) + dot_tn(v.waves[...], low)
    for place in range(4):
        at = place * share
        v.sums[place] = jnp.concatenate([mixed[at : at + share], turned[at : at + share]], axis=1)
    sum_pair.give_far(v.sums[w ^ 3])
    sum_pair.give_near(v.sums[w ^ 1])
    up_spread.finish()
    up.start()
    sum_pair.pass_on(v.sums[w ^ 2])
    down.step(0)
    v.pair_all[c] = sum_pair.total(v.sums[w]).astype(bf16)
    pair.start()
    for copy in late:
        copy.wait()
    near_count = v.near_grad.shape[0]

    def near_part(r):
        return dot_nt(v.near_rows[r * near_count : (r + 1) * near_count, :], v.pair_cols[...])

    sum_near.give_far(near_part(3))
    sum_near.give_near(near_part(1))
    cross_sum.finish_z()
    cross_spread.start()
    sum_near.pass_on(near_part(2))
    v.near_grad[...] = near_part(0)
    up.step(0)
    down.step(1)
    cross_spread.finish()
    cross.start()
    for j in (4, 6, 5, 7, 2, 3, 1):
        for m in range(3):
            block_copy(j, m, c).start()
    for weight in weights:
        weight.start()
    ctx_o_sum.finish_z()
    v.cross_o_out[c] = v.ctx_o_share[...]
    ctx_o.start()
    out_o_sum.finish_z()
    v.output_out[c] = v.out_o_share[...]
    out_o.start()
    up.step(1)
    cross.step(0)
    pair.step(0)
    down.step(2)
    ctx_o.step(0)
    out_o.step(0)
    up.step(2)
    cross.step(1)
    pair.step(1)
    ctx_o.step(1)
    out_o.step(1)

    for j in range(1, 8):
        for m in range(3):
            block_copy(j, m, c ^ j).wait_recv()
    for copy in own_blocks:
        copy.wait()
    pair.step(2)
    for weight in weights:
        weight.relay()
    for weight in weights:
        weight.finish()
    normed_grad = dot_nt(v.mine[0], v.full[0])
    normed_grad = normed_grad + dot_nt(v.mine[1], v.full[1])
    normed_grad = normed_grad + dot_nt(v.mine[2], v.full[2])
    hidden = v.tokens[...].astype(f32)
    inverse = inverse_rms(hidden)
    v.tokens_grad[...] = v.one_grad[...] + norm_pull(hidden, inverse, v.gains[0:1, :], normed_grad)
    leaving.leave("tokens_grad")
    v.total[...] = v.small[...]
    v.total[0:1, 0:width] = jnp.sum(normed_grad * hidden * inverse, axis=0, keepdims=True)
    stages[0].start()
    ctx_o.step(2)
    out_o.step(2)
    cross.step(2)
    stages[0].finish()
    stages[1].start()
    v.near_grad[...] = sum_near.total(v.near_grad[...])
    leaving.leave("near_grad")
    stages[1].finish()
    stages[2].start()
    down.finish()
    leaving.leave("down_out")
    up.finish()
    used = share // 8
    for part in range(8):
        v.up_out[part * used : (part + 1) * used, :] = v.up_all[part, 0:used, :].astype(f32)
    leaving.leave("up_out")
    pair.finish()
    pair_outs = (v.query_out, v.key_out, v.value_out, v.relative_out)
    for part in range(8):
        for m, out in enumerate(pair_outs):
            out[:, 128 * part : 128 * (part + 1)] = v.pair_all[part, :, 128 * m : 128 * (m + 1)]
    for name in ("query_out", "key_out", "value_out", "relative_out"):
        leaving.leave(name)
    ctx_o.finish()
    leaving.leave("cross_o_out")
    out_o.finish()
    leaving.leave("output_out")
    cross.finish()
    for m, out in enumerate((v.cross_query_out, v.cross_key_out, v.cross_value_out)):
        for part in range(8):
            for place in range(4):
                at = (place * 3 + m) * cols
                out[part * used : (part + 1) * used, place * cols : (place + 1) * cols] = v.cross_all[
                    part, 0:used, at : at + cols
                ].astype(f32)
    for name in ("cross_query_out", "cross_key_out", "cross_value_out"):
        leaving.leave(name)
    stages[2].finish()
    devices = 32.0
    loss = v.total[5:6, :] * devices / (2.0 * width * v.total[6:7, :])
    v.total[7:8, :] = loss
    leaving.leave("total")
    for j in range(1, 8):
        for m in range(3):
            block_copy(j, m, c).wait_send()
    leaving.finish()


def finish(given, collective_id):
    tok, width = given["tokens"].shape
    near = given["near_any"].shape[0]
    padded = given["up_share"].shape[1]
    hidden = given["up_share"].shape[2]
    cols = given["out_o_half"].shape[1] * 8
    share = width // 4
    any_space = pl.BlockSpec(memory_space=pl.ANY)
    shape = jax.ShapeDtypeStruct
    vmem = pltpu.VMEM
    dma = pltpu.SemaphoreType.DMA
    part = (cols // 8, width)
    kept = dict(
        tokens_grad=shape((tok, width), f32),
        near_grad=shape((near // 4, width), f32),
        total=shape(given["small"].shape, f32),
        down_out=shape((8,) + given["down_share"].shape, bf16),
        up_out=shape((share, 4 * hidden), f32),
        cross_query_out=shape((share, 4 * cols), f32),
        cross_key_out=shape((share, 4 * cols), f32),
        cross_value_out=shape((share, 4 * cols), f32),
        cross_o_out=shape((8,) + part, bf16),
        output_out=shape((8,) + part, bf16),
        query_out=shape((share, 1024), bf16),
        key_out=shape((share, 1024), bf16),
        value_out=shape((share, 1024), bf16),
        relative_out=shape((share, 1024), bf16),
    )
    results = {name + "_any": value for name, value in kept.items()}
    scratch = dict(
        normed_a=vmem(given["normed_a_any"].shape, bf16),
        waves=vmem(given["waves_any"].shape, bf16),
        pair_cols=vmem(given["pair_cols_any"].shape, bf16),
        near_rows=vmem(given["near_any"].shape, bf16),
        full=vmem((3, width, 1024), bf16),
        mine=vmem((3, tok, 1024), bf16),
        sums=vmem((4, share, 512), f32),
        up_all=vmem((8, padded, 4 * hidden), bf16),
        cross_all=vmem((8, padded, 12 * cols), bf16),
        pair_all=vmem((8, share, 512), bf16),
        cross_part=vmem((3, 4, padded, 3 * cols), bf16),
        cross_share=vmem((4, padded, 3 * cols), bf16),
        ctx_o_part=vmem((3,) + part, bf16),
        ctx_o_share=vmem(part, bf16),
        out_o_part=vmem((3,) + part, bf16),
        out_o_share=vmem(part, bf16),
        pair_give=vmem((3, share, 512), bf16),
        pair_take=vmem((3, share, 512), bf16),
        near_give=vmem((3, near // 4, width), bf16),
        near_take=vmem((3, near // 4, width), bf16),
        got_wa=vmem((3,) + given["small"].shape, f32),
        got_y=vmem((1,) + given["small"].shape, f32),
        got_z=vmem((3,) + given["small"].shape, f32),
        send=dma((184,)),
        recv=dma((184,)),
        local=dma((24,)),
    )
    scratch.update({name: vmem(value.shape, value.dtype) for name, value in kept.items()})
    names = [*given, *results, *scratch]
    got = pl.pallas_call(
        functools.partial(finish_kernel, names),
        out_shape=list(results.values()),
        in_specs=[any_space if name.endswith("_any") else in_vmem for name in given],
        out_specs=[any_space] * len(results),
        scratch_shapes=list(scratch.values()),
        compiler_params=pltpu.CompilerParams(
            collective_id=collective_id, has_side_effects=True, vmem_limit_bytes=62 * 2**20
        ),
        name="finish",
    )(*given.values())
    return types.SimpleNamespace(**dict(zip(kept, got, strict=True)))


def skew(wide, count):
    lead = wide.shape[:-2]
    rows, span = wide.shape[-2:]
    edge = [(0, 0)] * len(lead)
    padded = jnp.pad(wide, edge + [(0, 0), (0, 1)])
    flat = padded.reshape(lead + (rows * (span + 1),))
    flat = lax.slice_in_dim(flat, rows - 1, rows - 1 + rows * span, axis=len(lead))
    return flat.reshape(lead + (rows, span))[..., :count]


def unskew(grad, span):
    lead = grad.shape[:-2]
    rows, count = grad.shape[-2:]
    edge = [(0, 0)] * len(lead)
    wide = jnp.pad(grad, edge + [(0, 0), (0, span - count)])
    flat = jnp.pad(wide.reshape(lead + (rows * span,)), edge + [(rows - 1, 1)])
    return flat.reshape(lead + (rows, span + 1))[..., :span]


def tile_scores(content_rows, position_rows, key_rows, relative, row_start, key_start):
    rows = content_rows.shape[0]
    count = key_rows.shape[0]
    scale = content_rows.shape[-1] ** (-0.5)
    content = jnp.einsum("qhe,khe->hqk", content_rows, key_rows, preferred_element_type=f32)
    wide = jnp.einsum("qhe,whe->hqw", position_rows, relative, preferred_element_type=f32)
    scores = (content + skew(wide, count)) * scale
    causal = (row_start + jnp.arange(rows))[:, None] >= (key_start + jnp.arange(count))[None, :]
    return (scores, causal[None])


def tile_forward(
    content_rows, position_rows, row_start, relative, key_rows, value_rows, key_start, state
):
    top, total, accum = state
    scores, causal = tile_scores(
        content_rows, position_rows, key_rows, relative, row_start, key_start
    )
    scores = jnp.where(causal, scores, neg_big)
    new_top = jnp.maximum(top, jnp.max(scores, axis=-1))
    raised = jnp.where(causal, jnp.exp(scores - new_top[..., None]), 0.0)
    fade = jnp.exp(top - new_top)
    total = total * fade + jnp.sum(raised, axis=-1)
    accum = accum * fade[..., None] + jnp.einsum(
        "hqk,khe->hqe", raised.astype(bf16), value_rows, preferred_element_type=f32
    )
    return (new_top, total, accum)


def tile_backward(
    content_rows,
    position_rows,
    row_start,
    relative,
    key_rows,
    value_rows,
    grad_rows,
    log_rows,
    delta_rows,
    key_start,
):
    scores, causal = tile_scores(
        content_rows, position_rows, key_rows, relative, row_start, key_start
    )
    scale = content_rows.shape[-1] ** (-0.5)
    shares = jnp.where(causal, jnp.exp(scores - log_rows[..., None]), 0.0)
    share_grad = jnp.einsum("qhe,khe->hqk", grad_rows, value_rows, preferred_element_type=f32)
    score_grad = (shares * (share_grad - delta_rows[..., None])).astype(bf16)
    content_grad = jnp.einsum("hqk,khe->qhe", score_grad, key_rows, preferred_element_type=f32)
    wide_grad = unskew(score_grad, relative.shape[0])
    position_grad = jnp.einsum("hqw,whe->qhe", wide_grad, relative, preferred_element_type=f32)
    table_part = jnp.einsum("hqw,qhe->whe", wide_grad, position_rows, preferred_element_type=f32)
    key_grad = jnp.einsum("hqk,qhe->khe", score_grad, content_rows, preferred_element_type=f32)
    value_grad = jnp.einsum(
        "hqk,qhe->khe", shares.astype(bf16), grad_rows, preferred_element_type=f32
    )
    return (
        content_grad * scale,
        position_grad * scale,
        table_part * scale,
        key_grad * scale,
        value_grad,
    )


def nest_tiles(tile_fn):
    inner = jax.vmap(tile_fn, in_axes=(0, 0, 0, 0, None, None, 0))
    return jax.vmap(inner, in_axes=(0, 0, None, None, 0, 0, 0))


def to_global(stored, inverse, block):
    seqs, seq_len, width = stored.shape
    blocks = stored.reshape(seqs, seq_len // block, block * width)
    chosen = (inverse[:, None] == jnp.arange(seq_len // block)[None, :]).astype(bf16)
    moved = jnp.einsum("gs,nsx->ngx", chosen, blocks, preferred_element_type=f32)
    return moved.astype(bf16).reshape(stored.shape)


class SplitQueries:

    def __init__(self, query, keys, values, biases, relative, block_order, inverse, block):
        self.seqs, self.tok_dev, self.width = keys.shape
        self.heads = self.width // HEAD_DIM
        self.block = block
        self.block_order = block_order
        ctx_count = lax.axis_size("ctx")
        self.seq_len = self.tok_dev * ctx_count
        self.key_len = min(512, self.seq_len)
        pad = jnp.zeros((self.key_len + block, self.width), bf16)
        table = jnp.concatenate([relative, pad], axis=0)
        self.table = table.reshape(-1, self.heads, HEAD_DIM)
        lead = (self.seqs, 2, block, self.heads, HEAD_DIM)
        self.content = (query + biases[0]).astype(bf16).reshape(lead)
        self.position = (query + biases[1]).astype(bf16).reshape(lead)
        gathered = [lax.all_gather(part, "ctx", axis=1, tiled=True) for part in (keys, values)]
        shape = (self.seqs, self.seq_len, self.heads, HEAD_DIM)
        self.keys, self.values = [to_global(part, inverse, block).reshape(shape) for part in gathered]
        self.starts = lax.dynamic_slice_in_dim(block_order, 2 * lax.axis_index("ctx"), 2, 0) * block

    def rows(self, index):
        start = index * self.key_len
        keys = lax.dynamic_slice_in_dim(self.keys, start, self.key_len, 1)
        values = lax.dynamic_slice_in_dim(self.values, start, self.key_len, 1)
        span = self.block + self.key_len
        offsets = [self.seq_len - self.block - self.starts[slot] + start for slot in range(2)]
        relative = [lax.dynamic_slice_in_dim(self.table, offset, span, 0) for offset in offsets]
        return start, keys, values, jnp.stack(relative), offsets

    def to_stored(self, part):
        count = self.seq_len // self.block
        blocks = part.reshape(self.seqs, count, self.block * self.width)
        chosen = (self.block_order[:, None] == jnp.arange(count)[None, :]).astype(f32)
        moved = jnp.einsum("sg,ngx->nsx", chosen, blocks, precision=highest)
        return moved.reshape(self.seqs, self.seq_len, self.width)

    def forward(self):
        def step(state, index):
            start, keys, values, relative, _ = self.rows(index)

            def tile(content, position, row_start, table, keys_seq, values_seq, tile_state):
                return tile_forward(
                    content, position, row_start, table, keys_seq, values_seq, start, tile_state
                )

            return nest_tiles(tile)(
                self.content, self.position, self.starts, relative, keys, values, state
            ), None

        shape = (self.seqs, 2, self.heads, self.block)
        state = (
            jnp.full(shape, neg_big, f32),
            jnp.zeros(shape, f32),
            jnp.zeros(shape + (HEAD_DIM,), f32),
        )
        (top, total, accum), _ = lax.scan(step, state, jnp.arange(self.seq_len // self.key_len))
        self.log_total = top + jnp.log(total)
        self.out = accum / total[..., None]
        moved = jnp.transpose(self.out, (0, 1, 3, 2, 4))
        return moved.reshape(self.seqs * self.tok_dev, self.width).astype(bf16)

    def backward(self, grad):
        block, seq_len, key_len = self.block, self.seq_len, self.key_len
        lead = (self.seqs, 2, block, self.heads, HEAD_DIM)
        grad = grad.reshape(lead)
        delta = jnp.einsum("sbqhe,sbhqe->sbhq", grad.astype(f32), self.out)
        def step(carry, index):
            start, keys, values, relative, offsets = self.rows(index)

            def tile(content, position, row_start, table, keys_seq, values_seq, extra):
                return tile_backward(
                    content, position, row_start, table, keys_seq, values_seq, *extra, start
                )

            extra = (grad, self.log_total, delta)
            parts = nest_tiles(tile)(
                self.content, self.position, self.starts, relative, keys, values, extra
            )
            table = carry[2]
            table_sum = jnp.sum(parts[2], axis=0)
            for slot in range(2):
                offset = offsets[slot]
                current = lax.dynamic_slice_in_dim(table, offset, block + key_len, 0)
                table = lax.dynamic_update_slice_in_dim(table, current + table_sum[slot], offset, 0)
            sums = []
            for total, part in zip(carry[3:], parts[3:]):
                current = lax.dynamic_slice_in_dim(total, start, key_len, 1)
                part = current + jnp.sum(part, axis=1)
                sums.append(lax.dynamic_update_slice_in_dim(total, part, start, 1))
            key_acc, value_acc = sums
            return (carry[0] + parts[0], carry[1] + parts[1], table, key_acc, value_acc), None

        zero_tiles = jnp.zeros(lead, f32)
        zero_keys = jnp.zeros((self.seqs, seq_len, self.heads, HEAD_DIM), f32)
        carry = (zero_tiles, zero_tiles, jnp.zeros(self.table.shape, f32), zero_keys, zero_keys)
        carry, _ = lax.scan(step, carry, jnp.arange(seq_len // key_len))
        owned = [
            lax.psum_scatter(
                self.to_stored(part), "ctx", scatter_dimension=1, tiled=True
            )
            for part in carry[3:]
        ]
        flat = (self.seqs * self.tok_dev, self.width)
        query_grad = (carry[0] + carry[1]).reshape(flat).astype(bf16)
        key_grad, value_grad = [part.reshape(flat).astype(bf16) for part in owned]
        bias_grads = jnp.stack(
            [jnp.sum(part, axis=(0, 1, 2)).reshape(self.width) for part in carry[:2]]
        )
        table_grad = carry[2].reshape(-1, self.width)[:seq_len]
        return query_grad, key_grad, value_grad, bias_grads, table_grad


def local_general(
    tokens,
    neighbours,
    teacher,
    valid_mask,
    block_order,
    query_weight,
    key_weight,
    value_weight,
    output_weight,
    relative_weight,
    content_bias,
    position_bias,
    cross_query_weight,
    cross_key_weight,
    cross_value_weight,
    cross_output_weight,
    up_weight,
    down_weight,
    attention_gain,
    cross_gain,
    feedforward_gain,
):
    places = lax.axis_size("wa")
    ctx_count = lax.axis_size("ctx")
    place = lax.axis_index("wa")
    here = lax.axis_index("ctx")
    _, tok_dev, width = tokens.shape
    seq_len = tok_dev * ctx_count
    block = tok_dev // 2
    cols = HEADS * HEAD_DIM // places
    rows = places * tok_dev

    token_parts = gather_parts(tokens[0])
    query_cols, key_cols, value_cols = [
        take_columns(weight) for weight in (query_weight, key_weight, value_weight)
    ]
    relative_cols = take_columns(relative_weight)
    gains = lax.all_gather(
        jnp.stack([attention_gain, cross_gain, feedforward_gain]), "wa", axis=1, tiled=True
    ).astype(f32)
    gain_one, gain_two, gain_three = gains[0:1], gains[1:2], gains[2:3]
    cross_query_cols, cross_key_cols, cross_value_cols = [
        take_columns(weight) for weight in (cross_query_weight, cross_key_weight, cross_value_weight)
    ]
    cross_pair_cols = jnp.concatenate([cross_key_cols, cross_value_cols], axis=1)
    near_rows = jnp.concatenate(gather_parts(neighbours.reshape(-1, width)), axis=0)
    up_cols = take_columns(up_weight)
    valid = valid_mask.astype(f32).reshape(tok_dev, 1)
    count = jnp.sum(valid).reshape(1, 1)
    count = all_summed(all_summed(count, "wa"), "ctx")

    slots = jnp.arange(2 * ctx_count)
    inverse = jnp.sum(jnp.where(block_order[None, :] == slots[:, None], slots[None, :], 0), axis=1)
    inverse = inverse.astype(jnp.int32)
    distance = (seq_len - 1 - jnp.arange(seq_len)).astype(f32)
    waves = sinusoid(distance, width).astype(bf16)

    hidden_all = jnp.concatenate(token_parts, axis=0).astype(f32)
    scale_all = inverse_rms(hidden_all)
    normed_a = (hidden_all * scale_all * gain_one).astype(bf16)
    biases = jnp.stack([content_bias, position_bias]).astype(f32)
    mixed_cols = jnp.concatenate([query_cols, key_cols, value_cols], axis=1)
    qkv = dot_nn(normed_a, mixed_cols).reshape(places, tok_dev, 3 * cols)
    relative = dot_nn(waves, relative_cols).astype(bf16)
    general = SplitQueries(
        qkv[..., :cols],
        qkv[..., cols : 2 * cols].astype(bf16),
        qkv[..., 2 * cols :].astype(bf16),
        biases,
        relative,
        block_order,
        inverse,
        block,
    )
    attended = general.forward()

    def to_owner(product):
        return scatter_parts([product[r * tok_dev : (r + 1) * tok_dev] for r in range(places)])

    def from_all(value):
        return jnp.concatenate(gather_parts(value), axis=0)

    hidden_in = tokens[0].astype(f32)
    hidden_one = hidden_in + to_owner(dot_nn(attended, output_weight))

    scale_two = inverse_rms(hidden_one)
    normed_b = from_all((hidden_one * scale_two * gain_two).astype(bf16))
    cross_q = dot_nn(normed_b, cross_query_cols).astype(bf16)
    cross_pair = dot_nn(near_rows, cross_pair_cols).astype(bf16)
    crossed = cross_forward(cross_q, cross_pair)
    hidden_two = hidden_one + to_owner(dot_nn(crossed, cross_output_weight))

    scale_three = inverse_rms(hidden_two)
    normed_c = from_all((hidden_two * scale_three * gain_three).astype(bf16))
    pre_act = dot_nn(normed_c, up_cols)
    activated = gelu_tanh(pre_act).astype(bf16)
    layer_out = hidden_two + to_owner(dot_nn(activated, down_weight))

    error = layer_out - teacher[0].astype(f32)
    error_sum = jnp.sum(valid * error * error).reshape(1, 1)
    error_sum = all_summed(all_summed(error_sum, "wa"), "ctx")
    loss = (error_sum / (2.0 * count * width)).reshape(())
    out_grad = (places * seq_len) / count * valid * error

    out_low = from_all(out_grad.astype(bf16))
    act_grad = dot_nt(out_low, down_weight)
    _, gelu_pull = jax.vjp(gelu_tanh, pre_act)
    pre_grad = gelu_pull(act_grad)[0].astype(bf16)
    down_grad = dot_tn(activated, out_low).astype(bf16)
    up_grad = dot_tn(normed_c, pre_grad).astype(bf16)
    normed_c_grad = to_owner(dot_nt(pre_grad, up_cols))
    two_grad = out_grad + norm_pull(hidden_two, scale_three, gain_three, normed_c_grad)
    gain_three_grad = jnp.sum(normed_c_grad * hidden_two * scale_three, axis=0, keepdims=True)
    down_out = sum_row_grads(down_grad)
    up_out = sum_column_grads(up_grad[None])[0]

    two_low = from_all(two_grad.astype(bf16))
    crossed_grad = dot_nt(two_low, cross_output_weight).astype(bf16)
    cross_q_grad, cross_pair_grad = cross_backward(cross_q, cross_pair, crossed_grad)
    normed_b_grad = to_owner(dot_nt(cross_q_grad, cross_query_cols))
    one_grad = two_grad + norm_pull(hidden_one, scale_two, gain_two, normed_b_grad)
    gain_two_grad = jnp.sum(normed_b_grad * hidden_one * scale_two, axis=0, keepdims=True)
    cross_output_grad = dot_tn(crossed, two_low).astype(bf16)
    cross_query_grad = dot_tn(normed_b, cross_q_grad).astype(bf16)
    cross_key_grad = dot_tn(near_rows, cross_pair_grad[:, :cols]).astype(bf16)
    cross_value_grad = dot_tn(near_rows, cross_pair_grad[:, cols:]).astype(bf16)
    cross_output_out = sum_row_grads(cross_output_grad)
    cross_out = sum_column_grads(jnp.stack([cross_key_grad, cross_value_grad]))
    cross_query_out = sum_column_grads(cross_query_grad[None])[0]
    near_grad = dot_nt(cross_pair_grad, cross_pair_cols)
    near_count = near_rows.shape[0] // places
    near_grad = scatter_parts(
        [near_grad[r * near_count : (r + 1) * near_count] for r in range(places)]
    )
    neighbours_grad = near_grad.reshape(neighbours.shape)

    one_low = from_all(one_grad.astype(bf16))
    attended_grad = dot_nt(one_low, output_weight).astype(bf16)
    output_grad = dot_tn(attended, one_low).astype(bf16)
    output_out = sum_row_grads(output_grad)
    query_grad, key_grad, value_grad, bias_grads, table_grad = general.backward(attended_grad)
    qkv_grad = jnp.concatenate([query_grad, key_grad, value_grad], axis=1)
    table_high = table_grad.astype(bf16)
    table_low = (table_grad - table_high.astype(f32)).astype(bf16)
    relative_grad = (dot_tn(waves, table_high) + dot_tn(waves, table_low)).astype(bf16)
    mixed_grad = dot_tn(normed_a, qkv_grad).astype(bf16)
    whole = [mixed_grad[:, m * cols : (m + 1) * cols] for m in range(3)]
    attention_out = sum_column_grads(jnp.stack(whole + [relative_grad]))
    normed_a_part = dot_nt(qkv_grad, mixed_cols)
    gain_one_part = jnp.sum(normed_a_part * hidden_all * scale_all, axis=0, keepdims=True)
    normed_a_grad = to_owner(normed_a_part)
    tokens_grad = one_grad + norm_pull(hidden_in, scale_all[:tok_dev], gain_one, normed_a_grad)

    gain_grads = jnp.concatenate([gain_one_part, gain_two_grad, gain_three_grad], axis=0)
    gain_grads = all_summed(gain_grads, "wa")
    share = width // places
    gain_grads = lax.dynamic_slice_in_dim(gain_grads, place * share, share, 1)
    small = jnp.concatenate([gain_grads.reshape(1, -1), bias_grads.reshape(1, -1)], axis=1)
    small = all_summed(small, "ctx")[0]
    gain_out = small[: 3 * share].reshape(3, share)
    bias_out = small[3 * share :].reshape(2, cols)

    return (
        layer_out[None],
        loss,
        tokens_grad[None],
        neighbours_grad,
        attention_out[0],
        attention_out[1],
        attention_out[2],
        output_out,
        attention_out[3],
        bias_out[0],
        bias_out[1],
        cross_query_out,
        cross_out[0],
        cross_out[1],
        cross_output_out,
        up_out,
        down_out,
        gain_out[0],
        gain_out[1],
        gain_out[2],
    )


def local_by_heads(
    tokens,
    neighbours,
    teacher,
    valid_mask,
    block_order,
    query_weight,
    key_weight,
    value_weight,
    output_weight,
    relative_weight,
    content_bias,
    position_bias,
    cross_query_weight,
    cross_key_weight,
    cross_value_weight,
    cross_output_weight,
    up_weight,
    down_weight,
    attention_gain,
    cross_gain,
    feedforward_gain,
):
    places = 4
    ctx_count = 8
    place = lax.axis_index("wa")
    here = lax.axis_index("ctx")
    _, tok_dev, width = tokens.shape
    seq_len = tok_dev * ctx_count
    block = tok_dev // 2
    attn = HEADS * HEAD_DIM
    cols = attn // places
    share = width // places

    slots = jnp.arange(2 * ctx_count)
    inverse = jnp.sum(jnp.where(block_order[None, :] == slots[:, None], slots[None, :], 0), axis=1)
    inverse = inverse.astype(jnp.int32)
    half = width // 2
    freq = jnp.exp(-jnp.log(10000.0) * jnp.arange(half, dtype=f32) * 2.0 / width)
    coarse = (64.0 * jnp.arange(seq_len // 64, dtype=f32)[::-1])[:, None] * freq
    fine = jnp.arange(64, dtype=f32)[::-1][:, None] * freq
    sin_a, cos_a, sin_b, cos_b = jnp.sin(coarse), jnp.cos(coarse), jnp.sin(fine), jnp.cos(fine)
    left = jnp.concatenate([sin_a, cos_a, cos_b, sin_b], axis=0)
    right = jnp.concatenate([cos_a, -sin_a, cos_b, sin_b], axis=0)
    tables = jnp.concatenate([left, right], axis=1)

    done = layer(
        float(places * seq_len),
        block,
        dict(inverse=inverse, order=block_order),
        dict(
            tokens=tokens[0],
            teacher=teacher[0],
            mask=valid_mask,
            gain_row=jnp.concatenate(
                [attention_gain, cross_gain, feedforward_gain, content_bias, position_bias]
            )[None],
            tables=tables,
            neighbours=neighbours.reshape(-1, width),
            query_any=query_weight,
            key_any=key_weight,
            value_any=value_weight,
            relative_any=relative_weight,
            cross_query_any=cross_query_weight,
            cross_key_any=cross_key_weight,
            cross_value_any=cross_value_weight,
            up_any=up_weight,
            output_any=output_weight,
            cross_out_any=cross_output_weight,
            down_any=down_weight,
        ),
        1,
    )
    last = finish(
        dict(
            query_grad=done.query_grad,
            table_grad=done.table_grad,
            small=done.small,
            down_share=done.down_share,
            up_share=done.up_share,
            cross_half=done.cross_half,
            ctx_o_half=done.ctx_o_half,
            out_o_half=done.out_o_half,
            one_grad=done.one_grad,
            tokens=tokens[0],
            gains=done.gains,
            normed_a_any=done.normed_a,
            waves_any=done.waves,
            near_any=done.pair_grad,
            pair_cols_any=done.pair_cols,
            query_any=query_weight,
            key_any=key_weight,
            value_any=value_weight,
        ),
        2,
    )
    total = last.total
    gain_out = lax.dynamic_slice_in_dim(total[0:3], place * share, share, 1)
    bias_out = lax.dynamic_slice_in_dim(total[3:5].reshape(ctx_count, 2, 128), place * 2, 2, 0)
    bias_out = bias_out.transpose(1, 0, 2).reshape(2, cols)
    loss = total[7, 0]
    down_out = last.down_out.reshape(down_weight.shape).astype(f32)
    cross_output_out = last.cross_o_out.reshape(cols, width).astype(f32)
    output_out = last.output_out.reshape(cols, width).astype(f32)

    return (
        done.layer_out[None],
        loss,
        last.tokens_grad[None],
        last.near_grad.reshape(neighbours.shape),
        last.query_out.astype(f32),
        last.key_out.astype(f32),
        last.value_out.astype(f32),
        output_out,
        last.relative_out.astype(f32),
        bias_out[0],
        bias_out[1],
        last.cross_query_out,
        last.cross_key_out,
        last.cross_value_out,
        cross_output_out,
        last.up_out,
        down_out,
        gain_out[0],
        gain_out[1],
        gain_out[2],
    )


def solution(mesh):
    row = P("wa", None)
    flat = P("wa")
    in_specs = (
        P("wa", "ctx", None),
        P("wa", "ctx", None, None),
        P("wa", "ctx", None),
        P("wa", "ctx"),
        P(),
        row,
        row,
        row,
        row,
        row,
        flat,
        flat,
        row,
        row,
        row,
        row,
        row,
        row,
        flat,
        flat,
        flat,
    )
    out_specs = (
        P("wa", "ctx", None),
        P(),
        P("wa", "ctx", None),
        P("wa", "ctx", None, None),
        row,
        row,
        row,
        row,
        row,
        flat,
        flat,
        row,
        row,
        row,
        row,
        row,
        row,
        flat,
        flat,
        flat,
    )
    by_heads = mesh.shape["ctx"] == 8 and mesh.shape["wa"] == 4
    local = local_by_heads if by_heads else local_general
    return jax.shard_map(local, mesh=mesh, in_specs=in_specs, out_specs=out_specs, check_vma=False)
```

```python
import functools
import types

import jax
import jax.numpy as jnp
from jax import lax
from jax.experimental import pallas as pl
from jax.experimental.pallas import tpu as pltpu
from jax.sharding import PartitionSpec as P

HEADS = 16
HEAD_DIM = 64
GROUP = 64
NK = 256
TILE = 128

eps_norm = 1e-06
neg_big = -1e30
highest = lax.Precision.HIGHEST
f32 = jnp.float32
bf16 = jnp.bfloat16


def inverse_rms(hidden):
    return lax.rsqrt(jnp.mean(hidden * hidden, axis=-1, keepdims=True) + eps_norm)


def norm_pull(hidden, scale, gain, grad):
    scaled = grad * gain
    mean = jnp.mean(hidden * scaled, axis=-1, keepdims=True)
    return scale * scaled - hidden * (scale * scale * scale) * mean


def gelu_tanh(value):
    return jax.nn.gelu(value, approximate=True)


def sinusoid(distance, width):
    half = width // 2
    freq = jnp.exp(-jnp.log(10000.0) * jnp.arange(half, dtype=f32) * 2.0 / width)
    angle = distance[:, None] * freq[None, :]
    return jnp.concatenate([jnp.sin(angle), jnp.cos(angle)], axis=1)


def dot_nn(a, b):
    return lax.dot_general(a, b, (((1,), (0,)), ((), ())), preferred_element_type=f32)


def dot_nt(a, b):
    return lax.dot_general(a, b, (((1,), (1,)), ((), ())), preferred_element_type=f32)


def dot_tn(a, b):
    return lax.dot_general(a, b, (((0,), (0,)), ((), ())), preferred_element_type=f32)


def swap(value, axis, bit):
    pairs = [(i, i ^ bit) for i in range(lax.axis_size(axis))]
    return lax.ppermute(value, axis, pairs)


def bits_of(axis):
    bits, bit = [], 1
    while bit < lax.axis_size(axis):
        bits.append(bit)
        bit *= 2
    return bits


def my_bit(axis, bit):
    return (lax.axis_index(axis) // bit) % 2


def ordered(bit, own, other, dim):
    return jnp.where(
        bit == 0,
        jnp.concatenate([own, other], axis=dim),
        jnp.concatenate([other, own], axis=dim),
    )


def split(value, bit, dim):
    half = value.shape[dim] // 2
    keep = lax.dynamic_slice_in_dim(value, bit * half, half, dim)
    send = lax.dynamic_slice_in_dim(value, (1 - bit) * half, half, dim)
    return keep, send


def gather_parts(value):
    parts = {0: value}
    for bit in reversed(bits_of("wa")):
        parts.update({r | bit: swap(part, "wa", bit) for r, part in list(parts.items())})
    return [parts[r] for r in sorted(parts)]


def scatter_parts(parts):
    parts = dict(enumerate(parts))
    for bit in bits_of("wa"):
        kept = {}
        for r, part in parts.items():
            if not r & bit:
                got = swap(parts[r | bit].astype(bf16), "wa", bit)
                kept[r] = part + got.astype(f32)
        parts = kept
    return parts[0]


def take_columns(weight):
    value = weight[None]
    for bit in reversed(bits_of("wa")):
        mine = my_bit("wa", bit)
        keep, send = split(value, mine, 2)
        value = ordered(mine, keep[:, None], swap(send, "wa", bit)[:, None], 1)
        value = value.reshape((-1,) + value.shape[2:])
    return value.reshape(-1, value.shape[-1])


def spread_columns(value):
    for bit in bits_of("wa"):
        mine = my_bit("wa", bit)
        paired = value.reshape((value.shape[0], value.shape[1] // 2, 2) + value.shape[2:])
        keep, send = split(paired, mine, 2)
        value = ordered(mine, keep[:, :, 0], swap(send[:, :, 0], "wa", bit), 3)
    return value[:, 0]


def halving_dim(shape):
    if shape[-2] % 16 == 0:
        return len(shape) - 2
    if shape[0] % 2 == 0:
        return 0
    if shape[-2] % 2 == 0:
        return len(shape) - 2
    return len(shape) - 1


def sum_over_ctx(value, bits, finish):
    dims = []
    for bit in bits:
        dim = halving_dim(value.shape)
        keep, send = split(value, my_bit("ctx", bit), dim)
        value = (keep.astype(f32) + swap(send, "ctx", bit).astype(f32)).astype(bf16)
        dims.append(dim - value.ndim if dim else 0)
    value = finish(value)
    for bit, dim in reversed(list(zip(bits, dims))):
        dim = dim % value.ndim
        value = ordered(my_bit("ctx", bit), value, swap(value, "ctx", bit), dim)
    return value


def all_summed(value, axis):
    for bit in bits_of(axis):
        value = value + swap(value, axis, bit)
    return value


def sum_column_grads(grads):
    places = lax.axis_size("wa")
    grads = grads.reshape(grads.shape[0], places, grads.shape[1] // places, grads.shape[2])
    bits = bits_of("ctx")
    if grads.shape[2] % lax.axis_size("ctx") == 0:
        return sum_over_ctx(grads, bits, spread_columns).astype(f32)
    return sum_over_ctx(spread_columns(grads), bits, lambda value: value).astype(f32)


def sum_row_grads(grads):
    return sum_over_ctx(grads[None], bits_of("ctx"), lambda value: value)[0].astype(f32)


def first_half(shape):
    return lax.broadcasted_iota(jnp.int32, shape, 1) < HEAD_DIM


def stack_heads(rows):
    mask = first_half(rows.shape)
    zero = jnp.zeros_like(rows)
    return jnp.concatenate([jnp.where(mask, rows, zero), jnp.where(mask, zero, rows)], axis=0)


def join_heads(stacked):
    rows = stacked.shape[0] // 2
    return jnp.where(first_half((rows, stacked.shape[1])), stacked[:rows], stacked[rows:])


def copy_blocks(order_ref, source, target, block, inward):
    for place in range(source.shape[0] // block):
        start = pl.multiple_of(order_ref[place] * block, block)
        if inward:
            target[place * block : (place + 1) * block, :] = source[pl.ds(start, block), :]
        else:
            target[pl.ds(start, block), :] = source[place * block : (place + 1) * block, :]


def attention_shares(content, position, key_ref, rel_ref, row_start, seq_len):
    length = row_start + TILE
    wide_len = length + TILE
    offset = seq_len - TILE - row_start
    scale = HEAD_DIM ** (-0.5)
    scores = dot_nt(content, key_ref[0:length, :])
    wide = dot_nt(position, rel_ref[offset : offset + wide_len, :])
    halves = []
    for head in range(2):
        part = wide[head * TILE : (head + 1) * TILE]
        turned = pltpu.roll(part, wide_len - (TILE - 1), 1, stride=1, stride_axis=0)
        halves.append(turned[:, :length])
    scores = (scores + jnp.concatenate(halves, axis=0)) * scale
    row = lax.broadcasted_iota(jnp.int32, scores.shape, 0) % TILE + row_start
    col = lax.broadcasted_iota(jnp.int32, scores.shape, 1)
    scores = jnp.where(col <= row, scores, neg_big)
    top = jnp.max(scores, axis=1, keepdims=True)
    raised = jnp.exp(scores - top)
    total = jnp.sum(raised, axis=1, keepdims=True)
    return raised * (1.0 / total)


def attend_tiles(qkv, rel_ref, content_bias, position_bias, out):
    seq_len = qkv.shape[0]
    keys = qkv.at[:, 128:256]
    values = qkv.at[:, 256:384]
    for tile in range(seq_len // TILE):
        start = tile * TILE
        query = qkv[start : start + TILE, 0:128].astype(f32)
        content = stack_heads((query + content_bias).astype(bf16))
        position = stack_heads((query + position_bias).astype(bf16))
        shares = attention_shares(content, position, keys, rel_ref, start, seq_len)
        got = dot_nn(shares.astype(bf16), values[0 : start + TILE, :])
        got = join_heads(got).astype(bf16)
        block = out.shape[1]
        for part in range(TILE // block):
            out[start // block + part] = got[part * block : (part + 1) * block]


def attend_back_tiles(
    qkv, grad, rel_ref, content_bias, position_bias, dqkv, dkey, dvalue, drel, poll
):
    scale = HEAD_DIM ** (-0.5)
    seq_len = qkv.shape[0]
    block = dqkv.shape[1]
    keys = qkv.at[:, 128:256]
    values = qkv.at[:, 256:384]
    dkey[...] = jnp.zeros_like(dkey)
    dvalue[...] = jnp.zeros_like(dvalue)
    drel[...] = jnp.zeros_like(drel)
    row = lax.broadcasted_iota(jnp.int32, (TILE, TILE), 0)
    col = lax.broadcasted_iota(jnp.int32, (TILE, TILE), 1)
    flip = jnp.where(row + col == TILE - 1, 1.0, 0.0).astype(bf16)
    content_sum = jnp.zeros((1, 128), f32)
    position_sum = jnp.zeros((1, 128), f32)
    for tile in range(seq_len // TILE):
        poll(tile)
        start = tile * TILE
        length = start + TILE
        wide_len = length + TILE
        offset = seq_len - TILE - start
        query = qkv[start : start + TILE, 0:128].astype(f32)
        content = stack_heads((query + content_bias).astype(bf16))
        plain = (query + position_bias).astype(bf16)
        position = stack_heads(plain)
        shares = attention_shares(content, position, keys, rel_ref, start, seq_len)
        out_grad = stack_heads(grad[start : start + TILE, :])
        share_grad = dot_nt(out_grad, values[0:length, :])
        delta = jnp.sum(shares * share_grad, axis=1, keepdims=True)
        score_grad = (shares * (share_grad - delta)).astype(bf16)
        content_grad = join_heads(dot_nn(score_grad, keys[0:length, :])) * scale
        parts = []
        for head in range(2):
            turned = dot_nn(flip, score_grad[head * TILE : (head + 1) * TILE])
            turned = jnp.concatenate([turned, jnp.zeros((TILE, TILE), f32)], axis=1)
            parts.append(pltpu.roll(turned, 0, 1, stride=1, stride_axis=0))
        wide_grad = jnp.concatenate(parts, axis=0).astype(bf16)
        relative = rel_ref[offset : offset + wide_len, :]
        turned_grad = join_heads(dot_nn(wide_grad, relative)) * scale
        turned_rows = stack_heads(dot_nn(flip, plain).astype(bf16))
        drel[offset : offset + wide_len, :] += dot_tn(wide_grad, turned_rows)
        high = turned_grad.astype(bf16)
        low = (turned_grad - high.astype(f32)).astype(bf16)
        position_grad = dot_nn(flip, high) + dot_nn(flip, low)
        content_sum += jnp.sum(content_grad, axis=0, keepdims=True)
        position_sum += jnp.sum(turned_grad, axis=0, keepdims=True)
        query_grad = (content_grad + position_grad).astype(bf16)
        for part in range(TILE // block):
            dqkv[start // block + part, :, 0:128] = query_grad[part * block : (part + 1) * block]
        dkey[0:length, :] += dot_tn(score_grad, content)
        dvalue[0:length, :] += dot_tn(shares.astype(bf16), out_grad)
    for part in range(seq_len // block):
        rows = slice(part * block, (part + 1) * block)
        dqkv[part, :, 128:256] = (dkey[rows, :] * scale).astype(bf16)
        dqkv[part, :, 256:384] = dvalue[rows, :].astype(bf16)
    return content_sum, position_sum


in_vmem = pl.BlockSpec(memory_space=pltpu.VMEM)
in_smem = pl.BlockSpec(memory_space=pltpu.SMEM)


def head_mask(shape, head):
    lane = lax.broadcasted_iota(jnp.int32, shape, 1)
    return (lane >= head * HEAD_DIM) & (lane < (head + 1) * HEAD_DIM)


def stack_all(rows):
    zero = jnp.zeros_like(rows)
    heads = rows.shape[1] // HEAD_DIM
    return jnp.concatenate(
        [jnp.where(head_mask(rows.shape, head), rows, zero) for head in range(heads)], axis=0
    )


def join_all(stacked):
    heads = stacked.shape[1] // HEAD_DIM
    rows = stacked.shape[0] // heads
    out = jnp.zeros((rows, stacked.shape[1]), stacked.dtype)
    for head in range(heads):
        part = stacked[head * rows : (head + 1) * rows]
        out = jnp.where(head_mask(part.shape, head), part, out)
    return out


def cross_shares(query, keys):
    scores = dot_nt(query, keys) * (HEAD_DIM ** (-0.5))
    raised = jnp.exp(scores - jnp.max(scores, axis=1, keepdims=True))
    return raised / jnp.sum(raised, axis=1, keepdims=True)


def cross_forward_kernel(q_ref, kv_ref, out_ref):
    width = q_ref.shape[1]
    shares = cross_shares(stack_all(q_ref[...]), kv_ref[:, 0:width])
    out_ref[...] = join_all(dot_nn(shares.astype(bf16), kv_ref[:, width:])).astype(bf16)


def cross_backward_kernel(q_ref, kv_ref, grad_ref, dq_ref, dkv_ref):
    width = q_ref.shape[1]
    scale = HEAD_DIM ** (-0.5)
    keys = kv_ref[:, 0:width]
    query = stack_all(q_ref[...])
    grad = stack_all(grad_ref[...])
    shares = cross_shares(query, keys)
    share_grad = dot_nt(grad, kv_ref[:, width:])
    delta = jnp.sum(shares * share_grad, axis=1, keepdims=True)
    score_grad = (shares * (share_grad - delta)).astype(bf16)
    dq_ref[...] = (join_all(dot_nn(score_grad, keys)) * scale).astype(bf16)
    dkv_ref[:, 0:width] = (dot_tn(score_grad, query) * scale).astype(bf16)
    dkv_ref[:, width:] = dot_tn(shares.astype(bf16), grad).astype(bf16)


def cross_forward(query, pair):
    width = query.shape[1]
    groups = query.shape[0] // GROUP
    return pl.pallas_call(
        cross_forward_kernel,
        out_shape=jax.ShapeDtypeStruct(query.shape, bf16),
        grid=(groups,),
        in_specs=[
            pl.BlockSpec((GROUP, width), lambda g: (g, 0)),
            pl.BlockSpec((NK, 2 * width), lambda g: (g, 0)),
        ],
        out_specs=pl.BlockSpec((GROUP, width), lambda g: (g, 0)),
        cost_estimate=pl.CostEstimate(
            flops=groups * 4 * 256 * 256 * 256, bytes_accessed=groups * 330000, transcendentals=groups * 65536
        ),
        name="cross_forward",
    )(query, pair)


def cross_backward(query, pair, grad):
    width = query.shape[1]
    groups = query.shape[0] // GROUP
    return pl.pallas_call(
        cross_backward_kernel,
        out_shape=[
            jax.ShapeDtypeStruct(query.shape, bf16),
            jax.ShapeDtypeStruct(pair.shape, bf16),
        ],
        grid=(groups,),
        in_specs=[
            pl.BlockSpec((GROUP, width), lambda g: (g, 0)),
            pl.BlockSpec((NK, 2 * width), lambda g: (g, 0)),
            pl.BlockSpec((GROUP, width), lambda g: (g, 0)),
        ],
        out_specs=[
            pl.BlockSpec((GROUP, width), lambda g: (g, 0)),
            pl.BlockSpec((NK, 2 * width), lambda g: (g, 0)),
        ],
        cost_estimate=pl.CostEstimate(
            flops=groups * 10 * 256 * 256 * 256, bytes_accessed=groups * 660000, transcendentals=groups * 65536
        ),
        name="cross_backward",
    )(query, pair, grad)


mesh_id = pl.DeviceIdType.MESH


def signal_to(barrier, ctx, wa):
    pl.semaphore_signal(barrier, inc=1, device_id=(ctx, wa), device_id_type=mesh_id)


def tree_sum(values):
    while len(values) > 1:
        values = [a + b for a, b in zip(values[::2], values[1::2])]
    return values[0]


def gelu_slope(value):
    inner = 0.7978845608028654 * (value + 0.044715 * value * value * value)
    turned = jnp.tanh(inner)
    slope = 0.7978845608028654 * (1.0 + 3.0 * 0.044715 * value * value)
    return 0.5 * (1.0 + turned) + 0.5 * value * (1.0 - turned * turned) * slope


def places_here():
    return lax.axis_index("ctx"), lax.axis_index("wa")


def meet_all():
    c, w = places_here()
    owner = c // 2
    own = owner == w
    barrier = pltpu.get_barrier_semaphore()
    for j in range(1, 8):
        signal_to(barrier, c ^ j, w)
    for j in range(1, 4):
        signal_to(barrier, c, w ^ j)
    for j in range(1, 8):
        signal_to(barrier, c ^ j, owner)
    for r in range(4):
        for h in range(2):

            @pl.when(jnp.logical_not(jnp.logical_and(2 * w + h == c, r == 0)))
            def _(r=r, h=h):
                signal_to(barrier, 2 * w + h, w ^ r)

    @pl.when(jnp.logical_not(own))
    def _():
        signal_to(barrier, c, owner)

    pl.semaphore_wait(barrier, 26 - 2 * own.astype(jnp.int32))


def meet_lines():
    c, w = places_here()
    barrier = pltpu.get_barrier_semaphore()
    for j in range(1, 8):
        signal_to(barrier, c ^ j, w)
    for j in range(1, 4):
        signal_to(barrier, c, w ^ j)
    pl.semaphore_wait(barrier, 10)


def remote(source, target, send, recv, ctx, wa):
    return pltpu.make_async_remote_copy(
        src_ref=source,
        dst_ref=target,
        send_sem=send,
        recv_sem=recv,
        device_id=(ctx, wa),
        device_id_type=mesh_id,
    )


class GatherRows:

    def __init__(self, buf, send, recv):
        self.buf, self.send, self.recv = buf, send, recv
        self.c, self.w = places_here()

    def copy(self, k):
        source, entry, j = ((0, 1, 1), (0, 2, 2), (2, 3, 1))[k]
        return remote(
            self.buf.at[source],
            self.buf.at[entry],
            self.send.at[k],
            self.recv.at[k],
            self.c,
            self.w ^ j,
        )

    def start(self):
        self.copy(1).start()
        self.copy(0).start()

    def near(self):
        self.copy(0).wait()

    def relay(self):
        self.copy(1).wait()
        self.copy(2).start()

    def far(self):
        self.copy(2).wait()


class SumRows:

    def __init__(self, out_buf, in_buf, send, recv):
        self.out, self.inn, self.send, self.recv = out_buf, in_buf, send, recv
        self.c, self.w = places_here()

    def copy(self, k):
        j = (1, 1, 2)[k]
        return remote(
            self.out.at[k], self.inn.at[k], self.send.at[k], self.recv.at[k], self.c, self.w ^ j
        )

    def give_near(self, value):
        self.out[0] = value.astype(bf16)
        self.copy(0).start()

    def give_far(self, value):
        self.out[1] = value.astype(bf16)
        self.copy(1).start()

    def pass_on(self, value):
        self.copy(1).wait()
        self.out[2] = (value + self.inn[1].astype(f32)).astype(bf16)
        self.copy(2).start()

    def total(self, value):
        self.copy(0).wait()
        value = value + self.inn[0].astype(f32)
        self.copy(2).wait()
        return value + self.inn[2].astype(f32)


class CtxSum:

    def __init__(self, send, recv, x=None, half=None, part=None, share=None, out=None, spread=0):
        self.send, self.recv = send, recv
        self.x, self.half, self.part, self.share, self.out = x, half, part, share, out
        self.spread = spread
        self.c, self.w = places_here()
        self.z, self.y = self.c // 2, self.c % 2

    def y_copy(self):
        return remote(
            self.x.at[:, 1 - self.y], self.half, self.send.at[0], self.recv.at[0], self.c ^ 1, self.w
        )

    def start_y(self):
        self.y_copy().start()

    def finish_y(self):
        self.y_copy().wait()
        for z in range(4):
            mine = self.x[z, self.y].astype(f32)
            self.half[z] = (self.half[z].astype(f32) + mine).astype(bf16)

    def z_copy(self, j):
        return remote(
            self.half.at[self.z ^ j],
            self.part.at[j - 1],
            self.send.at[j],
            self.recv.at[j],
            self.c ^ (2 * j),
            self.w,
        )

    def start_z(self, order=(2, 3, 1)):
        for j in order:
            self.z_copy(j).start()

    def finish_z(self):
        total = self.half[self.z].astype(f32)
        for j in (1, 2, 3):
            self.z_copy(j).wait()
            total = total + self.part[j - 1].astype(f32)
        if len(self.share.shape) == 2:
            self.share[...] = total.astype(bf16)
            return
        count = total.shape[0] // 4
        blank = jnp.zeros((self.share.shape[1] - count, total.shape[1]), f32)
        for place in range(4):
            part = jnp.concatenate([total[place * count : (place + 1) * count], blank], axis=0)
            self.share[place] = part.astype(bf16)

    def columns(self, place):
        width = self.spread
        return self.out.at[self.z, self.y, :, pl.ds(pl.multiple_of(place * width, 128), width)]

    def wa_copy(self, j, place):
        return remote(
            self.share.at[self.w ^ j],
            self.columns(place),
            self.send.at[3 + j],
            self.recv.at[3 + j],
            self.c,
            self.w ^ j,
        )

    def own_copy(self):
        source = self.share.at[self.w] if self.spread else self.share
        target = self.columns(self.w) if self.spread else self.out.at[self.z, self.y]
        return pltpu.make_async_copy(source, target, self.send.at[11])

    def start_wa(self):
        if self.spread:
            for j in (2, 3, 1):
                self.wa_copy(j, self.w).start()
        self.own_copy().start()

    def finish_wa(self):
        self.own_copy().wait()
        if self.spread:
            for j in (1, 2, 3):
                self.wa_copy(j, self.w).wait_send()
                self.wa_copy(j, self.w ^ j).wait_recv()

    def back_z_copy(self, j, z):
        mine = self.out.at[z, self.y]
        return remote(mine, mine, self.send.at[6 + j], self.recv.at[6 + j], self.c ^ (2 * j), self.w)

    def start_back_z(self):
        for j in (2, 3, 1):
            self.back_z_copy(j, self.z).start()

    def finish_back_z(self):
        for j in (1, 2, 3):
            self.back_z_copy(j, self.z).wait_send()
            self.back_z_copy(j, self.z ^ j).wait_recv()

    def back_y_copy(self, y):
        part = self.out.at[:, y]
        return remote(part, part, self.send.at[10], self.recv.at[10], self.c ^ 1, self.w)

    def start_back_y(self):
        self.back_y_copy(self.y).start()

    def finish_back_y(self):
        self.back_y_copy(self.y).wait_send()
        self.back_y_copy(1 - self.y).wait_recv()


def put_shares(target, grads, first=0):
    count = grads.shape[0] // 32
    for share in range(8):
        starts = [(place * 8 + share) * count for place in range(4)]
        part = jnp.concatenate([grads[start : start + count] for start in starts], axis=0)
        target[share // 2, share % 2, :, first : first + part.shape[1]] = part.astype(bf16)


def put_rows(target, grads):
    count = grads.shape[0] // 8
    for share in range(8):
        target[share // 2, share % 2] = grads[share * count : (share + 1) * count].astype(bf16)


class Cut:

    def __init__(self, ref, start):
        self.ref, self.start = ref, start

    @property
    def at(self):
        return self

    def __getitem__(self, k):
        return self.ref.at[self.start + k]


class Pool:
    def __init__(self, ref):
        self.ref, self.used = ref, 0

    def take(self, count):
        cut = Cut(self.ref, self.used)
        self.used += count
        return cut


class LineGather:

    def __init__(self, out, send, recv):
        self.out, self.send, self.recv = out, send, recv
        self.c, self.w = places_here()
        self.z = self.c // 2
        self.right, self.left = self.z < 3, self.z > 0

    def y_copy(self, block, slot):
        ref = self.out.at[block]
        return remote(ref, ref, self.send.at[slot], self.recv.at[slot], self.c ^ 1, self.w)

    def z_copy(self, block, slot, step):
        k = slot + (7 if step > 0 else 10)
        ref = self.out.at[block]
        return remote(ref, ref, self.send.at[k], self.recv.at[k], self.c + step, self.w)

    def start(self):
        @pl.when(self.right)
        def _():
            self.z_copy(self.c, 0, 2).start()

        @pl.when(self.left)
        def _():
            self.z_copy(self.c, 0, -2).start()

        self.y_copy(self.c, 0).start()

    def step(self, t):
        @pl.when(self.z > t)
        def _():
            block = self.c - 2 * (t + 1)
            self.z_copy(block, t, 2).wait_recv()
            if t < 2:

                @pl.when(self.right)
                def _():
                    self.z_copy(block, t + 1, 2).start()

            self.y_copy(block, t + 1).start()

        @pl.when(self.z < 3 - t)
        def _():
            block = self.c + 2 * (t + 1)
            self.z_copy(block, t, -2).wait_recv()
            if t < 2:

                @pl.when(self.left)
                def _():
                    self.z_copy(block, t + 1, -2).start()

            self.y_copy(block, t + 4).start()

    def finish(self):
        self.y_copy(self.c, 0).wait_send()
        self.y_copy(self.c ^ 1, 0).wait_recv()
        for t in range(3):
            for step, at, near in ((-2, t + 1, self.z > t), (2, t + 4, self.z < 3 - t)):

                @pl.when(near)
                def _(step=step, at=at):
                    self.y_copy(self.c + step * (t + 1), at).wait_send()
                    self.y_copy((self.c ^ 1) + step * (t + 1), at).wait_recv()

        @pl.when(self.right)
        def _():
            self.z_copy(self.c, 0, 2).wait_send()

        @pl.when(self.left)
        def _():
            self.z_copy(self.c, 0, -2).wait_send()

        for t in range(2):

            @pl.when(jnp.logical_and(self.z > t, self.right))
            def _():
                self.z_copy(self.c, t + 1, 2).wait_send()

            @pl.when(jnp.logical_and(self.z < 3 - t, self.left))
            def _():
                self.z_copy(self.c, t + 1, -2).wait_send()


class Columns:

    def __init__(self, source, target, width, first, send, recv, at=None):
        self.source, self.target, self.width, self.first = source, target, width, first
        self.send, self.recv, self.column = send, recv, at
        self.shared = at is None
        self.c, self.w = places_here()
        self.y = self.c % 2

    def taken(self, place, half=None):
        start = place * self.width if self.column is None else self.column
        rows = self.source.shape[0]
        which = slice(None) if half is None else pl.ds(pl.multiple_of(half * (rows // 2), 16), rows // 2)
        return self.source.at[which, pl.ds(pl.multiple_of(start, 128), self.width)]

    def put(self, place, half=None):
        rows = self.source.shape[0]
        start, count = place * rows, rows
        if half is not None:
            start, count = start + half * (rows // 2), rows // 2
        return self.target.at[
            pl.ds(pl.multiple_of(start, 16), count), self.first : self.first + self.width
        ]

    def copy(self, j, place):
        half = self.y if self.shared and j > 1 else None
        return remote(
            self.taken(self.w ^ j, half),
            self.put(place, half),
            self.send.at[j],
            self.recv.at[j],
            self.c,
            self.w ^ j,
        )

    def handed(self, place):
        ref = self.put(place)
        return remote(ref, ref, self.send.at[3], self.recv.at[3], self.c, self.w ^ 1)

    def passed(self, j, half):
        ref = self.put(self.w ^ j, half)
        return remote(ref, ref, self.send.at[2 + j], self.recv.at[2 + j], self.c ^ 1, self.w)

    def own(self):
        return pltpu.make_async_copy(self.taken(self.w), self.put(self.w), self.send.at[0])

    def start(self):
        for j in (2, 3, 1) if self.shared else (2, 1):
            self.copy(j, self.w).start()
        self.own().start()

    def relay(self):
        if not self.shared:
            self.copy(2, self.w).wait_send()
            self.copy(2, self.w ^ 2).wait_recv()
            self.handed(self.w ^ 2).start()
            return
        for j in (2, 3):
            self.copy(j, self.w).wait_send()
            self.copy(j, self.w ^ j).wait_recv()
            self.passed(j, self.y).start()

    def finish(self):
        self.own().wait()
        self.copy(1, self.w).wait_send()
        self.copy(1, self.w ^ 1).wait_recv()
        if not self.shared:
            self.handed(self.w ^ 2).wait_send()
            self.handed(self.w ^ 3).wait_recv()
        else:
            for j in (2, 3):
                self.passed(j, self.y).wait_send()
                self.passed(j, 1 - self.y).wait_recv()


class SmallSum:

    def __init__(self, ref, got, axis, send, recv):
        self.ref, self.got, self.axis, self.send, self.recv = ref, got, axis, send, recv
        self.c, self.w = places_here()

    def copy(self, k):
        j = k + 1
        ctx, wa = (self.c ^ j, self.w) if self.axis == "ctx" else (self.c, self.w ^ j)
        return remote(self.ref, self.got.at[k], self.send.at[k], self.recv.at[k], ctx, wa)

    def start(self):
        for k in range(self.got.shape[0]):
            self.copy(k).start()

    def finish(self):
        count = self.got.shape[0]
        for k in range(count):
            self.copy(k).wait()
        self.ref[...] = tree_sum([self.ref[...]] + [self.got[k] for k in range(count)])


class SwapHeads:

    def __init__(self, by_heads, by_rows, outward, send, recv):
        self.heads, self.rows, self.outward = by_heads, by_rows, outward
        self.send, self.recv = send, recv
        self.c, self.w = places_here()
        self.owner, self.half = self.c // 2, self.c % 2
        self.own = self.owner == self.w
        self.other = jnp.logical_not(self.own)

    def lanes(self):
        return pl.ds(pl.multiple_of(self.half * 128, 128), 128)

    def out_copy(self, j):
        slot = self.w ^ self.owner
        return remote(
            self.heads.at[self.c ^ j],
            self.rows.at[slot, :, self.lanes()],
            self.send.at[j],
            self.recv.at[slot * 2 + self.half],
            self.c ^ j,
            self.owner,
        )

    def start_out(self):
        for j in range(7, 0, -1):
            self.out_copy(j).start()

        @pl.when(self.other)
        def _():
            self.out_copy(0).start()

        @pl.when(self.own)
        def _():
            slot = self.w ^ self.owner
            pltpu.make_async_copy(
                self.heads.at[self.c],
                self.rows.at[slot, :, self.lanes()],
                self.recv.at[slot * 2 + self.half],
            ).start()

    def wait_rows(self, r):
        for h in range(2):
            remote(
                self.heads.at[0],
                self.rows.at[r, :, h * 128 : (h + 1) * 128],
                self.send.at[0],
                self.recv.at[r * 2 + h],
                self.c ^ 1,
                self.w,
            ).wait_recv()

    def finish_out(self):
        for j in range(1, 8):
            self.out_copy(j).wait_send()

        @pl.when(self.other)
        def _():
            self.out_copy(0).wait_send()

    def in_copy(self, r, h):
        return remote(
            self.rows.at[r, :, h * 128 : (h + 1) * 128],
            self.heads.at[self.c],
            self.send.at[r * 2 + h],
            self.recv.at[self.c],
            2 * self.w + h,
            self.w ^ r,
        )

    def mine(self, r, h):
        return jnp.logical_and(2 * self.w + h == self.c, r == 0)

    def start_in(self, r):
        for h in range(2):

            @pl.when(jnp.logical_not(self.mine(r, h)))
            def _():
                self.in_copy(r, h).start()

            @pl.when(self.mine(r, h))
            def _():
                pltpu.make_async_copy(
                    self.rows.at[r, :, h * 128 : (h + 1) * 128],
                    self.heads.at[self.c],
                    self.recv.at[self.c],
                ).start()

    def finish_in(self):
        for block in range(8):
            remote(
                self.rows.at[0, :, 0:128],
                self.heads.at[block],
                self.send.at[0],
                self.recv.at[block],
                self.c ^ 1,
                self.w,
            ).wait_recv()
        for r in range(4):
            for h in range(2):

                @pl.when(jnp.logical_not(self.mine(r, h)))
                def _(r=r, h=h):
                    self.in_copy(r, h).wait_send()


def layer_kernel(names, total_tokens, block, *refs):
    v = types.SimpleNamespace(**dict(zip(names, refs, strict=True)))
    c, w = places_here()
    send, recv, local = Pool(v.send), Pool(v.recv), Pool(v.local)
    tok, width = v.tokens.shape
    seq_len = 8 * tok
    rows = 4 * tok
    cols = v.output_w.shape[0]
    hidden = v.down_w.shape[0]
    scale = HEAD_DIM ** (-0.5)

    def load(source, target):
        copy = pltpu.make_async_copy(source, target, local.take(1).at[0])
        copy.start()
        return copy

    near_load = load(v.neighbours, v.near.at[0])
    late = [
        load(v.output_any, v.output_w),
        load(v.cross_out_any, v.cross_out_w),
        load(v.down_any, v.down_w),
    ]
    mask = v.mask[...].astype(f32)
    v.tokens_all[c] = v.tokens[...]
    meet_all()

    near_sum = SmallSum(v.small_all, v.small_near, "wa", send.take(3), recv.take(3))
    count_sum = SmallSum(v.count, v.count_far, "ctx", send.take(7), recv.take(7))
    gather = LineGather(v.tokens_all, send.take(13), recv.take(13))
    pair = [
        Columns(weight, v.pair, 128, 128 * m, send.take(4), recv.take(4), c * 128)
        for m, weight in enumerate((v.query_any, v.key_any, v.value_any, v.relative_any))
    ]
    cross = [
        Columns(weight, target, cols, first, send.take(6), recv.take(6))
        for weight, target, first in (
            (v.cross_key_any, v.pair_cols, 0),
            (v.cross_value_any, v.pair_cols, cols),
            (v.cross_query_any, v.query_cols, 0),
        )
    ]
    up_columns = Columns(v.up_any, v.up_cols, hidden, 0, send.take(6), recv.take(6))
    near_send, near_recv = send.take(3), recv.take(3)
    near_gather = GatherRows(v.near, near_send, near_recv)
    gather.start()
    for part in pair:
        part.start()

    part_width = width // 4
    count = 3 * part_width + 2 * cols
    entry = lax.broadcasted_iota(jnp.int32, (count, 1024), 0)
    for k in range(1, 3):
        entry = jnp.where(
            lax.broadcasted_iota(jnp.int32, (count, 1024), 0) >= k * part_width, entry - part_width, entry
        )
    bias = lax.broadcasted_iota(jnp.int32, (count, 1024), 0) - 3 * part_width
    entry = jnp.where(bias >= 0, bias, entry)
    entry = jnp.where(bias >= cols, bias - cols, entry)
    start = jnp.where(bias >= 0, w * cols, w * part_width)
    chosen = lax.broadcasted_iota(jnp.int32, (count, 1024), 1) == entry + start
    lane = lax.broadcasted_iota(jnp.int32, (8, count), 1)
    row = lax.broadcasted_iota(jnp.int32, (8, count), 0)
    bounds = (0, part_width, 2 * part_width, 3 * part_width, 3 * part_width + cols, count)
    picked = jnp.zeros((8, count), f32)
    for k in range(5):
        inside = (row == k) & (lane >= bounds[k]) & (lane < bounds[k + 1])
        picked = jnp.where(inside, v.gain_row[...].astype(f32), picked)
    v.small_all[...] = dot_nn(picked.astype(bf16), jnp.where(chosen, 1.0, 0.0).astype(bf16))
    v.small_all[5:6, :] = jnp.broadcast_to(jnp.sum(mask, keepdims=True), (1, 1024))
    near_sum.start()
    near_load.wait()
    near_gather.start()
    for part in cross:
        part.start()

    def wave_rows(part, carry):
        start = pl.multiple_of(part * 64, 64)
        first = v.tables[pl.ds(part, 1), :] * v.tables[32:96, :]
        second = v.tables[pl.ds(part + 16, 1), :] * v.tables[96:160, :]
        v.waves[pl.ds(start, 64), :] = (first + second).astype(bf16)
        return carry

    lax.fori_loop(0, seq_len // 64, wave_rows, 0)
    leaving = Leaving(v, local)
    leaving.leave("waves")
    gather.step(0)
    near_sum.finish()
    v.count[...] = jnp.broadcast_to(v.small_all[5:6, 0:128], v.count.shape)
    count_sum.start()
    for part in pair:
        part.relay()
    gather.step(1)
    for part in pair:
        part.finish()
    v.table[0:seq_len, :] = dot_nn(v.waves[...], v.pair[:, 384:512]).astype(bf16)
    v.table[seq_len:, :] = jnp.zeros((TILE, 128), bf16)
    v.biases[...] = v.small_all[:, pl.ds(pl.multiple_of(c * 128, 128), 128)]
    v.gains[...] = v.small_all[:, 0:width]
    gather.step(2)
    gather.finish()
    gain_one, gain_two, gain_three = (v.gains[k : k + 1, :] for k in range(3))

    def project(part, carry):
        start = pl.multiple_of(part * tok, tok)
        value = v.tokens_all[part].astype(f32)
        normed = (value * inverse_rms(value) * gain_one).astype(bf16)
        v.normed_a[pl.ds(start, tok), :] = normed
        mixed = dot_nn(normed, v.pair[:, 0:384]).astype(bf16)
        for h in range(tok // block):
            v.qkv[part * (tok // block) + h] = mixed[h * block : (h + 1) * block]
        return carry

    lax.fori_loop(0, 8, project, 0)
    leaving.leave("normed_a")
    for place in range(seq_len // block):
        take_block(v.qkv, v.inverse, place, v.qkv_order.at[place * block : (place + 1) * block, :])
    attend_tiles(v.qkv_order, v.table, v.biases[3:4, :], v.biases[4:5, :], v.heads_order)
    per = tok // block
    for place in range(seq_len // block):
        at = (place % per) * block
        take_block(v.heads_order, v.order, place, v.heads.at[place // per, at : at + block, :])
    out_swap = SwapHeads(v.heads, v.attended, True, send.take(8), recv.take(8))
    out_swap.start_out()
    for copy in late:
        copy.wait()

    gathers = [GatherRows(ref, send.take(3), recv.take(3)) for ref in (v.rows_b, v.rows_c)]
    sums = [SumRows(v.give.at[k], v.take.at[k], send.take(3), recv.take(3)) for k in range(3)]

    def output_part(r):
        return dot_nn(v.attended[r], v.output_w[...])

    out_swap.wait_rows(3)
    sums[0].give_far(output_part(3))
    out_swap.wait_rows(1)
    sums[0].give_near(output_part(1))
    out_swap.wait_rows(2)
    sums[0].pass_on(output_part(2))
    near_gather.near()
    near_gather.relay()
    for part in cross:
        part.relay()
    out_swap.wait_rows(0)
    v.hidden_one[...] = v.tokens[...].astype(f32) + sums[0].total(output_part(0))
    value = v.hidden_one[...]
    v.rows_b[0] = (value * inverse_rms(value) * gain_two).astype(bf16)

    gathers[0].start()
    out_swap.finish_out()
    near_gather.far()
    for part in cross:
        part.finish()
    leaving.leave("pair_cols")
    near_count = v.near.shape[1]

    def near_project(r, carry):
        start = pl.multiple_of(r * near_count, near_count)
        v.cross_pair[pl.ds(start, near_count), :] = dot_nn(v.near[r], v.pair_cols[...]).astype(bf16)
        return carry

    lax.fori_loop(0, 4, near_project, 0)

    def cross_part(r):
        v.cross_q[r * tok : (r + 1) * tok, :] = dot_nn(v.rows_b[r], v.query_cols[...]).astype(bf16)

        def group(g, carry):
            at = pl.multiple_of(r * tok + g * GROUP, GROUP)
            near = pl.multiple_of((r * (tok // GROUP) + g) * NK, NK)
            query = stack_all(v.cross_q[pl.ds(at, GROUP), :])
            shares = cross_shares(query, v.cross_pair[pl.ds(near, NK), 0:cols])
            out = dot_nn(shares.astype(bf16), v.cross_pair[pl.ds(near, NK), cols:])
            v.crossed[pl.ds(at, GROUP), :] = join_all(out).astype(bf16)
            return carry

        lax.fori_loop(0, tok // GROUP, group, 0, unroll=True)
        return dot_nn(v.crossed[r * tok : (r + 1) * tok, :], v.cross_out_w[...])

    def in_turn(gathered, summed, part, arrived=None, between=None):
        v.keep[0] = part(0)
        gathered.near()
        summed.give_near(part(1))
        gathered.relay()
        if arrived is not None:
            arrived()
        v.keep[2] = part(2)
        gathered.far()
        summed.give_far(part(3))
        summed.pass_on(v.keep[2])
        if between is not None:
            between()
        return summed.total(v.keep[0])

    v.hidden_two[...] = v.hidden_one[...] + in_turn(
        gathers[0], sums[1], cross_part, up_columns.start, up_columns.relay
    )
    value = v.hidden_two[...]
    v.rows_c[0] = (value * inverse_rms(value) * gain_three).astype(bf16)

    gathers[1].start()
    up_columns.finish()

    def feed_part(r):
        part = pl.ds(r * tok, tok)
        v.pre_act[part, :] = dot_nn(v.rows_c[r], v.up_cols[...])
        v.activated[part, :] = gelu_tanh(v.pre_act[part, :]).astype(bf16)
        return dot_nn(v.activated[part, :], v.down_w[...])

    layer_out = v.hidden_two[...] + in_turn(gathers[1], sums[2], feed_part)
    v.layer_out[...] = layer_out

    count_sum.finish()
    error = layer_out - v.teacher[...].astype(f32)
    square = (tok, tok)
    same = lax.broadcasted_iota(jnp.int32, square, 0) == lax.broadcasted_iota(jnp.int32, square, 1)
    valid = jnp.sum(jnp.where(same, mask, 0.0), axis=1, keepdims=True)
    weighted = valid * error
    v.small[0:5, :] = jnp.zeros((5, 1024), f32)
    v.small[5:6, :] = jnp.broadcast_to(jnp.sum(weighted * error, keepdims=True), (1, 1024))
    v.small[6:8, :] = jnp.broadcast_to(v.count[0:1, 0:1], (2, 1024))
    v.out_grad[...] = (total_tokens / v.count[0:1, 0:1]) * weighted

    leaving.leave("layer_out")
    middle_back(v, send, recv, leaving, block)
    leaving.finish()


class Leaving:

    def __init__(self, v, local):
        self.v, self.local, self.copies = v, local, []

    def leave(self, name):
        copy = pltpu.make_async_copy(
            getattr(self.v, name), getattr(self.v, name + "_any"), self.local.take(1).at[0]
        )
        copy.start()
        self.copies.append(copy)

    def finish(self):
        for copy in self.copies:
            copy.wait()


def take_block(source, chosen, place, target):
    target[...] = source[chosen[place]]


def middle_back(v, send, recv, leaving, block):
    c, w = places_here()
    tok, width = v.tokens.shape
    rows = 4 * tok
    cols = v.output_w.shape[0]
    scale = HEAD_DIM ** (-0.5)
    first, second, third = (
        GatherRows(ref, send.take(3), recv.take(3)) for ref in (v.rows_o, v.rows_two, v.rows_one)
    )
    sum_c, sum_b = (
        SumRows(v.give.at[k], v.take.at[k], send.take(3), recv.take(3)) for k in (3, 4)
    )
    down = CtxSum(send.take(12), recv.take(12), v.down_x, v.down_half, v.down_part, v.down_share)
    up = CtxSum(send.take(12), recv.take(12), v.up_x, v.up_half, v.up_part, v.up_share)
    cross = CtxSum(send.take(12), recv.take(12), v.cross_x, v.cross_half)
    heads = SwapHeads(v.heads_grad, v.heads_out, False, send.take(8), recv.take(8))
    v.rows_o[0] = v.out_grad[...].astype(bf16)

    first.start()

    def feed_back(r):
        part = pl.ds(r * tok, tok)
        act_grad = dot_nt(v.rows_o[r], v.down_w[...])
        v.pre_grad[part, :] = (act_grad * gelu_slope(v.pre_act[part, :])).astype(bf16)
        return dot_nt(v.pre_grad[part, :], v.up_cols[...])

    v.keep[0] = feed_back(0)
    first.near()
    sum_c.give_near(feed_back(1))
    first.relay()
    v.keep[1] = feed_back(2)
    first.far()
    sum_c.give_far(feed_back(3))
    sum_c.pass_on(v.keep[1])
    put_rows(v.down_x, dot_tn(v.activated[...], v.rows_o[...].reshape(rows, width)))
    down.start_y()
    put_shares(v.up_x, dot_tn(v.rows_c[...].reshape(rows, width), v.pre_grad[...]))
    up.start_y()
    normed_grad = sum_c.total(v.keep[0])
    value = v.hidden_two[...]
    inverse = inverse_rms(value)
    two_grad = v.out_grad[...] + norm_pull(value, inverse, v.gains[2:3, :], normed_grad)
    gain_three = jnp.sum(normed_grad * value * inverse, axis=0, keepdims=True)
    v.keep[1] = two_grad
    v.rows_two[0] = two_grad.astype(bf16)

    second.start()

    def cross_back(r):
        part = slice(r * tok, (r + 1) * tok)
        v.crossed_grad[...] = dot_nt(v.rows_two[r], v.cross_out_w[...]).astype(bf16)

        def group(g, carry):
            within = pl.multiple_of(g * GROUP, GROUP)
            at = pl.multiple_of(r * tok + g * GROUP, GROUP)
            near = pl.ds(pl.multiple_of((r * (tok // GROUP) + g) * NK, NK), NK)
            query = stack_all(v.cross_q[pl.ds(at, GROUP), :])
            grad = stack_all(v.crossed_grad[pl.ds(within, GROUP), :])
            keys = v.cross_pair[near, 0:cols]
            shares = cross_shares(query, keys)
            share_grad = dot_nt(grad, v.cross_pair[near, cols:])
            delta = jnp.sum(shares * share_grad, axis=1, keepdims=True)
            score_grad = (shares * (share_grad - delta)).astype(bf16)
            query_grad = join_all(dot_nn(score_grad, keys)) * scale
            v.cross_grad[pl.ds(at, GROUP), :] = query_grad.astype(bf16)
            v.pair_grad[near, 0:cols] = (dot_tn(score_grad, query) * scale).astype(bf16)
            v.pair_grad[near, cols:] = dot_tn(shares.astype(bf16), grad).astype(bf16)
            return carry

        lax.fori_loop(0, tok // GROUP, group, 0, unroll=True)
        return dot_nt(v.cross_grad[part, :], v.query_cols[...])

    v.keep[0] = cross_back(0)
    second.near()
    sum_b.give_near(cross_back(1))
    second.relay()
    v.keep[2] = cross_back(2)
    second.far()
    down.finish_y()
    down.start_z()
    sum_b.give_far(cross_back(3))
    sum_b.pass_on(v.keep[2])
    leaving.leave("pair_grad")
    normed_b = v.rows_b[...].reshape(rows, width)
    put_rows(v.cross_out_x, dot_tn(v.crossed[...], v.rows_two[...].reshape(rows, width)))
    leaving.leave("cross_out_x")
    put_shares(v.cross_x, dot_tn(normed_b, v.cross_grad[...]), 0)
    normed_grad = sum_b.total(v.keep[0])
    value = v.hidden_one[...]
    inverse = inverse_rms(value)
    one_grad = v.keep[1] + norm_pull(value, inverse, v.gains[1:2, :], normed_grad)
    gain_two = jnp.sum(normed_grad * value * inverse, axis=0, keepdims=True)
    v.small[1:2, 0:width] = gain_two
    v.small[2:3, 0:width] = gain_three
    v.one_grad[...] = one_grad
    leaving.leave("one_grad")
    v.rows_one[0] = one_grad.astype(bf16)

    third.start()
    near = v.near[...].reshape(-1, width)
    put_shares(v.cross_x, dot_tn(near, v.pair_grad[...]), cols)

    def head_back(r):
        v.heads_out[r] = dot_nt(v.rows_one[r], v.output_w[...]).astype(bf16)
        heads.start_in(r)

    head_back(0)
    third.near()
    head_back(1)
    third.relay()
    head_back(2)
    third.far()
    head_back(3)
    attended = jnp.concatenate([v.attended[r] for r in range(4)], axis=0)
    put_rows(v.output_x, dot_tn(attended, v.rows_one[...].reshape(rows, width)))
    heads.finish_in()
    up.finish_y()
    up.start_z()
    cross.start_y()
    leaving.leave("output_x")
    leaving.leave("gains")

    per = tok // block
    for place in range(8 * per):
        at = (place % per) * block
        v.heads_stored[place] = v.heads_grad[place // per, at : at + block, :]
    for place in range(8 * per):
        take_block(
            v.heads_stored, v.inverse, place, v.grad_order.at[place * block : (place + 1) * block, :]
        )

    def poll(tile):
        if tile == 1:
            down.finish_z()
            leaving.leave("down_share")

    content_sum, position_sum = attend_back_tiles(
        v.qkv_order,
        v.grad_order,
        v.table,
        v.biases[3:4, :],
        v.biases[4:5, :],
        v.qkv_grad_order,
        v.dkey,
        v.dvalue,
        v.drel,
        poll,
    )
    v.table_grad[...] = v.drel[0 : v.table_grad.shape[0], :] * scale
    leaving.leave("table_grad")
    both = jnp.concatenate([content_sum, position_sum] * 4, axis=1)
    pairs = lax.broadcasted_iota(jnp.int32, both.shape, 1) // 256
    v.small[3:4, :] = jnp.where(pairs == c, both, 0.0)
    v.small[4:5, :] = jnp.where(pairs + 4 == c, both, 0.0)
    leaving.leave("small")
    for place in range(8 * per):
        at = (place % per) * block
        take_block(
            v.qkv_grad_order, v.order, place, v.query_grad.at[place // per, at : at + block, :]
        )
    leaving.leave("query_grad")
    cross.finish_y()
    leaving.leave("cross_half")
    up.finish_z()
    leaving.leave("up_share")


def layer(total_tokens, block, orders, given, collective_id):
    tok, width = given["tokens"].shape
    hidden = given["down_any"].shape[0]
    cols = given["output_any"].shape[0]
    near = given["neighbours"].shape[0]
    seq_len = 8 * tok
    rows = 4 * tok
    padded = -(-(width // 32) // 8) * 8
    any_space = pl.BlockSpec(memory_space=pl.ANY)
    shape = jax.ShapeDtypeStruct
    vmem = pltpu.VMEM
    dma = pltpu.SemaphoreType.DMA
    kept = dict(
        layer_out=shape((tok, width), f32),
        small=shape((8, 1024), f32),
        gains=shape((8, width), f32),
        waves=shape((seq_len, width), bf16),
        normed_a=shape((seq_len, width), bf16),
        pair_cols=shape((width, 2 * cols), bf16),
        one_grad=shape((tok, width), f32),
        pair_grad=shape((4 * near, 2 * cols), bf16),
        query_grad=shape((8, tok, 384), bf16),
        table_grad=shape((seq_len, 128), f32),
        down_share=shape((hidden // 8, width), bf16),
        up_share=shape((4, padded, hidden), bf16),
        cross_half=shape((4, width // 8, 3 * cols), bf16),
        cross_out_x=shape((4, 2, cols // 8, width), bf16),
        output_x=shape((4, 2, cols // 8, width), bf16),
    )
    results = {name + "_any": value for name, value in kept.items()}
    scratch = dict(
        small_all=vmem((8, 1024), f32),
        small_near=vmem((3, 8, 1024), f32),
        qkv=vmem((seq_len // block, block, 384), bf16),
        table=vmem((seq_len + TILE, 128), bf16),
        biases=vmem((8, 128), f32),
        count=vmem((8, 128), f32),
        heads_grad=vmem((8, tok, 128), bf16),
        grad_order=vmem((seq_len, 128), bf16),
        qkv_grad_order=vmem((seq_len // block, block, 384), bf16),
        dkey=vmem((seq_len, 128), f32),
        dvalue=vmem((seq_len, 128), f32),
        drel=vmem((seq_len + TILE, 128), f32),
        count_far=vmem((7, 8, 128), f32),
        tokens_all=vmem((8, tok, width), bf16),
        pair=vmem((width, 512), bf16),
        qkv_order=vmem((seq_len, 384), bf16),
        heads_order=vmem((seq_len // block, block, 128), bf16),
        heads_stored=vmem((seq_len // block, block, 128), bf16),
        heads=vmem((8, tok, 128), bf16),
        attended=vmem((4, tok, cols), bf16),
        near=vmem((4, near, width), bf16),
        query_cols=vmem((width, cols), bf16),
        up_cols=vmem((width, hidden), bf16),
        output_w=vmem((cols, width), bf16),
        cross_out_w=vmem((cols, width), bf16),
        down_w=vmem((hidden, width), bf16),
        cross_pair=vmem((4 * near, 2 * cols), bf16),
        cross_q=vmem((rows, cols), bf16),
        crossed=vmem((rows, cols), bf16),
        crossed_grad=vmem((tok, cols), bf16),
        hidden_one=vmem((tok, width), f32),
        hidden_two=vmem((tok, width), f32),
        out_grad=vmem((tok, width), f32),
        pre_act=vmem((rows, hidden), f32),
        activated=vmem((rows, hidden), bf16),
        rows_b=vmem((4, tok, width), bf16),
        rows_c=vmem((4, tok, width), bf16),
        rows_o=vmem((4, tok, width), bf16),
        rows_two=vmem((4, tok, width), bf16),
        rows_one=vmem((4, tok, width), bf16),
        give=vmem((5, 3, tok, width), bf16),
        take=vmem((5, 3, tok, width), bf16),
        keep=vmem((3, tok, width), f32),
        pre_grad=vmem((rows, hidden), bf16),
        cross_grad=vmem((rows, cols), bf16),
        heads_out=vmem((4, tok, cols), bf16),
        down_x=vmem((4, 2, hidden // 8, width), bf16),
        down_half=vmem((4, hidden // 8, width), bf16),
        down_part=vmem((3, hidden // 8, width), bf16),
        up_x=vmem((4, 2, width // 8, hidden), bf16),
        up_half=vmem((4, width // 8, hidden), bf16),
        up_part=vmem((3, width // 8, hidden), bf16),
        cross_x=vmem((4, 2, width // 8, 3 * cols), bf16),
        send=dma((232,)),
        recv=dma((232,)),
        local=dma((24,)),
    )
    scratch.update({name: vmem(value.shape, value.dtype) for name, value in kept.items()})
    names = [*orders, *given, *results, *scratch]
    specs = [in_smem] * len(orders) + [
        any_space if name.endswith("_any") or name == "neighbours" else in_vmem for name in given
    ]
    got = pl.pallas_call(
        functools.partial(layer_kernel, names, total_tokens, block),
        out_shape=list(results.values()),
        in_specs=specs,
        out_specs=[any_space] * len(results),
        scratch_shapes=list(scratch.values()),
        compiler_params=pltpu.CompilerParams(
            collective_id=collective_id, has_side_effects=True, vmem_limit_bytes=62 * 2**20
        ),
        name="layer",
    )(*orders.values(), *given.values())
    return types.SimpleNamespace(**dict(zip(kept, got, strict=True)))


class Spread:

    def __init__(self, share, out, send, recv):
        self.share, self.out, self.send, self.recv = share, out, send, recv
        self.c, self.w = places_here()

    def columns(self, place):
        width = self.share.shape[2]
        return self.out.at[self.c, :, pl.ds(pl.multiple_of(place * width, 128), width)]

    def copy(self, j, place):
        return remote(
            self.share.at[self.w ^ j],
            self.columns(place),
            self.send.at[j],
            self.recv.at[j],
            self.c,
            self.w ^ j,
        )

    def own(self):
        return pltpu.make_async_copy(
            self.share.at[self.w], self.columns(self.w), self.send.at[0]
        )

    def start(self):
        for j in (2, 3, 1):
            self.copy(j, self.w).start()
        self.own().start()

    def finish(self):
        self.own().wait()
        for j in (1, 2, 3):
            self.copy(j, self.w).wait_send()
            self.copy(j, self.w ^ j).wait_recv()


class Whole:

    def __init__(self, source, target, send, recv):
        self.source, self.target, self.send, self.recv = source, target, send, recv
        self.c, self.w = places_here()

    def put(self, place):
        rows = self.source.shape[0]
        return self.target.at[pl.ds(pl.multiple_of(place * rows, 32), rows), :]

    def copy(self, j, place):
        return remote(
            self.source, self.put(place), self.send.at[j], self.recv.at[j], self.c, self.w ^ j
        )

    def passed(self, place):
        ref = self.put(place)
        return remote(ref, ref, self.send.at[3], self.recv.at[3], self.c, self.w ^ 1)

    def own(self):
        return pltpu.make_async_copy(self.source, self.put(self.w), self.send.at[0])

    def start(self):
        self.copy(2, self.w).start()
        self.copy(1, self.w).start()
        self.own().start()

    def relay(self):
        self.copy(2, self.w).wait_send()
        self.copy(2, self.w ^ 2).wait_recv()
        self.passed(self.w ^ 2).start()

    def finish(self):
        self.own().wait()
        self.copy(1, self.w).wait_send()
        self.copy(1, self.w ^ 1).wait_recv()
        self.passed(self.w ^ 2).wait_send()
        self.passed(self.w ^ 3).wait_recv()


class MaskSum:

    def __init__(self, ref, got, masks, send, recv):
        self.ref, self.got, self.masks, self.send, self.recv = ref, got, masks, send, recv
        self.c, self.w = places_here()

    def copy(self, k):
        ctx, wa = self.masks[k]
        return remote(
            self.ref, self.got.at[k], self.send.at[k], self.recv.at[k], self.c ^ ctx, self.w ^ wa
        )

    def start(self):
        for k in range(len(self.masks)):
            self.copy(k).start()

    def finish(self):
        for k in range(len(self.masks)):
            self.copy(k).wait()
        self.ref[...] = tree_sum([self.ref[...]] + [self.got[k] for k in range(len(self.masks))])


def finish_kernel(names, *refs):
    v = types.SimpleNamespace(**dict(zip(names, refs, strict=True)))
    c, w = places_here()
    send, recv, local = Pool(v.send), Pool(v.recv), Pool(v.local)
    tok, width = v.tokens.shape
    cols = v.output_x.shape[2] * 8
    share = width // 4

    def load(source, target):
        copy = pltpu.make_async_copy(source, target, local.take(1).at[0])
        copy.start()
        return copy

    loads = [load(v.normed_a_any, v.normed_a), load(v.waves_any, v.waves)]
    late = [load(v.pair_cols_any, v.pair_cols), load(v.near_any, v.near_rows)]
    leaving = Leaving(v, local)

    def line(out):
        return LineGather(out, send.take(13), recv.take(13))

    def summed(x, half, part, got):
        return CtxSum(send.take(12), recv.take(12), x, half, part, got)

    down, up, cross, ctx_o, out_o, pair = (
        line(out)
        for out in (v.down_out, v.up_all, v.cross_all, v.cross_o_out, v.output_out, v.pair_all)
    )
    cross_sum = summed(None, v.cross_half, v.cross_part, v.cross_share)
    ctx_o_sum = summed(v.cross_out_x, v.ctx_o_half, v.ctx_o_part, v.ctx_o_share)
    out_o_sum = summed(v.output_x, v.out_o_half, v.out_o_part, v.out_o_share)
    up_spread = Spread(v.up_share, v.up_all, send.take(4), recv.take(4))
    cross_spread = Spread(v.cross_share, v.cross_all, send.take(4), recv.take(4))
    sum_pair = SumRows(v.pair_give, v.pair_take, send.take(3), recv.take(3))
    sum_near = SumRows(v.near_give, v.near_take, send.take(3), recv.take(3))
    weights = [
        Whole(weight, v.full.at[m], send.take(4), recv.take(4))
        for m, weight in enumerate((v.query_any, v.key_any, v.value_any))
    ]
    stages = [
        MaskSum(v.total, got, masks, send.take(3), recv.take(3))
        for got, masks in (
            (v.got_wa, ((0, 1), (0, 2), (0, 3))),
            (v.got_y, ((1, 0),)),
            (v.got_z, ((2, 0), (4, 0), (6, 0))),
        )
    ]
    b_send, b_recv = send.take(24), recv.take(24)

    def block_copy(j, m, place):
        return remote(
            v.query_grad.at[c ^ j, :, 128 * m : 128 * (m + 1)],
            v.mine.at[m, :, pl.ds(pl.multiple_of(place * 128, 128), 128)],
            b_send.at[3 * j + m],
            b_recv.at[3 * j + m],
            c ^ j,
            w,
        )

    own_blocks = [
        pltpu.make_async_copy(
            v.query_grad.at[c, :, 128 * m : 128 * (m + 1)],
            v.mine.at[m, :, pl.ds(pl.multiple_of(c * 128, 128), 128)],
            b_recv.at[m],
        )
        for m in range(3)
    ]
    v.down_out[c] = v.down_share[...]
    meet_lines()
    down.start()
    up_spread.start()
    cross_sum.start_z((2,))
    ctx_o_sum.start_y()
    out_o_sum.start_y()
    for copy in own_blocks:
        copy.start()

    query_grad = v.query_grad[...].reshape(-1, v.query_grad.shape[2])
    high = v.table_grad[...].astype(bf16)
    low = (v.table_grad[...] - high.astype(f32)).astype(bf16)
    for copy in loads:
        copy.wait()
    mixed = dot_tn(v.normed_a[...], query_grad)
    up_spread.finish()
    up.start()
    down.step(0)
    cross_sum.start_z((3, 1))
    turned = dot_tn(v.waves[...], high) + dot_tn(v.waves[...], low)
    for place in range(4):
        at = place * share
        v.sums[place] = jnp.concatenate([mixed[at : at + share], turned[at : at + share]], axis=1)
    sum_pair.give_far(v.sums[w ^ 3])
    sum_pair.give_near(v.sums[w ^ 1])
    down.step(1)
    up.step(0)
    ctx_o_sum.finish_y()
    ctx_o_sum.start_z()
    out_o_sum.finish_y()
    out_o_sum.start_z()
    sum_pair.pass_on(v.sums[w ^ 2])
    for copy in late:
        copy.wait()
    near_count = v.near_grad.shape[0]

    def near_part(r):
        return dot_nt(v.near_rows[r * near_count : (r + 1) * near_count, :], v.pair_cols[...])

    sum_near.give_far(near_part(3))
    sum_near.give_near(near_part(1))
    v.pair_all[c] = sum_pair.total(v.sums[w]).astype(bf16)
    pair.start()
    up.step(1)
    down.step(2)
    cross_sum.finish_z()
    cross_spread.start()
    sum_near.pass_on(near_part(2))
    v.near_grad[...] = near_part(0)
    cross_spread.finish()
    cross.start()
    for j in (4, 6, 5, 7, 2, 3, 1):
        for m in range(3):
            block_copy(j, m, c).start()
    for weight in weights:
        weight.start()
    up.step(2)
    pair.step(0)
    ctx_o_sum.finish_z()
    v.cross_o_out[c] = v.ctx_o_share[...]
    ctx_o.start()
    out_o_sum.finish_z()
    v.output_out[c] = v.out_o_share[...]
    out_o.start()
    cross.step(0)
    pair.step(1)
    ctx_o.step(0)
    out_o.step(0)
    cross.step(1)
    ctx_o.step(1)
    out_o.step(1)

    for j in range(1, 8):
        for m in range(3):
            block_copy(j, m, c ^ j).wait_recv()
    for copy in own_blocks:
        copy.wait()
    pair.step(2)
    for weight in weights:
        weight.relay()
    for weight in weights:
        weight.finish()
    normed_grad = dot_nt(v.mine[0], v.full[0])
    normed_grad = normed_grad + dot_nt(v.mine[1], v.full[1])
    normed_grad = normed_grad + dot_nt(v.mine[2], v.full[2])
    hidden = v.tokens[...].astype(f32)
    inverse = inverse_rms(hidden)
    v.tokens_grad[...] = v.one_grad[...] + norm_pull(hidden, inverse, v.gains[0:1, :], normed_grad)
    leaving.leave("tokens_grad")
    v.total[...] = v.small[...]
    v.total[0:1, 0:width] = jnp.sum(normed_grad * hidden * inverse, axis=0, keepdims=True)
    stages[0].start()
    ctx_o.step(2)
    out_o.step(2)
    cross.step(2)
    stages[0].finish()
    stages[1].start()
    v.near_grad[...] = sum_near.total(v.near_grad[...])
    leaving.leave("near_grad")
    stages[1].finish()
    stages[2].start()
    down.finish()
    leaving.leave("down_out")
    up.finish()
    used = share // 8
    for part in range(8):
        v.up_out[part * used : (part + 1) * used, :] = v.up_all[part, 0:used, :].astype(f32)
    leaving.leave("up_out")
    pair.finish()
    pair_outs = (v.query_out, v.key_out, v.value_out, v.relative_out)
    for part in range(8):
        for m, out in enumerate(pair_outs):
            out[:, 128 * part : 128 * (part + 1)] = v.pair_all[part, :, 128 * m : 128 * (m + 1)]
    for name in ("query_out", "key_out", "value_out", "relative_out"):
        leaving.leave(name)
    ctx_o.finish()
    leaving.leave("cross_o_out")
    out_o.finish()
    leaving.leave("output_out")
    cross.finish()
    for m, out in enumerate((v.cross_query_out, v.cross_key_out, v.cross_value_out)):
        for part in range(8):
            for place in range(4):
                at = (place * 3 + m) * cols
                out[part * used : (part + 1) * used, place * cols : (place + 1) * cols] = v.cross_all[
                    part, 0:used, at : at + cols
                ].astype(f32)
    for name in ("cross_query_out", "cross_key_out", "cross_value_out"):
        leaving.leave(name)
    stages[2].finish()
    devices = 32.0
    loss = v.total[5:6, :] * devices / (2.0 * width * v.total[6:7, :])
    v.total[7:8, :] = loss
    leaving.leave("total")
    for j in range(1, 8):
        for m in range(3):
            block_copy(j, m, c).wait_send()
    leaving.finish()


def finish(given, collective_id):
    tok, width = given["tokens"].shape
    near = given["near_any"].shape[0]
    padded = given["up_share"].shape[1]
    hidden = given["up_share"].shape[2]
    cols = given["output_x"].shape[2] * 8
    share = width // 4
    any_space = pl.BlockSpec(memory_space=pl.ANY)
    shape = jax.ShapeDtypeStruct
    vmem = pltpu.VMEM
    dma = pltpu.SemaphoreType.DMA
    part = (cols // 8, width)
    kept = dict(
        tokens_grad=shape((tok, width), f32),
        near_grad=shape((near // 4, width), f32),
        total=shape(given["small"].shape, f32),
        down_out=shape((8,) + given["down_share"].shape, bf16),
        up_out=shape((share, 4 * hidden), f32),
        cross_query_out=shape((share, 4 * cols), f32),
        cross_key_out=shape((share, 4 * cols), f32),
        cross_value_out=shape((share, 4 * cols), f32),
        cross_o_out=shape((8,) + part, bf16),
        output_out=shape((8,) + part, bf16),
        query_out=shape((share, 1024), bf16),
        key_out=shape((share, 1024), bf16),
        value_out=shape((share, 1024), bf16),
        relative_out=shape((share, 1024), bf16),
    )
    results = {name + "_any": value for name, value in kept.items()}
    scratch = dict(
        normed_a=vmem(given["normed_a_any"].shape, bf16),
        waves=vmem(given["waves_any"].shape, bf16),
        pair_cols=vmem(given["pair_cols_any"].shape, bf16),
        near_rows=vmem(given["near_any"].shape, bf16),
        full=vmem((3, width, 1024), bf16),
        mine=vmem((3, tok, 1024), bf16),
        sums=vmem((4, share, 512), f32),
        up_all=vmem((8, padded, 4 * hidden), bf16),
        cross_all=vmem((8, padded, 12 * cols), bf16),
        pair_all=vmem((8, share, 512), bf16),
        cross_part=vmem((3, width // 8, 3 * cols), bf16),
        cross_share=vmem((4, padded, 3 * cols), bf16),
        ctx_o_half=vmem((4,) + part, bf16),
        out_o_half=vmem((4,) + part, bf16),
        ctx_o_part=vmem((3,) + part, bf16),
        ctx_o_share=vmem(part, bf16),
        out_o_part=vmem((3,) + part, bf16),
        out_o_share=vmem(part, bf16),
        pair_give=vmem((3, share, 512), bf16),
        pair_take=vmem((3, share, 512), bf16),
        near_give=vmem((3, near // 4, width), bf16),
        near_take=vmem((3, near // 4, width), bf16),
        got_wa=vmem((3,) + given["small"].shape, f32),
        got_y=vmem((1,) + given["small"].shape, f32),
        got_z=vmem((3,) + given["small"].shape, f32),
        send=dma((184,)),
        recv=dma((184,)),
        local=dma((24,)),
    )
    scratch.update({name: vmem(value.shape, value.dtype) for name, value in kept.items()})
    names = [*given, *results, *scratch]
    got = pl.pallas_call(
        functools.partial(finish_kernel, names),
        out_shape=list(results.values()),
        in_specs=[any_space if name.endswith("_any") else in_vmem for name in given],
        out_specs=[any_space] * len(results),
        scratch_shapes=list(scratch.values()),
        compiler_params=pltpu.CompilerParams(
            collective_id=collective_id, has_side_effects=True, vmem_limit_bytes=62 * 2**20
        ),
        name="finish",
    )(*given.values())
    return types.SimpleNamespace(**dict(zip(kept, got, strict=True)))


def skew(wide, count):
    lead = wide.shape[:-2]
    rows, span = wide.shape[-2:]
    edge = [(0, 0)] * len(lead)
    padded = jnp.pad(wide, edge + [(0, 0), (0, 1)])
    flat = padded.reshape(lead + (rows * (span + 1),))
    flat = lax.slice_in_dim(flat, rows - 1, rows - 1 + rows * span, axis=len(lead))
    return flat.reshape(lead + (rows, span))[..., :count]


def unskew(grad, span):
    lead = grad.shape[:-2]
    rows, count = grad.shape[-2:]
    edge = [(0, 0)] * len(lead)
    wide = jnp.pad(grad, edge + [(0, 0), (0, span - count)])
    flat = jnp.pad(wide.reshape(lead + (rows * span,)), edge + [(rows - 1, 1)])
    return flat.reshape(lead + (rows, span + 1))[..., :span]


def tile_scores(content_rows, position_rows, key_rows, relative, row_start, key_start):
    rows = content_rows.shape[0]
    count = key_rows.shape[0]
    scale = content_rows.shape[-1] ** (-0.5)
    content = jnp.einsum("qhe,khe->hqk", content_rows, key_rows, preferred_element_type=f32)
    wide = jnp.einsum("qhe,whe->hqw", position_rows, relative, preferred_element_type=f32)
    scores = (content + skew(wide, count)) * scale
    causal = (row_start + jnp.arange(rows))[:, None] >= (key_start + jnp.arange(count))[None, :]
    return (scores, causal[None])


def tile_forward(
    content_rows, position_rows, row_start, relative, key_rows, value_rows, key_start, state
):
    top, total, accum = state
    scores, causal = tile_scores(
        content_rows, position_rows, key_rows, relative, row_start, key_start
    )
    scores = jnp.where(causal, scores, neg_big)
    new_top = jnp.maximum(top, jnp.max(scores, axis=-1))
    raised = jnp.where(causal, jnp.exp(scores - new_top[..., None]), 0.0)
    fade = jnp.exp(top - new_top)
    total = total * fade + jnp.sum(raised, axis=-1)
    accum = accum * fade[..., None] + jnp.einsum(
        "hqk,khe->hqe", raised.astype(bf16), value_rows, preferred_element_type=f32
    )
    return (new_top, total, accum)


def tile_backward(
    content_rows,
    position_rows,
    row_start,
    relative,
    key_rows,
    value_rows,
    grad_rows,
    log_rows,
    delta_rows,
    key_start,
):
    scores, causal = tile_scores(
        content_rows, position_rows, key_rows, relative, row_start, key_start
    )
    scale = content_rows.shape[-1] ** (-0.5)
    shares = jnp.where(causal, jnp.exp(scores - log_rows[..., None]), 0.0)
    share_grad = jnp.einsum("qhe,khe->hqk", grad_rows, value_rows, preferred_element_type=f32)
    score_grad = (shares * (share_grad - delta_rows[..., None])).astype(bf16)
    content_grad = jnp.einsum("hqk,khe->qhe", score_grad, key_rows, preferred_element_type=f32)
    wide_grad = unskew(score_grad, relative.shape[0])
    position_grad = jnp.einsum("hqw,whe->qhe", wide_grad, relative, preferred_element_type=f32)
    table_part = jnp.einsum("hqw,qhe->whe", wide_grad, position_rows, preferred_element_type=f32)
    key_grad = jnp.einsum("hqk,qhe->khe", score_grad, content_rows, preferred_element_type=f32)
    value_grad = jnp.einsum(
        "hqk,qhe->khe", shares.astype(bf16), grad_rows, preferred_element_type=f32
    )
    return (
        content_grad * scale,
        position_grad * scale,
        table_part * scale,
        key_grad * scale,
        value_grad,
    )


def nest_tiles(tile_fn):
    inner = jax.vmap(tile_fn, in_axes=(0, 0, 0, 0, None, None, 0))
    return jax.vmap(inner, in_axes=(0, 0, None, None, 0, 0, 0))


def to_global(stored, inverse, block):
    seqs, seq_len, width = stored.shape
    blocks = stored.reshape(seqs, seq_len // block, block * width)
    chosen = (inverse[:, None] == jnp.arange(seq_len // block)[None, :]).astype(bf16)
    moved = jnp.einsum("gs,nsx->ngx", chosen, blocks, preferred_element_type=f32)
    return moved.astype(bf16).reshape(stored.shape)


class SplitQueries:

    def __init__(self, query, keys, values, biases, relative, block_order, inverse, block):
        self.seqs, self.tok_dev, self.width = keys.shape
        self.heads = self.width // HEAD_DIM
        self.block = block
        self.block_order = block_order
        ctx_count = lax.axis_size("ctx")
        self.seq_len = self.tok_dev * ctx_count
        self.key_len = min(512, self.seq_len)
        pad = jnp.zeros((self.key_len + block, self.width), bf16)
        table = jnp.concatenate([relative, pad], axis=0)
        self.table = table.reshape(-1, self.heads, HEAD_DIM)
        lead = (self.seqs, 2, block, self.heads, HEAD_DIM)
        self.content = (query + biases[0]).astype(bf16).reshape(lead)
        self.position = (query + biases[1]).astype(bf16).reshape(lead)
        gathered = [lax.all_gather(part, "ctx", axis=1, tiled=True) for part in (keys, values)]
        shape = (self.seqs, self.seq_len, self.heads, HEAD_DIM)
        self.keys, self.values = [to_global(part, inverse, block).reshape(shape) for part in gathered]
        self.starts = lax.dynamic_slice_in_dim(block_order, 2 * lax.axis_index("ctx"), 2, 0) * block

    def rows(self, index):
        start = index * self.key_len
        keys = lax.dynamic_slice_in_dim(self.keys, start, self.key_len, 1)
        values = lax.dynamic_slice_in_dim(self.values, start, self.key_len, 1)
        span = self.block + self.key_len
        offsets = [self.seq_len - self.block - self.starts[slot] + start for slot in range(2)]
        relative = [lax.dynamic_slice_in_dim(self.table, offset, span, 0) for offset in offsets]
        return start, keys, values, jnp.stack(relative), offsets

    def to_stored(self, part):
        count = self.seq_len // self.block
        blocks = part.reshape(self.seqs, count, self.block * self.width)
        chosen = (self.block_order[:, None] == jnp.arange(count)[None, :]).astype(f32)
        moved = jnp.einsum("sg,ngx->nsx", chosen, blocks, precision=highest)
        return moved.reshape(self.seqs, self.seq_len, self.width)

    def forward(self):
        def step(state, index):
            start, keys, values, relative, _ = self.rows(index)

            def tile(content, position, row_start, table, keys_seq, values_seq, tile_state):
                return tile_forward(
                    content, position, row_start, table, keys_seq, values_seq, start, tile_state
                )

            return nest_tiles(tile)(
                self.content, self.position, self.starts, relative, keys, values, state
            ), None

        shape = (self.seqs, 2, self.heads, self.block)
        state = (
            jnp.full(shape, neg_big, f32),
            jnp.zeros(shape, f32),
            jnp.zeros(shape + (HEAD_DIM,), f32),
        )
        (top, total, accum), _ = lax.scan(step, state, jnp.arange(self.seq_len // self.key_len))
        self.log_total = top + jnp.log(total)
        self.out = accum / total[..., None]
        moved = jnp.transpose(self.out, (0, 1, 3, 2, 4))
        return moved.reshape(self.seqs * self.tok_dev, self.width).astype(bf16)

    def backward(self, grad):
        block, seq_len, key_len = self.block, self.seq_len, self.key_len
        lead = (self.seqs, 2, block, self.heads, HEAD_DIM)
        grad = grad.reshape(lead)
        delta = jnp.einsum("sbqhe,sbhqe->sbhq", grad.astype(f32), self.out)
        def step(carry, index):
            start, keys, values, relative, offsets = self.rows(index)

            def tile(content, position, row_start, table, keys_seq, values_seq, extra):
                return tile_backward(
                    content, position, row_start, table, keys_seq, values_seq, *extra, start
                )

            extra = (grad, self.log_total, delta)
            parts = nest_tiles(tile)(
                self.content, self.position, self.starts, relative, keys, values, extra
            )
            table = carry[2]
            table_sum = jnp.sum(parts[2], axis=0)
            for slot in range(2):
                offset = offsets[slot]
                current = lax.dynamic_slice_in_dim(table, offset, block + key_len, 0)
                table = lax.dynamic_update_slice_in_dim(table, current + table_sum[slot], offset, 0)
            sums = []
            for total, part in zip(carry[3:], parts[3:]):
                current = lax.dynamic_slice_in_dim(total, start, key_len, 1)
                part = current + jnp.sum(part, axis=1)
                sums.append(lax.dynamic_update_slice_in_dim(total, part, start, 1))
            key_acc, value_acc = sums
            return (carry[0] + parts[0], carry[1] + parts[1], table, key_acc, value_acc), None

        zero_tiles = jnp.zeros(lead, f32)
        zero_keys = jnp.zeros((self.seqs, seq_len, self.heads, HEAD_DIM), f32)
        carry = (zero_tiles, zero_tiles, jnp.zeros(self.table.shape, f32), zero_keys, zero_keys)
        carry, _ = lax.scan(step, carry, jnp.arange(seq_len // key_len))
        owned = [
            lax.psum_scatter(
                self.to_stored(part), "ctx", scatter_dimension=1, tiled=True
            )
            for part in carry[3:]
        ]
        flat = (self.seqs * self.tok_dev, self.width)
        query_grad = (carry[0] + carry[1]).reshape(flat).astype(bf16)
        key_grad, value_grad = [part.reshape(flat).astype(bf16) for part in owned]
        bias_grads = jnp.stack(
            [jnp.sum(part, axis=(0, 1, 2)).reshape(self.width) for part in carry[:2]]
        )
        table_grad = carry[2].reshape(-1, self.width)[:seq_len]
        return query_grad, key_grad, value_grad, bias_grads, table_grad


def local_general(
    tokens,
    neighbours,
    teacher,
    valid_mask,
    block_order,
    query_weight,
    key_weight,
    value_weight,
    output_weight,
    relative_weight,
    content_bias,
    position_bias,
    cross_query_weight,
    cross_key_weight,
    cross_value_weight,
    cross_output_weight,
    up_weight,
    down_weight,
    attention_gain,
    cross_gain,
    feedforward_gain,
):
    places = lax.axis_size("wa")
    ctx_count = lax.axis_size("ctx")
    place = lax.axis_index("wa")
    here = lax.axis_index("ctx")
    _, tok_dev, width = tokens.shape
    seq_len = tok_dev * ctx_count
    block = tok_dev // 2
    cols = HEADS * HEAD_DIM // places
    rows = places * tok_dev

    token_parts = gather_parts(tokens[0])
    query_cols, key_cols, value_cols = [
        take_columns(weight) for weight in (query_weight, key_weight, value_weight)
    ]
    relative_cols = take_columns(relative_weight)
    gains = lax.all_gather(
        jnp.stack([attention_gain, cross_gain, feedforward_gain]), "wa", axis=1, tiled=True
    ).astype(f32)
    gain_one, gain_two, gain_three = gains[0:1], gains[1:2], gains[2:3]
    cross_query_cols, cross_key_cols, cross_value_cols = [
        take_columns(weight) for weight in (cross_query_weight, cross_key_weight, cross_value_weight)
    ]
    cross_pair_cols = jnp.concatenate([cross_key_cols, cross_value_cols], axis=1)
    near_rows = jnp.concatenate(gather_parts(neighbours.reshape(-1, width)), axis=0)
    up_cols = take_columns(up_weight)
    valid = valid_mask.astype(f32).reshape(tok_dev, 1)
    count = jnp.sum(valid).reshape(1, 1)
    count = all_summed(all_summed(count, "wa"), "ctx")

    slots = jnp.arange(2 * ctx_count)
    inverse = jnp.sum(jnp.where(block_order[None, :] == slots[:, None], slots[None, :], 0), axis=1)
    inverse = inverse.astype(jnp.int32)
    distance = (seq_len - 1 - jnp.arange(seq_len)).astype(f32)
    waves = sinusoid(distance, width).astype(bf16)

    hidden_all = jnp.concatenate(token_parts, axis=0).astype(f32)
    scale_all = inverse_rms(hidden_all)
    normed_a = (hidden_all * scale_all * gain_one).astype(bf16)
    biases = jnp.stack([content_bias, position_bias]).astype(f32)
    mixed_cols = jnp.concatenate([query_cols, key_cols, value_cols], axis=1)
    qkv = dot_nn(normed_a, mixed_cols).reshape(places, tok_dev, 3 * cols)
    relative = dot_nn(waves, relative_cols).astype(bf16)
    general = SplitQueries(
        qkv[..., :cols],
        qkv[..., cols : 2 * cols].astype(bf16),
        qkv[..., 2 * cols :].astype(bf16),
        biases,
        relative,
        block_order,
        inverse,
        block,
    )
    attended = general.forward()

    def to_owner(product):
        return scatter_parts([product[r * tok_dev : (r + 1) * tok_dev] for r in range(places)])

    def from_all(value):
        return jnp.concatenate(gather_parts(value), axis=0)

    hidden_in = tokens[0].astype(f32)
    hidden_one = hidden_in + to_owner(dot_nn(attended, output_weight))

    scale_two = inverse_rms(hidden_one)
    normed_b = from_all((hidden_one * scale_two * gain_two).astype(bf16))
    cross_q = dot_nn(normed_b, cross_query_cols).astype(bf16)
    cross_pair = dot_nn(near_rows, cross_pair_cols).astype(bf16)
    crossed = cross_forward(cross_q, cross_pair)
    hidden_two = hidden_one + to_owner(dot_nn(crossed, cross_output_weight))

    scale_three = inverse_rms(hidden_two)
    normed_c = from_all((hidden_two * scale_three * gain_three).astype(bf16))
    pre_act = dot_nn(normed_c, up_cols)
    activated = gelu_tanh(pre_act).astype(bf16)
    layer_out = hidden_two + to_owner(dot_nn(activated, down_weight))

    error = layer_out - teacher[0].astype(f32)
    error_sum = jnp.sum(valid * error * error).reshape(1, 1)
    error_sum = all_summed(all_summed(error_sum, "wa"), "ctx")
    loss = (error_sum / (2.0 * count * width)).reshape(())
    out_grad = (places * seq_len) / count * valid * error

    out_low = from_all(out_grad.astype(bf16))
    act_grad = dot_nt(out_low, down_weight)
    _, gelu_pull = jax.vjp(gelu_tanh, pre_act)
    pre_grad = gelu_pull(act_grad)[0].astype(bf16)
    down_grad = dot_tn(activated, out_low).astype(bf16)
    up_grad = dot_tn(normed_c, pre_grad).astype(bf16)
    normed_c_grad = to_owner(dot_nt(pre_grad, up_cols))
    two_grad = out_grad + norm_pull(hidden_two, scale_three, gain_three, normed_c_grad)
    gain_three_grad = jnp.sum(normed_c_grad * hidden_two * scale_three, axis=0, keepdims=True)
    down_out = sum_row_grads(down_grad)
    up_out = sum_column_grads(up_grad[None])[0]

    two_low = from_all(two_grad.astype(bf16))
    crossed_grad = dot_nt(two_low, cross_output_weight).astype(bf16)
    cross_q_grad, cross_pair_grad = cross_backward(cross_q, cross_pair, crossed_grad)
    normed_b_grad = to_owner(dot_nt(cross_q_grad, cross_query_cols))
    one_grad = two_grad + norm_pull(hidden_one, scale_two, gain_two, normed_b_grad)
    gain_two_grad = jnp.sum(normed_b_grad * hidden_one * scale_two, axis=0, keepdims=True)
    cross_output_grad = dot_tn(crossed, two_low).astype(bf16)
    cross_query_grad = dot_tn(normed_b, cross_q_grad).astype(bf16)
    cross_key_grad = dot_tn(near_rows, cross_pair_grad[:, :cols]).astype(bf16)
    cross_value_grad = dot_tn(near_rows, cross_pair_grad[:, cols:]).astype(bf16)
    cross_output_out = sum_row_grads(cross_output_grad)
    cross_out = sum_column_grads(jnp.stack([cross_key_grad, cross_value_grad]))
    cross_query_out = sum_column_grads(cross_query_grad[None])[0]
    near_grad = dot_nt(cross_pair_grad, cross_pair_cols)
    near_count = near_rows.shape[0] // places
    near_grad = scatter_parts(
        [near_grad[r * near_count : (r + 1) * near_count] for r in range(places)]
    )
    neighbours_grad = near_grad.reshape(neighbours.shape)

    one_low = from_all(one_grad.astype(bf16))
    attended_grad = dot_nt(one_low, output_weight).astype(bf16)
    output_grad = dot_tn(attended, one_low).astype(bf16)
    output_out = sum_row_grads(output_grad)
    query_grad, key_grad, value_grad, bias_grads, table_grad = general.backward(attended_grad)
    qkv_grad = jnp.concatenate([query_grad, key_grad, value_grad], axis=1)
    table_high = table_grad.astype(bf16)
    table_low = (table_grad - table_high.astype(f32)).astype(bf16)
    relative_grad = (dot_tn(waves, table_high) + dot_tn(waves, table_low)).astype(bf16)
    mixed_grad = dot_tn(normed_a, qkv_grad).astype(bf16)
    whole = [mixed_grad[:, m * cols : (m + 1) * cols] for m in range(3)]
    attention_out = sum_column_grads(jnp.stack(whole + [relative_grad]))
    normed_a_part = dot_nt(qkv_grad, mixed_cols)
    gain_one_part = jnp.sum(normed_a_part * hidden_all * scale_all, axis=0, keepdims=True)
    normed_a_grad = to_owner(normed_a_part)
    tokens_grad = one_grad + norm_pull(hidden_in, scale_all[:tok_dev], gain_one, normed_a_grad)

    gain_grads = jnp.concatenate([gain_one_part, gain_two_grad, gain_three_grad], axis=0)
    gain_grads = all_summed(gain_grads, "wa")
    share = width // places
    gain_grads = lax.dynamic_slice_in_dim(gain_grads, place * share, share, 1)
    small = jnp.concatenate([gain_grads.reshape(1, -1), bias_grads.reshape(1, -1)], axis=1)
    small = all_summed(small, "ctx")[0]
    gain_out = small[: 3 * share].reshape(3, share)
    bias_out = small[3 * share :].reshape(2, cols)

    return (
        layer_out[None],
        loss,
        tokens_grad[None],
        neighbours_grad,
        attention_out[0],
        attention_out[1],
        attention_out[2],
        output_out,
        attention_out[3],
        bias_out[0],
        bias_out[1],
        cross_query_out,
        cross_out[0],
        cross_out[1],
        cross_output_out,
        up_out,
        down_out,
        gain_out[0],
        gain_out[1],
        gain_out[2],
    )


def local_by_heads(
    tokens,
    neighbours,
    teacher,
    valid_mask,
    block_order,
    query_weight,
    key_weight,
    value_weight,
    output_weight,
    relative_weight,
    content_bias,
    position_bias,
    cross_query_weight,
    cross_key_weight,
    cross_value_weight,
    cross_output_weight,
    up_weight,
    down_weight,
    attention_gain,
    cross_gain,
    feedforward_gain,
):
    places = 4
    ctx_count = 8
    place = lax.axis_index("wa")
    here = lax.axis_index("ctx")
    _, tok_dev, width = tokens.shape
    seq_len = tok_dev * ctx_count
    block = tok_dev // 2
    attn = HEADS * HEAD_DIM
    cols = attn // places
    share = width // places

    slots = jnp.arange(2 * ctx_count)
    inverse = jnp.sum(jnp.where(block_order[None, :] == slots[:, None], slots[None, :], 0), axis=1)
    inverse = inverse.astype(jnp.int32)
    half = width // 2
    freq = jnp.exp(-jnp.log(10000.0) * jnp.arange(half, dtype=f32) * 2.0 / width)
    coarse = (64.0 * jnp.arange(seq_len // 64, dtype=f32)[::-1])[:, None] * freq
    fine = jnp.arange(64, dtype=f32)[::-1][:, None] * freq
    sin_a, cos_a, sin_b, cos_b = jnp.sin(coarse), jnp.cos(coarse), jnp.sin(fine), jnp.cos(fine)
    left = jnp.concatenate([sin_a, cos_a, cos_b, sin_b], axis=0)
    right = jnp.concatenate([cos_a, -sin_a, cos_b, sin_b], axis=0)
    tables = jnp.concatenate([left, right], axis=1)

    done = layer(
        float(places * seq_len),
        block,
        dict(inverse=inverse, order=block_order),
        dict(
            tokens=tokens[0],
            teacher=teacher[0],
            mask=valid_mask,
            gain_row=jnp.concatenate(
                [attention_gain, cross_gain, feedforward_gain, content_bias, position_bias]
            )[None],
            tables=tables,
            neighbours=neighbours.reshape(-1, width),
            query_any=query_weight,
            key_any=key_weight,
            value_any=value_weight,
            relative_any=relative_weight,
            cross_query_any=cross_query_weight,
            cross_key_any=cross_key_weight,
            cross_value_any=cross_value_weight,
            up_any=up_weight,
            output_any=output_weight,
            cross_out_any=cross_output_weight,
            down_any=down_weight,
        ),
        1,
    )
    last = finish(
        dict(
            query_grad=done.query_grad,
            table_grad=done.table_grad,
            small=done.small,
            down_share=done.down_share,
            up_share=done.up_share,
            cross_half=done.cross_half,
            cross_out_x=done.cross_out_x,
            output_x=done.output_x,
            one_grad=done.one_grad,
            tokens=tokens[0],
            gains=done.gains,
            normed_a_any=done.normed_a,
            waves_any=done.waves,
            near_any=done.pair_grad,
            pair_cols_any=done.pair_cols,
            query_any=query_weight,
            key_any=key_weight,
            value_any=value_weight,
        ),
        2,
    )
    total = last.total
    gain_out = lax.dynamic_slice_in_dim(total[0:3], place * share, share, 1)
    bias_out = lax.dynamic_slice_in_dim(total[3:5].reshape(ctx_count, 2, 128), place * 2, 2, 0)
    bias_out = bias_out.transpose(1, 0, 2).reshape(2, cols)
    loss = total[7, 0]
    down_out = last.down_out.reshape(down_weight.shape).astype(f32)
    cross_output_out = last.cross_o_out.reshape(cols, width).astype(f32)
    output_out = last.output_out.reshape(cols, width).astype(f32)

    return (
        done.layer_out[None],
        loss,
        last.tokens_grad[None],
        last.near_grad.reshape(neighbours.shape),
        last.query_out.astype(f32),
        last.key_out.astype(f32),
        last.value_out.astype(f32),
        output_out,
        last.relative_out.astype(f32),
        bias_out[0],
        bias_out[1],
        last.cross_query_out,
        last.cross_key_out,
        last.cross_value_out,
        cross_output_out,
        last.up_out,
        down_out,
        gain_out[0],
        gain_out[1],
        gain_out[2],
    )


def solution(mesh):
    row = P("wa", None)
    flat = P("wa")
    in_specs = (
        P("wa", "ctx", None),
        P("wa", "ctx", None, None),
        P("wa", "ctx", None),
        P("wa", "ctx"),
        P(),
        row,
        row,
        row,
        row,
        row,
        flat,
        flat,
        row,
        row,
        row,
        row,
        row,
        row,
        flat,
        flat,
        flat,
    )
    out_specs = (
        P("wa", "ctx", None),
        P(),
        P("wa", "ctx", None),
        P("wa", "ctx", None, None),
        row,
        row,
        row,
        row,
        row,
        flat,
        flat,
        row,
        row,
        row,
        row,
        row,
        row,
        flat,
        flat,
        flat,
    )
    by_heads = mesh.shape["ctx"] == 8 and mesh.shape["wa"] == 4
    local = local_by_heads if by_heads else local_general
    return jax.shard_map(local, mesh=mesh, in_specs=in_specs, out_specs=out_specs, check_vma=False)
```

```python
import functools
import types

import jax
import jax.numpy as jnp
from jax import lax
from jax.experimental import pallas as pl
from jax.experimental.pallas import tpu as pltpu
from jax.sharding import PartitionSpec as P

HEADS = 16
HEAD_DIM = 64
GROUP = 64
NK = 256
TILE = 128

eps_norm = 1e-06
neg_big = -1e30
highest = lax.Precision.HIGHEST
f32 = jnp.float32
bf16 = jnp.bfloat16


def inverse_rms(hidden):
    return lax.rsqrt(jnp.mean(hidden * hidden, axis=-1, keepdims=True) + eps_norm)


def norm_pull(hidden, scale, gain, grad):
    scaled = grad * gain
    mean = jnp.mean(hidden * scaled, axis=-1, keepdims=True)
    return scale * scaled - hidden * (scale * scale * scale) * mean


def gelu_tanh(value):
    return jax.nn.gelu(value, approximate=True)


def sinusoid(distance, width):
    half = width // 2
    freq = jnp.exp(-jnp.log(10000.0) * jnp.arange(half, dtype=f32) * 2.0 / width)
    angle = distance[:, None] * freq[None, :]
    return jnp.concatenate([jnp.sin(angle), jnp.cos(angle)], axis=1)


def dot_nn(a, b):
    return lax.dot_general(a, b, (((1,), (0,)), ((), ())), preferred_element_type=f32)


def dot_nt(a, b):
    return lax.dot_general(a, b, (((1,), (1,)), ((), ())), preferred_element_type=f32)


def dot_tn(a, b):
    return lax.dot_general(a, b, (((0,), (0,)), ((), ())), preferred_element_type=f32)


def swap(value, axis, bit):
    pairs = [(i, i ^ bit) for i in range(lax.axis_size(axis))]
    return lax.ppermute(value, axis, pairs)


def bits_of(axis):
    bits, bit = [], 1
    while bit < lax.axis_size(axis):
        bits.append(bit)
        bit *= 2
    return bits


def my_bit(axis, bit):
    return (lax.axis_index(axis) // bit) % 2


def ordered(bit, own, other, dim):
    return jnp.where(
        bit == 0,
        jnp.concatenate([own, other], axis=dim),
        jnp.concatenate([other, own], axis=dim),
    )


def split(value, bit, dim):
    half = value.shape[dim] // 2
    keep = lax.dynamic_slice_in_dim(value, bit * half, half, dim)
    send = lax.dynamic_slice_in_dim(value, (1 - bit) * half, half, dim)
    return keep, send


def gather_parts(value):
    parts = {0: value}
    for bit in reversed(bits_of("wa")):
        parts.update({r | bit: swap(part, "wa", bit) for r, part in list(parts.items())})
    return [parts[r] for r in sorted(parts)]


def scatter_parts(parts):
    parts = dict(enumerate(parts))
    for bit in bits_of("wa"):
        kept = {}
        for r, part in parts.items():
            if not r & bit:
                got = swap(parts[r | bit].astype(bf16), "wa", bit)
                kept[r] = part + got.astype(f32)
        parts = kept
    return parts[0]


def take_columns(weight):
    value = weight[None]
    for bit in reversed(bits_of("wa")):
        mine = my_bit("wa", bit)
        keep, send = split(value, mine, 2)
        value = ordered(mine, keep[:, None], swap(send, "wa", bit)[:, None], 1)
        value = value.reshape((-1,) + value.shape[2:])
    return value.reshape(-1, value.shape[-1])


def spread_columns(value):
    for bit in bits_of("wa"):
        mine = my_bit("wa", bit)
        paired = value.reshape((value.shape[0], value.shape[1] // 2, 2) + value.shape[2:])
        keep, send = split(paired, mine, 2)
        value = ordered(mine, keep[:, :, 0], swap(send[:, :, 0], "wa", bit), 3)
    return value[:, 0]


def halving_dim(shape):
    if shape[-2] % 16 == 0:
        return len(shape) - 2
    if shape[0] % 2 == 0:
        return 0
    if shape[-2] % 2 == 0:
        return len(shape) - 2
    return len(shape) - 1


def sum_over_ctx(value, bits, finish):
    dims = []
    for bit in bits:
        dim = halving_dim(value.shape)
        keep, send = split(value, my_bit("ctx", bit), dim)
        value = (keep.astype(f32) + swap(send, "ctx", bit).astype(f32)).astype(bf16)
        dims.append(dim - value.ndim if dim else 0)
    value = finish(value)
    for bit, dim in reversed(list(zip(bits, dims))):
        dim = dim % value.ndim
        value = ordered(my_bit("ctx", bit), value, swap(value, "ctx", bit), dim)
    return value


def all_summed(value, axis):
    for bit in bits_of(axis):
        value = value + swap(value, axis, bit)
    return value


def sum_column_grads(grads):
    places = lax.axis_size("wa")
    grads = grads.reshape(grads.shape[0], places, grads.shape[1] // places, grads.shape[2])
    bits = bits_of("ctx")
    if grads.shape[2] % lax.axis_size("ctx") == 0:
        return sum_over_ctx(grads, bits, spread_columns).astype(f32)
    return sum_over_ctx(spread_columns(grads), bits, lambda value: value).astype(f32)


def sum_row_grads(grads):
    return sum_over_ctx(grads[None], bits_of("ctx"), lambda value: value)[0].astype(f32)


def first_half(shape):
    return lax.broadcasted_iota(jnp.int32, shape, 1) < HEAD_DIM


def stack_heads(rows):
    mask = first_half(rows.shape)
    zero = jnp.zeros_like(rows)
    return jnp.concatenate([jnp.where(mask, rows, zero), jnp.where(mask, zero, rows)], axis=0)


def join_heads(stacked):
    rows = stacked.shape[0] // 2
    return jnp.where(first_half((rows, stacked.shape[1])), stacked[:rows], stacked[rows:])


def copy_blocks(order_ref, source, target, block, inward):
    for place in range(source.shape[0] // block):
        start = pl.multiple_of(order_ref[place] * block, block)
        if inward:
            target[place * block : (place + 1) * block, :] = source[pl.ds(start, block), :]
        else:
            target[pl.ds(start, block), :] = source[place * block : (place + 1) * block, :]


def attention_shares(content, position, key_ref, rel_ref, row_start, seq_len):
    length = row_start + TILE
    wide_len = length + TILE
    offset = seq_len - TILE - row_start
    scale = HEAD_DIM ** (-0.5)
    scores = dot_nt(content, key_ref[0:length, :])
    wide = dot_nt(position, rel_ref[offset : offset + wide_len, :])
    halves = []
    for head in range(2):
        part = wide[head * TILE : (head + 1) * TILE]
        turned = pltpu.roll(part, wide_len - (TILE - 1), 1, stride=1, stride_axis=0)
        halves.append(turned[:, :length])
    scores = (scores + jnp.concatenate(halves, axis=0)) * scale
    row = lax.broadcasted_iota(jnp.int32, scores.shape, 0) % TILE + row_start
    col = lax.broadcasted_iota(jnp.int32, scores.shape, 1)
    scores = jnp.where(col <= row, scores, neg_big)
    top = jnp.max(scores, axis=1, keepdims=True)
    raised = jnp.exp(scores - top)
    total = jnp.sum(raised, axis=1, keepdims=True)
    return raised * (1.0 / total)


def attend_tiles(qkv, rel_ref, content_bias, position_bias, out):
    seq_len = qkv.shape[0]
    keys = qkv.at[:, 128:256]
    values = qkv.at[:, 256:384]
    for tile in range(seq_len // TILE):
        start = tile * TILE
        query = qkv[start : start + TILE, 0:128].astype(f32)
        content = stack_heads((query + content_bias).astype(bf16))
        position = stack_heads((query + position_bias).astype(bf16))
        shares = attention_shares(content, position, keys, rel_ref, start, seq_len)
        got = dot_nn(shares.astype(bf16), values[0 : start + TILE, :])
        got = join_heads(got).astype(bf16)
        block = out.shape[1]
        for part in range(TILE // block):
            out[start // block + part] = got[part * block : (part + 1) * block]


def attend_back_tiles(
    qkv, grad, rel_ref, content_bias, position_bias, dqkv, dkey, dvalue, drel, poll
):
    scale = HEAD_DIM ** (-0.5)
    seq_len = qkv.shape[0]
    block = dqkv.shape[1]
    keys = qkv.at[:, 128:256]
    values = qkv.at[:, 256:384]
    dkey[...] = jnp.zeros_like(dkey)
    dvalue[...] = jnp.zeros_like(dvalue)
    drel[...] = jnp.zeros_like(drel)
    row = lax.broadcasted_iota(jnp.int32, (TILE, TILE), 0)
    col = lax.broadcasted_iota(jnp.int32, (TILE, TILE), 1)
    flip = jnp.where(row + col == TILE - 1, 1.0, 0.0).astype(bf16)
    content_sum = jnp.zeros((1, 128), f32)
    position_sum = jnp.zeros((1, 128), f32)
    for tile in range(seq_len // TILE):
        poll(tile)
        start = tile * TILE
        length = start + TILE
        wide_len = length + TILE
        offset = seq_len - TILE - start
        query = qkv[start : start + TILE, 0:128].astype(f32)
        content = stack_heads((query + content_bias).astype(bf16))
        plain = (query + position_bias).astype(bf16)
        position = stack_heads(plain)
        shares = attention_shares(content, position, keys, rel_ref, start, seq_len)
        out_grad = stack_heads(grad[start : start + TILE, :])
        share_grad = dot_nt(out_grad, values[0:length, :])
        delta = jnp.sum(shares * share_grad, axis=1, keepdims=True)
        score_grad = (shares * (share_grad - delta)).astype(bf16)
        content_grad = join_heads(dot_nn(score_grad, keys[0:length, :])) * scale
        parts = []
        for head in range(2):
            turned = dot_nn(flip, score_grad[head * TILE : (head + 1) * TILE])
            turned = jnp.concatenate([turned, jnp.zeros((TILE, TILE), f32)], axis=1)
            parts.append(pltpu.roll(turned, 0, 1, stride=1, stride_axis=0))
        wide_grad = jnp.concatenate(parts, axis=0).astype(bf16)
        relative = rel_ref[offset : offset + wide_len, :]
        turned_grad = join_heads(dot_nn(wide_grad, relative)) * scale
        turned_rows = stack_heads(dot_nn(flip, plain).astype(bf16))
        drel[offset : offset + wide_len, :] += dot_tn(wide_grad, turned_rows)
        high = turned_grad.astype(bf16)
        low = (turned_grad - high.astype(f32)).astype(bf16)
        position_grad = dot_nn(flip, high) + dot_nn(flip, low)
        content_sum += jnp.sum(content_grad, axis=0, keepdims=True)
        position_sum += jnp.sum(turned_grad, axis=0, keepdims=True)
        query_grad = (content_grad + position_grad).astype(bf16)
        for part in range(TILE // block):
            dqkv[start // block + part, :, 0:128] = query_grad[part * block : (part + 1) * block]
        dkey[0:length, :] += dot_tn(score_grad, content)
        dvalue[0:length, :] += dot_tn(shares.astype(bf16), out_grad)
    for part in range(seq_len // block):
        rows = slice(part * block, (part + 1) * block)
        dqkv[part, :, 128:256] = (dkey[rows, :] * scale).astype(bf16)
        dqkv[part, :, 256:384] = dvalue[rows, :].astype(bf16)
    return content_sum, position_sum


in_vmem = pl.BlockSpec(memory_space=pltpu.VMEM)
in_smem = pl.BlockSpec(memory_space=pltpu.SMEM)


def head_mask(shape, head):
    lane = lax.broadcasted_iota(jnp.int32, shape, 1)
    return (lane >= head * HEAD_DIM) & (lane < (head + 1) * HEAD_DIM)


def stack_all(rows):
    zero = jnp.zeros_like(rows)
    heads = rows.shape[1] // HEAD_DIM
    return jnp.concatenate(
        [jnp.where(head_mask(rows.shape, head), rows, zero) for head in range(heads)], axis=0
    )


def join_all(stacked):
    heads = stacked.shape[1] // HEAD_DIM
    rows = stacked.shape[0] // heads
    out = jnp.zeros((rows, stacked.shape[1]), stacked.dtype)
    for head in range(heads):
        part = stacked[head * rows : (head + 1) * rows]
        out = jnp.where(head_mask(part.shape, head), part, out)
    return out


def cross_shares(query, keys):
    scores = dot_nt(query, keys) * (HEAD_DIM ** (-0.5))
    raised = jnp.exp(scores - jnp.max(scores, axis=1, keepdims=True))
    return raised / jnp.sum(raised, axis=1, keepdims=True)


def cross_forward_kernel(q_ref, kv_ref, out_ref):
    width = q_ref.shape[1]
    shares = cross_shares(stack_all(q_ref[...]), kv_ref[:, 0:width])
    out_ref[...] = join_all(dot_nn(shares.astype(bf16), kv_ref[:, width:])).astype(bf16)


def cross_backward_kernel(q_ref, kv_ref, grad_ref, dq_ref, dkv_ref):
    width = q_ref.shape[1]
    scale = HEAD_DIM ** (-0.5)
    keys = kv_ref[:, 0:width]
    query = stack_all(q_ref[...])
    grad = stack_all(grad_ref[...])
    shares = cross_shares(query, keys)
    share_grad = dot_nt(grad, kv_ref[:, width:])
    delta = jnp.sum(shares * share_grad, axis=1, keepdims=True)
    score_grad = (shares * (share_grad - delta)).astype(bf16)
    dq_ref[...] = (join_all(dot_nn(score_grad, keys)) * scale).astype(bf16)
    dkv_ref[:, 0:width] = (dot_tn(score_grad, query) * scale).astype(bf16)
    dkv_ref[:, width:] = dot_tn(shares.astype(bf16), grad).astype(bf16)


def cross_forward(query, pair):
    width = query.shape[1]
    groups = query.shape[0] // GROUP
    return pl.pallas_call(
        cross_forward_kernel,
        out_shape=jax.ShapeDtypeStruct(query.shape, bf16),
        grid=(groups,),
        in_specs=[
            pl.BlockSpec((GROUP, width), lambda g: (g, 0)),
            pl.BlockSpec((NK, 2 * width), lambda g: (g, 0)),
        ],
        out_specs=pl.BlockSpec((GROUP, width), lambda g: (g, 0)),
        cost_estimate=pl.CostEstimate(
            flops=groups * 4 * 256 * 256 * 256, bytes_accessed=groups * 330000, transcendentals=groups * 65536
        ),
        name="cross_forward",
    )(query, pair)


def cross_backward(query, pair, grad):
    width = query.shape[1]
    groups = query.shape[0] // GROUP
    return pl.pallas_call(
        cross_backward_kernel,
        out_shape=[
            jax.ShapeDtypeStruct(query.shape, bf16),
            jax.ShapeDtypeStruct(pair.shape, bf16),
        ],
        grid=(groups,),
        in_specs=[
            pl.BlockSpec((GROUP, width), lambda g: (g, 0)),
            pl.BlockSpec((NK, 2 * width), lambda g: (g, 0)),
            pl.BlockSpec((GROUP, width), lambda g: (g, 0)),
        ],
        out_specs=[
            pl.BlockSpec((GROUP, width), lambda g: (g, 0)),
            pl.BlockSpec((NK, 2 * width), lambda g: (g, 0)),
        ],
        cost_estimate=pl.CostEstimate(
            flops=groups * 10 * 256 * 256 * 256, bytes_accessed=groups * 660000, transcendentals=groups * 65536
        ),
        name="cross_backward",
    )(query, pair, grad)


mesh_id = pl.DeviceIdType.MESH


def signal_to(barrier, ctx, wa):
    pl.semaphore_signal(barrier, inc=1, device_id=(ctx, wa), device_id_type=mesh_id)


def tree_sum(values):
    while len(values) > 1:
        values = [a + b for a, b in zip(values[::2], values[1::2])]
    return values[0]


def gelu_slope(value):
    inner = 0.7978845608028654 * (value + 0.044715 * value * value * value)
    turned = jnp.tanh(inner)
    slope = 0.7978845608028654 * (1.0 + 3.0 * 0.044715 * value * value)
    return 0.5 * (1.0 + turned) + 0.5 * value * (1.0 - turned * turned) * slope


def places_here():
    return lax.axis_index("ctx"), lax.axis_index("wa")


def meet_all():
    c, w = places_here()
    owner = c // 2
    own = owner == w
    barrier = pltpu.get_barrier_semaphore()
    for j in range(1, 8):
        signal_to(barrier, c ^ j, w)
    for j in range(1, 4):
        signal_to(barrier, c, w ^ j)
    for j in range(1, 8):
        signal_to(barrier, c ^ j, owner)
    for r in range(4):
        for h in range(2):

            @pl.when(jnp.logical_not(jnp.logical_and(2 * w + h == c, r == 0)))
            def _(r=r, h=h):
                signal_to(barrier, 2 * w + h, w ^ r)

    @pl.when(jnp.logical_not(own))
    def _():
        signal_to(barrier, c, owner)

    pl.semaphore_wait(barrier, 26 - 2 * own.astype(jnp.int32))


def meet_lines():
    c, w = places_here()
    barrier = pltpu.get_barrier_semaphore()
    for j in range(1, 8):
        signal_to(barrier, c ^ j, w)
    for j in range(1, 4):
        signal_to(barrier, c, w ^ j)
    pl.semaphore_wait(barrier, 10)


def remote(source, target, send, recv, ctx, wa):
    return pltpu.make_async_remote_copy(
        src_ref=source,
        dst_ref=target,
        send_sem=send,
        recv_sem=recv,
        device_id=(ctx, wa),
        device_id_type=mesh_id,
    )


class GatherRows:

    def __init__(self, buf, send, recv):
        self.buf, self.send, self.recv = buf, send, recv
        self.c, self.w = places_here()

    def copy(self, k):
        source, entry, j = ((0, 1, 1), (0, 2, 2), (2, 3, 1))[k]
        return remote(
            self.buf.at[source],
            self.buf.at[entry],
            self.send.at[k],
            self.recv.at[k],
            self.c,
            self.w ^ j,
        )

    def start(self):
        self.copy(1).start()
        self.copy(0).start()

    def near(self):
        self.copy(0).wait()

    def relay(self):
        self.copy(1).wait()
        self.copy(2).start()

    def far(self):
        self.copy(2).wait()


class SumRows:

    def __init__(self, out_buf, in_buf, send, recv):
        self.out, self.inn, self.send, self.recv = out_buf, in_buf, send, recv
        self.c, self.w = places_here()

    def copy(self, k):
        j = (1, 1, 2)[k]
        return remote(
            self.out.at[k], self.inn.at[k], self.send.at[k], self.recv.at[k], self.c, self.w ^ j
        )

    def give_near(self, value):
        self.out[0] = value.astype(bf16)
        self.copy(0).start()

    def give_far(self, value):
        self.out[1] = value.astype(bf16)
        self.copy(1).start()

    def pass_on(self, value):
        self.copy(1).wait()
        self.out[2] = (value + self.inn[1].astype(f32)).astype(bf16)
        self.copy(2).start()

    def total(self, value):
        self.copy(0).wait()
        value = value + self.inn[0].astype(f32)
        self.copy(2).wait()
        return value + self.inn[2].astype(f32)


class CtxSum:

    def __init__(self, send, recv, x=None, half=None, part=None, share=None, out=None, spread=0):
        self.send, self.recv = send, recv
        self.x, self.half, self.part, self.share, self.out = x, half, part, share, out
        self.spread = spread
        self.c, self.w = places_here()
        self.z, self.y = self.c // 2, self.c % 2

    def y_copy(self):
        return remote(
            self.x.at[:, 1 - self.y], self.half, self.send.at[0], self.recv.at[0], self.c ^ 1, self.w
        )

    def start_y(self):
        self.y_copy().start()

    def finish_y(self):
        self.y_copy().wait()
        for z in range(4):
            mine = self.x[z, self.y].astype(f32)
            self.half[z] = (self.half[z].astype(f32) + mine).astype(bf16)

    def z_copy(self, j):
        return remote(
            self.half.at[self.z ^ j],
            self.part.at[j - 1],
            self.send.at[j],
            self.recv.at[j],
            self.c ^ (2 * j),
            self.w,
        )

    def start_z(self, order=(2, 3, 1)):
        for j in order:
            self.z_copy(j).start()

    def finish_z(self):
        total = self.half[self.z].astype(f32)
        for j in (1, 2, 3):
            self.z_copy(j).wait()
            total = total + self.part[j - 1].astype(f32)
        if len(self.share.shape) == 2:
            self.share[...] = total.astype(bf16)
            return
        count = total.shape[0] // 4
        blank = jnp.zeros((self.share.shape[1] - count, total.shape[1]), f32)
        for place in range(4):
            part = jnp.concatenate([total[place * count : (place + 1) * count], blank], axis=0)
            self.share[place] = part.astype(bf16)

    def columns(self, place):
        width = self.spread
        return self.out.at[self.z, self.y, :, pl.ds(pl.multiple_of(place * width, 128), width)]

    def wa_copy(self, j, place):
        return remote(
            self.share.at[self.w ^ j],
            self.columns(place),
            self.send.at[3 + j],
            self.recv.at[3 + j],
            self.c,
            self.w ^ j,
        )

    def own_copy(self):
        source = self.share.at[self.w] if self.spread else self.share
        target = self.columns(self.w) if self.spread else self.out.at[self.z, self.y]
        return pltpu.make_async_copy(source, target, self.send.at[11])

    def start_wa(self):
        if self.spread:
            for j in (2, 3, 1):
                self.wa_copy(j, self.w).start()
        self.own_copy().start()

    def finish_wa(self):
        self.own_copy().wait()
        if self.spread:
            for j in (1, 2, 3):
                self.wa_copy(j, self.w).wait_send()
                self.wa_copy(j, self.w ^ j).wait_recv()

    def back_z_copy(self, j, z):
        mine = self.out.at[z, self.y]
        return remote(mine, mine, self.send.at[6 + j], self.recv.at[6 + j], self.c ^ (2 * j), self.w)

    def start_back_z(self):
        for j in (2, 3, 1):
            self.back_z_copy(j, self.z).start()

    def finish_back_z(self):
        for j in (1, 2, 3):
            self.back_z_copy(j, self.z).wait_send()
            self.back_z_copy(j, self.z ^ j).wait_recv()

    def back_y_copy(self, y):
        part = self.out.at[:, y]
        return remote(part, part, self.send.at[10], self.recv.at[10], self.c ^ 1, self.w)

    def start_back_y(self):
        self.back_y_copy(self.y).start()

    def finish_back_y(self):
        self.back_y_copy(self.y).wait_send()
        self.back_y_copy(1 - self.y).wait_recv()


def put_shares(target, grads, first=0):
    count = grads.shape[0] // 32
    for share in range(8):
        starts = [(place * 8 + share) * count for place in range(4)]
        part = jnp.concatenate([grads[start : start + count] for start in starts], axis=0)
        target[share // 2, share % 2, :, first : first + part.shape[1]] = part.astype(bf16)


def put_rows(target, grads):
    count = grads.shape[0] // 8
    for share in range(8):
        target[share // 2, share % 2] = grads[share * count : (share + 1) * count].astype(bf16)


class Cut:

    def __init__(self, ref, start):
        self.ref, self.start = ref, start

    @property
    def at(self):
        return self

    def __getitem__(self, k):
        return self.ref.at[self.start + k]


class Pool:
    def __init__(self, ref):
        self.ref, self.used = ref, 0

    def take(self, count):
        cut = Cut(self.ref, self.used)
        self.used += count
        return cut


class LineGather:

    def __init__(self, out, send, recv):
        self.out, self.send, self.recv = out, send, recv
        self.c, self.w = places_here()
        self.z = self.c // 2
        self.right, self.left = self.z < 3, self.z > 0

    def y_copy(self, block, slot):
        ref = self.out.at[block]
        return remote(ref, ref, self.send.at[slot], self.recv.at[slot], self.c ^ 1, self.w)

    def z_copy(self, block, slot, step):
        k = slot + (7 if step > 0 else 10)
        ref = self.out.at[block]
        return remote(ref, ref, self.send.at[k], self.recv.at[k], self.c + step, self.w)

    def start(self):
        @pl.when(self.right)
        def _():
            self.z_copy(self.c, 0, 2).start()

        @pl.when(self.left)
        def _():
            self.z_copy(self.c, 0, -2).start()

        self.y_copy(self.c, 0).start()

    def step(self, t):
        @pl.when(self.z > t)
        def _():
            block = self.c - 2 * (t + 1)
            self.z_copy(block, t, 2).wait_recv()
            if t < 2:

                @pl.when(self.right)
                def _():
                    self.z_copy(block, t + 1, 2).start()

            self.y_copy(block, t + 1).start()

        @pl.when(self.z < 3 - t)
        def _():
            block = self.c + 2 * (t + 1)
            self.z_copy(block, t, -2).wait_recv()
            if t < 2:

                @pl.when(self.left)
                def _():
                    self.z_copy(block, t + 1, -2).start()

            self.y_copy(block, t + 4).start()

    def finish(self):
        self.y_copy(self.c, 0).wait_send()
        self.y_copy(self.c ^ 1, 0).wait_recv()
        for t in range(3):
            for step, at, near in ((-2, t + 1, self.z > t), (2, t + 4, self.z < 3 - t)):

                @pl.when(near)
                def _(step=step, at=at):
                    self.y_copy(self.c + step * (t + 1), at).wait_send()
                    self.y_copy((self.c ^ 1) + step * (t + 1), at).wait_recv()

        @pl.when(self.right)
        def _():
            self.z_copy(self.c, 0, 2).wait_send()

        @pl.when(self.left)
        def _():
            self.z_copy(self.c, 0, -2).wait_send()

        for t in range(2):

            @pl.when(jnp.logical_and(self.z > t, self.right))
            def _():
                self.z_copy(self.c, t + 1, 2).wait_send()

            @pl.when(jnp.logical_and(self.z < 3 - t, self.left))
            def _():
                self.z_copy(self.c, t + 1, -2).wait_send()


class Columns:

    def __init__(self, source, target, width, first, send, recv, at=None):
        self.source, self.target, self.width, self.first = source, target, width, first
        self.send, self.recv, self.column = send, recv, at
        self.shared = at is None
        self.c, self.w = places_here()
        self.y = self.c % 2

    def taken(self, place, half=None):
        start = place * self.width if self.column is None else self.column
        rows = self.source.shape[0]
        which = slice(None) if half is None else pl.ds(pl.multiple_of(half * (rows // 2), 16), rows // 2)
        return self.source.at[which, pl.ds(pl.multiple_of(start, 128), self.width)]

    def put(self, place, half=None):
        rows = self.source.shape[0]
        start, count = place * rows, rows
        if half is not None:
            start, count = start + half * (rows // 2), rows // 2
        return self.target.at[
            pl.ds(pl.multiple_of(start, 16), count), self.first : self.first + self.width
        ]

    def copy(self, j, place):
        half = self.y if self.shared and j > 1 else None
        return remote(
            self.taken(self.w ^ j, half),
            self.put(place, half),
            self.send.at[j],
            self.recv.at[j],
            self.c,
            self.w ^ j,
        )

    def handed(self, place):
        ref = self.put(place)
        return remote(ref, ref, self.send.at[3], self.recv.at[3], self.c, self.w ^ 1)

    def passed(self, j, half):
        ref = self.put(self.w ^ j, half)
        return remote(ref, ref, self.send.at[2 + j], self.recv.at[2 + j], self.c ^ 1, self.w)

    def own(self):
        return pltpu.make_async_copy(self.taken(self.w), self.put(self.w), self.send.at[0])

    def start(self):
        for j in (2, 3, 1) if self.shared else (2, 1):
            self.copy(j, self.w).start()
        self.own().start()

    def relay(self):
        if not self.shared:
            self.copy(2, self.w).wait_send()
            self.copy(2, self.w ^ 2).wait_recv()
            self.handed(self.w ^ 2).start()
            return
        for j in (2, 3):
            self.copy(j, self.w).wait_send()
            self.copy(j, self.w ^ j).wait_recv()
            self.passed(j, self.y).start()

    def finish(self):
        self.own().wait()
        self.copy(1, self.w).wait_send()
        self.copy(1, self.w ^ 1).wait_recv()
        if not self.shared:
            self.handed(self.w ^ 2).wait_send()
            self.handed(self.w ^ 3).wait_recv()
        else:
            for j in (2, 3):
                self.passed(j, self.y).wait_send()
                self.passed(j, 1 - self.y).wait_recv()


class SmallSum:

    def __init__(self, ref, got, axis, send, recv):
        self.ref, self.got, self.axis, self.send, self.recv = ref, got, axis, send, recv
        self.c, self.w = places_here()

    def copy(self, k):
        j = k + 1
        ctx, wa = (self.c ^ j, self.w) if self.axis == "ctx" else (self.c, self.w ^ j)
        return remote(self.ref, self.got.at[k], self.send.at[k], self.recv.at[k], ctx, wa)

    def start(self):
        for k in range(self.got.shape[0]):
            self.copy(k).start()

    def finish(self):
        count = self.got.shape[0]
        for k in range(count):
            self.copy(k).wait()
        self.ref[...] = tree_sum([self.ref[...]] + [self.got[k] for k in range(count)])


class SwapHeads:

    def __init__(self, by_heads, by_rows, outward, send, recv):
        self.heads, self.rows, self.outward = by_heads, by_rows, outward
        self.send, self.recv = send, recv
        self.c, self.w = places_here()
        self.owner, self.half = self.c // 2, self.c % 2
        self.own = self.owner == self.w
        self.other = jnp.logical_not(self.own)

    def lanes(self):
        return pl.ds(pl.multiple_of(self.half * 128, 128), 128)

    def out_copy(self, j):
        slot = self.w ^ self.owner
        return remote(
            self.heads.at[self.c ^ j],
            self.rows.at[slot, :, self.lanes()],
            self.send.at[j],
            self.recv.at[slot * 2 + self.half],
            self.c ^ j,
            self.owner,
        )

    def start_out(self):
        for j in range(7, 0, -1):
            self.out_copy(j).start()

        @pl.when(self.other)
        def _():
            self.out_copy(0).start()

        @pl.when(self.own)
        def _():
            slot = self.w ^ self.owner
            pltpu.make_async_copy(
                self.heads.at[self.c],
                self.rows.at[slot, :, self.lanes()],
                self.recv.at[slot * 2 + self.half],
            ).start()

    def wait_rows(self, r):
        for h in range(2):
            remote(
                self.heads.at[0],
                self.rows.at[r, :, h * 128 : (h + 1) * 128],
                self.send.at[0],
                self.recv.at[r * 2 + h],
                self.c ^ 1,
                self.w,
            ).wait_recv()

    def finish_out(self):
        for j in range(1, 8):
            self.out_copy(j).wait_send()

        @pl.when(self.other)
        def _():
            self.out_copy(0).wait_send()

    def in_copy(self, r, h):
        return remote(
            self.rows.at[r, :, h * 128 : (h + 1) * 128],
            self.heads.at[self.c],
            self.send.at[r * 2 + h],
            self.recv.at[self.c],
            2 * self.w + h,
            self.w ^ r,
        )

    def mine(self, r, h):
        return jnp.logical_and(2 * self.w + h == self.c, r == 0)

    def start_in(self, r):
        for h in range(2):

            @pl.when(jnp.logical_not(self.mine(r, h)))
            def _():
                self.in_copy(r, h).start()

            @pl.when(self.mine(r, h))
            def _():
                pltpu.make_async_copy(
                    self.rows.at[r, :, h * 128 : (h + 1) * 128],
                    self.heads.at[self.c],
                    self.recv.at[self.c],
                ).start()

    def finish_in(self):
        for block in range(8):
            remote(
                self.rows.at[0, :, 0:128],
                self.heads.at[block],
                self.send.at[0],
                self.recv.at[block],
                self.c ^ 1,
                self.w,
            ).wait_recv()
        for r in range(4):
            for h in range(2):

                @pl.when(jnp.logical_not(self.mine(r, h)))
                def _(r=r, h=h):
                    self.in_copy(r, h).wait_send()


def layer_kernel(names, total_tokens, block, *refs):
    v = types.SimpleNamespace(**dict(zip(names, refs, strict=True)))
    c, w = places_here()
    send, recv, local = Pool(v.send), Pool(v.recv), Pool(v.local)
    tok, width = v.tokens.shape
    seq_len = 8 * tok
    rows = 4 * tok
    cols = v.output_w.shape[0]
    hidden = v.down_w.shape[0]
    scale = HEAD_DIM ** (-0.5)

    def load(source, target):
        copy = pltpu.make_async_copy(source, target, local.take(1).at[0])
        copy.start()
        return copy

    near_load = load(v.neighbours, v.near.at[0])
    late = [
        load(v.output_any, v.output_w),
        load(v.cross_out_any, v.cross_out_w),
        load(v.down_any, v.down_w),
    ]
    mask = v.mask[...].astype(f32)
    v.tokens_all[c] = v.tokens[...]
    meet_all()

    near_sum = SmallSum(v.small_all, v.small_near, "wa", send.take(3), recv.take(3))
    count_sum = SmallSum(v.count, v.count_far, "ctx", send.take(7), recv.take(7))
    gather = LineGather(v.tokens_all, send.take(13), recv.take(13))
    pair = [
        Columns(weight, v.pair, 128, 128 * m, send.take(4), recv.take(4), c * 128)
        for m, weight in enumerate((v.query_any, v.key_any, v.value_any, v.relative_any))
    ]
    cross = [
        Columns(weight, target, cols, first, send.take(6), recv.take(6))
        for weight, target, first in (
            (v.cross_key_any, v.pair_cols, 0),
            (v.cross_value_any, v.pair_cols, cols),
            (v.cross_query_any, v.query_cols, 0),
        )
    ]
    up_columns = Columns(v.up_any, v.up_cols, hidden, 0, send.take(6), recv.take(6))
    near_send, near_recv = send.take(3), recv.take(3)
    near_gather = GatherRows(v.near, near_send, near_recv)
    gather.start()
    for part in pair:
        part.start()

    part_width = width // 4
    count = 3 * part_width + 2 * cols
    entry = lax.broadcasted_iota(jnp.int32, (count, 1024), 0)
    for k in range(1, 3):
        entry = jnp.where(
            lax.broadcasted_iota(jnp.int32, (count, 1024), 0) >= k * part_width, entry - part_width, entry
        )
    bias = lax.broadcasted_iota(jnp.int32, (count, 1024), 0) - 3 * part_width
    entry = jnp.where(bias >= 0, bias, entry)
    entry = jnp.where(bias >= cols, bias - cols, entry)
    start = jnp.where(bias >= 0, w * cols, w * part_width)
    chosen = lax.broadcasted_iota(jnp.int32, (count, 1024), 1) == entry + start
    lane = lax.broadcasted_iota(jnp.int32, (8, count), 1)
    row = lax.broadcasted_iota(jnp.int32, (8, count), 0)
    bounds = (0, part_width, 2 * part_width, 3 * part_width, 3 * part_width + cols, count)
    picked = jnp.zeros((8, count), f32)
    for k in range(5):
        inside = (row == k) & (lane >= bounds[k]) & (lane < bounds[k + 1])
        picked = jnp.where(inside, v.gain_row[...].astype(f32), picked)
    v.small_all[...] = dot_nn(picked.astype(bf16), jnp.where(chosen, 1.0, 0.0).astype(bf16))
    v.small_all[5:6, :] = jnp.broadcast_to(jnp.sum(mask, keepdims=True), (1, 1024))
    near_sum.start()
    near_load.wait()
    near_gather.start()
    for part in cross:
        part.start()

    def wave_rows(part, carry):
        start = pl.multiple_of(part * 64, 64)
        first = v.tables[pl.ds(part, 1), :] * v.tables[32:96, :]
        second = v.tables[pl.ds(part + 16, 1), :] * v.tables[96:160, :]
        v.waves[pl.ds(start, 64), :] = (first + second).astype(bf16)
        return carry

    lax.fori_loop(0, seq_len // 64, wave_rows, 0)
    leaving = Leaving(v, local)
    leaving.leave("waves")
    gather.step(0)
    near_sum.finish()
    v.count[...] = jnp.broadcast_to(v.small_all[5:6, 0:128], v.count.shape)
    count_sum.start()
    for part in pair:
        part.relay()
    gather.step(1)
    for part in pair:
        part.finish()
    v.table[0:seq_len, :] = dot_nn(v.waves[...], v.pair[:, 384:512]).astype(bf16)
    v.table[seq_len:, :] = jnp.zeros((TILE, 128), bf16)
    v.biases[...] = v.small_all[:, pl.ds(pl.multiple_of(c * 128, 128), 128)]
    v.gains[...] = v.small_all[:, 0:width]
    gather.step(2)
    gather.finish()
    gain_one, gain_two, gain_three = (v.gains[k : k + 1, :] for k in range(3))

    def project(part, carry):
        start = pl.multiple_of(part * tok, tok)
        value = v.tokens_all[part].astype(f32)
        normed = (value * inverse_rms(value) * gain_one).astype(bf16)
        v.normed_a[pl.ds(start, tok), :] = normed
        mixed = dot_nn(normed, v.pair[:, 0:384]).astype(bf16)
        for h in range(tok // block):
            v.qkv[part * (tok // block) + h] = mixed[h * block : (h + 1) * block]
        return carry

    lax.fori_loop(0, 8, project, 0)
    leaving.leave("normed_a")
    for place in range(seq_len // block):
        take_block(v.qkv, v.inverse, place, v.qkv_order.at[place * block : (place + 1) * block, :])
    attend_tiles(v.qkv_order, v.table, v.biases[3:4, :], v.biases[4:5, :], v.heads_order)
    per = tok // block
    for place in range(seq_len // block):
        at = (place % per) * block
        take_block(v.heads_order, v.order, place, v.heads.at[place // per, at : at + block, :])
    out_swap = SwapHeads(v.heads, v.attended, True, send.take(8), recv.take(8))
    out_swap.start_out()
    for copy in late:
        copy.wait()

    gathers = [GatherRows(ref, send.take(3), recv.take(3)) for ref in (v.rows_b, v.rows_c)]
    sums = [SumRows(v.give.at[k], v.take.at[k], send.take(3), recv.take(3)) for k in range(3)]

    def output_part(r):
        return dot_nn(v.attended[r], v.output_w[...])

    out_swap.wait_rows(3)
    sums[0].give_far(output_part(3))
    out_swap.wait_rows(1)
    sums[0].give_near(output_part(1))
    out_swap.wait_rows(2)
    sums[0].pass_on(output_part(2))
    near_gather.near()
    near_gather.relay()
    for part in cross:
        part.relay()
    out_swap.wait_rows(0)
    v.hidden_one[...] = v.tokens[...].astype(f32) + sums[0].total(output_part(0))
    value = v.hidden_one[...]
    v.rows_b[0] = (value * inverse_rms(value) * gain_two).astype(bf16)

    gathers[0].start()
    out_swap.finish_out()
    near_gather.far()
    for part in cross:
        part.finish()
    leaving.leave("pair_cols")
    near_count = v.near.shape[1]

    def near_project(r, carry):
        start = pl.multiple_of(r * near_count, near_count)
        v.cross_pair[pl.ds(start, near_count), :] = dot_nn(v.near[r], v.pair_cols[...]).astype(bf16)
        return carry

    lax.fori_loop(0, 4, near_project, 0)

    def cross_part(r):
        v.cross_q[r * tok : (r + 1) * tok, :] = dot_nn(v.rows_b[r], v.query_cols[...]).astype(bf16)

        def group(g, carry):
            at = pl.multiple_of(r * tok + g * GROUP, GROUP)
            near = pl.multiple_of((r * (tok // GROUP) + g) * NK, NK)
            query = stack_all(v.cross_q[pl.ds(at, GROUP), :])
            shares = cross_shares(query, v.cross_pair[pl.ds(near, NK), 0:cols])
            out = dot_nn(shares.astype(bf16), v.cross_pair[pl.ds(near, NK), cols:])
            v.crossed[pl.ds(at, GROUP), :] = join_all(out).astype(bf16)
            return carry

        lax.fori_loop(0, tok // GROUP, group, 0, unroll=True)
        return dot_nn(v.crossed[r * tok : (r + 1) * tok, :], v.cross_out_w[...])

    def in_turn(gathered, summed, part, arrived=None, between=None):
        v.keep[0] = part(0)
        gathered.near()
        summed.give_near(part(1))
        gathered.relay()
        if arrived is not None:
            arrived()
        v.keep[2] = part(2)
        gathered.far()
        summed.give_far(part(3))
        summed.pass_on(v.keep[2])
        if between is not None:
            between()
        return summed.total(v.keep[0])

    v.hidden_two[...] = v.hidden_one[...] + in_turn(
        gathers[0], sums[1], cross_part, up_columns.start, up_columns.relay
    )
    value = v.hidden_two[...]
    v.rows_c[0] = (value * inverse_rms(value) * gain_three).astype(bf16)

    gathers[1].start()
    up_columns.finish()

    def feed_part(r):
        part = pl.ds(r * tok, tok)
        v.pre_act[part, :] = dot_nn(v.rows_c[r], v.up_cols[...])
        v.activated[part, :] = gelu_tanh(v.pre_act[part, :]).astype(bf16)
        return dot_nn(v.activated[part, :], v.down_w[...])

    layer_out = v.hidden_two[...] + in_turn(gathers[1], sums[2], feed_part)
    v.layer_out[...] = layer_out

    count_sum.finish()
    error = layer_out - v.teacher[...].astype(f32)
    square = (tok, tok)
    same = lax.broadcasted_iota(jnp.int32, square, 0) == lax.broadcasted_iota(jnp.int32, square, 1)
    valid = jnp.sum(jnp.where(same, mask, 0.0), axis=1, keepdims=True)
    weighted = valid * error
    v.small[0:5, :] = jnp.zeros((5, 1024), f32)
    v.small[5:6, :] = jnp.broadcast_to(jnp.sum(weighted * error, keepdims=True), (1, 1024))
    v.small[6:8, :] = jnp.broadcast_to(v.count[0:1, 0:1], (2, 1024))
    v.out_grad[...] = (total_tokens / v.count[0:1, 0:1]) * weighted

    leaving.leave("layer_out")
    middle_back(v, send, recv, leaving, block)
    leaving.finish()


class Leaving:

    def __init__(self, v, local):
        self.v, self.local, self.copies = v, local, []

    def leave(self, name):
        copy = pltpu.make_async_copy(
            getattr(self.v, name), getattr(self.v, name + "_any"), self.local.take(1).at[0]
        )
        copy.start()
        self.copies.append(copy)

    def finish(self):
        for copy in self.copies:
            copy.wait()


def take_block(source, chosen, place, target):
    target[...] = source[chosen[place]]


def middle_back(v, send, recv, leaving, block):
    c, w = places_here()
    tok, width = v.tokens.shape
    rows = 4 * tok
    cols = v.output_w.shape[0]
    scale = HEAD_DIM ** (-0.5)
    first, second, third = (
        GatherRows(ref, send.take(3), recv.take(3)) for ref in (v.rows_o, v.rows_two, v.rows_one)
    )
    sum_c, sum_b = (
        SumRows(v.give.at[k], v.take.at[k], send.take(3), recv.take(3)) for k in (3, 4)
    )
    down = CtxSum(send.take(12), recv.take(12), v.down_x, v.down_half, v.down_part, v.down_share)
    up = CtxSum(send.take(12), recv.take(12), v.up_x, v.up_half, v.up_part, v.up_share)
    cross = CtxSum(send.take(12), recv.take(12), v.cross_x, v.cross_half)
    heads = SwapHeads(v.heads_grad, v.heads_out, False, send.take(8), recv.take(8))
    v.rows_o[0] = v.out_grad[...].astype(bf16)

    first.start()

    def feed_back(r):
        part = pl.ds(r * tok, tok)
        act_grad = dot_nt(v.rows_o[r], v.down_w[...])
        v.pre_grad[part, :] = (act_grad * gelu_slope(v.pre_act[part, :])).astype(bf16)
        return dot_nt(v.pre_grad[part, :], v.up_cols[...])

    v.keep[0] = feed_back(0)
    first.near()
    sum_c.give_near(feed_back(1))
    first.relay()
    v.keep[1] = feed_back(2)
    first.far()
    sum_c.give_far(feed_back(3))
    sum_c.pass_on(v.keep[1])
    put_rows(v.down_x, dot_tn(v.activated[...], v.rows_o[...].reshape(rows, width)))
    down.start_y()
    put_shares(v.up_x, dot_tn(v.rows_c[...].reshape(rows, width), v.pre_grad[...]))
    up.start_y()
    normed_grad = sum_c.total(v.keep[0])
    value = v.hidden_two[...]
    inverse = inverse_rms(value)
    two_grad = v.out_grad[...] + norm_pull(value, inverse, v.gains[2:3, :], normed_grad)
    gain_three = jnp.sum(normed_grad * value * inverse, axis=0, keepdims=True)
    v.keep[1] = two_grad
    v.rows_two[0] = two_grad.astype(bf16)

    second.start()

    def cross_back(r):
        part = slice(r * tok, (r + 1) * tok)
        v.crossed_grad[...] = dot_nt(v.rows_two[r], v.cross_out_w[...]).astype(bf16)

        def group(g, carry):
            within = pl.multiple_of(g * GROUP, GROUP)
            at = pl.multiple_of(r * tok + g * GROUP, GROUP)
            near = pl.ds(pl.multiple_of((r * (tok // GROUP) + g) * NK, NK), NK)
            query = stack_all(v.cross_q[pl.ds(at, GROUP), :])
            grad = stack_all(v.crossed_grad[pl.ds(within, GROUP), :])
            keys = v.cross_pair[near, 0:cols]
            shares = cross_shares(query, keys)
            share_grad = dot_nt(grad, v.cross_pair[near, cols:])
            delta = jnp.sum(shares * share_grad, axis=1, keepdims=True)
            score_grad = (shares * (share_grad - delta)).astype(bf16)
            query_grad = join_all(dot_nn(score_grad, keys)) * scale
            v.cross_grad[pl.ds(at, GROUP), :] = query_grad.astype(bf16)
            v.pair_grad[near, 0:cols] = (dot_tn(score_grad, query) * scale).astype(bf16)
            v.pair_grad[near, cols:] = dot_tn(shares.astype(bf16), grad).astype(bf16)
            return carry

        lax.fori_loop(0, tok // GROUP, group, 0, unroll=True)
        return dot_nt(v.cross_grad[part, :], v.query_cols[...])

    v.keep[0] = cross_back(0)
    second.near()
    sum_b.give_near(cross_back(1))
    second.relay()
    v.keep[2] = cross_back(2)
    second.far()
    down.finish_y()
    down.start_z()
    sum_b.give_far(cross_back(3))
    sum_b.pass_on(v.keep[2])
    leaving.leave("pair_grad")
    normed_b = v.rows_b[...].reshape(rows, width)
    put_rows(v.cross_out_x, dot_tn(v.crossed[...], v.rows_two[...].reshape(rows, width)))
    leaving.leave("cross_out_x")
    put_shares(v.cross_x, dot_tn(normed_b, v.cross_grad[...]), 0)
    normed_grad = sum_b.total(v.keep[0])
    value = v.hidden_one[...]
    inverse = inverse_rms(value)
    one_grad = v.keep[1] + norm_pull(value, inverse, v.gains[1:2, :], normed_grad)
    gain_two = jnp.sum(normed_grad * value * inverse, axis=0, keepdims=True)
    v.small[1:2, 0:width] = gain_two
    v.small[2:3, 0:width] = gain_three
    v.one_grad[...] = one_grad
    leaving.leave("one_grad")
    v.rows_one[0] = one_grad.astype(bf16)

    third.start()
    near = v.near[...].reshape(-1, width)
    put_shares(v.cross_x, dot_tn(near, v.pair_grad[...]), cols)

    def head_back(r):
        v.heads_out[r] = dot_nt(v.rows_one[r], v.output_w[...]).astype(bf16)
        heads.start_in(r)

    head_back(0)
    third.near()
    head_back(1)
    third.relay()
    head_back(2)
    third.far()
    head_back(3)
    attended = jnp.concatenate([v.attended[r] for r in range(4)], axis=0)
    put_rows(v.output_x, dot_tn(attended, v.rows_one[...].reshape(rows, width)))
    heads.finish_in()
    up.finish_y()
    up.start_z()
    cross.start_y()
    leaving.leave("output_x")
    leaving.leave("gains")

    per = tok // block
    for place in range(8 * per):
        at = (place % per) * block
        v.heads_stored[place] = v.heads_grad[place // per, at : at + block, :]
    for place in range(8 * per):
        take_block(
            v.heads_stored, v.inverse, place, v.grad_order.at[place * block : (place + 1) * block, :]
        )

    def poll(tile):
        if tile == 1:
            down.finish_z()
            leaving.leave("down_share")

    content_sum, position_sum = attend_back_tiles(
        v.qkv_order,
        v.grad_order,
        v.table,
        v.biases[3:4, :],
        v.biases[4:5, :],
        v.qkv_grad_order,
        v.dkey,
        v.dvalue,
        v.drel,
        poll,
    )
    v.table_grad[...] = v.drel[0 : v.table_grad.shape[0], :] * scale
    leaving.leave("table_grad")
    both = jnp.concatenate([content_sum, position_sum] * 4, axis=1)
    pairs = lax.broadcasted_iota(jnp.int32, both.shape, 1) // 256
    v.small[3:4, :] = jnp.where(pairs == c, both, 0.0)
    v.small[4:5, :] = jnp.where(pairs + 4 == c, both, 0.0)
    leaving.leave("small")
    for place in range(8 * per):
        at = (place % per) * block
        take_block(
            v.qkv_grad_order, v.order, place, v.query_grad.at[place // per, at : at + block, :]
        )
    leaving.leave("query_grad")
    cross.finish_y()
    leaving.leave("cross_half")
    up.finish_z()
    leaving.leave("up_share")


def layer(total_tokens, block, orders, given, collective_id):
    tok, width = given["tokens"].shape
    hidden = given["down_any"].shape[0]
    cols = given["output_any"].shape[0]
    near = given["neighbours"].shape[0]
    seq_len = 8 * tok
    rows = 4 * tok
    padded = -(-(width // 32) // 8) * 8
    any_space = pl.BlockSpec(memory_space=pl.ANY)
    shape = jax.ShapeDtypeStruct
    vmem = pltpu.VMEM
    dma = pltpu.SemaphoreType.DMA
    kept = dict(
        layer_out=shape((tok, width), f32),
        small=shape((8, 1024), f32),
        gains=shape((8, width), f32),
        waves=shape((seq_len, width), bf16),
        normed_a=shape((seq_len, width), bf16),
        pair_cols=shape((width, 2 * cols), bf16),
        one_grad=shape((tok, width), f32),
        pair_grad=shape((4 * near, 2 * cols), bf16),
        query_grad=shape((8, tok, 384), bf16),
        table_grad=shape((seq_len, 128), f32),
        down_share=shape((hidden // 8, width), bf16),
        up_share=shape((4, padded, hidden), bf16),
        cross_half=shape((4, width // 8, 3 * cols), bf16),
        cross_out_x=shape((4, 2, cols // 8, width), bf16),
        output_x=shape((4, 2, cols // 8, width), bf16),
    )
    results = {name + "_any": value for name, value in kept.items()}
    scratch = dict(
        small_all=vmem((8, 1024), f32),
        small_near=vmem((3, 8, 1024), f32),
        qkv=vmem((seq_len // block, block, 384), bf16),
        table=vmem((seq_len + TILE, 128), bf16),
        biases=vmem((8, 128), f32),
        count=vmem((8, 128), f32),
        heads_grad=vmem((8, tok, 128), bf16),
        grad_order=vmem((seq_len, 128), bf16),
        qkv_grad_order=vmem((seq_len // block, block, 384), bf16),
        dkey=vmem((seq_len, 128), f32),
        dvalue=vmem((seq_len, 128), f32),
        drel=vmem((seq_len + TILE, 128), f32),
        count_far=vmem((7, 8, 128), f32),
        tokens_all=vmem((8, tok, width), bf16),
        pair=vmem((width, 512), bf16),
        qkv_order=vmem((seq_len, 384), bf16),
        heads_order=vmem((seq_len // block, block, 128), bf16),
        heads_stored=vmem((seq_len // block, block, 128), bf16),
        heads=vmem((8, tok, 128), bf16),
        attended=vmem((4, tok, cols), bf16),
        near=vmem((4, near, width), bf16),
        query_cols=vmem((width, cols), bf16),
        up_cols=vmem((width, hidden), bf16),
        output_w=vmem((cols, width), bf16),
        cross_out_w=vmem((cols, width), bf16),
        down_w=vmem((hidden, width), bf16),
        cross_pair=vmem((4 * near, 2 * cols), bf16),
        cross_q=vmem((rows, cols), bf16),
        crossed=vmem((rows, cols), bf16),
        crossed_grad=vmem((tok, cols), bf16),
        hidden_one=vmem((tok, width), f32),
        hidden_two=vmem((tok, width), f32),
        out_grad=vmem((tok, width), f32),
        pre_act=vmem((rows, hidden), f32),
        activated=vmem((rows, hidden), bf16),
        rows_b=vmem((4, tok, width), bf16),
        rows_c=vmem((4, tok, width), bf16),
        rows_o=vmem((4, tok, width), bf16),
        rows_two=vmem((4, tok, width), bf16),
        rows_one=vmem((4, tok, width), bf16),
        give=vmem((5, 3, tok, width), bf16),
        take=vmem((5, 3, tok, width), bf16),
        keep=vmem((3, tok, width), f32),
        pre_grad=vmem((rows, hidden), bf16),
        cross_grad=vmem((rows, cols), bf16),
        heads_out=vmem((4, tok, cols), bf16),
        down_x=vmem((4, 2, hidden // 8, width), bf16),
        down_half=vmem((4, hidden // 8, width), bf16),
        down_part=vmem((3, hidden // 8, width), bf16),
        up_x=vmem((4, 2, width // 8, hidden), bf16),
        up_half=vmem((4, width // 8, hidden), bf16),
        up_part=vmem((3, width // 8, hidden), bf16),
        cross_x=vmem((4, 2, width // 8, 3 * cols), bf16),
        send=dma((232,)),
        recv=dma((232,)),
        local=dma((24,)),
    )
    scratch.update({name: vmem(value.shape, value.dtype) for name, value in kept.items()})
    names = [*orders, *given, *results, *scratch]
    specs = [in_smem] * len(orders) + [
        any_space if name.endswith("_any") or name == "neighbours" else in_vmem for name in given
    ]
    got = pl.pallas_call(
        functools.partial(layer_kernel, names, total_tokens, block),
        out_shape=list(results.values()),
        in_specs=specs,
        out_specs=[any_space] * len(results),
        scratch_shapes=list(scratch.values()),
        compiler_params=pltpu.CompilerParams(
            collective_id=collective_id, has_side_effects=True, vmem_limit_bytes=62 * 2**20
        ),
        name="layer",
    )(*orders.values(), *given.values())
    return types.SimpleNamespace(**dict(zip(kept, got, strict=True)))


class Spread:

    def __init__(self, share, out, send, recv):
        self.share, self.out, self.send, self.recv = share, out, send, recv
        self.c, self.w = places_here()

    def columns(self, place):
        width = self.share.shape[2]
        return self.out.at[self.c, :, pl.ds(pl.multiple_of(place * width, 128), width)]

    def copy(self, j, place):
        return remote(
            self.share.at[self.w ^ j],
            self.columns(place),
            self.send.at[j],
            self.recv.at[j],
            self.c,
            self.w ^ j,
        )

    def own(self):
        return pltpu.make_async_copy(
            self.share.at[self.w], self.columns(self.w), self.send.at[0]
        )

    def start(self):
        for j in (2, 3, 1):
            self.copy(j, self.w).start()
        self.own().start()

    def finish(self):
        self.own().wait()
        for j in (1, 2, 3):
            self.copy(j, self.w).wait_send()
            self.copy(j, self.w ^ j).wait_recv()


class Whole:

    def __init__(self, source, target, send, recv):
        self.source, self.target, self.send, self.recv = source, target, send, recv
        self.c, self.w = places_here()

    def put(self, place):
        rows = self.source.shape[0]
        return self.target.at[pl.ds(pl.multiple_of(place * rows, 32), rows), :]

    def copy(self, j, place):
        return remote(
            self.source, self.put(place), self.send.at[j], self.recv.at[j], self.c, self.w ^ j
        )

    def passed(self, place):
        ref = self.put(place)
        return remote(ref, ref, self.send.at[3], self.recv.at[3], self.c, self.w ^ 1)

    def own(self):
        return pltpu.make_async_copy(self.source, self.put(self.w), self.send.at[0])

    def start(self):
        self.copy(2, self.w).start()
        self.copy(1, self.w).start()
        self.own().start()

    def relay(self):
        self.copy(2, self.w).wait_send()
        self.copy(2, self.w ^ 2).wait_recv()
        self.passed(self.w ^ 2).start()

    def finish(self):
        self.own().wait()
        self.copy(1, self.w).wait_send()
        self.copy(1, self.w ^ 1).wait_recv()
        self.passed(self.w ^ 2).wait_send()
        self.passed(self.w ^ 3).wait_recv()


class MaskSum:

    def __init__(self, ref, got, masks, send, recv):
        self.ref, self.got, self.masks, self.send, self.recv = ref, got, masks, send, recv
        self.c, self.w = places_here()

    def copy(self, k):
        ctx, wa = self.masks[k]
        return remote(
            self.ref, self.got.at[k], self.send.at[k], self.recv.at[k], self.c ^ ctx, self.w ^ wa
        )

    def start(self):
        for k in range(len(self.masks)):
            self.copy(k).start()

    def finish(self):
        for k in range(len(self.masks)):
            self.copy(k).wait()
        self.ref[...] = tree_sum([self.ref[...]] + [self.got[k] for k in range(len(self.masks))])


def finish_kernel(names, *refs):
    v = types.SimpleNamespace(**dict(zip(names, refs, strict=True)))
    c, w = places_here()
    send, recv, local = Pool(v.send), Pool(v.recv), Pool(v.local)
    tok, width = v.tokens.shape
    cols = v.output_x.shape[2] * 8
    share = width // 4

    def load(source, target):
        copy = pltpu.make_async_copy(source, target, local.take(1).at[0])
        copy.start()
        return copy

    loads = [load(v.normed_a_any, v.normed_a), load(v.waves_any, v.waves)]
    late = [load(v.pair_cols_any, v.pair_cols), load(v.near_any, v.near_rows)]
    leaving = Leaving(v, local)

    def line(out):
        return LineGather(out, send.take(13), recv.take(13))

    def summed(x, half, part, got):
        return CtxSum(send.take(12), recv.take(12), x, half, part, got)

    down, up, cross, ctx_o, out_o, pair = (
        line(out)
        for out in (v.down_out, v.up_all, v.cross_all, v.cross_o_out, v.output_out, v.pair_all)
    )
    cross_sum = summed(None, v.cross_half, v.cross_part, v.cross_share)
    ctx_o_sum = summed(v.cross_out_x, v.ctx_o_half, v.ctx_o_part, v.ctx_o_share)
    out_o_sum = summed(v.output_x, v.out_o_half, v.out_o_part, v.out_o_share)
    up_spread = Spread(v.up_share, v.up_all, send.take(4), recv.take(4))
    cross_spread = Spread(v.cross_share, v.cross_all, send.take(4), recv.take(4))
    sum_pair = SumRows(v.pair_give, v.pair_take, send.take(3), recv.take(3))
    sum_near = SumRows(v.near_give, v.near_take, send.take(3), recv.take(3))
    weights = [
        Whole(weight, v.full.at[m], send.take(4), recv.take(4))
        for m, weight in enumerate((v.query_any, v.key_any, v.value_any))
    ]
    stages = [
        MaskSum(v.total, got, masks, send.take(3), recv.take(3))
        for got, masks in (
            (v.got_wa, ((0, 1), (0, 2), (0, 3))),
            (v.got_y, ((1, 0),)),
            (v.got_z, ((2, 0), (4, 0), (6, 0))),
        )
    ]
    b_send, b_recv = send.take(24), recv.take(24)

    def block_copy(j, m, place):
        return remote(
            v.query_grad.at[c ^ j, :, 128 * m : 128 * (m + 1)],
            v.mine.at[m, :, pl.ds(pl.multiple_of(place * 128, 128), 128)],
            b_send.at[3 * j + m],
            b_recv.at[3 * j + m],
            c ^ j,
            w,
        )

    own_blocks = [
        pltpu.make_async_copy(
            v.query_grad.at[c, :, 128 * m : 128 * (m + 1)],
            v.mine.at[m, :, pl.ds(pl.multiple_of(c * 128, 128), 128)],
            b_recv.at[m],
        )
        for m in range(3)
    ]
    v.down_out[c] = v.down_share[...]
    meet_lines()
    down.start()
    up_spread.start()
    cross_sum.start_z((2,))
    ctx_o_sum.start_y()
    out_o_sum.start_y()
    for copy in own_blocks:
        copy.start()

    query_grad = v.query_grad[...].reshape(-1, v.query_grad.shape[2])
    high = v.table_grad[...].astype(bf16)
    low = (v.table_grad[...] - high.astype(f32)).astype(bf16)
    for copy in loads:
        copy.wait()
    mixed = dot_tn(v.normed_a[...], query_grad)
    up_spread.finish()
    up.start()
    down.step(0)
    cross_sum.start_z((3, 1))
    turned = dot_tn(v.waves[...], high) + dot_tn(v.waves[...], low)
    for place in range(4):
        at = place * share
        v.sums[place] = jnp.concatenate([mixed[at : at + share], turned[at : at + share]], axis=1)
    sum_pair.give_far(v.sums[w ^ 3])
    sum_pair.give_near(v.sums[w ^ 1])
    down.step(1)
    up.step(0)
    ctx_o_sum.finish_y()
    ctx_o_sum.start_z()
    out_o_sum.finish_y()
    out_o_sum.start_z()
    sum_pair.pass_on(v.sums[w ^ 2])
    for copy in late:
        copy.wait()
    near_count = v.near_grad.shape[0]

    def near_part(r):
        return dot_nt(v.near_rows[r * near_count : (r + 1) * near_count, :], v.pair_cols[...])

    sum_near.give_far(near_part(3))
    sum_near.give_near(near_part(1))
    v.pair_all[c] = sum_pair.total(v.sums[w]).astype(bf16)
    pair.start()
    up.step(1)
    down.step(2)
    cross_sum.finish_z()
    cross_spread.start()
    sum_near.pass_on(near_part(2))
    v.near_grad[...] = near_part(0)
    cross_spread.finish()
    cross.start()
    for j in (4, 6, 5, 7, 2, 3, 1):
        for m in range(3):
            block_copy(j, m, c).start()
    for weight in weights:
        weight.start()
    up.step(2)
    pair.step(0)
    ctx_o_sum.finish_z()
    v.cross_o_out[c] = v.ctx_o_share[...]
    ctx_o.start()
    out_o_sum.finish_z()
    v.output_out[c] = v.out_o_share[...]
    out_o.start()
    cross.step(0)
    pair.step(1)
    ctx_o.step(0)
    out_o.step(0)
    cross.step(1)
    ctx_o.step(1)
    out_o.step(1)

    for j in range(1, 8):
        for m in range(3):
            block_copy(j, m, c ^ j).wait_recv()
    for copy in own_blocks:
        copy.wait()
    pair.step(2)
    for weight in weights:
        weight.relay()
    for weight in weights:
        weight.finish()
    normed_grad = dot_nt(v.mine[0], v.full[0])
    normed_grad = normed_grad + dot_nt(v.mine[1], v.full[1])
    normed_grad = normed_grad + dot_nt(v.mine[2], v.full[2])
    hidden = v.tokens[...].astype(f32)
    inverse = inverse_rms(hidden)
    v.tokens_grad[...] = v.one_grad[...] + norm_pull(hidden, inverse, v.gains[0:1, :], normed_grad)
    leaving.leave("tokens_grad")
    v.total[...] = v.small[...]
    v.total[0:1, 0:width] = jnp.sum(normed_grad * hidden * inverse, axis=0, keepdims=True)
    stages[0].start()
    ctx_o.step(2)
    out_o.step(2)
    cross.step(2)
    stages[0].finish()
    stages[1].start()
    v.near_grad[...] = sum_near.total(v.near_grad[...])
    leaving.leave("near_grad")
    stages[1].finish()
    stages[2].start()
    down.finish()
    leaving.leave("down_out")
    up.finish()
    used = share // 8
    for part in range(8):
        v.up_out[part * used : (part + 1) * used, :] = v.up_all[part, 0:used, :].astype(f32)
    leaving.leave("up_out")
    pair.finish()
    pair_outs = (v.query_out, v.key_out, v.value_out, v.relative_out)
    for part in range(8):
        for m, out in enumerate(pair_outs):
            out[:, 128 * part : 128 * (part + 1)] = v.pair_all[part, :, 128 * m : 128 * (m + 1)]
    for name in ("query_out", "key_out", "value_out", "relative_out"):
        leaving.leave(name)
    ctx_o.finish()
    leaving.leave("cross_o_out")
    out_o.finish()
    leaving.leave("output_out")
    cross.finish()
    for m, out in enumerate((v.cross_query_out, v.cross_key_out, v.cross_value_out)):
        for part in range(8):
            for place in range(4):
                at = (place * 3 + m) * cols
                out[part * used : (part + 1) * used, place * cols : (place + 1) * cols] = v.cross_all[
                    part, 0:used, at : at + cols
                ].astype(f32)
    for name in ("cross_query_out", "cross_key_out", "cross_value_out"):
        leaving.leave(name)
    stages[2].finish()
    devices = 32.0
    loss = v.total[5:6, :] * devices / (2.0 * width * v.total[6:7, :])
    v.total[7:8, :] = loss
    leaving.leave("total")
    for j in range(1, 8):
        for m in range(3):
            block_copy(j, m, c).wait_send()
    leaving.finish()


def finish(given, collective_id):
    tok, width = given["tokens"].shape
    near = given["near_any"].shape[0]
    padded = given["up_share"].shape[1]
    hidden = given["up_share"].shape[2]
    cols = given["output_x"].shape[2] * 8
    share = width // 4
    any_space = pl.BlockSpec(memory_space=pl.ANY)
    shape = jax.ShapeDtypeStruct
    vmem = pltpu.VMEM
    dma = pltpu.SemaphoreType.DMA
    part = (cols // 8, width)
    kept = dict(
        tokens_grad=shape((tok, width), f32),
        near_grad=shape((near // 4, width), f32),
        total=shape(given["small"].shape, f32),
        down_out=shape((8,) + given["down_share"].shape, bf16),
        up_out=shape((share, 4 * hidden), f32),
        cross_query_out=shape((share, 4 * cols), f32),
        cross_key_out=shape((share, 4 * cols), f32),
        cross_value_out=shape((share, 4 * cols), f32),
        cross_o_out=shape((8,) + part, bf16),
        output_out=shape((8,) + part, bf16),
        query_out=shape((share, 1024), bf16),
        key_out=shape((share, 1024), bf16),
        value_out=shape((share, 1024), bf16),
        relative_out=shape((share, 1024), bf16),
    )
    results = {name + "_any": value for name, value in kept.items()}
    scratch = dict(
        normed_a=vmem(given["normed_a_any"].shape, bf16),
        waves=vmem(given["waves_any"].shape, bf16),
        pair_cols=vmem(given["pair_cols_any"].shape, bf16),
        near_rows=vmem(given["near_any"].shape, bf16),
        full=vmem((3, width, 1024), bf16),
        mine=vmem((3, tok, 1024), bf16),
        sums=vmem((4, share, 512), f32),
        up_all=vmem((8, padded, 4 * hidden), bf16),
        cross_all=vmem((8, padded, 12 * cols), bf16),
        pair_all=vmem((8, share, 512), bf16),
        cross_part=vmem((3, width // 8, 3 * cols), bf16),
        cross_share=vmem((4, padded, 3 * cols), bf16),
        ctx_o_half=vmem((4,) + part, bf16),
        out_o_half=vmem((4,) + part, bf16),
        ctx_o_part=vmem((3,) + part, bf16),
        ctx_o_share=vmem(part, bf16),
        out_o_part=vmem((3,) + part, bf16),
        out_o_share=vmem(part, bf16),
        pair_give=vmem((3, share, 512), bf16),
        pair_take=vmem((3, share, 512), bf16),
        near_give=vmem((3, near // 4, width), bf16),
        near_take=vmem((3, near // 4, width), bf16),
        got_wa=vmem((3,) + given["small"].shape, f32),
        got_y=vmem((1,) + given["small"].shape, f32),
        got_z=vmem((3,) + given["small"].shape, f32),
        send=dma((184,)),
        recv=dma((184,)),
        local=dma((24,)),
    )
    scratch.update({name: vmem(value.shape, value.dtype) for name, value in kept.items()})
    names = [*given, *results, *scratch]
    got = pl.pallas_call(
        functools.partial(finish_kernel, names),
        out_shape=list(results.values()),
        in_specs=[any_space if name.endswith("_any") else in_vmem for name in given],
        out_specs=[any_space] * len(results),
        scratch_shapes=list(scratch.values()),
        compiler_params=pltpu.CompilerParams(
            collective_id=collective_id, has_side_effects=True, vmem_limit_bytes=62 * 2**20
        ),
        name="finish",
    )(*given.values())
    return types.SimpleNamespace(**dict(zip(kept, got, strict=True)))


def skew(wide, count):
    lead = wide.shape[:-2]
    rows, span = wide.shape[-2:]
    edge = [(0, 0)] * len(lead)
    padded = jnp.pad(wide, edge + [(0, 0), (0, 1)])
    flat = padded.reshape(lead + (rows * (span + 1),))
    flat = lax.slice_in_dim(flat, rows - 1, rows - 1 + rows * span, axis=len(lead))
    return flat.reshape(lead + (rows, span))[..., :count]


def unskew(grad, span):
    lead = grad.shape[:-2]
    rows, count = grad.shape[-2:]
    edge = [(0, 0)] * len(lead)
    wide = jnp.pad(grad, edge + [(0, 0), (0, span - count)])
    flat = jnp.pad(wide.reshape(lead + (rows * span,)), edge + [(rows - 1, 1)])
    return flat.reshape(lead + (rows, span + 1))[..., :span]


def tile_scores(content_rows, position_rows, key_rows, relative, row_start, key_start):
    rows = content_rows.shape[0]
    count = key_rows.shape[0]
    scale = content_rows.shape[-1] ** (-0.5)
    content = jnp.einsum("qhe,khe->hqk", content_rows, key_rows, preferred_element_type=f32)
    wide = jnp.einsum("qhe,whe->hqw", position_rows, relative, preferred_element_type=f32)
    scores = (content + skew(wide, count)) * scale
    causal = (row_start + jnp.arange(rows))[:, None] >= (key_start + jnp.arange(count))[None, :]
    return (scores, causal[None])


def tile_forward(
    content_rows, position_rows, row_start, relative, key_rows, value_rows, key_start, state
):
    top, total, accum = state
    scores, causal = tile_scores(
        content_rows, position_rows, key_rows, relative, row_start, key_start
    )
    scores = jnp.where(causal, scores, neg_big)
    new_top = jnp.maximum(top, jnp.max(scores, axis=-1))
    raised = jnp.where(causal, jnp.exp(scores - new_top[..., None]), 0.0)
    fade = jnp.exp(top - new_top)
    total = total * fade + jnp.sum(raised, axis=-1)
    accum = accum * fade[..., None] + jnp.einsum(
        "hqk,khe->hqe", raised.astype(bf16), value_rows, preferred_element_type=f32
    )
    return (new_top, total, accum)


def tile_backward(
    content_rows,
    position_rows,
    row_start,
    relative,
    key_rows,
    value_rows,
    grad_rows,
    log_rows,
    delta_rows,
    key_start,
):
    scores, causal = tile_scores(
        content_rows, position_rows, key_rows, relative, row_start, key_start
    )
    scale = content_rows.shape[-1] ** (-0.5)
    shares = jnp.where(causal, jnp.exp(scores - log_rows[..., None]), 0.0)
    share_grad = jnp.einsum("qhe,khe->hqk", grad_rows, value_rows, preferred_element_type=f32)
    score_grad = (shares * (share_grad - delta_rows[..., None])).astype(bf16)
    content_grad = jnp.einsum("hqk,khe->qhe", score_grad, key_rows, preferred_element_type=f32)
    wide_grad = unskew(score_grad, relative.shape[0])
    position_grad = jnp.einsum("hqw,whe->qhe", wide_grad, relative, preferred_element_type=f32)
    table_part = jnp.einsum("hqw,qhe->whe", wide_grad, position_rows, preferred_element_type=f32)
    key_grad = jnp.einsum("hqk,qhe->khe", score_grad, content_rows, preferred_element_type=f32)
    value_grad = jnp.einsum(
        "hqk,qhe->khe", shares.astype(bf16), grad_rows, preferred_element_type=f32
    )
    return (
        content_grad * scale,
        position_grad * scale,
        table_part * scale,
        key_grad * scale,
        value_grad,
    )


def nest_tiles(tile_fn):
    inner = jax.vmap(tile_fn, in_axes=(0, 0, 0, 0, None, None, 0))
    return jax.vmap(inner, in_axes=(0, 0, None, None, 0, 0, 0))


def to_global(stored, inverse, block):
    seqs, seq_len, width = stored.shape
    blocks = stored.reshape(seqs, seq_len // block, block * width)
    chosen = (inverse[:, None] == jnp.arange(seq_len // block)[None, :]).astype(bf16)
    moved = jnp.einsum("gs,nsx->ngx", chosen, blocks, preferred_element_type=f32)
    return moved.astype(bf16).reshape(stored.shape)


class SplitQueries:

    def __init__(self, query, keys, values, biases, relative, block_order, inverse, block):
        self.seqs, self.tok_dev, self.width = keys.shape
        self.heads = self.width // HEAD_DIM
        self.block = block
        self.block_order = block_order
        ctx_count = lax.axis_size("ctx")
        self.seq_len = self.tok_dev * ctx_count
        self.key_len = min(512, self.seq_len)
        pad = jnp.zeros((self.key_len + block, self.width), bf16)
        table = jnp.concatenate([relative, pad], axis=0)
        self.table = table.reshape(-1, self.heads, HEAD_DIM)
        lead = (self.seqs, 2, block, self.heads, HEAD_DIM)
        self.content = (query + biases[0]).astype(bf16).reshape(lead)
        self.position = (query + biases[1]).astype(bf16).reshape(lead)
        gathered = [lax.all_gather(part, "ctx", axis=1, tiled=True) for part in (keys, values)]
        shape = (self.seqs, self.seq_len, self.heads, HEAD_DIM)
        self.keys, self.values = [to_global(part, inverse, block).reshape(shape) for part in gathered]
        self.starts = lax.dynamic_slice_in_dim(block_order, 2 * lax.axis_index("ctx"), 2, 0) * block

    def rows(self, index):
        start = index * self.key_len
        keys = lax.dynamic_slice_in_dim(self.keys, start, self.key_len, 1)
        values = lax.dynamic_slice_in_dim(self.values, start, self.key_len, 1)
        span = self.block + self.key_len
        offsets = [self.seq_len - self.block - self.starts[slot] + start for slot in range(2)]
        relative = [lax.dynamic_slice_in_dim(self.table, offset, span, 0) for offset in offsets]
        return start, keys, values, jnp.stack(relative), offsets

    def to_stored(self, part):
        count = self.seq_len // self.block
        blocks = part.reshape(self.seqs, count, self.block * self.width)
        chosen = (self.block_order[:, None] == jnp.arange(count)[None, :]).astype(f32)
        moved = jnp.einsum("sg,ngx->nsx", chosen, blocks, precision=highest)
        return moved.reshape(self.seqs, self.seq_len, self.width)

    def forward(self):
        def step(state, index):
            start, keys, values, relative, _ = self.rows(index)

            def tile(content, position, row_start, table, keys_seq, values_seq, tile_state):
                return tile_forward(
                    content, position, row_start, table, keys_seq, values_seq, start, tile_state
                )

            return nest_tiles(tile)(
                self.content, self.position, self.starts, relative, keys, values, state
            ), None

        shape = (self.seqs, 2, self.heads, self.block)
        state = (
            jnp.full(shape, neg_big, f32),
            jnp.zeros(shape, f32),
            jnp.zeros(shape + (HEAD_DIM,), f32),
        )
        (top, total, accum), _ = lax.scan(step, state, jnp.arange(self.seq_len // self.key_len))
        self.log_total = top + jnp.log(total)
        self.out = accum / total[..., None]
        moved = jnp.transpose(self.out, (0, 1, 3, 2, 4))
        return moved.reshape(self.seqs * self.tok_dev, self.width).astype(bf16)

    def backward(self, grad):
        block, seq_len, key_len = self.block, self.seq_len, self.key_len
        lead = (self.seqs, 2, block, self.heads, HEAD_DIM)
        grad = grad.reshape(lead)
        delta = jnp.einsum("sbqhe,sbhqe->sbhq", grad.astype(f32), self.out)
        def step(carry, index):
            start, keys, values, relative, offsets = self.rows(index)

            def tile(content, position, row_start, table, keys_seq, values_seq, extra):
                return tile_backward(
                    content, position, row_start, table, keys_seq, values_seq, *extra, start
                )

            extra = (grad, self.log_total, delta)
            parts = nest_tiles(tile)(
                self.content, self.position, self.starts, relative, keys, values, extra
            )
            table = carry[2]
            table_sum = jnp.sum(parts[2], axis=0)
            for slot in range(2):
                offset = offsets[slot]
                current = lax.dynamic_slice_in_dim(table, offset, block + key_len, 0)
                table = lax.dynamic_update_slice_in_dim(table, current + table_sum[slot], offset, 0)
            sums = []
            for total, part in zip(carry[3:], parts[3:]):
                current = lax.dynamic_slice_in_dim(total, start, key_len, 1)
                part = current + jnp.sum(part, axis=1)
                sums.append(lax.dynamic_update_slice_in_dim(total, part, start, 1))
            key_acc, value_acc = sums
            return (carry[0] + parts[0], carry[1] + parts[1], table, key_acc, value_acc), None

        zero_tiles = jnp.zeros(lead, f32)
        zero_keys = jnp.zeros((self.seqs, seq_len, self.heads, HEAD_DIM), f32)
        carry = (zero_tiles, zero_tiles, jnp.zeros(self.table.shape, f32), zero_keys, zero_keys)
        carry, _ = lax.scan(step, carry, jnp.arange(seq_len // key_len))
        owned = [
            lax.psum_scatter(
                self.to_stored(part), "ctx", scatter_dimension=1, tiled=True
            )
            for part in carry[3:]
        ]
        flat = (self.seqs * self.tok_dev, self.width)
        query_grad = (carry[0] + carry[1]).reshape(flat).astype(bf16)
        key_grad, value_grad = [part.reshape(flat).astype(bf16) for part in owned]
        bias_grads = jnp.stack(
            [jnp.sum(part, axis=(0, 1, 2)).reshape(self.width) for part in carry[:2]]
        )
        table_grad = carry[2].reshape(-1, self.width)[:seq_len]
        return query_grad, key_grad, value_grad, bias_grads, table_grad


def local_general(
    tokens,
    neighbours,
    teacher,
    valid_mask,
    block_order,
    query_weight,
    key_weight,
    value_weight,
    output_weight,
    relative_weight,
    content_bias,
    position_bias,
    cross_query_weight,
    cross_key_weight,
    cross_value_weight,
    cross_output_weight,
    up_weight,
    down_weight,
    attention_gain,
    cross_gain,
    feedforward_gain,
):
    places = lax.axis_size("wa")
    ctx_count = lax.axis_size("ctx")
    place = lax.axis_index("wa")
    here = lax.axis_index("ctx")
    _, tok_dev, width = tokens.shape
    seq_len = tok_dev * ctx_count
    block = tok_dev // 2
    cols = HEADS * HEAD_DIM // places
    rows = places * tok_dev

    token_parts = gather_parts(tokens[0])
    query_cols, key_cols, value_cols = [
        take_columns(weight) for weight in (query_weight, key_weight, value_weight)
    ]
    relative_cols = take_columns(relative_weight)
    gains = lax.all_gather(
        jnp.stack([attention_gain, cross_gain, feedforward_gain]), "wa", axis=1, tiled=True
    ).astype(f32)
    gain_one, gain_two, gain_three = gains[0:1], gains[1:2], gains[2:3]
    cross_query_cols, cross_key_cols, cross_value_cols = [
        take_columns(weight) for weight in (cross_query_weight, cross_key_weight, cross_value_weight)
    ]
    cross_pair_cols = jnp.concatenate([cross_key_cols, cross_value_cols], axis=1)
    near_rows = jnp.concatenate(gather_parts(neighbours.reshape(-1, width)), axis=0)
    up_cols = take_columns(up_weight)
    valid = valid_mask.astype(f32).reshape(tok_dev, 1)
    count = jnp.sum(valid).reshape(1, 1)
    count = all_summed(all_summed(count, "wa"), "ctx")

    slots = jnp.arange(2 * ctx_count)
    inverse = jnp.sum(jnp.where(block_order[None, :] == slots[:, None], slots[None, :], 0), axis=1)
    inverse = inverse.astype(jnp.int32)
    distance = (seq_len - 1 - jnp.arange(seq_len)).astype(f32)
    waves = sinusoid(distance, width).astype(bf16)

    hidden_all = jnp.concatenate(token_parts, axis=0).astype(f32)
    scale_all = inverse_rms(hidden_all)
    normed_a = (hidden_all * scale_all * gain_one).astype(bf16)
    biases = jnp.stack([content_bias, position_bias]).astype(f32)
    mixed_cols = jnp.concatenate([query_cols, key_cols, value_cols], axis=1)
    qkv = dot_nn(normed_a, mixed_cols).reshape(places, tok_dev, 3 * cols)
    relative = dot_nn(waves, relative_cols).astype(bf16)
    general = SplitQueries(
        qkv[..., :cols],
        qkv[..., cols : 2 * cols].astype(bf16),
        qkv[..., 2 * cols :].astype(bf16),
        biases,
        relative,
        block_order,
        inverse,
        block,
    )
    attended = general.forward()

    def to_owner(product):
        return scatter_parts([product[r * tok_dev : (r + 1) * tok_dev] for r in range(places)])

    def from_all(value):
        return jnp.concatenate(gather_parts(value), axis=0)

    hidden_in = tokens[0].astype(f32)
    hidden_one = hidden_in + to_owner(dot_nn(attended, output_weight))

    scale_two = inverse_rms(hidden_one)
    normed_b = from_all((hidden_one * scale_two * gain_two).astype(bf16))
    cross_q = dot_nn(normed_b, cross_query_cols).astype(bf16)
    cross_pair = dot_nn(near_rows, cross_pair_cols).astype(bf16)
    crossed = cross_forward(cross_q, cross_pair)
    hidden_two = hidden_one + to_owner(dot_nn(crossed, cross_output_weight))

    scale_three = inverse_rms(hidden_two)
    normed_c = from_all((hidden_two * scale_three * gain_three).astype(bf16))
    pre_act = dot_nn(normed_c, up_cols)
    activated = gelu_tanh(pre_act).astype(bf16)
    layer_out = hidden_two + to_owner(dot_nn(activated, down_weight))

    error = layer_out - teacher[0].astype(f32)
    error_sum = jnp.sum(valid * error * error).reshape(1, 1)
    error_sum = all_summed(all_summed(error_sum, "wa"), "ctx")
    loss = (error_sum / (2.0 * count * width)).reshape(())
    out_grad = (places * seq_len) / count * valid * error

    out_low = from_all(out_grad.astype(bf16))
    act_grad = dot_nt(out_low, down_weight)
    _, gelu_pull = jax.vjp(gelu_tanh, pre_act)
    pre_grad = gelu_pull(act_grad)[0].astype(bf16)
    down_grad = dot_tn(activated, out_low).astype(bf16)
    up_grad = dot_tn(normed_c, pre_grad).astype(bf16)
    normed_c_grad = to_owner(dot_nt(pre_grad, up_cols))
    two_grad = out_grad + norm_pull(hidden_two, scale_three, gain_three, normed_c_grad)
    gain_three_grad = jnp.sum(normed_c_grad * hidden_two * scale_three, axis=0, keepdims=True)
    down_out = sum_row_grads(down_grad)
    up_out = sum_column_grads(up_grad[None])[0]

    two_low = from_all(two_grad.astype(bf16))
    crossed_grad = dot_nt(two_low, cross_output_weight).astype(bf16)
    cross_q_grad, cross_pair_grad = cross_backward(cross_q, cross_pair, crossed_grad)
    normed_b_grad = to_owner(dot_nt(cross_q_grad, cross_query_cols))
    one_grad = two_grad + norm_pull(hidden_one, scale_two, gain_two, normed_b_grad)
    gain_two_grad = jnp.sum(normed_b_grad * hidden_one * scale_two, axis=0, keepdims=True)
    cross_output_grad = dot_tn(crossed, two_low).astype(bf16)
    cross_query_grad = dot_tn(normed_b, cross_q_grad).astype(bf16)
    cross_key_grad = dot_tn(near_rows, cross_pair_grad[:, :cols]).astype(bf16)
    cross_value_grad = dot_tn(near_rows, cross_pair_grad[:, cols:]).astype(bf16)
    cross_output_out = sum_row_grads(cross_output_grad)
    cross_out = sum_column_grads(jnp.stack([cross_key_grad, cross_value_grad]))
    cross_query_out = sum_column_grads(cross_query_grad[None])[0]
    near_grad = dot_nt(cross_pair_grad, cross_pair_cols)
    near_count = near_rows.shape[0] // places
    near_grad = scatter_parts(
        [near_grad[r * near_count : (r + 1) * near_count] for r in range(places)]
    )
    neighbours_grad = near_grad.reshape(neighbours.shape)

    one_low = from_all(one_grad.astype(bf16))
    attended_grad = dot_nt(one_low, output_weight).astype(bf16)
    output_grad = dot_tn(attended, one_low).astype(bf16)
    output_out = sum_row_grads(output_grad)
    query_grad, key_grad, value_grad, bias_grads, table_grad = general.backward(attended_grad)
    qkv_grad = jnp.concatenate([query_grad, key_grad, value_grad], axis=1)
    table_high = table_grad.astype(bf16)
    table_low = (table_grad - table_high.astype(f32)).astype(bf16)
    relative_grad = (dot_tn(waves, table_high) + dot_tn(waves, table_low)).astype(bf16)
    mixed_grad = dot_tn(normed_a, qkv_grad).astype(bf16)
    whole = [mixed_grad[:, m * cols : (m + 1) * cols] for m in range(3)]
    attention_out = sum_column_grads(jnp.stack(whole + [relative_grad]))
    normed_a_part = dot_nt(qkv_grad, mixed_cols)
    gain_one_part = jnp.sum(normed_a_part * hidden_all * scale_all, axis=0, keepdims=True)
    normed_a_grad = to_owner(normed_a_part)
    tokens_grad = one_grad + norm_pull(hidden_in, scale_all[:tok_dev], gain_one, normed_a_grad)

    gain_grads = jnp.concatenate([gain_one_part, gain_two_grad, gain_three_grad], axis=0)
    gain_grads = all_summed(gain_grads, "wa")
    share = width // places
    gain_grads = lax.dynamic_slice_in_dim(gain_grads, place * share, share, 1)
    small = jnp.concatenate([gain_grads.reshape(1, -1), bias_grads.reshape(1, -1)], axis=1)
    small = all_summed(small, "ctx")[0]
    gain_out = small[: 3 * share].reshape(3, share)
    bias_out = small[3 * share :].reshape(2, cols)

    return (
        layer_out[None],
        loss,
        tokens_grad[None],
        neighbours_grad,
        attention_out[0],
        attention_out[1],
        attention_out[2],
        output_out,
        attention_out[3],
        bias_out[0],
        bias_out[1],
        cross_query_out,
        cross_out[0],
        cross_out[1],
        cross_output_out,
        up_out,
        down_out,
        gain_out[0],
        gain_out[1],
        gain_out[2],
    )


def local_by_heads(
    tokens,
    neighbours,
    teacher,
    valid_mask,
    block_order,
    query_weight,
    key_weight,
    value_weight,
    output_weight,
    relative_weight,
    content_bias,
    position_bias,
    cross_query_weight,
    cross_key_weight,
    cross_value_weight,
    cross_output_weight,
    up_weight,
    down_weight,
    attention_gain,
    cross_gain,
    feedforward_gain,
):
    places = 4
    ctx_count = 8
    place = lax.axis_index("wa")
    here = lax.axis_index("ctx")
    _, tok_dev, width = tokens.shape
    seq_len = tok_dev * ctx_count
    block = tok_dev // 2
    attn = HEADS * HEAD_DIM
    cols = attn // places
    share = width // places

    slots = jnp.arange(2 * ctx_count)
    inverse = jnp.sum(jnp.where(block_order[None, :] == slots[:, None], slots[None, :], 0), axis=1)
    inverse = inverse.astype(jnp.int32)
    half = width // 2
    freq = jnp.exp(-jnp.log(10000.0) * jnp.arange(half, dtype=f32) * 2.0 / width)
    coarse = (64.0 * jnp.arange(seq_len // 64, dtype=f32)[::-1])[:, None] * freq
    fine = jnp.arange(64, dtype=f32)[::-1][:, None] * freq
    sin_a, cos_a, sin_b, cos_b = jnp.sin(coarse), jnp.cos(coarse), jnp.sin(fine), jnp.cos(fine)
    left = jnp.concatenate([sin_a, cos_a, cos_b, sin_b], axis=0)
    right = jnp.concatenate([cos_a, -sin_a, cos_b, sin_b], axis=0)
    tables = jnp.concatenate([left, right], axis=1)

    done = layer(
        float(places * seq_len),
        block,
        dict(inverse=inverse, order=block_order),
        dict(
            tokens=tokens[0],
            teacher=teacher[0],
            mask=valid_mask,
            gain_row=jnp.concatenate(
                [
                    row.astype(f32)
                    for row in (
                        attention_gain,
                        cross_gain,
                        feedforward_gain,
                        content_bias,
                        position_bias,
                    )
                ]
            )[None],
            tables=tables,
            neighbours=neighbours.reshape(-1, width),
            query_any=query_weight,
            key_any=key_weight,
            value_any=value_weight,
            relative_any=relative_weight,
            cross_query_any=cross_query_weight,
            cross_key_any=cross_key_weight,
            cross_value_any=cross_value_weight,
            up_any=up_weight,
            output_any=output_weight,
            cross_out_any=cross_output_weight,
            down_any=down_weight,
        ),
        1,
    )
    last = finish(
        dict(
            query_grad=done.query_grad,
            table_grad=done.table_grad,
            small=done.small,
            down_share=done.down_share,
            up_share=done.up_share,
            cross_half=done.cross_half,
            cross_out_x=done.cross_out_x,
            output_x=done.output_x,
            one_grad=done.one_grad,
            tokens=tokens[0],
            gains=done.gains,
            normed_a_any=done.normed_a,
            waves_any=done.waves,
            near_any=done.pair_grad,
            pair_cols_any=done.pair_cols,
            query_any=query_weight,
            key_any=key_weight,
            value_any=value_weight,
        ),
        2,
    )
    total = last.total
    gain_out = lax.dynamic_slice_in_dim(total[0:3], place * share, share, 1)
    bias_out = lax.dynamic_slice_in_dim(total[3:5].reshape(ctx_count, 2, 128), place * 2, 2, 0)
    bias_out = bias_out.transpose(1, 0, 2).reshape(2, cols)
    loss = total[7, 0]
    down_out = last.down_out.reshape(down_weight.shape).astype(f32)
    cross_output_out = last.cross_o_out.reshape(cols, width).astype(f32)
    output_out = last.output_out.reshape(cols, width).astype(f32)

    return (
        done.layer_out[None],
        loss,
        last.tokens_grad[None],
        last.near_grad.reshape(neighbours.shape),
        last.query_out.astype(f32),
        last.key_out.astype(f32),
        last.value_out.astype(f32),
        output_out,
        last.relative_out.astype(f32),
        bias_out[0],
        bias_out[1],
        last.cross_query_out,
        last.cross_key_out,
        last.cross_value_out,
        cross_output_out,
        last.up_out,
        down_out,
        gain_out[0],
        gain_out[1],
        gain_out[2],
    )


def solution(mesh):
    row = P("wa", None)
    flat = P("wa")
    in_specs = (
        P("wa", "ctx", None),
        P("wa", "ctx", None, None),
        P("wa", "ctx", None),
        P("wa", "ctx"),
        P(),
        row,
        row,
        row,
        row,
        row,
        flat,
        flat,
        row,
        row,
        row,
        row,
        row,
        row,
        flat,
        flat,
        flat,
    )
    out_specs = (
        P("wa", "ctx", None),
        P(),
        P("wa", "ctx", None),
        P("wa", "ctx", None, None),
        row,
        row,
        row,
        row,
        row,
        flat,
        flat,
        row,
        row,
        row,
        row,
        row,
        row,
        flat,
        flat,
        flat,
    )
    by_heads = mesh.shape["ctx"] == 8 and mesh.shape["wa"] == 4
    local = local_by_heads if by_heads else local_general
    return jax.shard_map(local, mesh=mesh, in_specs=in_specs, out_specs=out_specs, check_vma=False)
```
